32 devices in a mesh: replica: 4 (over x, core), group: 8 (over z, y).
Axes of the slice: x: 2, y: 2, z: 4, core: 2. Of those that a mesh axis runs over, the one named last changes fastest.
Arguments:
- tokens: bfloat16 [25216, 512], P(('replica', 'group')), may hold values from -6 to 6
- cotangent: bfloat16 [25216, 512], P(('replica', 'group')), may hold values from -6 to 6
- expert_index: int32 [25216, 2], P(('replica', 'group')), may hold values from 0 to 3, all different within a row; in each aligned block of 394 rows (0 to 393, 394 to 787, ...) at most 392 rows name the same one
- qkv_weight: float32 [512, 1536], P('group'), may hold values from -0.25 to 0.25
- out_weight: float32 [512, 512], P('group'), may hold values from -1.5 to 1.5
- router_weight: float32 [512, 4], P('group'), may hold values from -0.1875 to 0.1875
- up_weight: float32 [4, 512, 2048], P(None, 'group'), may hold values from -0.25 to 0.25
- up_bias: float32 [4, 2048], P(None, 'group'), may hold values from -0.5 to 0.5
- down_weight: float32 [4, 2048, 512], P(None, 'group'), may hold values from -0.5 to 0.5
- vectors: float32 [11, 512], P(None, 'group'), may hold values from -0.4 to 1.4, as said below
- qkv_moments: float32 [2, 512, 1536], P(None, 'group'), as said below
- out_moments: float32 [2, 512, 512], P(None, 'group'), as said below
- router_moments: float32 [2, 512, 4], P(None, 'group'), as said below
- up_moments: float32 [2, 4, 512, 2048], P(None, None, 'group'), as said below
- up_bias_moments: float32 [2, 4, 2048], P(None, None, 'group'), as said below
- down_moments: float32 [2, 4, 2048, 512], P(None, None, 'group'), as said below
- vector_moments: float32 [2, 11, 512], P(None, None, 'group'), as said below
Outputs:
- block_out: bfloat16 [25216, 512], P(('replica', 'group'))
- input_grad: float32 [25216, 512], P(('replica', 'group'))
- qkv_grad: float32 [512, 1536], P('group')
- out_grad: float32 [512, 512], P('group')
- router_grad: float32 [512, 4], P('group')
- up_grad: float32 [4, 512, 2048], P(None, 'group')
- up_bias_grad: float32 [4, 2048], P(None, 'group')
- down_grad: float32 [4, 2048, 512], P(None, 'group')
- vectors_grad: float32 [11, 512], P(None, 'group')
- qkv_new: float32 [512, 1536], P('group')
- out_new: float32 [512, 512], P('group')
- router_new: float32 [512, 4], P('group')
- up_new: float32 [4, 512, 2048], P(None, 'group')
- up_bias_new: float32 [4, 2048], P(None, 'group')
- down_new: float32 [4, 2048, 512], P(None, 'group')
- vectors_new: float32 [11, 512], P(None, 'group')
- qkv_moments_new: float32 [2, 512, 1536], P(None, 'group')
- out_moments_new: float32 [2, 512, 512], P(None, 'group')
- router_moments_new: float32 [2, 512, 4], P(None, 'group')
- up_moments_new: float32 [2, 4, 512, 2048], P(None, None, 'group')
- up_bias_moments_new: float32 [2, 4, 2048], P(None, None, 'group')
- down_moments_new: float32 [2, 4, 2048, 512], P(None, None, 'group')
- vector_moments_new: float32 [2, 11, 512], P(None, None, 'group')
The draws below stay inside these ranges and needn't reach their ends.
Inputs may be any that keep to these rules, and one draw needn't show every extreme that they name: `expert_index`: in each aligned block of 394 rows (one micro-batch of one device) no expert is named by more than 392 rows; a row names two different experts. `vectors`: rows 0 and 5 are gains near one, the others biases near zero. `qkv_moments`: index 1 of the first dimension is positive. `out_moments`: index 1 of the first dimension is positive. `router_moments`: index 1 of the first dimension is positive. `up_moments`: index 1 of the first dimension is positive. `up_bias_moments`: index 1 of the first dimension is positive. `down_moments`: index 1 of the first dimension is positive. `vector_moments`: index 1 of the first dimension is positive.
All inputs are finite; a program needn't handle non-finite values.
Results may differ from the reference program's by a relative error of at most 0.019.
Values may be sent and summed in bfloat16 or wider, within the bound.
A program may use at most 256 MiB of HBM per device.

```python
import math
import jax
import jax.numpy as jnp
import numpy as np
from jax import lax

D = 512
HEADS = 8
HEAD_DIM = 64
F = 2048
E = 4
S = 197
IMG_MB = 2
MB_TOK = 394
CAP = 392
NV = 11
TOKENS = 25216


def moment_pair(key, shape, scale):
    key_one, key_two = jax.random.split(key)
    first = scale * jnp.clip(jax.random.normal(key_one, shape, jnp.float32), -4.0, 4.0)
    factor = jnp.exp(jax.random.uniform(key_two, shape, jnp.float32, -0.6931, 0.6931))
    root = scale * jnp.sqrt(2.0 * factor)
    return jnp.stack([first, root])


def draw_vectors(key, part):
    base = 0.1 * jnp.clip(jax.random.normal(key, (NV, D), jnp.float32), -4.0, 4.0)
    rows = jnp.arange(NV)[:, None]
    is_gain = (rows == 0) | (rows == 5)
    return jnp.where(is_gain, 1.0 + base, base)


def draw_qkv_moments(key, part):
    return moment_pair(key, (D, 3 * D), float(TOKENS) ** 0.5)


def draw_out_moments(key, part):
    return moment_pair(key, (D, D), 0.15 * float(TOKENS) ** 0.5)


def draw_router_moments(key, part):
    return moment_pair(key, (D, E), 10.0 * float(TOKENS) ** 0.5)


def draw_up_moments(key, part):
    return moment_pair(key, (E, D, F), 0.3 * float(TOKENS // 2) ** 0.5)


def draw_up_bias_moments(key, part):
    return moment_pair(key, (E, F), 0.3 * float(TOKENS // 2) ** 0.5)


def draw_down_moments(key, part):
    return moment_pair(key, (E, F, D), 0.2 * float(TOKENS // 2) ** 0.5)


def draw_vector_moments(key, part):
    return moment_pair(key, (NV, D), float(TOKENS) ** 0.5)


def levels(rng, dims, cuts, low, high):
    level, own = 1.0, jax.random.fold_in(rng, 6)
    for position, parts in cuts:
        heights = jnp.exp(jax.random.uniform(jax.random.fold_in(own, position), (parts,), jnp.float32, low / len(cuts), high / len(cuts)))
        level = level * jnp.repeat(heights, dims[position] // parts).reshape([-1 if axis == position else 1 for axis in range(len(dims))])
    return level


def assign_block(own_key, own, number, rows, amount, top, reach, lean):
    sequence = jax.random.permutation(own_key, amount)
    packed, ordinary = load_shares(amount, rows * top, reach, lean, True), load_shares(amount, rows * top, reach, lean, False)
    places = jnp.arange(amount)

    def named(tallies, offset_by):
        used = int((tallies > 0).sum())
        fixed = max(1, used // 4)
        passed = fixed + (places - fixed + offset_by * (used - fixed)) % max(1, amount - fixed)
        return jnp.zeros((amount,), jnp.int32).at[sequence[jnp.where(places < fixed, places, passed)]].set(jnp.asarray(tallies, jnp.int32))

    tallies = jnp.where(number % 4 == 0, named(packed, number // 4), named(ordinary, number - number // 4 - 1))
    mixed = jax.random.permutation(jax.random.fold_in(own, 3), amount)
    source_of, sink = mixed[0:amount // 2 * 2:2], mixed[1:amount // 2 * 2:2]
    margin = jnp.minimum(tallies[source_of] - 1, reach - tallies[sink]) // 2
    margin = jnp.where((source_of == sequence[0]) | (sink == sequence[0]) | (tallies[sink] == 0), 0, jnp.maximum(margin, 0))
    passed = jax.random.randint(jax.random.fold_in(own, 4), (amount // 2,), 0, 1 << 20) % (margin + 1)
    tallies = tallies.at[source_of].add(-passed).at[sink].add(passed)
    labels = jnp.searchsorted(jnp.cumsum(tallies), jnp.arange(rows * top), side="right").astype(jnp.int32)
    listing = labels.reshape(top, rows).T
    listing = listing[jax.random.permutation(jax.random.fold_in(own, 1), rows)]
    offset_by = jax.random.randint(jax.random.fold_in(own, 2), (rows, 1), 0, top)
    return jnp.take_along_axis(listing, (jnp.arange(top)[None, :] + offset_by) % top, axis=1)


def load_shares(amount, total, limit, lean, full):
    portions = [(1 << 20) // math.isqrt(standing ** lean) + 1 for standing in range(1, amount + 1)]
    largest = limit if full else min(limit, max(-(-total // amount), total * portions[0] // sum(portions)))
    least = 1 if total - largest >= amount - 1 else 0
    holding, spare = [largest] + [least] * (amount - 1), total - largest - least * (amount - 1)
    while spare > 0:
        free = [i for i in range(1, amount) if holding[i] < largest] or [i for i in range(1, amount) if holding[i] < limit]
        pool, left = sum([portions[i] for i in free]), spare
        for i in free:
            extra = min(limit - holding[i], max(1, left * portions[i] // pool), spare)
            holding[i] = holding[i] + extra
            spare = spare - extra
    return np.array(holding)


def normal_values(rng, extent, width, limit, cuts=(), kind=jnp.bfloat16):
    array = width * jax.random.normal(rng, extent, jnp.float32)
    if cuts:
        array = array * levels(rng, extent, cuts, -0.22, 0.18)
    return jnp.clip(array, -limit, limit).astype(kind)


def setup_inputs(seed: int = 0) -> dict:
    splits = jax.random.split(jax.random.key(seed), 18)
    tokens = normal_values(splits[0], (TOKENS, D), 1.0, 6.0, ((0, 32),))
    cotangent = normal_values(splits[1], (TOKENS, D), 1.0, 6.0, ((0, 32),))
    expert_index_keys = jax.random.split(jax.random.fold_in(splits[2], 1), TOKENS // MB_TOK)
    expert_index_turns = jax.random.permutation(jax.random.fold_in(splits[2], 3), TOKENS // MB_TOK)
    expert_index = jax.vmap(lambda own, number: assign_block(jax.random.fold_in(splits[2], 2), own, number, MB_TOK, E, 2, CAP, 2))(expert_index_keys, expert_index_turns).reshape((TOKENS, 2))
    qkv_weight = normal_values(splits[3], (D, 3 * D), D ** -0.5, 0.25, ((0, 8),), jnp.float32)
    out_weight = normal_values(splits[4], (D, D), (D // 32) ** -0.5, 1.5, ((0, 8),), jnp.float32)
    router_weight = normal_values(splits[5], (D, E), (2 * D) ** -0.5, 0.1875, ((0, 8),), jnp.float32)
    up_weight = normal_values(splits[6], (E, D, F), D ** -0.5, 0.25, ((1, 8),), jnp.float32)
    up_bias = normal_values(splits[7], (E, F), 0.1, 0.5, ((1, 8),), jnp.float32)
    down_weight = normal_values(splits[8], (E, F, D), (F // 16) ** -0.5, 0.5, ((1, 8),), jnp.float32)
    vectors = draw_vectors(jax.random.fold_in(splits[17], 71), 0)
    qkv_moments = draw_qkv_moments(jax.random.fold_in(splits[17], 71), 0)
    out_moments = draw_out_moments(jax.random.fold_in(splits[17], 71), 0)
    router_moments = draw_router_moments(jax.random.fold_in(splits[17], 71), 0)
    up_moments = draw_up_moments(jax.random.fold_in(splits[17], 71), 0)
    up_bias_moments = draw_up_bias_moments(jax.random.fold_in(splits[17], 71), 0)
    down_moments = draw_down_moments(jax.random.fold_in(splits[17], 71), 0)
    vector_moments = draw_vector_moments(jax.random.fold_in(splits[17], 71), 0)
    return {"tokens": tokens, "cotangent": cotangent, "expert_index": expert_index, "qkv_weight": qkv_weight, "out_weight": out_weight, "router_weight": router_weight, "up_weight": up_weight, "up_bias": up_bias, "down_weight": down_weight, "vectors": vectors, "qkv_moments": qkv_moments, "out_moments": out_moments, "router_moments": router_moments, "up_moments": up_moments, "up_bias_moments": up_bias_moments, "down_moments": down_moments, "vector_moments": vector_moments}


@jax.custom_vjp
def low(v):
    return lax.optimization_barrier(v.astype(jnp.bfloat16)).astype(jnp.float32)

@jax.custom_vjp
def low_back(v):
    return v

def low_keep(v):
    return (low(v), None)

def low_pass(kept, grad):
    return (grad,)

def back_keep(v):
    return (v, None)

def back_low(kept, grad):
    return (low(grad),)
low.defvjp(low_keep, low_pass)
low_back.defvjp(back_keep, back_low)
HIGH = lax.Precision.HIGHEST

def layer_norm(value, gain, shift):
    center = value - lax.optimization_barrier(jnp.mean(value, -1, keepdims=True))
    spread = lax.optimization_barrier(jnp.mean(center * center, -1, keepdims=True))
    return center * lax.rsqrt(spread + 1e-06) * gain + shift

def assign_places(route):
    chosen = jnp.concatenate([route[:, 0], route[:, 1]]).astype(jnp.int32)
    hits = (chosen[:, None] == jnp.arange(E, dtype=jnp.int32)[None, :]).astype(jnp.int32)
    before = (jnp.cumsum(hits, 0) - hits).astype(jnp.int32)
    slot = lax.optimization_barrier(jnp.sum(before * hits, 1)).astype(jnp.int32)
    return (chosen * CAP + slot).astype(jnp.int32)

def block_forward(weights, value, route):
    w_qkv, w_out, w_router, w_up, b_up, w_down, table = weights
    gain_one, shift_one, bias_q, bias_v, bias_o = (table[0], table[1], table[2], table[3], table[4])
    gain_two, shift_two, bias_down = (table[5], table[6], table[7:7 + E])
    rows = value.shape[0]
    scale = HEAD_DIM ** (-0.5)
    first = low(layer_norm(value, gain_one, shift_one))
    qkv_bias = jnp.concatenate([bias_q, jnp.zeros((D,), jnp.float32), bias_v])
    qkv = low(low_back(jnp.dot(first, w_qkv, precision=HIGH) + qkv_bias))
    query = qkv[:, :D].reshape(IMG_MB, S, HEADS, HEAD_DIM)
    key_part = qkv[:, D:2 * D].reshape(IMG_MB, S, HEADS, HEAD_DIM)
    val_part = qkv[:, 2 * D:].reshape(IMG_MB, S, HEADS, HEAD_DIM)
    scores = low_back(jnp.einsum('bqhd,bkhd->bhqk', query, key_part, precision=HIGH) * scale)
    probs_att = low(jax.nn.softmax(scores, -1))
    attended = jnp.einsum('bhqk,bkhd->bqhd', probs_att, val_part, precision=HIGH).reshape(rows, D)
    attended = low(low_back(attended))
    branch = low_back(jnp.dot(attended, w_out, precision=HIGH) + bias_o)
    resid = value + branch
    second = low(layer_norm(resid, gain_two, shift_two))
    logits = low_back(jnp.dot(second, w_router, precision=HIGH))
    probs = jax.nn.softmax(logits, -1)
    gate = jnp.take_along_axis(probs, route, 1)
    places = assign_places(route)
    table_in = jnp.zeros((E * CAP, D), jnp.float32).at[places].set(jnp.concatenate([second, second]))
    table_in = table_in.reshape(E, CAP, D)
    hidden_pre = low_back(jnp.einsum('ecd,edf->ecf', table_in, w_up, precision=HIGH) + b_up[:, None, :])
    hidden = low(jax.nn.gelu(hidden_pre, approximate=False))
    expert_out = low_back(jnp.einsum('ecf,efd->ecd', hidden, w_down, precision=HIGH) + bias_down[:, None, :])
    expert_out = expert_out.reshape(E * CAP, D)
    mixed = gate[:, 0:1] * expert_out[places[:rows]] + gate[:, 1:2] * expert_out[places[rows:]]
    return resid + mixed

def adamw(weight, moments, grad, rate):
    first = 0.5 * moments[0] + 0.5 * grad
    root = jnp.sqrt(0.5 * moments[1] * moments[1] + 0.5 * grad * grad)
    update = first / (root + 1e-08)
    return (weight - rate * (update + 0.1 * weight), jnp.stack([first, root]))

def reference(tokens, cotangent, expert_index, qkv_weight, out_weight, router_weight, up_weight, up_bias, down_weight, vectors, qkv_moments, out_moments, router_moments, up_moments, up_bias_moments, down_moments, vector_moments):
    blocks = TOKENS // MB_TOK
    values = tokens.astype(jnp.float32).reshape(blocks, MB_TOK, D)
    routes = expert_index.reshape(blocks, MB_TOK, 2).astype(jnp.int32)
    params = (qkv_weight, out_weight, router_weight, up_weight, up_bias, down_weight, vectors)

    def whole(weights, inputs):
        rounded = tuple((low(w) for w in weights))

        def one(pair):
            return block_forward(rounded, pair[0], pair[1])
        return lax.map(jax.checkpoint(one), (inputs, routes))
    outputs, pull = jax.vjp(whole, params, values)
    grads, input_grad = pull(cotangent.astype(jnp.float32).reshape(blocks, MB_TOK, D))
    rates = (2.0 * D ** (-0.5), 2.0 * (D // 32) ** (-0.5), 2.0 * (2 * D) ** (-0.5), 2.0 * D ** (-0.5), 0.2, 2.0 * (F // 16) ** (-0.5), 0.2)
    moments = (qkv_moments, out_moments, router_moments, up_moments, up_bias_moments, down_moments, vector_moments)
    news = []
    states = []
    for weight, state, grad, rate in zip(params, moments, grads, rates):
        new_weight, new_state = adamw(weight, state, grad, rate)
        news.append(new_weight)
        states.append(new_state)
    return (outputs.reshape(TOKENS, D).astype(jnp.bfloat16), input_grad.reshape(TOKENS, D), grads[0], grads[1], grads[2], grads[3], grads[4], grads[5], grads[6], news[0], news[1], news[2], news[3], news[4], news[5], news[6], states[0], states[1], states[2], states[3], states[4], states[5], states[6])
```

```python
import jax
import jax.numpy as jnp
import numpy as np
from jax import lax
from jax.sharding import Mesh
from jax.sharding import PartitionSpec as P

D = 512
HEADS = 8
HEAD_DIM = 64
F = 2048
E = 4
S = 197
MB_TOK = 394
CAP = 392
NV = 11
F32 = jnp.float32
BF16 = jnp.bfloat16
TOK = ("rx", "core", "group")


def layer_norm(value, gain, shift):
    center = value - jnp.mean(value, -1, keepdims=True)
    spread = jnp.mean(center * center, -1, keepdims=True)
    return center * lax.rsqrt(spread + 1e-06) * gain + shift


def gelu_exact(value):
    return jax.nn.gelu(value, approximate=False)


def split_heads(part):
    return part.reshape(-1, S, HEADS, HEAD_DIM)


def dot(a, b):
    return jnp.dot(a, b, preferred_element_type=F32)


def assign_places(route):
    chosen = jnp.concatenate([route[:, :, 0], route[:, :, 1]], 1)
    hits = (chosen[:, :, None] == jnp.arange(E, dtype=jnp.int32)).astype(jnp.int32)
    before = jnp.cumsum(hits, 1) - hits
    slot = jnp.sum(before * hits, 2)
    return chosen * CAP + slot


def hi_lo(v):
    hi = v.astype(BF16)
    lo = (v - hi.astype(F32)).astype(BF16)
    return jnp.concatenate([hi, lo], -1)


def pick_rows(onehot, table):
    both = jnp.einsum("mnr,mrd->mnd", onehot, hi_lo(table), preferred_element_type=F32)
    return both[..., :D] + both[..., D:]


def pack_dense(qkv_w, out_w, router_w, vectors, up_bias):
    rows = qkv_w.shape[0]
    ub = up_bias.reshape(E, rows, 4).transpose(1, 0, 2).reshape(rows, E * 4)
    return jnp.concatenate([qkv_w, out_w, router_w, vectors.T, ub], 1)


def unpack_dense(packed):
    rows = packed.shape[0]
    w_qkv = packed[:, : 3 * D]
    w_out = packed[:, 3 * D : 4 * D]
    w_router = packed[:, 4 * D : 4 * D + E]
    table = packed[:, 4 * D + E : 4 * D + E + NV].T
    ub = packed[:, 4 * D + E + NV :].reshape(rows, E, 4).transpose(1, 0, 2).reshape(E, rows * 4)
    return w_qkv, w_out, w_router, table, ub


def attention_fwd(w_qkv, w_out, table, value):
    rows = value.shape[0]
    scale = HEAD_DIM ** (-0.5)
    first = layer_norm(value, table[0], table[1]).astype(BF16)
    qkv_bias = jnp.concatenate([table[2], jnp.zeros((D,), F32), table[3]])
    qkv = (dot(first, w_qkv) + qkv_bias).astype(BF16)
    query, key_part, val_part = (
        split_heads(qkv[:, :D]),
        split_heads(qkv[:, D : 2 * D]),
        split_heads(qkv[:, 2 * D :]),
    )
    scores = jnp.einsum("bqhd,bkhd->bhqk", query, key_part, preferred_element_type=F32) * scale
    peak = jnp.max(scores, -1, keepdims=True)
    expo = jnp.exp(scores - peak)
    total = jnp.sum(expo, -1, keepdims=True)
    probs_att = (expo / total).astype(BF16)
    log_total = peak + jnp.log(total)
    attended = jnp.einsum("bhqk,bkhd->bqhd", probs_att, val_part, preferred_element_type=F32)
    attended = attended.reshape(rows, D).astype(BF16)
    resid = value + (dot(attended, w_out) + table[4])
    return first, qkv, log_total, attended, resid


def attention_bwd(w_qkv, w_out, table, value, first, qkv, log_total, attended, d_resid):
    rows = value.shape[0]
    scale = HEAD_DIM ** (-0.5)
    d_branch = d_resid.astype(BF16)
    g_bias_out = jnp.sum(d_branch.astype(F32), 0)
    g_out = lax.dot_general(attended, d_branch, (((0,), (0,)), ((), ())), preferred_element_type=F32)
    d_att = split_heads(
        lax.dot_general(d_branch, w_out, (((1,), (1,)), ((), ())), preferred_element_type=F32).astype(BF16)
    )
    query, key_part, val_part = (
        split_heads(qkv[:, :D]),
        split_heads(qkv[:, D : 2 * D]),
        split_heads(qkv[:, 2 * D :]),
    )
    scores = jnp.einsum("bqhd,bkhd->bhqk", query, key_part, preferred_element_type=F32) * scale
    probs_f = jnp.exp(scores - log_total)
    probs_att = probs_f.astype(BF16)
    d_val = jnp.einsum("bhqk,bqhd->bkhd", probs_att, d_att, preferred_element_type=F32)
    d_prob = jnp.einsum("bqhd,bkhd->bhqk", d_att, val_part, preferred_element_type=F32)
    d_score = (probs_f * (d_prob - jnp.sum(d_prob * probs_f, -1, keepdims=True))).astype(BF16)
    d_query = jnp.einsum("bhqk,bkhd->bqhd", d_score, key_part, preferred_element_type=F32) * scale
    d_key = jnp.einsum("bhqk,bqhd->bkhd", d_score, query, preferred_element_type=F32) * scale
    d_qkv = jnp.concatenate(
        [d_query.reshape(rows, D), d_key.reshape(rows, D), d_val.reshape(rows, D)], 1
    ).astype(BF16)
    d_qkv_f = d_qkv.astype(F32)
    g_bias_q = jnp.sum(d_qkv_f[:, :D], 0)
    g_bias_v = jnp.sum(d_qkv_f[:, 2 * D :], 0)
    g_qkv = lax.dot_general(first, d_qkv, (((0,), (0,)), ((), ())), preferred_element_type=F32)
    d_first = lax.dot_general(d_qkv, w_qkv, (((1,), (1,)), ((), ())), preferred_element_type=F32)
    first_pull = jax.vjp(layer_norm, value, table[0], table[1])[1]
    d_input, g_gain_one, g_shift_one = first_pull(d_first)
    return (g_qkv, g_out, g_bias_out, g_bias_q, g_bias_v, g_gain_one, g_shift_one), d_input


def adamw(weight, moments, grad, rate):
    first = 0.5 * moments[0] + 0.5 * grad
    root = jnp.sqrt(0.5 * moments[1] * moments[1] + 0.5 * grad * grad)
    update = first / (root + 1e-08)
    return (weight - rate * (update + 0.1 * weight), jnp.stack([first, root]))


def shards(
    tokens,
    cotangent,
    expert_index,
    qkv_weight,
    out_weight,
    router_weight,
    up_weight,
    up_bias,
    down_weight,
    vectors,
    qkv_moments,
    out_moments,
    router_moments,
    up_moments,
    up_bias_moments,
    down_moments,
    vector_moments,
):
    rows = tokens.shape[0]
    micro = rows // MB_TOK
    gs = qkv_weight.shape[0]
    core = lax.axis_index("core")

    dense = lax.all_gather(
        pack_dense(qkv_weight, out_weight, router_weight, vectors, up_bias).astype(BF16),
        "group",
        axis=0,
        tiled=True,
    )
    w_qkv, w_out, w_router, table_b, b_up_b = unpack_dense(dense)
    table = table_b.astype(F32)
    b_up = b_up_b.astype(F32)

    chunk_w = []
    for k in range(2):
        e = 2 * k + core
        up_piece = lax.dynamic_index_in_dim(up_weight, e, 0, keepdims=False)
        down_piece = lax.dynamic_index_in_dim(down_weight, e, 0, keepdims=False).reshape(gs, F)
        piece = jnp.stack([up_piece, down_piece]).astype(BF16)
        piece = lax.all_gather(piece, "group", axis=1, tiled=True)
        piece = lax.all_gather(piece, "core", axis=0, tiled=False)
        chunk_w.append((piece[:, 0], piece[:, 1].reshape(2, F, D)))

    value = tokens.astype(F32)
    d_out = cotangent.astype(F32)
    first, qkv, log_total, attended, resid = attention_fwd(w_qkv, w_out, table, value)
    second = layer_norm(resid, table[5], table[6]).astype(BF16)
    logits = dot(second, w_router)
    probs = jax.nn.softmax(logits, -1)
    picked = expert_index[:, :, None] == jnp.arange(E, dtype=jnp.int32)
    gate = jnp.sum(jnp.where(picked, probs[:, None, :], 0.0), -1)

    route = expert_index.reshape(micro, MB_TOK, 2)
    places = assign_places(route)
    onehot = (places[:, :, None] == jnp.arange(E * CAP, dtype=jnp.int32)).astype(BF16)
    second_m = second.reshape(micro, MB_TOK, D)
    pair = jnp.concatenate([second_m, second_m], 1)
    table_in = jnp.einsum("mnr,mnd->mrd", onehot, pair, preferred_element_type=F32).astype(BF16)
    table_in = table_in.reshape(micro, E, CAP, D).transpose(1, 0, 2, 3).reshape(E, micro * CAP, D)

    hidden_pre, hidden, expert_out = [], [], []
    for k in range(2):
        w_up, w_down = chunk_w[k]
        t_in = table_in[2 * k : 2 * k + 2]
        hp = jnp.einsum("ecd,edf->ecf", t_in, w_up, preferred_element_type=F32) + b_up[2 * k : 2 * k + 2, None, :]
        h = gelu_exact(hp).astype(BF16)
        y = jnp.einsum("ecf,efd->ecd", h, w_down, preferred_element_type=F32) + table[7 + 2 * k : 9 + 2 * k][:, None, :]
        hidden_pre.append(hp)
        hidden.append(h)
        expert_out.append(y)
    y_all = jnp.concatenate(expert_out, 0)
    y_m = y_all.reshape(E, micro, CAP, D).transpose(1, 0, 2, 3).reshape(micro, E * CAP, D)
    picked_rows = pick_rows(onehot, y_m)
    out_zero = picked_rows[:, :MB_TOK].reshape(rows, D)
    out_one = picked_rows[:, MB_TOK:].reshape(rows, D)
    result = resid + (gate[:, 0:1] * out_zero + gate[:, 1:2] * out_one)

    d_gate = jnp.stack([jnp.sum(d_out * out_zero, -1), jnp.sum(d_out * out_one, -1)], 1)
    d_out_m = d_out.reshape(micro, MB_TOK, D)
    gate_m = gate.reshape(micro, MB_TOK, 2)
    weighted = jnp.concatenate([gate_m[:, :, 0:1] * d_out_m, gate_m[:, :, 1:2] * d_out_m], 1).astype(BF16)
    d_expert = jnp.einsum("mnr,mnd->mrd", onehot, weighted, preferred_element_type=F32).astype(BF16)
    d_expert = d_expert.reshape(micro, E, CAP, D).transpose(1, 0, 2, 3).reshape(E, micro * CAP, D)
    g_bias_down = jnp.sum(d_expert.astype(F32), 1)

    d_tables = []
    expert_grads = []
    for k in range(2):
        w_up, w_down = chunk_w[k]
        dy = d_expert[2 * k : 2 * k + 2]
        g_down = jnp.einsum("ecf,ecd->efd", hidden[k], dy, preferred_element_type=F32)
        d_hidden = jnp.einsum("ecd,efd->ecf", dy, w_down, preferred_element_type=F32)
        gelu_pull = jax.vjp(gelu_exact, hidden_pre[k])[1]
        d_pre = gelu_pull(d_hidden)[0].astype(BF16)
        g_up_bias = jnp.sum(d_pre.astype(F32), 1)
        g_up = jnp.einsum("ecd,ecf->edf", table_in[2 * k : 2 * k + 2], d_pre, preferred_element_type=F32)
        d_tables.append(jnp.einsum("ecf,edf->ecd", d_pre, w_up, preferred_element_type=F32))
        expert_grads.append((g_up, g_down, g_up_bias))

    owned_experts = []
    for k in range(2):
        g_up, g_down, _ = expert_grads[k]
        packed = jnp.stack([g_up, g_down.reshape(2, D, F)], 1).astype(BF16)
        packed = lax.psum_scatter(packed, "core", scatter_dimension=0, tiled=True)
        packed = lax.psum_scatter(packed, "group", scatter_dimension=2, tiled=True)
        packed = lax.psum(packed, "rx")
        packed = lax.all_gather(packed, "core", axis=0, tiled=True)
        owned_experts.append(packed)

    d_table = jnp.concatenate(d_tables, 0)
    d_table_m = d_table.reshape(E, micro, CAP, D).transpose(1, 0, 2, 3).reshape(micro, E * CAP, D)
    onehot_sum = onehot[:, :MB_TOK] + onehot[:, MB_TOK:]
    d_picked = pick_rows(onehot_sum, d_table_m).reshape(rows, D)

    d_probs = jnp.sum(jnp.where(picked, d_gate[:, :, None], 0.0), 1)
    d_logit = (probs * (d_probs - jnp.sum(d_probs * probs, -1, keepdims=True))).astype(BF16)
    g_router = lax.dot_general(second, d_logit, (((0,), (0,)), ((), ())), preferred_element_type=F32)
    d_second = d_picked + lax.dot_general(d_logit, w_router, (((1,), (1,)), ((), ())), preferred_element_type=F32)
    norm_pull = jax.vjp(layer_norm, resid, table[5], table[6])[1]
    d_resid, g_gain_two, g_shift_two = norm_pull(d_second)
    d_resid = d_out + d_resid

    att_grads, d_input = attention_bwd(w_qkv, w_out, table, value, first, qkv, log_total, attended, d_resid)
    g_qkv, g_out, g_bias_out, g_bias_q, g_bias_v, g_gain_one, g_shift_one = att_grads
    input_grad = d_resid + d_input

    g_table = jnp.concatenate(
        [
            jnp.stack([g_gain_one, g_shift_one, g_bias_q, g_bias_v, g_bias_out, g_gain_two, g_shift_two]),
            g_bias_down,
        ],
        0,
    )
    g_up_bias_all = jnp.concatenate([expert_grads[0][2], expert_grads[1][2]], 0)
    dense_g = pack_dense(g_qkv, g_out, g_router, g_table, g_up_bias_all)
    dense_g = lax.psum_scatter(dense_g.astype(BF16), "group", scatter_dimension=0, tiled=True)
    dense_g = lax.psum(dense_g, ("rx", "core")).astype(F32)
    r_qkv, r_out, r_router, r_table, r_ub = unpack_dense(dense_g)
    r_up = jnp.concatenate([owned_experts[0][:, 0], owned_experts[1][:, 0]], 0).astype(F32)
    r_down = jnp.concatenate([owned_experts[0][:, 1], owned_experts[1][:, 1]], 0).astype(F32).reshape(E, gs * 4, D)

    reduced = (r_qkv, r_out, r_router, r_up, r_ub, r_down, r_table)
    rates = (
        2.0 * D ** (-0.5),
        2.0 * (D // 32) ** (-0.5),
        2.0 * (2 * D) ** (-0.5),
        2.0 * D ** (-0.5),
        0.2,
        2.0 * (F // 16) ** (-0.5),
        0.2,
    )
    params = (qkv_weight, out_weight, router_weight, up_weight, up_bias, down_weight, vectors)
    moments = (qkv_moments, out_moments, router_moments, up_moments, up_bias_moments, down_moments, vector_moments)
    news = []
    states = []
    for weight, state, grad, rate in zip(params, moments, reduced, rates):
        new_weight, new_state = adamw(weight, state, grad, rate)
        news.append(new_weight)
        states.append(new_state)
    return (result.astype(BF16), input_grad) + reduced + tuple(news) + tuple(states)


def solution(mesh):
    replica, group = mesh.shape["replica"], mesh.shape["group"]
    view = Mesh(np.asarray(mesh.devices).reshape(replica // 2, 2, group), ("rx", "core", "group"))
    in_specs = (
        P(TOK, None),
        P(TOK, None),
        P(TOK, None),
        P("group", None),
        P("group", None),
        P("group", None),
        P(None, "group", None),
        P(None, "group"),
        P(None, "group", None),
        P(None, "group"),
        P(None, "group", None),
        P(None, "group", None),
        P(None, "group", None),
        P(None, None, "group", None),
        P(None, None, "group"),
        P(None, None, "group", None),
        P(None, None, "group"),
    )
    out_specs = (
        P(TOK, None),
        P(TOK, None),
        P("group", None),
        P("group", None),
        P("group", None),
        P(None, "group", None),
        P(None, "group"),
        P(None, "group", None),
        P(None, "group"),
        P("group", None),
        P("group", None),
        P("group", None),
        P(None, "group", None),
        P(None, "group"),
        P(None, "group", None),
        P(None, "group"),
        P(None, "group", None),
        P(None, "group", None),
        P(None, "group", None),
        P(None, None, "group", None),
        P(None, None, "group"),
        P(None, None, "group", None),
        P(None, None, "group"),
    )
    return jax.shard_map(shards, mesh=view, in_specs=in_specs, out_specs=out_specs, check_vma=False)
```

```python
import functools

import jax
import jax.numpy as jnp
import numpy as np
from jax import lax
from jax.sharding import Mesh
from jax.sharding import PartitionSpec as P
from jax.experimental import pallas as pl
from jax.experimental.pallas import tpu as pltpu

D = 512
HEADS = 8
HEAD_DIM = 64
F = 2048
E = 4
S = 197
MB_TOK = 394
CAP = 392
NV = 11
DENSE_PAD = 2304
F32 = jnp.float32
BF16 = jnp.bfloat16
TOK = ("rx", "core", "group")


MESH_ID = pl.DeviceIdType.MESH


def ring_order(groups):
    if groups in (4, 8):
        zs = groups // 2

        def pos_of(g):
            y = g % 2
            z = g // 2
            return z + y * (2 * zs - 1 - 2 * z)

        def dev_at(p):
            p = p % groups
            yy = p // zs
            return 2 * (p + yy * (2 * zs - 1 - 2 * p)) + yy

        return pos_of, dev_at
    return (lambda g: g), (lambda p: p % groups)


def ring_rs_kernel(groups, n_in, *refs):
    ins = refs[:n_in]
    outs = refs[n_in : 2 * n_in]
    rbufs = refs[2 * n_in : 3 * n_in]
    sbufs = refs[3 * n_in : 4 * n_in]
    owns = refs[4 * n_in : 5 * n_in]
    send_sem, recv_sem, load_sem = refs[5 * n_in :]
    pos_of, dev_at = ring_order(groups)
    rx = lax.axis_index("rx")
    core = lax.axis_index("core")
    g = lax.axis_index("group")
    pos = pos_of(g)
    nbr = (dev_at(pos + 1), dev_at(pos + groups - 1))

    barrier = pltpu.get_barrier_semaphore()
    for n in nbr:
        pl.semaphore_signal(barrier, inc=1, device_id=(rx, core, n), device_id_type=MESH_ID)
    pl.semaphore_wait(barrier, 2)

    def block_dev(d, s):
        if d == 0:
            return dev_at(pos + 2 * groups - s - 1)
        return dev_at(pos + s + 1)

    def load(d, s, slot):
        b = block_dev(d, s)
        copies = []
        for i in range(n_in):
            rows = ins[i].shape[1] // groups
            half = ins[i].shape[2] // 2
            src = ins[i].at[:, pl.ds(pl.multiple_of(b * rows, rows), rows), pl.ds(d * half, half)]
            copies.append(pltpu.make_async_copy(src, owns[i].at[d, slot], load_sem.at[d, slot, i]))
        return copies

    def remote(d, s, i):
        return pltpu.make_async_remote_copy(
            src_ref=sbufs[i].at[d, s],
            dst_ref=rbufs[i].at[d, s],
            send_sem=send_sem.at[d, s, i],
            recv_sem=recv_sem.at[d, s, i],
            device_id=(rx, core, nbr[d]),
            device_id_type=MESH_ID,
        )

    for d in range(2):
        for c in load(d, 0, 0):
            c.start()
    sends = []
    for s in range(groups):
        slot = s % 2
        for d in range(2):
            for c in load(d, s, slot):
                c.wait()
            if s + 1 < groups:
                for c in load(d, s + 1, 1 - slot):
                    c.start()
            for i in range(n_in):
                if s > 0:
                    remote(d, s - 1, i).wait_recv()
                for a in range(ins[i].shape[0]):
                    mine = owns[i][d, slot, a].astype(F32)
                    if s > 0:
                        mine = mine + rbufs[i][d, s - 1, a].astype(F32)
                    if s < groups - 1:
                        sbufs[i][d, s, a] = mine.astype(sbufs[i].dtype)
                    else:
                        half = ins[i].shape[2] // 2
                        outs[i][a, :, pl.ds(d * half, half)] = mine.astype(outs[i].dtype)
                if s < groups - 1:
                    c = remote(d, s, i)
                    c.start()
                    sends.append(c)
    for c in sends:
        c.wait_send()


def ring_reduce_scatter(xs, groups, collective_id):
    n_in = len(xs)
    outs, rb, own = [], [], []
    flops = 0
    nbytes = 0
    for x in xs:
        a, total, c = x.shape
        rows = total // groups
        outs.append(jax.ShapeDtypeStruct((a, rows, c), x.dtype))
        rb.append(pltpu.VMEM((2, groups - 1, a, rows, c // 2), x.dtype))
        own.append(pltpu.VMEM((2, 2, a, rows, c // 2), x.dtype))
        flops += a * total * c
        nbytes += 3 * x.size * x.dtype.itemsize
    scratch = rb + rb + own + [
        pltpu.SemaphoreType.DMA((2, groups - 1, n_in)),
        pltpu.SemaphoreType.DMA((2, groups - 1, n_in)),
        pltpu.SemaphoreType.DMA((2, 2, n_in)),
    ]
    return pl.pallas_call(
        functools.partial(ring_rs_kernel, groups, n_in),
        out_shape=outs,
        in_specs=[pl.BlockSpec(memory_space=pl.ANY)] * n_in,
        out_specs=[pl.BlockSpec(memory_space=pltpu.VMEM)] * n_in,
        scratch_shapes=scratch,
        compiler_params=pltpu.CompilerParams(
            collective_id=collective_id, has_side_effects=True, vmem_limit_bytes=60 * 1024 * 1024
        ),
        cost_estimate=pl.CostEstimate(flops=flops, bytes_accessed=nbytes, transcendentals=0),
    )(*xs)


def layer_norm(value, gain, shift):
    center = value - jnp.mean(value, -1, keepdims=True)
    spread = jnp.mean(center * center, -1, keepdims=True)
    return center * lax.rsqrt(spread + 1e-06) * gain + shift


def gelu_exact(value):
    return jax.nn.gelu(value, approximate=False)


def split_heads(part):
    return part.reshape(-1, S, HEADS, HEAD_DIM)


def dot(a, b):
    return jnp.dot(a, b, preferred_element_type=F32)


def assign_places(route):
    chosen = jnp.concatenate([route[:, :, 0], route[:, :, 1]], 1)
    hits = (chosen[:, :, None] == jnp.arange(E, dtype=jnp.int32)).astype(jnp.int32)
    before = jnp.cumsum(hits, 1) - hits
    slot = jnp.sum(before * hits, 2)
    return chosen * CAP + slot


def hi_lo(v):
    hi = v.astype(BF16)
    lo = (v - hi.astype(F32)).astype(BF16)
    return jnp.concatenate([hi, lo], -1)


def pick_rows(onehot, table):
    both = jnp.einsum("mnr,mrd->mnd", onehot, hi_lo(table), preferred_element_type=F32)
    return both[..., :D] + both[..., D:]


def pack_dense(qkv_w, out_w, router_w, vectors, up_bias):
    rows = qkv_w.shape[0]
    ub = up_bias.reshape(E, rows, 4).transpose(1, 0, 2).reshape(rows, E * 4)
    return jnp.concatenate([qkv_w, out_w, router_w, vectors.T, ub], 1)


def unpack_dense(packed):
    rows = packed.shape[0]
    w_qkv = packed[:, : 3 * D]
    w_out = packed[:, 3 * D : 4 * D]
    w_router = packed[:, 4 * D : 4 * D + E]
    table = packed[:, 4 * D + E : 4 * D + E + NV].T
    ub = packed[:, 4 * D + E + NV :].reshape(rows, E, 4).transpose(1, 0, 2).reshape(E, rows * 4)
    return w_qkv, w_out, w_router, table, ub


def attention_fwd(w_qkv, w_out, table, value):
    rows = value.shape[0]
    scale = HEAD_DIM ** (-0.5)
    first = layer_norm(value, table[0], table[1]).astype(BF16)
    qkv_bias = jnp.concatenate([table[2], jnp.zeros((D,), F32), table[3]])
    qkv = (dot(first, w_qkv) + qkv_bias).astype(BF16)
    query, key_part, val_part = (
        split_heads(qkv[:, :D]),
        split_heads(qkv[:, D : 2 * D]),
        split_heads(qkv[:, 2 * D :]),
    )
    scores = jnp.einsum("bqhd,bkhd->bhqk", query, key_part, preferred_element_type=F32) * scale
    peak = jnp.max(scores, -1, keepdims=True)
    expo = jnp.exp(scores - peak)
    total = jnp.sum(expo, -1, keepdims=True)
    probs_att = (expo / total).astype(BF16)
    log_total = peak + jnp.log(total)
    attended = jnp.einsum("bhqk,bkhd->bqhd", probs_att, val_part, preferred_element_type=F32)
    attended = attended.reshape(rows, D).astype(BF16)
    resid = value + (dot(attended, w_out) + table[4])
    return first, qkv, log_total, attended, resid


def attention_bwd(w_qkv, w_out, table, value, first, qkv, log_total, attended, d_resid):
    rows = value.shape[0]
    scale = HEAD_DIM ** (-0.5)
    d_branch = d_resid.astype(BF16)
    g_bias_out = jnp.sum(d_branch.astype(F32), 0)
    g_out = lax.dot_general(attended, d_branch, (((0,), (0,)), ((), ())), preferred_element_type=F32)
    d_att = split_heads(
        lax.dot_general(d_branch, w_out, (((1,), (1,)), ((), ())), preferred_element_type=F32).astype(BF16)
    )
    query, key_part, val_part = (
        split_heads(qkv[:, :D]),
        split_heads(qkv[:, D : 2 * D]),
        split_heads(qkv[:, 2 * D :]),
    )
    scores = jnp.einsum("bqhd,bkhd->bhqk", query, key_part, preferred_element_type=F32) * scale
    probs_f = jnp.exp(scores - log_total)
    probs_att = probs_f.astype(BF16)
    d_val = jnp.einsum("bhqk,bqhd->bkhd", probs_att, d_att, preferred_element_type=F32)
    d_prob = jnp.einsum("bqhd,bkhd->bhqk", d_att, val_part, preferred_element_type=F32)
    d_score = (probs_f * (d_prob - jnp.sum(d_prob * probs_f, -1, keepdims=True))).astype(BF16)
    d_query = jnp.einsum("bhqk,bkhd->bqhd", d_score, key_part, preferred_element_type=F32) * scale
    d_key = jnp.einsum("bhqk,bqhd->bkhd", d_score, query, preferred_element_type=F32) * scale
    d_qkv = jnp.concatenate(
        [d_query.reshape(rows, D), d_key.reshape(rows, D), d_val.reshape(rows, D)], 1
    ).astype(BF16)
    d_qkv_f = d_qkv.astype(F32)
    g_bias_q = jnp.sum(d_qkv_f[:, :D], 0)
    g_bias_v = jnp.sum(d_qkv_f[:, 2 * D :], 0)
    g_qkv = lax.dot_general(first, d_qkv, (((0,), (0,)), ((), ())), preferred_element_type=F32)
    d_first = lax.dot_general(d_qkv, w_qkv, (((1,), (1,)), ((), ())), preferred_element_type=F32)
    first_pull = jax.vjp(layer_norm, value, table[0], table[1])[1]
    d_input, g_gain_one, g_shift_one = first_pull(d_first)
    return (g_qkv, g_out, g_bias_out, g_bias_q, g_bias_v, g_gain_one, g_shift_one), d_input


def adamw(weight, moments, grad, rate):
    first = 0.5 * moments[0] + 0.5 * grad
    root = jnp.sqrt(0.5 * moments[1] * moments[1] + 0.5 * grad * grad)
    update = first / (root + 1e-08)
    return (weight - rate * (update + 0.1 * weight), jnp.stack([first, root]))


def shards(
    tokens,
    cotangent,
    expert_index,
    qkv_weight,
    out_weight,
    router_weight,
    up_weight,
    up_bias,
    down_weight,
    vectors,
    qkv_moments,
    out_moments,
    router_moments,
    up_moments,
    up_bias_moments,
    down_moments,
    vector_moments,
):
    rows = tokens.shape[0]
    micro = rows // MB_TOK
    gs = qkv_weight.shape[0]
    group_size = D // gs
    core = lax.axis_index("core")

    dense = lax.all_gather(
        pack_dense(qkv_weight, out_weight, router_weight, vectors, up_bias).astype(BF16),
        "group",
        axis=0,
        tiled=True,
    )
    w_qkv, w_out, w_router, table_b, b_up_b = unpack_dense(dense)
    table = table_b.astype(F32)
    b_up = b_up_b.astype(F32)

    chunk_w = []
    for k in range(2):
        e = 2 * k + core
        up_piece = lax.dynamic_index_in_dim(up_weight, e, 0, keepdims=False)
        down_piece = lax.dynamic_index_in_dim(down_weight, e, 0, keepdims=False).reshape(gs, F)
        piece = jnp.stack([up_piece, down_piece]).astype(BF16)
        piece = lax.all_gather(piece, "group", axis=1, tiled=True)
        piece = lax.all_gather(piece, "core", axis=0, tiled=False)
        chunk_w.append((piece[:, 0], piece[:, 1].reshape(2, F, D)))

    value = tokens.astype(F32)
    d_out = cotangent.astype(F32)
    first, qkv, log_total, attended, resid = attention_fwd(w_qkv, w_out, table, value)
    second = layer_norm(resid, table[5], table[6]).astype(BF16)
    logits = dot(second, w_router)
    probs = jax.nn.softmax(logits, -1)
    picked = expert_index[:, :, None] == jnp.arange(E, dtype=jnp.int32)
    gate = jnp.sum(jnp.where(picked, probs[:, None, :], 0.0), -1)

    route = expert_index.reshape(micro, MB_TOK, 2)
    places = assign_places(route)
    onehot = (places[:, :, None] == jnp.arange(E * CAP, dtype=jnp.int32)).astype(BF16)
    second_m = second.reshape(micro, MB_TOK, D)
    pair = jnp.concatenate([second_m, second_m], 1)
    table_in = jnp.einsum("mnr,mnd->mrd", onehot, pair, preferred_element_type=F32).astype(BF16)
    table_in = table_in.reshape(micro, E, CAP, D).transpose(1, 0, 2, 3).reshape(E, micro * CAP, D)

    hidden_pre, hidden, expert_out = [], [], []
    for k in range(2):
        w_up, w_down = chunk_w[k]
        t_in = table_in[2 * k : 2 * k + 2]
        hp = jnp.einsum("ecd,edf->ecf", t_in, w_up, preferred_element_type=F32) + b_up[2 * k : 2 * k + 2, None, :]
        h = gelu_exact(hp).astype(BF16)
        y = jnp.einsum("ecf,efd->ecd", h, w_down, preferred_element_type=F32) + table[7 + 2 * k : 9 + 2 * k][:, None, :]
        hidden_pre.append(hp)
        hidden.append(h)
        expert_out.append(y)
    y_all = jnp.concatenate(expert_out, 0)
    y_m = y_all.reshape(E, micro, CAP, D).transpose(1, 0, 2, 3).reshape(micro, E * CAP, D)
    picked_rows = pick_rows(onehot, y_m)
    out_zero = picked_rows[:, :MB_TOK].reshape(rows, D)
    out_one = picked_rows[:, MB_TOK:].reshape(rows, D)
    result = resid + (gate[:, 0:1] * out_zero + gate[:, 1:2] * out_one)

    d_gate = jnp.stack([jnp.sum(d_out * out_zero, -1), jnp.sum(d_out * out_one, -1)], 1)
    d_out_m = d_out.reshape(micro, MB_TOK, D)
    gate_m = gate.reshape(micro, MB_TOK, 2)
    weighted = jnp.concatenate([gate_m[:, :, 0:1] * d_out_m, gate_m[:, :, 1:2] * d_out_m], 1).astype(BF16)
    d_expert = jnp.einsum("mnr,mnd->mrd", onehot, weighted, preferred_element_type=F32).astype(BF16)
    d_expert = d_expert.reshape(micro, E, CAP, D).transpose(1, 0, 2, 3).reshape(E, micro * CAP, D)
    g_bias_down = jnp.sum(d_expert.astype(F32), 1)

    d_tables = []
    expert_grads = []
    for k in range(2):
        w_up, w_down = chunk_w[k]
        dy = d_expert[2 * k : 2 * k + 2]
        g_down = jnp.einsum("ecf,ecd->efd", hidden[k], dy, preferred_element_type=F32)
        d_hidden = jnp.einsum("ecd,efd->ecf", dy, w_down, preferred_element_type=F32)
        gelu_pull = jax.vjp(gelu_exact, hidden_pre[k])[1]
        d_pre = gelu_pull(d_hidden)[0].astype(BF16)
        g_up_bias = jnp.sum(d_pre.astype(F32), 1)
        g_up = jnp.einsum("ecd,ecf->edf", table_in[2 * k : 2 * k + 2], d_pre, preferred_element_type=F32)
        d_tables.append(jnp.einsum("ecf,edf->ecd", d_pre, w_up, preferred_element_type=F32))
        expert_grads.append((g_up, g_down, g_up_bias))

    d_table = jnp.concatenate(d_tables, 0)
    d_table_m = d_table.reshape(E, micro, CAP, D).transpose(1, 0, 2, 3).reshape(micro, E * CAP, D)
    onehot_sum = onehot[:, :MB_TOK] + onehot[:, MB_TOK:]
    d_picked = pick_rows(onehot_sum, d_table_m).reshape(rows, D)

    d_probs = jnp.sum(jnp.where(picked, d_gate[:, :, None], 0.0), 1)
    d_logit = (probs * (d_probs - jnp.sum(d_probs * probs, -1, keepdims=True))).astype(BF16)
    g_router = lax.dot_general(second, d_logit, (((0,), (0,)), ((), ())), preferred_element_type=F32)
    d_second = d_picked + lax.dot_general(d_logit, w_router, (((1,), (1,)), ((), ())), preferred_element_type=F32)
    norm_pull = jax.vjp(layer_norm, resid, table[5], table[6])[1]
    d_resid, g_gain_two, g_shift_two = norm_pull(d_second)
    d_resid = d_out + d_resid

    att_grads, d_input = attention_bwd(w_qkv, w_out, table, value, first, qkv, log_total, attended, d_resid)
    g_qkv, g_out, g_bias_out, g_bias_q, g_bias_v, g_gain_one, g_shift_one = att_grads
    input_grad = d_resid + d_input

    g_table = jnp.concatenate(
        [
            jnp.stack([g_gain_one, g_shift_one, g_bias_q, g_bias_v, g_bias_out, g_gain_two, g_shift_two]),
            g_bias_down,
        ],
        0,
    )
    g_up_bias_all = jnp.concatenate([expert_grads[0][2], expert_grads[1][2]], 0)
    mine_list, send_list = [], []
    for k in range(2):
        g_up, g_down, _ = expert_grads[k]
        both = jnp.stack([g_up, g_down.reshape(2, D, F)], 1)
        mine_list.append(lax.dynamic_index_in_dim(both, core, 0, keepdims=False))
        send_list.append(lax.dynamic_index_in_dim(both, 1 - core, 0, keepdims=False))
    sent = jnp.stack(send_list).astype(BF16)
    got = lax.ppermute(sent, "core", [(0, 1), (1, 0)])
    expert_sum = (jnp.stack(mine_list) + got.astype(F32)).astype(BF16).reshape(4, D, F)
    dense_g = pack_dense(g_qkv, g_out, g_router, g_table, g_up_bias_all)
    width = dense_g.shape[1]
    dense_g = jnp.pad(dense_g, ((0, 0), (0, DENSE_PAD - width))).astype(BF16)[None]
    e_out, d_out_g = ring_reduce_scatter([expert_sum, dense_g], group_size, 0)
    e_red = lax.psum(e_out, "rx").reshape(2, 2, gs, F)
    d_red = lax.psum(d_out_g[0, :, :width], ("rx", "core")).astype(F32)
    r_qkv, r_out, r_router, r_table, r_ub = unpack_dense(d_red)
    e_all = lax.all_gather(e_red, "core", axis=0, tiled=False).transpose(1, 0, 2, 3, 4).reshape(E, 2, gs, F)
    r_up = e_all[:, 0].astype(F32)
    r_down = e_all[:, 1].astype(F32).reshape(E, gs * 4, D)

    reduced = (r_qkv, r_out, r_router, r_up, r_ub, r_down, r_table)
    rates = (
        2.0 * D ** (-0.5),
        2.0 * (D // 32) ** (-0.5),
        2.0 * (2 * D) ** (-0.5),
        2.0 * D ** (-0.5),
        0.2,
        2.0 * (F // 16) ** (-0.5),
        0.2,
    )
    params = (qkv_weight, out_weight, router_weight, up_weight, up_bias, down_weight, vectors)
    moments = (qkv_moments, out_moments, router_moments, up_moments, up_bias_moments, down_moments, vector_moments)
    news = []
    states = []
    for weight, state, grad, rate in zip(params, moments, reduced, rates):
        new_weight, new_state = adamw(weight, state, grad, rate)
        news.append(new_weight)
        states.append(new_state)
    return (result.astype(BF16), input_grad) + reduced + tuple(news) + tuple(states)


def solution(mesh):
    replica, group = mesh.shape["replica"], mesh.shape["group"]
    view = Mesh(np.asarray(mesh.devices).reshape(replica // 2, 2, group), ("rx", "core", "group"))
    in_specs = (
        P(TOK, None),
        P(TOK, None),
        P(TOK, None),
        P("group", None),
        P("group", None),
        P("group", None),
        P(None, "group", None),
        P(None, "group"),
        P(None, "group", None),
        P(None, "group"),
        P(None, "group", None),
        P(None, "group", None),
        P(None, "group", None),
        P(None, None, "group", None),
        P(None, None, "group"),
        P(None, None, "group", None),
        P(None, None, "group"),
    )
    out_specs = (
        P(TOK, None),
        P(TOK, None),
        P("group", None),
        P("group", None),
        P("group", None),
        P(None, "group", None),
        P(None, "group"),
        P(None, "group", None),
        P(None, "group"),
        P("group", None),
        P("group", None),
        P("group", None),
        P(None, "group", None),
        P(None, "group"),
        P(None, "group", None),
        P(None, "group"),
        P(None, "group", None),
        P(None, "group", None),
        P(None, "group", None),
        P(None, None, "group", None),
        P(None, None, "group"),
        P(None, None, "group", None),
        P(None, None, "group"),
    )
    return jax.shard_map(shards, mesh=view, in_specs=in_specs, out_specs=out_specs, check_vma=False)
```

```python
import functools

import jax
import jax.numpy as jnp
import numpy as np
from jax import lax
from jax.sharding import Mesh
from jax.sharding import PartitionSpec as P
from jax.experimental import pallas as pl
from jax.experimental.pallas import tpu as pltpu

D = 512
HEADS = 8
HEAD_DIM = 64
F = 2048
E = 4
S = 197
MB_TOK = 394
CAP = 392
NV = 11
DENSE_AG = 2560
DENSE_PAD = 2304
F32 = jnp.float32
BF16 = jnp.bfloat16
TOK = ("rx", "core", "group")


MESH_ID = pl.DeviceIdType.MESH


def ring_order(groups):
    if groups in (4, 8):
        zs = groups // 2

        def pos_of(g):
            y = g % 2
            z = g // 2
            return z + y * (2 * zs - 1 - 2 * z)

        def dev_at(p):
            p = p % groups
            yy = p // zs
            return 2 * (p + yy * (2 * zs - 1 - 2 * p)) + yy

        return pos_of, dev_at
    return (lambda g: g), (lambda p: p % groups)


def ring_rs_kernel(groups, n_in, *refs):
    ins = refs[:n_in]
    outs = refs[n_in : 2 * n_in]
    rbufs = refs[2 * n_in : 3 * n_in]
    sbufs = refs[3 * n_in : 4 * n_in]
    owns = refs[4 * n_in : 5 * n_in]
    send_sem, recv_sem, load_sem = refs[5 * n_in :]
    pos_of, dev_at = ring_order(groups)
    rx = lax.axis_index("rx")
    core = lax.axis_index("core")
    g = lax.axis_index("group")
    pos = pos_of(g)
    nbr = (dev_at(pos + 1), dev_at(pos + groups - 1))

    barrier = pltpu.get_barrier_semaphore()
    for n in nbr:
        pl.semaphore_signal(barrier, inc=1, device_id=(rx, core, n), device_id_type=MESH_ID)
    pl.semaphore_wait(barrier, 2)

    def block_dev(d, s):
        if d == 0:
            return dev_at(pos + 2 * groups - s - 1)
        return dev_at(pos + s + 1)

    def load(d, s, slot):
        b = block_dev(d, s)
        copies = []
        for i in range(n_in):
            rows = ins[i].shape[1] // groups
            half = ins[i].shape[2] // 2
            src = ins[i].at[:, pl.ds(pl.multiple_of(b * rows, rows), rows), pl.ds(d * half, half)]
            copies.append(pltpu.make_async_copy(src, owns[i].at[d, slot], load_sem.at[d, slot, i]))
        return copies

    def remote(d, s, i):
        return pltpu.make_async_remote_copy(
            src_ref=sbufs[i].at[d, s],
            dst_ref=rbufs[i].at[d, s],
            send_sem=send_sem.at[d, s, i],
            recv_sem=recv_sem.at[d, s, i],
            device_id=(rx, core, nbr[d]),
            device_id_type=MESH_ID,
        )

    for d in range(2):
        for c in load(d, 0, 0):
            c.start()
    sends = []
    for s in range(groups):
        slot = s % 2
        for d in range(2):
            for c in load(d, s, slot):
                c.wait()
            if s + 1 < groups:
                for c in load(d, s + 1, 1 - slot):
                    c.start()
            for i in range(n_in):
                if s > 0:
                    remote(d, s - 1, i).wait_recv()
                for a in range(ins[i].shape[0]):
                    mine = owns[i][d, slot, a].astype(F32)
                    if s > 0:
                        mine = mine + rbufs[i][d, s - 1, a].astype(F32)
                    if s < groups - 1:
                        sbufs[i][d, s, a] = mine.astype(sbufs[i].dtype)
                    else:
                        half = ins[i].shape[2] // 2
                        outs[i][a, :, pl.ds(d * half, half)] = mine.astype(outs[i].dtype)
                if s < groups - 1:
                    c = remote(d, s, i)
                    c.start()
                    sends.append(c)
    for c in sends:
        c.wait_send()


def ring_reduce_scatter(xs, groups, collective_id):
    n_in = len(xs)
    outs, rb, own = [], [], []
    flops = 0
    nbytes = 0
    for x in xs:
        a, total, c = x.shape
        rows = total // groups
        outs.append(jax.ShapeDtypeStruct((a, rows, c), x.dtype))
        rb.append(pltpu.VMEM((2, groups - 1, a, rows, c // 2), x.dtype))
        own.append(pltpu.VMEM((2, 2, a, rows, c // 2), x.dtype))
        flops += a * total * c
        nbytes += 3 * x.size * x.dtype.itemsize
    scratch = rb + rb + own + [
        pltpu.SemaphoreType.DMA((2, groups - 1, n_in)),
        pltpu.SemaphoreType.DMA((2, groups - 1, n_in)),
        pltpu.SemaphoreType.DMA((2, 2, n_in)),
    ]
    return pl.pallas_call(
        functools.partial(ring_rs_kernel, groups, n_in),
        out_shape=outs,
        in_specs=[pl.BlockSpec(memory_space=pl.ANY)] * n_in,
        out_specs=[pl.BlockSpec(memory_space=pltpu.VMEM)] * n_in,
        scratch_shapes=scratch,
        compiler_params=pltpu.CompilerParams(
            collective_id=collective_id, has_side_effects=True, vmem_limit_bytes=60 * 1024 * 1024
        ),
        cost_estimate=pl.CostEstimate(flops=flops, bytes_accessed=nbytes, transcendentals=0),
    )(*xs)


def ring_ag_kernel(groups, *refs):
    in_up, in_down, in_dense, out_up, out_down, out_dense = refs[:6]
    ring_send, ring_recv, part_send, part_recv, local_sem = refs[6:]
    pos_of, dev_at = ring_order(groups)
    rx = lax.axis_index("rx")
    core = lax.axis_index("core")
    g = lax.axis_index("group")
    other = 1 - core
    pos = pos_of(g)
    nbr = (dev_at(pos + 1), dev_at(pos + groups - 1))
    gs = in_up.shape[1]
    fs = in_down.shape[1]
    width = in_dense.shape[1] // 2

    barrier = pltpu.get_barrier_semaphore()
    for n in nbr:
        pl.semaphore_signal(barrier, inc=1, device_id=(rx, core, n), device_id_type=MESH_ID)
    pl.semaphore_signal(barrier, inc=1, device_id=(rx, other, g), device_id_type=MESH_ID)
    pl.semaphore_wait(barrier, 3)

    def items(owner):
        found = []
        for k in range(2):
            e = 2 * k + owner
            found.append((in_up.at[e], lambda b, e=e: out_up.at[e, pl.ds(pl.multiple_of(b * gs, gs), gs)], F // 2))
            found.append((in_down.at[e], lambda b, e=e: out_down.at[e, pl.ds(pl.multiple_of(b * fs, fs), fs)], D // 2))
        dense_in = in_dense.at[:, pl.ds(owner * width, width)]
        found.append(
            (dense_in, lambda b: out_dense.at[pl.ds(pl.multiple_of(b * gs, gs), gs), pl.ds(owner * width, width)], width // 2)
        )
        return found

    mine = items(core)
    theirs = items(other)
    n_items = len(mine)

    locals_ = [pltpu.make_async_copy(in_up.at[e], out_up.at[e, pl.ds(pl.multiple_of(g * gs, gs), gs)], local_sem.at[e]) for e in range(E)]
    locals_ += [
        pltpu.make_async_copy(in_down.at[e], out_down.at[e, pl.ds(pl.multiple_of(g * fs, fs), fs)], local_sem.at[E + e])
        for e in range(E)
    ]
    locals_.append(pltpu.make_async_copy(in_dense, out_dense.at[pl.ds(pl.multiple_of(g * gs, gs), gs)], local_sem.at[2 * E]))
    for c in locals_:
        c.start()

    def block_at(d, s):
        if d == 0:
            return dev_at(pos + 2 * groups - 1 - s)
        return dev_at(pos + 1 + s)

    def ring_copy(d, s, j, src_block):
        src_in, dst_of, half = mine[j]
        cols = pl.ds(d * half, half)
        if src_block is None:
            src = src_in.at[:, cols]
            dst = dst_of(g).at[:, cols]
        else:
            src = dst_of(src_block).at[:, cols]
            dst = src
        return pltpu.make_async_remote_copy(
            src_ref=src, dst_ref=dst, send_sem=ring_send.at[d, s, j], recv_sem=ring_recv.at[d, s, j],
            device_id=(rx, core, nbr[d]), device_id_type=MESH_ID,
        )

    def part_copy(d, s, j, table, block):
        _, dst_of, half = table[j]
        view = dst_of(block).at[:, pl.ds(d * half, half)]
        return pltpu.make_async_remote_copy(
            src_ref=view, dst_ref=view, send_sem=part_send.at[d, s, j], recv_sem=part_recv.at[d, s, j],
            device_id=(rx, other, g), device_id_type=MESH_ID,
        )

    sends = []
    for d in range(2):
        for j in range(n_items):
            c = ring_copy(d, 0, j, None)
            c.start()
            sends.append(c)
    for s in range(groups - 1):
        for d in range(2):
            b = block_at(d, s)
            for j in range(n_items):
                pltpu.make_async_remote_copy(
                    src_ref=mine[j][1](b).at[:, pl.ds(d * mine[j][2], mine[j][2])],
                    dst_ref=mine[j][1](b).at[:, pl.ds(d * mine[j][2], mine[j][2])],
                    send_sem=ring_send.at[d, s, j], recv_sem=ring_recv.at[d, s, j],
                    device_id=(rx, core, nbr[d]), device_id_type=MESH_ID,
                ).wait_recv()
                if s + 1 < groups - 1:
                    c = ring_copy(d, s + 1, j, b)
                    c.start()
                    sends.append(c)
                c = part_copy(d, s, j, mine, b)
                c.start()
                sends.append(c)
    for s in range(groups - 1):
        for d in range(2):
            b = block_at(d, s)
            for j in range(n_items):
                part_copy(d, s, j, theirs, b).wait_recv()
    for c in sends:
        c.wait_send()
    for c in locals_:
        c.wait()


def ring_all_gather(up_b, down_b, dense_b, groups, collective_id):
    n_items = 5
    gs = up_b.shape[1]
    shapes = [
        jax.ShapeDtypeStruct((E, gs * groups, F), BF16),
        jax.ShapeDtypeStruct((E, down_b.shape[1] * groups, D), BF16),
        jax.ShapeDtypeStruct((gs * groups, dense_b.shape[1]), BF16),
    ]
    nbytes = sum(int(np.prod(s.shape)) * 2 for s in shapes)
    return pl.pallas_call(
        functools.partial(ring_ag_kernel, groups),
        out_shape=shapes,
        in_specs=[pl.BlockSpec(memory_space=pl.ANY)] * 3,
        out_specs=[pl.BlockSpec(memory_space=pl.ANY)] * 3,
        scratch_shapes=[
            pltpu.SemaphoreType.DMA((2, groups - 1, n_items)),
            pltpu.SemaphoreType.DMA((2, groups - 1, n_items)),
            pltpu.SemaphoreType.DMA((2, groups - 1, n_items)),
            pltpu.SemaphoreType.DMA((2, groups - 1, n_items)),
            pltpu.SemaphoreType.DMA((2 * E + 1,)),
        ],
        compiler_params=pltpu.CompilerParams(collective_id=collective_id, has_side_effects=True),
        cost_estimate=pl.CostEstimate(flops=0, bytes_accessed=nbytes, transcendentals=0),
    )(up_b, down_b, dense_b)


def layer_norm(value, gain, shift):
    center = value - jnp.mean(value, -1, keepdims=True)
    spread = jnp.mean(center * center, -1, keepdims=True)
    return center * lax.rsqrt(spread + 1e-06) * gain + shift


def gelu_exact(value):
    return jax.nn.gelu(value, approximate=False)


def split_heads(part):
    return part.reshape(-1, S, HEADS, HEAD_DIM)


def dot(a, b):
    return jnp.dot(a, b, preferred_element_type=F32)


def assign_places(route):
    chosen = jnp.concatenate([route[:, :, 0], route[:, :, 1]], 1)
    hits = (chosen[:, :, None] == jnp.arange(E, dtype=jnp.int32)).astype(jnp.int32)
    before = jnp.cumsum(hits, 1) - hits
    slot = jnp.sum(before * hits, 2)
    return chosen * CAP + slot


def hi_lo(v):
    hi = v.astype(BF16)
    lo = (v - hi.astype(F32)).astype(BF16)
    return jnp.concatenate([hi, lo], -1)


def pick_rows(onehot, table):
    both = jnp.einsum("mnr,mrd->mnd", onehot, hi_lo(table), preferred_element_type=F32)
    return both[..., :D] + both[..., D:]


def pack_dense(qkv_w, out_w, router_w, vectors, up_bias):
    rows = qkv_w.shape[0]
    ub = up_bias.reshape(E, rows, 4).transpose(1, 0, 2).reshape(rows, E * 4)
    return jnp.concatenate([qkv_w, out_w, router_w, vectors.T, ub], 1)


def unpack_dense(packed):
    rows = packed.shape[0]
    w_qkv = packed[:, : 3 * D]
    w_out = packed[:, 3 * D : 4 * D]
    w_router = packed[:, 4 * D : 4 * D + E]
    table = packed[:, 4 * D + E : 4 * D + E + NV].T
    ub = packed[:, 4 * D + E + NV :].reshape(rows, E, 4).transpose(1, 0, 2).reshape(E, rows * 4)
    return w_qkv, w_out, w_router, table, ub


def attention_fwd(w_qkv, w_out, table, value):
    rows = value.shape[0]
    scale = HEAD_DIM ** (-0.5)
    first = layer_norm(value, table[0], table[1]).astype(BF16)
    qkv_bias = jnp.concatenate([table[2], jnp.zeros((D,), F32), table[3]])
    qkv = (dot(first, w_qkv) + qkv_bias).astype(BF16)
    query, key_part, val_part = (
        split_heads(qkv[:, :D]),
        split_heads(qkv[:, D : 2 * D]),
        split_heads(qkv[:, 2 * D :]),
    )
    scores = jnp.einsum("bqhd,bkhd->bhqk", query, key_part, preferred_element_type=F32) * scale
    peak = jnp.max(scores, -1, keepdims=True)
    expo = jnp.exp(scores - peak)
    total = jnp.sum(expo, -1, keepdims=True)
    probs_att = (expo / total).astype(BF16)
    log_total = peak + jnp.log(total)
    attended = jnp.einsum("bhqk,bkhd->bqhd", probs_att, val_part, preferred_element_type=F32)
    attended = attended.reshape(rows, D).astype(BF16)
    resid = value + (dot(attended, w_out) + table[4])
    return first, qkv, log_total, attended, resid


def attention_bwd(w_qkv, w_out, table, value, first, qkv, log_total, attended, d_resid):
    rows = value.shape[0]
    scale = HEAD_DIM ** (-0.5)
    d_branch = d_resid.astype(BF16)
    g_bias_out = jnp.sum(d_branch.astype(F32), 0)
    g_out = lax.dot_general(attended, d_branch, (((0,), (0,)), ((), ())), preferred_element_type=F32)
    d_att = split_heads(
        lax.dot_general(d_branch, w_out, (((1,), (1,)), ((), ())), preferred_element_type=F32).astype(BF16)
    )
    query, key_part, val_part = (
        split_heads(qkv[:, :D]),
        split_heads(qkv[:, D : 2 * D]),
        split_heads(qkv[:, 2 * D :]),
    )
    scores = jnp.einsum("bqhd,bkhd->bhqk", query, key_part, preferred_element_type=F32) * scale
    probs_f = jnp.exp(scores - log_total)
    probs_att = probs_f.astype(BF16)
    d_val = jnp.einsum("bhqk,bqhd->bkhd", probs_att, d_att, preferred_element_type=F32)
    d_prob = jnp.einsum("bqhd,bkhd->bhqk", d_att, val_part, preferred_element_type=F32)
    d_score = (probs_f * (d_prob - jnp.sum(d_prob * probs_f, -1, keepdims=True))).astype(BF16)
    d_query = jnp.einsum("bhqk,bkhd->bqhd", d_score, key_part, preferred_element_type=F32) * scale
    d_key = jnp.einsum("bhqk,bqhd->bkhd", d_score, query, preferred_element_type=F32) * scale
    d_qkv = jnp.concatenate(
        [d_query.reshape(rows, D), d_key.reshape(rows, D), d_val.reshape(rows, D)], 1
    ).astype(BF16)
    d_qkv_f = d_qkv.astype(F32)
    g_bias_q = jnp.sum(d_qkv_f[:, :D], 0)
    g_bias_v = jnp.sum(d_qkv_f[:, 2 * D :], 0)
    g_qkv = lax.dot_general(first, d_qkv, (((0,), (0,)), ((), ())), preferred_element_type=F32)
    d_first = lax.dot_general(d_qkv, w_qkv, (((1,), (1,)), ((), ())), preferred_element_type=F32)
    first_pull = jax.vjp(layer_norm, value, table[0], table[1])[1]
    d_input, g_gain_one, g_shift_one = first_pull(d_first)
    return (g_qkv, g_out, g_bias_out, g_bias_q, g_bias_v, g_gain_one, g_shift_one), d_input


def adamw(weight, moments, grad, rate):
    first = 0.5 * moments[0] + 0.5 * grad
    root = jnp.sqrt(0.5 * moments[1] * moments[1] + 0.5 * grad * grad)
    update = first / (root + 1e-08)
    return (weight - rate * (update + 0.1 * weight), jnp.stack([first, root]))


def shards(
    tokens,
    cotangent,
    expert_index,
    qkv_weight,
    out_weight,
    router_weight,
    up_weight,
    up_bias,
    down_weight,
    vectors,
    qkv_moments,
    out_moments,
    router_moments,
    up_moments,
    up_bias_moments,
    down_moments,
    vector_moments,
):
    rows = tokens.shape[0]
    micro = rows // MB_TOK
    gs = qkv_weight.shape[0]
    group_size = D // gs
    core = lax.axis_index("core")

    dense_in = pack_dense(qkv_weight, out_weight, router_weight, vectors, up_bias)
    width = dense_in.shape[1]
    dense_in = jnp.pad(dense_in, ((0, 0), (0, DENSE_AG - width))).astype(BF16)
    w_up_all, w_down_all, dense = ring_all_gather(
        up_weight.astype(BF16), down_weight.astype(BF16), dense_in, group_size, 1
    )
    w_qkv, w_out, w_router, table_b, b_up_b = unpack_dense(dense[:, :width])
    table = table_b.astype(F32)
    b_up = b_up_b.astype(F32)

    value = tokens.astype(F32)
    d_out = cotangent.astype(F32)
    first, qkv, log_total, attended, resid = attention_fwd(w_qkv, w_out, table, value)
    second = layer_norm(resid, table[5], table[6]).astype(BF16)
    logits = dot(second, w_router)
    probs = jax.nn.softmax(logits, -1)
    picked = expert_index[:, :, None] == jnp.arange(E, dtype=jnp.int32)
    gate = jnp.sum(jnp.where(picked, probs[:, None, :], 0.0), -1)

    route = expert_index.reshape(micro, MB_TOK, 2)
    places = assign_places(route)
    onehot = (places[:, :, None] == jnp.arange(E * CAP, dtype=jnp.int32)).astype(BF16)
    second_m = second.reshape(micro, MB_TOK, D)
    pair = jnp.concatenate([second_m, second_m], 1)
    table_in = jnp.einsum("mnr,mnd->mrd", onehot, pair, preferred_element_type=F32).astype(BF16)
    table_in = table_in.reshape(micro, E, CAP, D).transpose(1, 0, 2, 3).reshape(E, micro * CAP, D)

    hidden_pre = jnp.einsum("ecd,edf->ecf", table_in, w_up_all, preferred_element_type=F32) + b_up[:, None, :]
    hidden = gelu_exact(hidden_pre).astype(BF16)
    y_all = jnp.einsum("ecf,efd->ecd", hidden, w_down_all, preferred_element_type=F32) + table[7 : 7 + E][:, None, :]
    y_m = y_all.reshape(E, micro, CAP, D).transpose(1, 0, 2, 3).reshape(micro, E * CAP, D)
    picked_rows = pick_rows(onehot, y_m)
    out_zero = picked_rows[:, :MB_TOK].reshape(rows, D)
    out_one = picked_rows[:, MB_TOK:].reshape(rows, D)
    result = resid + (gate[:, 0:1] * out_zero + gate[:, 1:2] * out_one)

    d_gate = jnp.stack([jnp.sum(d_out * out_zero, -1), jnp.sum(d_out * out_one, -1)], 1)
    d_out_m = d_out.reshape(micro, MB_TOK, D)
    gate_m = gate.reshape(micro, MB_TOK, 2)
    weighted = jnp.concatenate([gate_m[:, :, 0:1] * d_out_m, gate_m[:, :, 1:2] * d_out_m], 1).astype(BF16)
    d_expert = jnp.einsum("mnr,mnd->mrd", onehot, weighted, preferred_element_type=F32).astype(BF16)
    d_expert = d_expert.reshape(micro, E, CAP, D).transpose(1, 0, 2, 3).reshape(E, micro * CAP, D)
    g_bias_down = jnp.sum(d_expert.astype(F32), 1)

    g_down = jnp.einsum("ecf,ecd->efd", hidden, d_expert, preferred_element_type=F32)
    d_hidden = jnp.einsum("ecd,efd->ecf", d_expert, w_down_all, preferred_element_type=F32)
    gelu_pull = jax.vjp(gelu_exact, hidden_pre)[1]
    d_pre = gelu_pull(d_hidden)[0].astype(BF16)
    g_up_bias_all = jnp.sum(d_pre.astype(F32), 1)
    g_up = jnp.einsum("ecd,ecf->edf", table_in, d_pre, preferred_element_type=F32)
    d_table = jnp.einsum("ecf,edf->ecd", d_pre, w_up_all, preferred_element_type=F32)

    d_table_m = d_table.reshape(E, micro, CAP, D).transpose(1, 0, 2, 3).reshape(micro, E * CAP, D)
    onehot_sum = onehot[:, :MB_TOK] + onehot[:, MB_TOK:]
    d_picked = pick_rows(onehot_sum, d_table_m).reshape(rows, D)

    d_probs = jnp.sum(jnp.where(picked, d_gate[:, :, None], 0.0), 1)
    d_logit = (probs * (d_probs - jnp.sum(d_probs * probs, -1, keepdims=True))).astype(BF16)
    g_router = lax.dot_general(second, d_logit, (((0,), (0,)), ((), ())), preferred_element_type=F32)
    d_second = d_picked + lax.dot_general(d_logit, w_router, (((1,), (1,)), ((), ())), preferred_element_type=F32)
    norm_pull = jax.vjp(layer_norm, resid, table[5], table[6])[1]
    d_resid, g_gain_two, g_shift_two = norm_pull(d_second)
    d_resid = d_out + d_resid

    att_grads, d_input = attention_bwd(w_qkv, w_out, table, value, first, qkv, log_total, attended, d_resid)
    g_qkv, g_out, g_bias_out, g_bias_q, g_bias_v, g_gain_one, g_shift_one = att_grads
    input_grad = d_resid + d_input

    g_table = jnp.concatenate(
        [
            jnp.stack([g_gain_one, g_shift_one, g_bias_q, g_bias_v, g_bias_out, g_gain_two, g_shift_two]),
            g_bias_down,
        ],
        0,
    )
    both = jnp.stack([g_up, g_down.reshape(E, D, F)], 1).reshape(2, 2, 2, D, F)
    sent = lax.dynamic_index_in_dim(both, 1 - core, 1, keepdims=False).astype(BF16)
    got = lax.ppermute(sent, "core", [(0, 1), (1, 0)])
    mine = lax.dynamic_index_in_dim(both, core, 1, keepdims=False)
    expert_sum = (mine + got.astype(F32)).astype(BF16).reshape(4, D, F)
    dense_g = pack_dense(g_qkv, g_out, g_router, g_table, g_up_bias_all)
    width = dense_g.shape[1]
    dense_g = jnp.pad(dense_g, ((0, 0), (0, DENSE_PAD - width))).astype(BF16)[None]
    e_out, d_out_g = ring_reduce_scatter([expert_sum, dense_g], group_size, 0)
    e_red = lax.psum(e_out, "rx").reshape(2, 2, gs, F)
    d_red = lax.psum(d_out_g[0, :, :width], ("rx", "core")).astype(F32)
    r_qkv, r_out, r_router, r_table, r_ub = unpack_dense(d_red)
    e_all = lax.all_gather(e_red, "core", axis=0, tiled=False).transpose(1, 0, 2, 3, 4).reshape(E, 2, gs, F)
    r_up = e_all[:, 0].astype(F32)
    r_down = e_all[:, 1].astype(F32).reshape(E, gs * 4, D)

    reduced = (r_qkv, r_out, r_router, r_up, r_ub, r_down, r_table)
    rates = (
        2.0 * D ** (-0.5),
        2.0 * (D // 32) ** (-0.5),
        2.0 * (2 * D) ** (-0.5),
        2.0 * D ** (-0.5),
        0.2,
        2.0 * (F // 16) ** (-0.5),
        0.2,
    )
    params = (qkv_weight, out_weight, router_weight, up_weight, up_bias, down_weight, vectors)
    moments = (qkv_moments, out_moments, router_moments, up_moments, up_bias_moments, down_moments, vector_moments)
    news = []
    states = []
    for weight, state, grad, rate in zip(params, moments, reduced, rates):
        new_weight, new_state = adamw(weight, state, grad, rate)
        news.append(new_weight)
        states.append(new_state)
    return (result.astype(BF16), input_grad) + reduced + tuple(news) + tuple(states)


def solution(mesh):
    replica, group = mesh.shape["replica"], mesh.shape["group"]
    view = Mesh(np.asarray(mesh.devices).reshape(replica // 2, 2, group), ("rx", "core", "group"))
    in_specs = (
        P(TOK, None),
        P(TOK, None),
        P(TOK, None),
        P("group", None),
        P("group", None),
        P("group", None),
        P(None, "group", None),
        P(None, "group"),
        P(None, "group", None),
        P(None, "group"),
        P(None, "group", None),
        P(None, "group", None),
        P(None, "group", None),
        P(None, None, "group", None),
        P(None, None, "group"),
        P(None, None, "group", None),
        P(None, None, "group"),
    )
    out_specs = (
        P(TOK, None),
        P(TOK, None),
        P("group", None),
        P("group", None),
        P("group", None),
        P(None, "group", None),
        P(None, "group"),
        P(None, "group", None),
        P(None, "group"),
        P("group", None),
        P("group", None),
        P("group", None),
        P(None, "group", None),
        P(None, "group"),
        P(None, "group", None),
        P(None, "group"),
        P(None, "group", None),
        P(None, "group", None),
        P(None, "group", None),
        P(None, None, "group", None),
        P(None, None, "group"),
        P(None, None, "group", None),
        P(None, None, "group"),
    )
    return jax.shard_map(shards, mesh=view, in_specs=in_specs, out_specs=out_specs, check_vma=False)
```

```python
import functools

import jax
import jax.numpy as jnp
import numpy as np
from jax import lax
from jax.sharding import Mesh
from jax.sharding import PartitionSpec as P
from jax.experimental import pallas as pl
from jax.experimental.pallas import tpu as pltpu

D = 512
HEADS = 8
HEAD_DIM = 64
F = 2048
E = 4
S = 197
MB_TOK = 394
CAP = 392
NV = 11
DENSE_AG = 2560
DENSE_PAD = 2304
F32 = jnp.float32
BF16 = jnp.bfloat16
TOK = ("rx", "core", "group")


MESH_ID = pl.DeviceIdType.MESH


def ring_order(groups):
    if groups in (4, 8):
        zs = groups // 2

        def pos_of(g):
            y = g % 2
            z = g // 2
            return z + y * (2 * zs - 1 - 2 * z)

        def dev_at(p):
            p = p % groups
            yy = p // zs
            return 2 * (p + yy * (2 * zs - 1 - 2 * p)) + yy

        return pos_of, dev_at
    return (lambda g: g), (lambda p: p % groups)


def ring_rs_kernel(groups, n_in, *refs):
    ins = refs[:n_in]
    outs = refs[n_in : 2 * n_in]
    rbufs = refs[2 * n_in : 3 * n_in]
    sbufs = refs[3 * n_in : 4 * n_in]
    owns = refs[4 * n_in : 5 * n_in]
    send_sem, recv_sem, load_sem = refs[5 * n_in :]
    pos_of, dev_at = ring_order(groups)
    rx = lax.axis_index("rx")
    core = lax.axis_index("core")
    g = lax.axis_index("group")
    pos = pos_of(g)
    nbr = (dev_at(pos + 1), dev_at(pos + groups - 1))

    barrier = pltpu.get_barrier_semaphore()
    for n in nbr:
        pl.semaphore_signal(barrier, inc=1, device_id=(rx, core, n), device_id_type=MESH_ID)
    pl.semaphore_wait(barrier, 2)

    def block_dev(d, s):
        if d == 0:
            return dev_at(pos + 2 * groups - s - 1)
        return dev_at(pos + s + 1)

    def load(d, s, slot):
        b = block_dev(d, s)
        copies = []
        for i in range(n_in):
            rows = ins[i].shape[1] // groups
            half = ins[i].shape[2] // 2
            src = ins[i].at[:, pl.ds(pl.multiple_of(b * rows, rows), rows), pl.ds(d * half, half)]
            copies.append(pltpu.make_async_copy(src, owns[i].at[d, slot], load_sem.at[d, slot, i]))
        return copies

    def remote(d, s, i):
        return pltpu.make_async_remote_copy(
            src_ref=sbufs[i].at[d, s],
            dst_ref=rbufs[i].at[d, s],
            send_sem=send_sem.at[d, s, i],
            recv_sem=recv_sem.at[d, s, i],
            device_id=(rx, core, nbr[d]),
            device_id_type=MESH_ID,
        )

    for d in range(2):
        for c in load(d, 0, 0):
            c.start()
    sends = []
    for s in range(groups):
        slot = s % 2
        for d in range(2):
            for c in load(d, s, slot):
                c.wait()
            if s + 1 < groups:
                for c in load(d, s + 1, 1 - slot):
                    c.start()
            for i in range(n_in):
                if s > 0:
                    remote(d, s - 1, i).wait_recv()
                for a in range(ins[i].shape[0]):
                    mine = owns[i][d, slot, a].astype(F32)
                    if s > 0:
                        mine = mine + rbufs[i][d, s - 1, a].astype(F32)
                    if s < groups - 1:
                        sbufs[i][d, s, a] = mine.astype(sbufs[i].dtype)
                    else:
                        half = ins[i].shape[2] // 2
                        outs[i][a, :, pl.ds(d * half, half)] = mine.astype(outs[i].dtype)
                if s < groups - 1:
                    c = remote(d, s, i)
                    c.start()
                    sends.append(c)
    for c in sends:
        c.wait_send()


def ring_reduce_scatter(xs, groups, collective_id):
    n_in = len(xs)
    outs, rb, own = [], [], []
    flops = 0
    nbytes = 0
    for x in xs:
        a, total, c = x.shape
        rows = total // groups
        outs.append(jax.ShapeDtypeStruct((a, rows, c), x.dtype))
        rb.append(pltpu.VMEM((2, groups - 1, a, rows, c // 2), x.dtype))
        own.append(pltpu.VMEM((2, 2, a, rows, c // 2), x.dtype))
        flops += a * total * c
        nbytes += 3 * x.size * x.dtype.itemsize
    scratch = rb + rb + own + [
        pltpu.SemaphoreType.DMA((2, groups - 1, n_in)),
        pltpu.SemaphoreType.DMA((2, groups - 1, n_in)),
        pltpu.SemaphoreType.DMA((2, 2, n_in)),
    ]
    return pl.pallas_call(
        functools.partial(ring_rs_kernel, groups, n_in),
        out_shape=outs,
        in_specs=[pl.BlockSpec(memory_space=pl.ANY)] * n_in,
        out_specs=[pl.BlockSpec(memory_space=pltpu.VMEM)] * n_in,
        scratch_shapes=scratch,
        compiler_params=pltpu.CompilerParams(
            collective_id=collective_id, has_side_effects=True, vmem_limit_bytes=60 * 1024 * 1024
        ),
        cost_estimate=pl.CostEstimate(flops=flops, bytes_accessed=nbytes, transcendentals=0),
    )(*xs)


def ring_ag_kernel(groups, *refs):
    in_up, in_down, in_dense, out_up, out_down, out_dense = refs[:6]
    ring_send, ring_recv, part_send, part_recv, local_sem = refs[6:]
    pos_of, dev_at = ring_order(groups)
    rx = lax.axis_index("rx")
    core = lax.axis_index("core")
    g = lax.axis_index("group")
    other = 1 - core
    pos = pos_of(g)
    nbr = (dev_at(pos + 1), dev_at(pos + groups - 1))
    gs = in_up.shape[1]
    fs = in_down.shape[1]
    width = in_dense.shape[1] // 2

    barrier = pltpu.get_barrier_semaphore()
    for n in nbr:
        pl.semaphore_signal(barrier, inc=1, device_id=(rx, core, n), device_id_type=MESH_ID)
    pl.semaphore_signal(barrier, inc=1, device_id=(rx, other, g), device_id_type=MESH_ID)
    pl.semaphore_wait(barrier, 3)

    def items(owner):
        found = []
        for k in range(2):
            e = 2 * k + owner
            found.append((in_up.at[e], lambda b, e=e: out_up.at[e, pl.ds(pl.multiple_of(b * gs, gs), gs)], F // 2))
            found.append((in_down.at[e], lambda b, e=e: out_down.at[e, pl.ds(pl.multiple_of(b * fs, fs), fs)], D // 2))
        dense_in = in_dense.at[:, pl.ds(owner * width, width)]
        found.append(
            (dense_in, lambda b: out_dense.at[pl.ds(pl.multiple_of(b * gs, gs), gs), pl.ds(owner * width, width)], width // 2)
        )
        return found

    mine = items(core)
    theirs = items(other)
    n_items = len(mine)

    locals_ = [pltpu.make_async_copy(in_up.at[e], out_up.at[e, pl.ds(pl.multiple_of(g * gs, gs), gs)], local_sem.at[e]) for e in range(E)]
    locals_ += [
        pltpu.make_async_copy(in_down.at[e], out_down.at[e, pl.ds(pl.multiple_of(g * fs, fs), fs)], local_sem.at[E + e])
        for e in range(E)
    ]
    locals_.append(pltpu.make_async_copy(in_dense, out_dense.at[pl.ds(pl.multiple_of(g * gs, gs), gs)], local_sem.at[2 * E]))
    for c in locals_:
        c.start()

    def block_at(d, s):
        if d == 0:
            return dev_at(pos + 2 * groups - 1 - s)
        return dev_at(pos + 1 + s)

    def ring_copy(d, s, j, src_block):
        src_in, dst_of, half = mine[j]
        cols = pl.ds(d * half, half)
        if src_block is None:
            src = src_in.at[:, cols]
            dst = dst_of(g).at[:, cols]
        else:
            src = dst_of(src_block).at[:, cols]
            dst = src
        return pltpu.make_async_remote_copy(
            src_ref=src, dst_ref=dst, send_sem=ring_send.at[d, s, j], recv_sem=ring_recv.at[d, s, j],
            device_id=(rx, core, nbr[d]), device_id_type=MESH_ID,
        )

    def part_copy(d, s, j, table, block):
        _, dst_of, half = table[j]
        view = dst_of(block).at[:, pl.ds(d * half, half)]
        return pltpu.make_async_remote_copy(
            src_ref=view, dst_ref=view, send_sem=part_send.at[d, s, j], recv_sem=part_recv.at[d, s, j],
            device_id=(rx, other, g), device_id_type=MESH_ID,
        )

    sends = []
    for d in range(2):
        for j in range(n_items):
            c = ring_copy(d, 0, j, None)
            c.start()
            sends.append(c)
    for s in range(groups - 1):
        for d in range(2):
            b = block_at(d, s)
            for j in range(n_items):
                pltpu.make_async_remote_copy(
                    src_ref=mine[j][1](b).at[:, pl.ds(d * mine[j][2], mine[j][2])],
                    dst_ref=mine[j][1](b).at[:, pl.ds(d * mine[j][2], mine[j][2])],
                    send_sem=ring_send.at[d, s, j], recv_sem=ring_recv.at[d, s, j],
                    device_id=(rx, core, nbr[d]), device_id_type=MESH_ID,
                ).wait_recv()
                if s + 1 < groups - 1:
                    c = ring_copy(d, s + 1, j, b)
                    c.start()
                    sends.append(c)
                c = part_copy(d, s, j, mine, b)
                c.start()
                sends.append(c)
    for s in range(groups - 1):
        for d in range(2):
            b = block_at(d, s)
            for j in range(n_items):
                part_copy(d, s, j, theirs, b).wait_recv()
    for c in sends:
        c.wait_send()
    for c in locals_:
        c.wait()


def ring_all_gather(up_b, down_b, dense_b, groups, collective_id):
    n_items = 5
    gs = up_b.shape[1]
    shapes = [
        jax.ShapeDtypeStruct((E, gs * groups, F), BF16),
        jax.ShapeDtypeStruct((E, down_b.shape[1] * groups, D), BF16),
        jax.ShapeDtypeStruct((gs * groups, dense_b.shape[1]), BF16),
    ]
    nbytes = sum(int(np.prod(s.shape)) * 2 for s in shapes)
    return pl.pallas_call(
        functools.partial(ring_ag_kernel, groups),
        out_shape=shapes,
        in_specs=[pl.BlockSpec(memory_space=pl.ANY)] * 3,
        out_specs=[pl.BlockSpec(memory_space=pl.ANY)] * 3,
        scratch_shapes=[
            pltpu.SemaphoreType.DMA((2, groups - 1, n_items)),
            pltpu.SemaphoreType.DMA((2, groups - 1, n_items)),
            pltpu.SemaphoreType.DMA((2, groups - 1, n_items)),
            pltpu.SemaphoreType.DMA((2, groups - 1, n_items)),
            pltpu.SemaphoreType.DMA((2 * E + 1,)),
        ],
        compiler_params=pltpu.CompilerParams(collective_id=collective_id, has_side_effects=True),
        cost_estimate=pl.CostEstimate(flops=0, bytes_accessed=nbytes, transcendentals=0),
    )(up_b, down_b, dense_b)


def grad_items(gu, gd, gdense, owner, gs, fs, width):
    found = []
    for k in range(2):
        e = 2 * k + owner
        found.append((lambda b, e=e: gu.at[e, pl.ds(pl.multiple_of(b * gs, gs), gs)], F // 2))
        found.append((lambda b, e=e: gd.at[e, pl.ds(pl.multiple_of(b * fs, fs), fs)], D // 2))
    found.append((lambda b: gdense.at[pl.ds(pl.multiple_of(b * gs, gs), gs), pl.ds(owner * width, width)], width // 2))
    return found


def ring_rs2_kernel(groups, x_pair, *refs):
    gu, gd, gdense, out_up, out_down, out_dense = refs[:6]
    n_items = 5
    scr = refs[6:]
    rbuf, sbuf, pbuf, own, fin, xr, cr = (scr[i * n_items : (i + 1) * n_items] for i in range(7))
    ring_send, ring_recv, part_send, part_recv, load_sem, x_send, x_recv, c_send, c_recv = scr[7 * n_items :]
    pos_of, dev_at = ring_order(groups)
    rx = lax.axis_index("rx")
    core = lax.axis_index("core")
    g = lax.axis_index("group")
    other = 1 - core
    pos = pos_of(g)
    nbr = (dev_at(pos + 1), dev_at(pos + groups - 1))
    gs = gu.shape[1] // groups
    fs = gd.shape[1] // groups
    width = gdense.shape[1] // 2
    mine = grad_items(gu, gd, gdense, core, gs, fs, width)
    theirs = grad_items(gu, gd, gdense, other, gs, fs, width)

    barrier = pltpu.get_barrier_semaphore()
    for n in nbr:
        pl.semaphore_signal(barrier, inc=1, device_id=(rx, core, n), device_id_type=MESH_ID)
    pl.semaphore_signal(barrier, inc=1, device_id=(rx, other, g), device_id_type=MESH_ID)
    count = 3
    if x_pair:
        pl.semaphore_signal(barrier, inc=1, device_id=(1 - rx, core, g), device_id_type=MESH_ID)
        count = 4
    pl.semaphore_wait(barrier, count)

    def block_at(d, s):
        if d == 0:
            return dev_at(pos + 2 * groups - 1 - s)
        return dev_at(pos + 1 + s)

    def cols(j, d):
        half = mine[j][1]
        return pl.ds(d * half, half)

    def load(d, s, slot, j):
        return pltpu.make_async_copy(mine[j][0](block_at(d, s)).at[:, cols(j, d)], own[j].at[d, slot], load_sem.at[d, slot, j])

    def part(d, s, j):
        return pltpu.make_async_remote_copy(
            src_ref=theirs[j][0](block_at(d, s)).at[:, cols(j, d)], dst_ref=pbuf[j].at[d, s],
            send_sem=part_send.at[d, s, j], recv_sem=part_recv.at[d, s, j],
            device_id=(rx, other, g), device_id_type=MESH_ID,
        )

    def ring(d, s, j):
        return pltpu.make_async_remote_copy(
            src_ref=sbuf[j].at[d, s], dst_ref=rbuf[j].at[d, s],
            send_sem=ring_send.at[d, s, j], recv_sem=ring_recv.at[d, s, j],
            device_id=(rx, core, nbr[d]), device_id_type=MESH_ID,
        )

    sends = []
    for d in range(2):
        for j in range(n_items):
            load(d, 0, 0, j).start()
            c = part(d, 0, j)
            c.start()
            sends.append(c)
    for s in range(groups):
        slot = s % 2
        for d in range(2):
            for j in range(n_items):
                load(d, s, slot, j).wait()
                if s + 1 < groups:
                    load(d, s + 1, 1 - slot, j).start()
                    c = part(d, s + 1, j)
                    c.start()
                    sends.append(c)
                part(d, s, j).wait_recv()
                val = own[j][d, slot].astype(F32) + pbuf[j][d, s].astype(F32)
                if s > 0:
                    ring(d, s - 1, j).wait_recv()
                    val = val + rbuf[j][d, s - 1].astype(F32)
                if s < groups - 1:
                    sbuf[j][d, s] = val.astype(BF16)
                    c = ring(d, s, j)
                    c.start()
                    sends.append(c)
                else:
                    fin[j][d] = val

    for c in sends:
        c.wait_send()
    sends = []
    if x_pair:
        x_copies = []
        for d in range(2):
            for j in range(n_items):
                sbuf[j][d, 0] = fin[j][d].astype(BF16)
                c = pltpu.make_async_remote_copy(
                    src_ref=sbuf[j].at[d, 0], dst_ref=xr[j].at[d], send_sem=x_send.at[d, j], recv_sem=x_recv.at[d, j],
                    device_id=(1 - rx, core, g), device_id_type=MESH_ID,
                )
                c.start()
                x_copies.append(c)
        for c in x_copies:
            c.wait_recv()
        for d in range(2):
            for j in range(n_items):
                fin[j][d] = sbuf[j][d, 0].astype(F32) + xr[j][d].astype(F32)
        sends += x_copies

    c_copies = []
    for d in range(2):
        for j in range(n_items):
            c = pltpu.make_async_remote_copy(
                src_ref=fin[j].at[d], dst_ref=cr[j].at[d], send_sem=c_send.at[d, j], recv_sem=c_recv.at[d, j],
                device_id=(rx, other, g), device_id_type=MESH_ID,
            )
            c.start()
            c_copies.append(c)

    def out_items(owner):
        found = []
        for k in range(2):
            e = 2 * k + owner
            found.append(lambda d, e=e: out_up.at[e, :, pl.ds(d * (F // 2), F // 2)])
            found.append(lambda d, e=e: out_down.at[e, :, pl.ds(d * (D // 2), D // 2)])
        found.append(lambda d: out_dense.at[:, pl.ds(owner * width + d * (width // 2), width // 2)])
        return found

    mine_out = out_items(core)
    theirs_out = out_items(other)
    for d in range(2):
        for j in range(n_items):
            mine_out[j](d)[...] = fin[j][d]
    for c in c_copies:
        c.wait_recv()
    for d in range(2):
        for j in range(n_items):
            theirs_out[j](d)[...] = cr[j][d]
    for c in sends + c_copies:
        c.wait_send()


def grad_reduce(gu, gd, gdense, groups, x_pair, collective_id):
    gs = gu.shape[1] // groups
    fs = gd.shape[1] // groups
    width = gdense.shape[1] // 2
    item_shapes = [(gs, F // 2), (fs, D // 2), (gs, F // 2), (fs, D // 2), (gs, width // 2)]
    scratch = []
    for lead, dtype in (((2, groups - 1), BF16), ((2, groups - 1), BF16), ((2, groups), BF16), ((2, 2), BF16), ((2,), F32), ((2,), BF16), ((2,), F32)):
        scratch += [pltpu.VMEM(lead + shp, dtype) for shp in item_shapes]
    scratch += [
        pltpu.SemaphoreType.DMA((2, groups - 1, 5)),
        pltpu.SemaphoreType.DMA((2, groups - 1, 5)),
        pltpu.SemaphoreType.DMA((2, groups, 5)),
        pltpu.SemaphoreType.DMA((2, groups, 5)),
        pltpu.SemaphoreType.DMA((2, 2, 5)),
        pltpu.SemaphoreType.DMA((2, 5)),
        pltpu.SemaphoreType.DMA((2, 5)),
        pltpu.SemaphoreType.DMA((2, 5)),
        pltpu.SemaphoreType.DMA((2, 5)),
    ]
    outs = [
        jax.ShapeDtypeStruct((E, gs, F), F32),
        jax.ShapeDtypeStruct((E, fs, D), F32),
        jax.ShapeDtypeStruct((gs, gdense.shape[1]), F32),
    ]
    nbytes = 2 * (gu.size + gd.size + gdense.size)
    return pl.pallas_call(
        functools.partial(ring_rs2_kernel, groups, x_pair),
        out_shape=outs,
        in_specs=[pl.BlockSpec(memory_space=pl.ANY)] * 3,
        out_specs=[pl.BlockSpec(memory_space=pltpu.VMEM)] * 3,
        scratch_shapes=scratch,
        compiler_params=pltpu.CompilerParams(
            collective_id=collective_id, has_side_effects=True, vmem_limit_bytes=62 * 1024 * 1024
        ),
        cost_estimate=pl.CostEstimate(flops=gu.size + gd.size + gdense.size, bytes_accessed=nbytes, transcendentals=0),
    )(gu, gd, gdense)


def layer_norm(value, gain, shift):
    center = value - jnp.mean(value, -1, keepdims=True)
    spread = jnp.mean(center * center, -1, keepdims=True)
    return center * lax.rsqrt(spread + 1e-06) * gain + shift


def gelu_exact(value):
    return jax.nn.gelu(value, approximate=False)


def split_heads(part):
    return part.reshape(-1, S, HEADS, HEAD_DIM)


def dot(a, b):
    return jnp.dot(a, b, preferred_element_type=F32)


def assign_places(route):
    chosen = jnp.concatenate([route[:, :, 0], route[:, :, 1]], 1)
    hits = (chosen[:, :, None] == jnp.arange(E, dtype=jnp.int32)).astype(jnp.int32)
    before = jnp.cumsum(hits, 1) - hits
    slot = jnp.sum(before * hits, 2)
    return chosen * CAP + slot


def hi_lo(v):
    hi = v.astype(BF16)
    lo = (v - hi.astype(F32)).astype(BF16)
    return jnp.concatenate([hi, lo], -1)


def pick_rows(onehot, table):
    both = jnp.einsum("mnr,mrd->mnd", onehot, hi_lo(table), preferred_element_type=F32)
    return both[..., :D] + both[..., D:]


def pack_dense(qkv_w, out_w, router_w, vectors, up_bias):
    rows = qkv_w.shape[0]
    ub = up_bias.reshape(E, rows, 4).transpose(1, 0, 2).reshape(rows, E * 4)
    return jnp.concatenate([qkv_w, out_w, router_w, vectors.T, ub], 1)


def unpack_dense(packed):
    rows = packed.shape[0]
    w_qkv = packed[:, : 3 * D]
    w_out = packed[:, 3 * D : 4 * D]
    w_router = packed[:, 4 * D : 4 * D + E]
    table = packed[:, 4 * D + E : 4 * D + E + NV].T
    ub = packed[:, 4 * D + E + NV :].reshape(rows, E, 4).transpose(1, 0, 2).reshape(E, rows * 4)
    return w_qkv, w_out, w_router, table, ub


def attention_fwd(w_qkv, w_out, table, value):
    rows = value.shape[0]
    scale = HEAD_DIM ** (-0.5)
    first = layer_norm(value, table[0], table[1]).astype(BF16)
    qkv_bias = jnp.concatenate([table[2], jnp.zeros((D,), F32), table[3]])
    qkv = (dot(first, w_qkv) + qkv_bias).astype(BF16)
    query, key_part, val_part = (
        split_heads(qkv[:, :D]),
        split_heads(qkv[:, D : 2 * D]),
        split_heads(qkv[:, 2 * D :]),
    )
    scores = jnp.einsum("bqhd,bkhd->bhqk", query, key_part, preferred_element_type=F32) * scale
    peak = jnp.max(scores, -1, keepdims=True)
    expo = jnp.exp(scores - peak)
    total = jnp.sum(expo, -1, keepdims=True)
    probs_att = (expo / total).astype(BF16)
    log_total = peak + jnp.log(total)
    attended = jnp.einsum("bhqk,bkhd->bqhd", probs_att, val_part, preferred_element_type=F32)
    attended = attended.reshape(rows, D).astype(BF16)
    resid = value + (dot(attended, w_out) + table[4])
    return first, qkv, log_total, attended, resid


def attention_bwd(w_qkv, w_out, table, value, first, qkv, log_total, attended, d_resid):
    rows = value.shape[0]
    scale = HEAD_DIM ** (-0.5)
    d_branch = d_resid.astype(BF16)
    g_bias_out = jnp.sum(d_branch.astype(F32), 0)
    g_out = lax.dot_general(attended, d_branch, (((0,), (0,)), ((), ())), preferred_element_type=F32)
    d_att = split_heads(
        lax.dot_general(d_branch, w_out, (((1,), (1,)), ((), ())), preferred_element_type=F32).astype(BF16)
    )
    query, key_part, val_part = (
        split_heads(qkv[:, :D]),
        split_heads(qkv[:, D : 2 * D]),
        split_heads(qkv[:, 2 * D :]),
    )
    scores = jnp.einsum("bqhd,bkhd->bhqk", query, key_part, preferred_element_type=F32) * scale
    probs_f = jnp.exp(scores - log_total)
    probs_att = probs_f.astype(BF16)
    d_val = jnp.einsum("bhqk,bqhd->bkhd", probs_att, d_att, preferred_element_type=F32)
    d_prob = jnp.einsum("bqhd,bkhd->bhqk", d_att, val_part, preferred_element_type=F32)
    d_score = (probs_f * (d_prob - jnp.sum(d_prob * probs_f, -1, keepdims=True))).astype(BF16)
    d_query = jnp.einsum("bhqk,bkhd->bqhd", d_score, key_part, preferred_element_type=F32) * scale
    d_key = jnp.einsum("bhqk,bqhd->bkhd", d_score, query, preferred_element_type=F32) * scale
    d_qkv = jnp.concatenate(
        [d_query.reshape(rows, D), d_key.reshape(rows, D), d_val.reshape(rows, D)], 1
    ).astype(BF16)
    d_qkv_f = d_qkv.astype(F32)
    g_bias_q = jnp.sum(d_qkv_f[:, :D], 0)
    g_bias_v = jnp.sum(d_qkv_f[:, 2 * D :], 0)
    g_qkv = lax.dot_general(first, d_qkv, (((0,), (0,)), ((), ())), preferred_element_type=F32)
    d_first = lax.dot_general(d_qkv, w_qkv, (((1,), (1,)), ((), ())), preferred_element_type=F32)
    first_pull = jax.vjp(layer_norm, value, table[0], table[1])[1]
    d_input, g_gain_one, g_shift_one = first_pull(d_first)
    return (g_qkv, g_out, g_bias_out, g_bias_q, g_bias_v, g_gain_one, g_shift_one), d_input


def adamw(weight, moments, grad, rate):
    first = 0.5 * moments[0] + 0.5 * grad
    root = jnp.sqrt(0.5 * moments[1] * moments[1] + 0.5 * grad * grad)
    update = first / (root + 1e-08)
    return (weight - rate * (update + 0.1 * weight), jnp.stack([first, root]))


def shards(
    tokens,
    cotangent,
    expert_index,
    qkv_weight,
    out_weight,
    router_weight,
    up_weight,
    up_bias,
    down_weight,
    vectors,
    qkv_moments,
    out_moments,
    router_moments,
    up_moments,
    up_bias_moments,
    down_moments,
    vector_moments,
):
    rows = tokens.shape[0]
    micro = rows // MB_TOK
    gs = qkv_weight.shape[0]
    group_size = D // gs
    core = lax.axis_index("core")

    dense_in = pack_dense(qkv_weight, out_weight, router_weight, vectors, up_bias)
    width = dense_in.shape[1]
    dense_in = jnp.pad(dense_in, ((0, 0), (0, DENSE_AG - width))).astype(BF16)
    w_up_all, w_down_all, dense = ring_all_gather(
        up_weight.astype(BF16), down_weight.astype(BF16), dense_in, group_size, 1
    )
    w_qkv, w_out, w_router, table_b, b_up_b = unpack_dense(dense[:, :width])
    table = table_b.astype(F32)
    b_up = b_up_b.astype(F32)

    value = tokens.astype(F32)
    d_out = cotangent.astype(F32)
    first, qkv, log_total, attended, resid = attention_fwd(w_qkv, w_out, table, value)
    second = layer_norm(resid, table[5], table[6]).astype(BF16)
    logits = dot(second, w_router)
    probs = jax.nn.softmax(logits, -1)
    picked = expert_index[:, :, None] == jnp.arange(E, dtype=jnp.int32)
    gate = jnp.sum(jnp.where(picked, probs[:, None, :], 0.0), -1)

    route = expert_index.reshape(micro, MB_TOK, 2)
    places = assign_places(route)
    onehot = (places[:, :, None] == jnp.arange(E * CAP, dtype=jnp.int32)).astype(BF16)
    second_m = second.reshape(micro, MB_TOK, D)
    pair = jnp.concatenate([second_m, second_m], 1)
    table_in = jnp.einsum("mnr,mnd->mrd", onehot, pair, preferred_element_type=F32).astype(BF16)
    table_in = table_in.reshape(micro, E, CAP, D).transpose(1, 0, 2, 3).reshape(E, micro * CAP, D)

    hidden_pre = jnp.einsum("ecd,edf->ecf", table_in, w_up_all, preferred_element_type=F32) + b_up[:, None, :]
    hidden = gelu_exact(hidden_pre).astype(BF16)
    y_all = jnp.einsum("ecf,efd->ecd", hidden, w_down_all, preferred_element_type=F32) + table[7 : 7 + E][:, None, :]
    y_m = y_all.reshape(E, micro, CAP, D).transpose(1, 0, 2, 3).reshape(micro, E * CAP, D)
    picked_rows = pick_rows(onehot, y_m)
    out_zero = picked_rows[:, :MB_TOK].reshape(rows, D)
    out_one = picked_rows[:, MB_TOK:].reshape(rows, D)
    result = resid + (gate[:, 0:1] * out_zero + gate[:, 1:2] * out_one)

    d_gate = jnp.stack([jnp.sum(d_out * out_zero, -1), jnp.sum(d_out * out_one, -1)], 1)
    d_out_m = d_out.reshape(micro, MB_TOK, D)
    gate_m = gate.reshape(micro, MB_TOK, 2)
    weighted = jnp.concatenate([gate_m[:, :, 0:1] * d_out_m, gate_m[:, :, 1:2] * d_out_m], 1).astype(BF16)
    d_expert = jnp.einsum("mnr,mnd->mrd", onehot, weighted, preferred_element_type=F32).astype(BF16)
    d_expert = d_expert.reshape(micro, E, CAP, D).transpose(1, 0, 2, 3).reshape(E, micro * CAP, D)
    g_bias_down = jnp.sum(d_expert.astype(F32), 1)

    g_down = jnp.einsum("ecf,ecd->efd", hidden, d_expert, preferred_element_type=F32)
    d_hidden = jnp.einsum("ecd,efd->ecf", d_expert, w_down_all, preferred_element_type=F32)
    gelu_pull = jax.vjp(gelu_exact, hidden_pre)[1]
    d_pre = gelu_pull(d_hidden)[0].astype(BF16)
    g_up_bias_all = jnp.sum(d_pre.astype(F32), 1)
    g_up = jnp.einsum("ecd,ecf->edf", table_in, d_pre, preferred_element_type=F32)
    d_table = jnp.einsum("ecf,edf->ecd", d_pre, w_up_all, preferred_element_type=F32)

    d_table_m = d_table.reshape(E, micro, CAP, D).transpose(1, 0, 2, 3).reshape(micro, E * CAP, D)
    onehot_sum = onehot[:, :MB_TOK] + onehot[:, MB_TOK:]
    d_picked = pick_rows(onehot_sum, d_table_m).reshape(rows, D)

    d_probs = jnp.sum(jnp.where(picked, d_gate[:, :, None], 0.0), 1)
    d_logit = (probs * (d_probs - jnp.sum(d_probs * probs, -1, keepdims=True))).astype(BF16)
    g_router = lax.dot_general(second, d_logit, (((0,), (0,)), ((), ())), preferred_element_type=F32)
    d_second = d_picked + lax.dot_general(d_logit, w_router, (((1,), (1,)), ((), ())), preferred_element_type=F32)
    norm_pull = jax.vjp(layer_norm, resid, table[5], table[6])[1]
    d_resid, g_gain_two, g_shift_two = norm_pull(d_second)
    d_resid = d_out + d_resid

    att_grads, d_input = attention_bwd(w_qkv, w_out, table, value, first, qkv, log_total, attended, d_resid)
    g_qkv, g_out, g_bias_out, g_bias_q, g_bias_v, g_gain_one, g_shift_one = att_grads
    input_grad = d_resid + d_input

    g_table = jnp.concatenate(
        [
            jnp.stack([g_gain_one, g_shift_one, g_bias_q, g_bias_v, g_bias_out, g_gain_two, g_shift_two]),
            g_bias_down,
        ],
        0,
    )
    dense_g = pack_dense(g_qkv, g_out, g_router, g_table, g_up_bias_all)
    width = dense_g.shape[1]
    dense_g = jnp.pad(dense_g, ((0, 0), (0, DENSE_AG - width))).astype(BF16)
    x_pair = lax.axis_size("rx") == 2
    r_up, r_down, r_dense = grad_reduce(g_up.astype(BF16), g_down.astype(BF16), dense_g, group_size, x_pair, 0)
    if not x_pair:
        r_up, r_down, r_dense = lax.psum((r_up, r_down, r_dense), "rx")
    r_qkv, r_out, r_router, r_table, r_ub = unpack_dense(r_dense[:, :width])

    reduced = (r_qkv, r_out, r_router, r_up, r_ub, r_down, r_table)
    rates = (
        2.0 * D ** (-0.5),
        2.0 * (D // 32) ** (-0.5),
        2.0 * (2 * D) ** (-0.5),
        2.0 * D ** (-0.5),
        0.2,
        2.0 * (F // 16) ** (-0.5),
        0.2,
    )
    params = (qkv_weight, out_weight, router_weight, up_weight, up_bias, down_weight, vectors)
    moments = (qkv_moments, out_moments, router_moments, up_moments, up_bias_moments, down_moments, vector_moments)
    news = []
    states = []
    for weight, state, grad, rate in zip(params, moments, reduced, rates):
        new_weight, new_state = adamw(weight, state, grad, rate)
        news.append(new_weight)
        states.append(new_state)
    return (result.astype(BF16), input_grad) + reduced + tuple(news) + tuple(states)


def solution(mesh):
    replica, group = mesh.shape["replica"], mesh.shape["group"]
    view = Mesh(np.asarray(mesh.devices).reshape(replica // 2, 2, group), ("rx", "core", "group"))
    in_specs = (
        P(TOK, None),
        P(TOK, None),
        P(TOK, None),
        P("group", None),
        P("group", None),
        P("group", None),
        P(None, "group", None),
        P(None, "group"),
        P(None, "group", None),
        P(None, "group"),
        P(None, "group", None),
        P(None, "group", None),
        P(None, "group", None),
        P(None, None, "group", None),
        P(None, None, "group"),
        P(None, None, "group", None),
        P(None, None, "group"),
    )
    out_specs = (
        P(TOK, None),
        P(TOK, None),
        P("group", None),
        P("group", None),
        P("group", None),
        P(None, "group", None),
        P(None, "group"),
        P(None, "group", None),
        P(None, "group"),
        P("group", None),
        P("group", None),
        P("group", None),
        P(None, "group", None),
        P(None, "group"),
        P(None, "group", None),
        P(None, "group"),
        P(None, "group", None),
        P(None, "group", None),
        P(None, "group", None),
        P(None, None, "group", None),
        P(None, None, "group"),
        P(None, None, "group", None),
        P(None, None, "group"),
    )
    return jax.shard_map(shards, mesh=view, in_specs=in_specs, out_specs=out_specs, check_vma=False)
```

```python
import functools

import jax
import jax.numpy as jnp
import numpy as np
from jax import lax
from jax.sharding import Mesh
from jax.sharding import PartitionSpec as P
from jax.experimental import pallas as pl
from jax.experimental.pallas import tpu as pltpu

D = 512
HEADS = 8
HEAD_DIM = 64
F = 2048
E = 4
S = 197
MB_TOK = 394
CAP = 392
NV = 11
DENSE_AG = 2560
DENSE_PAD = 2304
F32 = jnp.float32
BF16 = jnp.bfloat16
TOK = ("rx", "core", "group")


MESH_ID = pl.DeviceIdType.MESH


def ring_order(groups):
    if groups in (4, 8):
        zs = groups // 2

        def pos_of(g):
            y = g % 2
            z = g // 2
            return z + y * (2 * zs - 1 - 2 * z)

        def dev_at(p):
            p = p % groups
            yy = p // zs
            return 2 * (p + yy * (2 * zs - 1 - 2 * p)) + yy

        return pos_of, dev_at
    return (lambda g: g), (lambda p: p % groups)


def ring_rs_kernel(groups, n_in, *refs):
    ins = refs[:n_in]
    outs = refs[n_in : 2 * n_in]
    rbufs = refs[2 * n_in : 3 * n_in]
    sbufs = refs[3 * n_in : 4 * n_in]
    owns = refs[4 * n_in : 5 * n_in]
    send_sem, recv_sem, load_sem = refs[5 * n_in :]
    pos_of, dev_at = ring_order(groups)
    rx = lax.axis_index("rx")
    core = lax.axis_index("core")
    g = lax.axis_index("group")
    pos = pos_of(g)
    nbr = (dev_at(pos + 1), dev_at(pos + groups - 1))

    barrier = pltpu.get_barrier_semaphore()
    for n in nbr:
        pl.semaphore_signal(barrier, inc=1, device_id=(rx, core, n), device_id_type=MESH_ID)
    pl.semaphore_wait(barrier, 2)

    def block_dev(d, s):
        if d == 0:
            return dev_at(pos + 2 * groups - s - 1)
        return dev_at(pos + s + 1)

    def load(d, s, slot):
        b = block_dev(d, s)
        copies = []
        for i in range(n_in):
            rows = ins[i].shape[1] // groups
            half = ins[i].shape[2] // 2
            src = ins[i].at[:, pl.ds(pl.multiple_of(b * rows, rows), rows), pl.ds(d * half, half)]
            copies.append(pltpu.make_async_copy(src, owns[i].at[d, slot], load_sem.at[d, slot, i]))
        return copies

    def remote(d, s, i):
        return pltpu.make_async_remote_copy(
            src_ref=sbufs[i].at[d, s],
            dst_ref=rbufs[i].at[d, s],
            send_sem=send_sem.at[d, s, i],
            recv_sem=recv_sem.at[d, s, i],
            device_id=(rx, core, nbr[d]),
            device_id_type=MESH_ID,
        )

    for d in range(2):
        for c in load(d, 0, 0):
            c.start()
    sends = []
    for s in range(groups):
        slot = s % 2
        for d in range(2):
            for c in load(d, s, slot):
                c.wait()
            if s + 1 < groups:
                for c in load(d, s + 1, 1 - slot):
                    c.start()
            for i in range(n_in):
                if s > 0:
                    remote(d, s - 1, i).wait_recv()
                for a in range(ins[i].shape[0]):
                    mine = owns[i][d, slot, a].astype(F32)
                    if s > 0:
                        mine = mine + rbufs[i][d, s - 1, a].astype(F32)
                    if s < groups - 1:
                        sbufs[i][d, s, a] = mine.astype(sbufs[i].dtype)
                    else:
                        half = ins[i].shape[2] // 2
                        outs[i][a, :, pl.ds(d * half, half)] = mine.astype(outs[i].dtype)
                if s < groups - 1:
                    c = remote(d, s, i)
                    c.start()
                    sends.append(c)
    for c in sends:
        c.wait_send()


def ring_reduce_scatter(xs, groups, collective_id):
    n_in = len(xs)
    outs, rb, own = [], [], []
    flops = 0
    nbytes = 0
    for x in xs:
        a, total, c = x.shape
        rows = total // groups
        outs.append(jax.ShapeDtypeStruct((a, rows, c), x.dtype))
        rb.append(pltpu.VMEM((2, groups - 1, a, rows, c // 2), x.dtype))
        own.append(pltpu.VMEM((2, 2, a, rows, c // 2), x.dtype))
        flops += a * total * c
        nbytes += 3 * x.size * x.dtype.itemsize
    scratch = rb + rb + own + [
        pltpu.SemaphoreType.DMA((2, groups - 1, n_in)),
        pltpu.SemaphoreType.DMA((2, groups - 1, n_in)),
        pltpu.SemaphoreType.DMA((2, 2, n_in)),
    ]
    return pl.pallas_call(
        functools.partial(ring_rs_kernel, groups, n_in),
        out_shape=outs,
        in_specs=[pl.BlockSpec(memory_space=pl.ANY)] * n_in,
        out_specs=[pl.BlockSpec(memory_space=pltpu.VMEM)] * n_in,
        scratch_shapes=scratch,
        compiler_params=pltpu.CompilerParams(
            collective_id=collective_id, has_side_effects=True, vmem_limit_bytes=60 * 1024 * 1024
        ),
        cost_estimate=pl.CostEstimate(flops=flops, bytes_accessed=nbytes, transcendentals=0),
    )(*xs)


def ring_ag_kernel(groups, *refs):
    in_up, in_down, in_dense, out_up, out_down, out_dense = refs[:6]
    ring_send, ring_recv, part_send, part_recv, local_sem = refs[6:]
    pos_of, dev_at = ring_order(groups)
    rx = lax.axis_index("rx")
    core = lax.axis_index("core")
    g = lax.axis_index("group")
    other = 1 - core
    pos = pos_of(g)
    nbr = (dev_at(pos + 1), dev_at(pos + groups - 1))
    gs = in_up.shape[1]
    fs = in_down.shape[1]
    width = in_dense.shape[1] // 2

    barrier = pltpu.get_barrier_semaphore()
    for n in nbr:
        pl.semaphore_signal(barrier, inc=1, device_id=(rx, core, n), device_id_type=MESH_ID)
    pl.semaphore_signal(barrier, inc=1, device_id=(rx, other, g), device_id_type=MESH_ID)
    pl.semaphore_wait(barrier, 3)

    def items(owner):
        found = []
        for k in range(2):
            e = 2 * k + owner
            found.append((in_up.at[e], lambda b, e=e: out_up.at[e, pl.ds(pl.multiple_of(b * gs, gs), gs)], F // 2))
            found.append((in_down.at[e], lambda b, e=e: out_down.at[e, pl.ds(pl.multiple_of(b * fs, fs), fs)], D // 2))
        dense_in = in_dense.at[:, pl.ds(owner * width, width)]
        found.append(
            (dense_in, lambda b: out_dense.at[pl.ds(pl.multiple_of(b * gs, gs), gs), pl.ds(owner * width, width)], width // 2)
        )
        return found

    mine = items(core)
    theirs = items(other)
    n_items = len(mine)

    locals_ = [pltpu.make_async_copy(in_up.at[e], out_up.at[e, pl.ds(pl.multiple_of(g * gs, gs), gs)], local_sem.at[e]) for e in range(E)]
    locals_ += [
        pltpu.make_async_copy(in_down.at[e], out_down.at[e, pl.ds(pl.multiple_of(g * fs, fs), fs)], local_sem.at[E + e])
        for e in range(E)
    ]
    locals_.append(pltpu.make_async_copy(in_dense, out_dense.at[pl.ds(pl.multiple_of(g * gs, gs), gs)], local_sem.at[2 * E]))
    for c in locals_:
        c.start()

    def block_at(d, s):
        if d == 0:
            return dev_at(pos + 2 * groups - 1 - s)
        return dev_at(pos + 1 + s)

    def ring_copy(d, s, j, src_block):
        src_in, dst_of, half = mine[j]
        cols = pl.ds(d * half, half)
        if src_block is None:
            src = src_in.at[:, cols]
            dst = dst_of(g).at[:, cols]
        else:
            src = dst_of(src_block).at[:, cols]
            dst = src
        return pltpu.make_async_remote_copy(
            src_ref=src, dst_ref=dst, send_sem=ring_send.at[d, s, j], recv_sem=ring_recv.at[d, s, j],
            device_id=(rx, core, nbr[d]), device_id_type=MESH_ID,
        )

    def part_copy(d, s, j, table, block):
        _, dst_of, half = table[j]
        view = dst_of(block).at[:, pl.ds(d * half, half)]
        return pltpu.make_async_remote_copy(
            src_ref=view, dst_ref=view, send_sem=part_send.at[d, s, j], recv_sem=part_recv.at[d, s, j],
            device_id=(rx, other, g), device_id_type=MESH_ID,
        )

    sends = []
    for d in range(2):
        for j in range(n_items):
            c = ring_copy(d, 0, j, None)
            c.start()
            sends.append(c)
    for s in range(groups - 1):
        for d in range(2):
            b = block_at(d, s)
            for j in range(n_items):
                pltpu.make_async_remote_copy(
                    src_ref=mine[j][1](b).at[:, pl.ds(d * mine[j][2], mine[j][2])],
                    dst_ref=mine[j][1](b).at[:, pl.ds(d * mine[j][2], mine[j][2])],
                    send_sem=ring_send.at[d, s, j], recv_sem=ring_recv.at[d, s, j],
                    device_id=(rx, core, nbr[d]), device_id_type=MESH_ID,
                ).wait_recv()
                if s + 1 < groups - 1:
                    c = ring_copy(d, s + 1, j, b)
                    c.start()
                    sends.append(c)
                c = part_copy(d, s, j, mine, b)
                c.start()
                sends.append(c)
    for s in range(groups - 1):
        for d in range(2):
            b = block_at(d, s)
            for j in range(n_items):
                part_copy(d, s, j, theirs, b).wait_recv()
    for c in sends:
        c.wait_send()
    for c in locals_:
        c.wait()


def ring_all_gather(up_b, down_b, dense_b, groups, collective_id):
    n_items = 5
    gs = up_b.shape[1]
    shapes = [
        jax.ShapeDtypeStruct((E, gs * groups, F), BF16),
        jax.ShapeDtypeStruct((E, down_b.shape[1] * groups, D), BF16),
        jax.ShapeDtypeStruct((gs * groups, dense_b.shape[1]), BF16),
    ]
    nbytes = sum(int(np.prod(s.shape)) * 2 for s in shapes)
    return pl.pallas_call(
        functools.partial(ring_ag_kernel, groups),
        out_shape=shapes,
        in_specs=[pl.BlockSpec(memory_space=pl.ANY)] * 3,
        out_specs=[pl.BlockSpec(memory_space=pl.ANY)] * 3,
        scratch_shapes=[
            pltpu.SemaphoreType.DMA((2, groups - 1, n_items)),
            pltpu.SemaphoreType.DMA((2, groups - 1, n_items)),
            pltpu.SemaphoreType.DMA((2, groups - 1, n_items)),
            pltpu.SemaphoreType.DMA((2, groups - 1, n_items)),
            pltpu.SemaphoreType.DMA((2 * E + 1,)),
        ],
        compiler_params=pltpu.CompilerParams(collective_id=collective_id, has_side_effects=True),
        cost_estimate=pl.CostEstimate(flops=0, bytes_accessed=nbytes, transcendentals=0),
    )(up_b, down_b, dense_b)


def grad_items(gu, gd, gdense, owner, gs, fs, width):
    found = []
    for k in range(2):
        e = 2 * k + owner
        found.append((lambda b, e=e: gu.at[e, pl.ds(pl.multiple_of(b * gs, gs), gs)], F // 2))
        found.append((lambda b, e=e: gd.at[e, pl.ds(pl.multiple_of(b * fs, fs), fs)], D // 2))
    found.append((lambda b: gdense.at[pl.ds(pl.multiple_of(b * gs, gs), gs), pl.ds(owner * width, width)], width // 2))
    return found


def ring_rs2_kernel(groups, x_pair, *refs):
    gu, gd, gdense, out_up, out_down, out_dense = refs[:6]
    n_items = 5
    scr = refs[6:]
    rbuf, sbuf, pbuf, own, fin, xr, cr = (scr[i * n_items : (i + 1) * n_items] for i in range(7))
    ring_send, ring_recv, part_send, part_recv, load_sem, x_send, x_recv, c_send, c_recv = scr[7 * n_items :]
    pos_of, dev_at = ring_order(groups)
    rx = lax.axis_index("rx")
    core = lax.axis_index("core")
    g = lax.axis_index("group")
    other = 1 - core
    pos = pos_of(g)
    nbr = (dev_at(pos + 1), dev_at(pos + groups - 1))
    gs = gu.shape[1] // groups
    fs = gd.shape[1] // groups
    width = gdense.shape[1] // 2
    mine = grad_items(gu, gd, gdense, core, gs, fs, width)
    theirs = grad_items(gu, gd, gdense, other, gs, fs, width)

    barrier = pltpu.get_barrier_semaphore()
    for n in nbr:
        pl.semaphore_signal(barrier, inc=1, device_id=(rx, core, n), device_id_type=MESH_ID)
    pl.semaphore_signal(barrier, inc=1, device_id=(rx, other, g), device_id_type=MESH_ID)
    count = 3
    if x_pair:
        pl.semaphore_signal(barrier, inc=1, device_id=(1 - rx, core, g), device_id_type=MESH_ID)
        count = 4
    pl.semaphore_wait(barrier, count)

    def block_at(d, s):
        if d == 0:
            return dev_at(pos + 2 * groups - 1 - s)
        return dev_at(pos + 1 + s)

    def cols(j, d):
        half = mine[j][1]
        return pl.ds(d * half, half)

    def load(d, s, slot, j):
        return pltpu.make_async_copy(mine[j][0](block_at(d, s)).at[:, cols(j, d)], own[j].at[d, slot], load_sem.at[d, slot, j])

    def part(d, s, j):
        return pltpu.make_async_remote_copy(
            src_ref=theirs[j][0](block_at(d, s)).at[:, cols(j, d)], dst_ref=pbuf[j].at[d, s],
            send_sem=part_send.at[d, s, j], recv_sem=part_recv.at[d, s, j],
            device_id=(rx, other, g), device_id_type=MESH_ID,
        )

    def ring(d, s, j):
        return pltpu.make_async_remote_copy(
            src_ref=sbuf[j].at[d, s], dst_ref=rbuf[j].at[d, s],
            send_sem=ring_send.at[d, s, j], recv_sem=ring_recv.at[d, s, j],
            device_id=(rx, core, nbr[d]), device_id_type=MESH_ID,
        )

    sends = []
    for d in range(2):
        for j in range(n_items):
            load(d, 0, 0, j).start()
            c = part(d, 0, j)
            c.start()
            sends.append(c)
    for s in range(groups):
        slot = s % 2
        for d in range(2):
            for j in range(n_items):
                load(d, s, slot, j).wait()
                if s + 1 < groups:
                    load(d, s + 1, 1 - slot, j).start()
                    c = part(d, s + 1, j)
                    c.start()
                    sends.append(c)
                part(d, s, j).wait_recv()
                val = own[j][d, slot].astype(F32) + pbuf[j][d, s].astype(F32)
                if s > 0:
                    ring(d, s - 1, j).wait_recv()
                    val = val + rbuf[j][d, s - 1].astype(F32)
                if s < groups - 1:
                    sbuf[j][d, s] = val.astype(BF16)
                    c = ring(d, s, j)
                    c.start()
                    sends.append(c)
                else:
                    fin[j][d] = val

    for c in sends:
        c.wait_send()
    sends = []
    if x_pair:
        x_copies = []
        for d in range(2):
            for j in range(n_items):
                sbuf[j][d, 0] = fin[j][d].astype(BF16)
                c = pltpu.make_async_remote_copy(
                    src_ref=sbuf[j].at[d, 0], dst_ref=xr[j].at[d], send_sem=x_send.at[d, j], recv_sem=x_recv.at[d, j],
                    device_id=(1 - rx, core, g), device_id_type=MESH_ID,
                )
                c.start()
                x_copies.append(c)
        for c in x_copies:
            c.wait_recv()
        for d in range(2):
            for j in range(n_items):
                fin[j][d] = sbuf[j][d, 0].astype(F32) + xr[j][d].astype(F32)
        sends += x_copies

    c_copies = []
    for d in range(2):
        for j in range(n_items):
            c = pltpu.make_async_remote_copy(
                src_ref=fin[j].at[d], dst_ref=cr[j].at[d], send_sem=c_send.at[d, j], recv_sem=c_recv.at[d, j],
                device_id=(rx, other, g), device_id_type=MESH_ID,
            )
            c.start()
            c_copies.append(c)

    def out_items(owner):
        found = []
        for k in range(2):
            e = 2 * k + owner
            found.append(lambda d, e=e: out_up.at[e, :, pl.ds(d * (F // 2), F // 2)])
            found.append(lambda d, e=e: out_down.at[e, :, pl.ds(d * (D // 2), D // 2)])
        found.append(lambda d: out_dense.at[:, pl.ds(owner * width + d * (width // 2), width // 2)])
        return found

    mine_out = out_items(core)
    theirs_out = out_items(other)
    for d in range(2):
        for j in range(n_items):
            mine_out[j](d)[...] = fin[j][d]
    for c in c_copies:
        c.wait_recv()
    for d in range(2):
        for j in range(n_items):
            theirs_out[j](d)[...] = cr[j][d]
    for c in sends + c_copies:
        c.wait_send()


def grad_reduce(gu, gd, gdense, groups, x_pair, collective_id):
    gs = gu.shape[1] // groups
    fs = gd.shape[1] // groups
    width = gdense.shape[1] // 2
    item_shapes = [(gs, F // 2), (fs, D // 2), (gs, F // 2), (fs, D // 2), (gs, width // 2)]
    scratch = []
    for lead, dtype in (((2, groups - 1), BF16), ((2, groups - 1), BF16), ((2, groups), BF16), ((2, 2), BF16), ((2,), F32), ((2,), BF16), ((2,), F32)):
        scratch += [pltpu.VMEM(lead + shp, dtype) for shp in item_shapes]
    scratch += [
        pltpu.SemaphoreType.DMA((2, groups - 1, 5)),
        pltpu.SemaphoreType.DMA((2, groups - 1, 5)),
        pltpu.SemaphoreType.DMA((2, groups, 5)),
        pltpu.SemaphoreType.DMA((2, groups, 5)),
        pltpu.SemaphoreType.DMA((2, 2, 5)),
        pltpu.SemaphoreType.DMA((2, 5)),
        pltpu.SemaphoreType.DMA((2, 5)),
        pltpu.SemaphoreType.DMA((2, 5)),
        pltpu.SemaphoreType.DMA((2, 5)),
    ]
    outs = [
        jax.ShapeDtypeStruct((E, gs, F), F32),
        jax.ShapeDtypeStruct((E, fs, D), F32),
        jax.ShapeDtypeStruct((gs, gdense.shape[1]), F32),
    ]
    nbytes = 2 * (gu.size + gd.size + gdense.size)
    return pl.pallas_call(
        functools.partial(ring_rs2_kernel, groups, x_pair),
        out_shape=outs,
        in_specs=[pl.BlockSpec(memory_space=pl.ANY)] * 3,
        out_specs=[pl.BlockSpec(memory_space=pltpu.VMEM)] * 3,
        scratch_shapes=scratch,
        compiler_params=pltpu.CompilerParams(
            collective_id=collective_id, has_side_effects=True, vmem_limit_bytes=62 * 1024 * 1024
        ),
        cost_estimate=pl.CostEstimate(flops=gu.size + gd.size + gdense.size, bytes_accessed=nbytes, transcendentals=0),
    )(gu, gd, gdense)


TILE = 128
CAPP = 512
SQRT_HALF = float(np.sqrt(0.5))
INV_SQRT_2PI = float(1.0 / np.sqrt(2.0 * np.pi))


def ffn_fwd_kernel(micro, counts, x_ref, w1_ref, b1_ref, w2_ref, b2_ref, hp_ref, h_ref, y_ref):
    e, m, t = pl.program_id(0), pl.program_id(1), pl.program_id(2)
    active = t * TILE < counts[e * micro + m]

    @pl.when(active)
    def _():
        hp = jnp.dot(x_ref[0], w1_ref[0], preferred_element_type=F32) + b1_ref[0]
        h = (0.5 * hp * (1.0 + lax.erf(hp * SQRT_HALF))).astype(BF16)
        hp_ref[0] = hp
        h_ref[0] = h
        y_ref[0] = jnp.dot(h, w2_ref[0], preferred_element_type=F32) + b2_ref[0]

    @pl.when(jnp.logical_not(active))
    def _():
        y_ref[0] = jnp.zeros(y_ref.shape[1:], F32)


def ffn_forward(counts, table_in, w1, b1, w2, b2, micro):
    tiles = CAPP // TILE
    rows = table_in.shape[1]
    row_map = lambda e, m, t, c: (e, m * tiles + t, 0)
    w_map = lambda e, m, t, c: (e, 0, 0)
    grid_spec = pltpu.PrefetchScalarGridSpec(
        num_scalar_prefetch=1,
        grid=(E, micro, tiles),
        in_specs=[
            pl.BlockSpec((1, TILE, D), row_map),
            pl.BlockSpec((1, D, F), w_map),
            pl.BlockSpec((1, 1, F), w_map),
            pl.BlockSpec((1, F, D), w_map),
            pl.BlockSpec((1, 1, D), w_map),
        ],
        out_specs=[
            pl.BlockSpec((1, TILE, F), row_map),
            pl.BlockSpec((1, TILE, F), row_map),
            pl.BlockSpec((1, TILE, D), row_map),
        ],
    )
    work = E * rows
    return pl.pallas_call(
        functools.partial(ffn_fwd_kernel, micro),
        grid_spec=grid_spec,
        out_shape=[
            jax.ShapeDtypeStruct((E, rows, F), F32),
            jax.ShapeDtypeStruct((E, rows, F), BF16),
            jax.ShapeDtypeStruct((E, rows, D), F32),
        ],
        compiler_params=pltpu.CompilerParams(vmem_limit_bytes=48 * 1024 * 1024),
        cost_estimate=pl.CostEstimate(
            flops=4 * work * D * F // 2, bytes_accessed=work * (2 * D + 6 * F + 4 * D) // 2, transcendentals=work * F // 2
        ),
    )(counts, table_in, w1, b1, w2, b2)


def ffn_bwd_kernel(micro, counts, dy_ref, x_ref, hp_ref, h_ref, w1_ref, w2_ref, dt_ref, gu_ref, gd_ref, gb_ref):
    e, m, t = pl.program_id(0), pl.program_id(1), pl.program_id(2)
    active = t * TILE < counts[e * micro + m]

    @pl.when((m == 0) & (t == 0))
    def _():
        gu_ref[...] = jnp.zeros(gu_ref.shape, F32)
        gd_ref[...] = jnp.zeros(gd_ref.shape, F32)
        gb_ref[...] = jnp.zeros(gb_ref.shape, F32)

    @pl.when(active)
    def _():
        dy = dy_ref[0]
        hp = hp_ref[0]
        d_hidden = lax.dot_general(dy, w2_ref[0], (((1,), (1,)), ((), ())), preferred_element_type=F32)
        slope = 0.5 * (1.0 + lax.erf(hp * SQRT_HALF)) + hp * jnp.exp(-0.5 * hp * hp) * INV_SQRT_2PI
        d_pre = (d_hidden * slope).astype(BF16)
        dt_ref[0] = lax.dot_general(d_pre, w1_ref[0], (((1,), (1,)), ((), ())), preferred_element_type=F32)
        gu_ref[0] += lax.dot_general(x_ref[0], d_pre, (((0,), (0,)), ((), ())), preferred_element_type=F32)
        gd_ref[0] += lax.dot_general(h_ref[0], dy, (((0,), (0,)), ((), ())), preferred_element_type=F32)
        gb_ref[0] += jnp.sum(d_pre.astype(F32), 0, keepdims=True)

    @pl.when(jnp.logical_not(active))
    def _():
        dt_ref[0] = jnp.zeros(dt_ref.shape[1:], F32)


def ffn_backward(counts, d_expert, table_in, hp, h, w1, w2, micro):
    tiles = CAPP // TILE
    rows = table_in.shape[1]
    row_map = lambda e, m, t, c: (e, m * tiles + t, 0)
    w_map = lambda e, m, t, c: (e, 0, 0)
    grid_spec = pltpu.PrefetchScalarGridSpec(
        num_scalar_prefetch=1,
        grid=(E, micro, tiles),
        in_specs=[
            pl.BlockSpec((1, TILE, D), row_map),
            pl.BlockSpec((1, TILE, D), row_map),
            pl.BlockSpec((1, TILE, F), row_map),
            pl.BlockSpec((1, TILE, F), row_map),
            pl.BlockSpec((1, D, F), w_map),
            pl.BlockSpec((1, F, D), w_map),
        ],
        out_specs=[
            pl.BlockSpec((1, TILE, D), row_map),
            pl.BlockSpec((1, D, F), w_map),
            pl.BlockSpec((1, F, D), w_map),
            pl.BlockSpec((1, 1, F), w_map),
        ],
    )
    work = E * rows
    return pl.pallas_call(
        functools.partial(ffn_bwd_kernel, micro),
        grid_spec=grid_spec,
        out_shape=[
            jax.ShapeDtypeStruct((E, rows, D), F32),
            jax.ShapeDtypeStruct((E, D, F), F32),
            jax.ShapeDtypeStruct((E, F, D), F32),
            jax.ShapeDtypeStruct((E, 1, F), F32),
        ],
        compiler_params=pltpu.CompilerParams(vmem_limit_bytes=56 * 1024 * 1024),
        cost_estimate=pl.CostEstimate(
            flops=8 * work * D * F // 2, bytes_accessed=work * (8 * D + 6 * F) // 2 + 32 * E * D * F, transcendentals=2 * work * F // 2
        ),
    )(counts, d_expert, table_in, hp, h, w1, w2)


def layer_norm(value, gain, shift):
    center = value - jnp.mean(value, -1, keepdims=True)
    spread = jnp.mean(center * center, -1, keepdims=True)
    return center * lax.rsqrt(spread + 1e-06) * gain + shift


def gelu_exact(value):
    return jax.nn.gelu(value, approximate=False)


def split_heads(part):
    return part.reshape(-1, S, HEADS, HEAD_DIM)


def dot(a, b):
    return jnp.dot(a, b, preferred_element_type=F32)


def assign_places(route):
    chosen = jnp.concatenate([route[:, :, 0], route[:, :, 1]], 1)
    hits = (chosen[:, :, None] == jnp.arange(E, dtype=jnp.int32)).astype(jnp.int32)
    before = jnp.cumsum(hits, 1) - hits
    slot = jnp.sum(before * hits, 2)
    return chosen * CAPP + slot, jnp.sum(hits, 1)


def hi_lo(v):
    hi = v.astype(BF16)
    lo = (v - hi.astype(F32)).astype(BF16)
    return jnp.concatenate([hi, lo], -1)


def pick_rows(onehot, table):
    both = jnp.einsum("mnr,mrd->mnd", onehot, hi_lo(table), preferred_element_type=F32)
    return both[..., :D] + both[..., D:]


def pack_dense(qkv_w, out_w, router_w, vectors, up_bias):
    rows = qkv_w.shape[0]
    ub = up_bias.reshape(E, rows, 4).transpose(1, 0, 2).reshape(rows, E * 4)
    return jnp.concatenate([qkv_w, out_w, router_w, vectors.T, ub], 1)


def unpack_dense(packed):
    rows = packed.shape[0]
    w_qkv = packed[:, : 3 * D]
    w_out = packed[:, 3 * D : 4 * D]
    w_router = packed[:, 4 * D : 4 * D + E]
    table = packed[:, 4 * D + E : 4 * D + E + NV].T
    ub = packed[:, 4 * D + E + NV :].reshape(rows, E, 4).transpose(1, 0, 2).reshape(E, rows * 4)
    return w_qkv, w_out, w_router, table, ub


def attention_fwd(w_qkv, w_out, table, value):
    rows = value.shape[0]
    scale = HEAD_DIM ** (-0.5)
    first = layer_norm(value, table[0], table[1]).astype(BF16)
    qkv_bias = jnp.concatenate([table[2], jnp.zeros((D,), F32), table[3]])
    qkv = (dot(first, w_qkv) + qkv_bias).astype(BF16)
    query, key_part, val_part = (
        split_heads(qkv[:, :D]),
        split_heads(qkv[:, D : 2 * D]),
        split_heads(qkv[:, 2 * D :]),
    )
    scores = jnp.einsum("bqhd,bkhd->bhqk", query, key_part, preferred_element_type=F32) * scale
    peak = jnp.max(scores, -1, keepdims=True)
    expo = jnp.exp(scores - peak)
    total = jnp.sum(expo, -1, keepdims=True)
    probs_att = (expo / total).astype(BF16)
    log_total = peak + jnp.log(total)
    attended = jnp.einsum("bhqk,bkhd->bqhd", probs_att, val_part, preferred_element_type=F32)
    attended = attended.reshape(rows, D).astype(BF16)
    resid = value + (dot(attended, w_out) + table[4])
    return first, qkv, log_total, attended, resid


def attention_bwd(w_qkv, w_out, table, value, first, qkv, log_total, attended, d_resid):
    rows = value.shape[0]
    scale = HEAD_DIM ** (-0.5)
    d_branch = d_resid.astype(BF16)
    g_bias_out = jnp.sum(d_branch.astype(F32), 0)
    g_out = lax.dot_general(attended, d_branch, (((0,), (0,)), ((), ())), preferred_element_type=F32)
    d_att = split_heads(
        lax.dot_general(d_branch, w_out, (((1,), (1,)), ((), ())), preferred_element_type=F32).astype(BF16)
    )
    query, key_part, val_part = (
        split_heads(qkv[:, :D]),
        split_heads(qkv[:, D : 2 * D]),
        split_heads(qkv[:, 2 * D :]),
    )
    scores = jnp.einsum("bqhd,bkhd->bhqk", query, key_part, preferred_element_type=F32) * scale
    probs_f = jnp.exp(scores - log_total)
    probs_att = probs_f.astype(BF16)
    d_val = jnp.einsum("bhqk,bqhd->bkhd", probs_att, d_att, preferred_element_type=F32)
    d_prob = jnp.einsum("bqhd,bkhd->bhqk", d_att, val_part, preferred_element_type=F32)
    d_score = (probs_f * (d_prob - jnp.sum(d_prob * probs_f, -1, keepdims=True))).astype(BF16)
    d_query = jnp.einsum("bhqk,bkhd->bqhd", d_score, key_part, preferred_element_type=F32) * scale
    d_key = jnp.einsum("bhqk,bqhd->bkhd", d_score, query, preferred_element_type=F32) * scale
    d_qkv = jnp.concatenate(
        [d_query.reshape(rows, D), d_key.reshape(rows, D), d_val.reshape(rows, D)], 1
    ).astype(BF16)
    d_qkv_f = d_qkv.astype(F32)
    g_bias_q = jnp.sum(d_qkv_f[:, :D], 0)
    g_bias_v = jnp.sum(d_qkv_f[:, 2 * D :], 0)
    g_qkv = lax.dot_general(first, d_qkv, (((0,), (0,)), ((), ())), preferred_element_type=F32)
    d_first = lax.dot_general(d_qkv, w_qkv, (((1,), (1,)), ((), ())), preferred_element_type=F32)
    first_pull = jax.vjp(layer_norm, value, table[0], table[1])[1]
    d_input, g_gain_one, g_shift_one = first_pull(d_first)
    return (g_qkv, g_out, g_bias_out, g_bias_q, g_bias_v, g_gain_one, g_shift_one), d_input


def adamw(weight, moments, grad, rate):
    first = 0.5 * moments[0] + 0.5 * grad
    root = jnp.sqrt(0.5 * moments[1] * moments[1] + 0.5 * grad * grad)
    update = first / (root + 1e-08)
    return (weight - rate * (update + 0.1 * weight), jnp.stack([first, root]))


def shards(
    tokens,
    cotangent,
    expert_index,
    qkv_weight,
    out_weight,
    router_weight,
    up_weight,
    up_bias,
    down_weight,
    vectors,
    qkv_moments,
    out_moments,
    router_moments,
    up_moments,
    up_bias_moments,
    down_moments,
    vector_moments,
):
    rows = tokens.shape[0]
    micro = rows // MB_TOK
    gs = qkv_weight.shape[0]
    group_size = D // gs
    core = lax.axis_index("core")

    dense_in = pack_dense(qkv_weight, out_weight, router_weight, vectors, up_bias)
    width = dense_in.shape[1]
    dense_in = jnp.pad(dense_in, ((0, 0), (0, DENSE_AG - width))).astype(BF16)
    w_up_all, w_down_all, dense = ring_all_gather(
        up_weight.astype(BF16), down_weight.astype(BF16), dense_in, group_size, 1
    )
    w_qkv, w_out, w_router, table_b, b_up_b = unpack_dense(dense[:, :width])
    table = table_b.astype(F32)
    b_up = b_up_b.astype(F32)

    value = tokens.astype(F32)
    d_out = cotangent.astype(F32)
    first, qkv, log_total, attended, resid = attention_fwd(w_qkv, w_out, table, value)
    second = layer_norm(resid, table[5], table[6]).astype(BF16)
    logits = dot(second, w_router)
    probs = jax.nn.softmax(logits, -1)
    picked = expert_index[:, :, None] == jnp.arange(E, dtype=jnp.int32)
    gate = jnp.sum(jnp.where(picked, probs[:, None, :], 0.0), -1)

    route = expert_index.reshape(micro, MB_TOK, 2)
    places, counts = assign_places(route)
    counts = counts.T.reshape(E * micro)
    onehot = (places[:, :, None] == jnp.arange(E * CAPP, dtype=jnp.int32)).astype(BF16)
    second_m = second.reshape(micro, MB_TOK, D)
    pair = jnp.concatenate([second_m, second_m], 1)
    table_in = jnp.einsum("mnr,mnd->mrd", onehot, pair, preferred_element_type=F32).astype(BF16)
    table_in = table_in.reshape(micro, E, CAPP, D).transpose(1, 0, 2, 3).reshape(E, micro * CAPP, D)

    hidden_pre, hidden, y_all = ffn_forward(
        counts, table_in, w_up_all, b_up[:, None, :], w_down_all, table[7 : 7 + E][:, None, :], micro
    )
    y_m = y_all.reshape(E, micro, CAPP, D).transpose(1, 0, 2, 3).reshape(micro, E * CAPP, D)
    picked_rows = pick_rows(onehot, y_m)
    out_zero = picked_rows[:, :MB_TOK].reshape(rows, D)
    out_one = picked_rows[:, MB_TOK:].reshape(rows, D)
    result = resid + (gate[:, 0:1] * out_zero + gate[:, 1:2] * out_one)

    d_gate = jnp.stack([jnp.sum(d_out * out_zero, -1), jnp.sum(d_out * out_one, -1)], 1)
    d_out_m = d_out.reshape(micro, MB_TOK, D)
    gate_m = gate.reshape(micro, MB_TOK, 2)
    weighted = jnp.concatenate([gate_m[:, :, 0:1] * d_out_m, gate_m[:, :, 1:2] * d_out_m], 1).astype(BF16)
    d_expert = jnp.einsum("mnr,mnd->mrd", onehot, weighted, preferred_element_type=F32).astype(BF16)
    d_expert = d_expert.reshape(micro, E, CAPP, D).transpose(1, 0, 2, 3).reshape(E, micro * CAPP, D)
    g_bias_down = jnp.sum(d_expert.astype(F32), 1)

    d_table, g_up, g_down, g_b1 = ffn_backward(counts, d_expert, table_in, hidden_pre, hidden, w_up_all, w_down_all, micro)
    g_up_bias_all = g_b1[:, 0, :]

    d_table_m = d_table.reshape(E, micro, CAPP, D).transpose(1, 0, 2, 3).reshape(micro, E * CAPP, D)
    onehot_sum = onehot[:, :MB_TOK] + onehot[:, MB_TOK:]
    d_picked = pick_rows(onehot_sum, d_table_m).reshape(rows, D)

    d_probs = jnp.sum(jnp.where(picked, d_gate[:, :, None], 0.0), 1)
    d_logit = (probs * (d_probs - jnp.sum(d_probs * probs, -1, keepdims=True))).astype(BF16)
    g_router = lax.dot_general(second, d_logit, (((0,), (0,)), ((), ())), preferred_element_type=F32)
    d_second = d_picked + lax.dot_general(d_logit, w_router, (((1,), (1,)), ((), ())), preferred_element_type=F32)
    norm_pull = jax.vjp(layer_norm, resid, table[5], table[6])[1]
    d_resid, g_gain_two, g_shift_two = norm_pull(d_second)
    d_resid = d_out + d_resid

    att_grads, d_input = attention_bwd(w_qkv, w_out, table, value, first, qkv, log_total, attended, d_resid)
    g_qkv, g_out, g_bias_out, g_bias_q, g_bias_v, g_gain_one, g_shift_one = att_grads
    input_grad = d_resid + d_input

    g_table = jnp.concatenate(
        [
            jnp.stack([g_gain_one, g_shift_one, g_bias_q, g_bias_v, g_bias_out, g_gain_two, g_shift_two]),
            g_bias_down,
        ],
        0,
    )
    dense_g = pack_dense(g_qkv, g_out, g_router, g_table, g_up_bias_all)
    width = dense_g.shape[1]
    dense_g = jnp.pad(dense_g, ((0, 0), (0, DENSE_AG - width))).astype(BF16)
    x_pair = lax.axis_size("rx") == 2
    r_up, r_down, r_dense = grad_reduce(g_up.astype(BF16), g_down.astype(BF16), dense_g, group_size, x_pair, 0)
    if not x_pair:
        r_up, r_down, r_dense = lax.psum((r_up, r_down, r_dense), "rx")
    r_qkv, r_out, r_router, r_table, r_ub = unpack_dense(r_dense[:, :width])

    reduced = (r_qkv, r_out, r_router, r_up, r_ub, r_down, r_table)
    rates = (
        2.0 * D ** (-0.5),
        2.0 * (D // 32) ** (-0.5),
        2.0 * (2 * D) ** (-0.5),
        2.0 * D ** (-0.5),
        0.2,
        2.0 * (F // 16) ** (-0.5),
        0.2,
    )
    params = (qkv_weight, out_weight, router_weight, up_weight, up_bias, down_weight, vectors)
    moments = (qkv_moments, out_moments, router_moments, up_moments, up_bias_moments, down_moments, vector_moments)
    news = []
    states = []
    for weight, state, grad, rate in zip(params, moments, reduced, rates):
        new_weight, new_state = adamw(weight, state, grad, rate)
        news.append(new_weight)
        states.append(new_state)
    return (result.astype(BF16), input_grad) + reduced + tuple(news) + tuple(states)


def solution(mesh):
    replica, group = mesh.shape["replica"], mesh.shape["group"]
    view = Mesh(np.asarray(mesh.devices).reshape(replica // 2, 2, group), ("rx", "core", "group"))
    in_specs = (
        P(TOK, None),
        P(TOK, None),
        P(TOK, None),
        P("group", None),
        P("group", None),
        P("group", None),
        P(None, "group", None),
        P(None, "group"),
        P(None, "group", None),
        P(None, "group"),
        P(None, "group", None),
        P(None, "group", None),
        P(None, "group", None),
        P(None, None, "group", None),
        P(None, None, "group"),
        P(None, None, "group", None),
        P(None, None, "group"),
    )
    out_specs = (
        P(TOK, None),
        P(TOK, None),
        P("group", None),
        P("group", None),
        P("group", None),
        P(None, "group", None),
        P(None, "group"),
        P(None, "group", None),
        P(None, "group"),
        P("group", None),
        P("group", None),
        P("group", None),
        P(None, "group", None),
        P(None, "group"),
        P(None, "group", None),
        P(None, "group"),
        P(None, "group", None),
        P(None, "group", None),
        P(None, "group", None),
        P(None, None, "group", None),
        P(None, None, "group"),
        P(None, None, "group", None),
        P(None, None, "group"),
    )
    return jax.shard_map(shards, mesh=view, in_specs=in_specs, out_specs=out_specs, check_vma=False)
```

```python
import functools

import jax
import jax.numpy as jnp
import numpy as np
from jax import lax
from jax.sharding import Mesh
from jax.sharding import PartitionSpec as P
from jax.experimental import pallas as pl
from jax.experimental.pallas import tpu as pltpu

D = 512
HEADS = 8
HEAD_DIM = 64
F = 2048
E = 4
S = 197
MB_TOK = 394
CAP = 392
NV = 11
DENSE_AG = 2560
DENSE_PAD = 2304
F32 = jnp.float32
BF16 = jnp.bfloat16
TOK = ("rx", "core", "group")


MESH_ID = pl.DeviceIdType.MESH


def ring_order(groups):
    if groups in (4, 8):
        zs = groups // 2

        def pos_of(g):
            y = g % 2
            z = g // 2
            return z + y * (2 * zs - 1 - 2 * z)

        def dev_at(p):
            p = p % groups
            yy = p // zs
            return 2 * (p + yy * (2 * zs - 1 - 2 * p)) + yy

        return pos_of, dev_at
    return (lambda g: g), (lambda p: p % groups)


def ring_rs_kernel(groups, n_in, *refs):
    ins = refs[:n_in]
    outs = refs[n_in : 2 * n_in]
    rbufs = refs[2 * n_in : 3 * n_in]
    sbufs = refs[3 * n_in : 4 * n_in]
    owns = refs[4 * n_in : 5 * n_in]
    send_sem, recv_sem, load_sem = refs[5 * n_in :]
    pos_of, dev_at = ring_order(groups)
    rx = lax.axis_index("rx")
    core = lax.axis_index("core")
    g = lax.axis_index("group")
    pos = pos_of(g)
    nbr = (dev_at(pos + 1), dev_at(pos + groups - 1))

    barrier = pltpu.get_barrier_semaphore()
    for n in nbr:
        pl.semaphore_signal(barrier, inc=1, device_id=(rx, core, n), device_id_type=MESH_ID)
    pl.semaphore_wait(barrier, 2)

    def block_dev(d, s):
        if d == 0:
            return dev_at(pos + 2 * groups - s - 1)
        return dev_at(pos + s + 1)

    def load(d, s, slot):
        b = block_dev(d, s)
        copies = []
        for i in range(n_in):
            rows = ins[i].shape[1] // groups
            half = ins[i].shape[2] // 2
            src = ins[i].at[:, pl.ds(pl.multiple_of(b * rows, rows), rows), pl.ds(d * half, half)]
            copies.append(pltpu.make_async_copy(src, owns[i].at[d, slot], load_sem.at[d, slot, i]))
        return copies

    def remote(d, s, i):
        return pltpu.make_async_remote_copy(
            src_ref=sbufs[i].at[d, s],
            dst_ref=rbufs[i].at[d, s],
            send_sem=send_sem.at[d, s, i],
            recv_sem=recv_sem.at[d, s, i],
            device_id=(rx, core, nbr[d]),
            device_id_type=MESH_ID,
        )

    for d in range(2):
        for c in load(d, 0, 0):
            c.start()
    sends = []
    for s in range(groups):
        slot = s % 2
        for d in range(2):
            for c in load(d, s, slot):
                c.wait()
            if s + 1 < groups:
                for c in load(d, s + 1, 1 - slot):
                    c.start()
            for i in range(n_in):
                if s > 0:
                    remote(d, s - 1, i).wait_recv()
                for a in range(ins[i].shape[0]):
                    mine = owns[i][d, slot, a].astype(F32)
                    if s > 0:
                        mine = mine + rbufs[i][d, s - 1, a].astype(F32)
                    if s < groups - 1:
                        sbufs[i][d, s, a] = mine.astype(sbufs[i].dtype)
                    else:
                        half = ins[i].shape[2] // 2
                        outs[i][a, :, pl.ds(d * half, half)] = mine.astype(outs[i].dtype)
                if s < groups - 1:
                    c = remote(d, s, i)
                    c.start()
                    sends.append(c)
    for c in sends:
        c.wait_send()


def ring_reduce_scatter(xs, groups, collective_id):
    n_in = len(xs)
    outs, rb, own = [], [], []
    flops = 0
    nbytes = 0
    for x in xs:
        a, total, c = x.shape
        rows = total // groups
        outs.append(jax.ShapeDtypeStruct((a, rows, c), x.dtype))
        rb.append(pltpu.VMEM((2, groups - 1, a, rows, c // 2), x.dtype))
        own.append(pltpu.VMEM((2, 2, a, rows, c // 2), x.dtype))
        flops += a * total * c
        nbytes += 3 * x.size * x.dtype.itemsize
    scratch = rb + rb + own + [
        pltpu.SemaphoreType.DMA((2, groups - 1, n_in)),
        pltpu.SemaphoreType.DMA((2, groups - 1, n_in)),
        pltpu.SemaphoreType.DMA((2, 2, n_in)),
    ]
    return pl.pallas_call(
        functools.partial(ring_rs_kernel, groups, n_in),
        out_shape=outs,
        in_specs=[pl.BlockSpec(memory_space=pl.ANY)] * n_in,
        out_specs=[pl.BlockSpec(memory_space=pltpu.VMEM)] * n_in,
        scratch_shapes=scratch,
        compiler_params=pltpu.CompilerParams(
            collective_id=collective_id, has_side_effects=True, vmem_limit_bytes=60 * 1024 * 1024
        ),
        cost_estimate=pl.CostEstimate(flops=flops, bytes_accessed=nbytes, transcendentals=0),
    )(*xs)


def ring_ag_kernel(groups, *refs):
    in_up, in_down, in_dense, out_up, out_down, out_dense = refs[:6]
    ring_send, ring_recv, part_send, part_recv, local_sem = refs[6:]
    pos_of, dev_at = ring_order(groups)
    rx = lax.axis_index("rx")
    core = lax.axis_index("core")
    g = lax.axis_index("group")
    other = 1 - core
    pos = pos_of(g)
    nbr = (dev_at(pos + 1), dev_at(pos + groups - 1))
    gs = in_up.shape[1]
    fs = in_down.shape[1]
    width = in_dense.shape[1] // 2

    barrier = pltpu.get_barrier_semaphore()
    for n in nbr:
        pl.semaphore_signal(barrier, inc=1, device_id=(rx, core, n), device_id_type=MESH_ID)
    pl.semaphore_signal(barrier, inc=1, device_id=(rx, other, g), device_id_type=MESH_ID)
    pl.semaphore_wait(barrier, 3)

    def items(owner):
        found = []
        for k in range(2):
            e = 2 * k + owner
            found.append((in_up.at[e], lambda b, e=e: out_up.at[e, pl.ds(pl.multiple_of(b * gs, gs), gs)], F // 2))
            found.append((in_down.at[e], lambda b, e=e: out_down.at[e, pl.ds(pl.multiple_of(b * fs, fs), fs)], D // 2))
        dense_in = in_dense.at[:, pl.ds(owner * width, width)]
        found.append(
            (dense_in, lambda b: out_dense.at[pl.ds(pl.multiple_of(b * gs, gs), gs), pl.ds(owner * width, width)], width // 2)
        )
        return found

    mine = items(core)
    theirs = items(other)
    n_items = len(mine)

    locals_ = [pltpu.make_async_copy(in_up.at[e], out_up.at[e, pl.ds(pl.multiple_of(g * gs, gs), gs)], local_sem.at[e]) for e in range(E)]
    locals_ += [
        pltpu.make_async_copy(in_down.at[e], out_down.at[e, pl.ds(pl.multiple_of(g * fs, fs), fs)], local_sem.at[E + e])
        for e in range(E)
    ]
    locals_.append(pltpu.make_async_copy(in_dense, out_dense.at[pl.ds(pl.multiple_of(g * gs, gs), gs)], local_sem.at[2 * E]))
    for c in locals_:
        c.start()

    def block_at(d, s):
        if d == 0:
            return dev_at(pos + 2 * groups - 1 - s)
        return dev_at(pos + 1 + s)

    def ring_copy(d, s, j, src_block):
        src_in, dst_of, half = mine[j]
        cols = pl.ds(d * half, half)
        if src_block is None:
            src = src_in.at[:, cols]
            dst = dst_of(g).at[:, cols]
        else:
            src = dst_of(src_block).at[:, cols]
            dst = src
        return pltpu.make_async_remote_copy(
            src_ref=src, dst_ref=dst, send_sem=ring_send.at[d, s, j], recv_sem=ring_recv.at[d, s, j],
            device_id=(rx, core, nbr[d]), device_id_type=MESH_ID,
        )

    def part_copy(d, s, j, table, block):
        _, dst_of, half = table[j]
        view = dst_of(block).at[:, pl.ds(d * half, half)]
        return pltpu.make_async_remote_copy(
            src_ref=view, dst_ref=view, send_sem=part_send.at[d, s, j], recv_sem=part_recv.at[d, s, j],
            device_id=(rx, other, g), device_id_type=MESH_ID,
        )

    sends = []
    for d in range(2):
        for j in range(n_items):
            c = ring_copy(d, 0, j, None)
            c.start()
            sends.append(c)
    for s in range(groups - 1):
        for d in range(2):
            b = block_at(d, s)
            for j in range(n_items):
                pltpu.make_async_remote_copy(
                    src_ref=mine[j][1](b).at[:, pl.ds(d * mine[j][2], mine[j][2])],
                    dst_ref=mine[j][1](b).at[:, pl.ds(d * mine[j][2], mine[j][2])],
                    send_sem=ring_send.at[d, s, j], recv_sem=ring_recv.at[d, s, j],
                    device_id=(rx, core, nbr[d]), device_id_type=MESH_ID,
                ).wait_recv()
                if s + 1 < groups - 1:
                    c = ring_copy(d, s + 1, j, b)
                    c.start()
                    sends.append(c)
                c = part_copy(d, s, j, mine, b)
                c.start()
                sends.append(c)
    for s in range(groups - 1):
        for d in range(2):
            b = block_at(d, s)
            for j in range(n_items):
                part_copy(d, s, j, theirs, b).wait_recv()
    for c in sends:
        c.wait_send()
    for c in locals_:
        c.wait()


def ring_all_gather(up_b, down_b, dense_b, groups, collective_id):
    n_items = 5
    gs = up_b.shape[1]
    shapes = [
        jax.ShapeDtypeStruct((E, gs * groups, F), BF16),
        jax.ShapeDtypeStruct((E, down_b.shape[1] * groups, D), BF16),
        jax.ShapeDtypeStruct((gs * groups, dense_b.shape[1]), BF16),
    ]
    nbytes = sum(int(np.prod(s.shape)) * 2 for s in shapes)
    return pl.pallas_call(
        functools.partial(ring_ag_kernel, groups),
        out_shape=shapes,
        in_specs=[pl.BlockSpec(memory_space=pl.ANY)] * 3,
        out_specs=[pl.BlockSpec(memory_space=pl.ANY)] * 3,
        scratch_shapes=[
            pltpu.SemaphoreType.DMA((2, groups - 1, n_items)),
            pltpu.SemaphoreType.DMA((2, groups - 1, n_items)),
            pltpu.SemaphoreType.DMA((2, groups - 1, n_items)),
            pltpu.SemaphoreType.DMA((2, groups - 1, n_items)),
            pltpu.SemaphoreType.DMA((2 * E + 1,)),
        ],
        compiler_params=pltpu.CompilerParams(collective_id=collective_id, has_side_effects=True),
        cost_estimate=pl.CostEstimate(flops=0, bytes_accessed=nbytes, transcendentals=0),
    )(up_b, down_b, dense_b)


def grad_items(gu, gd, gdense, owner, gs, fs, width):
    found = []
    for k in range(2):
        e = 2 * k + owner
        found.append((lambda b, e=e: gu.at[e, pl.ds(pl.multiple_of(b * gs, gs), gs)], F // 2))
        found.append((lambda b, e=e: gd.at[e, pl.ds(pl.multiple_of(b * fs, fs), fs)], D // 2))
    found.append((lambda b: gdense.at[pl.ds(pl.multiple_of(b * gs, gs), gs), pl.ds(owner * width, width)], width // 2))
    return found


def ring_rs2_kernel(groups, x_pair, *refs):
    gu, gd, gdense, out_up, out_down, out_dense = refs[:6]
    n_items = 5
    scr = refs[6:]
    rbuf, sbuf, pbuf, own, fin, xr, cr = (scr[i * n_items : (i + 1) * n_items] for i in range(7))
    ring_send, ring_recv, part_send, part_recv, load_sem, x_send, x_recv, c_send, c_recv = scr[7 * n_items :]
    pos_of, dev_at = ring_order(groups)
    rx = lax.axis_index("rx")
    core = lax.axis_index("core")
    g = lax.axis_index("group")
    other = 1 - core
    pos = pos_of(g)
    nbr = (dev_at(pos + 1), dev_at(pos + groups - 1))
    gs = gu.shape[1] // groups
    fs = gd.shape[1] // groups
    width = gdense.shape[1] // 2
    mine = grad_items(gu, gd, gdense, core, gs, fs, width)
    theirs = grad_items(gu, gd, gdense, other, gs, fs, width)

    barrier = pltpu.get_barrier_semaphore()
    for n in nbr:
        pl.semaphore_signal(barrier, inc=1, device_id=(rx, core, n), device_id_type=MESH_ID)
    pl.semaphore_signal(barrier, inc=1, device_id=(rx, other, g), device_id_type=MESH_ID)
    count = 3
    if x_pair:
        pl.semaphore_signal(barrier, inc=1, device_id=(1 - rx, core, g), device_id_type=MESH_ID)
        count = 4
    pl.semaphore_wait(barrier, count)

    def block_at(d, s):
        if d == 0:
            return dev_at(pos + 2 * groups - 1 - s)
        return dev_at(pos + 1 + s)

    def cols(j, d):
        half = mine[j][1]
        return pl.ds(d * half, half)

    def load(d, s, slot, j):
        return pltpu.make_async_copy(mine[j][0](block_at(d, s)).at[:, cols(j, d)], own[j].at[d, slot], load_sem.at[d, slot, j])

    def part(d, s, j):
        return pltpu.make_async_remote_copy(
            src_ref=theirs[j][0](block_at(d, s)).at[:, cols(j, d)], dst_ref=pbuf[j].at[d, s],
            send_sem=part_send.at[d, s, j], recv_sem=part_recv.at[d, s, j],
            device_id=(rx, other, g), device_id_type=MESH_ID,
        )

    def ring(d, s, j):
        return pltpu.make_async_remote_copy(
            src_ref=sbuf[j].at[d, s], dst_ref=rbuf[j].at[d, s],
            send_sem=ring_send.at[d, s, j], recv_sem=ring_recv.at[d, s, j],
            device_id=(rx, core, nbr[d]), device_id_type=MESH_ID,
        )

    sends = []
    for d in range(2):
        for j in range(n_items):
            load(d, 0, 0, j).start()
            c = part(d, 0, j)
            c.start()
            sends.append(c)
    for s in range(groups):
        slot = s % 2
        for d in range(2):
            for j in range(n_items):
                load(d, s, slot, j).wait()
                if s + 1 < groups:
                    load(d, s + 1, 1 - slot, j).start()
                    c = part(d, s + 1, j)
                    c.start()
                    sends.append(c)
                part(d, s, j).wait_recv()
                val = own[j][d, slot].astype(F32) + pbuf[j][d, s].astype(F32)
                if s > 0:
                    ring(d, s - 1, j).wait_recv()
                    val = val + rbuf[j][d, s - 1].astype(F32)
                if s < groups - 1:
                    sbuf[j][d, s] = val.astype(BF16)
                    c = ring(d, s, j)
                    c.start()
                    sends.append(c)
                else:
                    fin[j][d] = val

    for c in sends:
        c.wait_send()
    sends = []
    if x_pair:
        x_copies = []
        for d in range(2):
            for j in range(n_items):
                sbuf[j][d, 0] = fin[j][d].astype(BF16)
                c = pltpu.make_async_remote_copy(
                    src_ref=sbuf[j].at[d, 0], dst_ref=xr[j].at[d], send_sem=x_send.at[d, j], recv_sem=x_recv.at[d, j],
                    device_id=(1 - rx, core, g), device_id_type=MESH_ID,
                )
                c.start()
                x_copies.append(c)
        for c in x_copies:
            c.wait_recv()
        for d in range(2):
            for j in range(n_items):
                fin[j][d] = sbuf[j][d, 0].astype(F32) + xr[j][d].astype(F32)
        sends += x_copies

    c_copies = []
    for d in range(2):
        for j in range(n_items):
            c = pltpu.make_async_remote_copy(
                src_ref=fin[j].at[d], dst_ref=cr[j].at[d], send_sem=c_send.at[d, j], recv_sem=c_recv.at[d, j],
                device_id=(rx, other, g), device_id_type=MESH_ID,
            )
            c.start()
            c_copies.append(c)

    def out_items(owner):
        found = []
        for k in range(2):
            e = 2 * k + owner
            found.append(lambda d, e=e: out_up.at[e, :, pl.ds(d * (F // 2), F // 2)])
            found.append(lambda d, e=e: out_down.at[e, :, pl.ds(d * (D // 2), D // 2)])
        found.append(lambda d: out_dense.at[:, pl.ds(owner * width + d * (width // 2), width // 2)])
        return found

    mine_out = out_items(core)
    theirs_out = out_items(other)
    for d in range(2):
        for j in range(n_items):
            mine_out[j](d)[...] = fin[j][d]
    for c in c_copies:
        c.wait_recv()
    for d in range(2):
        for j in range(n_items):
            theirs_out[j](d)[...] = cr[j][d]
    for c in sends + c_copies:
        c.wait_send()


def grad_reduce(gu, gd, gdense, groups, x_pair, collective_id):
    gs = gu.shape[1] // groups
    fs = gd.shape[1] // groups
    width = gdense.shape[1] // 2
    item_shapes = [(gs, F // 2), (fs, D // 2), (gs, F // 2), (fs, D // 2), (gs, width // 2)]
    scratch = []
    for lead, dtype in (((2, groups - 1), BF16), ((2, groups - 1), BF16), ((2, groups), BF16), ((2, 2), BF16), ((2,), F32), ((2,), BF16), ((2,), F32)):
        scratch += [pltpu.VMEM(lead + shp, dtype) for shp in item_shapes]
    scratch += [
        pltpu.SemaphoreType.DMA((2, groups - 1, 5)),
        pltpu.SemaphoreType.DMA((2, groups - 1, 5)),
        pltpu.SemaphoreType.DMA((2, groups, 5)),
        pltpu.SemaphoreType.DMA((2, groups, 5)),
        pltpu.SemaphoreType.DMA((2, 2, 5)),
        pltpu.SemaphoreType.DMA((2, 5)),
        pltpu.SemaphoreType.DMA((2, 5)),
        pltpu.SemaphoreType.DMA((2, 5)),
        pltpu.SemaphoreType.DMA((2, 5)),
    ]
    outs = [
        jax.ShapeDtypeStruct((E, gs, F), F32),
        jax.ShapeDtypeStruct((E, fs, D), F32),
        jax.ShapeDtypeStruct((gs, gdense.shape[1]), F32),
    ]
    nbytes = 2 * (gu.size + gd.size + gdense.size)
    return pl.pallas_call(
        functools.partial(ring_rs2_kernel, groups, x_pair),
        out_shape=outs,
        in_specs=[pl.BlockSpec(memory_space=pl.ANY)] * 3,
        out_specs=[pl.BlockSpec(memory_space=pltpu.VMEM)] * 3,
        scratch_shapes=scratch,
        compiler_params=pltpu.CompilerParams(
            collective_id=collective_id, has_side_effects=True, vmem_limit_bytes=62 * 1024 * 1024
        ),
        cost_estimate=pl.CostEstimate(flops=gu.size + gd.size + gdense.size, bytes_accessed=nbytes, transcendentals=0),
    )(gu, gd, gdense)


TILE = 128
TILE_B = 256
CAPP = 512
SQRT_HALF = float(np.sqrt(0.5))
INV_SQRT_2PI = float(1.0 / np.sqrt(2.0 * np.pi))


def ffn_fwd_kernel(micro, counts, x_ref, w1_ref, b1_ref, w2_ref, b2_ref, hp_ref, h_ref, y_ref):
    e, m, t = pl.program_id(0), pl.program_id(1), pl.program_id(2)
    active = t * TILE < counts[e * micro + m]

    @pl.when(active)
    def _():
        hp = jnp.dot(x_ref[0], w1_ref[0], preferred_element_type=F32) + b1_ref[0]
        h = (0.5 * hp * (1.0 + lax.erf(hp * SQRT_HALF))).astype(BF16)
        hp_ref[0] = hp
        h_ref[0] = h
        y_ref[0] = jnp.dot(h, w2_ref[0], preferred_element_type=F32) + b2_ref[0]

    @pl.when(jnp.logical_not(active))
    def _():
        y_ref[0] = jnp.zeros(y_ref.shape[1:], F32)


def ffn_forward(counts, table_in, w1, b1, w2, b2, micro):
    tiles = CAPP // TILE
    rows = table_in.shape[1]
    row_map = lambda e, m, t, c: (e, m * tiles + t, 0)
    w_map = lambda e, m, t, c: (e, 0, 0)
    grid_spec = pltpu.PrefetchScalarGridSpec(
        num_scalar_prefetch=1,
        grid=(E, micro, tiles),
        in_specs=[
            pl.BlockSpec((1, TILE, D), row_map),
            pl.BlockSpec((1, D, F), w_map),
            pl.BlockSpec((1, 1, F), w_map),
            pl.BlockSpec((1, F, D), w_map),
            pl.BlockSpec((1, 1, D), w_map),
        ],
        out_specs=[
            pl.BlockSpec((1, TILE, F), row_map),
            pl.BlockSpec((1, TILE, F), row_map),
            pl.BlockSpec((1, TILE, D), row_map),
        ],
    )
    work = E * rows
    return pl.pallas_call(
        functools.partial(ffn_fwd_kernel, micro),
        grid_spec=grid_spec,
        out_shape=[
            jax.ShapeDtypeStruct((E, rows, F), F32),
            jax.ShapeDtypeStruct((E, rows, F), BF16),
            jax.ShapeDtypeStruct((E, rows, D), F32),
        ],
        compiler_params=pltpu.CompilerParams(vmem_limit_bytes=48 * 1024 * 1024),
        cost_estimate=pl.CostEstimate(
            flops=4 * work * D * F // 2, bytes_accessed=work * (2 * D + 6 * F + 4 * D) // 2, transcendentals=work * F // 2
        ),
    )(counts, table_in, w1, b1, w2, b2)


def ffn_bwd_kernel(micro, counts, dy_ref, x_ref, hp_ref, h_ref, w1_ref, w2_ref, dt_ref, gu_ref, gd_ref, gb_ref, gu_acc, gd_acc):
    e, m, t = pl.program_id(0), pl.program_id(1), pl.program_id(2)
    active = t * TILE_B < counts[e * micro + m]

    @pl.when((m == 0) & (t == 0))
    def _():
        gu_acc[...] = jnp.zeros(gu_acc.shape, F32)
        gd_acc[...] = jnp.zeros(gd_acc.shape, F32)
        gb_ref[...] = jnp.zeros(gb_ref.shape, F32)

    @pl.when(active)
    def _():
        dy = dy_ref[0]
        hp = hp_ref[0]
        d_hidden = lax.dot_general(dy, w2_ref[0], (((1,), (1,)), ((), ())), preferred_element_type=F32)
        slope = 0.5 * (1.0 + lax.erf(hp * SQRT_HALF)) + hp * jnp.exp(-0.5 * hp * hp) * INV_SQRT_2PI
        d_pre = (d_hidden * slope).astype(BF16)
        dt_ref[0] = lax.dot_general(d_pre, w1_ref[0], (((1,), (1,)), ((), ())), preferred_element_type=F32)
        gu_acc[...] += lax.dot_general(x_ref[0], d_pre, (((0,), (0,)), ((), ())), preferred_element_type=F32)
        gd_acc[...] += lax.dot_general(h_ref[0], dy, (((0,), (0,)), ((), ())), preferred_element_type=F32)
        gb_ref[0] += jnp.sum(d_pre.astype(F32), 0, keepdims=True)

    @pl.when(jnp.logical_not(active))
    def _():
        dt_ref[0] = jnp.zeros(dt_ref.shape[1:], F32)

    @pl.when((m == micro - 1) & (t == pl.num_programs(2) - 1))
    def _():
        gu_ref[0] = gu_acc[...].astype(BF16)
        gd_ref[0] = gd_acc[...].astype(BF16)


def ffn_backward(counts, d_expert, table_in, hp, h, w1, w2, micro):
    tiles = CAPP // TILE_B
    rows = table_in.shape[1]
    row_map = lambda e, m, t, c: (e, m * tiles + t, 0)
    w_map = lambda e, m, t, c: (e, 0, 0)
    grid_spec = pltpu.PrefetchScalarGridSpec(
        num_scalar_prefetch=1,
        grid=(E, micro, tiles),
        in_specs=[
            pl.BlockSpec((1, TILE_B, D), row_map),
            pl.BlockSpec((1, TILE_B, D), row_map),
            pl.BlockSpec((1, TILE_B, F), row_map),
            pl.BlockSpec((1, TILE_B, F), row_map),
            pl.BlockSpec((1, D, F), w_map),
            pl.BlockSpec((1, F, D), w_map),
        ],
        out_specs=[
            pl.BlockSpec((1, TILE_B, D), row_map),
            pl.BlockSpec((1, D, F), w_map),
            pl.BlockSpec((1, F, D), w_map),
            pl.BlockSpec((1, 1, F), w_map),
        ],
        scratch_shapes=[pltpu.VMEM((D, F), F32), pltpu.VMEM((F, D), F32)],
    )
    work = E * rows
    return pl.pallas_call(
        functools.partial(ffn_bwd_kernel, micro),
        grid_spec=grid_spec,
        out_shape=[
            jax.ShapeDtypeStruct((E, rows, D), F32),
            jax.ShapeDtypeStruct((E, D, F), BF16),
            jax.ShapeDtypeStruct((E, F, D), BF16),
            jax.ShapeDtypeStruct((E, 1, F), F32),
        ],
        compiler_params=pltpu.CompilerParams(vmem_limit_bytes=60 * 1024 * 1024),
        cost_estimate=pl.CostEstimate(
            flops=8 * work * D * F // 2, bytes_accessed=work * (8 * D + 6 * F) // 2 + 16 * E * D * F, transcendentals=2 * work * F // 2
        ),
    )(counts, d_expert, table_in, hp, h, w1, w2)

def layer_norm(value, gain, shift):
    center = value - jnp.mean(value, -1, keepdims=True)
    spread = jnp.mean(center * center, -1, keepdims=True)
    return center * lax.rsqrt(spread + 1e-06) * gain + shift


def gelu_exact(value):
    return jax.nn.gelu(value, approximate=False)


def split_heads(part):
    return part.reshape(-1, S, HEADS, HEAD_DIM)


def dot(a, b):
    return jnp.dot(a, b, preferred_element_type=F32)


def assign_places(route):
    chosen = jnp.concatenate([route[:, :, 0], route[:, :, 1]], 1)
    hits = (chosen[:, :, None] == jnp.arange(E, dtype=jnp.int32)).astype(jnp.int32)
    before = jnp.cumsum(hits, 1) - hits
    slot = jnp.sum(before * hits, 2)
    return chosen * CAPP + slot, jnp.sum(hits, 1)


def hi_lo(v):
    hi = v.astype(BF16)
    lo = (v - hi.astype(F32)).astype(BF16)
    return jnp.concatenate([hi, lo], -1)


def pick_rows(onehot, table):
    both = jnp.einsum("mnr,mrd->mnd", onehot, hi_lo(table), preferred_element_type=F32)
    return both[..., :D] + both[..., D:]


def pack_dense(qkv_w, out_w, router_w, vectors, up_bias):
    rows = qkv_w.shape[0]
    ub = up_bias.reshape(E, rows, 4).transpose(1, 0, 2).reshape(rows, E * 4)
    return jnp.concatenate([qkv_w, out_w, router_w, vectors.T, ub], 1)


def unpack_dense(packed):
    rows = packed.shape[0]
    w_qkv = packed[:, : 3 * D]
    w_out = packed[:, 3 * D : 4 * D]
    w_router = packed[:, 4 * D : 4 * D + E]
    table = packed[:, 4 * D + E : 4 * D + E + NV].T
    ub = packed[:, 4 * D + E + NV :].reshape(rows, E, 4).transpose(1, 0, 2).reshape(E, rows * 4)
    return w_qkv, w_out, w_router, table, ub


def attention_fwd(w_qkv, w_out, table, value):
    rows = value.shape[0]
    scale = HEAD_DIM ** (-0.5)
    first = layer_norm(value, table[0], table[1]).astype(BF16)
    qkv_bias = jnp.concatenate([table[2], jnp.zeros((D,), F32), table[3]])
    qkv = (dot(first, w_qkv) + qkv_bias).astype(BF16)
    query, key_part, val_part = (
        split_heads(qkv[:, :D]),
        split_heads(qkv[:, D : 2 * D]),
        split_heads(qkv[:, 2 * D :]),
    )
    scores = jnp.einsum("bqhd,bkhd->bhqk", query, key_part, preferred_element_type=F32) * scale
    peak = jnp.max(scores, -1, keepdims=True)
    expo = jnp.exp(scores - peak)
    total = jnp.sum(expo, -1, keepdims=True)
    probs_att = (expo / total).astype(BF16)
    log_total = peak + jnp.log(total)
    attended = jnp.einsum("bhqk,bkhd->bqhd", probs_att, val_part, preferred_element_type=F32)
    attended = attended.reshape(rows, D).astype(BF16)
    resid = value + (dot(attended, w_out) + table[4])
    return first, qkv, log_total, attended, resid


def attention_bwd(w_qkv, w_out, table, value, first, qkv, log_total, attended, d_resid):
    rows = value.shape[0]
    scale = HEAD_DIM ** (-0.5)
    d_branch = d_resid.astype(BF16)
    g_bias_out = jnp.sum(d_branch.astype(F32), 0)
    g_out = lax.dot_general(attended, d_branch, (((0,), (0,)), ((), ())), preferred_element_type=F32)
    d_att = split_heads(
        lax.dot_general(d_branch, w_out, (((1,), (1,)), ((), ())), preferred_element_type=F32).astype(BF16)
    )
    query, key_part, val_part = (
        split_heads(qkv[:, :D]),
        split_heads(qkv[:, D : 2 * D]),
        split_heads(qkv[:, 2 * D :]),
    )
    scores = jnp.einsum("bqhd,bkhd->bhqk", query, key_part, preferred_element_type=F32) * scale
    probs_f = jnp.exp(scores - log_total)
    probs_att = probs_f.astype(BF16)
    d_val = jnp.einsum("bhqk,bqhd->bkhd", probs_att, d_att, preferred_element_type=F32)
    d_prob = jnp.einsum("bqhd,bkhd->bhqk", d_att, val_part, preferred_element_type=F32)
    d_score = (probs_f * (d_prob - jnp.sum(d_prob * probs_f, -1, keepdims=True))).astype(BF16)
    d_query = jnp.einsum("bhqk,bkhd->bqhd", d_score, key_part, preferred_element_type=F32) * scale
    d_key = jnp.einsum("bhqk,bqhd->bkhd", d_score, query, preferred_element_type=F32) * scale
    d_qkv = jnp.concatenate(
        [d_query.reshape(rows, D), d_key.reshape(rows, D), d_val.reshape(rows, D)], 1
    ).astype(BF16)
    d_qkv_f = d_qkv.astype(F32)
    g_bias_q = jnp.sum(d_qkv_f[:, :D], 0)
    g_bias_v = jnp.sum(d_qkv_f[:, 2 * D :], 0)
    g_qkv = lax.dot_general(first, d_qkv, (((0,), (0,)), ((), ())), preferred_element_type=F32)
    d_first = lax.dot_general(d_qkv, w_qkv, (((1,), (1,)), ((), ())), preferred_element_type=F32)
    first_pull = jax.vjp(layer_norm, value, table[0], table[1])[1]
    d_input, g_gain_one, g_shift_one = first_pull(d_first)
    return (g_qkv, g_out, g_bias_out, g_bias_q, g_bias_v, g_gain_one, g_shift_one), d_input


def adamw(weight, moments, grad, rate):
    first = 0.5 * moments[0] + 0.5 * grad
    root = jnp.sqrt(0.5 * moments[1] * moments[1] + 0.5 * grad * grad)
    update = first / (root + 1e-08)
    return (weight - rate * (update + 0.1 * weight), jnp.stack([first, root]))


def shards(
    tokens,
    cotangent,
    expert_index,
    qkv_weight,
    out_weight,
    router_weight,
    up_weight,
    up_bias,
    down_weight,
    vectors,
    qkv_moments,
    out_moments,
    router_moments,
    up_moments,
    up_bias_moments,
    down_moments,
    vector_moments,
):
    rows = tokens.shape[0]
    micro = rows // MB_TOK
    gs = qkv_weight.shape[0]
    group_size = D // gs
    core = lax.axis_index("core")

    dense_in = pack_dense(qkv_weight, out_weight, router_weight, vectors, up_bias)
    width = dense_in.shape[1]
    dense_in = jnp.pad(dense_in, ((0, 0), (0, DENSE_AG - width))).astype(BF16)
    w_up_all, w_down_all, dense = ring_all_gather(
        up_weight.astype(BF16), down_weight.astype(BF16), dense_in, group_size, 1
    )
    w_qkv, w_out, w_router, table_b, b_up_b = unpack_dense(dense[:, :width])
    table = table_b.astype(F32)
    b_up = b_up_b.astype(F32)

    value = tokens.astype(F32)
    d_out = cotangent.astype(F32)
    first, qkv, log_total, attended, resid = attention_fwd(w_qkv, w_out, table, value)
    second = layer_norm(resid, table[5], table[6]).astype(BF16)
    logits = dot(second, w_router)
    probs = jax.nn.softmax(logits, -1)
    picked = expert_index[:, :, None] == jnp.arange(E, dtype=jnp.int32)
    gate = jnp.sum(jnp.where(picked, probs[:, None, :], 0.0), -1)

    route = expert_index.reshape(micro, MB_TOK, 2)
    places, counts = assign_places(route)
    counts = counts.T.reshape(E * micro)
    onehot = (places[:, :, None] == jnp.arange(E * CAPP, dtype=jnp.int32)).astype(BF16)
    second_m = second.reshape(micro, MB_TOK, D)
    pair = jnp.concatenate([second_m, second_m], 1)
    table_in = jnp.einsum("mnr,mnd->mrd", onehot, pair, preferred_element_type=F32).astype(BF16)
    table_in = table_in.reshape(micro, E, CAPP, D).transpose(1, 0, 2, 3).reshape(E, micro * CAPP, D)

    hidden_pre, hidden, y_all = ffn_forward(
        counts, table_in, w_up_all, b_up[:, None, :], w_down_all, table[7 : 7 + E][:, None, :], micro
    )
    y_m = y_all.reshape(E, micro, CAPP, D).transpose(1, 0, 2, 3).reshape(micro, E * CAPP, D)
    picked_rows = pick_rows(onehot, y_m)
    out_zero = picked_rows[:, :MB_TOK].reshape(rows, D)
    out_one = picked_rows[:, MB_TOK:].reshape(rows, D)
    result = resid + (gate[:, 0:1] * out_zero + gate[:, 1:2] * out_one)

    d_gate = jnp.stack([jnp.sum(d_out * out_zero, -1), jnp.sum(d_out * out_one, -1)], 1)
    d_out_m = d_out.reshape(micro, MB_TOK, D)
    gate_m = gate.reshape(micro, MB_TOK, 2)
    weighted = jnp.concatenate([gate_m[:, :, 0:1] * d_out_m, gate_m[:, :, 1:2] * d_out_m], 1).astype(BF16)
    d_expert = jnp.einsum("mnr,mnd->mrd", onehot, weighted, preferred_element_type=F32).astype(BF16)
    d_expert = d_expert.reshape(micro, E, CAPP, D).transpose(1, 0, 2, 3).reshape(E, micro * CAPP, D)
    g_bias_down = jnp.sum(d_expert.astype(F32), 1)

    d_table, g_up, g_down, g_b1 = ffn_backward(counts, d_expert, table_in, hidden_pre, hidden, w_up_all, w_down_all, micro)
    g_up_bias_all = g_b1[:, 0, :]

    d_table_m = d_table.reshape(E, micro, CAPP, D).transpose(1, 0, 2, 3).reshape(micro, E * CAPP, D)
    onehot_sum = onehot[:, :MB_TOK] + onehot[:, MB_TOK:]
    d_picked = pick_rows(onehot_sum, d_table_m).reshape(rows, D)

    d_probs = jnp.sum(jnp.where(picked, d_gate[:, :, None], 0.0), 1)
    d_logit = (probs * (d_probs - jnp.sum(d_probs * probs, -1, keepdims=True))).astype(BF16)
    g_router = lax.dot_general(second, d_logit, (((0,), (0,)), ((), ())), preferred_element_type=F32)
    d_second = d_picked + lax.dot_general(d_logit, w_router, (((1,), (1,)), ((), ())), preferred_element_type=F32)
    norm_pull = jax.vjp(layer_norm, resid, table[5], table[6])[1]
    d_resid, g_gain_two, g_shift_two = norm_pull(d_second)
    d_resid = d_out + d_resid

    att_grads, d_input = attention_bwd(w_qkv, w_out, table, value, first, qkv, log_total, attended, d_resid)
    g_qkv, g_out, g_bias_out, g_bias_q, g_bias_v, g_gain_one, g_shift_one = att_grads
    input_grad = d_resid + d_input

    g_table = jnp.concatenate(
        [
            jnp.stack([g_gain_one, g_shift_one, g_bias_q, g_bias_v, g_bias_out, g_gain_two, g_shift_two]),
            g_bias_down,
        ],
        0,
    )
    dense_g = pack_dense(g_qkv, g_out, g_router, g_table, g_up_bias_all)
    width = dense_g.shape[1]
    dense_g = jnp.pad(dense_g, ((0, 0), (0, DENSE_AG - width))).astype(BF16)
    x_pair = lax.axis_size("rx") == 2
    r_up, r_down, r_dense = grad_reduce(g_up, g_down, dense_g, group_size, x_pair, 0)
    if not x_pair:
        r_up, r_down, r_dense = lax.psum((r_up, r_down, r_dense), "rx")
    r_qkv, r_out, r_router, r_table, r_ub = unpack_dense(r_dense[:, :width])

    reduced = (r_qkv, r_out, r_router, r_up, r_ub, r_down, r_table)
    rates = (
        2.0 * D ** (-0.5),
        2.0 * (D // 32) ** (-0.5),
        2.0 * (2 * D) ** (-0.5),
        2.0 * D ** (-0.5),
        0.2,
        2.0 * (F // 16) ** (-0.5),
        0.2,
    )
    params = (qkv_weight, out_weight, router_weight, up_weight, up_bias, down_weight, vectors)
    moments = (qkv_moments, out_moments, router_moments, up_moments, up_bias_moments, down_moments, vector_moments)
    news = []
    states = []
    for weight, state, grad, rate in zip(params, moments, reduced, rates):
        new_weight, new_state = adamw(weight, state, grad, rate)
        news.append(new_weight)
        states.append(new_state)
    return (result.astype(BF16), input_grad) + reduced + tuple(news) + tuple(states)


def solution(mesh):
    replica, group = mesh.shape["replica"], mesh.shape["group"]
    view = Mesh(np.asarray(mesh.devices).reshape(replica // 2, 2, group), ("rx", "core", "group"))
    in_specs = (
        P(TOK, None),
        P(TOK, None),
        P(TOK, None),
        P("group", None),
        P("group", None),
        P("group", None),
        P(None, "group", None),
        P(None, "group"),
        P(None, "group", None),
        P(None, "group"),
        P(None, "group", None),
        P(None, "group", None),
        P(None, "group", None),
        P(None, None, "group", None),
        P(None, None, "group"),
        P(None, None, "group", None),
        P(None, None, "group"),
    )
    out_specs = (
        P(TOK, None),
        P(TOK, None),
        P("group", None),
        P("group", None),
        P("group", None),
        P(None, "group", None),
        P(None, "group"),
        P(None, "group", None),
        P(None, "group"),
        P("group", None),
        P("group", None),
        P("group", None),
        P(None, "group", None),
        P(None, "group"),
        P(None, "group", None),
        P(None, "group"),
        P(None, "group", None),
        P(None, "group", None),
        P(None, "group", None),
        P(None, None, "group", None),
        P(None, None, "group"),
        P(None, None, "group", None),
        P(None, None, "group"),
    )
    return jax.shard_map(shards, mesh=view, in_specs=in_specs, out_specs=out_specs, check_vma=False)
```

```python
import functools

import jax
import jax.numpy as jnp
import numpy as np
from jax import lax
from jax.sharding import Mesh
from jax.sharding import PartitionSpec as P
from jax.experimental import pallas as pl
from jax.experimental.pallas import tpu as pltpu

D = 512
HEADS = 8
HEAD_DIM = 64
F = 2048
E = 4
S = 197
MB_TOK = 394
CAP = 392
NV = 11
DENSE_AG = 2560
DENSE_PAD = 2304
F32 = jnp.float32
BF16 = jnp.bfloat16
TOK = ("rx", "core", "group")


MESH_ID = pl.DeviceIdType.MESH


def ring_order(groups):
    if groups in (4, 8):
        zs = groups // 2

        def pos_of(g):
            y = g % 2
            z = g // 2
            return z + y * (2 * zs - 1 - 2 * z)

        def dev_at(p):
            p = p % groups
            yy = p // zs
            return 2 * (p + yy * (2 * zs - 1 - 2 * p)) + yy

        return pos_of, dev_at
    return (lambda g: g), (lambda p: p % groups)


def ring_rs_kernel(groups, n_in, *refs):
    ins = refs[:n_in]
    outs = refs[n_in : 2 * n_in]
    rbufs = refs[2 * n_in : 3 * n_in]
    sbufs = refs[3 * n_in : 4 * n_in]
    owns = refs[4 * n_in : 5 * n_in]
    send_sem, recv_sem, load_sem = refs[5 * n_in :]
    pos_of, dev_at = ring_order(groups)
    rx = lax.axis_index("rx")
    core = lax.axis_index("core")
    g = lax.axis_index("group")
    pos = pos_of(g)
    nbr = (dev_at(pos + 1), dev_at(pos + groups - 1))

    barrier = pltpu.get_barrier_semaphore()
    for n in nbr:
        pl.semaphore_signal(barrier, inc=1, device_id=(rx, core, n), device_id_type=MESH_ID)
    pl.semaphore_wait(barrier, 2)

    def block_dev(d, s):
        if d == 0:
            return dev_at(pos + 2 * groups - s - 1)
        return dev_at(pos + s + 1)

    def load(d, s, slot):
        b = block_dev(d, s)
        copies = []
        for i in range(n_in):
            rows = ins[i].shape[1] // groups
            half = ins[i].shape[2] // 2
            src = ins[i].at[:, pl.ds(pl.multiple_of(b * rows, rows), rows), pl.ds(d * half, half)]
            copies.append(pltpu.make_async_copy(src, owns[i].at[d, slot], load_sem.at[d, slot, i]))
        return copies

    def remote(d, s, i):
        return pltpu.make_async_remote_copy(
            src_ref=sbufs[i].at[d, s],
            dst_ref=rbufs[i].at[d, s],
            send_sem=send_sem.at[d, s, i],
            recv_sem=recv_sem.at[d, s, i],
            device_id=(rx, core, nbr[d]),
            device_id_type=MESH_ID,
        )

    for d in range(2):
        for c in load(d, 0, 0):
            c.start()
    sends = []
    for s in range(groups):
        slot = s % 2
        for d in range(2):
            for c in load(d, s, slot):
                c.wait()
            if s + 1 < groups:
                for c in load(d, s + 1, 1 - slot):
                    c.start()
            for i in range(n_in):
                if s > 0:
                    remote(d, s - 1, i).wait_recv()
                for a in range(ins[i].shape[0]):
                    mine = owns[i][d, slot, a].astype(F32)
                    if s > 0:
                        mine = mine + rbufs[i][d, s - 1, a].astype(F32)
                    if s < groups - 1:
                        sbufs[i][d, s, a] = mine.astype(sbufs[i].dtype)
                    else:
                        half = ins[i].shape[2] // 2
                        outs[i][a, :, pl.ds(d * half, half)] = mine.astype(outs[i].dtype)
                if s < groups - 1:
                    c = remote(d, s, i)
                    c.start()
                    sends.append(c)
    for c in sends:
        c.wait_send()


def ring_reduce_scatter(xs, groups, collective_id):
    n_in = len(xs)
    outs, rb, own = [], [], []
    flops = 0
    nbytes = 0
    for x in xs:
        a, total, c = x.shape
        rows = total // groups
        outs.append(jax.ShapeDtypeStruct((a, rows, c), x.dtype))
        rb.append(pltpu.VMEM((2, groups - 1, a, rows, c // 2), x.dtype))
        own.append(pltpu.VMEM((2, 2, a, rows, c // 2), x.dtype))
        flops += a * total * c
        nbytes += 3 * x.size * x.dtype.itemsize
    scratch = rb + rb + own + [
        pltpu.SemaphoreType.DMA((2, groups - 1, n_in)),
        pltpu.SemaphoreType.DMA((2, groups - 1, n_in)),
        pltpu.SemaphoreType.DMA((2, 2, n_in)),
    ]
    return pl.pallas_call(
        functools.partial(ring_rs_kernel, groups, n_in),
        out_shape=outs,
        in_specs=[pl.BlockSpec(memory_space=pl.ANY)] * n_in,
        out_specs=[pl.BlockSpec(memory_space=pltpu.VMEM)] * n_in,
        scratch_shapes=scratch,
        compiler_params=pltpu.CompilerParams(
            collective_id=collective_id, has_side_effects=True, vmem_limit_bytes=60 * 1024 * 1024
        ),
        cost_estimate=pl.CostEstimate(flops=flops, bytes_accessed=nbytes, transcendentals=0),
    )(*xs)


def ring_ag_kernel(groups, *refs):
    in_up, in_down, in_dense, out_up, out_down, out_dense = refs[:6]
    ring_send, ring_recv, part_send, part_recv, local_sem = refs[6:]
    pos_of, dev_at = ring_order(groups)
    rx = lax.axis_index("rx")
    core = lax.axis_index("core")
    g = lax.axis_index("group")
    other = 1 - core
    pos = pos_of(g)
    nbr = (dev_at(pos + 1), dev_at(pos + groups - 1))
    gs = in_up.shape[1]
    fs = in_down.shape[1]
    width = in_dense.shape[1] // 2

    barrier = pltpu.get_barrier_semaphore()
    for n in nbr:
        pl.semaphore_signal(barrier, inc=1, device_id=(rx, core, n), device_id_type=MESH_ID)
    pl.semaphore_signal(barrier, inc=1, device_id=(rx, other, g), device_id_type=MESH_ID)
    pl.semaphore_wait(barrier, 3)

    def items(owner):
        found = []
        for k in range(2):
            e = 2 * k + owner
            found.append((in_up.at[e], lambda b, e=e: out_up.at[e, pl.ds(pl.multiple_of(b * gs, gs), gs)], F // 2))
            found.append((in_down.at[e], lambda b, e=e: out_down.at[e, pl.ds(pl.multiple_of(b * fs, fs), fs)], D // 2))
        dense_in = in_dense.at[:, pl.ds(owner * width, width)]
        found.append(
            (dense_in, lambda b: out_dense.at[pl.ds(pl.multiple_of(b * gs, gs), gs), pl.ds(owner * width, width)], width // 2)
        )
        return found

    mine = items(core)
    theirs = items(other)
    n_items = len(mine)

    locals_ = [pltpu.make_async_copy(in_up.at[e], out_up.at[e, pl.ds(pl.multiple_of(g * gs, gs), gs)], local_sem.at[e]) for e in range(E)]
    locals_ += [
        pltpu.make_async_copy(in_down.at[e], out_down.at[e, pl.ds(pl.multiple_of(g * fs, fs), fs)], local_sem.at[E + e])
        for e in range(E)
    ]
    locals_.append(pltpu.make_async_copy(in_dense, out_dense.at[pl.ds(pl.multiple_of(g * gs, gs), gs)], local_sem.at[2 * E]))
    for c in locals_:
        c.start()

    def block_at(d, s):
        if d == 0:
            return dev_at(pos + 2 * groups - 1 - s)
        return dev_at(pos + 1 + s)

    def ring_copy(d, s, j, src_block):
        src_in, dst_of, half = mine[j]
        cols = pl.ds(d * half, half)
        if src_block is None:
            src = src_in.at[:, cols]
            dst = dst_of(g).at[:, cols]
        else:
            src = dst_of(src_block).at[:, cols]
            dst = src
        return pltpu.make_async_remote_copy(
            src_ref=src, dst_ref=dst, send_sem=ring_send.at[d, s, j], recv_sem=ring_recv.at[d, s, j],
            device_id=(rx, core, nbr[d]), device_id_type=MESH_ID,
        )

    def part_copy(d, s, j, table, block):
        _, dst_of, half = table[j]
        view = dst_of(block).at[:, pl.ds(d * half, half)]
        return pltpu.make_async_remote_copy(
            src_ref=view, dst_ref=view, send_sem=part_send.at[d, s, j], recv_sem=part_recv.at[d, s, j],
            device_id=(rx, other, g), device_id_type=MESH_ID,
        )

    sends = []
    for d in range(2):
        for j in range(n_items):
            c = ring_copy(d, 0, j, None)
            c.start()
            sends.append(c)
    for s in range(groups - 1):
        for d in range(2):
            b = block_at(d, s)
            for j in range(n_items):
                pltpu.make_async_remote_copy(
                    src_ref=mine[j][1](b).at[:, pl.ds(d * mine[j][2], mine[j][2])],
                    dst_ref=mine[j][1](b).at[:, pl.ds(d * mine[j][2], mine[j][2])],
                    send_sem=ring_send.at[d, s, j], recv_sem=ring_recv.at[d, s, j],
                    device_id=(rx, core, nbr[d]), device_id_type=MESH_ID,
                ).wait_recv()
                if s + 1 < groups - 1:
                    c = ring_copy(d, s + 1, j, b)
                    c.start()
                    sends.append(c)
                c = part_copy(d, s, j, mine, b)
                c.start()
                sends.append(c)
    for s in range(groups - 1):
        for d in range(2):
            b = block_at(d, s)
            for j in range(n_items):
                part_copy(d, s, j, theirs, b).wait_recv()
    for c in sends:
        c.wait_send()
    for c in locals_:
        c.wait()


def ring_all_gather(up_b, down_b, dense_b, groups, collective_id):
    n_items = 5
    gs = up_b.shape[1]
    shapes = [
        jax.ShapeDtypeStruct((E, gs * groups, F), BF16),
        jax.ShapeDtypeStruct((E, down_b.shape[1] * groups, D), BF16),
        jax.ShapeDtypeStruct((gs * groups, dense_b.shape[1]), BF16),
    ]
    nbytes = sum(int(np.prod(s.shape)) * 2 for s in shapes)
    return pl.pallas_call(
        functools.partial(ring_ag_kernel, groups),
        out_shape=shapes,
        in_specs=[pl.BlockSpec(memory_space=pl.ANY)] * 3,
        out_specs=[pl.BlockSpec(memory_space=pl.ANY)] * 3,
        scratch_shapes=[
            pltpu.SemaphoreType.DMA((2, groups - 1, n_items)),
            pltpu.SemaphoreType.DMA((2, groups - 1, n_items)),
            pltpu.SemaphoreType.DMA((2, groups - 1, n_items)),
            pltpu.SemaphoreType.DMA((2, groups - 1, n_items)),
            pltpu.SemaphoreType.DMA((2 * E + 1,)),
        ],
        compiler_params=pltpu.CompilerParams(collective_id=collective_id, has_side_effects=True),
        cost_estimate=pl.CostEstimate(flops=0, bytes_accessed=nbytes, transcendentals=0),
    )(up_b, down_b, dense_b)


def grad_items(gu, gd, gdense, owner, gs, fs, width):
    found = []
    for k in range(2):
        e = 2 * k + owner
        found.append((lambda b, e=e: gu.at[e, pl.ds(pl.multiple_of(b * gs, gs), gs)], F // 2))
        found.append((lambda b, e=e: gd.at[e, pl.ds(pl.multiple_of(b * fs, fs), fs)], D // 2))
    found.append((lambda b: gdense.at[pl.ds(pl.multiple_of(b * gs, gs), gs), pl.ds(owner * width, width)], width // 2))
    return found


def ring_rs2_kernel(groups, x_pair, *refs):
    gu, gd, gdense, out_up, out_down, out_dense = refs[:6]
    n_items = 5
    scr = refs[6:]
    rbuf, sbuf, pbuf, own, fin, xr, cr = (scr[i * n_items : (i + 1) * n_items] for i in range(7))
    ring_send, ring_recv, part_send, part_recv, load_sem, x_send, x_recv, c_send, c_recv = scr[7 * n_items :]
    pos_of, dev_at = ring_order(groups)
    rx = lax.axis_index("rx")
    core = lax.axis_index("core")
    g = lax.axis_index("group")
    other = 1 - core
    pos = pos_of(g)
    nbr = (dev_at(pos + 1), dev_at(pos + groups - 1))
    gs = gu.shape[1] // groups
    fs = gd.shape[1] // groups
    width = gdense.shape[1] // 2
    mine = grad_items(gu, gd, gdense, core, gs, fs, width)
    theirs = grad_items(gu, gd, gdense, other, gs, fs, width)

    barrier = pltpu.get_barrier_semaphore()
    for n in nbr:
        pl.semaphore_signal(barrier, inc=1, device_id=(rx, core, n), device_id_type=MESH_ID)
    pl.semaphore_signal(barrier, inc=1, device_id=(rx, other, g), device_id_type=MESH_ID)
    count = 3
    if x_pair:
        pl.semaphore_signal(barrier, inc=1, device_id=(1 - rx, core, g), device_id_type=MESH_ID)
        count = 4
    pl.semaphore_wait(barrier, count)

    def block_at(d, s):
        if d == 0:
            return dev_at(pos + 2 * groups - 1 - s)
        return dev_at(pos + 1 + s)

    def cols(j, d):
        half = mine[j][1]
        return pl.ds(d * half, half)

    def load(d, s, slot, j):
        return pltpu.make_async_copy(mine[j][0](block_at(d, s)).at[:, cols(j, d)], own[j].at[d, slot], load_sem.at[d, slot, j])

    def part(d, s, j):
        return pltpu.make_async_remote_copy(
            src_ref=theirs[j][0](block_at(d, s)).at[:, cols(j, d)], dst_ref=pbuf[j].at[d, s],
            send_sem=part_send.at[d, s, j], recv_sem=part_recv.at[d, s, j],
            device_id=(rx, other, g), device_id_type=MESH_ID,
        )

    def ring(d, s, j):
        return pltpu.make_async_remote_copy(
            src_ref=sbuf[j].at[d, s], dst_ref=rbuf[j].at[d, s],
            send_sem=ring_send.at[d, s, j], recv_sem=ring_recv.at[d, s, j],
            device_id=(rx, core, nbr[d]), device_id_type=MESH_ID,
        )

    sends = []
    for d in range(2):
        for j in range(n_items):
            load(d, 0, 0, j).start()
            c = part(d, 0, j)
            c.start()
            sends.append(c)
    for s in range(groups):
        slot = s % 2
        for d in range(2):
            for j in range(n_items):
                load(d, s, slot, j).wait()
                if s + 1 < groups:
                    load(d, s + 1, 1 - slot, j).start()
                    c = part(d, s + 1, j)
                    c.start()
                    sends.append(c)
                part(d, s, j).wait_recv()
                val = own[j][d, slot].astype(F32) + pbuf[j][d, s].astype(F32)
                if s > 0:
                    ring(d, s - 1, j).wait_recv()
                    val = val + rbuf[j][d, s - 1].astype(F32)
                if s < groups - 1:
                    sbuf[j][d, s] = val.astype(BF16)
                    c = ring(d, s, j)
                    c.start()
                    sends.append(c)
                else:
                    fin[j][d] = val

    for c in sends:
        c.wait_send()
    sends = []
    if x_pair:
        x_copies = []
        for d in range(2):
            for j in range(n_items):
                sbuf[j][d, 0] = fin[j][d].astype(BF16)
                c = pltpu.make_async_remote_copy(
                    src_ref=sbuf[j].at[d, 0], dst_ref=xr[j].at[d], send_sem=x_send.at[d, j], recv_sem=x_recv.at[d, j],
                    device_id=(1 - rx, core, g), device_id_type=MESH_ID,
                )
                c.start()
                x_copies.append(c)
        for c in x_copies:
            c.wait_recv()
        for d in range(2):
            for j in range(n_items):
                fin[j][d] = sbuf[j][d, 0].astype(F32) + xr[j][d].astype(F32)
        sends += x_copies

    c_copies = []
    for d in range(2):
        for j in range(n_items):
            c = pltpu.make_async_remote_copy(
                src_ref=fin[j].at[d], dst_ref=cr[j].at[d], send_sem=c_send.at[d, j], recv_sem=c_recv.at[d, j],
                device_id=(rx, other, g), device_id_type=MESH_ID,
            )
            c.start()
            c_copies.append(c)

    def out_items(owner):
        found = []
        for k in range(2):
            e = 2 * k + owner
            found.append(lambda d, e=e: out_up.at[e, :, pl.ds(d * (F // 2), F // 2)])
            found.append(lambda d, e=e: out_down.at[e, :, pl.ds(d * (D // 2), D // 2)])
        found.append(lambda d: out_dense.at[:, pl.ds(owner * width + d * (width // 2), width // 2)])
        return found

    mine_out = out_items(core)
    theirs_out = out_items(other)
    for d in range(2):
        for j in range(n_items):
            mine_out[j](d)[...] = fin[j][d]
    for c in c_copies:
        c.wait_recv()
    for d in range(2):
        for j in range(n_items):
            theirs_out[j](d)[...] = cr[j][d]
    for c in sends + c_copies:
        c.wait_send()


def grad_reduce(gu, gd, gdense, groups, x_pair, collective_id):
    gs = gu.shape[1] // groups
    fs = gd.shape[1] // groups
    width = gdense.shape[1] // 2
    item_shapes = [(gs, F // 2), (fs, D // 2), (gs, F // 2), (fs, D // 2), (gs, width // 2)]
    scratch = []
    for lead, dtype in (((2, groups - 1), BF16), ((2, groups - 1), BF16), ((2, groups), BF16), ((2, 2), BF16), ((2,), F32), ((2,), BF16), ((2,), F32)):
        scratch += [pltpu.VMEM(lead + shp, dtype) for shp in item_shapes]
    scratch += [
        pltpu.SemaphoreType.DMA((2, groups - 1, 5)),
        pltpu.SemaphoreType.DMA((2, groups - 1, 5)),
        pltpu.SemaphoreType.DMA((2, groups, 5)),
        pltpu.SemaphoreType.DMA((2, groups, 5)),
        pltpu.SemaphoreType.DMA((2, 2, 5)),
        pltpu.SemaphoreType.DMA((2, 5)),
        pltpu.SemaphoreType.DMA((2, 5)),
        pltpu.SemaphoreType.DMA((2, 5)),
        pltpu.SemaphoreType.DMA((2, 5)),
    ]
    outs = [
        jax.ShapeDtypeStruct((E, gs, F), F32),
        jax.ShapeDtypeStruct((E, fs, D), F32),
        jax.ShapeDtypeStruct((gs, gdense.shape[1]), F32),
    ]
    nbytes = 2 * (gu.size + gd.size + gdense.size)
    return pl.pallas_call(
        functools.partial(ring_rs2_kernel, groups, x_pair),
        out_shape=outs,
        in_specs=[pl.BlockSpec(memory_space=pl.ANY)] * 3,
        out_specs=[pl.BlockSpec(memory_space=pltpu.VMEM)] * 3,
        scratch_shapes=scratch,
        compiler_params=pltpu.CompilerParams(
            collective_id=collective_id, has_side_effects=True, vmem_limit_bytes=62 * 1024 * 1024
        ),
        cost_estimate=pl.CostEstimate(flops=gu.size + gd.size + gdense.size, bytes_accessed=nbytes, transcendentals=0),
    )(gu, gd, gdense)


TILE = 128
TILE_B = 256
CAPP = 512
SQRT_HALF = float(np.sqrt(0.5))
INV_SQRT_2PI = float(1.0 / np.sqrt(2.0 * np.pi))


def ffn_fwd_kernel(micro, counts, x_ref, w1_ref, b1_ref, w2_ref, b2_ref, hp_ref, h_ref, y_ref):
    e, m, t = pl.program_id(0), pl.program_id(1), pl.program_id(2)
    active = t * TILE < counts[e * micro + m]

    @pl.when(active)
    def _():
        hp = jnp.dot(x_ref[0], w1_ref[0], preferred_element_type=F32) + b1_ref[0]
        h = (0.5 * hp * (1.0 + lax.erf(hp * SQRT_HALF))).astype(BF16)
        hp_ref[0] = hp
        h_ref[0] = h
        y_ref[0] = jnp.dot(h, w2_ref[0], preferred_element_type=F32) + b2_ref[0]

    @pl.when(jnp.logical_not(active))
    def _():
        y_ref[0] = jnp.zeros(y_ref.shape[1:], F32)


def ffn_forward(counts, table_in, w1, b1, w2, b2, micro):
    tiles = CAPP // TILE
    rows = table_in.shape[1]
    row_map = lambda e, m, t, c: (m, e * tiles + t, 0)
    w_map = lambda e, m, t, c: (e, 0, 0)
    grid_spec = pltpu.PrefetchScalarGridSpec(
        num_scalar_prefetch=1,
        grid=(E, micro, tiles),
        in_specs=[
            pl.BlockSpec((1, TILE, D), row_map),
            pl.BlockSpec((1, D, F), w_map),
            pl.BlockSpec((1, 1, F), w_map),
            pl.BlockSpec((1, F, D), w_map),
            pl.BlockSpec((1, 1, D), w_map),
        ],
        out_specs=[
            pl.BlockSpec((1, TILE, F), row_map),
            pl.BlockSpec((1, TILE, F), row_map),
            pl.BlockSpec((1, TILE, D), row_map),
        ],
    )
    work = micro * rows
    return pl.pallas_call(
        functools.partial(ffn_fwd_kernel, micro),
        grid_spec=grid_spec,
        out_shape=[
            jax.ShapeDtypeStruct((micro, rows, F), F32),
            jax.ShapeDtypeStruct((micro, rows, F), BF16),
            jax.ShapeDtypeStruct((micro, rows, D), F32),
        ],
        compiler_params=pltpu.CompilerParams(vmem_limit_bytes=48 * 1024 * 1024),
        cost_estimate=pl.CostEstimate(
            flops=4 * work * D * F // 2, bytes_accessed=work * (2 * D + 6 * F + 4 * D) // 2, transcendentals=work * F // 2
        ),
    )(counts, table_in, w1, b1, w2, b2)


def ffn_bwd_kernel(micro, counts, dy_ref, x_ref, hp_ref, h_ref, w1_ref, w2_ref, dt_ref, gu_ref, gd_ref, gb_ref, gu_acc, gd_acc):
    e, m, t = pl.program_id(0), pl.program_id(1), pl.program_id(2)
    active = t * TILE_B < counts[e * micro + m]

    @pl.when((m == 0) & (t == 0))
    def _():
        gu_acc[...] = jnp.zeros(gu_acc.shape, F32)
        gd_acc[...] = jnp.zeros(gd_acc.shape, F32)
        gb_ref[...] = jnp.zeros(gb_ref.shape, F32)

    @pl.when(active)
    def _():
        dy = dy_ref[0]
        hp = hp_ref[0]
        d_hidden = lax.dot_general(dy, w2_ref[0], (((1,), (1,)), ((), ())), preferred_element_type=F32)
        slope = 0.5 * (1.0 + lax.erf(hp * SQRT_HALF)) + hp * jnp.exp(-0.5 * hp * hp) * INV_SQRT_2PI
        d_pre = (d_hidden * slope).astype(BF16)
        dt_ref[0] = lax.dot_general(d_pre, w1_ref[0], (((1,), (1,)), ((), ())), preferred_element_type=F32)
        gu_acc[...] += lax.dot_general(x_ref[0], d_pre, (((0,), (0,)), ((), ())), preferred_element_type=F32)
        gd_acc[...] += lax.dot_general(h_ref[0], dy, (((0,), (0,)), ((), ())), preferred_element_type=F32)
        gb_ref[0] += jnp.sum(d_pre.astype(F32), 0, keepdims=True)

    @pl.when(jnp.logical_not(active))
    def _():
        dt_ref[0] = jnp.zeros(dt_ref.shape[1:], F32)

    @pl.when((m == micro - 1) & (t == pl.num_programs(2) - 1))
    def _():
        gu_ref[0] = gu_acc[...].astype(BF16)
        gd_ref[0] = gd_acc[...].astype(BF16)


def ffn_backward(counts, d_expert, table_in, hp, h, w1, w2, micro):
    tiles = CAPP // TILE_B
    rows = table_in.shape[1]
    row_map = lambda e, m, t, c: (m, e * tiles + t, 0)
    w_map = lambda e, m, t, c: (e, 0, 0)
    grid_spec = pltpu.PrefetchScalarGridSpec(
        num_scalar_prefetch=1,
        grid=(E, micro, tiles),
        in_specs=[
            pl.BlockSpec((1, TILE_B, D), row_map),
            pl.BlockSpec((1, TILE_B, D), row_map),
            pl.BlockSpec((1, TILE_B, F), row_map),
            pl.BlockSpec((1, TILE_B, F), row_map),
            pl.BlockSpec((1, D, F), w_map),
            pl.BlockSpec((1, F, D), w_map),
        ],
        out_specs=[
            pl.BlockSpec((1, TILE_B, D), row_map),
            pl.BlockSpec((1, D, F), w_map),
            pl.BlockSpec((1, F, D), w_map),
            pl.BlockSpec((1, 1, F), w_map),
        ],
        scratch_shapes=[pltpu.VMEM((D, F), F32), pltpu.VMEM((F, D), F32)],
    )
    work = micro * rows
    return pl.pallas_call(
        functools.partial(ffn_bwd_kernel, micro),
        grid_spec=grid_spec,
        out_shape=[
            jax.ShapeDtypeStruct((micro, rows, D), F32),
            jax.ShapeDtypeStruct((E, D, F), BF16),
            jax.ShapeDtypeStruct((E, F, D), BF16),
            jax.ShapeDtypeStruct((E, 1, F), F32),
        ],
        compiler_params=pltpu.CompilerParams(vmem_limit_bytes=60 * 1024 * 1024),
        cost_estimate=pl.CostEstimate(
            flops=8 * work * D * F // 2, bytes_accessed=work * (8 * D + 6 * F) // 2 + 16 * E * D * F, transcendentals=2 * work * F // 2
        ),
    )(counts, d_expert, table_in, hp, h, w1, w2)

def layer_norm(value, gain, shift):
    center = value - jnp.mean(value, -1, keepdims=True)
    spread = jnp.mean(center * center, -1, keepdims=True)
    return center * lax.rsqrt(spread + 1e-06) * gain + shift


def gelu_exact(value):
    return jax.nn.gelu(value, approximate=False)


def split_heads(part):
    return part.reshape(-1, S, HEADS, HEAD_DIM)


def dot(a, b):
    return jnp.dot(a, b, preferred_element_type=F32)


def assign_places(route):
    chosen = jnp.concatenate([route[:, :, 0], route[:, :, 1]], 1)
    hits = (chosen[:, :, None] == jnp.arange(E, dtype=jnp.int32)).astype(jnp.int32)
    before = jnp.cumsum(hits, 1) - hits
    slot = jnp.sum(before * hits, 2)
    return chosen * CAPP + slot, jnp.sum(hits, 1)


def hi_lo(v):
    hi = v.astype(BF16)
    lo = (v - hi.astype(F32)).astype(BF16)
    return jnp.concatenate([hi, lo], -1)


def pick_rows(onehot, table):
    both = jnp.einsum("mnr,mrd->mnd", onehot, hi_lo(table), preferred_element_type=F32)
    return both[..., :D] + both[..., D:]


def pack_dense(qkv_w, out_w, router_w, vectors, up_bias):
    rows = qkv_w.shape[0]
    ub = up_bias.reshape(E, rows, 4).transpose(1, 0, 2).reshape(rows, E * 4)
    return jnp.concatenate([qkv_w, out_w, router_w, vectors.T, ub], 1)


def unpack_dense(packed):
    rows = packed.shape[0]
    w_qkv = packed[:, : 3 * D]
    w_out = packed[:, 3 * D : 4 * D]
    w_router = packed[:, 4 * D : 4 * D + E]
    table = packed[:, 4 * D + E : 4 * D + E + NV].T
    ub = packed[:, 4 * D + E + NV :].reshape(rows, E, 4).transpose(1, 0, 2).reshape(E, rows * 4)
    return w_qkv, w_out, w_router, table, ub


def attention_fwd(w_qkv, w_out, table, value):
    rows = value.shape[0]
    scale = HEAD_DIM ** (-0.5)
    first = layer_norm(value, table[0], table[1]).astype(BF16)
    qkv_bias = jnp.concatenate([table[2], jnp.zeros((D,), F32), table[3]])
    qkv = (dot(first, w_qkv) + qkv_bias).astype(BF16)
    query, key_part, val_part = (
        split_heads(qkv[:, :D]),
        split_heads(qkv[:, D : 2 * D]),
        split_heads(qkv[:, 2 * D :]),
    )
    scores = jnp.einsum("bqhd,bkhd->bhqk", query, key_part, preferred_element_type=F32) * scale
    peak = jnp.max(scores, -1, keepdims=True)
    expo = jnp.exp(scores - peak)
    total = jnp.sum(expo, -1, keepdims=True)
    probs_att = (expo / total).astype(BF16)
    log_total = peak + jnp.log(total)
    attended = jnp.einsum("bhqk,bkhd->bqhd", probs_att, val_part, preferred_element_type=F32)
    attended = attended.reshape(rows, D).astype(BF16)
    resid = value + (dot(attended, w_out) + table[4])
    return first, qkv, log_total, attended, resid


def attention_bwd(w_qkv, w_out, table, value, first, qkv, log_total, attended, d_resid):
    rows = value.shape[0]
    scale = HEAD_DIM ** (-0.5)
    d_branch = d_resid.astype(BF16)
    g_bias_out = jnp.sum(d_branch.astype(F32), 0)
    g_out = lax.dot_general(attended, d_branch, (((0,), (0,)), ((), ())), preferred_element_type=F32)
    d_att = split_heads(
        lax.dot_general(d_branch, w_out, (((1,), (1,)), ((), ())), preferred_element_type=F32).astype(BF16)
    )
    query, key_part, val_part = (
        split_heads(qkv[:, :D]),
        split_heads(qkv[:, D : 2 * D]),
        split_heads(qkv[:, 2 * D :]),
    )
    scores = jnp.einsum("bqhd,bkhd->bhqk", query, key_part, preferred_element_type=F32) * scale
    probs_f = jnp.exp(scores - log_total)
    probs_att = probs_f.astype(BF16)
    d_val = jnp.einsum("bhqk,bqhd->bkhd", probs_att, d_att, preferred_element_type=F32)
    d_prob = jnp.einsum("bqhd,bkhd->bhqk", d_att, val_part, preferred_element_type=F32)
    d_score = (probs_f * (d_prob - jnp.sum(d_prob * probs_f, -1, keepdims=True))).astype(BF16)
    d_query = jnp.einsum("bhqk,bkhd->bqhd", d_score, key_part, preferred_element_type=F32) * scale
    d_key = jnp.einsum("bhqk,bqhd->bkhd", d_score, query, preferred_element_type=F32) * scale
    d_qkv = jnp.concatenate(
        [d_query.reshape(rows, D), d_key.reshape(rows, D), d_val.reshape(rows, D)], 1
    ).astype(BF16)
    d_qkv_f = d_qkv.astype(F32)
    g_bias_q = jnp.sum(d_qkv_f[:, :D], 0)
    g_bias_v = jnp.sum(d_qkv_f[:, 2 * D :], 0)
    g_qkv = lax.dot_general(first, d_qkv, (((0,), (0,)), ((), ())), preferred_element_type=F32)
    d_first = lax.dot_general(d_qkv, w_qkv, (((1,), (1,)), ((), ())), preferred_element_type=F32)
    first_pull = jax.vjp(layer_norm, value, table[0], table[1])[1]
    d_input, g_gain_one, g_shift_one = first_pull(d_first)
    return (g_qkv, g_out, g_bias_out, g_bias_q, g_bias_v, g_gain_one, g_shift_one), d_input


def adamw(weight, moments, grad, rate):
    first = 0.5 * moments[0] + 0.5 * grad
    root = jnp.sqrt(0.5 * moments[1] * moments[1] + 0.5 * grad * grad)
    update = first / (root + 1e-08)
    return (weight - rate * (update + 0.1 * weight), jnp.stack([first, root]))


def shards(
    tokens,
    cotangent,
    expert_index,
    qkv_weight,
    out_weight,
    router_weight,
    up_weight,
    up_bias,
    down_weight,
    vectors,
    qkv_moments,
    out_moments,
    router_moments,
    up_moments,
    up_bias_moments,
    down_moments,
    vector_moments,
):
    rows = tokens.shape[0]
    micro = rows // MB_TOK
    gs = qkv_weight.shape[0]
    group_size = D // gs
    core = lax.axis_index("core")

    dense_in = pack_dense(qkv_weight, out_weight, router_weight, vectors, up_bias)
    width = dense_in.shape[1]
    dense_in = jnp.pad(dense_in, ((0, 0), (0, DENSE_AG - width))).astype(BF16)
    w_up_all, w_down_all, dense = ring_all_gather(
        up_weight.astype(BF16), down_weight.astype(BF16), dense_in, group_size, 1
    )
    w_qkv, w_out, w_router, table_b, b_up_b = unpack_dense(dense[:, :width])
    table = table_b.astype(F32)
    b_up = b_up_b.astype(F32)

    value = tokens.astype(F32)
    d_out = cotangent.astype(F32)
    first, qkv, log_total, attended, resid = attention_fwd(w_qkv, w_out, table, value)
    second = layer_norm(resid, table[5], table[6]).astype(BF16)
    logits = dot(second, w_router)
    probs = jax.nn.softmax(logits, -1)
    picked = expert_index[:, :, None] == jnp.arange(E, dtype=jnp.int32)
    gate = jnp.sum(jnp.where(picked, probs[:, None, :], 0.0), -1)

    route = expert_index.reshape(micro, MB_TOK, 2)
    places, counts = assign_places(route)
    counts = counts.T.reshape(E * micro)
    onehot = (places[:, :, None] == jnp.arange(E * CAPP, dtype=jnp.int32)).astype(BF16)
    second_m = second.reshape(micro, MB_TOK, D)
    pair = jnp.concatenate([second_m, second_m], 1)
    table_in = jnp.einsum("mnr,mnd->mrd", onehot, pair, preferred_element_type=F32).astype(BF16)

    hidden_pre, hidden, y_all = ffn_forward(
        counts, table_in, w_up_all, b_up[:, None, :], w_down_all, table[7 : 7 + E][:, None, :], micro
    )
    picked_rows = pick_rows(onehot, y_all)
    out_zero = picked_rows[:, :MB_TOK].reshape(rows, D)
    out_one = picked_rows[:, MB_TOK:].reshape(rows, D)
    result = resid + (gate[:, 0:1] * out_zero + gate[:, 1:2] * out_one)

    d_gate = jnp.stack([jnp.sum(d_out * out_zero, -1), jnp.sum(d_out * out_one, -1)], 1)
    d_out_m = d_out.reshape(micro, MB_TOK, D)
    gate_m = gate.reshape(micro, MB_TOK, 2)
    weighted = jnp.concatenate([gate_m[:, :, 0:1] * d_out_m, gate_m[:, :, 1:2] * d_out_m], 1).astype(BF16)
    d_expert = jnp.einsum("mnr,mnd->mrd", onehot, weighted, preferred_element_type=F32).astype(BF16)
    g_bias_down = jnp.sum(d_expert.astype(F32).reshape(micro, E, CAPP, D), (0, 2))

    d_table, g_up, g_down, g_b1 = ffn_backward(counts, d_expert, table_in, hidden_pre, hidden, w_up_all, w_down_all, micro)
    g_up_bias_all = g_b1[:, 0, :]

    onehot_sum = onehot[:, :MB_TOK] + onehot[:, MB_TOK:]
    d_picked = pick_rows(onehot_sum, d_table).reshape(rows, D)

    d_probs = jnp.sum(jnp.where(picked, d_gate[:, :, None], 0.0), 1)
    d_logit = (probs * (d_probs - jnp.sum(d_probs * probs, -1, keepdims=True))).astype(BF16)
    g_router = lax.dot_general(second, d_logit, (((0,), (0,)), ((), ())), preferred_element_type=F32)
    d_second = d_picked + lax.dot_general(d_logit, w_router, (((1,), (1,)), ((), ())), preferred_element_type=F32)
    norm_pull = jax.vjp(layer_norm, resid, table[5], table[6])[1]
    d_resid, g_gain_two, g_shift_two = norm_pull(d_second)
    d_resid = d_out + d_resid

    att_grads, d_input = attention_bwd(w_qkv, w_out, table, value, first, qkv, log_total, attended, d_resid)
    g_qkv, g_out, g_bias_out, g_bias_q, g_bias_v, g_gain_one, g_shift_one = att_grads
    input_grad = d_resid + d_input

    g_table = jnp.concatenate(
        [
            jnp.stack([g_gain_one, g_shift_one, g_bias_q, g_bias_v, g_bias_out, g_gain_two, g_shift_two]),
            g_bias_down,
        ],
        0,
    )
    dense_g = pack_dense(g_qkv, g_out, g_router, g_table, g_up_bias_all)
    width = dense_g.shape[1]
    dense_g = jnp.pad(dense_g, ((0, 0), (0, DENSE_AG - width))).astype(BF16)
    x_pair = lax.axis_size("rx") == 2
    r_up, r_down, r_dense = grad_reduce(g_up, g_down, dense_g, group_size, x_pair, 0)
    if not x_pair:
        r_up, r_down, r_dense = lax.psum((r_up, r_down, r_dense), "rx")
    r_qkv, r_out, r_router, r_table, r_ub = unpack_dense(r_dense[:, :width])

    reduced = (r_qkv, r_out, r_router, r_up, r_ub, r_down, r_table)
    rates = (
        2.0 * D ** (-0.5),
        2.0 * (D // 32) ** (-0.5),
        2.0 * (2 * D) ** (-0.5),
        2.0 * D ** (-0.5),
        0.2,
        2.0 * (F // 16) ** (-0.5),
        0.2,
    )
    params = (qkv_weight, out_weight, router_weight, up_weight, up_bias, down_weight, vectors)
    moments = (qkv_moments, out_moments, router_moments, up_moments, up_bias_moments, down_moments, vector_moments)
    news = []
    states = []
    for weight, state, grad, rate in zip(params, moments, reduced, rates):
        new_weight, new_state = adamw(weight, state, grad, rate)
        news.append(new_weight)
        states.append(new_state)
    return (result.astype(BF16), input_grad) + reduced + tuple(news) + tuple(states)


def solution(mesh):
    replica, group = mesh.shape["replica"], mesh.shape["group"]
    view = Mesh(np.asarray(mesh.devices).reshape(replica // 2, 2, group), ("rx", "core", "group"))
    in_specs = (
        P(TOK, None),
        P(TOK, None),
        P(TOK, None),
        P("group", None),
        P("group", None),
        P("group", None),
        P(None, "group", None),
        P(None, "group"),
        P(None, "group", None),
        P(None, "group"),
        P(None, "group", None),
        P(None, "group", None),
        P(None, "group", None),
        P(None, None, "group", None),
        P(None, None, "group"),
        P(None, None, "group", None),
        P(None, None, "group"),
    )
    out_specs = (
        P(TOK, None),
        P(TOK, None),
        P("group", None),
        P("group", None),
        P("group", None),
        P(None, "group", None),
        P(None, "group"),
        P(None, "group", None),
        P(None, "group"),
        P("group", None),
        P("group", None),
        P("group", None),
        P(None, "group", None),
        P(None, "group"),
        P(None, "group", None),
        P(None, "group"),
        P(None, "group", None),
        P(None, "group", None),
        P(None, "group", None),
        P(None, None, "group", None),
        P(None, None, "group"),
        P(None, None, "group", None),
        P(None, None, "group"),
    )
    return jax.shard_map(shards, mesh=view, in_specs=in_specs, out_specs=out_specs, check_vma=False)
```

```python
import functools

import jax
import jax.numpy as jnp
import numpy as np
from jax import lax
from jax.sharding import Mesh
from jax.sharding import PartitionSpec as P
from jax.experimental import pallas as pl
from jax.experimental.pallas import tpu as pltpu

D = 512
HEADS = 8
HEAD_DIM = 64
F = 2048
E = 4
S = 197
MB_TOK = 394
CAP = 392
NV = 11
DENSE_AG = 2560
DENSE_PAD = 2304
F32 = jnp.float32
BF16 = jnp.bfloat16
TOK = ("rx", "core", "group")


MESH_ID = pl.DeviceIdType.MESH


def ring_order(groups):
    if groups in (4, 8):
        zs = groups // 2

        def pos_of(g):
            y = g % 2
            z = g // 2
            return z + y * (2 * zs - 1 - 2 * z)

        def dev_at(p):
            p = p % groups
            yy = p // zs
            return 2 * (p + yy * (2 * zs - 1 - 2 * p)) + yy

        return pos_of, dev_at
    return (lambda g: g), (lambda p: p % groups)


def ring_rs_kernel(groups, n_in, *refs):
    ins = refs[:n_in]
    outs = refs[n_in : 2 * n_in]
    rbufs = refs[2 * n_in : 3 * n_in]
    sbufs = refs[3 * n_in : 4 * n_in]
    owns = refs[4 * n_in : 5 * n_in]
    send_sem, recv_sem, load_sem = refs[5 * n_in :]
    pos_of, dev_at = ring_order(groups)
    rx = lax.axis_index("rx")
    core = lax.axis_index("core")
    g = lax.axis_index("group")
    pos = pos_of(g)
    nbr = (dev_at(pos + 1), dev_at(pos + groups - 1))

    barrier = pltpu.get_barrier_semaphore()
    for n in nbr:
        pl.semaphore_signal(barrier, inc=1, device_id=(rx, core, n), device_id_type=MESH_ID)
    pl.semaphore_wait(barrier, 2)

    def block_dev(d, s):
        if d == 0:
            return dev_at(pos + 2 * groups - s - 1)
        return dev_at(pos + s + 1)

    def load(d, s, slot):
        b = block_dev(d, s)
        copies = []
        for i in range(n_in):
            rows = ins[i].shape[1] // groups
            half = ins[i].shape[2] // 2
            src = ins[i].at[:, pl.ds(pl.multiple_of(b * rows, rows), rows), pl.ds(d * half, half)]
            copies.append(pltpu.make_async_copy(src, owns[i].at[d, slot], load_sem.at[d, slot, i]))
        return copies

    def remote(d, s, i):
        return pltpu.make_async_remote_copy(
            src_ref=sbufs[i].at[d, s],
            dst_ref=rbufs[i].at[d, s],
            send_sem=send_sem.at[d, s, i],
            recv_sem=recv_sem.at[d, s, i],
            device_id=(rx, core, nbr[d]),
            device_id_type=MESH_ID,
        )

    for d in range(2):
        for c in load(d, 0, 0):
            c.start()
    sends = []
    for s in range(groups):
        slot = s % 2
        for d in range(2):
            for c in load(d, s, slot):
                c.wait()
            if s + 1 < groups:
                for c in load(d, s + 1, 1 - slot):
                    c.start()
            for i in range(n_in):
                if s > 0:
                    remote(d, s - 1, i).wait_recv()
                for a in range(ins[i].shape[0]):
                    mine = owns[i][d, slot, a].astype(F32)
                    if s > 0:
                        mine = mine + rbufs[i][d, s - 1, a].astype(F32)
                    if s < groups - 1:
                        sbufs[i][d, s, a] = mine.astype(sbufs[i].dtype)
                    else:
                        half = ins[i].shape[2] // 2
                        outs[i][a, :, pl.ds(d * half, half)] = mine.astype(outs[i].dtype)
                if s < groups - 1:
                    c = remote(d, s, i)
                    c.start()
                    sends.append(c)
    for c in sends:
        c.wait_send()


def ring_reduce_scatter(xs, groups, collective_id):
    n_in = len(xs)
    outs, rb, own = [], [], []
    flops = 0
    nbytes = 0
    for x in xs:
        a, total, c = x.shape
        rows = total // groups
        outs.append(jax.ShapeDtypeStruct((a, rows, c), x.dtype))
        rb.append(pltpu.VMEM((2, groups - 1, a, rows, c // 2), x.dtype))
        own.append(pltpu.VMEM((2, 2, a, rows, c // 2), x.dtype))
        flops += a * total * c
        nbytes += 3 * x.size * x.dtype.itemsize
    scratch = rb + rb + own + [
        pltpu.SemaphoreType.DMA((2, groups - 1, n_in)),
        pltpu.SemaphoreType.DMA((2, groups - 1, n_in)),
        pltpu.SemaphoreType.DMA((2, 2, n_in)),
    ]
    return pl.pallas_call(
        functools.partial(ring_rs_kernel, groups, n_in),
        out_shape=outs,
        in_specs=[pl.BlockSpec(memory_space=pl.ANY)] * n_in,
        out_specs=[pl.BlockSpec(memory_space=pltpu.VMEM)] * n_in,
        scratch_shapes=scratch,
        compiler_params=pltpu.CompilerParams(
            collective_id=collective_id, has_side_effects=True, vmem_limit_bytes=60 * 1024 * 1024
        ),
        cost_estimate=pl.CostEstimate(flops=flops, bytes_accessed=nbytes, transcendentals=0),
    )(*xs)


def ring_ag_kernel(groups, *refs):
    in_up, in_down, in_dense, out_up, out_down, out_dense = refs[:6]
    ring_send, ring_recv, part_send, part_recv, local_sem = refs[6:]
    pos_of, dev_at = ring_order(groups)
    rx = lax.axis_index("rx")
    core = lax.axis_index("core")
    g = lax.axis_index("group")
    other = 1 - core
    pos = pos_of(g)
    nbr = (dev_at(pos + 1), dev_at(pos + groups - 1))
    gs = in_up.shape[1]
    fs = in_down.shape[1]
    width = in_dense.shape[1] // 2

    barrier = pltpu.get_barrier_semaphore()
    for n in nbr:
        pl.semaphore_signal(barrier, inc=1, device_id=(rx, core, n), device_id_type=MESH_ID)
    pl.semaphore_signal(barrier, inc=1, device_id=(rx, other, g), device_id_type=MESH_ID)
    pl.semaphore_wait(barrier, 3)

    def items(owner):
        found = []
        for k in range(2):
            e = 2 * k + owner
            found.append((in_up.at[e], lambda b, e=e: out_up.at[e, pl.ds(pl.multiple_of(b * gs, gs), gs)], F // 2))
            found.append((in_down.at[e], lambda b, e=e: out_down.at[e, pl.ds(pl.multiple_of(b * fs, fs), fs)], D // 2))
        dense_in = in_dense.at[:, pl.ds(owner * width, width)]
        found.append(
            (dense_in, lambda b: out_dense.at[pl.ds(pl.multiple_of(b * gs, gs), gs), pl.ds(owner * width, width)], width // 2)
        )
        return found

    mine = items(core)
    theirs = items(other)
    n_items = len(mine)

    locals_ = [pltpu.make_async_copy(in_up.at[e], out_up.at[e, pl.ds(pl.multiple_of(g * gs, gs), gs)], local_sem.at[e]) for e in range(E)]
    locals_ += [
        pltpu.make_async_copy(in_down.at[e], out_down.at[e, pl.ds(pl.multiple_of(g * fs, fs), fs)], local_sem.at[E + e])
        for e in range(E)
    ]
    locals_.append(pltpu.make_async_copy(in_dense, out_dense.at[pl.ds(pl.multiple_of(g * gs, gs), gs)], local_sem.at[2 * E]))
    for c in locals_:
        c.start()

    def block_at(d, s):
        if d == 0:
            return dev_at(pos + 2 * groups - 1 - s)
        return dev_at(pos + 1 + s)

    def ring_copy(d, s, j, src_block):
        src_in, dst_of, half = mine[j]
        cols = pl.ds(d * half, half)
        if src_block is None:
            src = src_in.at[:, cols]
            dst = dst_of(g).at[:, cols]
        else:
            src = dst_of(src_block).at[:, cols]
            dst = src
        return pltpu.make_async_remote_copy(
            src_ref=src, dst_ref=dst, send_sem=ring_send.at[d, s, j], recv_sem=ring_recv.at[d, s, j],
            device_id=(rx, core, nbr[d]), device_id_type=MESH_ID,
        )

    def part_copy(d, s, j, table, block):
        _, dst_of, half = table[j]
        view = dst_of(block).at[:, pl.ds(d * half, half)]
        return pltpu.make_async_remote_copy(
            src_ref=view, dst_ref=view, send_sem=part_send.at[d, s, j], recv_sem=part_recv.at[d, s, j],
            device_id=(rx, other, g), device_id_type=MESH_ID,
        )

    sends = []
    for d in range(2):
        for j in range(n_items):
            c = ring_copy(d, 0, j, None)
            c.start()
            sends.append(c)
    for s in range(groups - 1):
        for d in range(2):
            b = block_at(d, s)
            for j in range(n_items):
                pltpu.make_async_remote_copy(
                    src_ref=mine[j][1](b).at[:, pl.ds(d * mine[j][2], mine[j][2])],
                    dst_ref=mine[j][1](b).at[:, pl.ds(d * mine[j][2], mine[j][2])],
                    send_sem=ring_send.at[d, s, j], recv_sem=ring_recv.at[d, s, j],
                    device_id=(rx, core, nbr[d]), device_id_type=MESH_ID,
                ).wait_recv()
                if s + 1 < groups - 1:
                    c = ring_copy(d, s + 1, j, b)
                    c.start()
                    sends.append(c)
                c = part_copy(d, s, j, mine, b)
                c.start()
                sends.append(c)
    for s in range(groups - 1):
        for d in range(2):
            b = block_at(d, s)
            for j in range(n_items):
                part_copy(d, s, j, theirs, b).wait_recv()
    for c in sends:
        c.wait_send()
    for c in locals_:
        c.wait()


def ring_all_gather(up_b, down_b, dense_b, groups, collective_id):
    n_items = 5
    gs = up_b.shape[1]
    shapes = [
        jax.ShapeDtypeStruct((E, gs * groups, F), BF16),
        jax.ShapeDtypeStruct((E, down_b.shape[1] * groups, D), BF16),
        jax.ShapeDtypeStruct((gs * groups, dense_b.shape[1]), BF16),
    ]
    nbytes = sum(int(np.prod(s.shape)) * 2 for s in shapes)
    return pl.pallas_call(
        functools.partial(ring_ag_kernel, groups),
        out_shape=shapes,
        in_specs=[pl.BlockSpec(memory_space=pl.ANY)] * 3,
        out_specs=[pl.BlockSpec(memory_space=pl.ANY)] * 3,
        scratch_shapes=[
            pltpu.SemaphoreType.DMA((2, groups - 1, n_items)),
            pltpu.SemaphoreType.DMA((2, groups - 1, n_items)),
            pltpu.SemaphoreType.DMA((2, groups - 1, n_items)),
            pltpu.SemaphoreType.DMA((2, groups - 1, n_items)),
            pltpu.SemaphoreType.DMA((2 * E + 1,)),
        ],
        compiler_params=pltpu.CompilerParams(collective_id=collective_id, has_side_effects=True),
        cost_estimate=pl.CostEstimate(flops=0, bytes_accessed=nbytes, transcendentals=0),
    )(up_b, down_b, dense_b)


def grad_items(gu, gd, gdense, owner, gs, fs, width):
    found = []
    for k in range(2):
        e = 2 * k + owner
        found.append((lambda b, e=e: gu.at[e, pl.ds(pl.multiple_of(b * gs, gs), gs)], F // 2))
        found.append((lambda b, e=e: gd.at[e, pl.ds(pl.multiple_of(b * fs, fs), fs)], D // 2))
    found.append((lambda b: gdense.at[pl.ds(pl.multiple_of(b * gs, gs), gs), pl.ds(owner * width, width)], width // 2))
    return found


def ring_rs2_kernel(groups, x_pair, *refs):
    gu, gd, gdense, out_up, out_down, out_dense = refs[:6]
    n_items = 5
    scr = refs[6:]
    rbuf, sbuf, pbuf, own, fin, xr, cr = (scr[i * n_items : (i + 1) * n_items] for i in range(7))
    ring_send, ring_recv, part_send, part_recv, load_sem, x_send, x_recv, c_send, c_recv = scr[7 * n_items :]
    pos_of, dev_at = ring_order(groups)
    rx = lax.axis_index("rx")
    core = lax.axis_index("core")
    g = lax.axis_index("group")
    other = 1 - core
    pos = pos_of(g)
    nbr = (dev_at(pos + 1), dev_at(pos + groups - 1))
    gs = gu.shape[1] // groups
    fs = gd.shape[1] // groups
    width = gdense.shape[1] // 2
    mine = grad_items(gu, gd, gdense, core, gs, fs, width)
    theirs = grad_items(gu, gd, gdense, other, gs, fs, width)

    barrier = pltpu.get_barrier_semaphore()
    for n in nbr:
        pl.semaphore_signal(barrier, inc=1, device_id=(rx, core, n), device_id_type=MESH_ID)
    pl.semaphore_signal(barrier, inc=1, device_id=(rx, other, g), device_id_type=MESH_ID)
    count = 3
    if x_pair:
        pl.semaphore_signal(barrier, inc=1, device_id=(1 - rx, core, g), device_id_type=MESH_ID)
        count = 4
    pl.semaphore_wait(barrier, count)

    def block_at(d, s):
        if d == 0:
            return dev_at(pos + 2 * groups - 1 - s)
        return dev_at(pos + 1 + s)

    def cols(j, d):
        half = mine[j][1]
        return pl.ds(d * half, half)

    def load(d, s, slot, j):
        return pltpu.make_async_copy(mine[j][0](block_at(d, s)).at[:, cols(j, d)], own[j].at[d, slot], load_sem.at[d, slot, j])

    def part(d, s, j):
        return pltpu.make_async_remote_copy(
            src_ref=theirs[j][0](block_at(d, s)).at[:, cols(j, d)], dst_ref=pbuf[j].at[d, s],
            send_sem=part_send.at[d, s, j], recv_sem=part_recv.at[d, s, j],
            device_id=(rx, other, g), device_id_type=MESH_ID,
        )

    def ring(d, s, j):
        return pltpu.make_async_remote_copy(
            src_ref=sbuf[j].at[d, s], dst_ref=rbuf[j].at[d, s],
            send_sem=ring_send.at[d, s, j], recv_sem=ring_recv.at[d, s, j],
            device_id=(rx, core, nbr[d]), device_id_type=MESH_ID,
        )

    sends = []
    for d in range(2):
        for j in range(n_items):
            load(d, 0, 0, j).start()
            c = part(d, 0, j)
            c.start()
            sends.append(c)
    for s in range(groups):
        slot = s % 2
        for d in range(2):
            for j in range(n_items):
                load(d, s, slot, j).wait()
                if s + 1 < groups:
                    load(d, s + 1, 1 - slot, j).start()
                    c = part(d, s + 1, j)
                    c.start()
                    sends.append(c)
                part(d, s, j).wait_recv()
                val = own[j][d, slot].astype(F32) + pbuf[j][d, s].astype(F32)
                if s > 0:
                    ring(d, s - 1, j).wait_recv()
                    val = val + rbuf[j][d, s - 1].astype(F32)
                if s < groups - 1:
                    sbuf[j][d, s] = val.astype(BF16)
                    c = ring(d, s, j)
                    c.start()
                    sends.append(c)
                else:
                    fin[j][d] = val

    for c in sends:
        c.wait_send()
    sends = []
    if x_pair:
        x_copies = []
        for d in range(2):
            for j in range(n_items):
                sbuf[j][d, 0] = fin[j][d].astype(BF16)
                c = pltpu.make_async_remote_copy(
                    src_ref=sbuf[j].at[d, 0], dst_ref=xr[j].at[d], send_sem=x_send.at[d, j], recv_sem=x_recv.at[d, j],
                    device_id=(1 - rx, core, g), device_id_type=MESH_ID,
                )
                c.start()
                x_copies.append(c)
        for c in x_copies:
            c.wait_recv()
        for d in range(2):
            for j in range(n_items):
                fin[j][d] = sbuf[j][d, 0].astype(F32) + xr[j][d].astype(F32)
        sends += x_copies

    c_copies = []
    for d in range(2):
        for j in range(n_items):
            c = pltpu.make_async_remote_copy(
                src_ref=fin[j].at[d], dst_ref=cr[j].at[d], send_sem=c_send.at[d, j], recv_sem=c_recv.at[d, j],
                device_id=(rx, other, g), device_id_type=MESH_ID,
            )
            c.start()
            c_copies.append(c)

    def out_items(owner):
        found = []
        for k in range(2):
            e = 2 * k + owner
            found.append(lambda d, e=e: out_up.at[e, :, pl.ds(d * (F // 2), F // 2)])
            found.append(lambda d, e=e: out_down.at[e, :, pl.ds(d * (D // 2), D // 2)])
        found.append(lambda d: out_dense.at[:, pl.ds(owner * width + d * (width // 2), width // 2)])
        return found

    mine_out = out_items(core)
    theirs_out = out_items(other)
    for d in range(2):
        for j in range(n_items):
            mine_out[j](d)[...] = fin[j][d]
    for c in c_copies:
        c.wait_recv()
    for d in range(2):
        for j in range(n_items):
            theirs_out[j](d)[...] = cr[j][d]
    for c in sends + c_copies:
        c.wait_send()


def grad_reduce(gu, gd, gdense, groups, x_pair, collective_id):
    gs = gu.shape[1] // groups
    fs = gd.shape[1] // groups
    width = gdense.shape[1] // 2
    item_shapes = [(gs, F // 2), (fs, D // 2), (gs, F // 2), (fs, D // 2), (gs, width // 2)]
    scratch = []
    for lead, dtype in (((2, groups - 1), BF16), ((2, groups - 1), BF16), ((2, groups), BF16), ((2, 2), BF16), ((2,), F32), ((2,), BF16), ((2,), F32)):
        scratch += [pltpu.VMEM(lead + shp, dtype) for shp in item_shapes]
    scratch += [
        pltpu.SemaphoreType.DMA((2, groups - 1, 5)),
        pltpu.SemaphoreType.DMA((2, groups - 1, 5)),
        pltpu.SemaphoreType.DMA((2, groups, 5)),
        pltpu.SemaphoreType.DMA((2, groups, 5)),
        pltpu.SemaphoreType.DMA((2, 2, 5)),
        pltpu.SemaphoreType.DMA((2, 5)),
        pltpu.SemaphoreType.DMA((2, 5)),
        pltpu.SemaphoreType.DMA((2, 5)),
        pltpu.SemaphoreType.DMA((2, 5)),
    ]
    outs = [
        jax.ShapeDtypeStruct((E, gs, F), F32),
        jax.ShapeDtypeStruct((E, fs, D), F32),
        jax.ShapeDtypeStruct((gs, gdense.shape[1]), F32),
    ]
    nbytes = 2 * (gu.size + gd.size + gdense.size)
    return pl.pallas_call(
        functools.partial(ring_rs2_kernel, groups, x_pair),
        out_shape=outs,
        in_specs=[pl.BlockSpec(memory_space=pl.ANY)] * 3,
        out_specs=[pl.BlockSpec(memory_space=pltpu.VMEM)] * 3,
        scratch_shapes=scratch,
        compiler_params=pltpu.CompilerParams(
            collective_id=collective_id, has_side_effects=True, vmem_limit_bytes=62 * 1024 * 1024
        ),
        cost_estimate=pl.CostEstimate(flops=gu.size + gd.size + gdense.size, bytes_accessed=nbytes, transcendentals=0),
    )(gu, gd, gdense)


TILE = 128
TILE_B = 256
CAPP = 512
SQRT_HALF = float(np.sqrt(0.5))
INV_SQRT_2PI = float(1.0 / np.sqrt(2.0 * np.pi))


def ffn_fwd_kernel(micro, counts, x_ref, w1_ref, b1_ref, w2_ref, b2_ref, hp_ref, h_ref, y_ref):
    e, m, t = pl.program_id(0), pl.program_id(1), pl.program_id(2)
    active = t * TILE < counts[e * micro + m]

    @pl.when(active)
    def _():
        hp = jnp.dot(x_ref[0], w1_ref[0], preferred_element_type=F32) + b1_ref[0]
        h = (0.5 * hp * (1.0 + lax.erf(hp * SQRT_HALF))).astype(BF16)
        hp_ref[0] = hp
        h_ref[0] = h
        y = jnp.dot(h, w2_ref[0], preferred_element_type=F32) + b2_ref[0]
        hi = y.astype(BF16)
        y_ref[0, :, :D] = hi
        y_ref[0, :, D:] = (y - hi.astype(F32)).astype(BF16)

    @pl.when(jnp.logical_not(active))
    def _():
        y_ref[0] = jnp.zeros(y_ref.shape[1:], BF16)


def ffn_forward(counts, table_in, w1, b1, w2, b2, micro):
    tiles = CAPP // TILE
    rows = table_in.shape[1]
    row_map = lambda e, m, t, c: (m, e * tiles + t, 0)
    w_map = lambda e, m, t, c: (e, 0, 0)
    grid_spec = pltpu.PrefetchScalarGridSpec(
        num_scalar_prefetch=1,
        grid=(E, micro, tiles),
        in_specs=[
            pl.BlockSpec((1, TILE, D), row_map),
            pl.BlockSpec((1, D, F), w_map),
            pl.BlockSpec((1, 1, F), w_map),
            pl.BlockSpec((1, F, D), w_map),
            pl.BlockSpec((1, 1, D), w_map),
        ],
        out_specs=[
            pl.BlockSpec((1, TILE, F), row_map),
            pl.BlockSpec((1, TILE, F), row_map),
            pl.BlockSpec((1, TILE, 2 * D), row_map),
        ],
    )
    work = micro * rows
    return pl.pallas_call(
        functools.partial(ffn_fwd_kernel, micro),
        grid_spec=grid_spec,
        out_shape=[
            jax.ShapeDtypeStruct((micro, rows, F), F32),
            jax.ShapeDtypeStruct((micro, rows, F), BF16),
            jax.ShapeDtypeStruct((micro, rows, 2 * D), BF16),
        ],
        compiler_params=pltpu.CompilerParams(vmem_limit_bytes=48 * 1024 * 1024),
        cost_estimate=pl.CostEstimate(
            flops=4 * work * D * F // 2, bytes_accessed=work * (2 * D + 6 * F + 4 * D) // 2, transcendentals=work * F // 2
        ),
    )(counts, table_in, w1, b1, w2, b2)


def ffn_bwd_kernel(micro, counts, dy_ref, x_ref, hp_ref, h_ref, w1_ref, w2_ref, dt_ref, gu_ref, gd_ref, gb_ref, gb2_ref, gu_acc, gd_acc):
    e, m, t = pl.program_id(0), pl.program_id(1), pl.program_id(2)
    active = t * TILE_B < counts[e * micro + m]

    @pl.when((m == 0) & (t == 0))
    def _():
        gu_acc[...] = jnp.zeros(gu_acc.shape, F32)
        gd_acc[...] = jnp.zeros(gd_acc.shape, F32)
        gb_ref[...] = jnp.zeros(gb_ref.shape, F32)
        gb2_ref[...] = jnp.zeros(gb2_ref.shape, F32)

    @pl.when(active)
    def _():
        dy = dy_ref[0]
        hp = hp_ref[0]
        d_hidden = lax.dot_general(dy, w2_ref[0], (((1,), (1,)), ((), ())), preferred_element_type=F32)
        slope = 0.5 * (1.0 + lax.erf(hp * SQRT_HALF)) + hp * jnp.exp(-0.5 * hp * hp) * INV_SQRT_2PI
        d_pre = (d_hidden * slope).astype(BF16)
        dt = lax.dot_general(d_pre, w1_ref[0], (((1,), (1,)), ((), ())), preferred_element_type=F32)
        hi = dt.astype(BF16)
        dt_ref[0, :, :D] = hi
        dt_ref[0, :, D:] = (dt - hi.astype(F32)).astype(BF16)
        gb2_ref[0] += jnp.sum(dy.astype(F32), 0, keepdims=True)
        gu_acc[...] += lax.dot_general(x_ref[0], d_pre, (((0,), (0,)), ((), ())), preferred_element_type=F32)
        gd_acc[...] += lax.dot_general(h_ref[0], dy, (((0,), (0,)), ((), ())), preferred_element_type=F32)
        gb_ref[0] += jnp.sum(d_pre.astype(F32), 0, keepdims=True)

    @pl.when(jnp.logical_not(active))
    def _():
        dt_ref[0] = jnp.zeros(dt_ref.shape[1:], BF16)

    @pl.when((m == micro - 1) & (t == pl.num_programs(2) - 1))
    def _():
        gu_ref[0] = gu_acc[...].astype(BF16)
        gd_ref[0] = gd_acc[...].astype(BF16)


def ffn_backward(counts, d_expert, table_in, hp, h, w1, w2, micro):
    tiles = CAPP // TILE_B
    rows = table_in.shape[1]
    row_map = lambda e, m, t, c: (m, e * tiles + t, 0)
    w_map = lambda e, m, t, c: (e, 0, 0)
    grid_spec = pltpu.PrefetchScalarGridSpec(
        num_scalar_prefetch=1,
        grid=(E, micro, tiles),
        in_specs=[
            pl.BlockSpec((1, TILE_B, D), row_map),
            pl.BlockSpec((1, TILE_B, D), row_map),
            pl.BlockSpec((1, TILE_B, F), row_map),
            pl.BlockSpec((1, TILE_B, F), row_map),
            pl.BlockSpec((1, D, F), w_map),
            pl.BlockSpec((1, F, D), w_map),
        ],
        out_specs=[
            pl.BlockSpec((1, TILE_B, 2 * D), row_map),
            pl.BlockSpec((1, D, F), w_map),
            pl.BlockSpec((1, F, D), w_map),
            pl.BlockSpec((1, 1, F), w_map),
            pl.BlockSpec((1, 1, D), w_map),
        ],
        scratch_shapes=[pltpu.VMEM((D, F), F32), pltpu.VMEM((F, D), F32)],
    )
    work = micro * rows
    return pl.pallas_call(
        functools.partial(ffn_bwd_kernel, micro),
        grid_spec=grid_spec,
        out_shape=[
            jax.ShapeDtypeStruct((micro, rows, 2 * D), BF16),
            jax.ShapeDtypeStruct((E, D, F), BF16),
            jax.ShapeDtypeStruct((E, F, D), BF16),
            jax.ShapeDtypeStruct((E, 1, F), F32),
            jax.ShapeDtypeStruct((E, 1, D), F32),
        ],
        compiler_params=pltpu.CompilerParams(vmem_limit_bytes=60 * 1024 * 1024),
        cost_estimate=pl.CostEstimate(
            flops=8 * work * D * F // 2, bytes_accessed=work * (8 * D + 6 * F) // 2 + 16 * E * D * F, transcendentals=2 * work * F // 2
        ),
    )(counts, d_expert, table_in, hp, h, w1, w2)

def layer_norm(value, gain, shift):
    center = value - jnp.mean(value, -1, keepdims=True)
    spread = jnp.mean(center * center, -1, keepdims=True)
    return center * lax.rsqrt(spread + 1e-06) * gain + shift


def gelu_exact(value):
    return jax.nn.gelu(value, approximate=False)


def split_heads(part):
    return part.reshape(-1, S, HEADS, HEAD_DIM)


def dot(a, b):
    return jnp.dot(a, b, preferred_element_type=F32)


def assign_places(route):
    chosen = jnp.concatenate([route[:, :, 0], route[:, :, 1]], 1)
    hits = (chosen[:, :, None] == jnp.arange(E, dtype=jnp.int32)).astype(jnp.int32)
    before = jnp.cumsum(hits, 1) - hits
    slot = jnp.sum(before * hits, 2)
    return chosen * CAPP + slot, jnp.sum(hits, 1)


def hi_lo(v):
    hi = v.astype(BF16)
    lo = (v - hi.astype(F32)).astype(BF16)
    return jnp.concatenate([hi, lo], -1)


def pick_rows(onehot, split):
    both = jnp.einsum("mnr,mrd->mnd", onehot, split, preferred_element_type=F32)
    return both[..., :D] + both[..., D:]


def pack_dense(qkv_w, out_w, router_w, vectors, up_bias):
    rows = qkv_w.shape[0]
    ub = up_bias.reshape(E, rows, 4).transpose(1, 0, 2).reshape(rows, E * 4)
    return jnp.concatenate([qkv_w, out_w, router_w, vectors.T, ub], 1)


def unpack_dense(packed):
    rows = packed.shape[0]
    w_qkv = packed[:, : 3 * D]
    w_out = packed[:, 3 * D : 4 * D]
    w_router = packed[:, 4 * D : 4 * D + E]
    table = packed[:, 4 * D + E : 4 * D + E + NV].T
    ub = packed[:, 4 * D + E + NV :].reshape(rows, E, 4).transpose(1, 0, 2).reshape(E, rows * 4)
    return w_qkv, w_out, w_router, table, ub


def attention_fwd(w_qkv, w_out, table, value):
    rows = value.shape[0]
    scale = HEAD_DIM ** (-0.5)
    first = layer_norm(value, table[0], table[1]).astype(BF16)
    qkv_bias = jnp.concatenate([table[2], jnp.zeros((D,), F32), table[3]])
    qkv = (dot(first, w_qkv) + qkv_bias).astype(BF16)
    query, key_part, val_part = (
        split_heads(qkv[:, :D]),
        split_heads(qkv[:, D : 2 * D]),
        split_heads(qkv[:, 2 * D :]),
    )
    scores = jnp.einsum("bqhd,bkhd->bhqk", query, key_part, preferred_element_type=F32) * scale
    peak = jnp.max(scores, -1, keepdims=True)
    expo = jnp.exp(scores - peak)
    total = jnp.sum(expo, -1, keepdims=True)
    probs_att = (expo / total).astype(BF16)
    log_total = peak + jnp.log(total)
    attended = jnp.einsum("bhqk,bkhd->bqhd", probs_att, val_part, preferred_element_type=F32)
    attended = attended.reshape(rows, D).astype(BF16)
    resid = value + (dot(attended, w_out) + table[4])
    return first, qkv, log_total, attended, resid


def attention_bwd(w_qkv, w_out, table, value, first, qkv, log_total, attended, d_resid):
    rows = value.shape[0]
    scale = HEAD_DIM ** (-0.5)
    d_branch = d_resid.astype(BF16)
    g_bias_out = jnp.sum(d_branch.astype(F32), 0)
    g_out = lax.dot_general(attended, d_branch, (((0,), (0,)), ((), ())), preferred_element_type=F32)
    d_att = split_heads(
        lax.dot_general(d_branch, w_out, (((1,), (1,)), ((), ())), preferred_element_type=F32).astype(BF16)
    )
    query, key_part, val_part = (
        split_heads(qkv[:, :D]),
        split_heads(qkv[:, D : 2 * D]),
        split_heads(qkv[:, 2 * D :]),
    )
    scores = jnp.einsum("bqhd,bkhd->bhqk", query, key_part, preferred_element_type=F32) * scale
    probs_f = jnp.exp(scores - log_total)
    probs_att = probs_f.astype(BF16)
    d_val = jnp.einsum("bhqk,bqhd->bkhd", probs_att, d_att, preferred_element_type=F32)
    d_prob = jnp.einsum("bqhd,bkhd->bhqk", d_att, val_part, preferred_element_type=F32)
    d_score = (probs_f * (d_prob - jnp.sum(d_prob * probs_f, -1, keepdims=True))).astype(BF16)
    d_query = jnp.einsum("bhqk,bkhd->bqhd", d_score, key_part, preferred_element_type=F32) * scale
    d_key = jnp.einsum("bhqk,bqhd->bkhd", d_score, query, preferred_element_type=F32) * scale
    d_qkv = jnp.concatenate(
        [d_query.reshape(rows, D), d_key.reshape(rows, D), d_val.reshape(rows, D)], 1
    ).astype(BF16)
    d_qkv_f = d_qkv.astype(F32)
    g_bias_q = jnp.sum(d_qkv_f[:, :D], 0)
    g_bias_v = jnp.sum(d_qkv_f[:, 2 * D :], 0)
    g_qkv = lax.dot_general(first, d_qkv, (((0,), (0,)), ((), ())), preferred_element_type=F32)
    d_first = lax.dot_general(d_qkv, w_qkv, (((1,), (1,)), ((), ())), preferred_element_type=F32)
    first_pull = jax.vjp(layer_norm, value, table[0], table[1])[1]
    d_input, g_gain_one, g_shift_one = first_pull(d_first)
    return (g_qkv, g_out, g_bias_out, g_bias_q, g_bias_v, g_gain_one, g_shift_one), d_input


def adamw(weight, moments, grad, rate):
    first = 0.5 * moments[0] + 0.5 * grad
    root = jnp.sqrt(0.5 * moments[1] * moments[1] + 0.5 * grad * grad)
    update = first / (root + 1e-08)
    return (weight - rate * (update + 0.1 * weight), jnp.stack([first, root]))


def shards(
    tokens,
    cotangent,
    expert_index,
    qkv_weight,
    out_weight,
    router_weight,
    up_weight,
    up_bias,
    down_weight,
    vectors,
    qkv_moments,
    out_moments,
    router_moments,
    up_moments,
    up_bias_moments,
    down_moments,
    vector_moments,
):
    rows = tokens.shape[0]
    micro = rows // MB_TOK
    gs = qkv_weight.shape[0]
    group_size = D // gs
    core = lax.axis_index("core")

    dense_in = pack_dense(qkv_weight, out_weight, router_weight, vectors, up_bias)
    width = dense_in.shape[1]
    dense_in = jnp.pad(dense_in, ((0, 0), (0, DENSE_AG - width))).astype(BF16)
    w_up_all, w_down_all, dense = ring_all_gather(
        up_weight.astype(BF16), down_weight.astype(BF16), dense_in, group_size, 1
    )
    w_qkv, w_out, w_router, table_b, b_up_b = unpack_dense(dense[:, :width])
    table = table_b.astype(F32)
    b_up = b_up_b.astype(F32)

    value = tokens.astype(F32)
    d_out = cotangent.astype(F32)
    first, qkv, log_total, attended, resid = attention_fwd(w_qkv, w_out, table, value)
    second = layer_norm(resid, table[5], table[6]).astype(BF16)
    logits = dot(second, w_router)
    probs = jax.nn.softmax(logits, -1)
    picked = expert_index[:, :, None] == jnp.arange(E, dtype=jnp.int32)
    gate = jnp.sum(jnp.where(picked, probs[:, None, :], 0.0), -1)

    route = expert_index.reshape(micro, MB_TOK, 2)
    places, counts = assign_places(route)
    counts = counts.T.reshape(E * micro)
    onehot = (places[:, :, None] == jnp.arange(E * CAPP, dtype=jnp.int32)).astype(BF16)
    second_m = second.reshape(micro, MB_TOK, D)
    pair = jnp.concatenate([second_m, second_m], 1)
    table_in = jnp.einsum("mnr,mnd->mrd", onehot, pair, preferred_element_type=F32).astype(BF16)

    hidden_pre, hidden, y_all = ffn_forward(
        counts, table_in, w_up_all, b_up[:, None, :], w_down_all, table[7 : 7 + E][:, None, :], micro
    )
    picked_rows = pick_rows(onehot, y_all)
    out_zero = picked_rows[:, :MB_TOK].reshape(rows, D)
    out_one = picked_rows[:, MB_TOK:].reshape(rows, D)
    result = resid + (gate[:, 0:1] * out_zero + gate[:, 1:2] * out_one)

    d_gate = jnp.stack([jnp.sum(d_out * out_zero, -1), jnp.sum(d_out * out_one, -1)], 1)
    d_out_m = d_out.reshape(micro, MB_TOK, D)
    gate_m = gate.reshape(micro, MB_TOK, 2)
    weighted = jnp.concatenate([gate_m[:, :, 0:1] * d_out_m, gate_m[:, :, 1:2] * d_out_m], 1).astype(BF16)
    d_expert = jnp.einsum("mnr,mnd->mrd", onehot, weighted, preferred_element_type=F32).astype(BF16)

    d_table, g_up, g_down, g_b1, g_b2 = ffn_backward(counts, d_expert, table_in, hidden_pre, hidden, w_up_all, w_down_all, micro)
    g_up_bias_all = g_b1[:, 0, :]
    g_bias_down = g_b2[:, 0, :]

    onehot_sum = onehot[:, :MB_TOK] + onehot[:, MB_TOK:]
    d_picked = pick_rows(onehot_sum, d_table).reshape(rows, D)

    d_probs = jnp.sum(jnp.where(picked, d_gate[:, :, None], 0.0), 1)
    d_logit = (probs * (d_probs - jnp.sum(d_probs * probs, -1, keepdims=True))).astype(BF16)
    g_router = lax.dot_general(second, d_logit, (((0,), (0,)), ((), ())), preferred_element_type=F32)
    d_second = d_picked + lax.dot_general(d_logit, w_router, (((1,), (1,)), ((), ())), preferred_element_type=F32)
    norm_pull = jax.vjp(layer_norm, resid, table[5], table[6])[1]
    d_resid, g_gain_two, g_shift_two = norm_pull(d_second)
    d_resid = d_out + d_resid

    att_grads, d_input = attention_bwd(w_qkv, w_out, table, value, first, qkv, log_total, attended, d_resid)
    g_qkv, g_out, g_bias_out, g_bias_q, g_bias_v, g_gain_one, g_shift_one = att_grads
    input_grad = d_resid + d_input

    g_table = jnp.concatenate(
        [
            jnp.stack([g_gain_one, g_shift_one, g_bias_q, g_bias_v, g_bias_out, g_gain_two, g_shift_two]),
            g_bias_down,
        ],
        0,
    )
    dense_g = pack_dense(g_qkv, g_out, g_router, g_table, g_up_bias_all)
    width = dense_g.shape[1]
    dense_g = jnp.pad(dense_g, ((0, 0), (0, DENSE_AG - width))).astype(BF16)
    x_pair = lax.axis_size("rx") == 2
    r_up, r_down, r_dense = grad_reduce(g_up, g_down, dense_g, group_size, x_pair, 0)
    if not x_pair:
        r_up, r_down, r_dense = lax.psum((r_up, r_down, r_dense), "rx")
    r_qkv, r_out, r_router, r_table, r_ub = unpack_dense(r_dense[:, :width])

    reduced = (r_qkv, r_out, r_router, r_up, r_ub, r_down, r_table)
    rates = (
        2.0 * D ** (-0.5),
        2.0 * (D // 32) ** (-0.5),
        2.0 * (2 * D) ** (-0.5),
        2.0 * D ** (-0.5),
        0.2,
        2.0 * (F // 16) ** (-0.5),
        0.2,
    )
    params = (qkv_weight, out_weight, router_weight, up_weight, up_bias, down_weight, vectors)
    moments = (qkv_moments, out_moments, router_moments, up_moments, up_bias_moments, down_moments, vector_moments)
    news = []
    states = []
    for weight, state, grad, rate in zip(params, moments, reduced, rates):
        new_weight, new_state = adamw(weight, state, grad, rate)
        news.append(new_weight)
        states.append(new_state)
    return (result.astype(BF16), input_grad) + reduced + tuple(news) + tuple(states)


def solution(mesh):
    replica, group = mesh.shape["replica"], mesh.shape["group"]
    view = Mesh(np.asarray(mesh.devices).reshape(replica // 2, 2, group), ("rx", "core", "group"))
    in_specs = (
        P(TOK, None),
        P(TOK, None),
        P(TOK, None),
        P("group", None),
        P("group", None),
        P("group", None),
        P(None, "group", None),
        P(None, "group"),
        P(None, "group", None),
        P(None, "group"),
        P(None, "group", None),
        P(None, "group", None),
        P(None, "group", None),
        P(None, None, "group", None),
        P(None, None, "group"),
        P(None, None, "group", None),
        P(None, None, "group"),
    )
    out_specs = (
        P(TOK, None),
        P(TOK, None),
        P("group", None),
        P("group", None),
        P("group", None),
        P(None, "group", None),
        P(None, "group"),
        P(None, "group", None),
        P(None, "group"),
        P("group", None),
        P("group", None),
        P("group", None),
        P(None, "group", None),
        P(None, "group"),
        P(None, "group", None),
        P(None, "group"),
        P(None, "group", None),
        P(None, "group", None),
        P(None, "group", None),
        P(None, None, "group", None),
        P(None, None, "group"),
        P(None, None, "group", None),
        P(None, None, "group"),
    )
    return jax.shard_map(shards, mesh=view, in_specs=in_specs, out_specs=out_specs, check_vma=False)
```

```python
import functools

import jax
import jax.numpy as jnp
import numpy as np
from jax import lax
from jax.sharding import Mesh
from jax.sharding import PartitionSpec as P
from jax.experimental import pallas as pl
from jax.experimental.pallas import tpu as pltpu

D = 512
HEADS = 8
HEAD_DIM = 64
F = 2048
E = 4
S = 197
MB_TOK = 394
CAP = 392
NV = 11
DENSE_AG = 2560
DENSE_PAD = 2304
F32 = jnp.float32
BF16 = jnp.bfloat16
TOK = ("rx", "core", "group")


MESH_ID = pl.DeviceIdType.MESH


def ring_order(groups):
    if groups in (4, 8):
        zs = groups // 2

        def pos_of(g):
            y = g % 2
            z = g // 2
            return z + y * (2 * zs - 1 - 2 * z)

        def dev_at(p):
            p = p % groups
            yy = p // zs
            return 2 * (p + yy * (2 * zs - 1 - 2 * p)) + yy

        return pos_of, dev_at
    return (lambda g: g), (lambda p: p % groups)


def ring_rs_kernel(groups, n_in, *refs):
    ins = refs[:n_in]
    outs = refs[n_in : 2 * n_in]
    rbufs = refs[2 * n_in : 3 * n_in]
    sbufs = refs[3 * n_in : 4 * n_in]
    owns = refs[4 * n_in : 5 * n_in]
    send_sem, recv_sem, load_sem = refs[5 * n_in :]
    pos_of, dev_at = ring_order(groups)
    rx = lax.axis_index("rx")
    core = lax.axis_index("core")
    g = lax.axis_index("group")
    pos = pos_of(g)
    nbr = (dev_at(pos + 1), dev_at(pos + groups - 1))

    barrier = pltpu.get_barrier_semaphore()
    for n in nbr:
        pl.semaphore_signal(barrier, inc=1, device_id=(rx, core, n), device_id_type=MESH_ID)
    pl.semaphore_wait(barrier, 2)

    def block_dev(d, s):
        if d == 0:
            return dev_at(pos + 2 * groups - s - 1)
        return dev_at(pos + s + 1)

    def load(d, s, slot):
        b = block_dev(d, s)
        copies = []
        for i in range(n_in):
            rows = ins[i].shape[1] // groups
            half = ins[i].shape[2] // 2
            src = ins[i].at[:, pl.ds(pl.multiple_of(b * rows, rows), rows), pl.ds(d * half, half)]
            copies.append(pltpu.make_async_copy(src, owns[i].at[d, slot], load_sem.at[d, slot, i]))
        return copies

    def remote(d, s, i):
        return pltpu.make_async_remote_copy(
            src_ref=sbufs[i].at[d, s],
            dst_ref=rbufs[i].at[d, s],
            send_sem=send_sem.at[d, s, i],
            recv_sem=recv_sem.at[d, s, i],
            device_id=(rx, core, nbr[d]),
            device_id_type=MESH_ID,
        )

    for d in range(2):
        for c in load(d, 0, 0):
            c.start()
    sends = []
    for s in range(groups):
        slot = s % 2
        for d in range(2):
            for c in load(d, s, slot):
                c.wait()
            if s + 1 < groups:
                for c in load(d, s + 1, 1 - slot):
                    c.start()
            for i in range(n_in):
                if s > 0:
                    remote(d, s - 1, i).wait_recv()
                for a in range(ins[i].shape[0]):
                    mine = owns[i][d, slot, a].astype(F32)
                    if s > 0:
                        mine = mine + rbufs[i][d, s - 1, a].astype(F32)
                    if s < groups - 1:
                        sbufs[i][d, s, a] = mine.astype(sbufs[i].dtype)
                    else:
                        half = ins[i].shape[2] // 2
                        outs[i][a, :, pl.ds(d * half, half)] = mine.astype(outs[i].dtype)
                if s < groups - 1:
                    c = remote(d, s, i)
                    c.start()
                    sends.append(c)
    for c in sends:
        c.wait_send()


def ring_reduce_scatter(xs, groups, collective_id):
    n_in = len(xs)
    outs, rb, own = [], [], []
    flops = 0
    nbytes = 0
    for x in xs:
        a, total, c = x.shape
        rows = total // groups
        outs.append(jax.ShapeDtypeStruct((a, rows, c), x.dtype))
        rb.append(pltpu.VMEM((2, groups - 1, a, rows, c // 2), x.dtype))
        own.append(pltpu.VMEM((2, 2, a, rows, c // 2), x.dtype))
        flops += a * total * c
        nbytes += 3 * x.size * x.dtype.itemsize
    scratch = rb + rb + own + [
        pltpu.SemaphoreType.DMA((2, groups - 1, n_in)),
        pltpu.SemaphoreType.DMA((2, groups - 1, n_in)),
        pltpu.SemaphoreType.DMA((2, 2, n_in)),
    ]
    return pl.pallas_call(
        functools.partial(ring_rs_kernel, groups, n_in),
        out_shape=outs,
        in_specs=[pl.BlockSpec(memory_space=pl.ANY)] * n_in,
        out_specs=[pl.BlockSpec(memory_space=pltpu.VMEM)] * n_in,
        scratch_shapes=scratch,
        compiler_params=pltpu.CompilerParams(
            collective_id=collective_id, has_side_effects=True, vmem_limit_bytes=60 * 1024 * 1024
        ),
        cost_estimate=pl.CostEstimate(flops=flops, bytes_accessed=nbytes, transcendentals=0),
    )(*xs)


def ring_ag_kernel(groups, *refs):
    in_up, in_down, in_dense, out_up, out_down, out_dense = refs[:6]
    ring_send, ring_recv, part_send, part_recv, local_sem = refs[6:]
    pos_of, dev_at = ring_order(groups)
    rx = lax.axis_index("rx")
    core = lax.axis_index("core")
    g = lax.axis_index("group")
    other = 1 - core
    pos = pos_of(g)
    nbr = (dev_at(pos + 1), dev_at(pos + groups - 1))
    gs = in_up.shape[1]
    fs = in_down.shape[1]
    width = in_dense.shape[1] // 2

    barrier = pltpu.get_barrier_semaphore()
    for n in nbr:
        pl.semaphore_signal(barrier, inc=1, device_id=(rx, core, n), device_id_type=MESH_ID)
    pl.semaphore_signal(barrier, inc=1, device_id=(rx, other, g), device_id_type=MESH_ID)
    pl.semaphore_wait(barrier, 3)

    def items(owner):
        found = []
        for k in range(2):
            e = 2 * k + owner
            found.append((in_up.at[e], lambda b, e=e: out_up.at[e, pl.ds(pl.multiple_of(b * gs, gs), gs)], F // 2))
            found.append((in_down.at[e], lambda b, e=e: out_down.at[e, pl.ds(pl.multiple_of(b * fs, fs), fs)], D // 2))
        dense_in = in_dense.at[:, pl.ds(owner * width, width)]
        found.append(
            (dense_in, lambda b: out_dense.at[pl.ds(pl.multiple_of(b * gs, gs), gs), pl.ds(owner * width, width)], width // 2)
        )
        return found

    mine = items(core)
    theirs = items(other)
    n_items = len(mine)

    locals_ = [pltpu.make_async_copy(in_up.at[e], out_up.at[e, pl.ds(pl.multiple_of(g * gs, gs), gs)], local_sem.at[e]) for e in range(E)]
    locals_ += [
        pltpu.make_async_copy(in_down.at[e], out_down.at[e, pl.ds(pl.multiple_of(g * fs, fs), fs)], local_sem.at[E + e])
        for e in range(E)
    ]
    locals_.append(pltpu.make_async_copy(in_dense, out_dense.at[pl.ds(pl.multiple_of(g * gs, gs), gs)], local_sem.at[2 * E]))
    for c in locals_:
        c.start()

    def block_at(d, s):
        if d == 0:
            return dev_at(pos + 2 * groups - 1 - s)
        return dev_at(pos + 1 + s)

    def ring_copy(d, s, j, src_block):
        src_in, dst_of, half = mine[j]
        cols = pl.ds(d * half, half)
        if src_block is None:
            src = src_in.at[:, cols]
            dst = dst_of(g).at[:, cols]
        else:
            src = dst_of(src_block).at[:, cols]
            dst = src
        return pltpu.make_async_remote_copy(
            src_ref=src, dst_ref=dst, send_sem=ring_send.at[d, s, j], recv_sem=ring_recv.at[d, s, j],
            device_id=(rx, core, nbr[d]), device_id_type=MESH_ID,
        )

    def part_copy(d, s, j, table, block):
        _, dst_of, half = table[j]
        view = dst_of(block).at[:, pl.ds(d * half, half)]
        return pltpu.make_async_remote_copy(
            src_ref=view, dst_ref=view, send_sem=part_send.at[d, s, j], recv_sem=part_recv.at[d, s, j],
            device_id=(rx, other, g), device_id_type=MESH_ID,
        )

    sends = []
    for d in range(2):
        for j in range(n_items):
            c = ring_copy(d, 0, j, None)
            c.start()
            sends.append(c)
    for s in range(groups - 1):
        for d in range(2):
            b = block_at(d, s)
            for j in range(n_items):
                pltpu.make_async_remote_copy(
                    src_ref=mine[j][1](b).at[:, pl.ds(d * mine[j][2], mine[j][2])],
                    dst_ref=mine[j][1](b).at[:, pl.ds(d * mine[j][2], mine[j][2])],
                    send_sem=ring_send.at[d, s, j], recv_sem=ring_recv.at[d, s, j],
                    device_id=(rx, core, nbr[d]), device_id_type=MESH_ID,
                ).wait_recv()
                if s + 1 < groups - 1:
                    c = ring_copy(d, s + 1, j, b)
                    c.start()
                    sends.append(c)
                c = part_copy(d, s, j, mine, b)
                c.start()
                sends.append(c)
    for s in range(groups - 1):
        for d in range(2):
            b = block_at(d, s)
            for j in range(n_items):
                part_copy(d, s, j, theirs, b).wait_recv()
    for c in sends:
        c.wait_send()
    for c in locals_:
        c.wait()


def ring_all_gather(up_b, down_b, dense_b, groups, collective_id):
    n_items = 5
    gs = up_b.shape[1]
    shapes = [
        jax.ShapeDtypeStruct((E, gs * groups, F), BF16),
        jax.ShapeDtypeStruct((E, down_b.shape[1] * groups, D), BF16),
        jax.ShapeDtypeStruct((gs * groups, dense_b.shape[1]), BF16),
    ]
    nbytes = sum(int(np.prod(s.shape)) * 2 for s in shapes)
    return pl.pallas_call(
        functools.partial(ring_ag_kernel, groups),
        out_shape=shapes,
        in_specs=[pl.BlockSpec(memory_space=pl.ANY)] * 3,
        out_specs=[pl.BlockSpec(memory_space=pl.ANY)] * 3,
        scratch_shapes=[
            pltpu.SemaphoreType.DMA((2, groups - 1, n_items)),
            pltpu.SemaphoreType.DMA((2, groups - 1, n_items)),
            pltpu.SemaphoreType.DMA((2, groups - 1, n_items)),
            pltpu.SemaphoreType.DMA((2, groups - 1, n_items)),
            pltpu.SemaphoreType.DMA((2 * E + 1,)),
        ],
        compiler_params=pltpu.CompilerParams(collective_id=collective_id, has_side_effects=True),
        cost_estimate=pl.CostEstimate(flops=0, bytes_accessed=nbytes, transcendentals=0),
    )(up_b, down_b, dense_b)


def grad_items(gu, gd, gdense, owner, gs, fs, width):
    found = []
    for k in range(2):
        e = 2 * k + owner
        found.append((lambda b, e=e: gu.at[e, pl.ds(pl.multiple_of(b * gs, gs), gs)], F // 2))
        found.append((lambda b, e=e: gd.at[e, pl.ds(pl.multiple_of(b * fs, fs), fs)], D // 2))
    found.append((lambda b: gdense.at[pl.ds(pl.multiple_of(b * gs, gs), gs), pl.ds(owner * width, width)], width // 2))
    return found


def ring_rs2_kernel(groups, x_pair, *refs):
    gu, gd, gdense, out_up, out_down, out_dense = refs[:6]
    n_items = 5
    scr = refs[6:]
    rbuf, sbuf, pbuf, own, fin, xr, cr = (scr[i * n_items : (i + 1) * n_items] for i in range(7))
    ring_send, ring_recv, part_send, part_recv, load_sem, x_send, x_recv, c_send, c_recv = scr[7 * n_items :]
    pos_of, dev_at = ring_order(groups)
    rx = lax.axis_index("rx")
    core = lax.axis_index("core")
    g = lax.axis_index("group")
    other = 1 - core
    pos = pos_of(g)
    nbr = (dev_at(pos + 1), dev_at(pos + groups - 1))
    gs = gu.shape[1] // groups
    fs = gd.shape[1] // groups
    width = gdense.shape[1] // 2
    mine = grad_items(gu, gd, gdense, core, gs, fs, width)
    theirs = grad_items(gu, gd, gdense, other, gs, fs, width)

    barrier = pltpu.get_barrier_semaphore()
    for n in nbr:
        pl.semaphore_signal(barrier, inc=1, device_id=(rx, core, n), device_id_type=MESH_ID)
    pl.semaphore_signal(barrier, inc=1, device_id=(rx, other, g), device_id_type=MESH_ID)
    count = 3
    if x_pair:
        pl.semaphore_signal(barrier, inc=1, device_id=(1 - rx, core, g), device_id_type=MESH_ID)
        count = 4
    pl.semaphore_wait(barrier, count)

    def block_at(d, s):
        if d == 0:
            return dev_at(pos + 2 * groups - 1 - s)
        return dev_at(pos + 1 + s)

    def cols(j, d):
        half = mine[j][1]
        return pl.ds(d * half, half)

    def load(d, s, slot, j):
        return pltpu.make_async_copy(mine[j][0](block_at(d, s)).at[:, cols(j, d)], own[j].at[d, slot], load_sem.at[d, slot, j])

    def part(d, s, j):
        return pltpu.make_async_remote_copy(
            src_ref=theirs[j][0](block_at(d, s)).at[:, cols(j, d)], dst_ref=pbuf[j].at[d, s],
            send_sem=part_send.at[d, s, j], recv_sem=part_recv.at[d, s, j],
            device_id=(rx, other, g), device_id_type=MESH_ID,
        )

    def ring(d, s, j):
        return pltpu.make_async_remote_copy(
            src_ref=sbuf[j].at[d, s], dst_ref=rbuf[j].at[d, s],
            send_sem=ring_send.at[d, s, j], recv_sem=ring_recv.at[d, s, j],
            device_id=(rx, core, nbr[d]), device_id_type=MESH_ID,
        )

    sends = []
    for d in range(2):
        for j in range(n_items):
            load(d, 0, 0, j).start()
            c = part(d, 0, j)
            c.start()
            sends.append(c)
    for s in range(groups):
        slot = s % 2
        for d in range(2):
            for j in range(n_items):
                load(d, s, slot, j).wait()
                if s + 1 < groups:
                    load(d, s + 1, 1 - slot, j).start()
                    c = part(d, s + 1, j)
                    c.start()
                    sends.append(c)
                part(d, s, j).wait_recv()
                val = own[j][d, slot].astype(F32) + pbuf[j][d, s].astype(F32)
                if s > 0:
                    ring(d, s - 1, j).wait_recv()
                    val = val + rbuf[j][d, s - 1].astype(F32)
                if s < groups - 1:
                    sbuf[j][d, s] = val.astype(BF16)
                    c = ring(d, s, j)
                    c.start()
                    sends.append(c)
                else:
                    fin[j][d] = val

    for c in sends:
        c.wait_send()
    sends = []
    if x_pair:
        x_copies = []
        for d in range(2):
            for j in range(n_items):
                sbuf[j][d, 0] = fin[j][d].astype(BF16)
                c = pltpu.make_async_remote_copy(
                    src_ref=sbuf[j].at[d, 0], dst_ref=xr[j].at[d], send_sem=x_send.at[d, j], recv_sem=x_recv.at[d, j],
                    device_id=(1 - rx, core, g), device_id_type=MESH_ID,
                )
                c.start()
                x_copies.append(c)
        for c in x_copies:
            c.wait_recv()
        for d in range(2):
            for j in range(n_items):
                fin[j][d] = sbuf[j][d, 0].astype(F32) + xr[j][d].astype(F32)
        sends += x_copies

    c_copies = []
    for d in range(2):
        for j in range(n_items):
            c = pltpu.make_async_remote_copy(
                src_ref=fin[j].at[d], dst_ref=cr[j].at[d], send_sem=c_send.at[d, j], recv_sem=c_recv.at[d, j],
                device_id=(rx, other, g), device_id_type=MESH_ID,
            )
            c.start()
            c_copies.append(c)

    def out_items(owner):
        found = []
        for k in range(2):
            e = 2 * k + owner
            found.append(lambda d, e=e: out_up.at[e, :, pl.ds(d * (F // 2), F // 2)])
            found.append(lambda d, e=e: out_down.at[e, :, pl.ds(d * (D // 2), D // 2)])
        found.append(lambda d: out_dense.at[:, pl.ds(owner * width + d * (width // 2), width // 2)])
        return found

    mine_out = out_items(core)
    theirs_out = out_items(other)
    for d in range(2):
        for j in range(n_items):
            mine_out[j](d)[...] = fin[j][d]
    for c in c_copies:
        c.wait_recv()
    for d in range(2):
        for j in range(n_items):
            theirs_out[j](d)[...] = cr[j][d]
    for c in sends + c_copies:
        c.wait_send()


def grad_reduce(gu, gd, gdense, groups, x_pair, collective_id):
    gs = gu.shape[1] // groups
    fs = gd.shape[1] // groups
    width = gdense.shape[1] // 2
    item_shapes = [(gs, F // 2), (fs, D // 2), (gs, F // 2), (fs, D // 2), (gs, width // 2)]
    scratch = []
    for lead, dtype in (((2, groups - 1), BF16), ((2, groups - 1), BF16), ((2, groups), BF16), ((2, 2), BF16), ((2,), F32), ((2,), BF16), ((2,), F32)):
        scratch += [pltpu.VMEM(lead + shp, dtype) for shp in item_shapes]
    scratch += [
        pltpu.SemaphoreType.DMA((2, groups - 1, 5)),
        pltpu.SemaphoreType.DMA((2, groups - 1, 5)),
        pltpu.SemaphoreType.DMA((2, groups, 5)),
        pltpu.SemaphoreType.DMA((2, groups, 5)),
        pltpu.SemaphoreType.DMA((2, 2, 5)),
        pltpu.SemaphoreType.DMA((2, 5)),
        pltpu.SemaphoreType.DMA((2, 5)),
        pltpu.SemaphoreType.DMA((2, 5)),
        pltpu.SemaphoreType.DMA((2, 5)),
    ]
    outs = [
        jax.ShapeDtypeStruct((E, gs, F), F32),
        jax.ShapeDtypeStruct((E, fs, D), F32),
        jax.ShapeDtypeStruct((gs, gdense.shape[1]), F32),
    ]
    nbytes = 2 * (gu.size + gd.size + gdense.size)
    return pl.pallas_call(
        functools.partial(ring_rs2_kernel, groups, x_pair),
        out_shape=outs,
        in_specs=[pl.BlockSpec(memory_space=pl.ANY)] * 3,
        out_specs=[pl.BlockSpec(memory_space=pltpu.VMEM)] * 3,
        scratch_shapes=scratch,
        compiler_params=pltpu.CompilerParams(
            collective_id=collective_id, has_side_effects=True, vmem_limit_bytes=62 * 1024 * 1024
        ),
        cost_estimate=pl.CostEstimate(flops=gu.size + gd.size + gdense.size, bytes_accessed=nbytes, transcendentals=0),
    )(gu, gd, gdense)


TILE = 128
TILE_B = 256
CAPP = 512
SQRT_HALF = float(np.sqrt(0.5))
INV_SQRT_2PI = float(1.0 / np.sqrt(2.0 * np.pi))


def ffn_fwd_kernel(micro, counts, x_ref, w1_ref, b1_ref, w2_ref, b2_ref, hp_ref, h_ref, y_ref):
    e, m, t = pl.program_id(0), pl.program_id(1), pl.program_id(2)
    active = t * TILE < counts[e * micro + m]

    @pl.when(active)
    def _():
        hp = jnp.dot(x_ref[0], w1_ref[0], preferred_element_type=F32) + b1_ref[0]
        h = (0.5 * hp * (1.0 + lax.erf(hp * SQRT_HALF))).astype(BF16)
        hp_ref[0] = hp
        h_ref[0] = h
        y = jnp.dot(h, w2_ref[0], preferred_element_type=F32) + b2_ref[0]
        hi = y.astype(BF16)
        y_ref[0, :, :D] = hi
        y_ref[0, :, D:] = (y - hi.astype(F32)).astype(BF16)

    @pl.when(jnp.logical_not(active))
    def _():
        y_ref[0] = jnp.zeros(y_ref.shape[1:], BF16)


def ffn_forward(counts, table_in, w1, b1, w2, b2, micro):
    tiles = CAPP // TILE
    rows = table_in.shape[1]
    row_map = lambda e, m, t, c: (m, e * tiles + t, 0)
    w_map = lambda e, m, t, c: (e, 0, 0)
    grid_spec = pltpu.PrefetchScalarGridSpec(
        num_scalar_prefetch=1,
        grid=(E, micro, tiles),
        in_specs=[
            pl.BlockSpec((1, TILE, D), row_map),
            pl.BlockSpec((1, D, F), w_map),
            pl.BlockSpec((1, 1, F), w_map),
            pl.BlockSpec((1, F, D), w_map),
            pl.BlockSpec((1, 1, D), w_map),
        ],
        out_specs=[
            pl.BlockSpec((1, TILE, F), row_map),
            pl.BlockSpec((1, TILE, F), row_map),
            pl.BlockSpec((1, TILE, 2 * D), row_map),
        ],
    )
    work = micro * rows
    return pl.pallas_call(
        functools.partial(ffn_fwd_kernel, micro),
        grid_spec=grid_spec,
        out_shape=[
            jax.ShapeDtypeStruct((micro, rows, F), F32),
            jax.ShapeDtypeStruct((micro, rows, F), BF16),
            jax.ShapeDtypeStruct((micro, rows, 2 * D), BF16),
        ],
        compiler_params=pltpu.CompilerParams(vmem_limit_bytes=48 * 1024 * 1024),
        cost_estimate=pl.CostEstimate(
            flops=4 * work * D * F // 2, bytes_accessed=work * (2 * D + 6 * F + 4 * D) // 2, transcendentals=work * F // 2
        ),
    )(counts, table_in, w1, b1, w2, b2)


def ffn_bwd_kernel(micro, counts, dy_ref, x_ref, hp_ref, h_ref, w1_ref, w2_ref, dt_ref, gu_ref, gd_ref, gb_ref, gb2_ref, gu_acc, gd_acc):
    e, m, t = pl.program_id(0), pl.program_id(1), pl.program_id(2)
    active = t * TILE_B < counts[e * micro + m]

    @pl.when((m == 0) & (t == 0))
    def _():
        gu_acc[...] = jnp.zeros(gu_acc.shape, F32)
        gd_acc[...] = jnp.zeros(gd_acc.shape, F32)
        gb_ref[...] = jnp.zeros(gb_ref.shape, F32)
        gb2_ref[...] = jnp.zeros(gb2_ref.shape, F32)

    @pl.when(active)
    def _():
        dy = dy_ref[0]
        hp = hp_ref[0]
        d_hidden = lax.dot_general(dy, w2_ref[0], (((1,), (1,)), ((), ())), preferred_element_type=F32)
        slope = 0.5 * (1.0 + lax.erf(hp * SQRT_HALF)) + hp * jnp.exp(-0.5 * hp * hp) * INV_SQRT_2PI
        d_pre = (d_hidden * slope).astype(BF16)
        dt = lax.dot_general(d_pre, w1_ref[0], (((1,), (1,)), ((), ())), preferred_element_type=F32)
        hi = dt.astype(BF16)
        dt_ref[0, :, :D] = hi
        dt_ref[0, :, D:] = (dt - hi.astype(F32)).astype(BF16)
        gb2_ref[0] += jnp.sum(dy.astype(F32), 0, keepdims=True)
        gu_acc[...] += lax.dot_general(x_ref[0], d_pre, (((0,), (0,)), ((), ())), preferred_element_type=F32)
        gd_acc[...] += lax.dot_general(h_ref[0], dy, (((0,), (0,)), ((), ())), preferred_element_type=F32)
        gb_ref[0] += jnp.sum(d_pre.astype(F32), 0, keepdims=True)

    @pl.when(jnp.logical_not(active))
    def _():
        dt_ref[0] = jnp.zeros(dt_ref.shape[1:], BF16)

    @pl.when((m == micro - 1) & (t == pl.num_programs(2) - 1))
    def _():
        gu_ref[0] = gu_acc[...].astype(BF16)
        gd_ref[0] = gd_acc[...].astype(BF16)


def ffn_backward(counts, d_expert, table_in, hp, h, w1, w2, micro):
    tiles = CAPP // TILE_B
    rows = table_in.shape[1]
    row_map = lambda e, m, t, c: (m, e * tiles + t, 0)
    w_map = lambda e, m, t, c: (e, 0, 0)
    grid_spec = pltpu.PrefetchScalarGridSpec(
        num_scalar_prefetch=1,
        grid=(E, micro, tiles),
        in_specs=[
            pl.BlockSpec((1, TILE_B, D), row_map),
            pl.BlockSpec((1, TILE_B, D), row_map),
            pl.BlockSpec((1, TILE_B, F), row_map),
            pl.BlockSpec((1, TILE_B, F), row_map),
            pl.BlockSpec((1, D, F), w_map),
            pl.BlockSpec((1, F, D), w_map),
        ],
        out_specs=[
            pl.BlockSpec((1, TILE_B, 2 * D), row_map),
            pl.BlockSpec((1, D, F), w_map),
            pl.BlockSpec((1, F, D), w_map),
            pl.BlockSpec((1, 1, F), w_map),
            pl.BlockSpec((1, 1, D), w_map),
        ],
        scratch_shapes=[pltpu.VMEM((D, F), F32), pltpu.VMEM((F, D), F32)],
    )
    work = micro * rows
    return pl.pallas_call(
        functools.partial(ffn_bwd_kernel, micro),
        grid_spec=grid_spec,
        out_shape=[
            jax.ShapeDtypeStruct((micro, rows, 2 * D), BF16),
            jax.ShapeDtypeStruct((E, D, F), BF16),
            jax.ShapeDtypeStruct((E, F, D), BF16),
            jax.ShapeDtypeStruct((E, 1, F), F32),
            jax.ShapeDtypeStruct((E, 1, D), F32),
        ],
        compiler_params=pltpu.CompilerParams(vmem_limit_bytes=60 * 1024 * 1024),
        cost_estimate=pl.CostEstimate(
            flops=8 * work * D * F // 2, bytes_accessed=work * (8 * D + 6 * F) // 2 + 16 * E * D * F, transcendentals=2 * work * F // 2
        ),
    )(counts, d_expert, table_in, hp, h, w1, w2)

def layer_norm(value, gain, shift):
    center = value - jnp.mean(value, -1, keepdims=True)
    spread = jnp.mean(center * center, -1, keepdims=True)
    return center * lax.rsqrt(spread + 1e-06) * gain + shift


def gelu_exact(value):
    return jax.nn.gelu(value, approximate=False)


def split_heads(part):
    return part.reshape(-1, S, HEADS, HEAD_DIM)


def dot(a, b):
    return jnp.dot(a, b, preferred_element_type=F32)


def assign_places(route):
    chosen = jnp.concatenate([route[:, :, 0], route[:, :, 1]], 1)
    hits = (chosen[:, :, None] == jnp.arange(E, dtype=jnp.int32)).astype(jnp.int32)
    before = jnp.cumsum(hits, 1) - hits
    slot = jnp.sum(before * hits, 2)
    return chosen * CAPP + slot, jnp.sum(hits, 1)


def hi_lo(v):
    hi = v.astype(BF16)
    lo = (v - hi.astype(F32)).astype(BF16)
    return jnp.concatenate([hi, lo], -1)


def pick_rows(onehot, split):
    both = jnp.einsum("mnr,mrd->mnd", onehot, split, preferred_element_type=F32)
    return both[..., :D] + both[..., D:]


def pack_dense(qkv_w, out_w, router_w, vectors, up_bias):
    rows = qkv_w.shape[0]
    ub = up_bias.reshape(E, rows, 4).transpose(1, 0, 2).reshape(rows, E * 4)
    return jnp.concatenate([qkv_w, out_w, router_w, vectors.T, ub], 1)


def unpack_dense(packed):
    rows = packed.shape[0]
    w_qkv = packed[:, : 3 * D]
    w_out = packed[:, 3 * D : 4 * D]
    w_router = packed[:, 4 * D : 4 * D + E]
    table = packed[:, 4 * D + E : 4 * D + E + NV].T
    ub = packed[:, 4 * D + E + NV :].reshape(rows, E, 4).transpose(1, 0, 2).reshape(E, rows * 4)
    return w_qkv, w_out, w_router, table, ub


def attention_fwd(w_qkv, w_out, table, value):
    rows = value.shape[0]
    scale = HEAD_DIM ** (-0.5)
    first = layer_norm(value, table[0], table[1]).astype(BF16)
    qkv_bias = jnp.concatenate([table[2], jnp.zeros((D,), F32), table[3]])
    qkv = (dot(first, w_qkv) + qkv_bias).astype(BF16)
    query, key_part, val_part = (
        split_heads(qkv[:, :D]),
        split_heads(qkv[:, D : 2 * D]),
        split_heads(qkv[:, 2 * D :]),
    )
    scores = jnp.einsum("bqhd,bkhd->bhqk", query, key_part, preferred_element_type=F32) * scale
    peak = jnp.max(scores, -1, keepdims=True)
    expo = jnp.exp(scores - peak)
    total = jnp.sum(expo, -1, keepdims=True)
    probs_att = (expo / total).astype(BF16)
    log_total = peak + jnp.log(total)
    attended = jnp.einsum("bhqk,bkhd->bqhd", probs_att, val_part, preferred_element_type=F32)
    attended = attended.reshape(rows, D).astype(BF16)
    resid = value + (dot(attended, w_out) + table[4])
    return first, qkv, log_total, attended, resid


def attention_bwd(w_qkv, w_out, table, value, first, qkv, log_total, attended, d_resid):
    rows = value.shape[0]
    scale = HEAD_DIM ** (-0.5)
    d_branch = d_resid.astype(BF16)
    g_bias_out = jnp.sum(d_branch.astype(F32), 0)
    g_out = lax.dot_general(attended, d_branch, (((0,), (0,)), ((), ())), preferred_element_type=F32)
    d_att = split_heads(
        lax.dot_general(d_branch, w_out, (((1,), (1,)), ((), ())), preferred_element_type=F32).astype(BF16)
    )
    query, key_part, val_part = (
        split_heads(qkv[:, :D]),
        split_heads(qkv[:, D : 2 * D]),
        split_heads(qkv[:, 2 * D :]),
    )
    scores = jnp.einsum("bqhd,bkhd->bhqk", query, key_part, preferred_element_type=F32) * scale
    probs_f = jnp.exp(scores - log_total)
    probs_att = probs_f.astype(BF16)
    d_val = jnp.einsum("bhqk,bqhd->bkhd", probs_att, d_att, preferred_element_type=F32)
    d_prob = jnp.einsum("bqhd,bkhd->bhqk", d_att, val_part, preferred_element_type=F32)
    d_score = (probs_f * (d_prob - jnp.sum(d_prob * probs_f, -1, keepdims=True))).astype(BF16)
    d_query = jnp.einsum("bhqk,bkhd->bqhd", d_score, key_part, preferred_element_type=F32) * scale
    d_key = jnp.einsum("bhqk,bqhd->bkhd", d_score, query, preferred_element_type=F32) * scale
    d_qkv = jnp.concatenate(
        [d_query.reshape(rows, D), d_key.reshape(rows, D), d_val.reshape(rows, D)], 1
    ).astype(BF16)
    d_qkv_f = d_qkv.astype(F32)
    g_bias_q = jnp.sum(d_qkv_f[:, :D], 0)
    g_bias_v = jnp.sum(d_qkv_f[:, 2 * D :], 0)
    g_qkv = lax.dot_general(first, d_qkv, (((0,), (0,)), ((), ())), preferred_element_type=F32)
    d_first = lax.dot_general(d_qkv, w_qkv, (((1,), (1,)), ((), ())), preferred_element_type=F32)
    first_pull = jax.vjp(layer_norm, value, table[0], table[1])[1]
    d_input, g_gain_one, g_shift_one = first_pull(d_first)
    return (g_qkv, g_out, g_bias_out, g_bias_q, g_bias_v, g_gain_one, g_shift_one), d_input


def adamw(weight, moments, grad, rate):
    first = 0.5 * moments[0] + 0.5 * grad
    root = jnp.sqrt(0.5 * moments[1] * moments[1] + 0.5 * grad * grad)
    update = first / (root + 1e-08)
    which = lax.broadcasted_iota(jnp.int32, moments.shape, 0) == 0
    both = jnp.where(which, 0.5 * moments + 0.5 * grad, jnp.sqrt(0.5 * moments * moments + 0.5 * grad * grad))
    return (weight - rate * (update + 0.1 * weight), both)


def shards(
    tokens,
    cotangent,
    expert_index,
    qkv_weight,
    out_weight,
    router_weight,
    up_weight,
    up_bias,
    down_weight,
    vectors,
    qkv_moments,
    out_moments,
    router_moments,
    up_moments,
    up_bias_moments,
    down_moments,
    vector_moments,
):
    rows = tokens.shape[0]
    micro = rows // MB_TOK
    gs = qkv_weight.shape[0]
    group_size = D // gs
    core = lax.axis_index("core")

    dense_in = pack_dense(qkv_weight, out_weight, router_weight, vectors, up_bias)
    width = dense_in.shape[1]
    dense_in = jnp.pad(dense_in, ((0, 0), (0, DENSE_AG - width))).astype(BF16)
    w_up_all, w_down_all, dense = ring_all_gather(
        up_weight.astype(BF16), down_weight.astype(BF16), dense_in, group_size, 1
    )
    w_qkv, w_out, w_router, table_b, b_up_b = unpack_dense(dense[:, :width])
    table = table_b.astype(F32)
    b_up = b_up_b.astype(F32)

    value = tokens.astype(F32)
    d_out = cotangent.astype(F32)
    first, qkv, log_total, attended, resid = attention_fwd(w_qkv, w_out, table, value)
    second = layer_norm(resid, table[5], table[6]).astype(BF16)
    logits = dot(second, w_router)
    probs = jax.nn.softmax(logits, -1)
    picked = expert_index[:, :, None] == jnp.arange(E, dtype=jnp.int32)
    gate = jnp.sum(jnp.where(picked, probs[:, None, :], 0.0), -1)

    route = expert_index.reshape(micro, MB_TOK, 2)
    places, counts = assign_places(route)
    counts = counts.T.reshape(E * micro)
    onehot = (places[:, :, None] == jnp.arange(E * CAPP, dtype=jnp.int32)).astype(BF16)
    second_m = second.reshape(micro, MB_TOK, D)
    pair = jnp.concatenate([second_m, second_m], 1)
    table_in = jnp.einsum("mnr,mnd->mrd", onehot, pair, preferred_element_type=F32).astype(BF16)

    hidden_pre, hidden, y_all = ffn_forward(
        counts, table_in, w_up_all, b_up[:, None, :], w_down_all, table[7 : 7 + E][:, None, :], micro
    )
    picked_rows = pick_rows(onehot, y_all)
    out_zero = picked_rows[:, :MB_TOK].reshape(rows, D)
    out_one = picked_rows[:, MB_TOK:].reshape(rows, D)
    result = resid + (gate[:, 0:1] * out_zero + gate[:, 1:2] * out_one)

    d_gate = jnp.stack([jnp.sum(d_out * out_zero, -1), jnp.sum(d_out * out_one, -1)], 1)
    d_out_m = d_out.reshape(micro, MB_TOK, D)
    gate_m = gate.reshape(micro, MB_TOK, 2)
    weighted = jnp.concatenate([gate_m[:, :, 0:1] * d_out_m, gate_m[:, :, 1:2] * d_out_m], 1).astype(BF16)
    d_expert = jnp.einsum("mnr,mnd->mrd", onehot, weighted, preferred_element_type=F32).astype(BF16)

    d_table, g_up, g_down, g_b1, g_b2 = ffn_backward(counts, d_expert, table_in, hidden_pre, hidden, w_up_all, w_down_all, micro)
    g_up_bias_all = g_b1[:, 0, :]
    g_bias_down = g_b2[:, 0, :]

    onehot_sum = onehot[:, :MB_TOK] + onehot[:, MB_TOK:]
    d_picked = pick_rows(onehot_sum, d_table).reshape(rows, D)

    d_probs = jnp.sum(jnp.where(picked, d_gate[:, :, None], 0.0), 1)
    d_logit = (probs * (d_probs - jnp.sum(d_probs * probs, -1, keepdims=True))).astype(BF16)
    g_router = lax.dot_general(second, d_logit, (((0,), (0,)), ((), ())), preferred_element_type=F32)
    d_second = d_picked + lax.dot_general(d_logit, w_router, (((1,), (1,)), ((), ())), preferred_element_type=F32)
    norm_pull = jax.vjp(layer_norm, resid, table[5], table[6])[1]
    d_resid, g_gain_two, g_shift_two = norm_pull(d_second)
    d_resid = d_out + d_resid

    att_grads, d_input = attention_bwd(w_qkv, w_out, table, value, first, qkv, log_total, attended, d_resid)
    g_qkv, g_out, g_bias_out, g_bias_q, g_bias_v, g_gain_one, g_shift_one = att_grads
    input_grad = d_resid + d_input

    g_table = jnp.concatenate(
        [
            jnp.stack([g_gain_one, g_shift_one, g_bias_q, g_bias_v, g_bias_out, g_gain_two, g_shift_two]),
            g_bias_down,
        ],
        0,
    )
    dense_g = pack_dense(g_qkv, g_out, g_router, g_table, g_up_bias_all)
    width = dense_g.shape[1]
    dense_g = jnp.pad(dense_g, ((0, 0), (0, DENSE_AG - width))).astype(BF16)
    x_pair = lax.axis_size("rx") == 2
    r_up, r_down, r_dense = grad_reduce(g_up, g_down, dense_g, group_size, x_pair, 0)
    if not x_pair:
        r_up, r_down, r_dense = lax.psum((r_up, r_down, r_dense), "rx")
    r_qkv, r_out, r_router, r_table, r_ub = unpack_dense(r_dense[:, :width])

    reduced = (r_qkv, r_out, r_router, r_up, r_ub, r_down, r_table)
    rates = (
        2.0 * D ** (-0.5),
        2.0 * (D // 32) ** (-0.5),
        2.0 * (2 * D) ** (-0.5),
        2.0 * D ** (-0.5),
        0.2,
        2.0 * (F // 16) ** (-0.5),
        0.2,
    )
    params = (qkv_weight, out_weight, router_weight, up_weight, up_bias, down_weight, vectors)
    moments = (qkv_moments, out_moments, router_moments, up_moments, up_bias_moments, down_moments, vector_moments)
    news = []
    states = []
    for weight, state, grad, rate in zip(params, moments, reduced, rates):
        new_weight, new_state = adamw(weight, state, grad, rate)
        news.append(new_weight)
        states.append(new_state)
    return (result.astype(BF16), input_grad) + reduced + tuple(news) + tuple(states)


def solution(mesh):
    replica, group = mesh.shape["replica"], mesh.shape["group"]
    view = Mesh(np.asarray(mesh.devices).reshape(replica // 2, 2, group), ("rx", "core", "group"))
    in_specs = (
        P(TOK, None),
        P(TOK, None),
        P(TOK, None),
        P("group", None),
        P("group", None),
        P("group", None),
        P(None, "group", None),
        P(None, "group"),
        P(None, "group", None),
        P(None, "group"),
        P(None, "group", None),
        P(None, "group", None),
        P(None, "group", None),
        P(None, None, "group", None),
        P(None, None, "group"),
        P(None, None, "group", None),
        P(None, None, "group"),
    )
    out_specs = (
        P(TOK, None),
        P(TOK, None),
        P("group", None),
        P("group", None),
        P("group", None),
        P(None, "group", None),
        P(None, "group"),
        P(None, "group", None),
        P(None, "group"),
        P("group", None),
        P("group", None),
        P("group", None),
        P(None, "group", None),
        P(None, "group"),
        P(None, "group", None),
        P(None, "group"),
        P(None, "group", None),
        P(None, "group", None),
        P(None, "group", None),
        P(None, None, "group", None),
        P(None, None, "group"),
        P(None, None, "group", None),
        P(None, None, "group"),
    )
    return jax.shard_map(shards, mesh=view, in_specs=in_specs, out_specs=out_specs, check_vma=False)
```

```python
import functools

import jax
import jax.numpy as jnp
import numpy as np
from jax import lax
from jax.sharding import Mesh
from jax.sharding import PartitionSpec as P
from jax.experimental import pallas as pl
from jax.experimental.pallas import tpu as pltpu

D = 512
HEADS = 8
HEAD_DIM = 64
F = 2048
E = 4
S = 197
MB_TOK = 394
CAP = 392
NV = 11
DENSE_AG = 2560
DENSE_PAD = 2304
F32 = jnp.float32
BF16 = jnp.bfloat16
TOK = ("rx", "core", "group")


MESH_ID = pl.DeviceIdType.MESH


def ring_order(groups):
    if groups in (4, 8):
        zs = groups // 2

        def pos_of(g):
            y = g % 2
            z = g // 2
            return z + y * (2 * zs - 1 - 2 * z)

        def dev_at(p):
            p = p % groups
            yy = p // zs
            return 2 * (p + yy * (2 * zs - 1 - 2 * p)) + yy

        return pos_of, dev_at
    return (lambda g: g), (lambda p: p % groups)


def ring_rs_kernel(groups, n_in, *refs):
    ins = refs[:n_in]
    outs = refs[n_in : 2 * n_in]
    rbufs = refs[2 * n_in : 3 * n_in]
    sbufs = refs[3 * n_in : 4 * n_in]
    owns = refs[4 * n_in : 5 * n_in]
    send_sem, recv_sem, load_sem = refs[5 * n_in :]
    pos_of, dev_at = ring_order(groups)
    rx = lax.axis_index("rx")
    core = lax.axis_index("core")
    g = lax.axis_index("group")
    pos = pos_of(g)
    nbr = (dev_at(pos + 1), dev_at(pos + groups - 1))

    barrier = pltpu.get_barrier_semaphore()
    for n in nbr:
        pl.semaphore_signal(barrier, inc=1, device_id=(rx, core, n), device_id_type=MESH_ID)
    pl.semaphore_wait(barrier, 2)

    def block_dev(d, s):
        if d == 0:
            return dev_at(pos + 2 * groups - s - 1)
        return dev_at(pos + s + 1)

    def load(d, s, slot):
        b = block_dev(d, s)
        copies = []
        for i in range(n_in):
            rows = ins[i].shape[1] // groups
            half = ins[i].shape[2] // 2
            src = ins[i].at[:, pl.ds(pl.multiple_of(b * rows, rows), rows), pl.ds(d * half, half)]
            copies.append(pltpu.make_async_copy(src, owns[i].at[d, slot], load_sem.at[d, slot, i]))
        return copies

    def remote(d, s, i):
        return pltpu.make_async_remote_copy(
            src_ref=sbufs[i].at[d, s],
            dst_ref=rbufs[i].at[d, s],
            send_sem=send_sem.at[d, s, i],
            recv_sem=recv_sem.at[d, s, i],
            device_id=(rx, core, nbr[d]),
            device_id_type=MESH_ID,
        )

    for d in range(2):
        for c in load(d, 0, 0):
            c.start()
    sends = []
    for s in range(groups):
        slot = s % 2
        for d in range(2):
            for c in load(d, s, slot):
                c.wait()
            if s + 1 < groups:
                for c in load(d, s + 1, 1 - slot):
                    c.start()
            for i in range(n_in):
                if s > 0:
                    remote(d, s - 1, i).wait_recv()
                for a in range(ins[i].shape[0]):
                    mine = owns[i][d, slot, a].astype(F32)
                    if s > 0:
                        mine = mine + rbufs[i][d, s - 1, a].astype(F32)
                    if s < groups - 1:
                        sbufs[i][d, s, a] = mine.astype(sbufs[i].dtype)
                    else:
                        half = ins[i].shape[2] // 2
                        outs[i][a, :, pl.ds(d * half, half)] = mine.astype(outs[i].dtype)
                if s < groups - 1:
                    c = remote(d, s, i)
                    c.start()
                    sends.append(c)
    for c in sends:
        c.wait_send()


def ring_reduce_scatter(xs, groups, collective_id):
    n_in = len(xs)
    outs, rb, own = [], [], []
    flops = 0
    nbytes = 0
    for x in xs:
        a, total, c = x.shape
        rows = total // groups
        outs.append(jax.ShapeDtypeStruct((a, rows, c), x.dtype))
        rb.append(pltpu.VMEM((2, groups - 1, a, rows, c // 2), x.dtype))
        own.append(pltpu.VMEM((2, 2, a, rows, c // 2), x.dtype))
        flops += a * total * c
        nbytes += 3 * x.size * x.dtype.itemsize
    scratch = rb + rb + own + [
        pltpu.SemaphoreType.DMA((2, groups - 1, n_in)),
        pltpu.SemaphoreType.DMA((2, groups - 1, n_in)),
        pltpu.SemaphoreType.DMA((2, 2, n_in)),
    ]
    return pl.pallas_call(
        functools.partial(ring_rs_kernel, groups, n_in),
        out_shape=outs,
        in_specs=[pl.BlockSpec(memory_space=pl.ANY)] * n_in,
        out_specs=[pl.BlockSpec(memory_space=pltpu.VMEM)] * n_in,
        scratch_shapes=scratch,
        compiler_params=pltpu.CompilerParams(
            collective_id=collective_id, has_side_effects=True, vmem_limit_bytes=60 * 1024 * 1024
        ),
        cost_estimate=pl.CostEstimate(flops=flops, bytes_accessed=nbytes, transcendentals=0),
    )(*xs)


def ring_ag_kernel(groups, *refs):
    in_up, in_down, in_dense, out_up, out_down, out_dense = refs[:6]
    ring_send, ring_recv, part_send, part_recv, local_sem = refs[6:]
    pos_of, dev_at = ring_order(groups)
    rx = lax.axis_index("rx")
    core = lax.axis_index("core")
    g = lax.axis_index("group")
    other = 1 - core
    pos = pos_of(g)
    nbr = (dev_at(pos + 1), dev_at(pos + groups - 1))
    gs = in_up.shape[1]
    fs = in_down.shape[1]
    width = in_dense.shape[1] // 2

    barrier = pltpu.get_barrier_semaphore()
    for n in nbr:
        pl.semaphore_signal(barrier, inc=1, device_id=(rx, core, n), device_id_type=MESH_ID)
    pl.semaphore_signal(barrier, inc=1, device_id=(rx, other, g), device_id_type=MESH_ID)
    pl.semaphore_wait(barrier, 3)

    def items(owner):
        found = []
        for k in range(2):
            e = 2 * k + owner
            found.append((in_up.at[e], lambda b, e=e: out_up.at[e, pl.ds(pl.multiple_of(b * gs, gs), gs)], F // 2))
            found.append((in_down.at[e], lambda b, e=e: out_down.at[e, pl.ds(pl.multiple_of(b * fs, fs), fs)], D // 2))
        dense_in = in_dense.at[:, pl.ds(owner * width, width)]
        found.append(
            (dense_in, lambda b: out_dense.at[pl.ds(pl.multiple_of(b * gs, gs), gs), pl.ds(owner * width, width)], width // 2)
        )
        return found

    mine = items(core)
    theirs = items(other)
    n_items = len(mine)

    locals_ = [pltpu.make_async_copy(in_up.at[e], out_up.at[e, pl.ds(pl.multiple_of(g * gs, gs), gs)], local_sem.at[e]) for e in range(E)]
    locals_ += [
        pltpu.make_async_copy(in_down.at[e], out_down.at[e, pl.ds(pl.multiple_of(g * fs, fs), fs)], local_sem.at[E + e])
        for e in range(E)
    ]
    locals_.append(pltpu.make_async_copy(in_dense, out_dense.at[pl.ds(pl.multiple_of(g * gs, gs), gs)], local_sem.at[2 * E]))
    for c in locals_:
        c.start()

    def block_at(d, s):
        if d == 0:
            return dev_at(pos + 2 * groups - 1 - s)
        return dev_at(pos + 1 + s)

    def ring_copy(d, s, j, src_block):
        src_in, dst_of, half = mine[j]
        cols = pl.ds(d * half, half)
        if src_block is None:
            src = src_in.at[:, cols]
            dst = dst_of(g).at[:, cols]
        else:
            src = dst_of(src_block).at[:, cols]
            dst = src
        return pltpu.make_async_remote_copy(
            src_ref=src, dst_ref=dst, send_sem=ring_send.at[d, s, j], recv_sem=ring_recv.at[d, s, j],
            device_id=(rx, core, nbr[d]), device_id_type=MESH_ID,
        )

    def part_copy(d, s, j, table, block):
        _, dst_of, half = table[j]
        view = dst_of(block).at[:, pl.ds(d * half, half)]
        return pltpu.make_async_remote_copy(
            src_ref=view, dst_ref=view, send_sem=part_send.at[d, s, j], recv_sem=part_recv.at[d, s, j],
            device_id=(rx, other, g), device_id_type=MESH_ID,
        )

    sends = []
    for d in range(2):
        for j in range(n_items):
            c = ring_copy(d, 0, j, None)
            c.start()
            sends.append(c)
    for s in range(groups - 1):
        for d in range(2):
            b = block_at(d, s)
            for j in range(n_items):
                pltpu.make_async_remote_copy(
                    src_ref=mine[j][1](b).at[:, pl.ds(d * mine[j][2], mine[j][2])],
                    dst_ref=mine[j][1](b).at[:, pl.ds(d * mine[j][2], mine[j][2])],
                    send_sem=ring_send.at[d, s, j], recv_sem=ring_recv.at[d, s, j],
                    device_id=(rx, core, nbr[d]), device_id_type=MESH_ID,
                ).wait_recv()
                if s + 1 < groups - 1:
                    c = ring_copy(d, s + 1, j, b)
                    c.start()
                    sends.append(c)
                c = part_copy(d, s, j, mine, b)
                c.start()
                sends.append(c)
    for s in range(groups - 1):
        for d in range(2):
            b = block_at(d, s)
            for j in range(n_items):
                part_copy(d, s, j, theirs, b).wait_recv()
    for c in sends:
        c.wait_send()
    for c in locals_:
        c.wait()


def ring_all_gather(up_b, down_b, dense_b, groups, collective_id):
    n_items = 5
    gs = up_b.shape[1]
    shapes = [
        jax.ShapeDtypeStruct((E, gs * groups, F), BF16),
        jax.ShapeDtypeStruct((E, down_b.shape[1] * groups, D), BF16),
        jax.ShapeDtypeStruct((gs * groups, dense_b.shape[1]), BF16),
    ]
    nbytes = sum(int(np.prod(s.shape)) * 2 for s in shapes)
    return pl.pallas_call(
        functools.partial(ring_ag_kernel, groups),
        out_shape=shapes,
        in_specs=[pl.BlockSpec(memory_space=pl.ANY)] * 3,
        out_specs=[pl.BlockSpec(memory_space=pl.ANY)] * 3,
        scratch_shapes=[
            pltpu.SemaphoreType.DMA((2, groups - 1, n_items)),
            pltpu.SemaphoreType.DMA((2, groups - 1, n_items)),
            pltpu.SemaphoreType.DMA((2, groups - 1, n_items)),
            pltpu.SemaphoreType.DMA((2, groups - 1, n_items)),
            pltpu.SemaphoreType.DMA((2 * E + 1,)),
        ],
        compiler_params=pltpu.CompilerParams(collective_id=collective_id, has_side_effects=True),
        cost_estimate=pl.CostEstimate(flops=0, bytes_accessed=nbytes, transcendentals=0),
    )(up_b, down_b, dense_b)


def grad_items(gu, gd, gdense, owner, gs, fs, width):
    found = []
    for k in range(2):
        e = 2 * k + owner
        found.append((lambda b, e=e: gu.at[e, pl.ds(pl.multiple_of(b * gs, gs), gs)], F // 2))
        found.append((lambda b, e=e: gd.at[e, pl.ds(pl.multiple_of(b * fs, fs), fs)], D // 2))
    found.append((lambda b: gdense.at[pl.ds(pl.multiple_of(b * gs, gs), gs), pl.ds(owner * width, width)], width // 2))
    return found


def ring_rs2_kernel(groups, x_pair, *refs):
    gu, gd, gdense, out_up, out_down, out_dense = refs[:6]
    n_items = 5
    scr = refs[6:]
    rbuf, sbuf, pbuf, own, fin, xr, cr = (scr[i * n_items : (i + 1) * n_items] for i in range(7))
    ring_send, ring_recv, part_send, part_recv, load_sem, x_send, x_recv, c_send, c_recv = scr[7 * n_items :]
    pos_of, dev_at = ring_order(groups)
    rx = lax.axis_index("rx")
    core = lax.axis_index("core")
    g = lax.axis_index("group")
    other = 1 - core
    pos = pos_of(g)
    nbr = (dev_at(pos + 1), dev_at(pos + groups - 1))
    gs = gu.shape[1] // groups
    fs = gd.shape[1] // groups
    width = gdense.shape[1] // 2
    mine = grad_items(gu, gd, gdense, core, gs, fs, width)
    theirs = grad_items(gu, gd, gdense, other, gs, fs, width)

    barrier = pltpu.get_barrier_semaphore()
    for n in nbr:
        pl.semaphore_signal(barrier, inc=1, device_id=(rx, core, n), device_id_type=MESH_ID)
    pl.semaphore_signal(barrier, inc=1, device_id=(rx, other, g), device_id_type=MESH_ID)
    count = 3
    if x_pair:
        pl.semaphore_signal(barrier, inc=1, device_id=(1 - rx, core, g), device_id_type=MESH_ID)
        count = 4
    pl.semaphore_wait(barrier, count)

    def block_at(d, s):
        if d == 0:
            return dev_at(pos + 2 * groups - 1 - s)
        return dev_at(pos + 1 + s)

    def cols(j, d):
        half = mine[j][1]
        return pl.ds(d * half, half)

    def load(d, s, slot, j):
        return pltpu.make_async_copy(mine[j][0](block_at(d, s)).at[:, cols(j, d)], own[j].at[d, slot], load_sem.at[d, slot, j])

    def part(d, s, j):
        return pltpu.make_async_remote_copy(
            src_ref=theirs[j][0](block_at(d, s)).at[:, cols(j, d)], dst_ref=pbuf[j].at[d, s],
            send_sem=part_send.at[d, s, j], recv_sem=part_recv.at[d, s, j],
            device_id=(rx, other, g), device_id_type=MESH_ID,
        )

    def ring(d, s, j):
        return pltpu.make_async_remote_copy(
            src_ref=sbuf[j].at[d, s], dst_ref=rbuf[j].at[d, s],
            send_sem=ring_send.at[d, s, j], recv_sem=ring_recv.at[d, s, j],
            device_id=(rx, core, nbr[d]), device_id_type=MESH_ID,
        )

    sends = []
    for d in range(2):
        for j in range(n_items):
            load(d, 0, 0, j).start()
            c = part(d, 0, j)
            c.start()
            sends.append(c)
    for s in range(groups):
        slot = s % 2
        for d in range(2):
            for j in range(n_items):
                load(d, s, slot, j).wait()
                if s + 1 < groups:
                    load(d, s + 1, 1 - slot, j).start()
                    c = part(d, s + 1, j)
                    c.start()
                    sends.append(c)
                part(d, s, j).wait_recv()
                val = own[j][d, slot].astype(F32) + pbuf[j][d, s].astype(F32)
                if s > 0:
                    ring(d, s - 1, j).wait_recv()
                    val = val + rbuf[j][d, s - 1].astype(F32)
                if s < groups - 1:
                    sbuf[j][d, s] = val.astype(BF16)
                    c = ring(d, s, j)
                    c.start()
                    sends.append(c)
                else:
                    fin[j][d] = val

    for c in sends:
        c.wait_send()
    sends = []
    if x_pair:
        x_copies = []
        for d in range(2):
            for j in range(n_items):
                sbuf[j][d, 0] = fin[j][d].astype(BF16)
                c = pltpu.make_async_remote_copy(
                    src_ref=sbuf[j].at[d, 0], dst_ref=xr[j].at[d], send_sem=x_send.at[d, j], recv_sem=x_recv.at[d, j],
                    device_id=(1 - rx, core, g), device_id_type=MESH_ID,
                )
                c.start()
                x_copies.append(c)
        for c in x_copies:
            c.wait_recv()
        for d in range(2):
            for j in range(n_items):
                fin[j][d] = sbuf[j][d, 0].astype(F32) + xr[j][d].astype(F32)
        sends += x_copies

    c_copies = []
    for d in range(2):
        for j in range(n_items):
            c = pltpu.make_async_remote_copy(
                src_ref=fin[j].at[d], dst_ref=cr[j].at[d], send_sem=c_send.at[d, j], recv_sem=c_recv.at[d, j],
                device_id=(rx, other, g), device_id_type=MESH_ID,
            )
            c.start()
            c_copies.append(c)

    def out_items(owner):
        found = []
        for k in range(2):
            e = 2 * k + owner
            found.append(lambda d, e=e: out_up.at[e, :, pl.ds(d * (F // 2), F // 2)])
            found.append(lambda d, e=e: out_down.at[e, :, pl.ds(d * (D // 2), D // 2)])
        found.append(lambda d: out_dense.at[:, pl.ds(owner * width + d * (width // 2), width // 2)])
        return found

    mine_out = out_items(core)
    theirs_out = out_items(other)
    for d in range(2):
        for j in range(n_items):
            mine_out[j](d)[...] = fin[j][d]
    for c in c_copies:
        c.wait_recv()
    for d in range(2):
        for j in range(n_items):
            theirs_out[j](d)[...] = cr[j][d]
    for c in sends + c_copies:
        c.wait_send()


def grad_reduce(gu, gd, gdense, groups, x_pair, collective_id):
    gs = gu.shape[1] // groups
    fs = gd.shape[1] // groups
    width = gdense.shape[1] // 2
    item_shapes = [(gs, F // 2), (fs, D // 2), (gs, F // 2), (fs, D // 2), (gs, width // 2)]
    scratch = []
    for lead, dtype in (((2, groups - 1), BF16), ((2, groups - 1), BF16), ((2, groups), BF16), ((2, 2), BF16), ((2,), F32), ((2,), BF16), ((2,), F32)):
        scratch += [pltpu.VMEM(lead + shp, dtype) for shp in item_shapes]
    scratch += [
        pltpu.SemaphoreType.DMA((2, groups - 1, 5)),
        pltpu.SemaphoreType.DMA((2, groups - 1, 5)),
        pltpu.SemaphoreType.DMA((2, groups, 5)),
        pltpu.SemaphoreType.DMA((2, groups, 5)),
        pltpu.SemaphoreType.DMA((2, 2, 5)),
        pltpu.SemaphoreType.DMA((2, 5)),
        pltpu.SemaphoreType.DMA((2, 5)),
        pltpu.SemaphoreType.DMA((2, 5)),
        pltpu.SemaphoreType.DMA((2, 5)),
    ]
    outs = [
        jax.ShapeDtypeStruct((E, gs, F), F32),
        jax.ShapeDtypeStruct((E, fs, D), F32),
        jax.ShapeDtypeStruct((gs, gdense.shape[1]), F32),
    ]
    nbytes = 2 * (gu.size + gd.size + gdense.size)
    return pl.pallas_call(
        functools.partial(ring_rs2_kernel, groups, x_pair),
        out_shape=outs,
        in_specs=[pl.BlockSpec(memory_space=pl.ANY)] * 3,
        out_specs=[pl.BlockSpec(memory_space=pltpu.VMEM)] * 3,
        scratch_shapes=scratch,
        compiler_params=pltpu.CompilerParams(
            collective_id=collective_id, has_side_effects=True, vmem_limit_bytes=62 * 1024 * 1024
        ),
        cost_estimate=pl.CostEstimate(flops=gu.size + gd.size + gdense.size, bytes_accessed=nbytes, transcendentals=0),
    )(gu, gd, gdense)


TILE = 256
TILE_B = 256
CAPP = 512
SQRT_HALF = float(np.sqrt(0.5))
INV_SQRT_2PI = float(1.0 / np.sqrt(2.0 * np.pi))


def ffn_fwd_kernel(micro, counts, x_ref, w1_ref, b1_ref, w2_ref, b2_ref, hp_ref, h_ref, y_ref):
    e, m, t = pl.program_id(0), pl.program_id(1), pl.program_id(2)
    active = t * TILE < counts[e * micro + m]

    @pl.when(active)
    def _():
        hp = jnp.dot(x_ref[0], w1_ref[0], preferred_element_type=F32) + b1_ref[0]
        h = (0.5 * hp * (1.0 + lax.erf(hp * SQRT_HALF))).astype(BF16)
        hp_ref[0] = hp
        h_ref[0] = h
        y = jnp.dot(h, w2_ref[0], preferred_element_type=F32) + b2_ref[0]
        hi = y.astype(BF16)
        y_ref[0, :, :D] = hi
        y_ref[0, :, D:] = (y - hi.astype(F32)).astype(BF16)

    @pl.when(jnp.logical_not(active))
    def _():
        y_ref[0] = jnp.zeros(y_ref.shape[1:], BF16)


def ffn_forward(counts, table_in, w1, b1, w2, b2, micro):
    tiles = CAPP // TILE
    rows = table_in.shape[1]
    row_map = lambda e, m, t, c: (m, e * tiles + t, 0)
    w_map = lambda e, m, t, c: (e, 0, 0)
    grid_spec = pltpu.PrefetchScalarGridSpec(
        num_scalar_prefetch=1,
        grid=(E, micro, tiles),
        in_specs=[
            pl.BlockSpec((1, TILE, D), row_map),
            pl.BlockSpec((1, D, F), w_map),
            pl.BlockSpec((1, 1, F), w_map),
            pl.BlockSpec((1, F, D), w_map),
            pl.BlockSpec((1, 1, D), w_map),
        ],
        out_specs=[
            pl.BlockSpec((1, TILE, F), row_map),
            pl.BlockSpec((1, TILE, F), row_map),
            pl.BlockSpec((1, TILE, 2 * D), row_map),
        ],
    )
    work = micro * rows
    return pl.pallas_call(
        functools.partial(ffn_fwd_kernel, micro),
        grid_spec=grid_spec,
        out_shape=[
            jax.ShapeDtypeStruct((micro, rows, F), F32),
            jax.ShapeDtypeStruct((micro, rows, F), BF16),
            jax.ShapeDtypeStruct((micro, rows, 2 * D), BF16),
        ],
        compiler_params=pltpu.CompilerParams(vmem_limit_bytes=48 * 1024 * 1024),
        cost_estimate=pl.CostEstimate(
            flops=4 * work * D * F // 2, bytes_accessed=work * (2 * D + 6 * F + 4 * D) // 2, transcendentals=work * F // 2
        ),
    )(counts, table_in, w1, b1, w2, b2)


def ffn_bwd_kernel(micro, counts, dy_ref, x_ref, hp_ref, h_ref, w1_ref, w2_ref, dt_ref, gu_ref, gd_ref, gb_ref, gb2_ref, gu_acc, gd_acc):
    e, m, t = pl.program_id(0), pl.program_id(1), pl.program_id(2)
    active = t * TILE_B < counts[e * micro + m]

    @pl.when((m == 0) & (t == 0))
    def _():
        gu_acc[...] = jnp.zeros(gu_acc.shape, F32)
        gd_acc[...] = jnp.zeros(gd_acc.shape, F32)
        gb_ref[...] = jnp.zeros(gb_ref.shape, F32)
        gb2_ref[...] = jnp.zeros(gb2_ref.shape, F32)

    @pl.when(active)
    def _():
        dy = dy_ref[0]
        hp = hp_ref[0]
        d_hidden = lax.dot_general(dy, w2_ref[0], (((1,), (1,)), ((), ())), preferred_element_type=F32)
        slope = 0.5 * (1.0 + lax.erf(hp * SQRT_HALF)) + hp * jnp.exp(-0.5 * hp * hp) * INV_SQRT_2PI
        d_pre = (d_hidden * slope).astype(BF16)
        dt = lax.dot_general(d_pre, w1_ref[0], (((1,), (1,)), ((), ())), preferred_element_type=F32)
        hi = dt.astype(BF16)
        dt_ref[0, :, :D] = hi
        dt_ref[0, :, D:] = (dt - hi.astype(F32)).astype(BF16)
        gb2_ref[0] += jnp.sum(dy.astype(F32), 0, keepdims=True)
        gu_acc[...] += lax.dot_general(x_ref[0], d_pre, (((0,), (0,)), ((), ())), preferred_element_type=F32)
        gd_acc[...] += lax.dot_general(h_ref[0], dy, (((0,), (0,)), ((), ())), preferred_element_type=F32)
        gb_ref[0] += jnp.sum(d_pre.astype(F32), 0, keepdims=True)

    @pl.when(jnp.logical_not(active))
    def _():
        dt_ref[0] = jnp.zeros(dt_ref.shape[1:], BF16)

    @pl.when((m == micro - 1) & (t == pl.num_programs(2) - 1))
    def _():
        gu_ref[0] = gu_acc[...].astype(BF16)
        gd_ref[0] = gd_acc[...].astype(BF16)


def ffn_backward(counts, d_expert, table_in, hp, h, w1, w2, micro):
    tiles = CAPP // TILE_B
    rows = table_in.shape[1]
    row_map = lambda e, m, t, c: (m, e * tiles + t, 0)
    w_map = lambda e, m, t, c: (e, 0, 0)
    grid_spec = pltpu.PrefetchScalarGridSpec(
        num_scalar_prefetch=1,
        grid=(E, micro, tiles),
        in_specs=[
            pl.BlockSpec((1, TILE_B, D), row_map),
            pl.BlockSpec((1, TILE_B, D), row_map),
            pl.BlockSpec((1, TILE_B, F), row_map),
            pl.BlockSpec((1, TILE_B, F), row_map),
            pl.BlockSpec((1, D, F), w_map),
            pl.BlockSpec((1, F, D), w_map),
        ],
        out_specs=[
            pl.BlockSpec((1, TILE_B, 2 * D), row_map),
            pl.BlockSpec((1, D, F), w_map),
            pl.BlockSpec((1, F, D), w_map),
            pl.BlockSpec((1, 1, F), w_map),
            pl.BlockSpec((1, 1, D), w_map),
        ],
        scratch_shapes=[pltpu.VMEM((D, F), F32), pltpu.VMEM((F, D), F32)],
    )
    work = micro * rows
    return pl.pallas_call(
        functools.partial(ffn_bwd_kernel, micro),
        grid_spec=grid_spec,
        out_shape=[
            jax.ShapeDtypeStruct((micro, rows, 2 * D), BF16),
            jax.ShapeDtypeStruct((E, D, F), BF16),
            jax.ShapeDtypeStruct((E, F, D), BF16),
            jax.ShapeDtypeStruct((E, 1, F), F32),
            jax.ShapeDtypeStruct((E, 1, D), F32),
        ],
        compiler_params=pltpu.CompilerParams(vmem_limit_bytes=60 * 1024 * 1024),
        cost_estimate=pl.CostEstimate(
            flops=8 * work * D * F // 2, bytes_accessed=work * (8 * D + 6 * F) // 2 + 16 * E * D * F, transcendentals=2 * work * F // 2
        ),
    )(counts, d_expert, table_in, hp, h, w1, w2)

def layer_norm(value, gain, shift):
    center = value - jnp.mean(value, -1, keepdims=True)
    spread = jnp.mean(center * center, -1, keepdims=True)
    return center * lax.rsqrt(spread + 1e-06) * gain + shift


def gelu_exact(value):
    return jax.nn.gelu(value, approximate=False)


def split_heads(part):
    return part.reshape(-1, S, HEADS, HEAD_DIM)


def dot(a, b):
    return jnp.dot(a, b, preferred_element_type=F32)


def assign_places(route):
    chosen = jnp.concatenate([route[:, :, 0], route[:, :, 1]], 1)
    hits = (chosen[:, :, None] == jnp.arange(E, dtype=jnp.int32)).astype(jnp.int32)
    before = jnp.cumsum(hits, 1) - hits
    slot = jnp.sum(before * hits, 2)
    return chosen * CAPP + slot, jnp.sum(hits, 1)


def hi_lo(v):
    hi = v.astype(BF16)
    lo = (v - hi.astype(F32)).astype(BF16)
    return jnp.concatenate([hi, lo], -1)


def pick_rows(onehot, split):
    both = jnp.einsum("mnr,mrd->mnd", onehot, split, preferred_element_type=F32)
    return both[..., :D] + both[..., D:]


def pack_dense(qkv_w, out_w, router_w, vectors, up_bias):
    rows = qkv_w.shape[0]
    ub = up_bias.reshape(E, rows, 4).transpose(1, 0, 2).reshape(rows, E * 4)
    return jnp.concatenate([qkv_w, out_w, router_w, vectors.T, ub], 1)


def unpack_dense(packed):
    rows = packed.shape[0]
    w_qkv = packed[:, : 3 * D]
    w_out = packed[:, 3 * D : 4 * D]
    w_router = packed[:, 4 * D : 4 * D + E]
    table = packed[:, 4 * D + E : 4 * D + E + NV].T
    ub = packed[:, 4 * D + E + NV :].reshape(rows, E, 4).transpose(1, 0, 2).reshape(E, rows * 4)
    return w_qkv, w_out, w_router, table, ub


def attention_fwd(w_qkv, w_out, table, value):
    rows = value.shape[0]
    scale = HEAD_DIM ** (-0.5)
    first = layer_norm(value, table[0], table[1]).astype(BF16)
    qkv_bias = jnp.concatenate([table[2], jnp.zeros((D,), F32), table[3]])
    qkv = (dot(first, w_qkv) + qkv_bias).astype(BF16)
    query, key_part, val_part = (
        split_heads(qkv[:, :D]),
        split_heads(qkv[:, D : 2 * D]),
        split_heads(qkv[:, 2 * D :]),
    )
    scores = jnp.einsum("bqhd,bkhd->bhqk", query, key_part, preferred_element_type=F32) * scale
    peak = jnp.max(scores, -1, keepdims=True)
    expo = jnp.exp(scores - peak)
    total = jnp.sum(expo, -1, keepdims=True)
    probs_att = (expo / total).astype(BF16)
    log_total = peak + jnp.log(total)
    attended = jnp.einsum("bhqk,bkhd->bqhd", probs_att, val_part, preferred_element_type=F32)
    attended = attended.reshape(rows, D).astype(BF16)
    resid = value + (dot(attended, w_out) + table[4])
    return first, qkv, log_total, attended, resid


def attention_bwd(w_qkv, w_out, table, value, first, qkv, log_total, attended, d_resid):
    rows = value.shape[0]
    scale = HEAD_DIM ** (-0.5)
    d_branch = d_resid.astype(BF16)
    g_bias_out = jnp.sum(d_branch.astype(F32), 0)
    g_out = lax.dot_general(attended, d_branch, (((0,), (0,)), ((), ())), preferred_element_type=F32)
    d_att = split_heads(
        lax.dot_general(d_branch, w_out, (((1,), (1,)), ((), ())), preferred_element_type=F32).astype(BF16)
    )
    query, key_part, val_part = (
        split_heads(qkv[:, :D]),
        split_heads(qkv[:, D : 2 * D]),
        split_heads(qkv[:, 2 * D :]),
    )
    scores = jnp.einsum("bqhd,bkhd->bhqk", query, key_part, preferred_element_type=F32) * scale
    probs_f = jnp.exp(scores - log_total)
    probs_att = probs_f.astype(BF16)
    d_val = jnp.einsum("bhqk,bqhd->bkhd", probs_att, d_att, preferred_element_type=F32)
    d_prob = jnp.einsum("bqhd,bkhd->bhqk", d_att, val_part, preferred_element_type=F32)
    d_score = (probs_f * (d_prob - jnp.sum(d_prob * probs_f, -1, keepdims=True))).astype(BF16)
    d_query = jnp.einsum("bhqk,bkhd->bqhd", d_score, key_part, preferred_element_type=F32) * scale
    d_key = jnp.einsum("bhqk,bqhd->bkhd", d_score, query, preferred_element_type=F32) * scale
    d_qkv = jnp.concatenate(
        [d_query.reshape(rows, D), d_key.reshape(rows, D), d_val.reshape(rows, D)], 1
    ).astype(BF16)
    d_qkv_f = d_qkv.astype(F32)
    g_bias_q = jnp.sum(d_qkv_f[:, :D], 0)
    g_bias_v = jnp.sum(d_qkv_f[:, 2 * D :], 0)
    g_qkv = lax.dot_general(first, d_qkv, (((0,), (0,)), ((), ())), preferred_element_type=F32)
    d_first = lax.dot_general(d_qkv, w_qkv, (((1,), (1,)), ((), ())), preferred_element_type=F32)
    first_pull = jax.vjp(layer_norm, value, table[0], table[1])[1]
    d_input, g_gain_one, g_shift_one = first_pull(d_first)
    return (g_qkv, g_out, g_bias_out, g_bias_q, g_bias_v, g_gain_one, g_shift_one), d_input


def adamw(weight, moments, grad, rate):
    first = 0.5 * moments[0] + 0.5 * grad
    root = jnp.sqrt(0.5 * moments[1] * moments[1] + 0.5 * grad * grad)
    update = first / (root + 1e-08)
    which = lax.broadcasted_iota(jnp.int32, moments.shape, 0) == 0
    both = jnp.where(which, 0.5 * moments + 0.5 * grad, jnp.sqrt(0.5 * moments * moments + 0.5 * grad * grad))
    return (weight - rate * (update + 0.1 * weight), both)


def shards(
    tokens,
    cotangent,
    expert_index,
    qkv_weight,
    out_weight,
    router_weight,
    up_weight,
    up_bias,
    down_weight,
    vectors,
    qkv_moments,
    out_moments,
    router_moments,
    up_moments,
    up_bias_moments,
    down_moments,
    vector_moments,
):
    rows = tokens.shape[0]
    micro = rows // MB_TOK
    gs = qkv_weight.shape[0]
    group_size = D // gs
    core = lax.axis_index("core")

    dense_in = pack_dense(qkv_weight, out_weight, router_weight, vectors, up_bias)
    width = dense_in.shape[1]
    dense_in = jnp.pad(dense_in, ((0, 0), (0, DENSE_AG - width))).astype(BF16)
    w_up_all, w_down_all, dense = ring_all_gather(
        up_weight.astype(BF16), down_weight.astype(BF16), dense_in, group_size, 1
    )
    w_qkv, w_out, w_router, table_b, b_up_b = unpack_dense(dense[:, :width])
    table = table_b.astype(F32)
    b_up = b_up_b.astype(F32)

    value = tokens.astype(F32)
    d_out = cotangent.astype(F32)
    first, qkv, log_total, attended, resid = attention_fwd(w_qkv, w_out, table, value)
    second = layer_norm(resid, table[5], table[6]).astype(BF16)
    logits = dot(second, w_router)
    probs = jax.nn.softmax(logits, -1)
    picked = expert_index[:, :, None] == jnp.arange(E, dtype=jnp.int32)
    gate = jnp.sum(jnp.where(picked, probs[:, None, :], 0.0), -1)

    route = expert_index.reshape(micro, MB_TOK, 2)
    places, counts = assign_places(route)
    counts = counts.T.reshape(E * micro)
    onehot = (places[:, :, None] == jnp.arange(E * CAPP, dtype=jnp.int32)).astype(BF16)
    second_m = second.reshape(micro, MB_TOK, D)
    pair = jnp.concatenate([second_m, second_m], 1)
    table_in = jnp.einsum("mnr,mnd->mrd", onehot, pair, preferred_element_type=F32).astype(BF16)

    hidden_pre, hidden, y_all = ffn_forward(
        counts, table_in, w_up_all, b_up[:, None, :], w_down_all, table[7 : 7 + E][:, None, :], micro
    )
    picked_rows = pick_rows(onehot, y_all)
    out_zero = picked_rows[:, :MB_TOK].reshape(rows, D)
    out_one = picked_rows[:, MB_TOK:].reshape(rows, D)
    result = resid + (gate[:, 0:1] * out_zero + gate[:, 1:2] * out_one)

    d_gate = jnp.stack([jnp.sum(d_out * out_zero, -1), jnp.sum(d_out * out_one, -1)], 1)
    d_out_m = d_out.reshape(micro, MB_TOK, D)
    gate_m = gate.reshape(micro, MB_TOK, 2)
    weighted = jnp.concatenate([gate_m[:, :, 0:1] * d_out_m, gate_m[:, :, 1:2] * d_out_m], 1).astype(BF16)
    d_expert = jnp.einsum("mnr,mnd->mrd", onehot, weighted, preferred_element_type=F32).astype(BF16)

    d_table, g_up, g_down, g_b1, g_b2 = ffn_backward(counts, d_expert, table_in, hidden_pre, hidden, w_up_all, w_down_all, micro)
    g_up_bias_all = g_b1[:, 0, :]
    g_bias_down = g_b2[:, 0, :]

    onehot_sum = onehot[:, :MB_TOK] + onehot[:, MB_TOK:]
    d_picked = pick_rows(onehot_sum, d_table).reshape(rows, D)

    d_probs = jnp.sum(jnp.where(picked, d_gate[:, :, None], 0.0), 1)
    d_logit = (probs * (d_probs - jnp.sum(d_probs * probs, -1, keepdims=True))).astype(BF16)
    g_router = lax.dot_general(second, d_logit, (((0,), (0,)), ((), ())), preferred_element_type=F32)
    d_second = d_picked + lax.dot_general(d_logit, w_router, (((1,), (1,)), ((), ())), preferred_element_type=F32)
    norm_pull = jax.vjp(layer_norm, resid, table[5], table[6])[1]
    d_resid, g_gain_two, g_shift_two = norm_pull(d_second)
    d_resid = d_out + d_resid

    att_grads, d_input = attention_bwd(w_qkv, w_out, table, value, first, qkv, log_total, attended, d_resid)
    g_qkv, g_out, g_bias_out, g_bias_q, g_bias_v, g_gain_one, g_shift_one = att_grads
    input_grad = d_resid + d_input

    g_table = jnp.concatenate(
        [
            jnp.stack([g_gain_one, g_shift_one, g_bias_q, g_bias_v, g_bias_out, g_gain_two, g_shift_two]),
            g_bias_down,
        ],
        0,
    )
    dense_g = pack_dense(g_qkv, g_out, g_router, g_table, g_up_bias_all)
    width = dense_g.shape[1]
    dense_g = jnp.pad(dense_g, ((0, 0), (0, DENSE_AG - width))).astype(BF16)
    x_pair = lax.axis_size("rx") == 2
    r_up, r_down, r_dense = grad_reduce(g_up, g_down, dense_g, group_size, x_pair, 0)
    if not x_pair:
        r_up, r_down, r_dense = lax.psum((r_up, r_down, r_dense), "rx")
    r_qkv, r_out, r_router, r_table, r_ub = unpack_dense(r_dense[:, :width])

    reduced = (r_qkv, r_out, r_router, r_up, r_ub, r_down, r_table)
    rates = (
        2.0 * D ** (-0.5),
        2.0 * (D // 32) ** (-0.5),
        2.0 * (2 * D) ** (-0.5),
        2.0 * D ** (-0.5),
        0.2,
        2.0 * (F // 16) ** (-0.5),
        0.2,
    )
    params = (qkv_weight, out_weight, router_weight, up_weight, up_bias, down_weight, vectors)
    moments = (qkv_moments, out_moments, router_moments, up_moments, up_bias_moments, down_moments, vector_moments)
    news = []
    states = []
    for weight, state, grad, rate in zip(params, moments, reduced, rates):
        new_weight, new_state = adamw(weight, state, grad, rate)
        news.append(new_weight)
        states.append(new_state)
    return (result.astype(BF16), input_grad) + reduced + tuple(news) + tuple(states)


def solution(mesh):
    replica, group = mesh.shape["replica"], mesh.shape["group"]
    view = Mesh(np.asarray(mesh.devices).reshape(replica // 2, 2, group), ("rx", "core", "group"))
    in_specs = (
        P(TOK, None),
        P(TOK, None),
        P(TOK, None),
        P("group", None),
        P("group", None),
        P("group", None),
        P(None, "group", None),
        P(None, "group"),
        P(None, "group", None),
        P(None, "group"),
        P(None, "group", None),
        P(None, "group", None),
        P(None, "group", None),
        P(None, None, "group", None),
        P(None, None, "group"),
        P(None, None, "group", None),
        P(None, None, "group"),
    )
    out_specs = (
        P(TOK, None),
        P(TOK, None),
        P("group", None),
        P("group", None),
        P("group", None),
        P(None, "group", None),
        P(None, "group"),
        P(None, "group", None),
        P(None, "group"),
        P("group", None),
        P("group", None),
        P("group", None),
        P(None, "group", None),
        P(None, "group"),
        P(None, "group", None),
        P(None, "group"),
        P(None, "group", None),
        P(None, "group", None),
        P(None, "group", None),
        P(None, None, "group", None),
        P(None, None, "group"),
        P(None, None, "group", None),
        P(None, None, "group"),
    )
    return jax.shard_map(shards, mesh=view, in_specs=in_specs, out_specs=out_specs, check_vma=False)
```

```python
import functools

import jax
import jax.numpy as jnp
import numpy as np
from jax import lax
from jax.sharding import Mesh
from jax.sharding import PartitionSpec as P
from jax.experimental import pallas as pl
from jax.experimental.pallas import tpu as pltpu

D = 512
HEADS = 8
HEAD_DIM = 64
F = 2048
E = 4
S = 197
MB_TOK = 394
CAP = 392
NV = 11
DENSE_AG = 2560
DENSE_PAD = 2304
F32 = jnp.float32
BF16 = jnp.bfloat16
TOK = ("rx", "core", "group")


MESH_ID = pl.DeviceIdType.MESH


def ring_order(groups):
    if groups in (4, 8):
        zs = groups // 2

        def pos_of(g):
            y = g % 2
            z = g // 2
            return z + y * (2 * zs - 1 - 2 * z)

        def dev_at(p):
            p = p % groups
            yy = p // zs
            return 2 * (p + yy * (2 * zs - 1 - 2 * p)) + yy

        return pos_of, dev_at
    return (lambda g: g), (lambda p: p % groups)


def ring_rs_kernel(groups, n_in, *refs):
    ins = refs[:n_in]
    outs = refs[n_in : 2 * n_in]
    rbufs = refs[2 * n_in : 3 * n_in]
    sbufs = refs[3 * n_in : 4 * n_in]
    owns = refs[4 * n_in : 5 * n_in]
    send_sem, recv_sem, load_sem = refs[5 * n_in :]
    pos_of, dev_at = ring_order(groups)
    rx = lax.axis_index("rx")
    core = lax.axis_index("core")
    g = lax.axis_index("group")
    pos = pos_of(g)
    nbr = (dev_at(pos + 1), dev_at(pos + groups - 1))

    barrier = pltpu.get_barrier_semaphore()
    for n in nbr:
        pl.semaphore_signal(barrier, inc=1, device_id=(rx, core, n), device_id_type=MESH_ID)
    pl.semaphore_wait(barrier, 2)

    def block_dev(d, s):
        if d == 0:
            return dev_at(pos + 2 * groups - s - 1)
        return dev_at(pos + s + 1)

    def load(d, s, slot):
        b = block_dev(d, s)
        copies = []
        for i in range(n_in):
            rows = ins[i].shape[1] // groups
            half = ins[i].shape[2] // 2
            src = ins[i].at[:, pl.ds(pl.multiple_of(b * rows, rows), rows), pl.ds(d * half, half)]
            copies.append(pltpu.make_async_copy(src, owns[i].at[d, slot], load_sem.at[d, slot, i]))
        return copies

    def remote(d, s, i):
        return pltpu.make_async_remote_copy(
            src_ref=sbufs[i].at[d, s],
            dst_ref=rbufs[i].at[d, s],
            send_sem=send_sem.at[d, s, i],
            recv_sem=recv_sem.at[d, s, i],
            device_id=(rx, core, nbr[d]),
            device_id_type=MESH_ID,
        )

    for d in range(2):
        for c in load(d, 0, 0):
            c.start()
    sends = []
    for s in range(groups):
        slot = s % 2
        for d in range(2):
            for c in load(d, s, slot):
                c.wait()
            if s + 1 < groups:
                for c in load(d, s + 1, 1 - slot):
                    c.start()
            for i in range(n_in):
                if s > 0:
                    remote(d, s - 1, i).wait_recv()
                for a in range(ins[i].shape[0]):
                    mine = owns[i][d, slot, a].astype(F32)
                    if s > 0:
                        mine = mine + rbufs[i][d, s - 1, a].astype(F32)
                    if s < groups - 1:
                        sbufs[i][d, s, a] = mine.astype(sbufs[i].dtype)
                    else:
                        half = ins[i].shape[2] // 2
                        outs[i][a, :, pl.ds(d * half, half)] = mine.astype(outs[i].dtype)
                if s < groups - 1:
                    c = remote(d, s, i)
                    c.start()
                    sends.append(c)
    for c in sends:
        c.wait_send()


def ring_reduce_scatter(xs, groups, collective_id):
    n_in = len(xs)
    outs, rb, own = [], [], []
    flops = 0
    nbytes = 0
    for x in xs:
        a, total, c = x.shape
        rows = total // groups
        outs.append(jax.ShapeDtypeStruct((a, rows, c), x.dtype))
        rb.append(pltpu.VMEM((2, groups - 1, a, rows, c // 2), x.dtype))
        own.append(pltpu.VMEM((2, 2, a, rows, c // 2), x.dtype))
        flops += a * total * c
        nbytes += 3 * x.size * x.dtype.itemsize
    scratch = rb + rb + own + [
        pltpu.SemaphoreType.DMA((2, groups - 1, n_in)),
        pltpu.SemaphoreType.DMA((2, groups - 1, n_in)),
        pltpu.SemaphoreType.DMA((2, 2, n_in)),
    ]
    return pl.pallas_call(
        functools.partial(ring_rs_kernel, groups, n_in),
        out_shape=outs,
        in_specs=[pl.BlockSpec(memory_space=pl.ANY)] * n_in,
        out_specs=[pl.BlockSpec(memory_space=pltpu.VMEM)] * n_in,
        scratch_shapes=scratch,
        compiler_params=pltpu.CompilerParams(
            collective_id=collective_id, has_side_effects=True, vmem_limit_bytes=60 * 1024 * 1024
        ),
        cost_estimate=pl.CostEstimate(flops=flops, bytes_accessed=nbytes, transcendentals=0),
    )(*xs)


def ring_ag_kernel(groups, *refs):
    in_up, in_down, in_dense, out_up, out_down, out_dense = refs[:6]
    ring_send, ring_recv, part_send, part_recv, local_sem = refs[6:]
    pos_of, dev_at = ring_order(groups)
    rx = lax.axis_index("rx")
    core = lax.axis_index("core")
    g = lax.axis_index("group")
    other = 1 - core
    pos = pos_of(g)
    nbr = (dev_at(pos + 1), dev_at(pos + groups - 1))
    gs = in_up.shape[1]
    fs = in_down.shape[1]
    width = in_dense.shape[1] // 2

    barrier = pltpu.get_barrier_semaphore()
    for n in nbr:
        pl.semaphore_signal(barrier, inc=1, device_id=(rx, core, n), device_id_type=MESH_ID)
    pl.semaphore_signal(barrier, inc=1, device_id=(rx, other, g), device_id_type=MESH_ID)
    pl.semaphore_wait(barrier, 3)

    def items(owner):
        found = []
        for k in range(2):
            e = 2 * k + owner
            found.append((in_up.at[e], lambda b, e=e: out_up.at[e, pl.ds(pl.multiple_of(b * gs, gs), gs)], F // 2))
            found.append((in_down.at[e], lambda b, e=e: out_down.at[e, pl.ds(pl.multiple_of(b * fs, fs), fs)], D // 2))
        dense_in = in_dense.at[:, pl.ds(owner * width, width)]
        found.append(
            (dense_in, lambda b: out_dense.at[pl.ds(pl.multiple_of(b * gs, gs), gs), pl.ds(owner * width, width)], width // 2)
        )
        return found

    mine = items(core)
    theirs = items(other)
    n_items = len(mine)

    locals_ = [pltpu.make_async_copy(in_up.at[e], out_up.at[e, pl.ds(pl.multiple_of(g * gs, gs), gs)], local_sem.at[e]) for e in range(E)]
    locals_ += [
        pltpu.make_async_copy(in_down.at[e], out_down.at[e, pl.ds(pl.multiple_of(g * fs, fs), fs)], local_sem.at[E + e])
        for e in range(E)
    ]
    locals_.append(pltpu.make_async_copy(in_dense, out_dense.at[pl.ds(pl.multiple_of(g * gs, gs), gs)], local_sem.at[2 * E]))
    for c in locals_:
        c.start()

    def block_at(d, s):
        if d == 0:
            return dev_at(pos + 2 * groups - 1 - s)
        return dev_at(pos + 1 + s)

    def ring_copy(d, s, j, src_block):
        src_in, dst_of, half = mine[j]
        cols = pl.ds(d * half, half)
        if src_block is None:
            src = src_in.at[:, cols]
            dst = dst_of(g).at[:, cols]
        else:
            src = dst_of(src_block).at[:, cols]
            dst = src
        return pltpu.make_async_remote_copy(
            src_ref=src, dst_ref=dst, send_sem=ring_send.at[d, s, j], recv_sem=ring_recv.at[d, s, j],
            device_id=(rx, core, nbr[d]), device_id_type=MESH_ID,
        )

    def part_copy(d, s, j, table, block):
        _, dst_of, half = table[j]
        view = dst_of(block).at[:, pl.ds(d * half, half)]
        return pltpu.make_async_remote_copy(
            src_ref=view, dst_ref=view, send_sem=part_send.at[d, s, j], recv_sem=part_recv.at[d, s, j],
            device_id=(rx, other, g), device_id_type=MESH_ID,
        )

    sends = []
    for d in range(2):
        for j in range(n_items):
            c = ring_copy(d, 0, j, None)
            c.start()
            sends.append(c)
    for s in range(groups - 1):
        for d in range(2):
            b = block_at(d, s)
            for j in range(n_items):
                pltpu.make_async_remote_copy(
                    src_ref=mine[j][1](b).at[:, pl.ds(d * mine[j][2], mine[j][2])],
                    dst_ref=mine[j][1](b).at[:, pl.ds(d * mine[j][2], mine[j][2])],
                    send_sem=ring_send.at[d, s, j], recv_sem=ring_recv.at[d, s, j],
                    device_id=(rx, core, nbr[d]), device_id_type=MESH_ID,
                ).wait_recv()
                if s + 1 < groups - 1:
                    c = ring_copy(d, s + 1, j, b)
                    c.start()
                    sends.append(c)
                c = part_copy(d, s, j, mine, b)
                c.start()
                sends.append(c)
    for s in range(groups - 1):
        for d in range(2):
            b = block_at(d, s)
            for j in range(n_items):
                part_copy(d, s, j, theirs, b).wait_recv()
    for c in sends:
        c.wait_send()
    for c in locals_:
        c.wait()


def ring_all_gather(up_b, down_b, dense_b, groups, collective_id):
    n_items = 5
    gs = up_b.shape[1]
    shapes = [
        jax.ShapeDtypeStruct((E, gs * groups, F), BF16),
        jax.ShapeDtypeStruct((E, down_b.shape[1] * groups, D), BF16),
        jax.ShapeDtypeStruct((gs * groups, dense_b.shape[1]), BF16),
    ]
    nbytes = sum(int(np.prod(s.shape)) * 2 for s in shapes)
    return pl.pallas_call(
        functools.partial(ring_ag_kernel, groups),
        out_shape=shapes,
        in_specs=[pl.BlockSpec(memory_space=pl.ANY)] * 3,
        out_specs=[pl.BlockSpec(memory_space=pl.ANY)] * 3,
        scratch_shapes=[
            pltpu.SemaphoreType.DMA((2, groups - 1, n_items)),
            pltpu.SemaphoreType.DMA((2, groups - 1, n_items)),
            pltpu.SemaphoreType.DMA((2, groups - 1, n_items)),
            pltpu.SemaphoreType.DMA((2, groups - 1, n_items)),
            pltpu.SemaphoreType.DMA((2 * E + 1,)),
        ],
        compiler_params=pltpu.CompilerParams(collective_id=collective_id, has_side_effects=True),
        cost_estimate=pl.CostEstimate(flops=0, bytes_accessed=nbytes, transcendentals=0),
    )(up_b, down_b, dense_b)


def grad_items(gu, gd, gdense, owner, gs, fs, width):
    found = []
    for k in range(2):
        e = 2 * k + owner
        found.append((lambda b, e=e: gu.at[e, pl.ds(pl.multiple_of(b * gs, gs), gs)], F // 2))
        found.append((lambda b, e=e: gd.at[e, pl.ds(pl.multiple_of(b * fs, fs), fs)], D // 2))
    found.append((lambda b: gdense.at[pl.ds(pl.multiple_of(b * gs, gs), gs), pl.ds(owner * width, width)], width // 2))
    return found


def ring_rs2_kernel(groups, x_pair, *refs):
    gu, gd, gdense, out_up, out_down, out_dense = refs[:6]
    n_items = 5
    scr = refs[6:]
    rbuf, sbuf, pbuf, own, fin, xr, cr, xs = (scr[i * n_items : (i + 1) * n_items] for i in range(8))
    ring_send, ring_recv, part_send, part_recv, load_sem, x_send, x_recv, c_send, c_recv = scr[8 * n_items :]
    pos_of, dev_at = ring_order(groups)
    rx = lax.axis_index("rx")
    core = lax.axis_index("core")
    g = lax.axis_index("group")
    other = 1 - core
    pos = pos_of(g)
    nbr = (dev_at(pos + 1), dev_at(pos + groups - 1))
    gs = gu.shape[1] // groups
    fs = gd.shape[1] // groups
    width = gdense.shape[1] // 2
    mine = grad_items(gu, gd, gdense, core, gs, fs, width)
    theirs = grad_items(gu, gd, gdense, other, gs, fs, width)

    barrier = pltpu.get_barrier_semaphore()
    for n in nbr:
        pl.semaphore_signal(barrier, inc=1, device_id=(rx, core, n), device_id_type=MESH_ID)
    pl.semaphore_signal(barrier, inc=1, device_id=(rx, other, g), device_id_type=MESH_ID)
    count = 3
    if x_pair:
        pl.semaphore_signal(barrier, inc=1, device_id=(1 - rx, core, g), device_id_type=MESH_ID)
        count = 4
    pl.semaphore_wait(barrier, count)

    def block_at(d, s):
        if d == 0:
            return dev_at(pos + 2 * groups - 1 - s)
        return dev_at(pos + 1 + s)

    def cols(j, d):
        half = mine[j][1]
        return pl.ds(d * half, half)

    def load(d, s, slot, j):
        return pltpu.make_async_copy(mine[j][0](block_at(d, s)).at[:, cols(j, d)], own[j].at[d, slot], load_sem.at[d, slot, j])

    def part(d, s, j):
        return pltpu.make_async_remote_copy(
            src_ref=theirs[j][0](block_at(d, s)).at[:, cols(j, d)], dst_ref=pbuf[j].at[d, s],
            send_sem=part_send.at[d, s, j], recv_sem=part_recv.at[d, s, j],
            device_id=(rx, other, g), device_id_type=MESH_ID,
        )

    def ring(d, s, j):
        return pltpu.make_async_remote_copy(
            src_ref=sbuf[j].at[d, s], dst_ref=rbuf[j].at[d, s],
            send_sem=ring_send.at[d, s, j], recv_sem=ring_recv.at[d, s, j],
            device_id=(rx, core, nbr[d]), device_id_type=MESH_ID,
        )

    sends = []

    def ring_wave(items):
        for d in range(2):
            for j in items:
                load(d, 0, 0, j).start()
                c = part(d, 0, j)
                c.start()
                sends.append(c)
        for s in range(groups):
            slot = s % 2
            for d in range(2):
                for j in items:
                    load(d, s, slot, j).wait()
                    if s + 1 < groups:
                        load(d, s + 1, 1 - slot, j).start()
                        c = part(d, s + 1, j)
                        c.start()
                        sends.append(c)
                    part(d, s, j).wait_recv()
                    val = own[j][d, slot].astype(F32) + pbuf[j][d, s].astype(F32)
                    if s > 0:
                        ring(d, s - 1, j).wait_recv()
                        val = val + rbuf[j][d, s - 1].astype(F32)
                    if s < groups - 1:
                        sbuf[j][d, s] = val.astype(BF16)
                        c = ring(d, s, j)
                        c.start()
                        sends.append(c)
                    else:
                        fin[j][d] = val

    def x_start(items):
        copies = []
        for d in range(2):
            for j in items:
                xs[j][d] = fin[j][d].astype(BF16)
                c = pltpu.make_async_remote_copy(
                    src_ref=xs[j].at[d], dst_ref=xr[j].at[d], send_sem=x_send.at[d, j], recv_sem=x_recv.at[d, j],
                    device_id=(1 - rx, core, g), device_id_type=MESH_ID,
                )
                c.start()
                copies.append(c)
        sends.extend(copies)
        return copies

    def x_finish(items, copies):
        for c in copies:
            c.wait_recv()
        for d in range(2):
            for j in items:
                fin[j][d] = xs[j][d].astype(F32) + xr[j][d].astype(F32)

    def c_start(items):
        copies = []
        for d in range(2):
            for j in items:
                c = pltpu.make_async_remote_copy(
                    src_ref=fin[j].at[d], dst_ref=cr[j].at[d], send_sem=c_send.at[d, j], recv_sem=c_recv.at[d, j],
                    device_id=(rx, other, g), device_id_type=MESH_ID,
                )
                c.start()
                copies.append(c)
        return copies

    wave_a, wave_b = (0, 1, 4), (2, 3)
    ring_wave(wave_a)
    if x_pair:
        xa = x_start(wave_a)
    ring_wave(wave_b)
    if x_pair:
        x_finish(wave_a, xa)
    c_copies = c_start(wave_a)
    if x_pair:
        x_finish(wave_b, x_start(wave_b))
    c_copies += c_start(wave_b)

    def out_items(owner):
        found = []
        for k in range(2):
            e = 2 * k + owner
            found.append(lambda d, e=e: out_up.at[e, :, pl.ds(d * (F // 2), F // 2)])
            found.append(lambda d, e=e: out_down.at[e, :, pl.ds(d * (D // 2), D // 2)])
        found.append(lambda d: out_dense.at[:, pl.ds(owner * width + d * (width // 2), width // 2)])
        return found

    mine_out = out_items(core)
    theirs_out = out_items(other)
    for d in range(2):
        for j in range(n_items):
            mine_out[j](d)[...] = fin[j][d]
    for c in c_copies:
        c.wait_recv()
    for d in range(2):
        for j in range(n_items):
            theirs_out[j](d)[...] = cr[j][d]
    for c in sends + c_copies:
        c.wait_send()


def grad_reduce(gu, gd, gdense, groups, x_pair, collective_id):
    gs = gu.shape[1] // groups
    fs = gd.shape[1] // groups
    width = gdense.shape[1] // 2
    item_shapes = [(gs, F // 2), (fs, D // 2), (gs, F // 2), (fs, D // 2), (gs, width // 2)]
    scratch = []
    for lead, dtype in (((2, groups - 1), BF16), ((2, groups - 1), BF16), ((2, groups), BF16), ((2, 2), BF16), ((2,), F32), ((2,), BF16), ((2,), F32), ((2,), BF16)):
        scratch += [pltpu.VMEM(lead + shp, dtype) for shp in item_shapes]
    scratch += [
        pltpu.SemaphoreType.DMA((2, groups - 1, 5)),
        pltpu.SemaphoreType.DMA((2, groups - 1, 5)),
        pltpu.SemaphoreType.DMA((2, groups, 5)),
        pltpu.SemaphoreType.DMA((2, groups, 5)),
        pltpu.SemaphoreType.DMA((2, 2, 5)),
        pltpu.SemaphoreType.DMA((2, 5)),
        pltpu.SemaphoreType.DMA((2, 5)),
        pltpu.SemaphoreType.DMA((2, 5)),
        pltpu.SemaphoreType.DMA((2, 5)),
    ]
    outs = [
        jax.ShapeDtypeStruct((E, gs, F), F32),
        jax.ShapeDtypeStruct((E, fs, D), F32),
        jax.ShapeDtypeStruct((gs, gdense.shape[1]), F32),
    ]
    nbytes = 2 * (gu.size + gd.size + gdense.size)
    return pl.pallas_call(
        functools.partial(ring_rs2_kernel, groups, x_pair),
        out_shape=outs,
        in_specs=[pl.BlockSpec(memory_space=pl.ANY)] * 3,
        out_specs=[pl.BlockSpec(memory_space=pltpu.VMEM)] * 3,
        scratch_shapes=scratch,
        compiler_params=pltpu.CompilerParams(
            collective_id=collective_id, has_side_effects=True, vmem_limit_bytes=62 * 1024 * 1024
        ),
        cost_estimate=pl.CostEstimate(flops=gu.size + gd.size + gdense.size, bytes_accessed=nbytes, transcendentals=0),
    )(gu, gd, gdense)


TILE = 256
TILE_B = 256
CAPP = 512
SQRT_HALF = float(np.sqrt(0.5))
INV_SQRT_2PI = float(1.0 / np.sqrt(2.0 * np.pi))


def ffn_fwd_kernel(micro, counts, x_ref, w1_ref, b1_ref, w2_ref, b2_ref, hp_ref, h_ref, y_ref):
    e, m, t = pl.program_id(0), pl.program_id(1), pl.program_id(2)
    active = t * TILE < counts[e * micro + m]

    @pl.when(active)
    def _():
        hp = jnp.dot(x_ref[0], w1_ref[0], preferred_element_type=F32) + b1_ref[0]
        h = (0.5 * hp * (1.0 + lax.erf(hp * SQRT_HALF))).astype(BF16)
        hp_ref[0] = hp
        h_ref[0] = h
        y = jnp.dot(h, w2_ref[0], preferred_element_type=F32) + b2_ref[0]
        hi = y.astype(BF16)
        y_ref[0, :, :D] = hi
        y_ref[0, :, D:] = (y - hi.astype(F32)).astype(BF16)

    @pl.when(jnp.logical_not(active))
    def _():
        y_ref[0] = jnp.zeros(y_ref.shape[1:], BF16)


def ffn_forward(counts, table_in, w1, b1, w2, b2, micro):
    tiles = CAPP // TILE
    rows = table_in.shape[1]
    row_map = lambda e, m, t, c: (m, e * tiles + t, 0)
    w_map = lambda e, m, t, c: (e, 0, 0)
    grid_spec = pltpu.PrefetchScalarGridSpec(
        num_scalar_prefetch=1,
        grid=(E, micro, tiles),
        in_specs=[
            pl.BlockSpec((1, TILE, D), row_map),
            pl.BlockSpec((1, D, F), w_map),
            pl.BlockSpec((1, 1, F), w_map),
            pl.BlockSpec((1, F, D), w_map),
            pl.BlockSpec((1, 1, D), w_map),
        ],
        out_specs=[
            pl.BlockSpec((1, TILE, F), row_map),
            pl.BlockSpec((1, TILE, F), row_map),
            pl.BlockSpec((1, TILE, 2 * D), row_map),
        ],
    )
    work = micro * rows
    return pl.pallas_call(
        functools.partial(ffn_fwd_kernel, micro),
        grid_spec=grid_spec,
        out_shape=[
            jax.ShapeDtypeStruct((micro, rows, F), F32),
            jax.ShapeDtypeStruct((micro, rows, F), BF16),
            jax.ShapeDtypeStruct((micro, rows, 2 * D), BF16),
        ],
        compiler_params=pltpu.CompilerParams(vmem_limit_bytes=48 * 1024 * 1024),
        cost_estimate=pl.CostEstimate(
            flops=4 * work * D * F // 2, bytes_accessed=work * (2 * D + 6 * F + 4 * D) // 2, transcendentals=work * F // 2
        ),
    )(counts, table_in, w1, b1, w2, b2)


def ffn_bwd_kernel(micro, counts, dy_ref, x_ref, hp_ref, h_ref, w1_ref, w2_ref, dt_ref, gu_ref, gd_ref, gb_ref, gb2_ref, gu_acc, gd_acc):
    e, m, t = pl.program_id(0), pl.program_id(1), pl.program_id(2)
    active = t * TILE_B < counts[e * micro + m]

    @pl.when((m == 0) & (t == 0))
    def _():
        gu_acc[...] = jnp.zeros(gu_acc.shape, F32)
        gd_acc[...] = jnp.zeros(gd_acc.shape, F32)
        gb_ref[...] = jnp.zeros(gb_ref.shape, F32)
        gb2_ref[...] = jnp.zeros(gb2_ref.shape, F32)

    @pl.when(active)
    def _():
        dy = dy_ref[0]
        hp = hp_ref[0]
        d_hidden = lax.dot_general(dy, w2_ref[0], (((1,), (1,)), ((), ())), preferred_element_type=F32)
        slope = 0.5 * (1.0 + lax.erf(hp * SQRT_HALF)) + hp * jnp.exp(-0.5 * hp * hp) * INV_SQRT_2PI
        d_pre = (d_hidden * slope).astype(BF16)
        dt = lax.dot_general(d_pre, w1_ref[0], (((1,), (1,)), ((), ())), preferred_element_type=F32)
        hi = dt.astype(BF16)
        dt_ref[0, :, :D] = hi
        dt_ref[0, :, D:] = (dt - hi.astype(F32)).astype(BF16)
        gb2_ref[0] += jnp.sum(dy.astype(F32), 0, keepdims=True)
        gu_acc[...] += lax.dot_general(x_ref[0], d_pre, (((0,), (0,)), ((), ())), preferred_element_type=F32)
        gd_acc[...] += lax.dot_general(h_ref[0], dy, (((0,), (0,)), ((), ())), preferred_element_type=F32)
        gb_ref[0] += jnp.sum(d_pre.astype(F32), 0, keepdims=True)

    @pl.when(jnp.logical_not(active))
    def _():
        dt_ref[0] = jnp.zeros(dt_ref.shape[1:], BF16)

    @pl.when((m == micro - 1) & (t == pl.num_programs(2) - 1))
    def _():
        gu_ref[0] = gu_acc[...].astype(BF16)
        gd_ref[0] = gd_acc[...].astype(BF16)


def ffn_backward(counts, d_expert, table_in, hp, h, w1, w2, micro):
    tiles = CAPP // TILE_B
    rows = table_in.shape[1]
    row_map = lambda e, m, t, c: (m, e * tiles + t, 0)
    w_map = lambda e, m, t, c: (e, 0, 0)
    grid_spec = pltpu.PrefetchScalarGridSpec(
        num_scalar_prefetch=1,
        grid=(E, micro, tiles),
        in_specs=[
            pl.BlockSpec((1, TILE_B, D), row_map),
            pl.BlockSpec((1, TILE_B, D), row_map),
            pl.BlockSpec((1, TILE_B, F), row_map),
            pl.BlockSpec((1, TILE_B, F), row_map),
            pl.BlockSpec((1, D, F), w_map),
            pl.BlockSpec((1, F, D), w_map),
        ],
        out_specs=[
            pl.BlockSpec((1, TILE_B, 2 * D), row_map),
            pl.BlockSpec((1, D, F), w_map),
            pl.BlockSpec((1, F, D), w_map),
            pl.BlockSpec((1, 1, F), w_map),
            pl.BlockSpec((1, 1, D), w_map),
        ],
        scratch_shapes=[pltpu.VMEM((D, F), F32), pltpu.VMEM((F, D), F32)],
    )
    work = micro * rows
    return pl.pallas_call(
        functools.partial(ffn_bwd_kernel, micro),
        grid_spec=grid_spec,
        out_shape=[
            jax.ShapeDtypeStruct((micro, rows, 2 * D), BF16),
            jax.ShapeDtypeStruct((E, D, F), BF16),
            jax.ShapeDtypeStruct((E, F, D), BF16),
            jax.ShapeDtypeStruct((E, 1, F), F32),
            jax.ShapeDtypeStruct((E, 1, D), F32),
        ],
        compiler_params=pltpu.CompilerParams(vmem_limit_bytes=60 * 1024 * 1024),
        cost_estimate=pl.CostEstimate(
            flops=8 * work * D * F // 2, bytes_accessed=work * (8 * D + 6 * F) // 2 + 16 * E * D * F, transcendentals=2 * work * F // 2
        ),
    )(counts, d_expert, table_in, hp, h, w1, w2)

def layer_norm(value, gain, shift):
    center = value - jnp.mean(value, -1, keepdims=True)
    spread = jnp.mean(center * center, -1, keepdims=True)
    return center * lax.rsqrt(spread + 1e-06) * gain + shift


def gelu_exact(value):
    return jax.nn.gelu(value, approximate=False)


def split_heads(part):
    return part.reshape(-1, S, HEADS, HEAD_DIM)


def dot(a, b):
    return jnp.dot(a, b, preferred_element_type=F32)


def assign_places(route):
    chosen = jnp.concatenate([route[:, :, 0], route[:, :, 1]], 1)
    hits = (chosen[:, :, None] == jnp.arange(E, dtype=jnp.int32)).astype(jnp.int32)
    before = jnp.cumsum(hits, 1) - hits
    slot = jnp.sum(before * hits, 2)
    return chosen * CAPP + slot, jnp.sum(hits, 1)


def hi_lo(v):
    hi = v.astype(BF16)
    lo = (v - hi.astype(F32)).astype(BF16)
    return jnp.concatenate([hi, lo], -1)


def pick_rows(onehot, split):
    both = jnp.einsum("mnr,mrd->mnd", onehot, split, preferred_element_type=F32)
    return both[..., :D] + both[..., D:]


def pack_dense(qkv_w, out_w, router_w, vectors, up_bias):
    rows = qkv_w.shape[0]
    ub = up_bias.reshape(E, rows, 4).transpose(1, 0, 2).reshape(rows, E * 4)
    return jnp.concatenate([qkv_w, out_w, router_w, vectors.T, ub], 1)


def unpack_dense(packed):
    rows = packed.shape[0]
    w_qkv = packed[:, : 3 * D]
    w_out = packed[:, 3 * D : 4 * D]
    w_router = packed[:, 4 * D : 4 * D + E]
    table = packed[:, 4 * D + E : 4 * D + E + NV].T
    ub = packed[:, 4 * D + E + NV :].reshape(rows, E, 4).transpose(1, 0, 2).reshape(E, rows * 4)
    return w_qkv, w_out, w_router, table, ub


def attention_fwd(w_qkv, w_out, table, value):
    rows = value.shape[0]
    scale = HEAD_DIM ** (-0.5)
    first = layer_norm(value, table[0], table[1]).astype(BF16)
    qkv_bias = jnp.concatenate([table[2], jnp.zeros((D,), F32), table[3]])
    qkv = (dot(first, w_qkv) + qkv_bias).astype(BF16)
    query, key_part, val_part = (
        split_heads(qkv[:, :D]),
        split_heads(qkv[:, D : 2 * D]),
        split_heads(qkv[:, 2 * D :]),
    )
    scores = jnp.einsum("bqhd,bkhd->bhqk", query, key_part, preferred_element_type=F32) * scale
    peak = jnp.max(scores, -1, keepdims=True)
    expo = jnp.exp(scores - peak)
    total = jnp.sum(expo, -1, keepdims=True)
    probs_att = (expo / total).astype(BF16)
    log_total = peak + jnp.log(total)
    attended = jnp.einsum("bhqk,bkhd->bqhd", probs_att, val_part, preferred_element_type=F32)
    attended = attended.reshape(rows, D).astype(BF16)
    resid = value + (dot(attended, w_out) + table[4])
    return first, qkv, log_total, attended, resid


def attention_bwd(w_qkv, w_out, table, value, first, qkv, log_total, attended, d_resid):
    rows = value.shape[0]
    scale = HEAD_DIM ** (-0.5)
    d_branch = d_resid.astype(BF16)
    g_bias_out = jnp.sum(d_branch.astype(F32), 0)
    g_out = lax.dot_general(attended, d_branch, (((0,), (0,)), ((), ())), preferred_element_type=F32)
    d_att = split_heads(
        lax.dot_general(d_branch, w_out, (((1,), (1,)), ((), ())), preferred_element_type=F32).astype(BF16)
    )
    query, key_part, val_part = (
        split_heads(qkv[:, :D]),
        split_heads(qkv[:, D : 2 * D]),
        split_heads(qkv[:, 2 * D :]),
    )
    scores = jnp.einsum("bqhd,bkhd->bhqk", query, key_part, preferred_element_type=F32) * scale
    probs_f = jnp.exp(scores - log_total)
    probs_att = probs_f.astype(BF16)
    d_val = jnp.einsum("bhqk,bqhd->bkhd", probs_att, d_att, preferred_element_type=F32)
    d_prob = jnp.einsum("bqhd,bkhd->bhqk", d_att, val_part, preferred_element_type=F32)
    d_score = (probs_f * (d_prob - jnp.sum(d_prob * probs_f, -1, keepdims=True))).astype(BF16)
    d_query = jnp.einsum("bhqk,bkhd->bqhd", d_score, key_part, preferred_element_type=F32) * scale
    d_key = jnp.einsum("bhqk,bqhd->bkhd", d_score, query, preferred_element_type=F32) * scale
    d_qkv = jnp.concatenate(
        [d_query.reshape(rows, D), d_key.reshape(rows, D), d_val.reshape(rows, D)], 1
    ).astype(BF16)
    d_qkv_f = d_qkv.astype(F32)
    g_bias_q = jnp.sum(d_qkv_f[:, :D], 0)
    g_bias_v = jnp.sum(d_qkv_f[:, 2 * D :], 0)
    g_qkv = lax.dot_general(first, d_qkv, (((0,), (0,)), ((), ())), preferred_element_type=F32)
    d_first = lax.dot_general(d_qkv, w_qkv, (((1,), (1,)), ((), ())), preferred_element_type=F32)
    first_pull = jax.vjp(layer_norm, value, table[0], table[1])[1]
    d_input, g_gain_one, g_shift_one = first_pull(d_first)
    return (g_qkv, g_out, g_bias_out, g_bias_q, g_bias_v, g_gain_one, g_shift_one), d_input


def adamw(weight, moments, grad, rate):
    first = 0.5 * moments[0] + 0.5 * grad
    root = jnp.sqrt(0.5 * moments[1] * moments[1] + 0.5 * grad * grad)
    update = first / (root + 1e-08)
    which = lax.broadcasted_iota(jnp.int32, moments.shape, 0) == 0
    both = jnp.where(which, 0.5 * moments + 0.5 * grad, jnp.sqrt(0.5 * moments * moments + 0.5 * grad * grad))
    return (weight - rate * (update + 0.1 * weight), both)


def shards(
    tokens,
    cotangent,
    expert_index,
    qkv_weight,
    out_weight,
    router_weight,
    up_weight,
    up_bias,
    down_weight,
    vectors,
    qkv_moments,
    out_moments,
    router_moments,
    up_moments,
    up_bias_moments,
    down_moments,
    vector_moments,
):
    rows = tokens.shape[0]
    micro = rows // MB_TOK
    gs = qkv_weight.shape[0]
    group_size = D // gs
    core = lax.axis_index("core")

    dense_in = pack_dense(qkv_weight, out_weight, router_weight, vectors, up_bias)
    width = dense_in.shape[1]
    dense_in = jnp.pad(dense_in, ((0, 0), (0, DENSE_AG - width))).astype(BF16)
    w_up_all, w_down_all, dense = ring_all_gather(
        up_weight.astype(BF16), down_weight.astype(BF16), dense_in, group_size, 1
    )
    w_qkv, w_out, w_router, table_b, b_up_b = unpack_dense(dense[:, :width])
    table = table_b.astype(F32)
    b_up = b_up_b.astype(F32)

    value = tokens.astype(F32)
    d_out = cotangent.astype(F32)
    first, qkv, log_total, attended, resid = attention_fwd(w_qkv, w_out, table, value)
    second = layer_norm(resid, table[5], table[6]).astype(BF16)
    logits = dot(second, w_router)
    probs = jax.nn.softmax(logits, -1)
    picked = expert_index[:, :, None] == jnp.arange(E, dtype=jnp.int32)
    gate = jnp.sum(jnp.where(picked, probs[:, None, :], 0.0), -1)

    route = expert_index.reshape(micro, MB_TOK, 2)
    places, counts = assign_places(route)
    counts = counts.T.reshape(E * micro)
    onehot = (places[:, :, None] == jnp.arange(E * CAPP, dtype=jnp.int32)).astype(BF16)
    second_m = second.reshape(micro, MB_TOK, D)
    pair = jnp.concatenate([second_m, second_m], 1)
    table_in = jnp.einsum("mnr,mnd->mrd", onehot, pair, preferred_element_type=F32).astype(BF16)

    hidden_pre, hidden, y_all = ffn_forward(
        counts, table_in, w_up_all, b_up[:, None, :], w_down_all, table[7 : 7 + E][:, None, :], micro
    )
    picked_rows = pick_rows(onehot, y_all)
    out_zero = picked_rows[:, :MB_TOK].reshape(rows, D)
    out_one = picked_rows[:, MB_TOK:].reshape(rows, D)
    result = resid + (gate[:, 0:1] * out_zero + gate[:, 1:2] * out_one)

    d_gate = jnp.stack([jnp.sum(d_out * out_zero, -1), jnp.sum(d_out * out_one, -1)], 1)
    d_out_m = d_out.reshape(micro, MB_TOK, D)
    gate_m = gate.reshape(micro, MB_TOK, 2)
    weighted = jnp.concatenate([gate_m[:, :, 0:1] * d_out_m, gate_m[:, :, 1:2] * d_out_m], 1).astype(BF16)
    d_expert = jnp.einsum("mnr,mnd->mrd", onehot, weighted, preferred_element_type=F32).astype(BF16)

    d_table, g_up, g_down, g_b1, g_b2 = ffn_backward(counts, d_expert, table_in, hidden_pre, hidden, w_up_all, w_down_all, micro)
    g_up_bias_all = g_b1[:, 0, :]
    g_bias_down = g_b2[:, 0, :]

    onehot_sum = onehot[:, :MB_TOK] + onehot[:, MB_TOK:]
    d_picked = pick_rows(onehot_sum, d_table).reshape(rows, D)

    d_probs = jnp.sum(jnp.where(picked, d_gate[:, :, None], 0.0), 1)
    d_logit = (probs * (d_probs - jnp.sum(d_probs * probs, -1, keepdims=True))).astype(BF16)
    g_router = lax.dot_general(second, d_logit, (((0,), (0,)), ((), ())), preferred_element_type=F32)
    d_second = d_picked + lax.dot_general(d_logit, w_router, (((1,), (1,)), ((), ())), preferred_element_type=F32)
    norm_pull = jax.vjp(layer_norm, resid, table[5], table[6])[1]
    d_resid, g_gain_two, g_shift_two = norm_pull(d_second)
    d_resid = d_out + d_resid

    att_grads, d_input = attention_bwd(w_qkv, w_out, table, value, first, qkv, log_total, attended, d_resid)
    g_qkv, g_out, g_bias_out, g_bias_q, g_bias_v, g_gain_one, g_shift_one = att_grads
    input_grad = d_resid + d_input

    g_table = jnp.concatenate(
        [
            jnp.stack([g_gain_one, g_shift_one, g_bias_q, g_bias_v, g_bias_out, g_gain_two, g_shift_two]),
            g_bias_down,
        ],
        0,
    )
    dense_g = pack_dense(g_qkv, g_out, g_router, g_table, g_up_bias_all)
    width = dense_g.shape[1]
    dense_g = jnp.pad(dense_g, ((0, 0), (0, DENSE_AG - width))).astype(BF16)
    x_pair = lax.axis_size("rx") == 2
    r_up, r_down, r_dense = grad_reduce(g_up, g_down, dense_g, group_size, x_pair, 0)
    if not x_pair:
        r_up, r_down, r_dense = lax.psum((r_up, r_down, r_dense), "rx")
    r_qkv, r_out, r_router, r_table, r_ub = unpack_dense(r_dense[:, :width])

    reduced = (r_qkv, r_out, r_router, r_up, r_ub, r_down, r_table)
    rates = (
        2.0 * D ** (-0.5),
        2.0 * (D // 32) ** (-0.5),
        2.0 * (2 * D) ** (-0.5),
        2.0 * D ** (-0.5),
        0.2,
        2.0 * (F // 16) ** (-0.5),
        0.2,
    )
    params = (qkv_weight, out_weight, router_weight, up_weight, up_bias, down_weight, vectors)
    moments = (qkv_moments, out_moments, router_moments, up_moments, up_bias_moments, down_moments, vector_moments)
    news = []
    states = []
    for weight, state, grad, rate in zip(params, moments, reduced, rates):
        new_weight, new_state = adamw(weight, state, grad, rate)
        news.append(new_weight)
        states.append(new_state)
    return (result.astype(BF16), input_grad) + reduced + tuple(news) + tuple(states)


def solution(mesh):
    replica, group = mesh.shape["replica"], mesh.shape["group"]
    view = Mesh(np.asarray(mesh.devices).reshape(replica // 2, 2, group), ("rx", "core", "group"))
    in_specs = (
        P(TOK, None),
        P(TOK, None),
        P(TOK, None),
        P("group", None),
        P("group", None),
        P("group", None),
        P(None, "group", None),
        P(None, "group"),
        P(None, "group", None),
        P(None, "group"),
        P(None, "group", None),
        P(None, "group", None),
        P(None, "group", None),
        P(None, None, "group", None),
        P(None, None, "group"),
        P(None, None, "group", None),
        P(None, None, "group"),
    )
    out_specs = (
        P(TOK, None),
        P(TOK, None),
        P("group", None),
        P("group", None),
        P("group", None),
        P(None, "group", None),
        P(None, "group"),
        P(None, "group", None),
        P(None, "group"),
        P("group", None),
        P("group", None),
        P("group", None),
        P(None, "group", None),
        P(None, "group"),
        P(None, "group", None),
        P(None, "group"),
        P(None, "group", None),
        P(None, "group", None),
        P(None, "group", None),
        P(None, None, "group", None),
        P(None, None, "group"),
        P(None, None, "group", None),
        P(None, None, "group"),
    )
    return jax.shard_map(shards, mesh=view, in_specs=in_specs, out_specs=out_specs, check_vma=False)
```

```python
import functools

import jax
import jax.numpy as jnp
import numpy as np
from jax import lax
from jax.sharding import Mesh
from jax.sharding import PartitionSpec as P
from jax.experimental import pallas as pl
from jax.experimental.pallas import tpu as pltpu

D = 512
HEADS = 8
HEAD_DIM = 64
F = 2048
E = 4
S = 197
MB_TOK = 394
CAP = 392
NV = 11
DENSE_AG = 2560
DENSE_PAD = 2304
F32 = jnp.float32
BF16 = jnp.bfloat16
TOK = ("rx", "core", "group")


MESH_ID = pl.DeviceIdType.MESH


def ring_order(groups):
    if groups in (4, 8):
        zs = groups // 2

        def pos_of(g):
            y = g % 2
            z = g // 2
            return z + y * (2 * zs - 1 - 2 * z)

        def dev_at(p):
            p = p % groups
            yy = p // zs
            return 2 * (p + yy * (2 * zs - 1 - 2 * p)) + yy

        return pos_of, dev_at
    return (lambda g: g), (lambda p: p % groups)


def ring_rs_kernel(groups, n_in, *refs):
    ins = refs[:n_in]
    outs = refs[n_in : 2 * n_in]
    rbufs = refs[2 * n_in : 3 * n_in]
    sbufs = refs[3 * n_in : 4 * n_in]
    owns = refs[4 * n_in : 5 * n_in]
    send_sem, recv_sem, load_sem = refs[5 * n_in :]
    pos_of, dev_at = ring_order(groups)
    rx = lax.axis_index("rx")
    core = lax.axis_index("core")
    g = lax.axis_index("group")
    pos = pos_of(g)
    nbr = (dev_at(pos + 1), dev_at(pos + groups - 1))

    barrier = pltpu.get_barrier_semaphore()
    for n in nbr:
        pl.semaphore_signal(barrier, inc=1, device_id=(rx, core, n), device_id_type=MESH_ID)
    pl.semaphore_wait(barrier, 2)

    def block_dev(d, s):
        if d == 0:
            return dev_at(pos + 2 * groups - s - 1)
        return dev_at(pos + s + 1)

    def load(d, s, slot):
        b = block_dev(d, s)
        copies = []
        for i in range(n_in):
            rows = ins[i].shape[1] // groups
            half = ins[i].shape[2] // 2
            src = ins[i].at[:, pl.ds(pl.multiple_of(b * rows, rows), rows), pl.ds(d * half, half)]
            copies.append(pltpu.make_async_copy(src, owns[i].at[d, slot], load_sem.at[d, slot, i]))
        return copies

    def remote(d, s, i):
        return pltpu.make_async_remote_copy(
            src_ref=sbufs[i].at[d, s],
            dst_ref=rbufs[i].at[d, s],
            send_sem=send_sem.at[d, s, i],
            recv_sem=recv_sem.at[d, s, i],
            device_id=(rx, core, nbr[d]),
            device_id_type=MESH_ID,
        )

    for d in range(2):
        for c in load(d, 0, 0):
            c.start()
    sends = []
    for s in range(groups):
        slot = s % 2
        for d in range(2):
            for c in load(d, s, slot):
                c.wait()
            if s + 1 < groups:
                for c in load(d, s + 1, 1 - slot):
                    c.start()
            for i in range(n_in):
                if s > 0:
                    remote(d, s - 1, i).wait_recv()
                for a in range(ins[i].shape[0]):
                    mine = owns[i][d, slot, a].astype(F32)
                    if s > 0:
                        mine = mine + rbufs[i][d, s - 1, a].astype(F32)
                    if s < groups - 1:
                        sbufs[i][d, s, a] = mine.astype(sbufs[i].dtype)
                    else:
                        half = ins[i].shape[2] // 2
                        outs[i][a, :, pl.ds(d * half, half)] = mine.astype(outs[i].dtype)
                if s < groups - 1:
                    c = remote(d, s, i)
                    c.start()
                    sends.append(c)
    for c in sends:
        c.wait_send()


def ring_reduce_scatter(xs, groups, collective_id):
    n_in = len(xs)
    outs, rb, own = [], [], []
    flops = 0
    nbytes = 0
    for x in xs:
        a, total, c = x.shape
        rows = total // groups
        outs.append(jax.ShapeDtypeStruct((a, rows, c), x.dtype))
        rb.append(pltpu.VMEM((2, groups - 1, a, rows, c // 2), x.dtype))
        own.append(pltpu.VMEM((2, 2, a, rows, c // 2), x.dtype))
        flops += a * total * c
        nbytes += 3 * x.size * x.dtype.itemsize
    scratch = rb + rb + own + [
        pltpu.SemaphoreType.DMA((2, groups - 1, n_in)),
        pltpu.SemaphoreType.DMA((2, groups - 1, n_in)),
        pltpu.SemaphoreType.DMA((2, 2, n_in)),
    ]
    return pl.pallas_call(
        functools.partial(ring_rs_kernel, groups, n_in),
        out_shape=outs,
        in_specs=[pl.BlockSpec(memory_space=pl.ANY)] * n_in,
        out_specs=[pl.BlockSpec(memory_space=pltpu.VMEM)] * n_in,
        scratch_shapes=scratch,
        compiler_params=pltpu.CompilerParams(
            collective_id=collective_id, has_side_effects=True, vmem_limit_bytes=60 * 1024 * 1024
        ),
        cost_estimate=pl.CostEstimate(flops=flops, bytes_accessed=nbytes, transcendentals=0),
    )(*xs)


def ring_ag_kernel(groups, *refs):
    in_up, in_down, in_dense, out_up, out_down, out_dense = refs[:6]
    ring_send, ring_recv, part_send, part_recv, local_sem = refs[6:]
    pos_of, dev_at = ring_order(groups)
    rx = lax.axis_index("rx")
    core = lax.axis_index("core")
    g = lax.axis_index("group")
    other = 1 - core
    pos = pos_of(g)
    nbr = (dev_at(pos + 1), dev_at(pos + groups - 1))
    gs = in_up.shape[1]
    fs = in_down.shape[1]
    width = in_dense.shape[1] // 2

    barrier = pltpu.get_barrier_semaphore()
    for n in nbr:
        pl.semaphore_signal(barrier, inc=1, device_id=(rx, core, n), device_id_type=MESH_ID)
    pl.semaphore_signal(barrier, inc=1, device_id=(rx, other, g), device_id_type=MESH_ID)
    pl.semaphore_wait(barrier, 3)

    def items(owner):
        found = []
        for k in range(2):
            e = 2 * k + owner
            found.append((in_up.at[e], lambda b, e=e: out_up.at[e, pl.ds(pl.multiple_of(b * gs, gs), gs)], F // 2))
            found.append((in_down.at[e], lambda b, e=e: out_down.at[e, pl.ds(pl.multiple_of(b * fs, fs), fs)], D // 2))
        dense_in = in_dense.at[:, pl.ds(owner * width, width)]
        found.append(
            (dense_in, lambda b: out_dense.at[pl.ds(pl.multiple_of(b * gs, gs), gs), pl.ds(owner * width, width)], width // 2)
        )
        return found

    mine = items(core)
    theirs = items(other)
    n_items = len(mine)

    locals_ = [pltpu.make_async_copy(in_up.at[e], out_up.at[e, pl.ds(pl.multiple_of(g * gs, gs), gs)], local_sem.at[e]) for e in range(E)]
    locals_ += [
        pltpu.make_async_copy(in_down.at[e], out_down.at[e, pl.ds(pl.multiple_of(g * fs, fs), fs)], local_sem.at[E + e])
        for e in range(E)
    ]
    locals_.append(pltpu.make_async_copy(in_dense, out_dense.at[pl.ds(pl.multiple_of(g * gs, gs), gs)], local_sem.at[2 * E]))
    for c in locals_:
        c.start()

    def block_at(d, s):
        if d == 0:
            return dev_at(pos + 2 * groups - 1 - s)
        return dev_at(pos + 1 + s)

    def ring_copy(d, s, j, src_block):
        src_in, dst_of, half = mine[j]
        cols = pl.ds(d * half, half)
        if src_block is None:
            src = src_in.at[:, cols]
            dst = dst_of(g).at[:, cols]
        else:
            src = dst_of(src_block).at[:, cols]
            dst = src
        return pltpu.make_async_remote_copy(
            src_ref=src, dst_ref=dst, send_sem=ring_send.at[d, s, j], recv_sem=ring_recv.at[d, s, j],
            device_id=(rx, core, nbr[d]), device_id_type=MESH_ID,
        )

    def part_copy(d, s, j, table, block):
        _, dst_of, half = table[j]
        view = dst_of(block).at[:, pl.ds(d * half, half)]
        return pltpu.make_async_remote_copy(
            src_ref=view, dst_ref=view, send_sem=part_send.at[d, s, j], recv_sem=part_recv.at[d, s, j],
            device_id=(rx, other, g), device_id_type=MESH_ID,
        )

    sends = []
    for d in range(2):
        for j in range(n_items):
            c = ring_copy(d, 0, j, None)
            c.start()
            sends.append(c)
    for s in range(groups - 1):
        for d in range(2):
            b = block_at(d, s)
            for j in range(n_items):
                pltpu.make_async_remote_copy(
                    src_ref=mine[j][1](b).at[:, pl.ds(d * mine[j][2], mine[j][2])],
                    dst_ref=mine[j][1](b).at[:, pl.ds(d * mine[j][2], mine[j][2])],
                    send_sem=ring_send.at[d, s, j], recv_sem=ring_recv.at[d, s, j],
                    device_id=(rx, core, nbr[d]), device_id_type=MESH_ID,
                ).wait_recv()
                if s + 1 < groups - 1:
                    c = ring_copy(d, s + 1, j, b)
                    c.start()
                    sends.append(c)
                c = part_copy(d, s, j, mine, b)
                c.start()
                sends.append(c)
    for s in range(groups - 1):
        for d in range(2):
            b = block_at(d, s)
            for j in range(n_items):
                part_copy(d, s, j, theirs, b).wait_recv()
    for c in sends:
        c.wait_send()
    for c in locals_:
        c.wait()


def ring_all_gather(up_b, down_b, dense_b, groups, collective_id):
    n_items = 5
    gs = up_b.shape[1]
    shapes = [
        jax.ShapeDtypeStruct((E, gs * groups, F), BF16),
        jax.ShapeDtypeStruct((E, down_b.shape[1] * groups, D), BF16),
        jax.ShapeDtypeStruct((gs * groups, dense_b.shape[1]), BF16),
    ]
    nbytes = sum(int(np.prod(s.shape)) * 2 for s in shapes)
    return pl.pallas_call(
        functools.partial(ring_ag_kernel, groups),
        out_shape=shapes,
        in_specs=[pl.BlockSpec(memory_space=pl.ANY)] * 3,
        out_specs=[pl.BlockSpec(memory_space=pl.ANY)] * 3,
        scratch_shapes=[
            pltpu.SemaphoreType.DMA((2, groups - 1, n_items)),
            pltpu.SemaphoreType.DMA((2, groups - 1, n_items)),
            pltpu.SemaphoreType.DMA((2, groups - 1, n_items)),
            pltpu.SemaphoreType.DMA((2, groups - 1, n_items)),
            pltpu.SemaphoreType.DMA((2 * E + 1,)),
        ],
        compiler_params=pltpu.CompilerParams(collective_id=collective_id, has_side_effects=True),
        cost_estimate=pl.CostEstimate(flops=0, bytes_accessed=nbytes, transcendentals=0),
    )(up_b, down_b, dense_b)


def grad_items(gu, gd, gdense, owner, gs, fs, width):
    found = []
    for k in range(2):
        e = 2 * k + owner
        found.append((lambda b, e=e: gu.at[e, pl.ds(pl.multiple_of(b * gs, gs), gs)], F // 2))
        found.append((lambda b, e=e: gd.at[e, pl.ds(pl.multiple_of(b * fs, fs), fs)], D // 2))
    found.append((lambda b: gdense.at[pl.ds(pl.multiple_of(b * gs, gs), gs), pl.ds(owner * width, width)], width // 2))
    return found


def ring_rs2_kernel(groups, x_pair, *refs):
    gu, gd, gdense, out_up, out_down, out_dense = refs[:6]
    n_items = 5
    scr = refs[6:]
    rbuf, sbuf, pbuf, own, fin, xr, cr, xs = (scr[i * n_items : (i + 1) * n_items] for i in range(8))
    ring_send, ring_recv, part_send, part_recv, load_sem, x_send, x_recv, c_send, c_recv = scr[8 * n_items :]
    pos_of, dev_at = ring_order(groups)
    rx = lax.axis_index("rx")
    core = lax.axis_index("core")
    g = lax.axis_index("group")
    other = 1 - core
    pos = pos_of(g)
    nbr = (dev_at(pos + 1), dev_at(pos + groups - 1))
    gs = gu.shape[1] // groups
    fs = gd.shape[1] // groups
    width = gdense.shape[1] // 2
    mine = grad_items(gu, gd, gdense, core, gs, fs, width)
    theirs = grad_items(gu, gd, gdense, other, gs, fs, width)

    barrier = pltpu.get_barrier_semaphore()
    for n in nbr:
        pl.semaphore_signal(barrier, inc=1, device_id=(rx, core, n), device_id_type=MESH_ID)
    pl.semaphore_signal(barrier, inc=1, device_id=(rx, other, g), device_id_type=MESH_ID)
    count = 3
    if x_pair:
        pl.semaphore_signal(barrier, inc=1, device_id=(1 - rx, core, g), device_id_type=MESH_ID)
        count = 4
    pl.semaphore_wait(barrier, count)

    def block_at(d, s):
        if d == 0:
            return dev_at(pos + 2 * groups - 1 - s)
        return dev_at(pos + 1 + s)

    def cols(j, d):
        half = mine[j][1]
        return pl.ds(d * half, half)

    def load(d, s, slot, j):
        return pltpu.make_async_copy(mine[j][0](block_at(d, s)).at[:, cols(j, d)], own[j].at[d, slot], load_sem.at[d, slot, j])

    def part(d, s, j):
        return pltpu.make_async_remote_copy(
            src_ref=theirs[j][0](block_at(d, s)).at[:, cols(j, d)], dst_ref=pbuf[j].at[d, s],
            send_sem=part_send.at[d, s, j], recv_sem=part_recv.at[d, s, j],
            device_id=(rx, other, g), device_id_type=MESH_ID,
        )

    def ring(d, s, j):
        return pltpu.make_async_remote_copy(
            src_ref=sbuf[j].at[d, s], dst_ref=rbuf[j].at[d, s],
            send_sem=ring_send.at[d, s, j], recv_sem=ring_recv.at[d, s, j],
            device_id=(rx, core, nbr[d]), device_id_type=MESH_ID,
        )

    sends = []

    def ring_wave(items):
        for d in range(2):
            for j in items:
                load(d, 0, 0, j).start()
                c = part(d, 0, j)
                c.start()
                sends.append(c)
        for s in range(groups):
            slot = s % 2
            for d in range(2):
                for j in items:
                    load(d, s, slot, j).wait()
                    if s + 1 < groups:
                        load(d, s + 1, 1 - slot, j).start()
                        c = part(d, s + 1, j)
                        c.start()
                        sends.append(c)
                    part(d, s, j).wait_recv()
                    val = own[j][d, slot].astype(F32) + pbuf[j][d, s].astype(F32)
                    if s > 0:
                        ring(d, s - 1, j).wait_recv()
                        val = val + rbuf[j][d, s - 1].astype(F32)
                    if s < groups - 1:
                        sbuf[j][d, s] = val.astype(BF16)
                        c = ring(d, s, j)
                        c.start()
                        sends.append(c)
                    else:
                        fin[j][d] = val

    def x_start(items):
        copies = []
        for d in range(2):
            for j in items:
                xs[j][d] = fin[j][d].astype(BF16)
                c = pltpu.make_async_remote_copy(
                    src_ref=xs[j].at[d], dst_ref=xr[j].at[d], send_sem=x_send.at[d, j], recv_sem=x_recv.at[d, j],
                    device_id=(1 - rx, core, g), device_id_type=MESH_ID,
                )
                c.start()
                copies.append(c)
        sends.extend(copies)
        return copies

    def x_finish(items, copies):
        for c in copies:
            c.wait_recv()
        for d in range(2):
            for j in items:
                fin[j][d] = xs[j][d].astype(F32) + xr[j][d].astype(F32)

    def c_start(items):
        copies = []
        for d in range(2):
            for j in items:
                c = pltpu.make_async_remote_copy(
                    src_ref=fin[j].at[d], dst_ref=cr[j].at[d], send_sem=c_send.at[d, j], recv_sem=c_recv.at[d, j],
                    device_id=(rx, other, g), device_id_type=MESH_ID,
                )
                c.start()
                copies.append(c)
        return copies

    wave_a, wave_b = (0, 1, 2, 4), (3,)
    ring_wave(wave_a)
    if x_pair:
        xa = x_start(wave_a)
    ring_wave(wave_b)
    if x_pair:
        x_finish(wave_a, xa)
    c_copies = c_start(wave_a)
    if x_pair:
        x_finish(wave_b, x_start(wave_b))
    c_copies += c_start(wave_b)

    def out_items(owner):
        found = []
        for k in range(2):
            e = 2 * k + owner
            found.append(lambda d, e=e: out_up.at[e, :, pl.ds(d * (F // 2), F // 2)])
            found.append(lambda d, e=e: out_down.at[e, :, pl.ds(d * (D // 2), D // 2)])
        found.append(lambda d: out_dense.at[:, pl.ds(owner * width + d * (width // 2), width // 2)])
        return found

    mine_out = out_items(core)
    theirs_out = out_items(other)
    for d in range(2):
        for j in range(n_items):
            mine_out[j](d)[...] = fin[j][d]
    for c in c_copies:
        c.wait_recv()
    for d in range(2):
        for j in range(n_items):
            theirs_out[j](d)[...] = cr[j][d]
    for c in sends + c_copies:
        c.wait_send()


def grad_reduce(gu, gd, gdense, groups, x_pair, collective_id):
    gs = gu.shape[1] // groups
    fs = gd.shape[1] // groups
    width = gdense.shape[1] // 2
    item_shapes = [(gs, F // 2), (fs, D // 2), (gs, F // 2), (fs, D // 2), (gs, width // 2)]
    scratch = []
    for lead, dtype in (((2, groups - 1), BF16), ((2, groups - 1), BF16), ((2, groups), BF16), ((2, 2), BF16), ((2,), F32), ((2,), BF16), ((2,), F32), ((2,), BF16)):
        scratch += [pltpu.VMEM(lead + shp, dtype) for shp in item_shapes]
    scratch += [
        pltpu.SemaphoreType.DMA((2, groups - 1, 5)),
        pltpu.SemaphoreType.DMA((2, groups - 1, 5)),
        pltpu.SemaphoreType.DMA((2, groups, 5)),
        pltpu.SemaphoreType.DMA((2, groups, 5)),
        pltpu.SemaphoreType.DMA((2, 2, 5)),
        pltpu.SemaphoreType.DMA((2, 5)),
        pltpu.SemaphoreType.DMA((2, 5)),
        pltpu.SemaphoreType.DMA((2, 5)),
        pltpu.SemaphoreType.DMA((2, 5)),
    ]
    outs = [
        jax.ShapeDtypeStruct((E, gs, F), F32),
        jax.ShapeDtypeStruct((E, fs, D), F32),
        jax.ShapeDtypeStruct((gs, gdense.shape[1]), F32),
    ]
    nbytes = 2 * (gu.size + gd.size + gdense.size)
    return pl.pallas_call(
        functools.partial(ring_rs2_kernel, groups, x_pair),
        out_shape=outs,
        in_specs=[pl.BlockSpec(memory_space=pl.ANY)] * 3,
        out_specs=[pl.BlockSpec(memory_space=pltpu.VMEM)] * 3,
        scratch_shapes=scratch,
        compiler_params=pltpu.CompilerParams(
            collective_id=collective_id, has_side_effects=True, vmem_limit_bytes=62 * 1024 * 1024
        ),
        cost_estimate=pl.CostEstimate(flops=gu.size + gd.size + gdense.size, bytes_accessed=nbytes, transcendentals=0),
    )(gu, gd, gdense)


TILE = 256
TILE_B = 256
CAPP = 512
SQRT_HALF = float(np.sqrt(0.5))
INV_SQRT_2PI = float(1.0 / np.sqrt(2.0 * np.pi))


def ffn_fwd_kernel(micro, counts, x_ref, w1_ref, b1_ref, w2_ref, b2_ref, hp_ref, h_ref, y_ref):
    e, m, t = pl.program_id(0), pl.program_id(1), pl.program_id(2)
    active = t * TILE < counts[e * micro + m]

    @pl.when(active)
    def _():
        hp = jnp.dot(x_ref[0], w1_ref[0], preferred_element_type=F32) + b1_ref[0]
        h = (0.5 * hp * (1.0 + lax.erf(hp * SQRT_HALF))).astype(BF16)
        hp_ref[0] = hp
        h_ref[0] = h
        y = jnp.dot(h, w2_ref[0], preferred_element_type=F32) + b2_ref[0]
        hi = y.astype(BF16)
        y_ref[0, :, :D] = hi
        y_ref[0, :, D:] = (y - hi.astype(F32)).astype(BF16)

    @pl.when(jnp.logical_not(active))
    def _():
        y_ref[0] = jnp.zeros(y_ref.shape[1:], BF16)


def ffn_forward(counts, table_in, w1, b1, w2, b2, micro):
    tiles = CAPP // TILE
    rows = table_in.shape[1]
    row_map = lambda e, m, t, c: (m, e * tiles + t, 0)
    w_map = lambda e, m, t, c: (e, 0, 0)
    grid_spec = pltpu.PrefetchScalarGridSpec(
        num_scalar_prefetch=1,
        grid=(E, micro, tiles),
        in_specs=[
            pl.BlockSpec((1, TILE, D), row_map),
            pl.BlockSpec((1, D, F), w_map),
            pl.BlockSpec((1, 1, F), w_map),
            pl.BlockSpec((1, F, D), w_map),
            pl.BlockSpec((1, 1, D), w_map),
        ],
        out_specs=[
            pl.BlockSpec((1, TILE, F), row_map),
            pl.BlockSpec((1, TILE, F), row_map),
            pl.BlockSpec((1, TILE, 2 * D), row_map),
        ],
    )
    work = micro * rows
    return pl.pallas_call(
        functools.partial(ffn_fwd_kernel, micro),
        grid_spec=grid_spec,
        out_shape=[
            jax.ShapeDtypeStruct((micro, rows, F), F32),
            jax.ShapeDtypeStruct((micro, rows, F), BF16),
            jax.ShapeDtypeStruct((micro, rows, 2 * D), BF16),
        ],
        compiler_params=pltpu.CompilerParams(vmem_limit_bytes=48 * 1024 * 1024),
        cost_estimate=pl.CostEstimate(
            flops=4 * work * D * F // 2, bytes_accessed=work * (2 * D + 6 * F + 4 * D) // 2, transcendentals=work * F // 2
        ),
    )(counts, table_in, w1, b1, w2, b2)


def ffn_bwd_kernel(micro, counts, dy_ref, x_ref, hp_ref, h_ref, w1_ref, w2_ref, dt_ref, gu_ref, gd_ref, gb_ref, gb2_ref, gu_acc, gd_acc):
    e, m, t = pl.program_id(0), pl.program_id(1), pl.program_id(2)
    active = t * TILE_B < counts[e * micro + m]

    @pl.when((m == 0) & (t == 0))
    def _():
        gu_acc[...] = jnp.zeros(gu_acc.shape, F32)
        gd_acc[...] = jnp.zeros(gd_acc.shape, F32)
        gb_ref[...] = jnp.zeros(gb_ref.shape, F32)
        gb2_ref[...] = jnp.zeros(gb2_ref.shape, F32)

    @pl.when(active)
    def _():
        dy = dy_ref[0]
        hp = hp_ref[0]
        d_hidden = lax.dot_general(dy, w2_ref[0], (((1,), (1,)), ((), ())), preferred_element_type=F32)
        slope = 0.5 * (1.0 + lax.erf(hp * SQRT_HALF)) + hp * jnp.exp(-0.5 * hp * hp) * INV_SQRT_2PI
        d_pre = (d_hidden * slope).astype(BF16)
        dt = lax.dot_general(d_pre, w1_ref[0], (((1,), (1,)), ((), ())), preferred_element_type=F32)
        hi = dt.astype(BF16)
        dt_ref[0, :, :D] = hi
        dt_ref[0, :, D:] = (dt - hi.astype(F32)).astype(BF16)
        gb2_ref[0] += jnp.sum(dy.astype(F32), 0, keepdims=True)
        gu_acc[...] += lax.dot_general(x_ref[0], d_pre, (((0,), (0,)), ((), ())), preferred_element_type=F32)
        gd_acc[...] += lax.dot_general(h_ref[0], dy, (((0,), (0,)), ((), ())), preferred_element_type=F32)
        gb_ref[0] += jnp.sum(d_pre.astype(F32), 0, keepdims=True)

    @pl.when(jnp.logical_not(active))
    def _():
        dt_ref[0] = jnp.zeros(dt_ref.shape[1:], BF16)

    @pl.when((m == micro - 1) & (t == pl.num_programs(2) - 1))
    def _():
        gu_ref[0] = gu_acc[...].astype(BF16)
        gd_ref[0] = gd_acc[...].astype(BF16)


def ffn_backward(counts, d_expert, table_in, hp, h, w1, w2, micro):
    tiles = CAPP // TILE_B
    rows = table_in.shape[1]
    row_map = lambda e, m, t, c: (m, e * tiles + t, 0)
    w_map = lambda e, m, t, c: (e, 0, 0)
    grid_spec = pltpu.PrefetchScalarGridSpec(
        num_scalar_prefetch=1,
        grid=(E, micro, tiles),
        in_specs=[
            pl.BlockSpec((1, TILE_B, D), row_map),
            pl.BlockSpec((1, TILE_B, D), row_map),
            pl.BlockSpec((1, TILE_B, F), row_map),
            pl.BlockSpec((1, TILE_B, F), row_map),
            pl.BlockSpec((1, D, F), w_map),
            pl.BlockSpec((1, F, D), w_map),
        ],
        out_specs=[
            pl.BlockSpec((1, TILE_B, 2 * D), row_map),
            pl.BlockSpec((1, D, F), w_map),
            pl.BlockSpec((1, F, D), w_map),
            pl.BlockSpec((1, 1, F), w_map),
            pl.BlockSpec((1, 1, D), w_map),
        ],
        scratch_shapes=[pltpu.VMEM((D, F), F32), pltpu.VMEM((F, D), F32)],
    )
    work = micro * rows
    return pl.pallas_call(
        functools.partial(ffn_bwd_kernel, micro),
        grid_spec=grid_spec,
        out_shape=[
            jax.ShapeDtypeStruct((micro, rows, 2 * D), BF16),
            jax.ShapeDtypeStruct((E, D, F), BF16),
            jax.ShapeDtypeStruct((E, F, D), BF16),
            jax.ShapeDtypeStruct((E, 1, F), F32),
            jax.ShapeDtypeStruct((E, 1, D), F32),
        ],
        compiler_params=pltpu.CompilerParams(vmem_limit_bytes=60 * 1024 * 1024),
        cost_estimate=pl.CostEstimate(
            flops=8 * work * D * F // 2, bytes_accessed=work * (8 * D + 6 * F) // 2 + 16 * E * D * F, transcendentals=2 * work * F // 2
        ),
    )(counts, d_expert, table_in, hp, h, w1, w2)

def layer_norm(value, gain, shift):
    center = value - jnp.mean(value, -1, keepdims=True)
    spread = jnp.mean(center * center, -1, keepdims=True)
    return center * lax.rsqrt(spread + 1e-06) * gain + shift


def gelu_exact(value):
    return jax.nn.gelu(value, approximate=False)


def split_heads(part):
    return part.reshape(-1, S, HEADS, HEAD_DIM)


def dot(a, b):
    return jnp.dot(a, b, preferred_element_type=F32)


def assign_places(route):
    chosen = jnp.concatenate([route[:, :, 0], route[:, :, 1]], 1)
    hits = (chosen[:, :, None] == jnp.arange(E, dtype=jnp.int32)).astype(jnp.int32)
    before = jnp.cumsum(hits, 1) - hits
    slot = jnp.sum(before * hits, 2)
    return chosen * CAPP + slot, jnp.sum(hits, 1)


def hi_lo(v):
    hi = v.astype(BF16)
    lo = (v - hi.astype(F32)).astype(BF16)
    return jnp.concatenate([hi, lo], -1)


def pick_rows(onehot, split):
    both = jnp.einsum("mnr,mrd->mnd", onehot, split, preferred_element_type=F32)
    return both[..., :D] + both[..., D:]


def pack_dense(qkv_w, out_w, router_w, vectors, up_bias):
    rows = qkv_w.shape[0]
    ub = up_bias.reshape(E, rows, 4).transpose(1, 0, 2).reshape(rows, E * 4)
    return jnp.concatenate([qkv_w, out_w, router_w, vectors.T, ub], 1)


def unpack_dense(packed):
    rows = packed.shape[0]
    w_qkv = packed[:, : 3 * D]
    w_out = packed[:, 3 * D : 4 * D]
    w_router = packed[:, 4 * D : 4 * D + E]
    table = packed[:, 4 * D + E : 4 * D + E + NV].T
    ub = packed[:, 4 * D + E + NV :].reshape(rows, E, 4).transpose(1, 0, 2).reshape(E, rows * 4)
    return w_qkv, w_out, w_router, table, ub


def attention_fwd(w_qkv, w_out, table, value):
    rows = value.shape[0]
    scale = HEAD_DIM ** (-0.5)
    first = layer_norm(value, table[0], table[1]).astype(BF16)
    qkv_bias = jnp.concatenate([table[2], jnp.zeros((D,), F32), table[3]])
    qkv = (dot(first, w_qkv) + qkv_bias).astype(BF16)
    query, key_part, val_part = (
        split_heads(qkv[:, :D]),
        split_heads(qkv[:, D : 2 * D]),
        split_heads(qkv[:, 2 * D :]),
    )
    scores = jnp.einsum("bqhd,bkhd->bhqk", query, key_part, preferred_element_type=F32) * scale
    peak = jnp.max(scores, -1, keepdims=True)
    expo = jnp.exp(scores - peak)
    total = jnp.sum(expo, -1, keepdims=True)
    probs_att = (expo / total).astype(BF16)
    log_total = peak + jnp.log(total)
    attended = jnp.einsum("bhqk,bkhd->bqhd", probs_att, val_part, preferred_element_type=F32)
    attended = attended.reshape(rows, D).astype(BF16)
    resid = value + (dot(attended, w_out) + table[4])
    return first, qkv, log_total, attended, resid


def attention_bwd(w_qkv, w_out, table, value, first, qkv, log_total, attended, d_resid):
    rows = value.shape[0]
    scale = HEAD_DIM ** (-0.5)
    d_branch = d_resid.astype(BF16)
    g_bias_out = jnp.sum(d_branch.astype(F32), 0)
    g_out = lax.dot_general(attended, d_branch, (((0,), (0,)), ((), ())), preferred_element_type=F32)
    d_att = split_heads(
        lax.dot_general(d_branch, w_out, (((1,), (1,)), ((), ())), preferred_element_type=F32).astype(BF16)
    )
    query, key_part, val_part = (
        split_heads(qkv[:, :D]),
        split_heads(qkv[:, D : 2 * D]),
        split_heads(qkv[:, 2 * D :]),
    )
    scores = jnp.einsum("bqhd,bkhd->bhqk", query, key_part, preferred_element_type=F32) * scale
    probs_f = jnp.exp(scores - log_total)
    probs_att = probs_f.astype(BF16)
    d_val = jnp.einsum("bhqk,bqhd->bkhd", probs_att, d_att, preferred_element_type=F32)
    d_prob = jnp.einsum("bqhd,bkhd->bhqk", d_att, val_part, preferred_element_type=F32)
    d_score = (probs_f * (d_prob - jnp.sum(d_prob * probs_f, -1, keepdims=True))).astype(BF16)
    d_query = jnp.einsum("bhqk,bkhd->bqhd", d_score, key_part, preferred_element_type=F32) * scale
    d_key = jnp.einsum("bhqk,bqhd->bkhd", d_score, query, preferred_element_type=F32) * scale
    d_qkv = jnp.concatenate(
        [d_query.reshape(rows, D), d_key.reshape(rows, D), d_val.reshape(rows, D)], 1
    ).astype(BF16)
    d_qkv_f = d_qkv.astype(F32)
    g_bias_q = jnp.sum(d_qkv_f[:, :D], 0)
    g_bias_v = jnp.sum(d_qkv_f[:, 2 * D :], 0)
    g_qkv = lax.dot_general(first, d_qkv, (((0,), (0,)), ((), ())), preferred_element_type=F32)
    d_first = lax.dot_general(d_qkv, w_qkv, (((1,), (1,)), ((), ())), preferred_element_type=F32)
    first_pull = jax.vjp(layer_norm, value, table[0], table[1])[1]
    d_input, g_gain_one, g_shift_one = first_pull(d_first)
    return (g_qkv, g_out, g_bias_out, g_bias_q, g_bias_v, g_gain_one, g_shift_one), d_input


def adamw(weight, moments, grad, rate):
    first = 0.5 * moments[0] + 0.5 * grad
    root = jnp.sqrt(0.5 * moments[1] * moments[1] + 0.5 * grad * grad)
    update = first / (root + 1e-08)
    which = lax.broadcasted_iota(jnp.int32, moments.shape, 0) == 0
    both = jnp.where(which, 0.5 * moments + 0.5 * grad, jnp.sqrt(0.5 * moments * moments + 0.5 * grad * grad))
    return (weight - rate * (update + 0.1 * weight), both)


def shards(
    tokens,
    cotangent,
    expert_index,
    qkv_weight,
    out_weight,
    router_weight,
    up_weight,
    up_bias,
    down_weight,
    vectors,
    qkv_moments,
    out_moments,
    router_moments,
    up_moments,
    up_bias_moments,
    down_moments,
    vector_moments,
):
    rows = tokens.shape[0]
    micro = rows // MB_TOK
    gs = qkv_weight.shape[0]
    group_size = D // gs
    core = lax.axis_index("core")

    dense_in = pack_dense(qkv_weight, out_weight, router_weight, vectors, up_bias)
    width = dense_in.shape[1]
    dense_in = jnp.pad(dense_in, ((0, 0), (0, DENSE_AG - width))).astype(BF16)
    w_up_all, w_down_all, dense = ring_all_gather(
        up_weight.astype(BF16), down_weight.astype(BF16), dense_in, group_size, 1
    )
    w_qkv, w_out, w_router, table_b, b_up_b = unpack_dense(dense[:, :width])
    table = table_b.astype(F32)
    b_up = b_up_b.astype(F32)

    value = tokens.astype(F32)
    d_out = cotangent.astype(F32)
    first, qkv, log_total, attended, resid = attention_fwd(w_qkv, w_out, table, value)
    second = layer_norm(resid, table[5], table[6]).astype(BF16)
    logits = dot(second, w_router)
    probs = jax.nn.softmax(logits, -1)
    picked = expert_index[:, :, None] == jnp.arange(E, dtype=jnp.int32)
    gate = jnp.sum(jnp.where(picked, probs[:, None, :], 0.0), -1)

    route = expert_index.reshape(micro, MB_TOK, 2)
    places, counts = assign_places(route)
    counts = counts.T.reshape(E * micro)
    onehot = (places[:, :, None] == jnp.arange(E * CAPP, dtype=jnp.int32)).astype(BF16)
    second_m = second.reshape(micro, MB_TOK, D)
    pair = jnp.concatenate([second_m, second_m], 1)
    table_in = jnp.einsum("mnr,mnd->mrd", onehot, pair, preferred_element_type=F32).astype(BF16)

    hidden_pre, hidden, y_all = ffn_forward(
        counts, table_in, w_up_all, b_up[:, None, :], w_down_all, table[7 : 7 + E][:, None, :], micro
    )
    picked_rows = pick_rows(onehot, y_all)
    out_zero = picked_rows[:, :MB_TOK].reshape(rows, D)
    out_one = picked_rows[:, MB_TOK:].reshape(rows, D)
    result = resid + (gate[:, 0:1] * out_zero + gate[:, 1:2] * out_one)

    d_gate = jnp.stack([jnp.sum(d_out * out_zero, -1), jnp.sum(d_out * out_one, -1)], 1)
    d_out_m = d_out.reshape(micro, MB_TOK, D)
    gate_m = gate.reshape(micro, MB_TOK, 2)
    weighted = jnp.concatenate([gate_m[:, :, 0:1] * d_out_m, gate_m[:, :, 1:2] * d_out_m], 1).astype(BF16)
    d_expert = jnp.einsum("mnr,mnd->mrd", onehot, weighted, preferred_element_type=F32).astype(BF16)

    d_table, g_up, g_down, g_b1, g_b2 = ffn_backward(counts, d_expert, table_in, hidden_pre, hidden, w_up_all, w_down_all, micro)
    g_up_bias_all = g_b1[:, 0, :]
    g_bias_down = g_b2[:, 0, :]

    onehot_sum = onehot[:, :MB_TOK] + onehot[:, MB_TOK:]
    d_picked = pick_rows(onehot_sum, d_table).reshape(rows, D)

    d_probs = jnp.sum(jnp.where(picked, d_gate[:, :, None], 0.0), 1)
    d_logit = (probs * (d_probs - jnp.sum(d_probs * probs, -1, keepdims=True))).astype(BF16)
    g_router = lax.dot_general(second, d_logit, (((0,), (0,)), ((), ())), preferred_element_type=F32)
    d_second = d_picked + lax.dot_general(d_logit, w_router, (((1,), (1,)), ((), ())), preferred_element_type=F32)
    norm_pull = jax.vjp(layer_norm, resid, table[5], table[6])[1]
    d_resid, g_gain_two, g_shift_two = norm_pull(d_second)
    d_resid = d_out + d_resid

    att_grads, d_input = attention_bwd(w_qkv, w_out, table, value, first, qkv, log_total, attended, d_resid)
    g_qkv, g_out, g_bias_out, g_bias_q, g_bias_v, g_gain_one, g_shift_one = att_grads
    input_grad = d_resid + d_input

    g_table = jnp.concatenate(
        [
            jnp.stack([g_gain_one, g_shift_one, g_bias_q, g_bias_v, g_bias_out, g_gain_two, g_shift_two]),
            g_bias_down,
        ],
        0,
    )
    dense_g = pack_dense(g_qkv, g_out, g_router, g_table, g_up_bias_all)
    width = dense_g.shape[1]
    dense_g = jnp.pad(dense_g, ((0, 0), (0, DENSE_AG - width))).astype(BF16)
    x_pair = lax.axis_size("rx") == 2
    r_up, r_down, r_dense = grad_reduce(g_up, g_down, dense_g, group_size, x_pair, 0)
    if not x_pair:
        r_up, r_down, r_dense = lax.psum((r_up, r_down, r_dense), "rx")
    r_qkv, r_out, r_router, r_table, r_ub = unpack_dense(r_dense[:, :width])

    reduced = (r_qkv, r_out, r_router, r_up, r_ub, r_down, r_table)
    rates = (
        2.0 * D ** (-0.5),
        2.0 * (D // 32) ** (-0.5),
        2.0 * (2 * D) ** (-0.5),
        2.0 * D ** (-0.5),
        0.2,
        2.0 * (F // 16) ** (-0.5),
        0.2,
    )
    params = (qkv_weight, out_weight, router_weight, up_weight, up_bias, down_weight, vectors)
    moments = (qkv_moments, out_moments, router_moments, up_moments, up_bias_moments, down_moments, vector_moments)
    news = []
    states = []
    for weight, state, grad, rate in zip(params, moments, reduced, rates):
        new_weight, new_state = adamw(weight, state, grad, rate)
        news.append(new_weight)
        states.append(new_state)
    return (result.astype(BF16), input_grad) + reduced + tuple(news) + tuple(states)


def solution(mesh):
    replica, group = mesh.shape["replica"], mesh.shape["group"]
    view = Mesh(np.asarray(mesh.devices).reshape(replica // 2, 2, group), ("rx", "core", "group"))
    in_specs = (
        P(TOK, None),
        P(TOK, None),
        P(TOK, None),
        P("group", None),
        P("group", None),
        P("group", None),
        P(None, "group", None),
        P(None, "group"),
        P(None, "group", None),
        P(None, "group"),
        P(None, "group", None),
        P(None, "group", None),
        P(None, "group", None),
        P(None, None, "group", None),
        P(None, None, "group"),
        P(None, None, "group", None),
        P(None, None, "group"),
    )
    out_specs = (
        P(TOK, None),
        P(TOK, None),
        P("group", None),
        P("group", None),
        P("group", None),
        P(None, "group", None),
        P(None, "group"),
        P(None, "group", None),
        P(None, "group"),
        P("group", None),
        P("group", None),
        P("group", None),
        P(None, "group", None),
        P(None, "group"),
        P(None, "group", None),
        P(None, "group"),
        P(None, "group", None),
        P(None, "group", None),
        P(None, "group", None),
        P(None, None, "group", None),
        P(None, None, "group"),
        P(None, None, "group", None),
        P(None, None, "group"),
    )
    return jax.shard_map(shards, mesh=view, in_specs=in_specs, out_specs=out_specs, check_vma=False)
```

```python
import functools

import jax
import jax.numpy as jnp
import numpy as np
from jax import lax
from jax.sharding import Mesh
from jax.sharding import PartitionSpec as P
from jax.experimental import pallas as pl
from jax.experimental.pallas import tpu as pltpu

D = 512
HEADS = 8
HEAD_DIM = 64
F = 2048
E = 4
S = 197
MB_TOK = 394
CAP = 392
NV = 11
DENSE_AG = 2560
DENSE_PAD = 2304
F32 = jnp.float32
BF16 = jnp.bfloat16
TOK = ("rx", "core", "group")


MESH_ID = pl.DeviceIdType.MESH


def ring_order(groups):
    if groups in (4, 8):
        zs = groups // 2

        def pos_of(g):
            y = g % 2
            z = g // 2
            return z + y * (2 * zs - 1 - 2 * z)

        def dev_at(p):
            p = p % groups
            yy = p // zs
            return 2 * (p + yy * (2 * zs - 1 - 2 * p)) + yy

        return pos_of, dev_at
    return (lambda g: g), (lambda p: p % groups)


def ring_rs_kernel(groups, n_in, *refs):
    ins = refs[:n_in]
    outs = refs[n_in : 2 * n_in]
    rbufs = refs[2 * n_in : 3 * n_in]
    sbufs = refs[3 * n_in : 4 * n_in]
    owns = refs[4 * n_in : 5 * n_in]
    send_sem, recv_sem, load_sem = refs[5 * n_in :]
    pos_of, dev_at = ring_order(groups)
    rx = lax.axis_index("rx")
    core = lax.axis_index("core")
    g = lax.axis_index("group")
    pos = pos_of(g)
    nbr = (dev_at(pos + 1), dev_at(pos + groups - 1))

    barrier = pltpu.get_barrier_semaphore()
    for n in nbr:
        pl.semaphore_signal(barrier, inc=1, device_id=(rx, core, n), device_id_type=MESH_ID)
    pl.semaphore_wait(barrier, 2)

    def block_dev(d, s):
        if d == 0:
            return dev_at(pos + 2 * groups - s - 1)
        return dev_at(pos + s + 1)

    def load(d, s, slot):
        b = block_dev(d, s)
        copies = []
        for i in range(n_in):
            rows = ins[i].shape[1] // groups
            half = ins[i].shape[2] // 2
            src = ins[i].at[:, pl.ds(pl.multiple_of(b * rows, rows), rows), pl.ds(d * half, half)]
            copies.append(pltpu.make_async_copy(src, owns[i].at[d, slot], load_sem.at[d, slot, i]))
        return copies

    def remote(d, s, i):
        return pltpu.make_async_remote_copy(
            src_ref=sbufs[i].at[d, s],
            dst_ref=rbufs[i].at[d, s],
            send_sem=send_sem.at[d, s, i],
            recv_sem=recv_sem.at[d, s, i],
            device_id=(rx, core, nbr[d]),
            device_id_type=MESH_ID,
        )

    for d in range(2):
        for c in load(d, 0, 0):
            c.start()
    sends = []
    for s in range(groups):
        slot = s % 2
        for d in range(2):
            for c in load(d, s, slot):
                c.wait()
            if s + 1 < groups:
                for c in load(d, s + 1, 1 - slot):
                    c.start()
            for i in range(n_in):
                if s > 0:
                    remote(d, s - 1, i).wait_recv()
                for a in range(ins[i].shape[0]):
                    mine = owns[i][d, slot, a].astype(F32)
                    if s > 0:
                        mine = mine + rbufs[i][d, s - 1, a].astype(F32)
                    if s < groups - 1:
                        sbufs[i][d, s, a] = mine.astype(sbufs[i].dtype)
                    else:
                        half = ins[i].shape[2] // 2
                        outs[i][a, :, pl.ds(d * half, half)] = mine.astype(outs[i].dtype)
                if s < groups - 1:
                    c = remote(d, s, i)
                    c.start()
                    sends.append(c)
    for c in sends:
        c.wait_send()


def ring_reduce_scatter(xs, groups, collective_id):
    n_in = len(xs)
    outs, rb, own = [], [], []
    flops = 0
    nbytes = 0
    for x in xs:
        a, total, c = x.shape
        rows = total // groups
        outs.append(jax.ShapeDtypeStruct((a, rows, c), x.dtype))
        rb.append(pltpu.VMEM((2, groups - 1, a, rows, c // 2), x.dtype))
        own.append(pltpu.VMEM((2, 2, a, rows, c // 2), x.dtype))
        flops += a * total * c
        nbytes += 3 * x.size * x.dtype.itemsize
    scratch = rb + rb + own + [
        pltpu.SemaphoreType.DMA((2, groups - 1, n_in)),
        pltpu.SemaphoreType.DMA((2, groups - 1, n_in)),
        pltpu.SemaphoreType.DMA((2, 2, n_in)),
    ]
    return pl.pallas_call(
        functools.partial(ring_rs_kernel, groups, n_in),
        out_shape=outs,
        in_specs=[pl.BlockSpec(memory_space=pl.ANY)] * n_in,
        out_specs=[pl.BlockSpec(memory_space=pltpu.VMEM)] * n_in,
        scratch_shapes=scratch,
        compiler_params=pltpu.CompilerParams(
            collective_id=collective_id, has_side_effects=True, vmem_limit_bytes=60 * 1024 * 1024
        ),
        cost_estimate=pl.CostEstimate(flops=flops, bytes_accessed=nbytes, transcendentals=0),
    )(*xs)


def ring_ag_kernel(groups, *refs):
    in_up, in_down, in_dense, out_up, out_down, out_dense = refs[:6]
    ring_send, ring_recv, part_send, part_recv, local_sem = refs[6:]
    pos_of, dev_at = ring_order(groups)
    rx = lax.axis_index("rx")
    core = lax.axis_index("core")
    g = lax.axis_index("group")
    other = 1 - core
    pos = pos_of(g)
    nbr = (dev_at(pos + 1), dev_at(pos + groups - 1))
    gs = in_up.shape[1]
    fs = in_down.shape[1]
    width = in_dense.shape[1] // 2

    barrier = pltpu.get_barrier_semaphore()
    for n in nbr:
        pl.semaphore_signal(barrier, inc=1, device_id=(rx, core, n), device_id_type=MESH_ID)
    pl.semaphore_signal(barrier, inc=1, device_id=(rx, other, g), device_id_type=MESH_ID)
    pl.semaphore_wait(barrier, 3)

    def items(owner):
        found = []
        for k in range(2):
            e = 2 * k + owner
            found.append((in_up.at[e], lambda b, e=e: out_up.at[e, pl.ds(pl.multiple_of(b * gs, gs), gs)], F // 2))
            found.append((in_down.at[e], lambda b, e=e: out_down.at[e, pl.ds(pl.multiple_of(b * fs, fs), fs)], D // 2))
        dense_in = in_dense.at[:, pl.ds(owner * width, width)]
        found.append(
            (dense_in, lambda b: out_dense.at[pl.ds(pl.multiple_of(b * gs, gs), gs), pl.ds(owner * width, width)], width // 2)
        )
        return found

    mine = items(core)
    theirs = items(other)
    n_items = len(mine)

    locals_ = [pltpu.make_async_copy(in_up.at[e], out_up.at[e, pl.ds(pl.multiple_of(g * gs, gs), gs)], local_sem.at[e]) for e in range(E)]
    locals_ += [
        pltpu.make_async_copy(in_down.at[e], out_down.at[e, pl.ds(pl.multiple_of(g * fs, fs), fs)], local_sem.at[E + e])
        for e in range(E)
    ]
    locals_.append(pltpu.make_async_copy(in_dense, out_dense.at[pl.ds(pl.multiple_of(g * gs, gs), gs)], local_sem.at[2 * E]))
    for c in locals_:
        c.start()

    def block_at(d, s):
        if d == 0:
            return dev_at(pos + 2 * groups - 1 - s)
        return dev_at(pos + 1 + s)

    def ring_copy(d, s, j, src_block):
        src_in, dst_of, half = mine[j]
        cols = pl.ds(d * half, half)
        if src_block is None:
            src = src_in.at[:, cols]
            dst = dst_of(g).at[:, cols]
        else:
            src = dst_of(src_block).at[:, cols]
            dst = src
        return pltpu.make_async_remote_copy(
            src_ref=src, dst_ref=dst, send_sem=ring_send.at[d, s, j], recv_sem=ring_recv.at[d, s, j],
            device_id=(rx, core, nbr[d]), device_id_type=MESH_ID,
        )

    def part_copy(d, s, j, table, block):
        _, dst_of, half = table[j]
        view = dst_of(block).at[:, pl.ds(d * half, half)]
        return pltpu.make_async_remote_copy(
            src_ref=view, dst_ref=view, send_sem=part_send.at[d, s, j], recv_sem=part_recv.at[d, s, j],
            device_id=(rx, other, g), device_id_type=MESH_ID,
        )

    sends = []
    for d in range(2):
        for j in range(n_items):
            c = ring_copy(d, 0, j, None)
            c.start()
            sends.append(c)
    for s in range(groups - 1):
        for d in range(2):
            b = block_at(d, s)
            for j in range(n_items):
                pltpu.make_async_remote_copy(
                    src_ref=mine[j][1](b).at[:, pl.ds(d * mine[j][2], mine[j][2])],
                    dst_ref=mine[j][1](b).at[:, pl.ds(d * mine[j][2], mine[j][2])],
                    send_sem=ring_send.at[d, s, j], recv_sem=ring_recv.at[d, s, j],
                    device_id=(rx, core, nbr[d]), device_id_type=MESH_ID,
                ).wait_recv()
                if s + 1 < groups - 1:
                    c = ring_copy(d, s + 1, j, b)
                    c.start()
                    sends.append(c)
                c = part_copy(d, s, j, mine, b)
                c.start()
                sends.append(c)
    for s in range(groups - 1):
        for d in range(2):
            b = block_at(d, s)
            for j in range(n_items):
                part_copy(d, s, j, theirs, b).wait_recv()
    for c in sends:
        c.wait_send()
    for c in locals_:
        c.wait()


def ring_all_gather(up_b, down_b, dense_b, groups, collective_id):
    n_items = 5
    gs = up_b.shape[1]
    shapes = [
        jax.ShapeDtypeStruct((E, gs * groups, F), BF16),
        jax.ShapeDtypeStruct((E, down_b.shape[1] * groups, D), BF16),
        jax.ShapeDtypeStruct((gs * groups, dense_b.shape[1]), BF16),
    ]
    nbytes = sum(int(np.prod(s.shape)) * 2 for s in shapes)
    return pl.pallas_call(
        functools.partial(ring_ag_kernel, groups),
        out_shape=shapes,
        in_specs=[pl.BlockSpec(memory_space=pl.ANY)] * 3,
        out_specs=[pl.BlockSpec(memory_space=pl.ANY)] * 3,
        scratch_shapes=[
            pltpu.SemaphoreType.DMA((2, groups - 1, n_items)),
            pltpu.SemaphoreType.DMA((2, groups - 1, n_items)),
            pltpu.SemaphoreType.DMA((2, groups - 1, n_items)),
            pltpu.SemaphoreType.DMA((2, groups - 1, n_items)),
            pltpu.SemaphoreType.DMA((2 * E + 1,)),
        ],
        compiler_params=pltpu.CompilerParams(collective_id=collective_id, has_side_effects=True),
        cost_estimate=pl.CostEstimate(flops=0, bytes_accessed=nbytes, transcendentals=0),
    )(up_b, down_b, dense_b)


def grad_items(gu, gd, gdense, owner, gs, fs, width):
    found = []
    for k in range(2):
        e = 2 * k + owner
        found.append((lambda b, e=e: gu.at[e, pl.ds(pl.multiple_of(b * gs, gs), gs)], F // 2))
        found.append((lambda b, e=e: gd.at[e, pl.ds(pl.multiple_of(b * fs, fs), fs)], D // 2))
    found.append((lambda b: gdense.at[pl.ds(pl.multiple_of(b * gs, gs), gs), pl.ds(owner * width, width)], width // 2))
    return found


def ring_rs2_kernel(groups, x_pair, *refs):
    gu, gd, gdense, out_up, out_down, out_dense = refs[:6]
    n_items = 5
    scr = refs[6:]
    rbuf, sbuf, pbuf, own, fin, xr, cr, xs = (scr[i * n_items : (i + 1) * n_items] for i in range(8))
    ring_send, ring_recv, part_send, part_recv, load_sem, x_send, x_recv, c_send, c_recv = scr[8 * n_items :]
    pos_of, dev_at = ring_order(groups)
    rx = lax.axis_index("rx")
    core = lax.axis_index("core")
    g = lax.axis_index("group")
    other = 1 - core
    pos = pos_of(g)
    nbr = (dev_at(pos + 1), dev_at(pos + groups - 1))
    gs = gu.shape[1] // groups
    fs = gd.shape[1] // groups
    width = gdense.shape[1] // 2
    mine = grad_items(gu, gd, gdense, core, gs, fs, width)
    theirs = grad_items(gu, gd, gdense, other, gs, fs, width)

    barrier = pltpu.get_barrier_semaphore()
    for n in nbr:
        pl.semaphore_signal(barrier, inc=1, device_id=(rx, core, n), device_id_type=MESH_ID)
    pl.semaphore_signal(barrier, inc=1, device_id=(rx, other, g), device_id_type=MESH_ID)
    count = 3
    if x_pair:
        pl.semaphore_signal(barrier, inc=1, device_id=(1 - rx, core, g), device_id_type=MESH_ID)
        count = 4
    pl.semaphore_wait(barrier, count)

    def block_at(d, s):
        if d == 0:
            return dev_at(pos + 2 * groups - 1 - s)
        return dev_at(pos + 1 + s)

    def cols(j, d):
        half = mine[j][1]
        return pl.ds(d * half, half)

    def load(d, s, slot, j):
        return pltpu.make_async_copy(mine[j][0](block_at(d, s)).at[:, cols(j, d)], own[j].at[d, slot], load_sem.at[d, slot, j])

    def part(d, s, j):
        return pltpu.make_async_remote_copy(
            src_ref=theirs[j][0](block_at(d, s)).at[:, cols(j, d)], dst_ref=pbuf[j].at[d, s],
            send_sem=part_send.at[d, s, j], recv_sem=part_recv.at[d, s, j],
            device_id=(rx, other, g), device_id_type=MESH_ID,
        )

    def ring(d, s, j):
        return pltpu.make_async_remote_copy(
            src_ref=sbuf[j].at[d, s], dst_ref=rbuf[j].at[d, s],
            send_sem=ring_send.at[d, s, j], recv_sem=ring_recv.at[d, s, j],
            device_id=(rx, core, nbr[d]), device_id_type=MESH_ID,
        )

    sends = []

    def ring_wave(items):
        for d in range(2):
            for j in items:
                load(d, 0, 0, j).start()
                c = part(d, 0, j)
                c.start()
                sends.append(c)
        for s in range(groups):
            slot = s % 2
            for d in range(2):
                for j in items:
                    load(d, s, slot, j).wait()
                    if s + 1 < groups:
                        load(d, s + 1, 1 - slot, j).start()
                        c = part(d, s + 1, j)
                        c.start()
                        sends.append(c)
                    part(d, s, j).wait_recv()
                    val = own[j][d, slot].astype(F32) + pbuf[j][d, s].astype(F32)
                    if s > 0:
                        ring(d, s - 1, j).wait_recv()
                        val = val + rbuf[j][d, s - 1].astype(F32)
                    if s < groups - 1:
                        sbuf[j][d, s] = val.astype(BF16)
                        c = ring(d, s, j)
                        c.start()
                        sends.append(c)
                    else:
                        fin[j][d] = val

    def x_start(items):
        copies = []
        for d in range(2):
            for j in items:
                xs[j][d] = fin[j][d].astype(BF16)
                c = pltpu.make_async_remote_copy(
                    src_ref=xs[j].at[d], dst_ref=xr[j].at[d], send_sem=x_send.at[d, j], recv_sem=x_recv.at[d, j],
                    device_id=(1 - rx, core, g), device_id_type=MESH_ID,
                )
                c.start()
                copies.append(c)
        sends.extend(copies)
        return copies

    def x_finish(items, copies):
        for c in copies:
            c.wait_recv()
        for d in range(2):
            for j in items:
                fin[j][d] = xs[j][d].astype(F32) + xr[j][d].astype(F32)

    def c_start(items):
        copies = []
        for d in range(2):
            for j in items:
                c = pltpu.make_async_remote_copy(
                    src_ref=fin[j].at[d], dst_ref=cr[j].at[d], send_sem=c_send.at[d, j], recv_sem=c_recv.at[d, j],
                    device_id=(rx, other, g), device_id_type=MESH_ID,
                )
                c.start()
                copies.append(c)
        return copies

    wave_a, wave_b = (0, 1, 2, 4), (3,)
    ring_wave(wave_a)
    if x_pair:
        xa = x_start(wave_a)
    ring_wave(wave_b)
    if x_pair:
        x_finish(wave_a, xa)
    c_copies = c_start(wave_a)
    if x_pair:
        x_finish(wave_b, x_start(wave_b))
    c_copies += c_start(wave_b)

    def out_items(owner):
        found = []
        for k in range(2):
            e = 2 * k + owner
            found.append(lambda d, e=e: out_up.at[e, :, pl.ds(d * (F // 2), F // 2)])
            found.append(lambda d, e=e: out_down.at[e, :, pl.ds(d * (D // 2), D // 2)])
        found.append(lambda d: out_dense.at[:, pl.ds(owner * width + d * (width // 2), width // 2)])
        return found

    mine_out = out_items(core)
    theirs_out = out_items(other)
    for d in range(2):
        for j in range(n_items):
            mine_out[j](d)[...] = fin[j][d]
    for c in c_copies:
        c.wait_recv()
    for d in range(2):
        for j in range(n_items):
            theirs_out[j](d)[...] = cr[j][d]
    for c in sends + c_copies:
        c.wait_send()


def grad_reduce(gu, gd, gdense, groups, x_pair, collective_id):
    gs = gu.shape[1] // groups
    fs = gd.shape[1] // groups
    width = gdense.shape[1] // 2
    item_shapes = [(gs, F // 2), (fs, D // 2), (gs, F // 2), (fs, D // 2), (gs, width // 2)]
    scratch = []
    for lead, dtype in (((2, groups - 1), BF16), ((2, groups - 1), BF16), ((2, groups), BF16), ((2, 2), BF16), ((2,), F32), ((2,), BF16), ((2,), F32), ((2,), BF16)):
        scratch += [pltpu.VMEM(lead + shp, dtype) for shp in item_shapes]
    scratch += [
        pltpu.SemaphoreType.DMA((2, groups - 1, 5)),
        pltpu.SemaphoreType.DMA((2, groups - 1, 5)),
        pltpu.SemaphoreType.DMA((2, groups, 5)),
        pltpu.SemaphoreType.DMA((2, groups, 5)),
        pltpu.SemaphoreType.DMA((2, 2, 5)),
        pltpu.SemaphoreType.DMA((2, 5)),
        pltpu.SemaphoreType.DMA((2, 5)),
        pltpu.SemaphoreType.DMA((2, 5)),
        pltpu.SemaphoreType.DMA((2, 5)),
    ]
    outs = [
        jax.ShapeDtypeStruct((E, gs, F), F32),
        jax.ShapeDtypeStruct((E, fs, D), F32),
        jax.ShapeDtypeStruct((gs, gdense.shape[1]), F32),
    ]
    nbytes = 2 * (gu.size + gd.size + gdense.size)
    return pl.pallas_call(
        functools.partial(ring_rs2_kernel, groups, x_pair),
        out_shape=outs,
        in_specs=[pl.BlockSpec(memory_space=pl.ANY)] * 3,
        out_specs=[pl.BlockSpec(memory_space=pltpu.VMEM)] * 3,
        scratch_shapes=scratch,
        compiler_params=pltpu.CompilerParams(
            collective_id=collective_id, has_side_effects=True, vmem_limit_bytes=62 * 1024 * 1024
        ),
        cost_estimate=pl.CostEstimate(flops=gu.size + gd.size + gdense.size, bytes_accessed=nbytes, transcendentals=0),
    )(gu, gd, gdense)


TILE = 256
TILE_B = 256
CAPP = 512
SQRT_HALF = float(np.sqrt(0.5))
INV_SQRT_2PI = float(1.0 / np.sqrt(2.0 * np.pi))


def ffn_fwd_kernel(micro, counts, x_ref, w1_ref, b1_ref, w2_ref, b2_ref, hp_ref, h_ref, y_ref):
    e, m, t = pl.program_id(0), pl.program_id(1), pl.program_id(2)
    active = t * TILE < counts[e * micro + m]

    @pl.when(active)
    def _():
        hp = jnp.dot(x_ref[0], w1_ref[0], preferred_element_type=F32) + b1_ref[0]
        cdf = 0.5 * (1.0 + lax.erf(hp * SQRT_HALF))
        h = (hp * cdf).astype(BF16)
        hp_ref[0] = cdf + hp * jnp.exp(-0.5 * hp * hp) * INV_SQRT_2PI
        h_ref[0] = h
        y = jnp.dot(h, w2_ref[0], preferred_element_type=F32) + b2_ref[0]
        hi = y.astype(BF16)
        y_ref[0, :, :D] = hi
        y_ref[0, :, D:] = (y - hi.astype(F32)).astype(BF16)

    @pl.when(jnp.logical_not(active))
    def _():
        y_ref[0] = jnp.zeros(y_ref.shape[1:], BF16)


def ffn_forward(counts, table_in, w1, b1, w2, b2, micro):
    tiles = CAPP // TILE
    rows = table_in.shape[1]
    row_map = lambda e, m, t, c: (m, e * tiles + t, 0)
    w_map = lambda e, m, t, c: (e, 0, 0)
    grid_spec = pltpu.PrefetchScalarGridSpec(
        num_scalar_prefetch=1,
        grid=(E, micro, tiles),
        in_specs=[
            pl.BlockSpec((1, TILE, D), row_map),
            pl.BlockSpec((1, D, F), w_map),
            pl.BlockSpec((1, 1, F), w_map),
            pl.BlockSpec((1, F, D), w_map),
            pl.BlockSpec((1, 1, D), w_map),
        ],
        out_specs=[
            pl.BlockSpec((1, TILE, F), row_map),
            pl.BlockSpec((1, TILE, F), row_map),
            pl.BlockSpec((1, TILE, 2 * D), row_map),
        ],
    )
    work = micro * rows
    return pl.pallas_call(
        functools.partial(ffn_fwd_kernel, micro),
        grid_spec=grid_spec,
        out_shape=[
            jax.ShapeDtypeStruct((micro, rows, F), F32),
            jax.ShapeDtypeStruct((micro, rows, F), BF16),
            jax.ShapeDtypeStruct((micro, rows, 2 * D), BF16),
        ],
        compiler_params=pltpu.CompilerParams(vmem_limit_bytes=48 * 1024 * 1024),
        cost_estimate=pl.CostEstimate(
            flops=4 * work * D * F // 2, bytes_accessed=work * (2 * D + 6 * F + 4 * D) // 2, transcendentals=work * F // 2
        ),
    )(counts, table_in, w1, b1, w2, b2)


def ffn_bwd_kernel(micro, counts, dy_ref, x_ref, hp_ref, h_ref, w1_ref, w2_ref, dt_ref, gu_ref, gd_ref, gb_ref, gb2_ref, gu_acc, gd_acc):
    e, m, t = pl.program_id(0), pl.program_id(1), pl.program_id(2)
    active = t * TILE_B < counts[e * micro + m]

    @pl.when((m == 0) & (t == 0))
    def _():
        gu_acc[...] = jnp.zeros(gu_acc.shape, F32)
        gd_acc[...] = jnp.zeros(gd_acc.shape, F32)
        gb_ref[...] = jnp.zeros(gb_ref.shape, F32)
        gb2_ref[...] = jnp.zeros(gb2_ref.shape, F32)

    @pl.when(active)
    def _():
        dy = dy_ref[0]
        d_hidden = lax.dot_general(dy, w2_ref[0], (((1,), (1,)), ((), ())), preferred_element_type=F32)
        d_pre = (d_hidden * hp_ref[0]).astype(BF16)
        dt = lax.dot_general(d_pre, w1_ref[0], (((1,), (1,)), ((), ())), preferred_element_type=F32)
        hi = dt.astype(BF16)
        dt_ref[0, :, :D] = hi
        dt_ref[0, :, D:] = (dt - hi.astype(F32)).astype(BF16)
        gb2_ref[0] += jnp.sum(dy.astype(F32), 0, keepdims=True)
        gu_acc[...] += lax.dot_general(x_ref[0], d_pre, (((0,), (0,)), ((), ())), preferred_element_type=F32)
        gd_acc[...] += lax.dot_general(h_ref[0], dy, (((0,), (0,)), ((), ())), preferred_element_type=F32)
        gb_ref[0] += jnp.sum(d_pre.astype(F32), 0, keepdims=True)

    @pl.when(jnp.logical_not(active))
    def _():
        dt_ref[0] = jnp.zeros(dt_ref.shape[1:], BF16)

    @pl.when((m == micro - 1) & (t == pl.num_programs(2) - 1))
    def _():
        gu_ref[0] = gu_acc[...].astype(BF16)
        gd_ref[0] = gd_acc[...].astype(BF16)


def ffn_backward(counts, d_expert, table_in, hp, h, w1, w2, micro):
    tiles = CAPP // TILE_B
    rows = table_in.shape[1]
    row_map = lambda e, m, t, c: (m, e * tiles + t, 0)
    w_map = lambda e, m, t, c: (e, 0, 0)
    grid_spec = pltpu.PrefetchScalarGridSpec(
        num_scalar_prefetch=1,
        grid=(E, micro, tiles),
        in_specs=[
            pl.BlockSpec((1, TILE_B, D), row_map),
            pl.BlockSpec((1, TILE_B, D), row_map),
            pl.BlockSpec((1, TILE_B, F), row_map),
            pl.BlockSpec((1, TILE_B, F), row_map),
            pl.BlockSpec((1, D, F), w_map),
            pl.BlockSpec((1, F, D), w_map),
        ],
        out_specs=[
            pl.BlockSpec((1, TILE_B, 2 * D), row_map),
            pl.BlockSpec((1, D, F), w_map),
            pl.BlockSpec((1, F, D), w_map),
            pl.BlockSpec((1, 1, F), w_map),
            pl.BlockSpec((1, 1, D), w_map),
        ],
        scratch_shapes=[pltpu.VMEM((D, F), F32), pltpu.VMEM((F, D), F32)],
    )
    work = micro * rows
    return pl.pallas_call(
        functools.partial(ffn_bwd_kernel, micro),
        grid_spec=grid_spec,
        out_shape=[
            jax.ShapeDtypeStruct((micro, rows, 2 * D), BF16),
            jax.ShapeDtypeStruct((E, D, F), BF16),
            jax.ShapeDtypeStruct((E, F, D), BF16),
            jax.ShapeDtypeStruct((E, 1, F), F32),
            jax.ShapeDtypeStruct((E, 1, D), F32),
        ],
        compiler_params=pltpu.CompilerParams(vmem_limit_bytes=60 * 1024 * 1024),
        cost_estimate=pl.CostEstimate(
            flops=8 * work * D * F // 2, bytes_accessed=work * (8 * D + 6 * F) // 2 + 16 * E * D * F, transcendentals=2 * work * F // 2
        ),
    )(counts, d_expert, table_in, hp, h, w1, w2)

def layer_norm(value, gain, shift):
    center = value - jnp.mean(value, -1, keepdims=True)
    spread = jnp.mean(center * center, -1, keepdims=True)
    return center * lax.rsqrt(spread + 1e-06) * gain + shift


def gelu_exact(value):
    return jax.nn.gelu(value, approximate=False)


def split_heads(part):
    return part.reshape(-1, S, HEADS, HEAD_DIM)


def dot(a, b):
    return jnp.dot(a, b, preferred_element_type=F32)


def assign_places(route):
    chosen = jnp.concatenate([route[:, :, 0], route[:, :, 1]], 1)
    hits = (chosen[:, :, None] == jnp.arange(E, dtype=jnp.int32)).astype(jnp.int32)
    before = jnp.cumsum(hits, 1) - hits
    slot = jnp.sum(before * hits, 2)
    return chosen * CAPP + slot, jnp.sum(hits, 1)


def hi_lo(v):
    hi = v.astype(BF16)
    lo = (v - hi.astype(F32)).astype(BF16)
    return jnp.concatenate([hi, lo], -1)


def pick_rows(onehot, split):
    both = jnp.einsum("mnr,mrd->mnd", onehot, split, preferred_element_type=F32)
    return both[..., :D] + both[..., D:]


def pack_dense(qkv_w, out_w, router_w, vectors, up_bias):
    rows = qkv_w.shape[0]
    ub = up_bias.reshape(E, rows, 4).transpose(1, 0, 2).reshape(rows, E * 4)
    return jnp.concatenate([qkv_w, out_w, router_w, vectors.T, ub], 1)


def unpack_dense(packed):
    rows = packed.shape[0]
    w_qkv = packed[:, : 3 * D]
    w_out = packed[:, 3 * D : 4 * D]
    w_router = packed[:, 4 * D : 4 * D + E]
    table = packed[:, 4 * D + E : 4 * D + E + NV].T
    ub = packed[:, 4 * D + E + NV :].reshape(rows, E, 4).transpose(1, 0, 2).reshape(E, rows * 4)
    return w_qkv, w_out, w_router, table, ub


def attention_fwd(w_qkv, w_out, table, value):
    rows = value.shape[0]
    scale = HEAD_DIM ** (-0.5)
    first = layer_norm(value, table[0], table[1]).astype(BF16)
    qkv_bias = jnp.concatenate([table[2], jnp.zeros((D,), F32), table[3]])
    qkv = (dot(first, w_qkv) + qkv_bias).astype(BF16)
    query, key_part, val_part = (
        split_heads(qkv[:, :D]),
        split_heads(qkv[:, D : 2 * D]),
        split_heads(qkv[:, 2 * D :]),
    )
    scores = jnp.einsum("bqhd,bkhd->bhqk", query, key_part, preferred_element_type=F32) * scale
    peak = jnp.max(scores, -1, keepdims=True)
    expo = jnp.exp(scores - peak)
    total = jnp.sum(expo, -1, keepdims=True)
    probs_att = (expo / total).astype(BF16)
    log_total = peak + jnp.log(total)
    attended = jnp.einsum("bhqk,bkhd->bqhd", probs_att, val_part, preferred_element_type=F32)
    attended = attended.reshape(rows, D).astype(BF16)
    resid = value + (dot(attended, w_out) + table[4])
    return first, qkv, log_total, attended, resid


def attention_bwd(w_qkv, w_out, table, value, first, qkv, log_total, attended, d_resid):
    rows = value.shape[0]
    scale = HEAD_DIM ** (-0.5)
    d_branch = d_resid.astype(BF16)
    g_bias_out = jnp.sum(d_branch.astype(F32), 0)
    g_out = lax.dot_general(attended, d_branch, (((0,), (0,)), ((), ())), preferred_element_type=F32)
    d_att = split_heads(
        lax.dot_general(d_branch, w_out, (((1,), (1,)), ((), ())), preferred_element_type=F32).astype(BF16)
    )
    query, key_part, val_part = (
        split_heads(qkv[:, :D]),
        split_heads(qkv[:, D : 2 * D]),
        split_heads(qkv[:, 2 * D :]),
    )
    scores = jnp.einsum("bqhd,bkhd->bhqk", query, key_part, preferred_element_type=F32) * scale
    probs_f = jnp.exp(scores - log_total)
    probs_att = probs_f.astype(BF16)
    d_val = jnp.einsum("bhqk,bqhd->bkhd", probs_att, d_att, preferred_element_type=F32)
    d_prob = jnp.einsum("bqhd,bkhd->bhqk", d_att, val_part, preferred_element_type=F32)
    d_score = (probs_f * (d_prob - jnp.sum(d_prob * probs_f, -1, keepdims=True))).astype(BF16)
    d_query = jnp.einsum("bhqk,bkhd->bqhd", d_score, key_part, preferred_element_type=F32) * scale
    d_key = jnp.einsum("bhqk,bqhd->bkhd", d_score, query, preferred_element_type=F32) * scale
    d_qkv = jnp.concatenate(
        [d_query.reshape(rows, D), d_key.reshape(rows, D), d_val.reshape(rows, D)], 1
    ).astype(BF16)
    d_qkv_f = d_qkv.astype(F32)
    g_bias_q = jnp.sum(d_qkv_f[:, :D], 0)
    g_bias_v = jnp.sum(d_qkv_f[:, 2 * D :], 0)
    g_qkv = lax.dot_general(first, d_qkv, (((0,), (0,)), ((), ())), preferred_element_type=F32)
    d_first = lax.dot_general(d_qkv, w_qkv, (((1,), (1,)), ((), ())), preferred_element_type=F32)
    first_pull = jax.vjp(layer_norm, value, table[0], table[1])[1]
    d_input, g_gain_one, g_shift_one = first_pull(d_first)
    return (g_qkv, g_out, g_bias_out, g_bias_q, g_bias_v, g_gain_one, g_shift_one), d_input


def adamw(weight, moments, grad, rate):
    first = 0.5 * moments[0] + 0.5 * grad
    root = jnp.sqrt(0.5 * moments[1] * moments[1] + 0.5 * grad * grad)
    update = first / (root + 1e-08)
    which = lax.broadcasted_iota(jnp.int32, moments.shape, 0) == 0
    both = jnp.where(which, 0.5 * moments + 0.5 * grad, jnp.sqrt(0.5 * moments * moments + 0.5 * grad * grad))
    return (weight - rate * (update + 0.1 * weight), both)


def shards(
    tokens,
    cotangent,
    expert_index,
    qkv_weight,
    out_weight,
    router_weight,
    up_weight,
    up_bias,
    down_weight,
    vectors,
    qkv_moments,
    out_moments,
    router_moments,
    up_moments,
    up_bias_moments,
    down_moments,
    vector_moments,
):
    rows = tokens.shape[0]
    micro = rows // MB_TOK
    gs = qkv_weight.shape[0]
    group_size = D // gs
    core = lax.axis_index("core")

    dense_in = pack_dense(qkv_weight, out_weight, router_weight, vectors, up_bias)
    width = dense_in.shape[1]
    dense_in = jnp.pad(dense_in, ((0, 0), (0, DENSE_AG - width))).astype(BF16)
    w_up_all, w_down_all, dense = ring_all_gather(
        up_weight.astype(BF16), down_weight.astype(BF16), dense_in, group_size, 1
    )
    w_qkv, w_out, w_router, table_b, b_up_b = unpack_dense(dense[:, :width])
    table = table_b.astype(F32)
    b_up = b_up_b.astype(F32)

    value = tokens.astype(F32)
    d_out = cotangent.astype(F32)
    first, qkv, log_total, attended, resid = attention_fwd(w_qkv, w_out, table, value)
    second = layer_norm(resid, table[5], table[6]).astype(BF16)
    logits = dot(second, w_router)
    probs = jax.nn.softmax(logits, -1)
    picked = expert_index[:, :, None] == jnp.arange(E, dtype=jnp.int32)
    gate = jnp.sum(jnp.where(picked, probs[:, None, :], 0.0), -1)

    route = expert_index.reshape(micro, MB_TOK, 2)
    places, counts = assign_places(route)
    counts = counts.T.reshape(E * micro)
    onehot = (places[:, :, None] == jnp.arange(E * CAPP, dtype=jnp.int32)).astype(BF16)
    second_m = second.reshape(micro, MB_TOK, D)
    pair = jnp.concatenate([second_m, second_m], 1)
    table_in = jnp.einsum("mnr,mnd->mrd", onehot, pair, preferred_element_type=F32).astype(BF16)

    hidden_pre, hidden, y_all = ffn_forward(
        counts, table_in, w_up_all, b_up[:, None, :], w_down_all, table[7 : 7 + E][:, None, :], micro
    )
    picked_rows = pick_rows(onehot, y_all)
    out_zero = picked_rows[:, :MB_TOK].reshape(rows, D)
    out_one = picked_rows[:, MB_TOK:].reshape(rows, D)
    result = resid + (gate[:, 0:1] * out_zero + gate[:, 1:2] * out_one)

    d_gate = jnp.stack([jnp.sum(d_out * out_zero, -1), jnp.sum(d_out * out_one, -1)], 1)
    d_out_m = d_out.reshape(micro, MB_TOK, D)
    gate_m = gate.reshape(micro, MB_TOK, 2)
    weighted = jnp.concatenate([gate_m[:, :, 0:1] * d_out_m, gate_m[:, :, 1:2] * d_out_m], 1).astype(BF16)
    d_expert = jnp.einsum("mnr,mnd->mrd", onehot, weighted, preferred_element_type=F32).astype(BF16)

    d_table, g_up, g_down, g_b1, g_b2 = ffn_backward(counts, d_expert, table_in, hidden_pre, hidden, w_up_all, w_down_all, micro)
    g_up_bias_all = g_b1[:, 0, :]
    g_bias_down = g_b2[:, 0, :]

    onehot_sum = onehot[:, :MB_TOK] + onehot[:, MB_TOK:]
    d_picked = pick_rows(onehot_sum, d_table).reshape(rows, D)

    d_probs = jnp.sum(jnp.where(picked, d_gate[:, :, None], 0.0), 1)
    d_logit = (probs * (d_probs - jnp.sum(d_probs * probs, -1, keepdims=True))).astype(BF16)
    g_router = lax.dot_general(second, d_logit, (((0,), (0,)), ((), ())), preferred_element_type=F32)
    d_second = d_picked + lax.dot_general(d_logit, w_router, (((1,), (1,)), ((), ())), preferred_element_type=F32)
    norm_pull = jax.vjp(layer_norm, resid, table[5], table[6])[1]
    d_resid, g_gain_two, g_shift_two = norm_pull(d_second)
    d_resid = d_out + d_resid

    att_grads, d_input = attention_bwd(w_qkv, w_out, table, value, first, qkv, log_total, attended, d_resid)
    g_qkv, g_out, g_bias_out, g_bias_q, g_bias_v, g_gain_one, g_shift_one = att_grads
    input_grad = d_resid + d_input

    g_table = jnp.concatenate(
        [
            jnp.stack([g_gain_one, g_shift_one, g_bias_q, g_bias_v, g_bias_out, g_gain_two, g_shift_two]),
            g_bias_down,
        ],
        0,
    )
    dense_g = pack_dense(g_qkv, g_out, g_router, g_table, g_up_bias_all)
    width = dense_g.shape[1]
    dense_g = jnp.pad(dense_g, ((0, 0), (0, DENSE_AG - width))).astype(BF16)
    x_pair = lax.axis_size("rx") == 2
    r_up, r_down, r_dense = grad_reduce(g_up, g_down, dense_g, group_size, x_pair, 0)
    if not x_pair:
        r_up, r_down, r_dense = lax.psum((r_up, r_down, r_dense), "rx")
    r_qkv, r_out, r_router, r_table, r_ub = unpack_dense(r_dense[:, :width])

    reduced = (r_qkv, r_out, r_router, r_up, r_ub, r_down, r_table)
    rates = (
        2.0 * D ** (-0.5),
        2.0 * (D // 32) ** (-0.5),
        2.0 * (2 * D) ** (-0.5),
        2.0 * D ** (-0.5),
        0.2,
        2.0 * (F // 16) ** (-0.5),
        0.2,
    )
    params = (qkv_weight, out_weight, router_weight, up_weight, up_bias, down_weight, vectors)
    moments = (qkv_moments, out_moments, router_moments, up_moments, up_bias_moments, down_moments, vector_moments)
    news = []
    states = []
    for weight, state, grad, rate in zip(params, moments, reduced, rates):
        new_weight, new_state = adamw(weight, state, grad, rate)
        news.append(new_weight)
        states.append(new_state)
    return (result.astype(BF16), input_grad) + reduced + tuple(news) + tuple(states)


def solution(mesh):
    replica, group = mesh.shape["replica"], mesh.shape["group"]
    view = Mesh(np.asarray(mesh.devices).reshape(replica // 2, 2, group), ("rx", "core", "group"))
    in_specs = (
        P(TOK, None),
        P(TOK, None),
        P(TOK, None),
        P("group", None),
        P("group", None),
        P("group", None),
        P(None, "group", None),
        P(None, "group"),
        P(None, "group", None),
        P(None, "group"),
        P(None, "group", None),
        P(None, "group", None),
        P(None, "group", None),
        P(None, None, "group", None),
        P(None, None, "group"),
        P(None, None, "group", None),
        P(None, None, "group"),
    )
    out_specs = (
        P(TOK, None),
        P(TOK, None),
        P("group", None),
        P("group", None),
        P("group", None),
        P(None, "group", None),
        P(None, "group"),
        P(None, "group", None),
        P(None, "group"),
        P("group", None),
        P("group", None),
        P("group", None),
        P(None, "group", None),
        P(None, "group"),
        P(None, "group", None),
        P(None, "group"),
        P(None, "group", None),
        P(None, "group", None),
        P(None, "group", None),
        P(None, None, "group", None),
        P(None, None, "group"),
        P(None, None, "group", None),
        P(None, None, "group"),
    )
    return jax.shard_map(shards, mesh=view, in_specs=in_specs, out_specs=out_specs, check_vma=False)
```

```python
import functools

import jax
import jax.numpy as jnp
import numpy as np
from jax import lax
from jax.sharding import Mesh
from jax.sharding import PartitionSpec as P
from jax.experimental import pallas as pl
from jax.experimental.pallas import tpu as pltpu

D = 512
HEADS = 8
HEAD_DIM = 64
F = 2048
E = 4
S = 197
MB_TOK = 394
CAP = 392
NV = 11
DENSE_AG = 2560
DENSE_PAD = 2304
F32 = jnp.float32
BF16 = jnp.bfloat16
TOK = ("rx", "core", "group")


MESH_ID = pl.DeviceIdType.MESH


def ring_order(groups):
    if groups in (4, 8):
        zs = groups // 2

        def pos_of(g):
            y = g % 2
            z = g // 2
            return z + y * (2 * zs - 1 - 2 * z)

        def dev_at(p):
            p = p % groups
            yy = p // zs
            return 2 * (p + yy * (2 * zs - 1 - 2 * p)) + yy

        return pos_of, dev_at
    return (lambda g: g), (lambda p: p % groups)


def ring_rs_kernel(groups, n_in, *refs):
    ins = refs[:n_in]
    outs = refs[n_in : 2 * n_in]
    rbufs = refs[2 * n_in : 3 * n_in]
    sbufs = refs[3 * n_in : 4 * n_in]
    owns = refs[4 * n_in : 5 * n_in]
    send_sem, recv_sem, load_sem = refs[5 * n_in :]
    pos_of, dev_at = ring_order(groups)
    rx = lax.axis_index("rx")
    core = lax.axis_index("core")
    g = lax.axis_index("group")
    pos = pos_of(g)
    nbr = (dev_at(pos + 1), dev_at(pos + groups - 1))

    barrier = pltpu.get_barrier_semaphore()
    for n in nbr:
        pl.semaphore_signal(barrier, inc=1, device_id=(rx, core, n), device_id_type=MESH_ID)
    pl.semaphore_wait(barrier, 2)

    def block_dev(d, s):
        if d == 0:
            return dev_at(pos + 2 * groups - s - 1)
        return dev_at(pos + s + 1)

    def load(d, s, slot):
        b = block_dev(d, s)
        copies = []
        for i in range(n_in):
            rows = ins[i].shape[1] // groups
            half = ins[i].shape[2] // 2
            src = ins[i].at[:, pl.ds(pl.multiple_of(b * rows, rows), rows), pl.ds(d * half, half)]
            copies.append(pltpu.make_async_copy(src, owns[i].at[d, slot], load_sem.at[d, slot, i]))
        return copies

    def remote(d, s, i):
        return pltpu.make_async_remote_copy(
            src_ref=sbufs[i].at[d, s],
            dst_ref=rbufs[i].at[d, s],
            send_sem=send_sem.at[d, s, i],
            recv_sem=recv_sem.at[d, s, i],
            device_id=(rx, core, nbr[d]),
            device_id_type=MESH_ID,
        )

    for d in range(2):
        for c in load(d, 0, 0):
            c.start()
    sends = []
    for s in range(groups):
        slot = s % 2
        for d in range(2):
            for c in load(d, s, slot):
                c.wait()
            if s + 1 < groups:
                for c in load(d, s + 1, 1 - slot):
                    c.start()
            for i in range(n_in):
                if s > 0:
                    remote(d, s - 1, i).wait_recv()
                for a in range(ins[i].shape[0]):
                    mine = owns[i][d, slot, a].astype(F32)
                    if s > 0:
                        mine = mine + rbufs[i][d, s - 1, a].astype(F32)
                    if s < groups - 1:
                        sbufs[i][d, s, a] = mine.astype(sbufs[i].dtype)
                    else:
                        half = ins[i].shape[2] // 2
                        outs[i][a, :, pl.ds(d * half, half)] = mine.astype(outs[i].dtype)
                if s < groups - 1:
                    c = remote(d, s, i)
                    c.start()
                    sends.append(c)
    for c in sends:
        c.wait_send()


def ring_reduce_scatter(xs, groups, collective_id):
    n_in = len(xs)
    outs, rb, own = [], [], []
    flops = 0
    nbytes = 0
    for x in xs:
        a, total, c = x.shape
        rows = total // groups
        outs.append(jax.ShapeDtypeStruct((a, rows, c), x.dtype))
        rb.append(pltpu.VMEM((2, groups - 1, a, rows, c // 2), x.dtype))
        own.append(pltpu.VMEM((2, 2, a, rows, c // 2), x.dtype))
        flops += a * total * c
        nbytes += 3 * x.size * x.dtype.itemsize
    scratch = rb + rb + own + [
        pltpu.SemaphoreType.DMA((2, groups - 1, n_in)),
        pltpu.SemaphoreType.DMA((2, groups - 1, n_in)),
        pltpu.SemaphoreType.DMA((2, 2, n_in)),
    ]
    return pl.pallas_call(
        functools.partial(ring_rs_kernel, groups, n_in),
        out_shape=outs,
        in_specs=[pl.BlockSpec(memory_space=pl.ANY)] * n_in,
        out_specs=[pl.BlockSpec(memory_space=pltpu.VMEM)] * n_in,
        scratch_shapes=scratch,
        compiler_params=pltpu.CompilerParams(
            collective_id=collective_id, has_side_effects=True, vmem_limit_bytes=60 * 1024 * 1024
        ),
        cost_estimate=pl.CostEstimate(flops=flops, bytes_accessed=nbytes, transcendentals=0),
    )(*xs)


def ring_ag_kernel(groups, *refs):
    in_up, in_down, in_dense, out_up, out_down, out_dense = refs[:6]
    ring_send, ring_recv, part_send, part_recv, local_sem = refs[6:]
    pos_of, dev_at = ring_order(groups)
    rx = lax.axis_index("rx")
    core = lax.axis_index("core")
    g = lax.axis_index("group")
    other = 1 - core
    pos = pos_of(g)
    nbr = (dev_at(pos + 1), dev_at(pos + groups - 1))
    gs = in_up.shape[1]
    fs = in_down.shape[1]
    width = in_dense.shape[1] // 2

    barrier = pltpu.get_barrier_semaphore()
    for n in nbr:
        pl.semaphore_signal(barrier, inc=1, device_id=(rx, core, n), device_id_type=MESH_ID)
    pl.semaphore_signal(barrier, inc=1, device_id=(rx, other, g), device_id_type=MESH_ID)
    pl.semaphore_wait(barrier, 3)

    def items(owner):
        found = []
        for k in range(2):
            e = 2 * k + owner
            found.append((in_up.at[e], lambda b, e=e: out_up.at[e, pl.ds(pl.multiple_of(b * gs, gs), gs)], F // 2))
            found.append((in_down.at[e], lambda b, e=e: out_down.at[e, pl.ds(pl.multiple_of(b * fs, fs), fs)], D // 2))
        dense_in = in_dense.at[:, pl.ds(owner * width, width)]
        found.append(
            (dense_in, lambda b: out_dense.at[pl.ds(pl.multiple_of(b * gs, gs), gs), pl.ds(owner * width, width)], width // 2)
        )
        return found

    mine = items(core)
    theirs = items(other)
    n_items = len(mine)

    locals_ = [pltpu.make_async_copy(in_up.at[e], out_up.at[e, pl.ds(pl.multiple_of(g * gs, gs), gs)], local_sem.at[e]) for e in range(E)]
    locals_ += [
        pltpu.make_async_copy(in_down.at[e], out_down.at[e, pl.ds(pl.multiple_of(g * fs, fs), fs)], local_sem.at[E + e])
        for e in range(E)
    ]
    locals_.append(pltpu.make_async_copy(in_dense, out_dense.at[pl.ds(pl.multiple_of(g * gs, gs), gs)], local_sem.at[2 * E]))
    for c in locals_:
        c.start()

    def block_at(d, s):
        if d == 0:
            return dev_at(pos + 2 * groups - 1 - s)
        return dev_at(pos + 1 + s)

    def ring_copy(d, s, j, src_block):
        src_in, dst_of, half = mine[j]
        cols = pl.ds(d * half, half)
        if src_block is None:
            src = src_in.at[:, cols]
            dst = dst_of(g).at[:, cols]
        else:
            src = dst_of(src_block).at[:, cols]
            dst = src
        return pltpu.make_async_remote_copy(
            src_ref=src, dst_ref=dst, send_sem=ring_send.at[d, s, j], recv_sem=ring_recv.at[d, s, j],
            device_id=(rx, core, nbr[d]), device_id_type=MESH_ID,
        )

    def part_copy(d, s, j, table, block):
        _, dst_of, half = table[j]
        view = dst_of(block).at[:, pl.ds(d * half, half)]
        return pltpu.make_async_remote_copy(
            src_ref=view, dst_ref=view, send_sem=part_send.at[d, s, j], recv_sem=part_recv.at[d, s, j],
            device_id=(rx, other, g), device_id_type=MESH_ID,
        )

    sends = []
    for d in range(2):
        for j in range(n_items):
            c = ring_copy(d, 0, j, None)
            c.start()
            sends.append(c)
    for s in range(groups - 1):
        for d in range(2):
            b = block_at(d, s)
            for j in range(n_items):
                pltpu.make_async_remote_copy(
                    src_ref=mine[j][1](b).at[:, pl.ds(d * mine[j][2], mine[j][2])],
                    dst_ref=mine[j][1](b).at[:, pl.ds(d * mine[j][2], mine[j][2])],
                    send_sem=ring_send.at[d, s, j], recv_sem=ring_recv.at[d, s, j],
                    device_id=(rx, core, nbr[d]), device_id_type=MESH_ID,
                ).wait_recv()
                if s + 1 < groups - 1:
                    c = ring_copy(d, s + 1, j, b)
                    c.start()
                    sends.append(c)
                c = part_copy(d, s, j, mine, b)
                c.start()
                sends.append(c)
    for s in range(groups - 1):
        for d in range(2):
            b = block_at(d, s)
            for j in range(n_items):
                part_copy(d, s, j, theirs, b).wait_recv()
    for c in sends:
        c.wait_send()
    for c in locals_:
        c.wait()


def ring_all_gather(up_b, down_b, dense_b, groups, collective_id):
    n_items = 5
    gs = up_b.shape[1]
    shapes = [
        jax.ShapeDtypeStruct((E, gs * groups, F), BF16),
        jax.ShapeDtypeStruct((E, down_b.shape[1] * groups, D), BF16),
        jax.ShapeDtypeStruct((gs * groups, dense_b.shape[1]), BF16),
    ]
    nbytes = sum(int(np.prod(s.shape)) * 2 for s in shapes)
    return pl.pallas_call(
        functools.partial(ring_ag_kernel, groups),
        out_shape=shapes,
        in_specs=[pl.BlockSpec(memory_space=pl.ANY)] * 3,
        out_specs=[pl.BlockSpec(memory_space=pl.ANY)] * 3,
        scratch_shapes=[
            pltpu.SemaphoreType.DMA((2, groups - 1, n_items)),
            pltpu.SemaphoreType.DMA((2, groups - 1, n_items)),
            pltpu.SemaphoreType.DMA((2, groups - 1, n_items)),
            pltpu.SemaphoreType.DMA((2, groups - 1, n_items)),
            pltpu.SemaphoreType.DMA((2 * E + 1,)),
        ],
        compiler_params=pltpu.CompilerParams(collective_id=collective_id, has_side_effects=True),
        cost_estimate=pl.CostEstimate(flops=0, bytes_accessed=nbytes, transcendentals=0),
    )(up_b, down_b, dense_b)


def grad_items(gu, gd, gdense, owner, gs, fs, width):
    found = []
    for k in range(2):
        e = 2 * k + owner
        found.append((lambda b, e=e: gu.at[e, pl.ds(pl.multiple_of(b * gs, gs), gs)], F // 2))
        found.append((lambda b, e=e: gd.at[e, pl.ds(pl.multiple_of(b * fs, fs), fs)], D // 2))
    found.append((lambda b: gdense.at[pl.ds(pl.multiple_of(b * gs, gs), gs), pl.ds(owner * width, width)], width // 2))
    return found


def ring_rs2_kernel(groups, x_pair, *refs):
    gu, gd, gdense, out_up, out_down, out_dense = refs[:6]
    n_items = 5
    scr = refs[6:]
    rbuf, sbuf, pbuf, own, fin, xr, cr, xs = (scr[i * n_items : (i + 1) * n_items] for i in range(8))
    ring_send, ring_recv, part_send, part_recv, load_sem, x_send, x_recv, c_send, c_recv = scr[8 * n_items :]
    pos_of, dev_at = ring_order(groups)
    rx = lax.axis_index("rx")
    core = lax.axis_index("core")
    g = lax.axis_index("group")
    other = 1 - core
    pos = pos_of(g)
    nbr = (dev_at(pos + 1), dev_at(pos + groups - 1))
    gs = gu.shape[1] // groups
    fs = gd.shape[1] // groups
    width = gdense.shape[1] // 2
    mine = grad_items(gu, gd, gdense, core, gs, fs, width)
    theirs = grad_items(gu, gd, gdense, other, gs, fs, width)

    barrier = pltpu.get_barrier_semaphore()
    for n in nbr:
        pl.semaphore_signal(barrier, inc=1, device_id=(rx, core, n), device_id_type=MESH_ID)
    pl.semaphore_signal(barrier, inc=1, device_id=(rx, other, g), device_id_type=MESH_ID)
    count = 3
    if x_pair:
        pl.semaphore_signal(barrier, inc=1, device_id=(1 - rx, core, g), device_id_type=MESH_ID)
        count = 4
    pl.semaphore_wait(barrier, count)

    def block_at(d, s):
        if d == 0:
            return dev_at(pos + 2 * groups - 1 - s)
        return dev_at(pos + 1 + s)

    def cols(j, d):
        half = mine[j][1]
        return pl.ds(d * half, half)

    def load(d, s, slot, j):
        return pltpu.make_async_copy(mine[j][0](block_at(d, s)).at[:, cols(j, d)], own[j].at[d, slot], load_sem.at[d, slot, j])

    def part(d, s, j):
        return pltpu.make_async_remote_copy(
            src_ref=theirs[j][0](block_at(d, s)).at[:, cols(j, d)], dst_ref=pbuf[j].at[d, s],
            send_sem=part_send.at[d, s, j], recv_sem=part_recv.at[d, s, j],
            device_id=(rx, other, g), device_id_type=MESH_ID,
        )

    def ring(d, s, j):
        return pltpu.make_async_remote_copy(
            src_ref=sbuf[j].at[d, s], dst_ref=rbuf[j].at[d, s],
            send_sem=ring_send.at[d, s, j], recv_sem=ring_recv.at[d, s, j],
            device_id=(rx, core, nbr[d]), device_id_type=MESH_ID,
        )

    sends = []

    def ring_wave(items):
        for d in range(2):
            for j in items:
                load(d, 0, 0, j).start()
                c = part(d, 0, j)
                c.start()
                sends.append(c)
        for s in range(groups):
            slot = s % 2
            for d in range(2):
                for j in items:
                    load(d, s, slot, j).wait()
                    if s + 1 < groups:
                        load(d, s + 1, 1 - slot, j).start()
                        c = part(d, s + 1, j)
                        c.start()
                        sends.append(c)
                    part(d, s, j).wait_recv()
                    val = own[j][d, slot].astype(F32) + pbuf[j][d, s].astype(F32)
                    if s > 0:
                        ring(d, s - 1, j).wait_recv()
                        val = val + rbuf[j][d, s - 1].astype(F32)
                    if s < groups - 1:
                        sbuf[j][d, s] = val.astype(BF16)
                        c = ring(d, s, j)
                        c.start()
                        sends.append(c)
                    else:
                        fin[j][d] = val

    def x_start(items):
        copies = []
        for d in range(2):
            for j in items:
                xs[j][d] = fin[j][d].astype(BF16)
                c = pltpu.make_async_remote_copy(
                    src_ref=xs[j].at[d], dst_ref=xr[j].at[d], send_sem=x_send.at[d, j], recv_sem=x_recv.at[d, j],
                    device_id=(1 - rx, core, g), device_id_type=MESH_ID,
                )
                c.start()
                copies.append(c)
        sends.extend(copies)
        return copies

    def x_finish(items, copies):
        for c in copies:
            c.wait_recv()
        for d in range(2):
            for j in items:
                fin[j][d] = xs[j][d].astype(F32) + xr[j][d].astype(F32)

    def c_start(items):
        copies = []
        for d in range(2):
            for j in items:
                c = pltpu.make_async_remote_copy(
                    src_ref=fin[j].at[d], dst_ref=cr[j].at[d], send_sem=c_send.at[d, j], recv_sem=c_recv.at[d, j],
                    device_id=(rx, other, g), device_id_type=MESH_ID,
                )
                c.start()
                copies.append(c)
        return copies

    wave_a, wave_b = (0, 1, 2, 4), (3,)
    ring_wave(wave_a)
    if x_pair:
        xa = x_start(wave_a)
    ring_wave(wave_b)
    if x_pair:
        x_finish(wave_a, xa)
    c_copies = c_start(wave_a)
    if x_pair:
        x_finish(wave_b, x_start(wave_b))
    c_copies += c_start(wave_b)

    def out_items(owner):
        found = []
        for k in range(2):
            e = 2 * k + owner
            found.append(lambda d, e=e: out_up.at[e, :, pl.ds(d * (F // 2), F // 2)])
            found.append(lambda d, e=e: out_down.at[e, :, pl.ds(d * (D // 2), D // 2)])
        found.append(lambda d: out_dense.at[:, pl.ds(owner * width + d * (width // 2), width // 2)])
        return found

    mine_out = out_items(core)
    theirs_out = out_items(other)
    for d in range(2):
        for j in range(n_items):
            mine_out[j](d)[...] = fin[j][d]
    for c in c_copies:
        c.wait_recv()
    for d in range(2):
        for j in range(n_items):
            theirs_out[j](d)[...] = cr[j][d]
    for c in sends + c_copies:
        c.wait_send()


def grad_reduce(gu, gd, gdense, groups, x_pair, collective_id):
    gs = gu.shape[1] // groups
    fs = gd.shape[1] // groups
    width = gdense.shape[1] // 2
    item_shapes = [(gs, F // 2), (fs, D // 2), (gs, F // 2), (fs, D // 2), (gs, width // 2)]
    scratch = []
    for lead, dtype in (((2, groups - 1), BF16), ((2, groups - 1), BF16), ((2, groups), BF16), ((2, 2), BF16), ((2,), F32), ((2,), BF16), ((2,), F32), ((2,), BF16)):
        scratch += [pltpu.VMEM(lead + shp, dtype) for shp in item_shapes]
    scratch += [
        pltpu.SemaphoreType.DMA((2, groups - 1, 5)),
        pltpu.SemaphoreType.DMA((2, groups - 1, 5)),
        pltpu.SemaphoreType.DMA((2, groups, 5)),
        pltpu.SemaphoreType.DMA((2, groups, 5)),
        pltpu.SemaphoreType.DMA((2, 2, 5)),
        pltpu.SemaphoreType.DMA((2, 5)),
        pltpu.SemaphoreType.DMA((2, 5)),
        pltpu.SemaphoreType.DMA((2, 5)),
        pltpu.SemaphoreType.DMA((2, 5)),
    ]
    outs = [
        jax.ShapeDtypeStruct((E, gs, F), F32),
        jax.ShapeDtypeStruct((E, fs, D), F32),
        jax.ShapeDtypeStruct((gs, gdense.shape[1]), F32),
    ]
    nbytes = 2 * (gu.size + gd.size + gdense.size)
    return pl.pallas_call(
        functools.partial(ring_rs2_kernel, groups, x_pair),
        out_shape=outs,
        in_specs=[pl.BlockSpec(memory_space=pl.ANY)] * 3,
        out_specs=[pl.BlockSpec(memory_space=pltpu.VMEM)] * 3,
        scratch_shapes=scratch,
        compiler_params=pltpu.CompilerParams(
            collective_id=collective_id, has_side_effects=True, vmem_limit_bytes=62 * 1024 * 1024
        ),
        cost_estimate=pl.CostEstimate(flops=gu.size + gd.size + gdense.size, bytes_accessed=nbytes, transcendentals=0),
    )(gu, gd, gdense)


TILE = 256
TILE_B = 256
CAPP = 512
SQRT_HALF = float(np.sqrt(0.5))
INV_SQRT_2PI = float(1.0 / np.sqrt(2.0 * np.pi))


def ffn_fwd_kernel(micro, counts, x_ref, w1_ref, b1_ref, w2_ref, b2_ref, hp_ref, h_ref, y_ref):
    e, m, t = pl.program_id(0), pl.program_id(1), pl.program_id(2)
    active = t * TILE < counts[e * micro + m]

    @pl.when(active)
    def _():
        hp = jnp.dot(x_ref[0], w1_ref[0], preferred_element_type=F32) + b1_ref[0]
        cdf = 0.5 * (1.0 + lax.erf(hp * SQRT_HALF))
        h = (hp * cdf).astype(BF16)
        hp_ref[0] = cdf + hp * jnp.exp(-0.5 * hp * hp) * INV_SQRT_2PI
        h_ref[0] = h
        y = jnp.dot(h, w2_ref[0], preferred_element_type=F32) + b2_ref[0]
        hi = y.astype(BF16)
        y_ref[0, :, :D] = hi
        y_ref[0, :, D:] = (y - hi.astype(F32)).astype(BF16)

    @pl.when(jnp.logical_not(active))
    def _():
        y_ref[0] = jnp.zeros(y_ref.shape[1:], BF16)


def ffn_forward(counts, table_in, w1, b1, w2, b2, micro):
    tiles = CAPP // TILE
    rows = table_in.shape[1]
    row_map = lambda e, m, t, c: (m, e * tiles + t, 0)
    w_map = lambda e, m, t, c: (e, 0, 0)
    grid_spec = pltpu.PrefetchScalarGridSpec(
        num_scalar_prefetch=1,
        grid=(E, micro, tiles),
        in_specs=[
            pl.BlockSpec((1, TILE, D), row_map),
            pl.BlockSpec((1, D, F), w_map),
            pl.BlockSpec((1, 1, F), w_map),
            pl.BlockSpec((1, F, D), w_map),
            pl.BlockSpec((1, 1, D), w_map),
        ],
        out_specs=[
            pl.BlockSpec((1, TILE, F), row_map),
            pl.BlockSpec((1, TILE, F), row_map),
            pl.BlockSpec((1, TILE, 2 * D), row_map),
        ],
    )
    work = micro * rows
    return pl.pallas_call(
        functools.partial(ffn_fwd_kernel, micro),
        grid_spec=grid_spec,
        out_shape=[
            jax.ShapeDtypeStruct((micro, rows, F), F32),
            jax.ShapeDtypeStruct((micro, rows, F), BF16),
            jax.ShapeDtypeStruct((micro, rows, 2 * D), BF16),
        ],
        compiler_params=pltpu.CompilerParams(vmem_limit_bytes=48 * 1024 * 1024),
        cost_estimate=pl.CostEstimate(
            flops=4 * work * D * F // 2, bytes_accessed=work * (2 * D + 6 * F + 4 * D) // 2, transcendentals=work * F // 2
        ),
    )(counts, table_in, w1, b1, w2, b2)


def ffn_bwd_kernel(micro, counts, dy_ref, x_ref, hp_ref, h_ref, w1_ref, w2_ref, dt_ref, gu_ref, gd_ref, gb_ref, gb2_ref, gu_acc, gd_acc):
    e, m, t = pl.program_id(0), pl.program_id(1), pl.program_id(2)
    active = t * TILE_B < counts[e * micro + m]

    @pl.when((m == 0) & (t == 0))
    def _():
        gu_acc[...] = jnp.zeros(gu_acc.shape, F32)
        gd_acc[...] = jnp.zeros(gd_acc.shape, F32)
        gb_ref[...] = jnp.zeros(gb_ref.shape, F32)
        gb2_ref[...] = jnp.zeros(gb2_ref.shape, F32)

    @pl.when(active)
    def _():
        dy = dy_ref[0]
        d_hidden = lax.dot_general(dy, w2_ref[0], (((1,), (1,)), ((), ())), preferred_element_type=F32)
        d_pre = (d_hidden * hp_ref[0]).astype(BF16)
        dt = lax.dot_general(d_pre, w1_ref[0], (((1,), (1,)), ((), ())), preferred_element_type=F32)
        hi = dt.astype(BF16)
        dt_ref[0, :, :D] = hi
        dt_ref[0, :, D:] = (dt - hi.astype(F32)).astype(BF16)
        gb2_ref[0] += jnp.sum(dy.astype(F32), 0, keepdims=True)
        gu_acc[...] += lax.dot_general(x_ref[0], d_pre, (((0,), (0,)), ((), ())), preferred_element_type=F32)
        gd_acc[...] += lax.dot_general(h_ref[0], dy, (((0,), (0,)), ((), ())), preferred_element_type=F32)
        gb_ref[0] += jnp.sum(d_pre.astype(F32), 0, keepdims=True)

    @pl.when(jnp.logical_not(active))
    def _():
        dt_ref[0] = jnp.zeros(dt_ref.shape[1:], BF16)

    @pl.when((m == micro - 1) & (t == pl.num_programs(2) - 1))
    def _():
        gu_ref[0] = gu_acc[...].astype(BF16)
        gd_ref[0] = gd_acc[...].astype(BF16)


def ffn_backward(counts, d_expert, table_in, hp, h, w1, w2, micro):
    tiles = CAPP // TILE_B
    rows = table_in.shape[1]
    row_map = lambda e, m, t, c: (m, e * tiles + t, 0)
    w_map = lambda e, m, t, c: (e, 0, 0)
    grid_spec = pltpu.PrefetchScalarGridSpec(
        num_scalar_prefetch=1,
        grid=(E, micro, tiles),
        in_specs=[
            pl.BlockSpec((1, TILE_B, D), row_map),
            pl.BlockSpec((1, TILE_B, D), row_map),
            pl.BlockSpec((1, TILE_B, F), row_map),
            pl.BlockSpec((1, TILE_B, F), row_map),
            pl.BlockSpec((1, D, F), w_map),
            pl.BlockSpec((1, F, D), w_map),
        ],
        out_specs=[
            pl.BlockSpec((1, TILE_B, 2 * D), row_map),
            pl.BlockSpec((1, D, F), w_map),
            pl.BlockSpec((1, F, D), w_map),
            pl.BlockSpec((1, 1, F), w_map),
            pl.BlockSpec((1, 1, D), w_map),
        ],
        scratch_shapes=[pltpu.VMEM((D, F), F32), pltpu.VMEM((F, D), F32)],
    )
    work = micro * rows
    return pl.pallas_call(
        functools.partial(ffn_bwd_kernel, micro),
        grid_spec=grid_spec,
        out_shape=[
            jax.ShapeDtypeStruct((micro, rows, 2 * D), BF16),
            jax.ShapeDtypeStruct((E, D, F), BF16),
            jax.ShapeDtypeStruct((E, F, D), BF16),
            jax.ShapeDtypeStruct((E, 1, F), F32),
            jax.ShapeDtypeStruct((E, 1, D), F32),
        ],
        compiler_params=pltpu.CompilerParams(vmem_limit_bytes=60 * 1024 * 1024),
        cost_estimate=pl.CostEstimate(
            flops=8 * work * D * F // 2, bytes_accessed=work * (8 * D + 6 * F) // 2 + 16 * E * D * F, transcendentals=2 * work * F // 2
        ),
    )(counts, d_expert, table_in, hp, h, w1, w2)

def adamw_kernel(rate, w_ref, m_ref, g_ref, wo_ref, mo_ref):
    g = g_ref[...]
    first = 0.5 * m_ref[0] + 0.5 * g
    root = jnp.sqrt(0.5 * m_ref[1] * m_ref[1] + 0.5 * g * g)
    w = w_ref[...]
    wo_ref[...] = w - rate * (first / (root + 1e-08) + 0.1 * w)
    mo_ref[0] = first
    mo_ref[1] = root


def adamw_pass(weight, moments, grad, rate):
    n, r, c = weight.shape
    spec = pl.BlockSpec((1, r, c), lambda i: (i, 0, 0))
    mspec = pl.BlockSpec((2, 1, r, c), lambda i: (0, i, 0, 0))
    return pl.pallas_call(
        functools.partial(adamw_kernel, rate),
        grid=(n,),
        in_specs=[spec, mspec, spec],
        out_specs=[spec, mspec],
        out_shape=[jax.ShapeDtypeStruct(weight.shape, F32), jax.ShapeDtypeStruct(moments.shape, F32)],
        cost_estimate=pl.CostEstimate(flops=12 * weight.size, bytes_accessed=28 * weight.size, transcendentals=2 * weight.size),
    )(weight, moments, grad)


def layer_norm(value, gain, shift):
    center = value - jnp.mean(value, -1, keepdims=True)
    spread = jnp.mean(center * center, -1, keepdims=True)
    return center * lax.rsqrt(spread + 1e-06) * gain + shift


def gelu_exact(value):
    return jax.nn.gelu(value, approximate=False)


def split_heads(part):
    return part.reshape(-1, S, HEADS, HEAD_DIM)


def dot(a, b):
    return jnp.dot(a, b, preferred_element_type=F32)


def assign_places(route):
    chosen = jnp.concatenate([route[:, :, 0], route[:, :, 1]], 1)
    hits = (chosen[:, :, None] == jnp.arange(E, dtype=jnp.int32)).astype(jnp.int32)
    before = jnp.cumsum(hits, 1) - hits
    slot = jnp.sum(before * hits, 2)
    return chosen * CAPP + slot, jnp.sum(hits, 1)


def hi_lo(v):
    hi = v.astype(BF16)
    lo = (v - hi.astype(F32)).astype(BF16)
    return jnp.concatenate([hi, lo], -1)


def pick_rows(onehot, split):
    both = jnp.einsum("mnr,mrd->mnd", onehot, split, preferred_element_type=F32)
    return both[..., :D] + both[..., D:]


def pack_dense(qkv_w, out_w, router_w, vectors, up_bias):
    rows = qkv_w.shape[0]
    ub = up_bias.reshape(E, rows, 4).transpose(1, 0, 2).reshape(rows, E * 4)
    return jnp.concatenate([qkv_w, out_w, router_w, vectors.T, ub], 1)


def unpack_dense(packed):
    rows = packed.shape[0]
    w_qkv = packed[:, : 3 * D]
    w_out = packed[:, 3 * D : 4 * D]
    w_router = packed[:, 4 * D : 4 * D + E]
    table = packed[:, 4 * D + E : 4 * D + E + NV].T
    ub = packed[:, 4 * D + E + NV :].reshape(rows, E, 4).transpose(1, 0, 2).reshape(E, rows * 4)
    return w_qkv, w_out, w_router, table, ub


def attention_fwd(w_qkv, w_out, table, value):
    rows = value.shape[0]
    scale = HEAD_DIM ** (-0.5)
    first = layer_norm(value, table[0], table[1]).astype(BF16)
    qkv_bias = jnp.concatenate([table[2], jnp.zeros((D,), F32), table[3]])
    qkv = (dot(first, w_qkv) + qkv_bias).astype(BF16)
    query, key_part, val_part = (
        split_heads(qkv[:, :D]),
        split_heads(qkv[:, D : 2 * D]),
        split_heads(qkv[:, 2 * D :]),
    )
    scores = jnp.einsum("bqhd,bkhd->bhqk", query, key_part, preferred_element_type=F32) * scale
    peak = jnp.max(scores, -1, keepdims=True)
    expo = jnp.exp(scores - peak)
    total = jnp.sum(expo, -1, keepdims=True)
    probs_att = (expo / total).astype(BF16)
    log_total = peak + jnp.log(total)
    attended = jnp.einsum("bhqk,bkhd->bqhd", probs_att, val_part, preferred_element_type=F32)
    attended = attended.reshape(rows, D).astype(BF16)
    resid = value + (dot(attended, w_out) + table[4])
    return first, qkv, log_total, attended, resid


def attention_bwd(w_qkv, w_out, table, value, first, qkv, log_total, attended, d_resid):
    rows = value.shape[0]
    scale = HEAD_DIM ** (-0.5)
    d_branch = d_resid.astype(BF16)
    g_bias_out = jnp.sum(d_branch.astype(F32), 0)
    g_out = lax.dot_general(attended, d_branch, (((0,), (0,)), ((), ())), preferred_element_type=F32)
    d_att = split_heads(
        lax.dot_general(d_branch, w_out, (((1,), (1,)), ((), ())), preferred_element_type=F32).astype(BF16)
    )
    query, key_part, val_part = (
        split_heads(qkv[:, :D]),
        split_heads(qkv[:, D : 2 * D]),
        split_heads(qkv[:, 2 * D :]),
    )
    scores = jnp.einsum("bqhd,bkhd->bhqk", query, key_part, preferred_element_type=F32) * scale
    probs_f = jnp.exp(scores - log_total)
    probs_att = probs_f.astype(BF16)
    d_val = jnp.einsum("bhqk,bqhd->bkhd", probs_att, d_att, preferred_element_type=F32)
    d_prob = jnp.einsum("bqhd,bkhd->bhqk", d_att, val_part, preferred_element_type=F32)
    d_score = (probs_f * (d_prob - jnp.sum(d_prob * probs_f, -1, keepdims=True))).astype(BF16)
    d_query = jnp.einsum("bhqk,bkhd->bqhd", d_score, key_part, preferred_element_type=F32) * scale
    d_key = jnp.einsum("bhqk,bqhd->bkhd", d_score, query, preferred_element_type=F32) * scale
    d_qkv = jnp.concatenate(
        [d_query.reshape(rows, D), d_key.reshape(rows, D), d_val.reshape(rows, D)], 1
    ).astype(BF16)
    d_qkv_f = d_qkv.astype(F32)
    g_bias_q = jnp.sum(d_qkv_f[:, :D], 0)
    g_bias_v = jnp.sum(d_qkv_f[:, 2 * D :], 0)
    g_qkv = lax.dot_general(first, d_qkv, (((0,), (0,)), ((), ())), preferred_element_type=F32)
    d_first = lax.dot_general(d_qkv, w_qkv, (((1,), (1,)), ((), ())), preferred_element_type=F32)
    first_pull = jax.vjp(layer_norm, value, table[0], table[1])[1]
    d_input, g_gain_one, g_shift_one = first_pull(d_first)
    return (g_qkv, g_out, g_bias_out, g_bias_q, g_bias_v, g_gain_one, g_shift_one), d_input


def adamw(weight, moments, grad, rate):
    first = 0.5 * moments[0] + 0.5 * grad
    root = jnp.sqrt(0.5 * moments[1] * moments[1] + 0.5 * grad * grad)
    update = first / (root + 1e-08)
    which = lax.broadcasted_iota(jnp.int32, moments.shape, 0) == 0
    both = jnp.where(which, 0.5 * moments + 0.5 * grad, jnp.sqrt(0.5 * moments * moments + 0.5 * grad * grad))
    return (weight - rate * (update + 0.1 * weight), both)


def shards(
    tokens,
    cotangent,
    expert_index,
    qkv_weight,
    out_weight,
    router_weight,
    up_weight,
    up_bias,
    down_weight,
    vectors,
    qkv_moments,
    out_moments,
    router_moments,
    up_moments,
    up_bias_moments,
    down_moments,
    vector_moments,
):
    rows = tokens.shape[0]
    micro = rows // MB_TOK
    gs = qkv_weight.shape[0]
    group_size = D // gs
    core = lax.axis_index("core")

    dense_in = pack_dense(qkv_weight, out_weight, router_weight, vectors, up_bias)
    width = dense_in.shape[1]
    dense_in = jnp.pad(dense_in, ((0, 0), (0, DENSE_AG - width))).astype(BF16)
    w_up_all, w_down_all, dense = ring_all_gather(
        up_weight.astype(BF16), down_weight.astype(BF16), dense_in, group_size, 1
    )
    w_qkv, w_out, w_router, table_b, b_up_b = unpack_dense(dense[:, :width])
    table = table_b.astype(F32)
    b_up = b_up_b.astype(F32)

    value = tokens.astype(F32)
    d_out = cotangent.astype(F32)
    first, qkv, log_total, attended, resid = attention_fwd(w_qkv, w_out, table, value)
    second = layer_norm(resid, table[5], table[6]).astype(BF16)
    logits = dot(second, w_router)
    probs = jax.nn.softmax(logits, -1)
    picked = expert_index[:, :, None] == jnp.arange(E, dtype=jnp.int32)
    gate = jnp.sum(jnp.where(picked, probs[:, None, :], 0.0), -1)

    route = expert_index.reshape(micro, MB_TOK, 2)
    places, counts = assign_places(route)
    counts = counts.T.reshape(E * micro)
    onehot = (places[:, :, None] == jnp.arange(E * CAPP, dtype=jnp.int32)).astype(BF16)
    second_m = second.reshape(micro, MB_TOK, D)
    pair = jnp.concatenate([second_m, second_m], 1)
    table_in = jnp.einsum("mnr,mnd->mrd", onehot, pair, preferred_element_type=F32).astype(BF16)

    hidden_pre, hidden, y_all = ffn_forward(
        counts, table_in, w_up_all, b_up[:, None, :], w_down_all, table[7 : 7 + E][:, None, :], micro
    )
    picked_rows = pick_rows(onehot, y_all)
    out_zero = picked_rows[:, :MB_TOK].reshape(rows, D)
    out_one = picked_rows[:, MB_TOK:].reshape(rows, D)
    result = resid + (gate[:, 0:1] * out_zero + gate[:, 1:2] * out_one)

    d_gate = jnp.stack([jnp.sum(d_out * out_zero, -1), jnp.sum(d_out * out_one, -1)], 1)
    d_out_m = d_out.reshape(micro, MB_TOK, D)
    gate_m = gate.reshape(micro, MB_TOK, 2)
    weighted = jnp.concatenate([gate_m[:, :, 0:1] * d_out_m, gate_m[:, :, 1:2] * d_out_m], 1).astype(BF16)
    d_expert = jnp.einsum("mnr,mnd->mrd", onehot, weighted, preferred_element_type=F32).astype(BF16)

    d_table, g_up, g_down, g_b1, g_b2 = ffn_backward(counts, d_expert, table_in, hidden_pre, hidden, w_up_all, w_down_all, micro)
    g_up_bias_all = g_b1[:, 0, :]
    g_bias_down = g_b2[:, 0, :]

    onehot_sum = onehot[:, :MB_TOK] + onehot[:, MB_TOK:]
    d_picked = pick_rows(onehot_sum, d_table).reshape(rows, D)

    d_probs = jnp.sum(jnp.where(picked, d_gate[:, :, None], 0.0), 1)
    d_logit = (probs * (d_probs - jnp.sum(d_probs * probs, -1, keepdims=True))).astype(BF16)
    g_router = lax.dot_general(second, d_logit, (((0,), (0,)), ((), ())), preferred_element_type=F32)
    d_second = d_picked + lax.dot_general(d_logit, w_router, (((1,), (1,)), ((), ())), preferred_element_type=F32)
    norm_pull = jax.vjp(layer_norm, resid, table[5], table[6])[1]
    d_resid, g_gain_two, g_shift_two = norm_pull(d_second)
    d_resid = d_out + d_resid

    att_grads, d_input = attention_bwd(w_qkv, w_out, table, value, first, qkv, log_total, attended, d_resid)
    g_qkv, g_out, g_bias_out, g_bias_q, g_bias_v, g_gain_one, g_shift_one = att_grads
    input_grad = d_resid + d_input

    g_table = jnp.concatenate(
        [
            jnp.stack([g_gain_one, g_shift_one, g_bias_q, g_bias_v, g_bias_out, g_gain_two, g_shift_two]),
            g_bias_down,
        ],
        0,
    )
    dense_g = pack_dense(g_qkv, g_out, g_router, g_table, g_up_bias_all)
    width = dense_g.shape[1]
    dense_g = jnp.pad(dense_g, ((0, 0), (0, DENSE_AG - width))).astype(BF16)
    x_pair = lax.axis_size("rx") == 2
    r_up, r_down, r_dense = grad_reduce(g_up, g_down, dense_g, group_size, x_pair, 0)
    if not x_pair:
        r_up, r_down, r_dense = lax.psum((r_up, r_down, r_dense), "rx")
    r_qkv, r_out, r_router, r_table, r_ub = unpack_dense(r_dense[:, :width])

    reduced = (r_qkv, r_out, r_router, r_up, r_ub, r_down, r_table)
    rates = (
        2.0 * D ** (-0.5),
        2.0 * (D // 32) ** (-0.5),
        2.0 * (2 * D) ** (-0.5),
        2.0 * D ** (-0.5),
        0.2,
        2.0 * (F // 16) ** (-0.5),
        0.2,
    )
    params = (qkv_weight, out_weight, router_weight, up_weight, up_bias, down_weight, vectors)
    moments = (qkv_moments, out_moments, router_moments, up_moments, up_bias_moments, down_moments, vector_moments)
    news = []
    states = []
    for weight, state, grad, rate in zip(params, moments, reduced, rates):
        if weight.ndim == 3:
            new_weight, new_state = adamw_pass(weight, state, grad, rate)
        else:
            new_weight, new_state = adamw(weight, state, grad, rate)
        news.append(new_weight)
        states.append(new_state)
    return (result.astype(BF16), input_grad) + reduced + tuple(news) + tuple(states)


def solution(mesh):
    replica, group = mesh.shape["replica"], mesh.shape["group"]
    view = Mesh(np.asarray(mesh.devices).reshape(replica // 2, 2, group), ("rx", "core", "group"))
    in_specs = (
        P(TOK, None),
        P(TOK, None),
        P(TOK, None),
        P("group", None),
        P("group", None),
        P("group", None),
        P(None, "group", None),
        P(None, "group"),
        P(None, "group", None),
        P(None, "group"),
        P(None, "group", None),
        P(None, "group", None),
        P(None, "group", None),
        P(None, None, "group", None),
        P(None, None, "group"),
        P(None, None, "group", None),
        P(None, None, "group"),
    )
    out_specs = (
        P(TOK, None),
        P(TOK, None),
        P("group", None),
        P("group", None),
        P("group", None),
        P(None, "group", None),
        P(None, "group"),
        P(None, "group", None),
        P(None, "group"),
        P("group", None),
        P("group", None),
        P("group", None),
        P(None, "group", None),
        P(None, "group"),
        P(None, "group", None),
        P(None, "group"),
        P(None, "group", None),
        P(None, "group", None),
        P(None, "group", None),
        P(None, None, "group", None),
        P(None, None, "group"),
        P(None, None, "group", None),
        P(None, None, "group"),
    )
    return jax.shard_map(shards, mesh=view, in_specs=in_specs, out_specs=out_specs, check_vma=False)
```

```python
import functools

import jax
import jax.numpy as jnp
import numpy as np
from jax import lax
from jax.sharding import Mesh
from jax.sharding import PartitionSpec as P
from jax.experimental import pallas as pl
from jax.experimental.pallas import tpu as pltpu

D = 512
HEADS = 8
HEAD_DIM = 64
F = 2048
E = 4
S = 197
MB_TOK = 394
CAP = 392
NV = 11
DENSE_AG = 2560
DENSE_PAD = 2304
F32 = jnp.float32
BF16 = jnp.bfloat16
TOK = ("rx", "core", "group")


MESH_ID = pl.DeviceIdType.MESH


def ring_order(groups):
    if groups in (4, 8):
        zs = groups // 2

        def pos_of(g):
            y = g % 2
            z = g // 2
            return z + y * (2 * zs - 1 - 2 * z)

        def dev_at(p):
            p = p % groups
            yy = p // zs
            return 2 * (p + yy * (2 * zs - 1 - 2 * p)) + yy

        return pos_of, dev_at
    return (lambda g: g), (lambda p: p % groups)


def ring_rs_kernel(groups, n_in, *refs):
    ins = refs[:n_in]
    outs = refs[n_in : 2 * n_in]
    rbufs = refs[2 * n_in : 3 * n_in]
    sbufs = refs[3 * n_in : 4 * n_in]
    owns = refs[4 * n_in : 5 * n_in]
    send_sem, recv_sem, load_sem = refs[5 * n_in :]
    pos_of, dev_at = ring_order(groups)
    rx = lax.axis_index("rx")
    core = lax.axis_index("core")
    g = lax.axis_index("group")
    pos = pos_of(g)
    nbr = (dev_at(pos + 1), dev_at(pos + groups - 1))

    barrier = pltpu.get_barrier_semaphore()
    for n in nbr:
        pl.semaphore_signal(barrier, inc=1, device_id=(rx, core, n), device_id_type=MESH_ID)
    pl.semaphore_wait(barrier, 2)

    def block_dev(d, s):
        if d == 0:
            return dev_at(pos + 2 * groups - s - 1)
        return dev_at(pos + s + 1)

    def load(d, s, slot):
        b = block_dev(d, s)
        copies = []
        for i in range(n_in):
            rows = ins[i].shape[1] // groups
            half = ins[i].shape[2] // 2
            src = ins[i].at[:, pl.ds(pl.multiple_of(b * rows, rows), rows), pl.ds(d * half, half)]
            copies.append(pltpu.make_async_copy(src, owns[i].at[d, slot], load_sem.at[d, slot, i]))
        return copies

    def remote(d, s, i):
        return pltpu.make_async_remote_copy(
            src_ref=sbufs[i].at[d, s],
            dst_ref=rbufs[i].at[d, s],
            send_sem=send_sem.at[d, s, i],
            recv_sem=recv_sem.at[d, s, i],
            device_id=(rx, core, nbr[d]),
            device_id_type=MESH_ID,
        )

    for d in range(2):
        for c in load(d, 0, 0):
            c.start()
    sends = []
    for s in range(groups):
        slot = s % 2
        for d in range(2):
            for c in load(d, s, slot):
                c.wait()
            if s + 1 < groups:
                for c in load(d, s + 1, 1 - slot):
                    c.start()
            for i in range(n_in):
                if s > 0:
                    remote(d, s - 1, i).wait_recv()
                for a in range(ins[i].shape[0]):
                    mine = owns[i][d, slot, a].astype(F32)
                    if s > 0:
                        mine = mine + rbufs[i][d, s - 1, a].astype(F32)
                    if s < groups - 1:
                        sbufs[i][d, s, a] = mine.astype(sbufs[i].dtype)
                    else:
                        half = ins[i].shape[2] // 2
                        outs[i][a, :, pl.ds(d * half, half)] = mine.astype(outs[i].dtype)
                if s < groups - 1:
                    c = remote(d, s, i)
                    c.start()
                    sends.append(c)
    for c in sends:
        c.wait_send()


def ring_reduce_scatter(xs, groups, collective_id):
    n_in = len(xs)
    outs, rb, own = [], [], []
    flops = 0
    nbytes = 0
    for x in xs:
        a, total, c = x.shape
        rows = total // groups
        outs.append(jax.ShapeDtypeStruct((a, rows, c), x.dtype))
        rb.append(pltpu.VMEM((2, groups - 1, a, rows, c // 2), x.dtype))
        own.append(pltpu.VMEM((2, 2, a, rows, c // 2), x.dtype))
        flops += a * total * c
        nbytes += 3 * x.size * x.dtype.itemsize
    scratch = rb + rb + own + [
        pltpu.SemaphoreType.DMA((2, groups - 1, n_in)),
        pltpu.SemaphoreType.DMA((2, groups - 1, n_in)),
        pltpu.SemaphoreType.DMA((2, 2, n_in)),
    ]
    return pl.pallas_call(
        functools.partial(ring_rs_kernel, groups, n_in),
        out_shape=outs,
        in_specs=[pl.BlockSpec(memory_space=pl.ANY)] * n_in,
        out_specs=[pl.BlockSpec(memory_space=pltpu.VMEM)] * n_in,
        scratch_shapes=scratch,
        compiler_params=pltpu.CompilerParams(
            collective_id=collective_id, has_side_effects=True, vmem_limit_bytes=60 * 1024 * 1024
        ),
        cost_estimate=pl.CostEstimate(flops=flops, bytes_accessed=nbytes, transcendentals=0),
    )(*xs)


def ring_ag_kernel(groups, *refs):
    in_up, in_down, in_dense, out_up, out_down, out_dense = refs[:6]
    ring_send, ring_recv, part_send, part_recv, local_sem = refs[6:]
    pos_of, dev_at = ring_order(groups)
    rx = lax.axis_index("rx")
    core = lax.axis_index("core")
    g = lax.axis_index("group")
    other = 1 - core
    pos = pos_of(g)
    nbr = (dev_at(pos + 1), dev_at(pos + groups - 1))
    gs = in_up.shape[1]
    fs = in_down.shape[1]
    width = in_dense.shape[1] // 2

    barrier = pltpu.get_barrier_semaphore()
    for n in nbr:
        pl.semaphore_signal(barrier, inc=1, device_id=(rx, core, n), device_id_type=MESH_ID)
    pl.semaphore_signal(barrier, inc=1, device_id=(rx, other, g), device_id_type=MESH_ID)
    pl.semaphore_wait(barrier, 3)

    def items(owner):
        found = []
        for k in range(2):
            e = 2 * k + owner
            found.append((in_up.at[e], lambda b, e=e: out_up.at[e, pl.ds(pl.multiple_of(b * gs, gs), gs)], F // 2))
            found.append((in_down.at[e], lambda b, e=e: out_down.at[e, pl.ds(pl.multiple_of(b * fs, fs), fs)], D // 2))
        dense_in = in_dense.at[:, pl.ds(owner * width, width)]
        found.append(
            (dense_in, lambda b: out_dense.at[pl.ds(pl.multiple_of(b * gs, gs), gs), pl.ds(owner * width, width)], width // 2)
        )
        return found

    mine = items(core)
    theirs = items(other)
    n_items = len(mine)

    locals_ = [pltpu.make_async_copy(in_up.at[e], out_up.at[e, pl.ds(pl.multiple_of(g * gs, gs), gs)], local_sem.at[e]) for e in range(E)]
    locals_ += [
        pltpu.make_async_copy(in_down.at[e], out_down.at[e, pl.ds(pl.multiple_of(g * fs, fs), fs)], local_sem.at[E + e])
        for e in range(E)
    ]
    locals_.append(pltpu.make_async_copy(in_dense, out_dense.at[pl.ds(pl.multiple_of(g * gs, gs), gs)], local_sem.at[2 * E]))
    for c in locals_:
        c.start()

    def block_at(d, s):
        if d == 0:
            return dev_at(pos + 2 * groups - 1 - s)
        return dev_at(pos + 1 + s)

    def ring_copy(d, s, j, src_block):
        src_in, dst_of, half = mine[j]
        cols = pl.ds(d * half, half)
        if src_block is None:
            src = src_in.at[:, cols]
            dst = dst_of(g).at[:, cols]
        else:
            src = dst_of(src_block).at[:, cols]
            dst = src
        return pltpu.make_async_remote_copy(
            src_ref=src, dst_ref=dst, send_sem=ring_send.at[d, s, j], recv_sem=ring_recv.at[d, s, j],
            device_id=(rx, core, nbr[d]), device_id_type=MESH_ID,
        )

    def part_copy(d, s, j, table, block):
        _, dst_of, half = table[j]
        view = dst_of(block).at[:, pl.ds(d * half, half)]
        return pltpu.make_async_remote_copy(
            src_ref=view, dst_ref=view, send_sem=part_send.at[d, s, j], recv_sem=part_recv.at[d, s, j],
            device_id=(rx, other, g), device_id_type=MESH_ID,
        )

    sends = []
    for d in range(2):
        for j in range(n_items):
            c = ring_copy(d, 0, j, None)
            c.start()
            sends.append(c)
    for s in range(groups - 1):
        for d in range(2):
            b = block_at(d, s)
            for j in range(n_items):
                pltpu.make_async_remote_copy(
                    src_ref=mine[j][1](b).at[:, pl.ds(d * mine[j][2], mine[j][2])],
                    dst_ref=mine[j][1](b).at[:, pl.ds(d * mine[j][2], mine[j][2])],
                    send_sem=ring_send.at[d, s, j], recv_sem=ring_recv.at[d, s, j],
                    device_id=(rx, core, nbr[d]), device_id_type=MESH_ID,
                ).wait_recv()
                if s + 1 < groups - 1:
                    c = ring_copy(d, s + 1, j, b)
                    c.start()
                    sends.append(c)
                c = part_copy(d, s, j, mine, b)
                c.start()
                sends.append(c)
    for s in range(groups - 1):
        for d in range(2):
            b = block_at(d, s)
            for j in range(n_items):
                part_copy(d, s, j, theirs, b).wait_recv()
    for c in sends:
        c.wait_send()
    for c in locals_:
        c.wait()


def ring_all_gather(up_b, down_b, dense_b, groups, collective_id):
    n_items = 5
    gs = up_b.shape[1]
    shapes = [
        jax.ShapeDtypeStruct((E, gs * groups, F), BF16),
        jax.ShapeDtypeStruct((E, down_b.shape[1] * groups, D), BF16),
        jax.ShapeDtypeStruct((gs * groups, dense_b.shape[1]), BF16),
    ]
    nbytes = sum(int(np.prod(s.shape)) * 2 for s in shapes)
    return pl.pallas_call(
        functools.partial(ring_ag_kernel, groups),
        out_shape=shapes,
        in_specs=[pl.BlockSpec(memory_space=pl.ANY)] * 3,
        out_specs=[pl.BlockSpec(memory_space=pl.ANY)] * 3,
        scratch_shapes=[
            pltpu.SemaphoreType.DMA((2, groups - 1, n_items)),
            pltpu.SemaphoreType.DMA((2, groups - 1, n_items)),
            pltpu.SemaphoreType.DMA((2, groups - 1, n_items)),
            pltpu.SemaphoreType.DMA((2, groups - 1, n_items)),
            pltpu.SemaphoreType.DMA((2 * E + 1,)),
        ],
        compiler_params=pltpu.CompilerParams(collective_id=collective_id, has_side_effects=True),
        cost_estimate=pl.CostEstimate(flops=0, bytes_accessed=nbytes, transcendentals=0),
    )(up_b, down_b, dense_b)


def grad_items(gu, gd, gdense, owner, gs, fs, width):
    found = []
    for k in range(2):
        e = 2 * k + owner
        found.append((lambda b, e=e: gu.at[e, pl.ds(pl.multiple_of(b * gs, gs), gs)], F // 2))
        found.append((lambda b, e=e: gd.at[e, pl.ds(pl.multiple_of(b * fs, fs), fs)], D // 2))
    found.append((lambda b: gdense.at[pl.ds(pl.multiple_of(b * gs, gs), gs), pl.ds(owner * width, width)], width // 2))
    return found


def ring_rs2_kernel(groups, x_pair, *refs):
    gu, gd, gdense, out_up, out_down, out_dense = refs[:6]
    n_items = 5
    scr = refs[6:]
    rbuf, sbuf, pbuf, own, fin, xr, cr, xs = (scr[i * n_items : (i + 1) * n_items] for i in range(8))
    ring_send, ring_recv, part_send, part_recv, load_sem, x_send, x_recv, c_send, c_recv = scr[8 * n_items :]
    pos_of, dev_at = ring_order(groups)
    rx = lax.axis_index("rx")
    core = lax.axis_index("core")
    g = lax.axis_index("group")
    other = 1 - core
    pos = pos_of(g)
    nbr = (dev_at(pos + 1), dev_at(pos + groups - 1))
    gs = gu.shape[1] // groups
    fs = gd.shape[1] // groups
    width = gdense.shape[1] // 2
    mine = grad_items(gu, gd, gdense, core, gs, fs, width)
    theirs = grad_items(gu, gd, gdense, other, gs, fs, width)

    barrier = pltpu.get_barrier_semaphore()
    for n in nbr:
        pl.semaphore_signal(barrier, inc=1, device_id=(rx, core, n), device_id_type=MESH_ID)
    pl.semaphore_signal(barrier, inc=1, device_id=(rx, other, g), device_id_type=MESH_ID)
    count = 3
    if x_pair:
        pl.semaphore_signal(barrier, inc=1, device_id=(1 - rx, core, g), device_id_type=MESH_ID)
        count = 4
    pl.semaphore_wait(barrier, count)

    def block_at(d, s):
        if d == 0:
            return dev_at(pos + 2 * groups - 1 - s)
        return dev_at(pos + 1 + s)

    def cols(j, d):
        half = mine[j][1]
        return pl.ds(d * half, half)

    def load(d, s, slot, j):
        return pltpu.make_async_copy(mine[j][0](block_at(d, s)).at[:, cols(j, d)], own[j].at[d, slot], load_sem.at[d, slot, j])

    def part(d, s, j):
        return pltpu.make_async_remote_copy(
            src_ref=theirs[j][0](block_at(d, s)).at[:, cols(j, d)], dst_ref=pbuf[j].at[d, s],
            send_sem=part_send.at[d, s, j], recv_sem=part_recv.at[d, s, j],
            device_id=(rx, other, g), device_id_type=MESH_ID,
        )

    def ring(d, s, j):
        return pltpu.make_async_remote_copy(
            src_ref=sbuf[j].at[d, s], dst_ref=rbuf[j].at[d, s],
            send_sem=ring_send.at[d, s, j], recv_sem=ring_recv.at[d, s, j],
            device_id=(rx, core, nbr[d]), device_id_type=MESH_ID,
        )

    sends = []

    def ring_wave(items):
        for d in range(2):
            for j in items:
                load(d, 0, 0, j).start()
                c = part(d, 0, j)
                c.start()
                sends.append(c)
        for s in range(groups):
            slot = s % 2
            for d in range(2):
                for j in items:
                    load(d, s, slot, j).wait()
                    if s + 1 < groups:
                        load(d, s + 1, 1 - slot, j).start()
                        c = part(d, s + 1, j)
                        c.start()
                        sends.append(c)
                    part(d, s, j).wait_recv()
                    val = own[j][d, slot].astype(F32) + pbuf[j][d, s].astype(F32)
                    if s > 0:
                        ring(d, s - 1, j).wait_recv()
                        val = val + rbuf[j][d, s - 1].astype(F32)
                    if s < groups - 1:
                        sbuf[j][d, s] = val.astype(BF16)
                        c = ring(d, s, j)
                        c.start()
                        sends.append(c)
                    else:
                        fin[j][d] = val

    def x_start(items):
        copies = []
        for d in range(2):
            for j in items:
                xs[j][d] = fin[j][d].astype(BF16)
                c = pltpu.make_async_remote_copy(
                    src_ref=xs[j].at[d], dst_ref=xr[j].at[d], send_sem=x_send.at[d, j], recv_sem=x_recv.at[d, j],
                    device_id=(1 - rx, core, g), device_id_type=MESH_ID,
                )
                c.start()
                copies.append(c)
        sends.extend(copies)
        return copies

    def x_finish(items, copies):
        for c in copies:
            c.wait_recv()
        for d in range(2):
            for j in items:
                fin[j][d] = xs[j][d].astype(F32) + xr[j][d].astype(F32)

    def c_start(items):
        copies = []
        for d in range(2):
            for j in items:
                c = pltpu.make_async_remote_copy(
                    src_ref=fin[j].at[d], dst_ref=cr[j].at[d], send_sem=c_send.at[d, j], recv_sem=c_recv.at[d, j],
                    device_id=(rx, other, g), device_id_type=MESH_ID,
                )
                c.start()
                copies.append(c)
        return copies

    wave_a, wave_b = (0, 1, 2, 4), (3,)
    ring_wave(wave_a)
    if x_pair:
        xa = x_start(wave_a)
    ring_wave(wave_b)
    if x_pair:
        x_finish(wave_a, xa)
    c_copies = c_start(wave_a)
    if x_pair:
        x_finish(wave_b, x_start(wave_b))
    c_copies += c_start(wave_b)

    def out_items(owner):
        found = []
        for k in range(2):
            e = 2 * k + owner
            found.append(lambda d, e=e: out_up.at[e, :, pl.ds(d * (F // 2), F // 2)])
            found.append(lambda d, e=e: out_down.at[e, :, pl.ds(d * (D // 2), D // 2)])
        found.append(lambda d: out_dense.at[:, pl.ds(owner * width + d * (width // 2), width // 2)])
        return found

    mine_out = out_items(core)
    theirs_out = out_items(other)
    for d in range(2):
        for j in range(n_items):
            mine_out[j](d)[...] = fin[j][d]
    for c in c_copies:
        c.wait_recv()
    for d in range(2):
        for j in range(n_items):
            theirs_out[j](d)[...] = cr[j][d]
    for c in sends + c_copies:
        c.wait_send()


def grad_reduce(gu, gd, gdense, groups, x_pair, collective_id):
    gs = gu.shape[1] // groups
    fs = gd.shape[1] // groups
    width = gdense.shape[1] // 2
    item_shapes = [(gs, F // 2), (fs, D // 2), (gs, F // 2), (fs, D // 2), (gs, width // 2)]
    scratch = []
    for lead, dtype in (((2, groups - 1), BF16), ((2, groups - 1), BF16), ((2, groups), BF16), ((2, 2), BF16), ((2,), F32), ((2,), BF16), ((2,), F32), ((2,), BF16)):
        scratch += [pltpu.VMEM(lead + shp, dtype) for shp in item_shapes]
    scratch += [
        pltpu.SemaphoreType.DMA((2, groups - 1, 5)),
        pltpu.SemaphoreType.DMA((2, groups - 1, 5)),
        pltpu.SemaphoreType.DMA((2, groups, 5)),
        pltpu.SemaphoreType.DMA((2, groups, 5)),
        pltpu.SemaphoreType.DMA((2, 2, 5)),
        pltpu.SemaphoreType.DMA((2, 5)),
        pltpu.SemaphoreType.DMA((2, 5)),
        pltpu.SemaphoreType.DMA((2, 5)),
        pltpu.SemaphoreType.DMA((2, 5)),
    ]
    outs = [
        jax.ShapeDtypeStruct((E, gs, F), F32),
        jax.ShapeDtypeStruct((E, fs, D), F32),
        jax.ShapeDtypeStruct((gs, gdense.shape[1]), F32),
    ]
    nbytes = 2 * (gu.size + gd.size + gdense.size)
    return pl.pallas_call(
        functools.partial(ring_rs2_kernel, groups, x_pair),
        out_shape=outs,
        in_specs=[pl.BlockSpec(memory_space=pl.ANY)] * 3,
        out_specs=[pl.BlockSpec(memory_space=pltpu.VMEM)] * 3,
        scratch_shapes=scratch,
        compiler_params=pltpu.CompilerParams(
            collective_id=collective_id, has_side_effects=True, vmem_limit_bytes=62 * 1024 * 1024
        ),
        cost_estimate=pl.CostEstimate(flops=gu.size + gd.size + gdense.size, bytes_accessed=nbytes, transcendentals=0),
    )(gu, gd, gdense)


TILE = 256
TILE_B = 256
CAPP = 512
SQRT_HALF = float(np.sqrt(0.5))
INV_SQRT_2PI = float(1.0 / np.sqrt(2.0 * np.pi))


def ffn_fwd_kernel(micro, counts, x_ref, w1_ref, b1_ref, w2_ref, b2_ref, hp_ref, h_ref, y_ref):
    e, m, t = pl.program_id(0), pl.program_id(1), pl.program_id(2)
    active = t * TILE < counts[e * micro + m]

    @pl.when(active)
    def _():
        hp = jnp.dot(x_ref[0], w1_ref[0], preferred_element_type=F32) + b1_ref[0]
        cdf = 0.5 * (1.0 + lax.erf(hp * SQRT_HALF))
        h = (hp * cdf).astype(BF16)
        hp_ref[0] = cdf + hp * jnp.exp(-0.5 * hp * hp) * INV_SQRT_2PI
        h_ref[0] = h
        y = jnp.dot(h, w2_ref[0], preferred_element_type=F32) + b2_ref[0]
        hi = y.astype(BF16)
        y_ref[0, :, :D] = hi
        y_ref[0, :, D:] = (y - hi.astype(F32)).astype(BF16)

    @pl.when(jnp.logical_not(active))
    def _():
        y_ref[0] = jnp.zeros(y_ref.shape[1:], BF16)


def ffn_forward(counts, table_in, w1, b1, w2, b2, micro):
    tiles = CAPP // TILE
    rows = table_in.shape[1]
    row_map = lambda e, m, t, c: (m, e * tiles + t, 0)
    w_map = lambda e, m, t, c: (e, 0, 0)
    grid_spec = pltpu.PrefetchScalarGridSpec(
        num_scalar_prefetch=1,
        grid=(E, micro, tiles),
        in_specs=[
            pl.BlockSpec((1, TILE, D), row_map),
            pl.BlockSpec((1, D, F), w_map),
            pl.BlockSpec((1, 1, F), w_map),
            pl.BlockSpec((1, F, D), w_map),
            pl.BlockSpec((1, 1, D), w_map),
        ],
        out_specs=[
            pl.BlockSpec((1, TILE, F), row_map),
            pl.BlockSpec((1, TILE, F), row_map),
            pl.BlockSpec((1, TILE, 2 * D), row_map),
        ],
    )
    work = micro * rows
    return pl.pallas_call(
        functools.partial(ffn_fwd_kernel, micro),
        grid_spec=grid_spec,
        out_shape=[
            jax.ShapeDtypeStruct((micro, rows, F), F32),
            jax.ShapeDtypeStruct((micro, rows, F), BF16),
            jax.ShapeDtypeStruct((micro, rows, 2 * D), BF16),
        ],
        compiler_params=pltpu.CompilerParams(vmem_limit_bytes=48 * 1024 * 1024),
        cost_estimate=pl.CostEstimate(
            flops=4 * work * D * F // 2, bytes_accessed=work * (2 * D + 6 * F + 4 * D) // 2, transcendentals=work * F // 2
        ),
    )(counts, table_in, w1, b1, w2, b2)


def ffn_bwd_kernel(micro, counts, dy_ref, x_ref, hp_ref, h_ref, w1_ref, w2_ref, dt_ref, gu_ref, gd_ref, gb_ref, gb2_ref, gu_acc, gd_acc):
    e, m, t = pl.program_id(0), pl.program_id(1), pl.program_id(2)
    active = t * TILE_B < counts[e * micro + m]

    @pl.when((m == 0) & (t == 0))
    def _():
        gu_acc[...] = jnp.zeros(gu_acc.shape, F32)
        gd_acc[...] = jnp.zeros(gd_acc.shape, F32)
        gb_ref[...] = jnp.zeros(gb_ref.shape, F32)
        gb2_ref[...] = jnp.zeros(gb2_ref.shape, F32)

    @pl.when(active)
    def _():
        dy = dy_ref[0]
        d_hidden = lax.dot_general(dy, w2_ref[0], (((1,), (1,)), ((), ())), preferred_element_type=F32)
        d_pre = (d_hidden * hp_ref[0]).astype(BF16)
        dt = lax.dot_general(d_pre, w1_ref[0], (((1,), (1,)), ((), ())), preferred_element_type=F32)
        hi = dt.astype(BF16)
        dt_ref[0, :, :D] = hi
        dt_ref[0, :, D:] = (dt - hi.astype(F32)).astype(BF16)
        gb2_ref[0] += jnp.sum(dy.astype(F32), 0, keepdims=True)
        gu_acc[...] += lax.dot_general(x_ref[0], d_pre, (((0,), (0,)), ((), ())), preferred_element_type=F32)
        gd_acc[...] += lax.dot_general(h_ref[0], dy, (((0,), (0,)), ((), ())), preferred_element_type=F32)
        gb_ref[0] += jnp.sum(d_pre.astype(F32), 0, keepdims=True)

    @pl.when(jnp.logical_not(active))
    def _():
        dt_ref[0] = jnp.zeros(dt_ref.shape[1:], BF16)

    @pl.when((m == micro - 1) & (t == pl.num_programs(2) - 1))
    def _():
        gu_ref[0] = gu_acc[...].astype(BF16)
        gd_ref[0] = gd_acc[...].astype(BF16)


def ffn_backward(counts, d_expert, table_in, hp, h, w1, w2, micro):
    tiles = CAPP // TILE_B
    rows = table_in.shape[1]
    row_map = lambda e, m, t, c: (m, e * tiles + t, 0)
    w_map = lambda e, m, t, c: (e, 0, 0)
    grid_spec = pltpu.PrefetchScalarGridSpec(
        num_scalar_prefetch=1,
        grid=(E, micro, tiles),
        in_specs=[
            pl.BlockSpec((1, TILE_B, D), row_map),
            pl.BlockSpec((1, TILE_B, D), row_map),
            pl.BlockSpec((1, TILE_B, F), row_map),
            pl.BlockSpec((1, TILE_B, F), row_map),
            pl.BlockSpec((1, D, F), w_map),
            pl.BlockSpec((1, F, D), w_map),
        ],
        out_specs=[
            pl.BlockSpec((1, TILE_B, 2 * D), row_map),
            pl.BlockSpec((1, D, F), w_map),
            pl.BlockSpec((1, F, D), w_map),
            pl.BlockSpec((1, 1, F), w_map),
            pl.BlockSpec((1, 1, D), w_map),
        ],
        scratch_shapes=[pltpu.VMEM((D, F), F32), pltpu.VMEM((F, D), F32)],
    )
    work = micro * rows
    return pl.pallas_call(
        functools.partial(ffn_bwd_kernel, micro),
        grid_spec=grid_spec,
        out_shape=[
            jax.ShapeDtypeStruct((micro, rows, 2 * D), BF16),
            jax.ShapeDtypeStruct((E, D, F), BF16),
            jax.ShapeDtypeStruct((E, F, D), BF16),
            jax.ShapeDtypeStruct((E, 1, F), F32),
            jax.ShapeDtypeStruct((E, 1, D), F32),
        ],
        compiler_params=pltpu.CompilerParams(vmem_limit_bytes=60 * 1024 * 1024),
        cost_estimate=pl.CostEstimate(
            flops=8 * work * D * F // 2, bytes_accessed=work * (8 * D + 6 * F) // 2 + 16 * E * D * F, transcendentals=2 * work * F // 2
        ),
    )(counts, d_expert, table_in, hp, h, w1, w2)

def adamw_kernel(rate, w_ref, m_ref, g_ref, wo_ref, mo_ref):
    g = g_ref[...]
    first = 0.5 * m_ref[0] + 0.5 * g
    root = jnp.sqrt(0.5 * m_ref[1] * m_ref[1] + 0.5 * g * g)
    w = w_ref[...]
    wo_ref[...] = w - rate * (first / (root + 1e-08) + 0.1 * w)
    mo_ref[0] = first
    mo_ref[1] = root


def adamw_pass(weight, moments, grad, rate):
    n, r, c = weight.shape
    spec = pl.BlockSpec((1, r, c), lambda i: (i, 0, 0))
    mspec = pl.BlockSpec((2, 1, r, c), lambda i: (0, i, 0, 0))
    return pl.pallas_call(
        functools.partial(adamw_kernel, rate),
        grid=(n,),
        in_specs=[spec, mspec, spec],
        out_specs=[spec, mspec],
        out_shape=[jax.ShapeDtypeStruct(weight.shape, F32), jax.ShapeDtypeStruct(moments.shape, F32)],
        cost_estimate=pl.CostEstimate(flops=12 * weight.size, bytes_accessed=28 * weight.size, transcendentals=2 * weight.size),
    )(weight, moments, grad)


def layer_norm(value, gain, shift):
    center = value - jnp.mean(value, -1, keepdims=True)
    spread = jnp.mean(center * center, -1, keepdims=True)
    return center * lax.rsqrt(spread + 1e-06) * gain + shift


def gelu_exact(value):
    return jax.nn.gelu(value, approximate=False)


def split_heads(part):
    return part.reshape(-1, S, HEADS, HEAD_DIM)


def dot(a, b):
    return jnp.dot(a, b, preferred_element_type=F32)


def assign_places(route):
    chosen = jnp.concatenate([route[:, :, 0], route[:, :, 1]], 1)
    hits = (chosen[:, :, None] == jnp.arange(E, dtype=jnp.int32)).astype(jnp.int32)
    before = jnp.cumsum(hits, 1) - hits
    slot = jnp.sum(before * hits, 2)
    return chosen * CAPP + slot, jnp.sum(hits, 1)


def hi_lo(v):
    hi = v.astype(BF16)
    lo = (v - hi.astype(F32)).astype(BF16)
    return jnp.concatenate([hi, lo], -1)


def pick_rows(onehot, split):
    both = jnp.einsum("mnr,mrd->mnd", onehot, split, preferred_element_type=F32)
    return both[..., :D] + both[..., D:]


def pack_dense(qkv_w, out_w, router_w, vectors, up_bias):
    rows = qkv_w.shape[0]
    ub = up_bias.reshape(E, rows, 4).transpose(1, 0, 2).reshape(rows, E * 4)
    return jnp.concatenate([qkv_w, out_w, router_w, vectors.T, ub], 1)


def unpack_dense(packed):
    rows = packed.shape[0]
    w_qkv = packed[:, : 3 * D]
    w_out = packed[:, 3 * D : 4 * D]
    w_router = packed[:, 4 * D : 4 * D + E]
    table = packed[:, 4 * D + E : 4 * D + E + NV].T
    ub = packed[:, 4 * D + E + NV :].reshape(rows, E, 4).transpose(1, 0, 2).reshape(E, rows * 4)
    return w_qkv, w_out, w_router, table, ub


def attention_fwd(w_qkv, w_out, table, value):
    rows = value.shape[0]
    scale = HEAD_DIM ** (-0.5)
    first = layer_norm(value, table[0], table[1]).astype(BF16)
    qkv_bias = jnp.concatenate([table[2], jnp.zeros((D,), F32), table[3]])
    qkv = (dot(first, w_qkv) + qkv_bias).astype(BF16)
    query, key_part, val_part = (
        split_heads(qkv[:, :D]),
        split_heads(qkv[:, D : 2 * D]),
        split_heads(qkv[:, 2 * D :]),
    )
    scores = jnp.einsum("bqhd,bkhd->bhqk", query, key_part, preferred_element_type=F32) * scale
    peak = jnp.max(scores, -1, keepdims=True)
    expo = jnp.exp(scores - peak)
    total = jnp.sum(expo, -1, keepdims=True)
    probs_att = (expo / total).astype(BF16)
    log_total = peak + jnp.log(total)
    attended = jnp.einsum("bhqk,bkhd->bqhd", probs_att, val_part, preferred_element_type=F32)
    attended = attended.reshape(rows, D).astype(BF16)
    resid = value + (dot(attended, w_out) + table[4])
    return first, qkv, log_total, attended, resid


def attention_bwd(w_qkv, w_out, table, value, first, qkv, log_total, attended, d_resid):
    rows = value.shape[0]
    scale = HEAD_DIM ** (-0.5)
    d_branch = d_resid.astype(BF16)
    g_bias_out = jnp.sum(d_branch.astype(F32), 0)
    g_out = lax.dot_general(attended, d_branch, (((0,), (0,)), ((), ())), preferred_element_type=F32)
    d_att = split_heads(
        lax.dot_general(d_branch, w_out, (((1,), (1,)), ((), ())), preferred_element_type=F32).astype(BF16)
    )
    query, key_part, val_part = (
        split_heads(qkv[:, :D]),
        split_heads(qkv[:, D : 2 * D]),
        split_heads(qkv[:, 2 * D :]),
    )
    scores = jnp.einsum("bqhd,bkhd->bhqk", query, key_part, preferred_element_type=F32) * scale
    probs_f = jnp.exp(scores - log_total)
    probs_att = probs_f.astype(BF16)
    d_val = jnp.einsum("bhqk,bqhd->bkhd", probs_att, d_att, preferred_element_type=F32)
    d_prob = jnp.einsum("bqhd,bkhd->bhqk", d_att, val_part, preferred_element_type=F32)
    d_score = (probs_f * (d_prob - jnp.sum(d_prob * probs_f, -1, keepdims=True))).astype(BF16)
    d_query = jnp.einsum("bhqk,bkhd->bqhd", d_score, key_part, preferred_element_type=F32) * scale
    d_key = jnp.einsum("bhqk,bqhd->bkhd", d_score, query, preferred_element_type=F32) * scale
    d_qkv = jnp.concatenate(
        [d_query.reshape(rows, D), d_key.reshape(rows, D), d_val.reshape(rows, D)], 1
    ).astype(BF16)
    d_qkv_f = d_qkv.astype(F32)
    g_bias_q = jnp.sum(d_qkv_f[:, :D], 0)
    g_bias_v = jnp.sum(d_qkv_f[:, 2 * D :], 0)
    g_qkv = lax.dot_general(first, d_qkv, (((0,), (0,)), ((), ())), preferred_element_type=F32)
    d_first = lax.dot_general(d_qkv, w_qkv, (((1,), (1,)), ((), ())), preferred_element_type=F32)
    first_pull = jax.vjp(layer_norm, value, table[0], table[1])[1]
    d_input, g_gain_one, g_shift_one = first_pull(d_first)
    return (g_qkv, g_out, g_bias_out, g_bias_q, g_bias_v, g_gain_one, g_shift_one), d_input


def adamw(weight, moments, grad, rate):
    first = 0.5 * moments[0] + 0.5 * grad
    root = jnp.sqrt(0.5 * moments[1] * moments[1] + 0.5 * grad * grad)
    update = first / (root + 1e-08)
    which = lax.broadcasted_iota(jnp.int32, moments.shape, 0) == 0
    both = jnp.where(which, 0.5 * moments + 0.5 * grad, jnp.sqrt(0.5 * moments * moments + 0.5 * grad * grad))
    return (weight - rate * (update + 0.1 * weight), both)


def shards(
    tokens,
    cotangent,
    expert_index,
    qkv_weight,
    out_weight,
    router_weight,
    up_weight,
    up_bias,
    down_weight,
    vectors,
    qkv_moments,
    out_moments,
    router_moments,
    up_moments,
    up_bias_moments,
    down_moments,
    vector_moments,
):
    rows = tokens.shape[0]
    micro = rows // MB_TOK
    gs = qkv_weight.shape[0]
    group_size = D // gs
    core = lax.axis_index("core")

    dense_in = pack_dense(qkv_weight, out_weight, router_weight, vectors, up_bias)
    width = dense_in.shape[1]
    dense_in = jnp.pad(dense_in, ((0, 0), (0, DENSE_AG - width))).astype(BF16)
    w_up_all, w_down_all, dense = ring_all_gather(
        up_weight.astype(BF16), down_weight.astype(BF16), dense_in, group_size, 1
    )
    w_qkv, w_out, w_router, table_b, b_up_b = unpack_dense(dense[:, :width])
    table = table_b.astype(F32)
    b_up = b_up_b.astype(F32)

    value = tokens.astype(F32)
    d_out = cotangent.astype(F32)
    first, qkv, log_total, attended, resid = attention_fwd(w_qkv, w_out, table, value)
    second = layer_norm(resid, table[5], table[6]).astype(BF16)
    logits = dot(second, w_router)
    probs = jax.nn.softmax(logits, -1)
    picked = expert_index[:, :, None] == jnp.arange(E, dtype=jnp.int32)
    gate = jnp.sum(jnp.where(picked, probs[:, None, :], 0.0), -1)

    route = expert_index.reshape(micro, MB_TOK, 2)
    places, counts = assign_places(route)
    counts = counts.T.reshape(E * micro)
    onehot = (places[:, :, None] == jnp.arange(E * CAPP, dtype=jnp.int32)).astype(BF16)
    second_m = second.reshape(micro, MB_TOK, D)
    onehot_sum = onehot[:, :MB_TOK] + onehot[:, MB_TOK:]
    table_in = jnp.einsum("mnr,mnd->mrd", onehot_sum, second_m, preferred_element_type=F32).astype(BF16)

    hidden_pre, hidden, y_all = ffn_forward(
        counts, table_in, w_up_all, b_up[:, None, :], w_down_all, table[7 : 7 + E][:, None, :], micro
    )
    picked_rows = pick_rows(onehot, y_all)
    out_zero = picked_rows[:, :MB_TOK].reshape(rows, D)
    out_one = picked_rows[:, MB_TOK:].reshape(rows, D)
    result = resid + (gate[:, 0:1] * out_zero + gate[:, 1:2] * out_one)

    d_gate = jnp.stack([jnp.sum(d_out * out_zero, -1), jnp.sum(d_out * out_one, -1)], 1)
    d_out_m = d_out.reshape(micro, MB_TOK, D)
    gate_m = gate.reshape(micro, MB_TOK, 2)
    weighted = jnp.concatenate([gate_m[:, :, 0:1] * d_out_m, gate_m[:, :, 1:2] * d_out_m], 1).astype(BF16)
    d_expert = jnp.einsum("mnr,mnd->mrd", onehot, weighted, preferred_element_type=F32).astype(BF16)

    d_table, g_up, g_down, g_b1, g_b2 = ffn_backward(counts, d_expert, table_in, hidden_pre, hidden, w_up_all, w_down_all, micro)
    g_up_bias_all = g_b1[:, 0, :]
    g_bias_down = g_b2[:, 0, :]

    d_picked = pick_rows(onehot_sum, d_table).reshape(rows, D)

    d_probs = jnp.sum(jnp.where(picked, d_gate[:, :, None], 0.0), 1)
    d_logit = (probs * (d_probs - jnp.sum(d_probs * probs, -1, keepdims=True))).astype(BF16)
    g_router = lax.dot_general(second, d_logit, (((0,), (0,)), ((), ())), preferred_element_type=F32)
    d_second = d_picked + lax.dot_general(d_logit, w_router, (((1,), (1,)), ((), ())), preferred_element_type=F32)
    norm_pull = jax.vjp(layer_norm, resid, table[5], table[6])[1]
    d_resid, g_gain_two, g_shift_two = norm_pull(d_second)
    d_resid = d_out + d_resid

    att_grads, d_input = attention_bwd(w_qkv, w_out, table, value, first, qkv, log_total, attended, d_resid)
    g_qkv, g_out, g_bias_out, g_bias_q, g_bias_v, g_gain_one, g_shift_one = att_grads
    input_grad = d_resid + d_input

    g_table = jnp.concatenate(
        [
            jnp.stack([g_gain_one, g_shift_one, g_bias_q, g_bias_v, g_bias_out, g_gain_two, g_shift_two]),
            g_bias_down,
        ],
        0,
    )
    dense_g = pack_dense(g_qkv, g_out, g_router, g_table, g_up_bias_all)
    width = dense_g.shape[1]
    dense_g = jnp.pad(dense_g, ((0, 0), (0, DENSE_AG - width))).astype(BF16)
    x_pair = lax.axis_size("rx") == 2
    r_up, r_down, r_dense = grad_reduce(g_up, g_down, dense_g, group_size, x_pair, 0)
    if not x_pair:
        r_up, r_down, r_dense = lax.psum((r_up, r_down, r_dense), "rx")
    r_qkv, r_out, r_router, r_table, r_ub = unpack_dense(r_dense[:, :width])

    reduced = (r_qkv, r_out, r_router, r_up, r_ub, r_down, r_table)
    rates = (
        2.0 * D ** (-0.5),
        2.0 * (D // 32) ** (-0.5),
        2.0 * (2 * D) ** (-0.5),
        2.0 * D ** (-0.5),
        0.2,
        2.0 * (F // 16) ** (-0.5),
        0.2,
    )
    params = (qkv_weight, out_weight, router_weight, up_weight, up_bias, down_weight, vectors)
    moments = (qkv_moments, out_moments, router_moments, up_moments, up_bias_moments, down_moments, vector_moments)
    news = []
    states = []
    for weight, state, grad, rate in zip(params, moments, reduced, rates):
        if weight.ndim == 3:
            new_weight, new_state = adamw_pass(weight, state, grad, rate)
        else:
            new_weight, new_state = adamw(weight, state, grad, rate)
        news.append(new_weight)
        states.append(new_state)
    return (result.astype(BF16), input_grad) + reduced + tuple(news) + tuple(states)


def solution(mesh):
    replica, group = mesh.shape["replica"], mesh.shape["group"]
    view = Mesh(np.asarray(mesh.devices).reshape(replica // 2, 2, group), ("rx", "core", "group"))
    in_specs = (
        P(TOK, None),
        P(TOK, None),
        P(TOK, None),
        P("group", None),
        P("group", None),
        P("group", None),
        P(None, "group", None),
        P(None, "group"),
        P(None, "group", None),
        P(None, "group"),
        P(None, "group", None),
        P(None, "group", None),
        P(None, "group", None),
        P(None, None, "group", None),
        P(None, None, "group"),
        P(None, None, "group", None),
        P(None, None, "group"),
    )
    out_specs = (
        P(TOK, None),
        P(TOK, None),
        P("group", None),
        P("group", None),
        P("group", None),
        P(None, "group", None),
        P(None, "group"),
        P(None, "group", None),
        P(None, "group"),
        P("group", None),
        P("group", None),
        P("group", None),
        P(None, "group", None),
        P(None, "group"),
        P(None, "group", None),
        P(None, "group"),
        P(None, "group", None),
        P(None, "group", None),
        P(None, "group", None),
        P(None, None, "group", None),
        P(None, None, "group"),
        P(None, None, "group", None),
        P(None, None, "group"),
    )
    return jax.shard_map(shards, mesh=view, in_specs=in_specs, out_specs=out_specs, check_vma=False)
```

```python
import functools

import jax
import jax.numpy as jnp
import numpy as np
from jax import lax
from jax.sharding import Mesh
from jax.sharding import PartitionSpec as P
from jax.experimental import pallas as pl
from jax.experimental.pallas import tpu as pltpu

D = 512
HEADS = 8
HEAD_DIM = 64
F = 2048
E = 4
S = 197
MB_TOK = 394
CAP = 392
NV = 11
DENSE_AG = 2560
DENSE_PAD = 2304
F32 = jnp.float32
BF16 = jnp.bfloat16
TOK = ("rx", "core", "group")


MESH_ID = pl.DeviceIdType.MESH


def ring_order(groups):
    if groups in (4, 8):
        zs = groups // 2

        def pos_of(g):
            y = g % 2
            z = g // 2
            return z + y * (2 * zs - 1 - 2 * z)

        def dev_at(p):
            p = p % groups
            yy = p // zs
            return 2 * (p + yy * (2 * zs - 1 - 2 * p)) + yy

        return pos_of, dev_at
    return (lambda g: g), (lambda p: p % groups)


def ring_rs_kernel(groups, n_in, *refs):
    ins = refs[:n_in]
    outs = refs[n_in : 2 * n_in]
    rbufs = refs[2 * n_in : 3 * n_in]
    sbufs = refs[3 * n_in : 4 * n_in]
    owns = refs[4 * n_in : 5 * n_in]
    send_sem, recv_sem, load_sem = refs[5 * n_in :]
    pos_of, dev_at = ring_order(groups)
    rx = lax.axis_index("rx")
    core = lax.axis_index("core")
    g = lax.axis_index("group")
    pos = pos_of(g)
    nbr = (dev_at(pos + 1), dev_at(pos + groups - 1))

    barrier = pltpu.get_barrier_semaphore()
    for n in nbr:
        pl.semaphore_signal(barrier, inc=1, device_id=(rx, core, n), device_id_type=MESH_ID)
    pl.semaphore_wait(barrier, 2)

    def block_dev(d, s):
        if d == 0:
            return dev_at(pos + 2 * groups - s - 1)
        return dev_at(pos + s + 1)

    def load(d, s, slot):
        b = block_dev(d, s)
        copies = []
        for i in range(n_in):
            rows = ins[i].shape[1] // groups
            half = ins[i].shape[2] // 2
            src = ins[i].at[:, pl.ds(pl.multiple_of(b * rows, rows), rows), pl.ds(d * half, half)]
            copies.append(pltpu.make_async_copy(src, owns[i].at[d, slot], load_sem.at[d, slot, i]))
        return copies

    def remote(d, s, i):
        return pltpu.make_async_remote_copy(
            src_ref=sbufs[i].at[d, s],
            dst_ref=rbufs[i].at[d, s],
            send_sem=send_sem.at[d, s, i],
            recv_sem=recv_sem.at[d, s, i],
            device_id=(rx, core, nbr[d]),
            device_id_type=MESH_ID,
        )

    for d in range(2):
        for c in load(d, 0, 0):
            c.start()
    sends = []
    for s in range(groups):
        slot = s % 2
        for d in range(2):
            for c in load(d, s, slot):
                c.wait()
            if s + 1 < groups:
                for c in load(d, s + 1, 1 - slot):
                    c.start()
            for i in range(n_in):
                if s > 0:
                    remote(d, s - 1, i).wait_recv()
                for a in range(ins[i].shape[0]):
                    mine = owns[i][d, slot, a].astype(F32)
                    if s > 0:
                        mine = mine + rbufs[i][d, s - 1, a].astype(F32)
                    if s < groups - 1:
                        sbufs[i][d, s, a] = mine.astype(sbufs[i].dtype)
                    else:
                        half = ins[i].shape[2] // 2
                        outs[i][a, :, pl.ds(d * half, half)] = mine.astype(outs[i].dtype)
                if s < groups - 1:
                    c = remote(d, s, i)
                    c.start()
                    sends.append(c)
    for c in sends:
        c.wait_send()


def ring_reduce_scatter(xs, groups, collective_id):
    n_in = len(xs)
    outs, rb, own = [], [], []
    flops = 0
    nbytes = 0
    for x in xs:
        a, total, c = x.shape
        rows = total // groups
        outs.append(jax.ShapeDtypeStruct((a, rows, c), x.dtype))
        rb.append(pltpu.VMEM((2, groups - 1, a, rows, c // 2), x.dtype))
        own.append(pltpu.VMEM((2, 2, a, rows, c // 2), x.dtype))
        flops += a * total * c
        nbytes += 3 * x.size * x.dtype.itemsize
    scratch = rb + rb + own + [
        pltpu.SemaphoreType.DMA((2, groups - 1, n_in)),
        pltpu.SemaphoreType.DMA((2, groups - 1, n_in)),
        pltpu.SemaphoreType.DMA((2, 2, n_in)),
    ]
    return pl.pallas_call(
        functools.partial(ring_rs_kernel, groups, n_in),
        out_shape=outs,
        in_specs=[pl.BlockSpec(memory_space=pl.ANY)] * n_in,
        out_specs=[pl.BlockSpec(memory_space=pltpu.VMEM)] * n_in,
        scratch_shapes=scratch,
        compiler_params=pltpu.CompilerParams(
            collective_id=collective_id, has_side_effects=True, vmem_limit_bytes=60 * 1024 * 1024
        ),
        cost_estimate=pl.CostEstimate(flops=flops, bytes_accessed=nbytes, transcendentals=0),
    )(*xs)


def ring_ag_kernel(groups, *refs):
    in_up, in_down, in_dense, out_up, out_down, out_dense = refs[:6]
    ring_send, ring_recv, part_send, part_recv, local_sem = refs[6:]
    pos_of, dev_at = ring_order(groups)
    rx = lax.axis_index("rx")
    core = lax.axis_index("core")
    g = lax.axis_index("group")
    other = 1 - core
    pos = pos_of(g)
    nbr = (dev_at(pos + 1), dev_at(pos + groups - 1))
    gs = in_up.shape[1]
    fs = in_down.shape[1]
    width = in_dense.shape[1] // 2

    barrier = pltpu.get_barrier_semaphore()
    for n in nbr:
        pl.semaphore_signal(barrier, inc=1, device_id=(rx, core, n), device_id_type=MESH_ID)
    pl.semaphore_signal(barrier, inc=1, device_id=(rx, other, g), device_id_type=MESH_ID)
    pl.semaphore_wait(barrier, 3)

    def items(owner):
        found = []
        for k in range(2):
            e = 2 * k + owner
            found.append((in_up.at[e], lambda b, e=e: out_up.at[e, pl.ds(pl.multiple_of(b * gs, gs), gs)], F // 2))
            found.append((in_down.at[e], lambda b, e=e: out_down.at[e, pl.ds(pl.multiple_of(b * fs, fs), fs)], D // 2))
        dense_in = in_dense.at[:, pl.ds(owner * width, width)]
        found.append(
            (dense_in, lambda b: out_dense.at[pl.ds(pl.multiple_of(b * gs, gs), gs), pl.ds(owner * width, width)], width // 2)
        )
        return found

    mine = items(core)
    theirs = items(other)
    n_items = len(mine)

    locals_ = [pltpu.make_async_copy(in_up.at[e], out_up.at[e, pl.ds(pl.multiple_of(g * gs, gs), gs)], local_sem.at[e]) for e in range(E)]
    locals_ += [
        pltpu.make_async_copy(in_down.at[e], out_down.at[e, pl.ds(pl.multiple_of(g * fs, fs), fs)], local_sem.at[E + e])
        for e in range(E)
    ]
    locals_.append(pltpu.make_async_copy(in_dense, out_dense.at[pl.ds(pl.multiple_of(g * gs, gs), gs)], local_sem.at[2 * E]))
    for c in locals_:
        c.start()

    def block_at(d, s):
        if d == 0:
            return dev_at(pos + 2 * groups - 1 - s)
        return dev_at(pos + 1 + s)

    def ring_copy(d, s, j, src_block):
        src_in, dst_of, half = mine[j]
        cols = pl.ds(d * half, half)
        if src_block is None:
            src = src_in.at[:, cols]
            dst = dst_of(g).at[:, cols]
        else:
            src = dst_of(src_block).at[:, cols]
            dst = src
        return pltpu.make_async_remote_copy(
            src_ref=src, dst_ref=dst, send_sem=ring_send.at[d, s, j], recv_sem=ring_recv.at[d, s, j],
            device_id=(rx, core, nbr[d]), device_id_type=MESH_ID,
        )

    def part_copy(d, s, j, table, block):
        _, dst_of, half = table[j]
        view = dst_of(block).at[:, pl.ds(d * half, half)]
        return pltpu.make_async_remote_copy(
            src_ref=view, dst_ref=view, send_sem=part_send.at[d, s, j], recv_sem=part_recv.at[d, s, j],
            device_id=(rx, other, g), device_id_type=MESH_ID,
        )

    sends = []
    for d in range(2):
        for j in range(n_items):
            c = ring_copy(d, 0, j, None)
            c.start()
            sends.append(c)
    for s in range(groups - 1):
        for d in range(2):
            b = block_at(d, s)
            for j in range(n_items):
                pltpu.make_async_remote_copy(
                    src_ref=mine[j][1](b).at[:, pl.ds(d * mine[j][2], mine[j][2])],
                    dst_ref=mine[j][1](b).at[:, pl.ds(d * mine[j][2], mine[j][2])],
                    send_sem=ring_send.at[d, s, j], recv_sem=ring_recv.at[d, s, j],
                    device_id=(rx, core, nbr[d]), device_id_type=MESH_ID,
                ).wait_recv()
                if s + 1 < groups - 1:
                    c = ring_copy(d, s + 1, j, b)
                    c.start()
                    sends.append(c)
                c = part_copy(d, s, j, mine, b)
                c.start()
                sends.append(c)
    for s in range(groups - 1):
        for d in range(2):
            b = block_at(d, s)
            for j in range(n_items):
                part_copy(d, s, j, theirs, b).wait_recv()
    for c in sends:
        c.wait_send()
    for c in locals_:
        c.wait()


def ring_all_gather(up_b, down_b, dense_b, groups, collective_id):
    n_items = 5
    gs = up_b.shape[1]
    shapes = [
        jax.ShapeDtypeStruct((E, gs * groups, F), BF16),
        jax.ShapeDtypeStruct((E, down_b.shape[1] * groups, D), BF16),
        jax.ShapeDtypeStruct((gs * groups, dense_b.shape[1]), BF16),
    ]
    nbytes = sum(int(np.prod(s.shape)) * 2 for s in shapes)
    return pl.pallas_call(
        functools.partial(ring_ag_kernel, groups),
        out_shape=shapes,
        in_specs=[pl.BlockSpec(memory_space=pltpu.VMEM)] * 3,
        out_specs=[pl.BlockSpec(memory_space=pl.ANY)] * 3,
        scratch_shapes=[
            pltpu.SemaphoreType.DMA((2, groups - 1, n_items)),
            pltpu.SemaphoreType.DMA((2, groups - 1, n_items)),
            pltpu.SemaphoreType.DMA((2, groups - 1, n_items)),
            pltpu.SemaphoreType.DMA((2, groups - 1, n_items)),
            pltpu.SemaphoreType.DMA((2 * E + 1,)),
        ],
        compiler_params=pltpu.CompilerParams(collective_id=collective_id, has_side_effects=True),
        cost_estimate=pl.CostEstimate(flops=0, bytes_accessed=nbytes, transcendentals=0),
    )(up_b, down_b, dense_b)


def grad_items(gu, gd, gdense, owner, gs, fs, width):
    found = []
    for k in range(2):
        e = 2 * k + owner
        found.append((lambda b, e=e: gu.at[e, pl.ds(pl.multiple_of(b * gs, gs), gs)], F // 2))
        found.append((lambda b, e=e: gd.at[e, pl.ds(pl.multiple_of(b * fs, fs), fs)], D // 2))
    found.append((lambda b: gdense.at[pl.ds(pl.multiple_of(b * gs, gs), gs), pl.ds(owner * width, width)], width // 2))
    return found


def ring_rs2_kernel(groups, x_pair, *refs):
    gu, gd, gdense, out_up, out_down, out_dense = refs[:6]
    n_items = 5
    scr = refs[6:]
    rbuf, sbuf, pbuf, own, fin, xr, cr, xs = (scr[i * n_items : (i + 1) * n_items] for i in range(8))
    ring_send, ring_recv, part_send, part_recv, load_sem, x_send, x_recv, c_send, c_recv = scr[8 * n_items :]
    pos_of, dev_at = ring_order(groups)
    rx = lax.axis_index("rx")
    core = lax.axis_index("core")
    g = lax.axis_index("group")
    other = 1 - core
    pos = pos_of(g)
    nbr = (dev_at(pos + 1), dev_at(pos + groups - 1))
    gs = gu.shape[1] // groups
    fs = gd.shape[1] // groups
    width = gdense.shape[1] // 2
    mine = grad_items(gu, gd, gdense, core, gs, fs, width)
    theirs = grad_items(gu, gd, gdense, other, gs, fs, width)

    barrier = pltpu.get_barrier_semaphore()
    for n in nbr:
        pl.semaphore_signal(barrier, inc=1, device_id=(rx, core, n), device_id_type=MESH_ID)
    pl.semaphore_signal(barrier, inc=1, device_id=(rx, other, g), device_id_type=MESH_ID)
    count = 3
    if x_pair:
        pl.semaphore_signal(barrier, inc=1, device_id=(1 - rx, core, g), device_id_type=MESH_ID)
        count = 4
    pl.semaphore_wait(barrier, count)

    def block_at(d, s):
        if d == 0:
            return dev_at(pos + 2 * groups - 1 - s)
        return dev_at(pos + 1 + s)

    def cols(j, d):
        half = mine[j][1]
        return pl.ds(d * half, half)

    def load(d, s, slot, j):
        return pltpu.make_async_copy(mine[j][0](block_at(d, s)).at[:, cols(j, d)], own[j].at[d, slot], load_sem.at[d, slot, j])

    def part(d, s, j):
        return pltpu.make_async_remote_copy(
            src_ref=theirs[j][0](block_at(d, s)).at[:, cols(j, d)], dst_ref=pbuf[j].at[d, s],
            send_sem=part_send.at[d, s, j], recv_sem=part_recv.at[d, s, j],
            device_id=(rx, other, g), device_id_type=MESH_ID,
        )

    def ring(d, s, j):
        return pltpu.make_async_remote_copy(
            src_ref=sbuf[j].at[d, s], dst_ref=rbuf[j].at[d, s],
            send_sem=ring_send.at[d, s, j], recv_sem=ring_recv.at[d, s, j],
            device_id=(rx, core, nbr[d]), device_id_type=MESH_ID,
        )

    sends = []

    def ring_wave(items):
        for d in range(2):
            for j in items:
                load(d, 0, 0, j).start()
                c = part(d, 0, j)
                c.start()
                sends.append(c)
        for s in range(groups):
            slot = s % 2
            for d in range(2):
                for j in items:
                    load(d, s, slot, j).wait()
                    if s + 1 < groups:
                        load(d, s + 1, 1 - slot, j).start()
                        c = part(d, s + 1, j)
                        c.start()
                        sends.append(c)
                    part(d, s, j).wait_recv()
                    val = own[j][d, slot].astype(F32) + pbuf[j][d, s].astype(F32)
                    if s > 0:
                        ring(d, s - 1, j).wait_recv()
                        val = val + rbuf[j][d, s - 1].astype(F32)
                    if s < groups - 1:
                        sbuf[j][d, s] = val.astype(BF16)
                        c = ring(d, s, j)
                        c.start()
                        sends.append(c)
                    else:
                        fin[j][d] = val

    def x_start(items):
        copies = []
        for d in range(2):
            for j in items:
                xs[j][d] = fin[j][d].astype(BF16)
                c = pltpu.make_async_remote_copy(
                    src_ref=xs[j].at[d], dst_ref=xr[j].at[d], send_sem=x_send.at[d, j], recv_sem=x_recv.at[d, j],
                    device_id=(1 - rx, core, g), device_id_type=MESH_ID,
                )
                c.start()
                copies.append(c)
        sends.extend(copies)
        return copies

    def x_finish(items, copies):
        for c in copies:
            c.wait_recv()
        for d in range(2):
            for j in items:
                fin[j][d] = xs[j][d].astype(F32) + xr[j][d].astype(F32)

    def c_start(items):
        copies = []
        for d in range(2):
            for j in items:
                c = pltpu.make_async_remote_copy(
                    src_ref=fin[j].at[d], dst_ref=cr[j].at[d], send_sem=c_send.at[d, j], recv_sem=c_recv.at[d, j],
                    device_id=(rx, other, g), device_id_type=MESH_ID,
                )
                c.start()
                copies.append(c)
        return copies

    wave_a, wave_b = (0, 1, 2, 4), (3,)
    ring_wave(wave_a)
    if x_pair:
        xa = x_start(wave_a)
    ring_wave(wave_b)
    if x_pair:
        x_finish(wave_a, xa)
    c_copies = c_start(wave_a)
    if x_pair:
        x_finish(wave_b, x_start(wave_b))
    c_copies += c_start(wave_b)

    def out_items(owner):
        found = []
        for k in range(2):
            e = 2 * k + owner
            found.append(lambda d, e=e: out_up.at[e, :, pl.ds(d * (F // 2), F // 2)])
            found.append(lambda d, e=e: out_down.at[e, :, pl.ds(d * (D // 2), D // 2)])
        found.append(lambda d: out_dense.at[:, pl.ds(owner * width + d * (width // 2), width // 2)])
        return found

    mine_out = out_items(core)
    theirs_out = out_items(other)
    for d in range(2):
        for j in range(n_items):
            mine_out[j](d)[...] = fin[j][d]
    for c in c_copies:
        c.wait_recv()
    for d in range(2):
        for j in range(n_items):
            theirs_out[j](d)[...] = cr[j][d]
    for c in sends + c_copies:
        c.wait_send()


def grad_reduce(gu, gd, gdense, groups, x_pair, collective_id):
    gs = gu.shape[1] // groups
    fs = gd.shape[1] // groups
    width = gdense.shape[1] // 2
    item_shapes = [(gs, F // 2), (fs, D // 2), (gs, F // 2), (fs, D // 2), (gs, width // 2)]
    scratch = []
    for lead, dtype in (((2, groups - 1), BF16), ((2, groups - 1), BF16), ((2, groups), BF16), ((2, 2), BF16), ((2,), F32), ((2,), BF16), ((2,), F32), ((2,), BF16)):
        scratch += [pltpu.VMEM(lead + shp, dtype) for shp in item_shapes]
    scratch += [
        pltpu.SemaphoreType.DMA((2, groups - 1, 5)),
        pltpu.SemaphoreType.DMA((2, groups - 1, 5)),
        pltpu.SemaphoreType.DMA((2, groups, 5)),
        pltpu.SemaphoreType.DMA((2, groups, 5)),
        pltpu.SemaphoreType.DMA((2, 2, 5)),
        pltpu.SemaphoreType.DMA((2, 5)),
        pltpu.SemaphoreType.DMA((2, 5)),
        pltpu.SemaphoreType.DMA((2, 5)),
        pltpu.SemaphoreType.DMA((2, 5)),
    ]
    outs = [
        jax.ShapeDtypeStruct((E, gs, F), F32),
        jax.ShapeDtypeStruct((E, fs, D), F32),
        jax.ShapeDtypeStruct((gs, gdense.shape[1]), F32),
    ]
    nbytes = 2 * (gu.size + gd.size + gdense.size)
    return pl.pallas_call(
        functools.partial(ring_rs2_kernel, groups, x_pair),
        out_shape=outs,
        in_specs=[pl.BlockSpec(memory_space=pl.ANY)] * 3,
        out_specs=[pl.BlockSpec(memory_space=pltpu.VMEM)] * 3,
        scratch_shapes=scratch,
        compiler_params=pltpu.CompilerParams(
            collective_id=collective_id, has_side_effects=True, vmem_limit_bytes=62 * 1024 * 1024
        ),
        cost_estimate=pl.CostEstimate(flops=gu.size + gd.size + gdense.size, bytes_accessed=nbytes, transcendentals=0),
    )(gu, gd, gdense)


TILE = 256
TILE_B = 256
CAPP = 512
SQRT_HALF = float(np.sqrt(0.5))
INV_SQRT_2PI = float(1.0 / np.sqrt(2.0 * np.pi))


def ffn_fwd_kernel(micro, counts, x_ref, w1_ref, b1_ref, w2_ref, b2_ref, hp_ref, h_ref, y_ref):
    e, m, t = pl.program_id(0), pl.program_id(1), pl.program_id(2)
    active = t * TILE < counts[e * micro + m]

    @pl.when(active)
    def _():
        hp = jnp.dot(x_ref[0], w1_ref[0], preferred_element_type=F32) + b1_ref[0]
        cdf = 0.5 * (1.0 + lax.erf(hp * SQRT_HALF))
        h = (hp * cdf).astype(BF16)
        hp_ref[0] = cdf + hp * jnp.exp(-0.5 * hp * hp) * INV_SQRT_2PI
        h_ref[0] = h
        y = jnp.dot(h, w2_ref[0], preferred_element_type=F32) + b2_ref[0]
        hi = y.astype(BF16)
        y_ref[0, :, :D] = hi
        y_ref[0, :, D:] = (y - hi.astype(F32)).astype(BF16)

    @pl.when(jnp.logical_not(active))
    def _():
        y_ref[0] = jnp.zeros(y_ref.shape[1:], BF16)


def ffn_forward(counts, table_in, w1, b1, w2, b2, micro):
    tiles = CAPP // TILE
    rows = table_in.shape[1]
    row_map = lambda e, m, t, c: (m, e * tiles + t, 0)
    w_map = lambda e, m, t, c: (e, 0, 0)
    grid_spec = pltpu.PrefetchScalarGridSpec(
        num_scalar_prefetch=1,
        grid=(E, micro, tiles),
        in_specs=[
            pl.BlockSpec((1, TILE, D), row_map),
            pl.BlockSpec((1, D, F), w_map),
            pl.BlockSpec((1, 1, F), w_map),
            pl.BlockSpec((1, F, D), w_map),
            pl.BlockSpec((1, 1, D), w_map),
        ],
        out_specs=[
            pl.BlockSpec((1, TILE, F), row_map),
            pl.BlockSpec((1, TILE, F), row_map),
            pl.BlockSpec((1, TILE, 2 * D), row_map),
        ],
    )
    work = micro * rows
    return pl.pallas_call(
        functools.partial(ffn_fwd_kernel, micro),
        grid_spec=grid_spec,
        out_shape=[
            jax.ShapeDtypeStruct((micro, rows, F), F32),
            jax.ShapeDtypeStruct((micro, rows, F), BF16),
            jax.ShapeDtypeStruct((micro, rows, 2 * D), BF16),
        ],
        compiler_params=pltpu.CompilerParams(vmem_limit_bytes=48 * 1024 * 1024),
        cost_estimate=pl.CostEstimate(
            flops=4 * work * D * F // 2, bytes_accessed=work * (2 * D + 6 * F + 4 * D) // 2, transcendentals=work * F // 2
        ),
    )(counts, table_in, w1, b1, w2, b2)


def ffn_bwd_kernel(micro, counts, dy_ref, x_ref, hp_ref, h_ref, w1_ref, w2_ref, dt_ref, gu_ref, gd_ref, gb_ref, gb2_ref, gu_acc, gd_acc):
    e, m, t = pl.program_id(0), pl.program_id(1), pl.program_id(2)
    active = t * TILE_B < counts[e * micro + m]

    @pl.when((m == 0) & (t == 0))
    def _():
        gu_acc[...] = jnp.zeros(gu_acc.shape, F32)
        gd_acc[...] = jnp.zeros(gd_acc.shape, F32)
        gb_ref[...] = jnp.zeros(gb_ref.shape, F32)
        gb2_ref[...] = jnp.zeros(gb2_ref.shape, F32)

    @pl.when(active)
    def _():
        dy = dy_ref[0]
        d_hidden = lax.dot_general(dy, w2_ref[0], (((1,), (1,)), ((), ())), preferred_element_type=F32)
        d_pre = (d_hidden * hp_ref[0]).astype(BF16)
        dt = lax.dot_general(d_pre, w1_ref[0], (((1,), (1,)), ((), ())), preferred_element_type=F32)
        hi = dt.astype(BF16)
        dt_ref[0, :, :D] = hi
        dt_ref[0, :, D:] = (dt - hi.astype(F32)).astype(BF16)
        gb2_ref[0] += jnp.sum(dy.astype(F32), 0, keepdims=True)
        gu_acc[...] += lax.dot_general(x_ref[0], d_pre, (((0,), (0,)), ((), ())), preferred_element_type=F32)
        gd_acc[...] += lax.dot_general(h_ref[0], dy, (((0,), (0,)), ((), ())), preferred_element_type=F32)
        gb_ref[0] += jnp.sum(d_pre.astype(F32), 0, keepdims=True)

    @pl.when(jnp.logical_not(active))
    def _():
        dt_ref[0] = jnp.zeros(dt_ref.shape[1:], BF16)

    @pl.when((m == micro - 1) & (t == pl.num_programs(2) - 1))
    def _():
        gu_ref[0] = gu_acc[...].astype(BF16)
        gd_ref[0] = gd_acc[...].astype(BF16)


def ffn_backward(counts, d_expert, table_in, hp, h, w1, w2, micro):
    tiles = CAPP // TILE_B
    rows = table_in.shape[1]
    row_map = lambda e, m, t, c: (m, e * tiles + t, 0)
    w_map = lambda e, m, t, c: (e, 0, 0)
    grid_spec = pltpu.PrefetchScalarGridSpec(
        num_scalar_prefetch=1,
        grid=(E, micro, tiles),
        in_specs=[
            pl.BlockSpec((1, TILE_B, D), row_map),
            pl.BlockSpec((1, TILE_B, D), row_map),
            pl.BlockSpec((1, TILE_B, F), row_map),
            pl.BlockSpec((1, TILE_B, F), row_map),
            pl.BlockSpec((1, D, F), w_map),
            pl.BlockSpec((1, F, D), w_map),
        ],
        out_specs=[
            pl.BlockSpec((1, TILE_B, 2 * D), row_map),
            pl.BlockSpec((1, D, F), w_map),
            pl.BlockSpec((1, F, D), w_map),
            pl.BlockSpec((1, 1, F), w_map),
            pl.BlockSpec((1, 1, D), w_map),
        ],
        scratch_shapes=[pltpu.VMEM((D, F), F32), pltpu.VMEM((F, D), F32)],
    )
    work = micro * rows
    return pl.pallas_call(
        functools.partial(ffn_bwd_kernel, micro),
        grid_spec=grid_spec,
        out_shape=[
            jax.ShapeDtypeStruct((micro, rows, 2 * D), BF16),
            jax.ShapeDtypeStruct((E, D, F), BF16),
            jax.ShapeDtypeStruct((E, F, D), BF16),
            jax.ShapeDtypeStruct((E, 1, F), F32),
            jax.ShapeDtypeStruct((E, 1, D), F32),
        ],
        compiler_params=pltpu.CompilerParams(vmem_limit_bytes=60 * 1024 * 1024),
        cost_estimate=pl.CostEstimate(
            flops=8 * work * D * F // 2, bytes_accessed=work * (8 * D + 6 * F) // 2 + 16 * E * D * F, transcendentals=2 * work * F // 2
        ),
    )(counts, d_expert, table_in, hp, h, w1, w2)

def adamw_kernel(rate, w_ref, m_ref, g_ref, wo_ref, mo_ref):
    g = g_ref[...]
    first = 0.5 * m_ref[0] + 0.5 * g
    root = jnp.sqrt(0.5 * m_ref[1] * m_ref[1] + 0.5 * g * g)
    w = w_ref[...]
    wo_ref[...] = w - rate * (first / (root + 1e-08) + 0.1 * w)
    mo_ref[0] = first
    mo_ref[1] = root


def adamw_pass(weight, moments, grad, rate):
    n, r, c = weight.shape
    spec = pl.BlockSpec((1, r, c), lambda i: (i, 0, 0))
    mspec = pl.BlockSpec((2, 1, r, c), lambda i: (0, i, 0, 0))
    return pl.pallas_call(
        functools.partial(adamw_kernel, rate),
        grid=(n,),
        in_specs=[spec, mspec, spec],
        out_specs=[spec, mspec],
        out_shape=[jax.ShapeDtypeStruct(weight.shape, F32), jax.ShapeDtypeStruct(moments.shape, F32)],
        cost_estimate=pl.CostEstimate(flops=12 * weight.size, bytes_accessed=28 * weight.size, transcendentals=2 * weight.size),
    )(weight, moments, grad)


def layer_norm(value, gain, shift):
    center = value - jnp.mean(value, -1, keepdims=True)
    spread = jnp.mean(center * center, -1, keepdims=True)
    return center * lax.rsqrt(spread + 1e-06) * gain + shift


def gelu_exact(value):
    return jax.nn.gelu(value, approximate=False)


def split_heads(part):
    return part.reshape(-1, S, HEADS, HEAD_DIM)


def dot(a, b):
    return jnp.dot(a, b, preferred_element_type=F32)


def assign_places(route):
    chosen = jnp.concatenate([route[:, :, 0], route[:, :, 1]], 1)
    hits = (chosen[:, :, None] == jnp.arange(E, dtype=jnp.int32)).astype(jnp.int32)
    before = jnp.cumsum(hits, 1) - hits
    slot = jnp.sum(before * hits, 2)
    return chosen * CAPP + slot, jnp.sum(hits, 1)


def hi_lo(v):
    hi = v.astype(BF16)
    lo = (v - hi.astype(F32)).astype(BF16)
    return jnp.concatenate([hi, lo], -1)


def pick_rows(onehot, split):
    both = jnp.einsum("mnr,mrd->mnd", onehot, split, preferred_element_type=F32)
    return both[..., :D] + both[..., D:]


def pack_dense(qkv_w, out_w, router_w, vectors, up_bias):
    rows = qkv_w.shape[0]
    ub = up_bias.reshape(E, rows, 4).transpose(1, 0, 2).reshape(rows, E * 4)
    return jnp.concatenate([qkv_w, out_w, router_w, vectors.T, ub], 1)


def unpack_dense(packed):
    rows = packed.shape[0]
    w_qkv = packed[:, : 3 * D]
    w_out = packed[:, 3 * D : 4 * D]
    w_router = packed[:, 4 * D : 4 * D + E]
    table = packed[:, 4 * D + E : 4 * D + E + NV].T
    ub = packed[:, 4 * D + E + NV :].reshape(rows, E, 4).transpose(1, 0, 2).reshape(E, rows * 4)
    return w_qkv, w_out, w_router, table, ub


def attention_fwd(w_qkv, w_out, table, value):
    rows = value.shape[0]
    scale = HEAD_DIM ** (-0.5)
    first = layer_norm(value, table[0], table[1]).astype(BF16)
    qkv_bias = jnp.concatenate([table[2], jnp.zeros((D,), F32), table[3]])
    qkv = (dot(first, w_qkv) + qkv_bias).astype(BF16)
    query, key_part, val_part = (
        split_heads(qkv[:, :D]),
        split_heads(qkv[:, D : 2 * D]),
        split_heads(qkv[:, 2 * D :]),
    )
    scores = jnp.einsum("bqhd,bkhd->bhqk", query, key_part, preferred_element_type=F32) * scale
    peak = jnp.max(scores, -1, keepdims=True)
    expo = jnp.exp(scores - peak)
    total = jnp.sum(expo, -1, keepdims=True)
    probs_att = (expo / total).astype(BF16)
    log_total = peak + jnp.log(total)
    attended = jnp.einsum("bhqk,bkhd->bqhd", probs_att, val_part, preferred_element_type=F32)
    attended = attended.reshape(rows, D).astype(BF16)
    resid = value + (dot(attended, w_out) + table[4])
    return first, qkv, log_total, attended, resid


def attention_bwd(w_qkv, w_out, table, value, first, qkv, log_total, attended, d_resid):
    rows = value.shape[0]
    scale = HEAD_DIM ** (-0.5)
    d_branch = d_resid.astype(BF16)
    g_bias_out = jnp.sum(d_branch.astype(F32), 0)
    g_out = lax.dot_general(attended, d_branch, (((0,), (0,)), ((), ())), preferred_element_type=F32)
    d_att = split_heads(
        lax.dot_general(d_branch, w_out, (((1,), (1,)), ((), ())), preferred_element_type=F32).astype(BF16)
    )
    query, key_part, val_part = (
        split_heads(qkv[:, :D]),
        split_heads(qkv[:, D : 2 * D]),
        split_heads(qkv[:, 2 * D :]),
    )
    scores = jnp.einsum("bqhd,bkhd->bhqk", query, key_part, preferred_element_type=F32) * scale
    probs_f = jnp.exp(scores - log_total)
    probs_att = probs_f.astype(BF16)
    d_val = jnp.einsum("bhqk,bqhd->bkhd", probs_att, d_att, preferred_element_type=F32)
    d_prob = jnp.einsum("bqhd,bkhd->bhqk", d_att, val_part, preferred_element_type=F32)
    d_score = (probs_f * (d_prob - jnp.sum(d_prob * probs_f, -1, keepdims=True))).astype(BF16)
    d_query = jnp.einsum("bhqk,bkhd->bqhd", d_score, key_part, preferred_element_type=F32) * scale
    d_key = jnp.einsum("bhqk,bqhd->bkhd", d_score, query, preferred_element_type=F32) * scale
    d_qkv = jnp.concatenate(
        [d_query.reshape(rows, D), d_key.reshape(rows, D), d_val.reshape(rows, D)], 1
    ).astype(BF16)
    d_qkv_f = d_qkv.astype(F32)
    g_bias_q = jnp.sum(d_qkv_f[:, :D], 0)
    g_bias_v = jnp.sum(d_qkv_f[:, 2 * D :], 0)
    g_qkv = lax.dot_general(first, d_qkv, (((0,), (0,)), ((), ())), preferred_element_type=F32)
    d_first = lax.dot_general(d_qkv, w_qkv, (((1,), (1,)), ((), ())), preferred_element_type=F32)
    first_pull = jax.vjp(layer_norm, value, table[0], table[1])[1]
    d_input, g_gain_one, g_shift_one = first_pull(d_first)
    return (g_qkv, g_out, g_bias_out, g_bias_q, g_bias_v, g_gain_one, g_shift_one), d_input


def adamw(weight, moments, grad, rate):
    first = 0.5 * moments[0] + 0.5 * grad
    root = jnp.sqrt(0.5 * moments[1] * moments[1] + 0.5 * grad * grad)
    update = first / (root + 1e-08)
    which = lax.broadcasted_iota(jnp.int32, moments.shape, 0) == 0
    both = jnp.where(which, 0.5 * moments + 0.5 * grad, jnp.sqrt(0.5 * moments * moments + 0.5 * grad * grad))
    return (weight - rate * (update + 0.1 * weight), both)


def shards(
    tokens,
    cotangent,
    expert_index,
    qkv_weight,
    out_weight,
    router_weight,
    up_weight,
    up_bias,
    down_weight,
    vectors,
    qkv_moments,
    out_moments,
    router_moments,
    up_moments,
    up_bias_moments,
    down_moments,
    vector_moments,
):
    rows = tokens.shape[0]
    micro = rows // MB_TOK
    gs = qkv_weight.shape[0]
    group_size = D // gs
    core = lax.axis_index("core")

    dense_in = pack_dense(qkv_weight, out_weight, router_weight, vectors, up_bias)
    width = dense_in.shape[1]
    dense_in = jnp.pad(dense_in, ((0, 0), (0, DENSE_AG - width))).astype(BF16)
    w_up_all, w_down_all, dense = ring_all_gather(
        up_weight.astype(BF16), down_weight.astype(BF16), dense_in, group_size, 1
    )
    w_qkv, w_out, w_router, table_b, b_up_b = unpack_dense(dense[:, :width])
    table = table_b.astype(F32)
    b_up = b_up_b.astype(F32)

    value = tokens.astype(F32)
    d_out = cotangent.astype(F32)
    first, qkv, log_total, attended, resid = attention_fwd(w_qkv, w_out, table, value)
    second = layer_norm(resid, table[5], table[6]).astype(BF16)
    logits = dot(second, w_router)
    probs = jax.nn.softmax(logits, -1)
    picked = expert_index[:, :, None] == jnp.arange(E, dtype=jnp.int32)
    gate = jnp.sum(jnp.where(picked, probs[:, None, :], 0.0), -1)

    route = expert_index.reshape(micro, MB_TOK, 2)
    places, counts = assign_places(route)
    counts = counts.T.reshape(E * micro)
    onehot = (places[:, :, None] == jnp.arange(E * CAPP, dtype=jnp.int32)).astype(BF16)
    second_m = second.reshape(micro, MB_TOK, D)
    pair = jnp.concatenate([second_m, second_m], 1)
    table_in = jnp.einsum("mnr,mnd->mrd", onehot, pair, preferred_element_type=F32).astype(BF16)

    hidden_pre, hidden, y_all = ffn_forward(
        counts, table_in, w_up_all, b_up[:, None, :], w_down_all, table[7 : 7 + E][:, None, :], micro
    )
    picked_rows = pick_rows(onehot, y_all)
    out_zero = picked_rows[:, :MB_TOK].reshape(rows, D)
    out_one = picked_rows[:, MB_TOK:].reshape(rows, D)
    result = resid + (gate[:, 0:1] * out_zero + gate[:, 1:2] * out_one)

    d_gate = jnp.stack([jnp.sum(d_out * out_zero, -1), jnp.sum(d_out * out_one, -1)], 1)
    d_out_m = d_out.reshape(micro, MB_TOK, D)
    gate_m = gate.reshape(micro, MB_TOK, 2)
    weighted = jnp.concatenate([gate_m[:, :, 0:1] * d_out_m, gate_m[:, :, 1:2] * d_out_m], 1).astype(BF16)
    d_expert = jnp.einsum("mnr,mnd->mrd", onehot, weighted, preferred_element_type=F32).astype(BF16)

    d_table, g_up, g_down, g_b1, g_b2 = ffn_backward(counts, d_expert, table_in, hidden_pre, hidden, w_up_all, w_down_all, micro)
    g_up_bias_all = g_b1[:, 0, :]
    g_bias_down = g_b2[:, 0, :]

    onehot_sum = onehot[:, :MB_TOK] + onehot[:, MB_TOK:]
    d_picked = pick_rows(onehot_sum, d_table).reshape(rows, D)

    d_probs = jnp.sum(jnp.where(picked, d_gate[:, :, None], 0.0), 1)
    d_logit = (probs * (d_probs - jnp.sum(d_probs * probs, -1, keepdims=True))).astype(BF16)
    g_router = lax.dot_general(second, d_logit, (((0,), (0,)), ((), ())), preferred_element_type=F32)
    d_second = d_picked + lax.dot_general(d_logit, w_router, (((1,), (1,)), ((), ())), preferred_element_type=F32)
    norm_pull = jax.vjp(layer_norm, resid, table[5], table[6])[1]
    d_resid, g_gain_two, g_shift_two = norm_pull(d_second)
    d_resid = d_out + d_resid

    att_grads, d_input = attention_bwd(w_qkv, w_out, table, value, first, qkv, log_total, attended, d_resid)
    g_qkv, g_out, g_bias_out, g_bias_q, g_bias_v, g_gain_one, g_shift_one = att_grads
    input_grad = d_resid + d_input

    g_table = jnp.concatenate(
        [
            jnp.stack([g_gain_one, g_shift_one, g_bias_q, g_bias_v, g_bias_out, g_gain_two, g_shift_two]),
            g_bias_down,
        ],
        0,
    )
    dense_g = pack_dense(g_qkv, g_out, g_router, g_table, g_up_bias_all)
    width = dense_g.shape[1]
    dense_g = jnp.pad(dense_g, ((0, 0), (0, DENSE_AG - width))).astype(BF16)
    x_pair = lax.axis_size("rx") == 2
    r_up, r_down, r_dense = grad_reduce(g_up, g_down, dense_g, group_size, x_pair, 0)
    if not x_pair:
        r_up, r_down, r_dense = lax.psum((r_up, r_down, r_dense), "rx")
    r_qkv, r_out, r_router, r_table, r_ub = unpack_dense(r_dense[:, :width])

    reduced = (r_qkv, r_out, r_router, r_up, r_ub, r_down, r_table)
    rates = (
        2.0 * D ** (-0.5),
        2.0 * (D // 32) ** (-0.5),
        2.0 * (2 * D) ** (-0.5),
        2.0 * D ** (-0.5),
        0.2,
        2.0 * (F // 16) ** (-0.5),
        0.2,
    )
    params = (qkv_weight, out_weight, router_weight, up_weight, up_bias, down_weight, vectors)
    moments = (qkv_moments, out_moments, router_moments, up_moments, up_bias_moments, down_moments, vector_moments)
    news = []
    states = []
    for weight, state, grad, rate in zip(params, moments, reduced, rates):
        if weight.ndim == 3:
            new_weight, new_state = adamw_pass(weight, state, grad, rate)
        else:
            new_weight, new_state = adamw(weight, state, grad, rate)
        news.append(new_weight)
        states.append(new_state)
    return (result.astype(BF16), input_grad) + reduced + tuple(news) + tuple(states)


def solution(mesh):
    replica, group = mesh.shape["replica"], mesh.shape["group"]
    view = Mesh(np.asarray(mesh.devices).reshape(replica // 2, 2, group), ("rx", "core", "group"))
    in_specs = (
        P(TOK, None),
        P(TOK, None),
        P(TOK, None),
        P("group", None),
        P("group", None),
        P("group", None),
        P(None, "group", None),
        P(None, "group"),
        P(None, "group", None),
        P(None, "group"),
        P(None, "group", None),
        P(None, "group", None),
        P(None, "group", None),
        P(None, None, "group", None),
        P(None, None, "group"),
        P(None, None, "group", None),
        P(None, None, "group"),
    )
    out_specs = (
        P(TOK, None),
        P(TOK, None),
        P("group", None),
        P("group", None),
        P("group", None),
        P(None, "group", None),
        P(None, "group"),
        P(None, "group", None),
        P(None, "group"),
        P("group", None),
        P("group", None),
        P("group", None),
        P(None, "group", None),
        P(None, "group"),
        P(None, "group", None),
        P(None, "group"),
        P(None, "group", None),
        P(None, "group", None),
        P(None, "group", None),
        P(None, None, "group", None),
        P(None, None, "group"),
        P(None, None, "group", None),
        P(None, None, "group"),
    )
    return jax.shard_map(shards, mesh=view, in_specs=in_specs, out_specs=out_specs, check_vma=False)
```

```python
import functools

import jax
import jax.numpy as jnp
import numpy as np
from jax import lax
from jax.sharding import Mesh
from jax.sharding import PartitionSpec as P
from jax.experimental import pallas as pl
from jax.experimental.pallas import tpu as pltpu

D = 512
HEADS = 8
HEAD_DIM = 64
F = 2048
E = 4
S = 197
MB_TOK = 394
CAP = 392
NV = 11
DENSE_AG = 2560
DENSE_PAD = 2304
F32 = jnp.float32
BF16 = jnp.bfloat16
TOK = ("rx", "core", "group")


MESH_ID = pl.DeviceIdType.MESH


def ring_order(groups):
    if groups in (4, 8):
        zs = groups // 2

        def pos_of(g):
            y = g % 2
            z = g // 2
            return z + y * (2 * zs - 1 - 2 * z)

        def dev_at(p):
            p = p % groups
            yy = p // zs
            return 2 * (p + yy * (2 * zs - 1 - 2 * p)) + yy

        return pos_of, dev_at
    return (lambda g: g), (lambda p: p % groups)


def ring_rs_kernel(groups, n_in, *refs):
    ins = refs[:n_in]
    outs = refs[n_in : 2 * n_in]
    rbufs = refs[2 * n_in : 3 * n_in]
    sbufs = refs[3 * n_in : 4 * n_in]
    owns = refs[4 * n_in : 5 * n_in]
    send_sem, recv_sem, load_sem = refs[5 * n_in :]
    pos_of, dev_at = ring_order(groups)
    rx = lax.axis_index("rx")
    core = lax.axis_index("core")
    g = lax.axis_index("group")
    pos = pos_of(g)
    nbr = (dev_at(pos + 1), dev_at(pos + groups - 1))

    barrier = pltpu.get_barrier_semaphore()
    for n in nbr:
        pl.semaphore_signal(barrier, inc=1, device_id=(rx, core, n), device_id_type=MESH_ID)
    pl.semaphore_wait(barrier, 2)

    def block_dev(d, s):
        if d == 0:
            return dev_at(pos + 2 * groups - s - 1)
        return dev_at(pos + s + 1)

    def load(d, s, slot):
        b = block_dev(d, s)
        copies = []
        for i in range(n_in):
            rows = ins[i].shape[1] // groups
            half = ins[i].shape[2] // 2
            src = ins[i].at[:, pl.ds(pl.multiple_of(b * rows, rows), rows), pl.ds(d * half, half)]
            copies.append(pltpu.make_async_copy(src, owns[i].at[d, slot], load_sem.at[d, slot, i]))
        return copies

    def remote(d, s, i):
        return pltpu.make_async_remote_copy(
            src_ref=sbufs[i].at[d, s],
            dst_ref=rbufs[i].at[d, s],
            send_sem=send_sem.at[d, s, i],
            recv_sem=recv_sem.at[d, s, i],
            device_id=(rx, core, nbr[d]),
            device_id_type=MESH_ID,
        )

    for d in range(2):
        for c in load(d, 0, 0):
            c.start()
    sends = []
    for s in range(groups):
        slot = s % 2
        for d in range(2):
            for c in load(d, s, slot):
                c.wait()
            if s + 1 < groups:
                for c in load(d, s + 1, 1 - slot):
                    c.start()
            for i in range(n_in):
                if s > 0:
                    remote(d, s - 1, i).wait_recv()
                for a in range(ins[i].shape[0]):
                    mine = owns[i][d, slot, a].astype(F32)
                    if s > 0:
                        mine = mine + rbufs[i][d, s - 1, a].astype(F32)
                    if s < groups - 1:
                        sbufs[i][d, s, a] = mine.astype(sbufs[i].dtype)
                    else:
                        half = ins[i].shape[2] // 2
                        outs[i][a, :, pl.ds(d * half, half)] = mine.astype(outs[i].dtype)
                if s < groups - 1:
                    c = remote(d, s, i)
                    c.start()
                    sends.append(c)
    for c in sends:
        c.wait_send()


def ring_reduce_scatter(xs, groups, collective_id):
    n_in = len(xs)
    outs, rb, own = [], [], []
    flops = 0
    nbytes = 0
    for x in xs:
        a, total, c = x.shape
        rows = total // groups
        outs.append(jax.ShapeDtypeStruct((a, rows, c), x.dtype))
        rb.append(pltpu.VMEM((2, groups - 1, a, rows, c // 2), x.dtype))
        own.append(pltpu.VMEM((2, 2, a, rows, c // 2), x.dtype))
        flops += a * total * c
        nbytes += 3 * x.size * x.dtype.itemsize
    scratch = rb + rb + own + [
        pltpu.SemaphoreType.DMA((2, groups - 1, n_in)),
        pltpu.SemaphoreType.DMA((2, groups - 1, n_in)),
        pltpu.SemaphoreType.DMA((2, 2, n_in)),
    ]
    return pl.pallas_call(
        functools.partial(ring_rs_kernel, groups, n_in),
        out_shape=outs,
        in_specs=[pl.BlockSpec(memory_space=pl.ANY)] * n_in,
        out_specs=[pl.BlockSpec(memory_space=pltpu.VMEM)] * n_in,
        scratch_shapes=scratch,
        compiler_params=pltpu.CompilerParams(
            collective_id=collective_id, has_side_effects=True, vmem_limit_bytes=60 * 1024 * 1024
        ),
        cost_estimate=pl.CostEstimate(flops=flops, bytes_accessed=nbytes, transcendentals=0),
    )(*xs)


def ring_ag_kernel(groups, *refs):
    in_up, in_down, in_dense, out_up, out_down, out_dense = refs[:6]
    ring_send, ring_recv, part_send, part_recv, local_sem = refs[6:]
    pos_of, dev_at = ring_order(groups)
    rx = lax.axis_index("rx")
    core = lax.axis_index("core")
    g = lax.axis_index("group")
    other = 1 - core
    pos = pos_of(g)
    nbr = (dev_at(pos + 1), dev_at(pos + groups - 1))
    gs = in_up.shape[1]
    fs = in_down.shape[1]
    width = in_dense.shape[1] // 2

    barrier = pltpu.get_barrier_semaphore()
    for n in nbr:
        pl.semaphore_signal(barrier, inc=1, device_id=(rx, core, n), device_id_type=MESH_ID)
    pl.semaphore_signal(barrier, inc=1, device_id=(rx, other, g), device_id_type=MESH_ID)
    pl.semaphore_wait(barrier, 3)

    def items(owner):
        found = []
        for k in range(2):
            e = 2 * k + owner
            found.append((in_up.at[e], lambda b, e=e: out_up.at[e, pl.ds(pl.multiple_of(b * gs, gs), gs)], F // 2))
            found.append((in_down.at[e], lambda b, e=e: out_down.at[e, pl.ds(pl.multiple_of(b * fs, fs), fs)], D // 2))
        dense_in = in_dense.at[:, pl.ds(owner * width, width)]
        found.append(
            (dense_in, lambda b: out_dense.at[pl.ds(pl.multiple_of(b * gs, gs), gs), pl.ds(owner * width, width)], width // 2)
        )
        return found

    mine = items(core)
    theirs = items(other)
    n_items = len(mine)

    locals_ = [pltpu.make_async_copy(in_up.at[e], out_up.at[e, pl.ds(pl.multiple_of(g * gs, gs), gs)], local_sem.at[e]) for e in range(E)]
    locals_ += [
        pltpu.make_async_copy(in_down.at[e], out_down.at[e, pl.ds(pl.multiple_of(g * fs, fs), fs)], local_sem.at[E + e])
        for e in range(E)
    ]
    locals_.append(pltpu.make_async_copy(in_dense, out_dense.at[pl.ds(pl.multiple_of(g * gs, gs), gs)], local_sem.at[2 * E]))
    for c in locals_:
        c.start()

    def block_at(d, s):
        if d == 0:
            return dev_at(pos + 2 * groups - 1 - s)
        return dev_at(pos + 1 + s)

    def ring_copy(d, s, j, src_block):
        src_in, dst_of, half = mine[j]
        cols = pl.ds(d * half, half)
        if src_block is None:
            src = src_in.at[:, cols]
            dst = dst_of(g).at[:, cols]
        else:
            src = dst_of(src_block).at[:, cols]
            dst = src
        return pltpu.make_async_remote_copy(
            src_ref=src, dst_ref=dst, send_sem=ring_send.at[d, s, j], recv_sem=ring_recv.at[d, s, j],
            device_id=(rx, core, nbr[d]), device_id_type=MESH_ID,
        )

    def part_copy(d, s, j, table, block):
        _, dst_of, half = table[j]
        view = dst_of(block).at[:, pl.ds(d * half, half)]
        return pltpu.make_async_remote_copy(
            src_ref=view, dst_ref=view, send_sem=part_send.at[d, s, j], recv_sem=part_recv.at[d, s, j],
            device_id=(rx, other, g), device_id_type=MESH_ID,
        )

    sends = []
    for d in range(2):
        for j in range(n_items):
            c = ring_copy(d, 0, j, None)
            c.start()
            sends.append(c)
    for s in range(groups - 1):
        for d in range(2):
            b = block_at(d, s)
            for j in range(n_items):
                pltpu.make_async_remote_copy(
                    src_ref=mine[j][1](b).at[:, pl.ds(d * mine[j][2], mine[j][2])],
                    dst_ref=mine[j][1](b).at[:, pl.ds(d * mine[j][2], mine[j][2])],
                    send_sem=ring_send.at[d, s, j], recv_sem=ring_recv.at[d, s, j],
                    device_id=(rx, core, nbr[d]), device_id_type=MESH_ID,
                ).wait_recv()
                if s + 1 < groups - 1:
                    c = ring_copy(d, s + 1, j, b)
                    c.start()
                    sends.append(c)
                c = part_copy(d, s, j, mine, b)
                c.start()
                sends.append(c)
    for s in range(groups - 1):
        for d in range(2):
            b = block_at(d, s)
            for j in range(n_items):
                part_copy(d, s, j, theirs, b).wait_recv()
    for c in sends:
        c.wait_send()
    for c in locals_:
        c.wait()


def ring_all_gather(up_b, down_b, dense_b, groups, collective_id):
    n_items = 5
    gs = up_b.shape[1]
    shapes = [
        jax.ShapeDtypeStruct((E, gs * groups, F), BF16),
        jax.ShapeDtypeStruct((E, down_b.shape[1] * groups, D), BF16),
        jax.ShapeDtypeStruct((gs * groups, dense_b.shape[1]), BF16),
    ]
    nbytes = sum(int(np.prod(s.shape)) * 2 for s in shapes)
    return pl.pallas_call(
        functools.partial(ring_ag_kernel, groups),
        out_shape=shapes,
        in_specs=[pl.BlockSpec(memory_space=pl.ANY)] * 3,
        out_specs=[pl.BlockSpec(memory_space=pl.ANY)] * 3,
        scratch_shapes=[
            pltpu.SemaphoreType.DMA((2, groups - 1, n_items)),
            pltpu.SemaphoreType.DMA((2, groups - 1, n_items)),
            pltpu.SemaphoreType.DMA((2, groups - 1, n_items)),
            pltpu.SemaphoreType.DMA((2, groups - 1, n_items)),
            pltpu.SemaphoreType.DMA((2 * E + 1,)),
        ],
        compiler_params=pltpu.CompilerParams(collective_id=collective_id, has_side_effects=True),
        cost_estimate=pl.CostEstimate(flops=0, bytes_accessed=nbytes, transcendentals=0),
    )(up_b, down_b, dense_b)


def grad_items(gu, gd, gdense, owner, gs, fs, width):
    found = []
    for k in range(2):
        e = 2 * k + owner
        found.append((lambda b, e=e: gu.at[e, pl.ds(pl.multiple_of(b * gs, gs), gs)], F // 2))
        found.append((lambda b, e=e: gd.at[e, pl.ds(pl.multiple_of(b * fs, fs), fs)], D // 2))
    found.append((lambda b: gdense.at[pl.ds(pl.multiple_of(b * gs, gs), gs), pl.ds(owner * width, width)], width // 2))
    return found


def ring_rs2_kernel(groups, x_pair, *refs):
    gu, gd, gdense, out_up, out_down, out_dense = refs[:6]
    n_items = 5
    scr = refs[6:]
    rbuf, sbuf, pbuf, own, fin, xr, cr, xs = (scr[i * n_items : (i + 1) * n_items] for i in range(8))
    ring_send, ring_recv, part_send, part_recv, load_sem, x_send, x_recv, c_send, c_recv = scr[8 * n_items :]
    pos_of, dev_at = ring_order(groups)
    rx = lax.axis_index("rx")
    core = lax.axis_index("core")
    g = lax.axis_index("group")
    other = 1 - core
    pos = pos_of(g)
    nbr = (dev_at(pos + 1), dev_at(pos + groups - 1))
    gs = gu.shape[1] // groups
    fs = gd.shape[1] // groups
    width = gdense.shape[1] // 2
    mine = grad_items(gu, gd, gdense, core, gs, fs, width)
    theirs = grad_items(gu, gd, gdense, other, gs, fs, width)

    barrier = pltpu.get_barrier_semaphore()
    for n in nbr:
        pl.semaphore_signal(barrier, inc=1, device_id=(rx, core, n), device_id_type=MESH_ID)
    pl.semaphore_signal(barrier, inc=1, device_id=(rx, other, g), device_id_type=MESH_ID)
    count = 3
    if x_pair:
        pl.semaphore_signal(barrier, inc=1, device_id=(1 - rx, core, g), device_id_type=MESH_ID)
        count = 4
    pl.semaphore_wait(barrier, count)

    def block_at(d, s):
        if d == 0:
            return dev_at(pos + 2 * groups - 1 - s)
        return dev_at(pos + 1 + s)

    def cols(j, d):
        half = mine[j][1]
        return pl.ds(d * half, half)

    def load(d, s, slot, j):
        return pltpu.make_async_copy(mine[j][0](block_at(d, s)).at[:, cols(j, d)], own[j].at[d, slot], load_sem.at[d, slot, j])

    def part(d, s, j):
        return pltpu.make_async_remote_copy(
            src_ref=theirs[j][0](block_at(d, s)).at[:, cols(j, d)], dst_ref=pbuf[j].at[d, s],
            send_sem=part_send.at[d, s, j], recv_sem=part_recv.at[d, s, j],
            device_id=(rx, other, g), device_id_type=MESH_ID,
        )

    def ring(d, s, j):
        return pltpu.make_async_remote_copy(
            src_ref=sbuf[j].at[d, s], dst_ref=rbuf[j].at[d, s],
            send_sem=ring_send.at[d, s, j], recv_sem=ring_recv.at[d, s, j],
            device_id=(rx, core, nbr[d]), device_id_type=MESH_ID,
        )

    sends = []

    def ring_wave(items):
        for d in range(2):
            for j in items:
                load(d, 0, 0, j).start()
                c = part(d, 0, j)
                c.start()
                sends.append(c)
        for s in range(groups):
            slot = s % 2
            for d in range(2):
                for j in items:
                    load(d, s, slot, j).wait()
                    if s + 1 < groups:
                        load(d, s + 1, 1 - slot, j).start()
                        c = part(d, s + 1, j)
                        c.start()
                        sends.append(c)
                    part(d, s, j).wait_recv()
                    val = own[j][d, slot].astype(F32) + pbuf[j][d, s].astype(F32)
                    if s > 0:
                        ring(d, s - 1, j).wait_recv()
                        val = val + rbuf[j][d, s - 1].astype(F32)
                    if s < groups - 1:
                        sbuf[j][d, s] = val.astype(BF16)
                        c = ring(d, s, j)
                        c.start()
                        sends.append(c)
                    else:
                        fin[j][d] = val

    def x_start(items):
        copies = []
        for d in range(2):
            for j in items:
                xs[j][d] = fin[j][d].astype(BF16)
                c = pltpu.make_async_remote_copy(
                    src_ref=xs[j].at[d], dst_ref=xr[j].at[d], send_sem=x_send.at[d, j], recv_sem=x_recv.at[d, j],
                    device_id=(1 - rx, core, g), device_id_type=MESH_ID,
                )
                c.start()
                copies.append(c)
        sends.extend(copies)
        return copies

    def x_finish(items, copies):
        for c in copies:
            c.wait_recv()
        for d in range(2):
            for j in items:
                fin[j][d] = xs[j][d].astype(F32) + xr[j][d].astype(F32)

    def c_start(items):
        copies = []
        for d in range(2):
            for j in items:
                c = pltpu.make_async_remote_copy(
                    src_ref=fin[j].at[d], dst_ref=cr[j].at[d], send_sem=c_send.at[d, j], recv_sem=c_recv.at[d, j],
                    device_id=(rx, other, g), device_id_type=MESH_ID,
                )
                c.start()
                copies.append(c)
        return copies

    wave_a, wave_b = (0, 1, 2, 4), (3,)
    ring_wave(wave_a)
    if x_pair:
        xa = x_start(wave_a)
    ring_wave(wave_b)
    if x_pair:
        x_finish(wave_a, xa)
    c_copies = c_start(wave_a)
    if x_pair:
        x_finish(wave_b, x_start(wave_b))
    c_copies += c_start(wave_b)

    def out_items(owner):
        found = []
        for k in range(2):
            e = 2 * k + owner
            found.append(lambda d, e=e: out_up.at[e, :, pl.ds(d * (F // 2), F // 2)])
            found.append(lambda d, e=e: out_down.at[e, :, pl.ds(d * (D // 2), D // 2)])
        found.append(lambda d: out_dense.at[:, pl.ds(owner * width + d * (width // 2), width // 2)])
        return found

    mine_out = out_items(core)
    theirs_out = out_items(other)
    for d in range(2):
        for j in range(n_items):
            mine_out[j](d)[...] = fin[j][d]
    for c in c_copies:
        c.wait_recv()
    for d in range(2):
        for j in range(n_items):
            theirs_out[j](d)[...] = cr[j][d]
    for c in sends + c_copies:
        c.wait_send()


def grad_reduce(gu, gd, gdense, groups, x_pair, collective_id):
    gs = gu.shape[1] // groups
    fs = gd.shape[1] // groups
    width = gdense.shape[1] // 2
    item_shapes = [(gs, F // 2), (fs, D // 2), (gs, F // 2), (fs, D // 2), (gs, width // 2)]
    scratch = []
    for lead, dtype in (((2, groups - 1), BF16), ((2, groups - 1), BF16), ((2, groups), BF16), ((2, 2), BF16), ((2,), F32), ((2,), BF16), ((2,), F32), ((2,), BF16)):
        scratch += [pltpu.VMEM(lead + shp, dtype) for shp in item_shapes]
    scratch += [
        pltpu.SemaphoreType.DMA((2, groups - 1, 5)),
        pltpu.SemaphoreType.DMA((2, groups - 1, 5)),
        pltpu.SemaphoreType.DMA((2, groups, 5)),
        pltpu.SemaphoreType.DMA((2, groups, 5)),
        pltpu.SemaphoreType.DMA((2, 2, 5)),
        pltpu.SemaphoreType.DMA((2, 5)),
        pltpu.SemaphoreType.DMA((2, 5)),
        pltpu.SemaphoreType.DMA((2, 5)),
        pltpu.SemaphoreType.DMA((2, 5)),
    ]
    outs = [
        jax.ShapeDtypeStruct((E, gs, F), F32),
        jax.ShapeDtypeStruct((E, fs, D), F32),
        jax.ShapeDtypeStruct((gs, gdense.shape[1]), F32),
    ]
    nbytes = 2 * (gu.size + gd.size + gdense.size)
    return pl.pallas_call(
        functools.partial(ring_rs2_kernel, groups, x_pair),
        out_shape=outs,
        in_specs=[pl.BlockSpec(memory_space=pl.ANY)] * 3,
        out_specs=[pl.BlockSpec(memory_space=pltpu.VMEM)] * 3,
        scratch_shapes=scratch,
        compiler_params=pltpu.CompilerParams(
            collective_id=collective_id, has_side_effects=True, vmem_limit_bytes=62 * 1024 * 1024
        ),
        cost_estimate=pl.CostEstimate(flops=gu.size + gd.size + gdense.size, bytes_accessed=nbytes, transcendentals=0),
    )(gu, gd, gdense)


TILE = 256
TILE_B = 256
CAPP = 512
SQRT_HALF = float(np.sqrt(0.5))
INV_SQRT_2PI = float(1.0 / np.sqrt(2.0 * np.pi))


def ffn_fwd_kernel(micro, counts, x_ref, w1_ref, b1_ref, w2_ref, b2_ref, hp_ref, h_ref, y_ref):
    e, m, t = pl.program_id(0), pl.program_id(1), pl.program_id(2)
    active = t * TILE < counts[e * micro + m]

    @pl.when(active)
    def _():
        hp = jnp.dot(x_ref[0], w1_ref[0], preferred_element_type=F32) + b1_ref[0]
        cdf = 0.5 * (1.0 + lax.erf(hp * SQRT_HALF))
        h = (hp * cdf).astype(BF16)
        hp_ref[0] = cdf + hp * jnp.exp(-0.5 * hp * hp) * INV_SQRT_2PI
        h_ref[0] = h
        y = jnp.dot(h, w2_ref[0], preferred_element_type=F32) + b2_ref[0]
        hi = y.astype(BF16)
        y_ref[0, :, :D] = hi
        y_ref[0, :, D:] = (y - hi.astype(F32)).astype(BF16)

    @pl.when(jnp.logical_not(active))
    def _():
        y_ref[0] = jnp.zeros(y_ref.shape[1:], BF16)


def ffn_forward(counts, table_in, w1, b1, w2, b2, micro):
    tiles = CAPP // TILE
    rows = table_in.shape[1]
    row_map = lambda e, m, t, c: (m, e * tiles + t, 0)
    w_map = lambda e, m, t, c: (e, 0, 0)
    grid_spec = pltpu.PrefetchScalarGridSpec(
        num_scalar_prefetch=1,
        grid=(E, micro, tiles),
        in_specs=[
            pl.BlockSpec((1, TILE, D), row_map),
            pl.BlockSpec((1, D, F), w_map),
            pl.BlockSpec((1, 1, F), w_map),
            pl.BlockSpec((1, F, D), w_map),
            pl.BlockSpec((1, 1, D), w_map),
        ],
        out_specs=[
            pl.BlockSpec((1, TILE, F), row_map),
            pl.BlockSpec((1, TILE, F), row_map),
            pl.BlockSpec((1, TILE, 2 * D), row_map),
        ],
    )
    work = micro * rows
    return pl.pallas_call(
        functools.partial(ffn_fwd_kernel, micro),
        grid_spec=grid_spec,
        out_shape=[
            jax.ShapeDtypeStruct((micro, rows, F), F32),
            jax.ShapeDtypeStruct((micro, rows, F), BF16),
            jax.ShapeDtypeStruct((micro, rows, 2 * D), BF16),
        ],
        compiler_params=pltpu.CompilerParams(vmem_limit_bytes=48 * 1024 * 1024),
        cost_estimate=pl.CostEstimate(
            flops=4 * work * D * F // 2, bytes_accessed=work * (2 * D + 6 * F + 4 * D) // 2, transcendentals=work * F // 2
        ),
    )(counts, table_in, w1, b1, w2, b2)


def ffn_bwd_kernel(micro, counts, dy_ref, x_ref, hp_ref, h_ref, w1_ref, w2_ref, dt_ref, gu_ref, gd_ref, gb_ref, gb2_ref, gu_acc, gd_acc):
    e, m, t = pl.program_id(0), pl.program_id(1), pl.program_id(2)
    active = t * TILE_B < counts[e * micro + m]

    @pl.when((m == 0) & (t == 0))
    def _():
        gu_acc[...] = jnp.zeros(gu_acc.shape, F32)
        gd_acc[...] = jnp.zeros(gd_acc.shape, F32)
        gb_ref[...] = jnp.zeros(gb_ref.shape, F32)
        gb2_ref[...] = jnp.zeros(gb2_ref.shape, F32)

    @pl.when(active)
    def _():
        dy = dy_ref[0]
        d_hidden = lax.dot_general(dy, w2_ref[0], (((1,), (1,)), ((), ())), preferred_element_type=F32)
        d_pre = (d_hidden * hp_ref[0]).astype(BF16)
        dt = lax.dot_general(d_pre, w1_ref[0], (((1,), (1,)), ((), ())), preferred_element_type=F32)
        hi = dt.astype(BF16)
        dt_ref[0, :, :D] = hi
        dt_ref[0, :, D:] = (dt - hi.astype(F32)).astype(BF16)
        gb2_ref[0] += jnp.sum(dy.astype(F32), 0, keepdims=True)
        gu_acc[...] += lax.dot_general(x_ref[0], d_pre, (((0,), (0,)), ((), ())), preferred_element_type=F32)
        gd_acc[...] += lax.dot_general(h_ref[0], dy, (((0,), (0,)), ((), ())), preferred_element_type=F32)
        gb_ref[0] += jnp.sum(d_pre.astype(F32), 0, keepdims=True)

    @pl.when(jnp.logical_not(active))
    def _():
        dt_ref[0] = jnp.zeros(dt_ref.shape[1:], BF16)

    @pl.when((m == micro - 1) & (t == pl.num_programs(2) - 1))
    def _():
        gu_ref[0] = gu_acc[...].astype(BF16)
        gd_ref[0] = gd_acc[...].astype(BF16)


def ffn_backward(counts, d_expert, table_in, hp, h, w1, w2, micro):
    tiles = CAPP // TILE_B
    rows = table_in.shape[1]
    row_map = lambda e, m, t, c: (m, e * tiles + t, 0)
    w_map = lambda e, m, t, c: (e, 0, 0)
    grid_spec = pltpu.PrefetchScalarGridSpec(
        num_scalar_prefetch=1,
        grid=(E, micro, tiles),
        in_specs=[
            pl.BlockSpec((1, TILE_B, D), row_map),
            pl.BlockSpec((1, TILE_B, D), row_map),
            pl.BlockSpec((1, TILE_B, F), row_map),
            pl.BlockSpec((1, TILE_B, F), row_map),
            pl.BlockSpec((1, D, F), w_map),
            pl.BlockSpec((1, F, D), w_map),
        ],
        out_specs=[
            pl.BlockSpec((1, TILE_B, 2 * D), row_map),
            pl.BlockSpec((1, D, F), w_map),
            pl.BlockSpec((1, F, D), w_map),
            pl.BlockSpec((1, 1, F), w_map),
            pl.BlockSpec((1, 1, D), w_map),
        ],
        scratch_shapes=[pltpu.VMEM((D, F), F32), pltpu.VMEM((F, D), F32)],
    )
    work = micro * rows
    return pl.pallas_call(
        functools.partial(ffn_bwd_kernel, micro),
        grid_spec=grid_spec,
        out_shape=[
            jax.ShapeDtypeStruct((micro, rows, 2 * D), BF16),
            jax.ShapeDtypeStruct((E, D, F), BF16),
            jax.ShapeDtypeStruct((E, F, D), BF16),
            jax.ShapeDtypeStruct((E, 1, F), F32),
            jax.ShapeDtypeStruct((E, 1, D), F32),
        ],
        compiler_params=pltpu.CompilerParams(vmem_limit_bytes=60 * 1024 * 1024),
        cost_estimate=pl.CostEstimate(
            flops=8 * work * D * F // 2, bytes_accessed=work * (8 * D + 6 * F) // 2 + 16 * E * D * F, transcendentals=2 * work * F // 2
        ),
    )(counts, d_expert, table_in, hp, h, w1, w2)

def adamw_kernel(rate, w_ref, m_ref, g_ref, wo_ref, mo_ref):
    g = g_ref[...]
    first = 0.5 * m_ref[0] + 0.5 * g
    root = jnp.sqrt(0.5 * m_ref[1] * m_ref[1] + 0.5 * g * g)
    w = w_ref[...]
    wo_ref[...] = w - rate * (first / (root + 1e-08) + 0.1 * w)
    mo_ref[0] = first
    mo_ref[1] = root


def adamw_pass(weight, moments, grad, rate):
    n, r, c = weight.shape
    spec = pl.BlockSpec((1, r, c), lambda i: (i, 0, 0))
    mspec = pl.BlockSpec((2, 1, r, c), lambda i: (0, i, 0, 0))
    return pl.pallas_call(
        functools.partial(adamw_kernel, rate),
        grid=(n,),
        in_specs=[spec, mspec, spec],
        out_specs=[spec, mspec],
        out_shape=[jax.ShapeDtypeStruct(weight.shape, F32), jax.ShapeDtypeStruct(moments.shape, F32)],
        cost_estimate=pl.CostEstimate(flops=12 * weight.size, bytes_accessed=28 * weight.size, transcendentals=2 * weight.size),
    )(weight, moments, grad)


def layer_norm(value, gain, shift):
    center = value - jnp.mean(value, -1, keepdims=True)
    spread = jnp.mean(center * center, -1, keepdims=True)
    return center * lax.rsqrt(spread + 1e-06) * gain + shift


def gelu_exact(value):
    return jax.nn.gelu(value, approximate=False)


def split_heads(part):
    return part.reshape(-1, S, HEADS, HEAD_DIM)


def dot(a, b):
    return jnp.dot(a, b, preferred_element_type=F32)


def assign_places(route):
    chosen = jnp.concatenate([route[:, :, 0], route[:, :, 1]], 1)
    hits = (chosen[:, :, None] == jnp.arange(E, dtype=jnp.int32)).astype(jnp.int32)
    before = jnp.cumsum(hits, 1) - hits
    slot = jnp.sum(before * hits, 2)
    return chosen * CAPP + slot, jnp.sum(hits, 1)


def hi_lo(v):
    hi = v.astype(BF16)
    lo = (v - hi.astype(F32)).astype(BF16)
    return jnp.concatenate([hi, lo], -1)


def pick_rows(onehot, split):
    both = jnp.einsum("mnr,mrd->mnd", onehot, split, preferred_element_type=F32)
    return both[..., :D] + both[..., D:]


def pack_dense(qkv_w, out_w, router_w, vectors, up_bias):
    rows = qkv_w.shape[0]
    ub = up_bias.reshape(E, rows, 4).transpose(1, 0, 2).reshape(rows, E * 4)
    return jnp.concatenate([qkv_w, out_w, router_w, vectors.T, ub], 1)


def unpack_dense(packed):
    rows = packed.shape[0]
    w_qkv = packed[:, : 3 * D]
    w_out = packed[:, 3 * D : 4 * D]
    w_router = packed[:, 4 * D : 4 * D + E]
    table = packed[:, 4 * D + E : 4 * D + E + NV].T
    ub = packed[:, 4 * D + E + NV :].reshape(rows, E, 4).transpose(1, 0, 2).reshape(E, rows * 4)
    return w_qkv, w_out, w_router, table, ub


def attention_fwd(w_qkv, w_out, table, value):
    rows = value.shape[0]
    nb = rows // S
    scale = HEAD_DIM ** (-0.5)
    first = layer_norm(value, table[0], table[1]).astype(BF16)
    qkv_bias = jnp.concatenate([table[2], jnp.zeros((D,), F32), table[3]]).reshape(3, 1, HEADS, 1, HEAD_DIM)
    w3 = w_qkv.reshape(D, 3, HEADS, HEAD_DIM)
    qkv = (jnp.einsum("bsk,kthd->tbhsd", first.reshape(nb, S, D), w3, preferred_element_type=F32) + qkv_bias).astype(BF16)
    query, key_part, val_part = qkv[0], qkv[1], qkv[2]
    scores = jnp.einsum("bhqd,bhkd->bhqk", query, key_part, preferred_element_type=F32) * scale
    peak = jnp.max(scores, -1, keepdims=True)
    expo = jnp.exp(scores - peak)
    total = jnp.sum(expo, -1, keepdims=True)
    probs_att = (expo / total).astype(BF16)
    log_total = peak + jnp.log(total)
    attended = jnp.einsum("bhqk,bhkd->bqhd", probs_att, val_part, preferred_element_type=F32)
    attended = attended.reshape(rows, D).astype(BF16)
    resid = value + (dot(attended, w_out) + table[4])
    return first, qkv, log_total, attended, resid


def attention_bwd(w_qkv, w_out, table, value, first, qkv, log_total, attended, d_resid):
    rows = value.shape[0]
    nb = rows // S
    scale = HEAD_DIM ** (-0.5)
    d_branch = d_resid.astype(BF16)
    g_bias_out = jnp.sum(d_branch.astype(F32), 0)
    g_out = lax.dot_general(attended, d_branch, (((0,), (0,)), ((), ())), preferred_element_type=F32)
    d_att = jnp.einsum(
        "bsn,hdn->bhsd", d_branch.reshape(nb, S, D), w_out.reshape(HEADS, HEAD_DIM, D), preferred_element_type=F32
    ).astype(BF16)
    query, key_part, val_part = qkv[0], qkv[1], qkv[2]
    scores = jnp.einsum("bhqd,bhkd->bhqk", query, key_part, preferred_element_type=F32) * scale
    probs_f = jnp.exp(scores - log_total)
    probs_att = probs_f.astype(BF16)
    d_val = jnp.einsum("bhqk,bhqd->bhkd", probs_att, d_att, preferred_element_type=F32)
    d_prob = jnp.einsum("bhqd,bhkd->bhqk", d_att, val_part, preferred_element_type=F32)
    d_score = (probs_f * (d_prob - jnp.sum(d_prob * probs_f, -1, keepdims=True))).astype(BF16)
    d_query = jnp.einsum("bhqk,bhkd->bhqd", d_score, key_part, preferred_element_type=F32) * scale
    d_key = jnp.einsum("bhqk,bhqd->bhkd", d_score, query, preferred_element_type=F32) * scale
    d_qkv = jnp.stack([d_query, d_key, d_val]).astype(BF16)
    d_qkv_f = d_qkv.astype(F32)
    g_bias_q = jnp.sum(d_qkv_f[0], (0, 2)).reshape(D)
    g_bias_v = jnp.sum(d_qkv_f[2], (0, 2)).reshape(D)
    first_b = first.reshape(nb, S, D)
    g_qkv = jnp.einsum("bsk,tbhsd->kthd", first_b, d_qkv, preferred_element_type=F32).reshape(D, 3 * D)
    w3 = w_qkv.reshape(D, 3, HEADS, HEAD_DIM)
    d_first = jnp.einsum("tbhsd,kthd->bsk", d_qkv, w3, preferred_element_type=F32).reshape(rows, D)
    first_pull = jax.vjp(layer_norm, value, table[0], table[1])[1]
    d_input, g_gain_one, g_shift_one = first_pull(d_first)
    return (g_qkv, g_out, g_bias_out, g_bias_q, g_bias_v, g_gain_one, g_shift_one), d_input


def adamw(weight, moments, grad, rate):
    first = 0.5 * moments[0] + 0.5 * grad
    root = jnp.sqrt(0.5 * moments[1] * moments[1] + 0.5 * grad * grad)
    update = first / (root + 1e-08)
    which = lax.broadcasted_iota(jnp.int32, moments.shape, 0) == 0
    both = jnp.where(which, 0.5 * moments + 0.5 * grad, jnp.sqrt(0.5 * moments * moments + 0.5 * grad * grad))
    return (weight - rate * (update + 0.1 * weight), both)


def shards(
    tokens,
    cotangent,
    expert_index,
    qkv_weight,
    out_weight,
    router_weight,
    up_weight,
    up_bias,
    down_weight,
    vectors,
    qkv_moments,
    out_moments,
    router_moments,
    up_moments,
    up_bias_moments,
    down_moments,
    vector_moments,
):
    rows = tokens.shape[0]
    micro = rows // MB_TOK
    gs = qkv_weight.shape[0]
    group_size = D // gs
    core = lax.axis_index("core")

    dense_in = pack_dense(qkv_weight, out_weight, router_weight, vectors, up_bias)
    width = dense_in.shape[1]
    dense_in = jnp.pad(dense_in, ((0, 0), (0, DENSE_AG - width))).astype(BF16)
    w_up_all, w_down_all, dense = ring_all_gather(
        up_weight.astype(BF16), down_weight.astype(BF16), dense_in, group_size, 1
    )
    w_qkv, w_out, w_router, table_b, b_up_b = unpack_dense(dense[:, :width])
    table = table_b.astype(F32)
    b_up = b_up_b.astype(F32)

    value = tokens.astype(F32)
    d_out = cotangent.astype(F32)
    first, qkv, log_total, attended, resid = attention_fwd(w_qkv, w_out, table, value)
    second = layer_norm(resid, table[5], table[6]).astype(BF16)
    logits = dot(second, w_router)
    probs = jax.nn.softmax(logits, -1)
    picked = expert_index[:, :, None] == jnp.arange(E, dtype=jnp.int32)
    gate = jnp.sum(jnp.where(picked, probs[:, None, :], 0.0), -1)

    route = expert_index.reshape(micro, MB_TOK, 2)
    places, counts = assign_places(route)
    counts = counts.T.reshape(E * micro)
    onehot = (places[:, :, None] == jnp.arange(E * CAPP, dtype=jnp.int32)).astype(BF16)
    second_m = second.reshape(micro, MB_TOK, D)
    pair = jnp.concatenate([second_m, second_m], 1)
    table_in = jnp.einsum("mnr,mnd->mrd", onehot, pair, preferred_element_type=F32).astype(BF16)

    hidden_pre, hidden, y_all = ffn_forward(
        counts, table_in, w_up_all, b_up[:, None, :], w_down_all, table[7 : 7 + E][:, None, :], micro
    )
    picked_rows = pick_rows(onehot, y_all)
    out_zero = picked_rows[:, :MB_TOK].reshape(rows, D)
    out_one = picked_rows[:, MB_TOK:].reshape(rows, D)
    result = resid + (gate[:, 0:1] * out_zero + gate[:, 1:2] * out_one)

    d_gate = jnp.stack([jnp.sum(d_out * out_zero, -1), jnp.sum(d_out * out_one, -1)], 1)
    d_out_m = d_out.reshape(micro, MB_TOK, D)
    gate_m = gate.reshape(micro, MB_TOK, 2)
    weighted = jnp.concatenate([gate_m[:, :, 0:1] * d_out_m, gate_m[:, :, 1:2] * d_out_m], 1).astype(BF16)
    d_expert = jnp.einsum("mnr,mnd->mrd", onehot, weighted, preferred_element_type=F32).astype(BF16)

    d_table, g_up, g_down, g_b1, g_b2 = ffn_backward(counts, d_expert, table_in, hidden_pre, hidden, w_up_all, w_down_all, micro)
    g_up_bias_all = g_b1[:, 0, :]
    g_bias_down = g_b2[:, 0, :]

    onehot_sum = onehot[:, :MB_TOK] + onehot[:, MB_TOK:]
    d_picked = pick_rows(onehot_sum, d_table).reshape(rows, D)

    d_probs = jnp.sum(jnp.where(picked, d_gate[:, :, None], 0.0), 1)
    d_logit = (probs * (d_probs - jnp.sum(d_probs * probs, -1, keepdims=True))).astype(BF16)
    g_router = lax.dot_general(second, d_logit, (((0,), (0,)), ((), ())), preferred_element_type=F32)
    d_second = d_picked + lax.dot_general(d_logit, w_router, (((1,), (1,)), ((), ())), preferred_element_type=F32)
    norm_pull = jax.vjp(layer_norm, resid, table[5], table[6])[1]
    d_resid, g_gain_two, g_shift_two = norm_pull(d_second)
    d_resid = d_out + d_resid

    att_grads, d_input = attention_bwd(w_qkv, w_out, table, value, first, qkv, log_total, attended, d_resid)
    g_qkv, g_out, g_bias_out, g_bias_q, g_bias_v, g_gain_one, g_shift_one = att_grads
    input_grad = d_resid + d_input

    g_table = jnp.concatenate(
        [
            jnp.stack([g_gain_one, g_shift_one, g_bias_q, g_bias_v, g_bias_out, g_gain_two, g_shift_two]),
            g_bias_down,
        ],
        0,
    )
    dense_g = pack_dense(g_qkv, g_out, g_router, g_table, g_up_bias_all)
    width = dense_g.shape[1]
    dense_g = jnp.pad(dense_g, ((0, 0), (0, DENSE_AG - width))).astype(BF16)
    x_pair = lax.axis_size("rx") == 2
    r_up, r_down, r_dense = grad_reduce(g_up, g_down, dense_g, group_size, x_pair, 0)
    if not x_pair:
        r_up, r_down, r_dense = lax.psum((r_up, r_down, r_dense), "rx")
    r_qkv, r_out, r_router, r_table, r_ub = unpack_dense(r_dense[:, :width])

    reduced = (r_qkv, r_out, r_router, r_up, r_ub, r_down, r_table)
    rates = (
        2.0 * D ** (-0.5),
        2.0 * (D // 32) ** (-0.5),
        2.0 * (2 * D) ** (-0.5),
        2.0 * D ** (-0.5),
        0.2,
        2.0 * (F // 16) ** (-0.5),
        0.2,
    )
    params = (qkv_weight, out_weight, router_weight, up_weight, up_bias, down_weight, vectors)
    moments = (qkv_moments, out_moments, router_moments, up_moments, up_bias_moments, down_moments, vector_moments)
    news = []
    states = []
    for weight, state, grad, rate in zip(params, moments, reduced, rates):
        if weight.ndim == 3:
            new_weight, new_state = adamw_pass(weight, state, grad, rate)
        else:
            new_weight, new_state = adamw(weight, state, grad, rate)
        news.append(new_weight)
        states.append(new_state)
    return (result.astype(BF16), input_grad) + reduced + tuple(news) + tuple(states)


def solution(mesh):
    replica, group = mesh.shape["replica"], mesh.shape["group"]
    view = Mesh(np.asarray(mesh.devices).reshape(replica // 2, 2, group), ("rx", "core", "group"))
    in_specs = (
        P(TOK, None),
        P(TOK, None),
        P(TOK, None),
        P("group", None),
        P("group", None),
        P("group", None),
        P(None, "group", None),
        P(None, "group"),
        P(None, "group", None),
        P(None, "group"),
        P(None, "group", None),
        P(None, "group", None),
        P(None, "group", None),
        P(None, None, "group", None),
        P(None, None, "group"),
        P(None, None, "group", None),
        P(None, None, "group"),
    )
    out_specs = (
        P(TOK, None),
        P(TOK, None),
        P("group", None),
        P("group", None),
        P("group", None),
        P(None, "group", None),
        P(None, "group"),
        P(None, "group", None),
        P(None, "group"),
        P("group", None),
        P("group", None),
        P("group", None),
        P(None, "group", None),
        P(None, "group"),
        P(None, "group", None),
        P(None, "group"),
        P(None, "group", None),
        P(None, "group", None),
        P(None, "group", None),
        P(None, None, "group", None),
        P(None, None, "group"),
        P(None, None, "group", None),
        P(None, None, "group"),
    )
    return jax.shard_map(shards, mesh=view, in_specs=in_specs, out_specs=out_specs, check_vma=False)
```

```python
import functools

import jax
import jax.numpy as jnp
import numpy as np
from jax import lax
from jax.sharding import Mesh
from jax.sharding import PartitionSpec as P
from jax.experimental import pallas as pl
from jax.experimental.pallas import tpu as pltpu

D = 512
HEADS = 8
HEAD_DIM = 64
F = 2048
E = 4
S = 197
MB_TOK = 394
CAP = 392
NV = 11
DENSE_AG = 2560
DENSE_PAD = 2304
F32 = jnp.float32
BF16 = jnp.bfloat16
TOK = ("rx", "core", "group")


MESH_ID = pl.DeviceIdType.MESH


def ring_order(groups):
    if groups in (4, 8):
        zs = groups // 2

        def pos_of(g):
            y = g % 2
            z = g // 2
            return z + y * (2 * zs - 1 - 2 * z)

        def dev_at(p):
            p = p % groups
            yy = p // zs
            return 2 * (p + yy * (2 * zs - 1 - 2 * p)) + yy

        return pos_of, dev_at
    return (lambda g: g), (lambda p: p % groups)


def ring_rs_kernel(groups, n_in, *refs):
    ins = refs[:n_in]
    outs = refs[n_in : 2 * n_in]
    rbufs = refs[2 * n_in : 3 * n_in]
    sbufs = refs[3 * n_in : 4 * n_in]
    owns = refs[4 * n_in : 5 * n_in]
    send_sem, recv_sem, load_sem = refs[5 * n_in :]
    pos_of, dev_at = ring_order(groups)
    rx = lax.axis_index("rx")
    core = lax.axis_index("core")
    g = lax.axis_index("group")
    pos = pos_of(g)
    nbr = (dev_at(pos + 1), dev_at(pos + groups - 1))

    barrier = pltpu.get_barrier_semaphore()
    for n in nbr:
        pl.semaphore_signal(barrier, inc=1, device_id=(rx, core, n), device_id_type=MESH_ID)
    pl.semaphore_wait(barrier, 2)

    def block_dev(d, s):
        if d == 0:
            return dev_at(pos + 2 * groups - s - 1)
        return dev_at(pos + s + 1)

    def load(d, s, slot):
        b = block_dev(d, s)
        copies = []
        for i in range(n_in):
            rows = ins[i].shape[1] // groups
            half = ins[i].shape[2] // 2
            src = ins[i].at[:, pl.ds(pl.multiple_of(b * rows, rows), rows), pl.ds(d * half, half)]
            copies.append(pltpu.make_async_copy(src, owns[i].at[d, slot], load_sem.at[d, slot, i]))
        return copies

    def remote(d, s, i):
        return pltpu.make_async_remote_copy(
            src_ref=sbufs[i].at[d, s],
            dst_ref=rbufs[i].at[d, s],
            send_sem=send_sem.at[d, s, i],
            recv_sem=recv_sem.at[d, s, i],
            device_id=(rx, core, nbr[d]),
            device_id_type=MESH_ID,
        )

    for d in range(2):
        for c in load(d, 0, 0):
            c.start()
    sends = []
    for s in range(groups):
        slot = s % 2
        for d in range(2):
            for c in load(d, s, slot):
                c.wait()
            if s + 1 < groups:
                for c in load(d, s + 1, 1 - slot):
                    c.start()
            for i in range(n_in):
                if s > 0:
                    remote(d, s - 1, i).wait_recv()
                for a in range(ins[i].shape[0]):
                    mine = owns[i][d, slot, a].astype(F32)
                    if s > 0:
                        mine = mine + rbufs[i][d, s - 1, a].astype(F32)
                    if s < groups - 1:
                        sbufs[i][d, s, a] = mine.astype(sbufs[i].dtype)
                    else:
                        half = ins[i].shape[2] // 2
                        outs[i][a, :, pl.ds(d * half, half)] = mine.astype(outs[i].dtype)
                if s < groups - 1:
                    c = remote(d, s, i)
                    c.start()
                    sends.append(c)
    for c in sends:
        c.wait_send()


def ring_reduce_scatter(xs, groups, collective_id):
    n_in = len(xs)
    outs, rb, own = [], [], []
    flops = 0
    nbytes = 0
    for x in xs:
        a, total, c = x.shape
        rows = total // groups
        outs.append(jax.ShapeDtypeStruct((a, rows, c), x.dtype))
        rb.append(pltpu.VMEM((2, groups - 1, a, rows, c // 2), x.dtype))
        own.append(pltpu.VMEM((2, 2, a, rows, c // 2), x.dtype))
        flops += a * total * c
        nbytes += 3 * x.size * x.dtype.itemsize
    scratch = rb + rb + own + [
        pltpu.SemaphoreType.DMA((2, groups - 1, n_in)),
        pltpu.SemaphoreType.DMA((2, groups - 1, n_in)),
        pltpu.SemaphoreType.DMA((2, 2, n_in)),
    ]
    return pl.pallas_call(
        functools.partial(ring_rs_kernel, groups, n_in),
        out_shape=outs,
        in_specs=[pl.BlockSpec(memory_space=pl.ANY)] * n_in,
        out_specs=[pl.BlockSpec(memory_space=pltpu.VMEM)] * n_in,
        scratch_shapes=scratch,
        compiler_params=pltpu.CompilerParams(
            collective_id=collective_id, has_side_effects=True, vmem_limit_bytes=60 * 1024 * 1024
        ),
        cost_estimate=pl.CostEstimate(flops=flops, bytes_accessed=nbytes, transcendentals=0),
    )(*xs)


def ring_ag_kernel(groups, *refs):
    in_up, in_down, in_dense, out_up, out_down, out_dense = refs[:6]
    ring_send, ring_recv, part_send, part_recv, local_sem = refs[6:]
    pos_of, dev_at = ring_order(groups)
    rx = lax.axis_index("rx")
    core = lax.axis_index("core")
    g = lax.axis_index("group")
    other = 1 - core
    pos = pos_of(g)
    nbr = (dev_at(pos + 1), dev_at(pos + groups - 1))
    gs = in_up.shape[1]
    fs = in_down.shape[1]
    width = in_dense.shape[1] // 2

    barrier = pltpu.get_barrier_semaphore()
    for n in nbr:
        pl.semaphore_signal(barrier, inc=1, device_id=(rx, core, n), device_id_type=MESH_ID)
    pl.semaphore_signal(barrier, inc=1, device_id=(rx, other, g), device_id_type=MESH_ID)
    pl.semaphore_wait(barrier, 3)

    def items(owner):
        found = []
        for k in range(2):
            e = 2 * k + owner
            found.append((in_up.at[e], lambda b, e=e: out_up.at[e, pl.ds(pl.multiple_of(b * gs, gs), gs)], F // 2))
            found.append((in_down.at[e], lambda b, e=e: out_down.at[e, pl.ds(pl.multiple_of(b * fs, fs), fs)], D // 2))
        dense_in = in_dense.at[:, pl.ds(owner * width, width)]
        found.append(
            (dense_in, lambda b: out_dense.at[pl.ds(pl.multiple_of(b * gs, gs), gs), pl.ds(owner * width, width)], width // 2)
        )
        return found

    mine = items(core)
    theirs = items(other)
    n_items = len(mine)

    locals_ = [pltpu.make_async_copy(in_up.at[e], out_up.at[e, pl.ds(pl.multiple_of(g * gs, gs), gs)], local_sem.at[e]) for e in range(E)]
    locals_ += [
        pltpu.make_async_copy(in_down.at[e], out_down.at[e, pl.ds(pl.multiple_of(g * fs, fs), fs)], local_sem.at[E + e])
        for e in range(E)
    ]
    locals_.append(pltpu.make_async_copy(in_dense, out_dense.at[pl.ds(pl.multiple_of(g * gs, gs), gs)], local_sem.at[2 * E]))
    for c in locals_:
        c.start()

    def block_at(d, s):
        if d == 0:
            return dev_at(pos + 2 * groups - 1 - s)
        return dev_at(pos + 1 + s)

    def ring_copy(d, s, j, src_block):
        src_in, dst_of, half = mine[j]
        cols = pl.ds(d * half, half)
        if src_block is None:
            src = src_in.at[:, cols]
            dst = dst_of(g).at[:, cols]
        else:
            src = dst_of(src_block).at[:, cols]
            dst = src
        return pltpu.make_async_remote_copy(
            src_ref=src, dst_ref=dst, send_sem=ring_send.at[d, s, j], recv_sem=ring_recv.at[d, s, j],
            device_id=(rx, core, nbr[d]), device_id_type=MESH_ID,
        )

    def part_copy(d, s, j, table, block):
        _, dst_of, half = table[j]
        view = dst_of(block).at[:, pl.ds(d * half, half)]
        return pltpu.make_async_remote_copy(
            src_ref=view, dst_ref=view, send_sem=part_send.at[d, s, j], recv_sem=part_recv.at[d, s, j],
            device_id=(rx, other, g), device_id_type=MESH_ID,
        )

    sends = []
    for d in range(2):
        for j in range(n_items):
            c = ring_copy(d, 0, j, None)
            c.start()
            sends.append(c)
    for s in range(groups - 1):
        for d in range(2):
            b = block_at(d, s)
            for j in range(n_items):
                pltpu.make_async_remote_copy(
                    src_ref=mine[j][1](b).at[:, pl.ds(d * mine[j][2], mine[j][2])],
                    dst_ref=mine[j][1](b).at[:, pl.ds(d * mine[j][2], mine[j][2])],
                    send_sem=ring_send.at[d, s, j], recv_sem=ring_recv.at[d, s, j],
                    device_id=(rx, core, nbr[d]), device_id_type=MESH_ID,
                ).wait_recv()
                if s + 1 < groups - 1:
                    c = ring_copy(d, s + 1, j, b)
                    c.start()
                    sends.append(c)
                c = part_copy(d, s, j, mine, b)
                c.start()
                sends.append(c)
    for s in range(groups - 1):
        for d in range(2):
            b = block_at(d, s)
            for j in range(n_items):
                part_copy(d, s, j, theirs, b).wait_recv()
    for c in sends:
        c.wait_send()
    for c in locals_:
        c.wait()


def ring_all_gather(up_b, down_b, dense_b, groups, collective_id):
    n_items = 5
    gs = up_b.shape[1]
    shapes = [
        jax.ShapeDtypeStruct((E, gs * groups, F), BF16),
        jax.ShapeDtypeStruct((E, down_b.shape[1] * groups, D), BF16),
        jax.ShapeDtypeStruct((gs * groups, dense_b.shape[1]), BF16),
    ]
    nbytes = sum(int(np.prod(s.shape)) * 2 for s in shapes)
    return pl.pallas_call(
        functools.partial(ring_ag_kernel, groups),
        out_shape=shapes,
        in_specs=[pl.BlockSpec(memory_space=pl.ANY)] * 3,
        out_specs=[pl.BlockSpec(memory_space=pl.ANY)] * 3,
        scratch_shapes=[
            pltpu.SemaphoreType.DMA((2, groups - 1, n_items)),
            pltpu.SemaphoreType.DMA((2, groups - 1, n_items)),
            pltpu.SemaphoreType.DMA((2, groups - 1, n_items)),
            pltpu.SemaphoreType.DMA((2, groups - 1, n_items)),
            pltpu.SemaphoreType.DMA((2 * E + 1,)),
        ],
        compiler_params=pltpu.CompilerParams(collective_id=collective_id, has_side_effects=True),
        cost_estimate=pl.CostEstimate(flops=0, bytes_accessed=nbytes, transcendentals=0),
    )(up_b, down_b, dense_b)


def grad_items(gu, gd, gdense, owner, gs, fs, width):
    found = []
    for k in range(2):
        e = 2 * k + owner
        found.append((lambda b, e=e: gu.at[e, pl.ds(pl.multiple_of(b * gs, gs), gs)], F // 2))
        found.append((lambda b, e=e: gd.at[e, pl.ds(pl.multiple_of(b * fs, fs), fs)], D // 2))
    found.append((lambda b: gdense.at[pl.ds(pl.multiple_of(b * gs, gs), gs), pl.ds(owner * width, width)], width // 2))
    return found


def ring_rs2_kernel(groups, x_pair, *refs):
    gu, gd, gdense, out_up, out_down, out_dense = refs[:6]
    n_items = 5
    scr = refs[6:]
    rbuf, sbuf, pbuf, own, fin, xr, cr, xs = (scr[i * n_items : (i + 1) * n_items] for i in range(8))
    ring_send, ring_recv, part_send, part_recv, load_sem, x_send, x_recv, c_send, c_recv = scr[8 * n_items :]
    pos_of, dev_at = ring_order(groups)
    rx = lax.axis_index("rx")
    core = lax.axis_index("core")
    g = lax.axis_index("group")
    other = 1 - core
    pos = pos_of(g)
    nbr = (dev_at(pos + 1), dev_at(pos + groups - 1))
    gs = gu.shape[1] // groups
    fs = gd.shape[1] // groups
    width = gdense.shape[1] // 2
    mine = grad_items(gu, gd, gdense, core, gs, fs, width)
    theirs = grad_items(gu, gd, gdense, other, gs, fs, width)

    barrier = pltpu.get_barrier_semaphore()
    for n in nbr:
        pl.semaphore_signal(barrier, inc=1, device_id=(rx, core, n), device_id_type=MESH_ID)
    pl.semaphore_signal(barrier, inc=1, device_id=(rx, other, g), device_id_type=MESH_ID)
    count = 3
    if x_pair:
        pl.semaphore_signal(barrier, inc=1, device_id=(1 - rx, core, g), device_id_type=MESH_ID)
        count = 4
    pl.semaphore_wait(barrier, count)

    def block_at(d, s):
        if d == 0:
            return dev_at(pos + 2 * groups - 1 - s)
        return dev_at(pos + 1 + s)

    def cols(j, d):
        half = mine[j][1]
        return pl.ds(d * half, half)

    def load(d, s, slot, j):
        return pltpu.make_async_copy(mine[j][0](block_at(d, s)).at[:, cols(j, d)], own[j].at[d, slot], load_sem.at[d, slot, j])

    def part(d, s, j):
        return pltpu.make_async_remote_copy(
            src_ref=theirs[j][0](block_at(d, s)).at[:, cols(j, d)], dst_ref=pbuf[j].at[d, s],
            send_sem=part_send.at[d, s, j], recv_sem=part_recv.at[d, s, j],
            device_id=(rx, other, g), device_id_type=MESH_ID,
        )

    def ring(d, s, j):
        return pltpu.make_async_remote_copy(
            src_ref=sbuf[j].at[d, s], dst_ref=rbuf[j].at[d, s],
            send_sem=ring_send.at[d, s, j], recv_sem=ring_recv.at[d, s, j],
            device_id=(rx, core, nbr[d]), device_id_type=MESH_ID,
        )

    sends = []

    def ring_wave(items):
        for d in range(2):
            for j in items:
                load(d, 0, 0, j).start()
                c = part(d, 0, j)
                c.start()
                sends.append(c)
        for s in range(groups):
            slot = s % 2
            for d in range(2):
                for j in items:
                    load(d, s, slot, j).wait()
                    if s + 1 < groups:
                        load(d, s + 1, 1 - slot, j).start()
                        c = part(d, s + 1, j)
                        c.start()
                        sends.append(c)
                    part(d, s, j).wait_recv()
                    val = own[j][d, slot].astype(F32) + pbuf[j][d, s].astype(F32)
                    if s > 0:
                        ring(d, s - 1, j).wait_recv()
                        val = val + rbuf[j][d, s - 1].astype(F32)
                    if s < groups - 1:
                        sbuf[j][d, s] = val.astype(BF16)
                        c = ring(d, s, j)
                        c.start()
                        sends.append(c)
                    else:
                        fin[j][d] = val

    def x_start(items):
        copies = []
        for d in range(2):
            for j in items:
                xs[j][d] = fin[j][d].astype(BF16)
                c = pltpu.make_async_remote_copy(
                    src_ref=xs[j].at[d], dst_ref=xr[j].at[d], send_sem=x_send.at[d, j], recv_sem=x_recv.at[d, j],
                    device_id=(1 - rx, core, g), device_id_type=MESH_ID,
                )
                c.start()
                copies.append(c)
        sends.extend(copies)
        return copies

    def x_finish(items, copies):
        for c in copies:
            c.wait_recv()
        for d in range(2):
            for j in items:
                fin[j][d] = xs[j][d].astype(F32) + xr[j][d].astype(F32)

    def c_start(items):
        copies = []
        for d in range(2):
            for j in items:
                c = pltpu.make_async_remote_copy(
                    src_ref=fin[j].at[d], dst_ref=cr[j].at[d], send_sem=c_send.at[d, j], recv_sem=c_recv.at[d, j],
                    device_id=(rx, other, g), device_id_type=MESH_ID,
                )
                c.start()
                copies.append(c)
        return copies

    wave_a, wave_b = (0, 1, 2, 4), (3,)
    ring_wave(wave_a)
    if x_pair:
        xa = x_start(wave_a)
    ring_wave(wave_b)
    if x_pair:
        x_finish(wave_a, xa)
    c_copies = c_start(wave_a)
    if x_pair:
        x_finish(wave_b, x_start(wave_b))
    c_copies += c_start(wave_b)

    def out_items(owner):
        found = []
        for k in range(2):
            e = 2 * k + owner
            found.append(lambda d, e=e: out_up.at[e, :, pl.ds(d * (F // 2), F // 2)])
            found.append(lambda d, e=e: out_down.at[e, :, pl.ds(d * (D // 2), D // 2)])
        found.append(lambda d: out_dense.at[:, pl.ds(owner * width + d * (width // 2), width // 2)])
        return found

    mine_out = out_items(core)
    theirs_out = out_items(other)
    for d in range(2):
        for j in range(n_items):
            mine_out[j](d)[...] = fin[j][d]
    for c in c_copies:
        c.wait_recv()
    for d in range(2):
        for j in range(n_items):
            theirs_out[j](d)[...] = cr[j][d]
    for c in sends + c_copies:
        c.wait_send()


def grad_reduce(gu, gd, gdense, groups, x_pair, collective_id):
    gs = gu.shape[1] // groups
    fs = gd.shape[1] // groups
    width = gdense.shape[1] // 2
    item_shapes = [(gs, F // 2), (fs, D // 2), (gs, F // 2), (fs, D // 2), (gs, width // 2)]
    scratch = []
    for lead, dtype in (((2, groups - 1), BF16), ((2, groups - 1), BF16), ((2, groups), BF16), ((2, 2), BF16), ((2,), F32), ((2,), BF16), ((2,), F32), ((2,), BF16)):
        scratch += [pltpu.VMEM(lead + shp, dtype) for shp in item_shapes]
    scratch += [
        pltpu.SemaphoreType.DMA((2, groups - 1, 5)),
        pltpu.SemaphoreType.DMA((2, groups - 1, 5)),
        pltpu.SemaphoreType.DMA((2, groups, 5)),
        pltpu.SemaphoreType.DMA((2, groups, 5)),
        pltpu.SemaphoreType.DMA((2, 2, 5)),
        pltpu.SemaphoreType.DMA((2, 5)),
        pltpu.SemaphoreType.DMA((2, 5)),
        pltpu.SemaphoreType.DMA((2, 5)),
        pltpu.SemaphoreType.DMA((2, 5)),
    ]
    outs = [
        jax.ShapeDtypeStruct((E, gs, F), F32),
        jax.ShapeDtypeStruct((E, fs, D), F32),
        jax.ShapeDtypeStruct((gs, gdense.shape[1]), F32),
    ]
    nbytes = 2 * (gu.size + gd.size + gdense.size)
    return pl.pallas_call(
        functools.partial(ring_rs2_kernel, groups, x_pair),
        out_shape=outs,
        in_specs=[pl.BlockSpec(memory_space=pl.ANY)] * 3,
        out_specs=[pl.BlockSpec(memory_space=pltpu.VMEM)] * 3,
        scratch_shapes=scratch,
        compiler_params=pltpu.CompilerParams(
            collective_id=collective_id, has_side_effects=True, vmem_limit_bytes=62 * 1024 * 1024
        ),
        cost_estimate=pl.CostEstimate(flops=gu.size + gd.size + gdense.size, bytes_accessed=nbytes, transcendentals=0),
    )(gu, gd, gdense)


TILE = 256
TILE_B = 256
CAPP = 512
SQRT_HALF = float(np.sqrt(0.5))
INV_SQRT_2PI = float(1.0 / np.sqrt(2.0 * np.pi))


def ffn_fwd_kernel(micro, counts, x_ref, w1_ref, b1_ref, w2_ref, b2_ref, hp_ref, h_ref, y_ref):
    e, m, t = pl.program_id(0), pl.program_id(1), pl.program_id(2)
    active = t * TILE < counts[e * micro + m]

    @pl.when(active)
    def _():
        hp = jnp.dot(x_ref[0], w1_ref[0], preferred_element_type=F32) + b1_ref[0]
        cdf = 0.5 * (1.0 + lax.erf(hp * SQRT_HALF))
        h = (hp * cdf).astype(BF16)
        hp_ref[0] = cdf + hp * jnp.exp(-0.5 * hp * hp) * INV_SQRT_2PI
        h_ref[0] = h
        y = jnp.dot(h, w2_ref[0], preferred_element_type=F32) + b2_ref[0]
        hi = y.astype(BF16)
        y_ref[0, :, :D] = hi
        y_ref[0, :, D:] = (y - hi.astype(F32)).astype(BF16)

    @pl.when(jnp.logical_not(active))
    def _():
        y_ref[0] = jnp.zeros(y_ref.shape[1:], BF16)


def ffn_forward(counts, table_in, w1, b1, w2, b2, micro):
    tiles = CAPP // TILE
    rows = table_in.shape[1]
    row_map = lambda e, m, t, c: (m, e * tiles + t, 0)
    w_map = lambda e, m, t, c: (e, 0, 0)
    grid_spec = pltpu.PrefetchScalarGridSpec(
        num_scalar_prefetch=1,
        grid=(E, micro, tiles),
        in_specs=[
            pl.BlockSpec((1, TILE, D), row_map),
            pl.BlockSpec((1, D, F), w_map),
            pl.BlockSpec((1, 1, F), w_map),
            pl.BlockSpec((1, F, D), w_map),
            pl.BlockSpec((1, 1, D), w_map),
        ],
        out_specs=[
            pl.BlockSpec((1, TILE, F), row_map),
            pl.BlockSpec((1, TILE, F), row_map),
            pl.BlockSpec((1, TILE, 2 * D), row_map),
        ],
    )
    work = micro * rows
    return pl.pallas_call(
        functools.partial(ffn_fwd_kernel, micro),
        grid_spec=grid_spec,
        out_shape=[
            jax.ShapeDtypeStruct((micro, rows, F), F32),
            jax.ShapeDtypeStruct((micro, rows, F), BF16),
            jax.ShapeDtypeStruct((micro, rows, 2 * D), BF16),
        ],
        compiler_params=pltpu.CompilerParams(vmem_limit_bytes=48 * 1024 * 1024),
        cost_estimate=pl.CostEstimate(
            flops=4 * work * D * F // 2, bytes_accessed=work * (2 * D + 6 * F + 4 * D) // 2, transcendentals=work * F // 2
        ),
    )(counts, table_in, w1, b1, w2, b2)


def ffn_bwd_kernel(micro, counts, dy_ref, x_ref, hp_ref, h_ref, w1_ref, w2_ref, dt_ref, gu_ref, gd_ref, gb_ref, gb2_ref, gu_acc, gd_acc):
    e, m, t = pl.program_id(0), pl.program_id(1), pl.program_id(2)
    active = t * TILE_B < counts[e * micro + m]

    @pl.when((m == 0) & (t == 0))
    def _():
        gu_acc[...] = jnp.zeros(gu_acc.shape, F32)
        gd_acc[...] = jnp.zeros(gd_acc.shape, F32)
        gb_ref[...] = jnp.zeros(gb_ref.shape, F32)
        gb2_ref[...] = jnp.zeros(gb2_ref.shape, F32)

    @pl.when(active)
    def _():
        dy = dy_ref[0]
        d_hidden = lax.dot_general(dy, w2_ref[0], (((1,), (1,)), ((), ())), preferred_element_type=F32)
        d_pre = (d_hidden * hp_ref[0]).astype(BF16)
        dt = lax.dot_general(d_pre, w1_ref[0], (((1,), (1,)), ((), ())), preferred_element_type=F32)
        hi = dt.astype(BF16)
        dt_ref[0, :, :D] = hi
        dt_ref[0, :, D:] = (dt - hi.astype(F32)).astype(BF16)
        gb2_ref[0] += jnp.sum(dy.astype(F32), 0, keepdims=True)
        gu_acc[...] += lax.dot_general(x_ref[0], d_pre, (((0,), (0,)), ((), ())), preferred_element_type=F32)
        gd_acc[...] += lax.dot_general(h_ref[0], dy, (((0,), (0,)), ((), ())), preferred_element_type=F32)
        gb_ref[0] += jnp.sum(d_pre.astype(F32), 0, keepdims=True)

    @pl.when(jnp.logical_not(active))
    def _():
        dt_ref[0] = jnp.zeros(dt_ref.shape[1:], BF16)

    @pl.when((m == micro - 1) & (t == pl.num_programs(2) - 1))
    def _():
        gu_ref[0] = gu_acc[...].astype(BF16)
        gd_ref[0] = gd_acc[...].astype(BF16)


def ffn_backward(counts, d_expert, table_in, hp, h, w1, w2, micro):
    tiles = CAPP // TILE_B
    rows = table_in.shape[1]
    row_map = lambda e, m, t, c: (m, e * tiles + t, 0)
    w_map = lambda e, m, t, c: (e, 0, 0)
    grid_spec = pltpu.PrefetchScalarGridSpec(
        num_scalar_prefetch=1,
        grid=(E, micro, tiles),
        in_specs=[
            pl.BlockSpec((1, TILE_B, D), row_map),
            pl.BlockSpec((1, TILE_B, D), row_map),
            pl.BlockSpec((1, TILE_B, F), row_map),
            pl.BlockSpec((1, TILE_B, F), row_map),
            pl.BlockSpec((1, D, F), w_map),
            pl.BlockSpec((1, F, D), w_map),
        ],
        out_specs=[
            pl.BlockSpec((1, TILE_B, 2 * D), row_map),
            pl.BlockSpec((1, D, F), w_map),
            pl.BlockSpec((1, F, D), w_map),
            pl.BlockSpec((1, 1, F), w_map),
            pl.BlockSpec((1, 1, D), w_map),
        ],
        scratch_shapes=[pltpu.VMEM((D, F), F32), pltpu.VMEM((F, D), F32)],
    )
    work = micro * rows
    return pl.pallas_call(
        functools.partial(ffn_bwd_kernel, micro),
        grid_spec=grid_spec,
        out_shape=[
            jax.ShapeDtypeStruct((micro, rows, 2 * D), BF16),
            jax.ShapeDtypeStruct((E, D, F), BF16),
            jax.ShapeDtypeStruct((E, F, D), BF16),
            jax.ShapeDtypeStruct((E, 1, F), F32),
            jax.ShapeDtypeStruct((E, 1, D), F32),
        ],
        compiler_params=pltpu.CompilerParams(vmem_limit_bytes=60 * 1024 * 1024),
        cost_estimate=pl.CostEstimate(
            flops=8 * work * D * F // 2, bytes_accessed=work * (8 * D + 6 * F) // 2 + 16 * E * D * F, transcendentals=2 * work * F // 2
        ),
    )(counts, d_expert, table_in, hp, h, w1, w2)

def adamw_kernel(rate, w_ref, m_ref, g_ref, wo_ref, mo_ref):
    g = g_ref[...]
    first = 0.5 * m_ref[0] + 0.5 * g
    root = jnp.sqrt(0.5 * m_ref[1] * m_ref[1] + 0.5 * g * g)
    w = w_ref[...]
    wo_ref[...] = w - rate * (first / (root + 1e-08) + 0.1 * w)
    mo_ref[0] = first
    mo_ref[1] = root


def adamw_pass(weight, moments, grad, rate):
    n, r, c = weight.shape
    spec = pl.BlockSpec((1, r, c), lambda i: (i, 0, 0))
    mspec = pl.BlockSpec((2, 1, r, c), lambda i: (0, i, 0, 0))
    return pl.pallas_call(
        functools.partial(adamw_kernel, rate),
        grid=(n,),
        in_specs=[spec, mspec, spec],
        out_specs=[spec, mspec],
        out_shape=[jax.ShapeDtypeStruct(weight.shape, F32), jax.ShapeDtypeStruct(moments.shape, F32)],
        cost_estimate=pl.CostEstimate(flops=12 * weight.size, bytes_accessed=28 * weight.size, transcendentals=2 * weight.size),
    )(weight, moments, grad)


def layer_norm(value, gain, shift):
    center = value - jnp.mean(value, -1, keepdims=True)
    spread = jnp.mean(center * center, -1, keepdims=True)
    return center * lax.rsqrt(spread + 1e-06) * gain + shift


def gelu_exact(value):
    return jax.nn.gelu(value, approximate=False)


def split_heads(part):
    return part.reshape(-1, S, HEADS, HEAD_DIM)


def dot(a, b):
    return jnp.dot(a, b, preferred_element_type=F32)


def assign_places(route):
    chosen = jnp.concatenate([route[:, :, 0], route[:, :, 1]], 1)
    hits = (chosen[:, :, None] == jnp.arange(E, dtype=jnp.int32)).astype(jnp.int32)
    before = jnp.cumsum(hits, 1) - hits
    slot = jnp.sum(before * hits, 2)
    return chosen * CAPP + slot, jnp.sum(hits, 1)


def hi_lo(v):
    hi = v.astype(BF16)
    lo = (v - hi.astype(F32)).astype(BF16)
    return jnp.concatenate([hi, lo], -1)


def pick_rows(onehot, split):
    both = jnp.einsum("mnr,mrd->mnd", onehot, split, preferred_element_type=F32)
    return both[..., :D] + both[..., D:]


def pack_dense(qkv_w, out_w, router_w, vectors, up_bias):
    rows = qkv_w.shape[0]
    ub = up_bias.reshape(E, rows, 4).transpose(1, 0, 2).reshape(rows, E * 4)
    return jnp.concatenate([qkv_w, out_w, router_w, vectors.T, ub], 1)


def unpack_dense(packed):
    rows = packed.shape[0]
    w_qkv = packed[:, : 3 * D]
    w_out = packed[:, 3 * D : 4 * D]
    w_router = packed[:, 4 * D : 4 * D + E]
    table = packed[:, 4 * D + E : 4 * D + E + NV].T
    ub = packed[:, 4 * D + E + NV :].reshape(rows, E, 4).transpose(1, 0, 2).reshape(E, rows * 4)
    return w_qkv, w_out, w_router, table, ub


def attention_fwd(w_qkv, w_out, table, value):
    rows = value.shape[0]
    nb = rows // S
    scale = HEAD_DIM ** (-0.5)
    first = layer_norm(value, table[0], table[1]).astype(BF16)
    qkv_bias = jnp.concatenate([table[2], jnp.zeros((D,), F32), table[3]]).reshape(3, 1, HEADS, 1, HEAD_DIM)
    w3 = w_qkv.reshape(D, 3, HEADS, HEAD_DIM)
    qkv = (jnp.einsum("bsk,kthd->tbhsd", first.reshape(nb, S, D), w3, preferred_element_type=F32) + qkv_bias).astype(BF16)
    query, key_part, val_part = qkv[0], qkv[1], qkv[2]
    scores = jnp.einsum("bhqd,bhkd->bhqk", query, key_part, preferred_element_type=F32) * scale
    peak = jnp.max(scores, -1, keepdims=True)
    expo = jnp.exp(scores - peak)
    total = jnp.sum(expo, -1, keepdims=True)
    probs_att = (expo / total).astype(BF16)
    log_total = peak + jnp.log(total)
    attended = jnp.einsum("bhqk,bhkd->bhqd", probs_att, val_part, preferred_element_type=F32).astype(BF16)
    branch = jnp.einsum("bhqd,hdn->bqn", attended, w_out.reshape(HEADS, HEAD_DIM, D), preferred_element_type=F32)
    resid = value + (branch.reshape(rows, D) + table[4])
    return first, qkv, log_total, attended, resid


def attention_bwd(w_qkv, w_out, table, value, first, qkv, log_total, attended, d_resid):
    rows = value.shape[0]
    nb = rows // S
    scale = HEAD_DIM ** (-0.5)
    d_branch = d_resid.astype(BF16)
    g_bias_out = jnp.sum(d_branch.astype(F32), 0)
    g_out = jnp.einsum("bhqd,bqn->hdn", attended, d_branch.reshape(nb, S, D), preferred_element_type=F32).reshape(D, D)
    d_att = jnp.einsum(
        "bsn,hdn->bhsd", d_branch.reshape(nb, S, D), w_out.reshape(HEADS, HEAD_DIM, D), preferred_element_type=F32
    ).astype(BF16)
    query, key_part, val_part = qkv[0], qkv[1], qkv[2]
    scores = jnp.einsum("bhqd,bhkd->bhqk", query, key_part, preferred_element_type=F32) * scale
    probs_f = jnp.exp(scores - log_total)
    probs_att = probs_f.astype(BF16)
    d_val = jnp.einsum("bhqk,bhqd->bhkd", probs_att, d_att, preferred_element_type=F32)
    d_prob = jnp.einsum("bhqd,bhkd->bhqk", d_att, val_part, preferred_element_type=F32)
    d_score = (probs_f * (d_prob - jnp.sum(d_prob * probs_f, -1, keepdims=True))).astype(BF16)
    d_query = jnp.einsum("bhqk,bhkd->bhqd", d_score, key_part, preferred_element_type=F32) * scale
    d_key = jnp.einsum("bhqk,bhqd->bhkd", d_score, query, preferred_element_type=F32) * scale
    d_qkv = jnp.stack([d_query, d_key, d_val]).astype(BF16)
    d_qkv_f = d_qkv.astype(F32)
    g_bias_q = jnp.sum(d_qkv_f[0], (0, 2)).reshape(D)
    g_bias_v = jnp.sum(d_qkv_f[2], (0, 2)).reshape(D)
    first_b = first.reshape(nb, S, D)
    g_qkv = jnp.einsum("bsk,tbhsd->kthd", first_b, d_qkv, preferred_element_type=F32).reshape(D, 3 * D)
    w3 = w_qkv.reshape(D, 3, HEADS, HEAD_DIM)
    d_first = jnp.einsum("tbhsd,kthd->bsk", d_qkv, w3, preferred_element_type=F32).reshape(rows, D)
    first_pull = jax.vjp(layer_norm, value, table[0], table[1])[1]
    d_input, g_gain_one, g_shift_one = first_pull(d_first)
    return (g_qkv, g_out, g_bias_out, g_bias_q, g_bias_v, g_gain_one, g_shift_one), d_input


def adamw(weight, moments, grad, rate):
    first = 0.5 * moments[0] + 0.5 * grad
    root = jnp.sqrt(0.5 * moments[1] * moments[1] + 0.5 * grad * grad)
    update = first / (root + 1e-08)
    which = lax.broadcasted_iota(jnp.int32, moments.shape, 0) == 0
    both = jnp.where(which, 0.5 * moments + 0.5 * grad, jnp.sqrt(0.5 * moments * moments + 0.5 * grad * grad))
    return (weight - rate * (update + 0.1 * weight), both)


def shards(
    tokens,
    cotangent,
    expert_index,
    qkv_weight,
    out_weight,
    router_weight,
    up_weight,
    up_bias,
    down_weight,
    vectors,
    qkv_moments,
    out_moments,
    router_moments,
    up_moments,
    up_bias_moments,
    down_moments,
    vector_moments,
):
    rows = tokens.shape[0]
    micro = rows // MB_TOK
    gs = qkv_weight.shape[0]
    group_size = D // gs
    core = lax.axis_index("core")

    dense_in = pack_dense(qkv_weight, out_weight, router_weight, vectors, up_bias)
    width = dense_in.shape[1]
    dense_in = jnp.pad(dense_in, ((0, 0), (0, DENSE_AG - width))).astype(BF16)
    w_up_all, w_down_all, dense = ring_all_gather(
        up_weight.astype(BF16), down_weight.astype(BF16), dense_in, group_size, 1
    )
    w_qkv, w_out, w_router, table_b, b_up_b = unpack_dense(dense[:, :width])
    table = table_b.astype(F32)
    b_up = b_up_b.astype(F32)

    value = tokens.astype(F32)
    d_out = cotangent.astype(F32)
    first, qkv, log_total, attended, resid = attention_fwd(w_qkv, w_out, table, value)
    second = layer_norm(resid, table[5], table[6]).astype(BF16)
    logits = dot(second, w_router)
    probs = jax.nn.softmax(logits, -1)
    picked = expert_index[:, :, None] == jnp.arange(E, dtype=jnp.int32)
    gate = jnp.sum(jnp.where(picked, probs[:, None, :], 0.0), -1)

    route = expert_index.reshape(micro, MB_TOK, 2)
    places, counts = assign_places(route)
    counts = counts.T.reshape(E * micro)
    onehot = (places[:, :, None] == jnp.arange(E * CAPP, dtype=jnp.int32)).astype(BF16)
    second_m = second.reshape(micro, MB_TOK, D)
    pair = jnp.concatenate([second_m, second_m], 1)
    table_in = jnp.einsum("mnr,mnd->mrd", onehot, pair, preferred_element_type=F32).astype(BF16)

    hidden_pre, hidden, y_all = ffn_forward(
        counts, table_in, w_up_all, b_up[:, None, :], w_down_all, table[7 : 7 + E][:, None, :], micro
    )
    picked_rows = pick_rows(onehot, y_all)
    out_zero = picked_rows[:, :MB_TOK].reshape(rows, D)
    out_one = picked_rows[:, MB_TOK:].reshape(rows, D)
    result = resid + (gate[:, 0:1] * out_zero + gate[:, 1:2] * out_one)

    d_gate = jnp.stack([jnp.sum(d_out * out_zero, -1), jnp.sum(d_out * out_one, -1)], 1)
    d_out_m = d_out.reshape(micro, MB_TOK, D)
    gate_m = gate.reshape(micro, MB_TOK, 2)
    weighted = jnp.concatenate([gate_m[:, :, 0:1] * d_out_m, gate_m[:, :, 1:2] * d_out_m], 1).astype(BF16)
    d_expert = jnp.einsum("mnr,mnd->mrd", onehot, weighted, preferred_element_type=F32).astype(BF16)

    d_table, g_up, g_down, g_b1, g_b2 = ffn_backward(counts, d_expert, table_in, hidden_pre, hidden, w_up_all, w_down_all, micro)
    g_up_bias_all = g_b1[:, 0, :]
    g_bias_down = g_b2[:, 0, :]

    onehot_sum = onehot[:, :MB_TOK] + onehot[:, MB_TOK:]
    d_picked = pick_rows(onehot_sum, d_table).reshape(rows, D)

    d_probs = jnp.sum(jnp.where(picked, d_gate[:, :, None], 0.0), 1)
    d_logit = (probs * (d_probs - jnp.sum(d_probs * probs, -1, keepdims=True))).astype(BF16)
    g_router = lax.dot_general(second, d_logit, (((0,), (0,)), ((), ())), preferred_element_type=F32)
    d_second = d_picked + lax.dot_general(d_logit, w_router, (((1,), (1,)), ((), ())), preferred_element_type=F32)
    norm_pull = jax.vjp(layer_norm, resid, table[5], table[6])[1]
    d_resid, g_gain_two, g_shift_two = norm_pull(d_second)
    d_resid = d_out + d_resid

    att_grads, d_input = attention_bwd(w_qkv, w_out, table, value, first, qkv, log_total, attended, d_resid)
    g_qkv, g_out, g_bias_out, g_bias_q, g_bias_v, g_gain_one, g_shift_one = att_grads
    input_grad = d_resid + d_input

    g_table = jnp.concatenate(
        [
            jnp.stack([g_gain_one, g_shift_one, g_bias_q, g_bias_v, g_bias_out, g_gain_two, g_shift_two]),
            g_bias_down,
        ],
        0,
    )
    dense_g = pack_dense(g_qkv, g_out, g_router, g_table, g_up_bias_all)
    width = dense_g.shape[1]
    dense_g = jnp.pad(dense_g, ((0, 0), (0, DENSE_AG - width))).astype(BF16)
    x_pair = lax.axis_size("rx") == 2
    r_up, r_down, r_dense = grad_reduce(g_up, g_down, dense_g, group_size, x_pair, 0)
    if not x_pair:
        r_up, r_down, r_dense = lax.psum((r_up, r_down, r_dense), "rx")
    r_qkv, r_out, r_router, r_table, r_ub = unpack_dense(r_dense[:, :width])

    reduced = (r_qkv, r_out, r_router, r_up, r_ub, r_down, r_table)
    rates = (
        2.0 * D ** (-0.5),
        2.0 * (D // 32) ** (-0.5),
        2.0 * (2 * D) ** (-0.5),
        2.0 * D ** (-0.5),
        0.2,
        2.0 * (F // 16) ** (-0.5),
        0.2,
    )
    params = (qkv_weight, out_weight, router_weight, up_weight, up_bias, down_weight, vectors)
    moments = (qkv_moments, out_moments, router_moments, up_moments, up_bias_moments, down_moments, vector_moments)
    news = []
    states = []
    for weight, state, grad, rate in zip(params, moments, reduced, rates):
        if weight.ndim == 3:
            new_weight, new_state = adamw_pass(weight, state, grad, rate)
        else:
            new_weight, new_state = adamw(weight, state, grad, rate)
        news.append(new_weight)
        states.append(new_state)
    return (result.astype(BF16), input_grad) + reduced + tuple(news) + tuple(states)


def solution(mesh):
    replica, group = mesh.shape["replica"], mesh.shape["group"]
    view = Mesh(np.asarray(mesh.devices).reshape(replica // 2, 2, group), ("rx", "core", "group"))
    in_specs = (
        P(TOK, None),
        P(TOK, None),
        P(TOK, None),
        P("group", None),
        P("group", None),
        P("group", None),
        P(None, "group", None),
        P(None, "group"),
        P(None, "group", None),
        P(None, "group"),
        P(None, "group", None),
        P(None, "group", None),
        P(None, "group", None),
        P(None, None, "group", None),
        P(None, None, "group"),
        P(None, None, "group", None),
        P(None, None, "group"),
    )
    out_specs = (
        P(TOK, None),
        P(TOK, None),
        P("group", None),
        P("group", None),
        P("group", None),
        P(None, "group", None),
        P(None, "group"),
        P(None, "group", None),
        P(None, "group"),
        P("group", None),
        P("group", None),
        P("group", None),
        P(None, "group", None),
        P(None, "group"),
        P(None, "group", None),
        P(None, "group"),
        P(None, "group", None),
        P(None, "group", None),
        P(None, "group", None),
        P(None, None, "group", None),
        P(None, None, "group"),
        P(None, None, "group", None),
        P(None, None, "group"),
    )
    return jax.shard_map(shards, mesh=view, in_specs=in_specs, out_specs=out_specs, check_vma=False)
```

```python
import functools

import jax
import jax.numpy as jnp
import numpy as np
from jax import lax
from jax.sharding import Mesh
from jax.sharding import PartitionSpec as P
from jax.experimental import pallas as pl
from jax.experimental.pallas import tpu as pltpu

D = 512
HEADS = 8
HEAD_DIM = 64
F = 2048
E = 4
S = 197
MB_TOK = 394
CAP = 392
NV = 11
DENSE_AG = 2560
DENSE_PAD = 2304
F32 = jnp.float32
BF16 = jnp.bfloat16
TOK = ("rx", "core", "group")


MESH_ID = pl.DeviceIdType.MESH


def ring_order(groups):
    if groups in (4, 8):
        zs = groups // 2

        def pos_of(g):
            y = g % 2
            z = g // 2
            return z + y * (2 * zs - 1 - 2 * z)

        def dev_at(p):
            p = p % groups
            yy = p // zs
            return 2 * (p + yy * (2 * zs - 1 - 2 * p)) + yy

        return pos_of, dev_at
    return (lambda g: g), (lambda p: p % groups)


def ring_rs_kernel(groups, n_in, *refs):
    ins = refs[:n_in]
    outs = refs[n_in : 2 * n_in]
    rbufs = refs[2 * n_in : 3 * n_in]
    sbufs = refs[3 * n_in : 4 * n_in]
    owns = refs[4 * n_in : 5 * n_in]
    send_sem, recv_sem, load_sem = refs[5 * n_in :]
    pos_of, dev_at = ring_order(groups)
    rx = lax.axis_index("rx")
    core = lax.axis_index("core")
    g = lax.axis_index("group")
    pos = pos_of(g)
    nbr = (dev_at(pos + 1), dev_at(pos + groups - 1))

    barrier = pltpu.get_barrier_semaphore()
    for n in nbr:
        pl.semaphore_signal(barrier, inc=1, device_id=(rx, core, n), device_id_type=MESH_ID)
    pl.semaphore_wait(barrier, 2)

    def block_dev(d, s):
        if d == 0:
            return dev_at(pos + 2 * groups - s - 1)
        return dev_at(pos + s + 1)

    def load(d, s, slot):
        b = block_dev(d, s)
        copies = []
        for i in range(n_in):
            rows = ins[i].shape[1] // groups
            half = ins[i].shape[2] // 2
            src = ins[i].at[:, pl.ds(pl.multiple_of(b * rows, rows), rows), pl.ds(d * half, half)]
            copies.append(pltpu.make_async_copy(src, owns[i].at[d, slot], load_sem.at[d, slot, i]))
        return copies

    def remote(d, s, i):
        return pltpu.make_async_remote_copy(
            src_ref=sbufs[i].at[d, s],
            dst_ref=rbufs[i].at[d, s],
            send_sem=send_sem.at[d, s, i],
            recv_sem=recv_sem.at[d, s, i],
            device_id=(rx, core, nbr[d]),
            device_id_type=MESH_ID,
        )

    for d in range(2):
        for c in load(d, 0, 0):
            c.start()
    sends = []
    for s in range(groups):
        slot = s % 2
        for d in range(2):
            for c in load(d, s, slot):
                c.wait()
            if s + 1 < groups:
                for c in load(d, s + 1, 1 - slot):
                    c.start()
            for i in range(n_in):
                if s > 0:
                    remote(d, s - 1, i).wait_recv()
                for a in range(ins[i].shape[0]):
                    mine = owns[i][d, slot, a].astype(F32)
                    if s > 0:
                        mine = mine + rbufs[i][d, s - 1, a].astype(F32)
                    if s < groups - 1:
                        sbufs[i][d, s, a] = mine.astype(sbufs[i].dtype)
                    else:
                        half = ins[i].shape[2] // 2
                        outs[i][a, :, pl.ds(d * half, half)] = mine.astype(outs[i].dtype)
                if s < groups - 1:
                    c = remote(d, s, i)
                    c.start()
                    sends.append(c)
    for c in sends:
        c.wait_send()


def ring_reduce_scatter(xs, groups, collective_id):
    n_in = len(xs)
    outs, rb, own = [], [], []
    flops = 0
    nbytes = 0
    for x in xs:
        a, total, c = x.shape
        rows = total // groups
        outs.append(jax.ShapeDtypeStruct((a, rows, c), x.dtype))
        rb.append(pltpu.VMEM((2, groups - 1, a, rows, c // 2), x.dtype))
        own.append(pltpu.VMEM((2, 2, a, rows, c // 2), x.dtype))
        flops += a * total * c
        nbytes += 3 * x.size * x.dtype.itemsize
    scratch = rb + rb + own + [
        pltpu.SemaphoreType.DMA((2, groups - 1, n_in)),
        pltpu.SemaphoreType.DMA((2, groups - 1, n_in)),
        pltpu.SemaphoreType.DMA((2, 2, n_in)),
    ]
    return pl.pallas_call(
        functools.partial(ring_rs_kernel, groups, n_in),
        out_shape=outs,
        in_specs=[pl.BlockSpec(memory_space=pl.ANY)] * n_in,
        out_specs=[pl.BlockSpec(memory_space=pltpu.VMEM)] * n_in,
        scratch_shapes=scratch,
        compiler_params=pltpu.CompilerParams(
            collective_id=collective_id, has_side_effects=True, vmem_limit_bytes=60 * 1024 * 1024
        ),
        cost_estimate=pl.CostEstimate(flops=flops, bytes_accessed=nbytes, transcendentals=0),
    )(*xs)


def ring_ag_kernel(groups, *refs):
    in_up, in_down, in_dense, out_up, out_down, out_dense = refs[:6]
    ring_send, ring_recv, part_send, part_recv, local_sem = refs[6:]
    pos_of, dev_at = ring_order(groups)
    rx = lax.axis_index("rx")
    core = lax.axis_index("core")
    g = lax.axis_index("group")
    other = 1 - core
    pos = pos_of(g)
    nbr = (dev_at(pos + 1), dev_at(pos + groups - 1))
    gs = in_up.shape[1]
    fs = in_down.shape[1]
    width = in_dense.shape[1] // 2

    barrier = pltpu.get_barrier_semaphore()
    for n in nbr:
        pl.semaphore_signal(barrier, inc=1, device_id=(rx, core, n), device_id_type=MESH_ID)
    pl.semaphore_signal(barrier, inc=1, device_id=(rx, other, g), device_id_type=MESH_ID)
    pl.semaphore_wait(barrier, 3)

    def items(owner):
        found = []
        for k in range(2):
            e = 2 * k + owner
            found.append((in_up.at[e], lambda b, e=e: out_up.at[e, pl.ds(pl.multiple_of(b * gs, gs), gs)], F // 2))
            found.append((in_down.at[e], lambda b, e=e: out_down.at[e, pl.ds(pl.multiple_of(b * fs, fs), fs)], D // 2))
        dense_in = in_dense.at[:, pl.ds(owner * width, width)]
        found.append(
            (dense_in, lambda b: out_dense.at[pl.ds(pl.multiple_of(b * gs, gs), gs), pl.ds(owner * width, width)], width // 2)
        )
        return found

    mine = items(core)
    theirs = items(other)
    n_items = len(mine)

    locals_ = [pltpu.make_async_copy(in_up.at[e], out_up.at[e, pl.ds(pl.multiple_of(g * gs, gs), gs)], local_sem.at[e]) for e in range(E)]
    locals_ += [
        pltpu.make_async_copy(in_down.at[e], out_down.at[e, pl.ds(pl.multiple_of(g * fs, fs), fs)], local_sem.at[E + e])
        for e in range(E)
    ]
    locals_.append(pltpu.make_async_copy(in_dense, out_dense.at[pl.ds(pl.multiple_of(g * gs, gs), gs)], local_sem.at[2 * E]))
    for c in locals_:
        c.start()

    def block_at(d, s):
        if d == 0:
            return dev_at(pos + 2 * groups - 1 - s)
        return dev_at(pos + 1 + s)

    def ring_copy(d, s, j, src_block):
        src_in, dst_of, half = mine[j]
        cols = pl.ds(d * half, half)
        if src_block is None:
            src = src_in.at[:, cols]
            dst = dst_of(g).at[:, cols]
        else:
            src = dst_of(src_block).at[:, cols]
            dst = src
        return pltpu.make_async_remote_copy(
            src_ref=src, dst_ref=dst, send_sem=ring_send.at[d, s, j], recv_sem=ring_recv.at[d, s, j],
            device_id=(rx, core, nbr[d]), device_id_type=MESH_ID,
        )

    def part_copy(d, s, j, table, block):
        _, dst_of, half = table[j]
        view = dst_of(block).at[:, pl.ds(d * half, half)]
        return pltpu.make_async_remote_copy(
            src_ref=view, dst_ref=view, send_sem=part_send.at[d, s, j], recv_sem=part_recv.at[d, s, j],
            device_id=(rx, other, g), device_id_type=MESH_ID,
        )

    sends = []
    for d in range(2):
        for j in range(n_items):
            c = ring_copy(d, 0, j, None)
            c.start()
            sends.append(c)
    for s in range(groups - 1):
        for d in range(2):
            b = block_at(d, s)
            for j in range(n_items):
                pltpu.make_async_remote_copy(
                    src_ref=mine[j][1](b).at[:, pl.ds(d * mine[j][2], mine[j][2])],
                    dst_ref=mine[j][1](b).at[:, pl.ds(d * mine[j][2], mine[j][2])],
                    send_sem=ring_send.at[d, s, j], recv_sem=ring_recv.at[d, s, j],
                    device_id=(rx, core, nbr[d]), device_id_type=MESH_ID,
                ).wait_recv()
                if s + 1 < groups - 1:
                    c = ring_copy(d, s + 1, j, b)
                    c.start()
                    sends.append(c)
                c = part_copy(d, s, j, mine, b)
                c.start()
                sends.append(c)
    for s in range(groups - 1):
        for d in range(2):
            b = block_at(d, s)
            for j in range(n_items):
                part_copy(d, s, j, theirs, b).wait_recv()
    for c in sends:
        c.wait_send()
    for c in locals_:
        c.wait()


def ring_all_gather(up_b, down_b, dense_b, groups, collective_id):
    n_items = 5
    gs = up_b.shape[1]
    shapes = [
        jax.ShapeDtypeStruct((E, gs * groups, F), BF16),
        jax.ShapeDtypeStruct((E, down_b.shape[1] * groups, D), BF16),
        jax.ShapeDtypeStruct((gs * groups, dense_b.shape[1]), BF16),
    ]
    nbytes = sum(int(np.prod(s.shape)) * 2 for s in shapes)
    return pl.pallas_call(
        functools.partial(ring_ag_kernel, groups),
        out_shape=shapes,
        in_specs=[pl.BlockSpec(memory_space=pl.ANY)] * 3,
        out_specs=[pl.BlockSpec(memory_space=pl.ANY)] * 3,
        scratch_shapes=[
            pltpu.SemaphoreType.DMA((2, groups - 1, n_items)),
            pltpu.SemaphoreType.DMA((2, groups - 1, n_items)),
            pltpu.SemaphoreType.DMA((2, groups - 1, n_items)),
            pltpu.SemaphoreType.DMA((2, groups - 1, n_items)),
            pltpu.SemaphoreType.DMA((2 * E + 1,)),
        ],
        compiler_params=pltpu.CompilerParams(collective_id=collective_id, has_side_effects=True),
        cost_estimate=pl.CostEstimate(flops=0, bytes_accessed=nbytes, transcendentals=0),
    )(up_b, down_b, dense_b)


def grad_items(gu, gd, gdense, owner, gs, fs, width):
    found = []
    for k in range(2):
        e = 2 * k + owner
        found.append((lambda b, e=e: gu.at[e, pl.ds(pl.multiple_of(b * gs, gs), gs)], F // 2))
        found.append((lambda b, e=e: gd.at[e, pl.ds(pl.multiple_of(b * fs, fs), fs)], D // 2))
    found.append((lambda b: gdense.at[pl.ds(pl.multiple_of(b * gs, gs), gs), pl.ds(owner * width, width)], width // 2))
    return found


def ring_rs2_kernel(groups, x_pair, *refs):
    gu, gd, gdense, out_up, out_down, out_dense = refs[:6]
    n_items = 5
    scr = refs[6:]
    rbuf, sbuf, pbuf, own, fin, xr, cr, xs = (scr[i * n_items : (i + 1) * n_items] for i in range(8))
    ring_send, ring_recv, part_send, part_recv, load_sem, x_send, x_recv, c_send, c_recv = scr[8 * n_items :]
    pos_of, dev_at = ring_order(groups)
    rx = lax.axis_index("rx")
    core = lax.axis_index("core")
    g = lax.axis_index("group")
    other = 1 - core
    pos = pos_of(g)
    nbr = (dev_at(pos + 1), dev_at(pos + groups - 1))
    gs = gu.shape[1] // groups
    fs = gd.shape[1] // groups
    width = gdense.shape[1] // 2
    mine = grad_items(gu, gd, gdense, core, gs, fs, width)
    theirs = grad_items(gu, gd, gdense, other, gs, fs, width)

    barrier = pltpu.get_barrier_semaphore()
    for n in nbr:
        pl.semaphore_signal(barrier, inc=1, device_id=(rx, core, n), device_id_type=MESH_ID)
    pl.semaphore_signal(barrier, inc=1, device_id=(rx, other, g), device_id_type=MESH_ID)
    count = 3
    if x_pair:
        pl.semaphore_signal(barrier, inc=1, device_id=(1 - rx, core, g), device_id_type=MESH_ID)
        count = 4
    pl.semaphore_wait(barrier, count)

    def block_at(d, s):
        if d == 0:
            return dev_at(pos + 2 * groups - 1 - s)
        return dev_at(pos + 1 + s)

    def cols(j, d):
        half = mine[j][1]
        return pl.ds(d * half, half)

    def load(d, s, slot, j):
        return pltpu.make_async_copy(mine[j][0](block_at(d, s)).at[:, cols(j, d)], own[j].at[d, slot], load_sem.at[d, slot, j])

    def part(d, s, j):
        return pltpu.make_async_remote_copy(
            src_ref=theirs[j][0](block_at(d, s)).at[:, cols(j, d)], dst_ref=pbuf[j].at[d, s],
            send_sem=part_send.at[d, s, j], recv_sem=part_recv.at[d, s, j],
            device_id=(rx, other, g), device_id_type=MESH_ID,
        )

    def ring(d, s, j):
        return pltpu.make_async_remote_copy(
            src_ref=sbuf[j].at[d, s], dst_ref=rbuf[j].at[d, s],
            send_sem=ring_send.at[d, s, j], recv_sem=ring_recv.at[d, s, j],
            device_id=(rx, core, nbr[d]), device_id_type=MESH_ID,
        )

    sends = []

    def ring_wave(items):
        for d in range(2):
            for j in items:
                load(d, 0, 0, j).start()
                c = part(d, 0, j)
                c.start()
                sends.append(c)
        for s in range(groups):
            slot = s % 2
            for d in range(2):
                for j in items:
                    load(d, s, slot, j).wait()
                    if s + 1 < groups:
                        load(d, s + 1, 1 - slot, j).start()
                        c = part(d, s + 1, j)
                        c.start()
                        sends.append(c)
                    part(d, s, j).wait_recv()
                    val = own[j][d, slot].astype(F32) + pbuf[j][d, s].astype(F32)
                    if s > 0:
                        ring(d, s - 1, j).wait_recv()
                        val = val + rbuf[j][d, s - 1].astype(F32)
                    if s < groups - 1:
                        sbuf[j][d, s] = val.astype(BF16)
                        c = ring(d, s, j)
                        c.start()
                        sends.append(c)
                    else:
                        fin[j][d] = val

    def x_start(items):
        copies = []
        for d in range(2):
            for j in items:
                xs[j][d] = fin[j][d].astype(BF16)
                c = pltpu.make_async_remote_copy(
                    src_ref=xs[j].at[d], dst_ref=xr[j].at[d], send_sem=x_send.at[d, j], recv_sem=x_recv.at[d, j],
                    device_id=(1 - rx, core, g), device_id_type=MESH_ID,
                )
                c.start()
                copies.append(c)
        sends.extend(copies)
        return copies

    def x_finish(items, copies):
        for c in copies:
            c.wait_recv()
        for d in range(2):
            for j in items:
                fin[j][d] = xs[j][d].astype(F32) + xr[j][d].astype(F32)

    def c_start(items):
        copies = []
        for d in range(2):
            for j in items:
                c = pltpu.make_async_remote_copy(
                    src_ref=fin[j].at[d], dst_ref=cr[j].at[d], send_sem=c_send.at[d, j], recv_sem=c_recv.at[d, j],
                    device_id=(rx, other, g), device_id_type=MESH_ID,
                )
                c.start()
                copies.append(c)
        return copies

    wave_a, wave_b = (0, 1, 2, 3), (4,)
    ring_wave(wave_a)
    if x_pair:
        xa = x_start(wave_a)
    ring_wave(wave_b)
    if x_pair:
        x_finish(wave_a, xa)
    c_copies = c_start(wave_a)
    if x_pair:
        x_finish(wave_b, x_start(wave_b))
    c_copies += c_start(wave_b)

    def out_items(owner):
        found = []
        for k in range(2):
            e = 2 * k + owner
            found.append(lambda d, e=e: out_up.at[e, :, pl.ds(d * (F // 2), F // 2)])
            found.append(lambda d, e=e: out_down.at[e, :, pl.ds(d * (D // 2), D // 2)])
        found.append(lambda d: out_dense.at[:, pl.ds(owner * width + d * (width // 2), width // 2)])
        return found

    mine_out = out_items(core)
    theirs_out = out_items(other)
    for d in range(2):
        for j in range(n_items):
            mine_out[j](d)[...] = fin[j][d]
    for c in c_copies:
        c.wait_recv()
    for d in range(2):
        for j in range(n_items):
            theirs_out[j](d)[...] = cr[j][d]
    for c in sends + c_copies:
        c.wait_send()


def grad_reduce(gu, gd, gdense, groups, x_pair, collective_id):
    gs = gu.shape[1] // groups
    fs = gd.shape[1] // groups
    width = gdense.shape[1] // 2
    item_shapes = [(gs, F // 2), (fs, D // 2), (gs, F // 2), (fs, D // 2), (gs, width // 2)]
    scratch = []
    for lead, dtype in (((2, groups - 1), BF16), ((2, groups - 1), BF16), ((2, groups), BF16), ((2, 2), BF16), ((2,), F32), ((2,), BF16), ((2,), F32), ((2,), BF16)):
        scratch += [pltpu.VMEM(lead + shp, dtype) for shp in item_shapes]
    scratch += [
        pltpu.SemaphoreType.DMA((2, groups - 1, 5)),
        pltpu.SemaphoreType.DMA((2, groups - 1, 5)),
        pltpu.SemaphoreType.DMA((2, groups, 5)),
        pltpu.SemaphoreType.DMA((2, groups, 5)),
        pltpu.SemaphoreType.DMA((2, 2, 5)),
        pltpu.SemaphoreType.DMA((2, 5)),
        pltpu.SemaphoreType.DMA((2, 5)),
        pltpu.SemaphoreType.DMA((2, 5)),
        pltpu.SemaphoreType.DMA((2, 5)),
    ]
    outs = [
        jax.ShapeDtypeStruct((E, gs, F), F32),
        jax.ShapeDtypeStruct((E, fs, D), F32),
        jax.ShapeDtypeStruct((gs, gdense.shape[1]), F32),
    ]
    nbytes = 2 * (gu.size + gd.size + gdense.size)
    return pl.pallas_call(
        functools.partial(ring_rs2_kernel, groups, x_pair),
        out_shape=outs,
        in_specs=[pl.BlockSpec(memory_space=pl.ANY)] * 3,
        out_specs=[pl.BlockSpec(memory_space=pltpu.VMEM)] * 3,
        scratch_shapes=scratch,
        compiler_params=pltpu.CompilerParams(
            collective_id=collective_id, has_side_effects=True, vmem_limit_bytes=62 * 1024 * 1024
        ),
        cost_estimate=pl.CostEstimate(flops=gu.size + gd.size + gdense.size, bytes_accessed=nbytes, transcendentals=0),
    )(gu, gd, gdense)


TILE = 256
TILE_B = 256
CAPP = 512
SQRT_HALF = float(np.sqrt(0.5))
INV_SQRT_2PI = float(1.0 / np.sqrt(2.0 * np.pi))


def ffn_fwd_kernel(micro, counts, x_ref, w1_ref, b1_ref, w2_ref, b2_ref, hp_ref, h_ref, y_ref):
    e, m, t = pl.program_id(0), pl.program_id(1), pl.program_id(2)
    active = t * TILE < counts[e * micro + m]

    @pl.when(active)
    def _():
        hp = jnp.dot(x_ref[0], w1_ref[0], preferred_element_type=F32) + b1_ref[0]
        cdf = 0.5 * (1.0 + lax.erf(hp * SQRT_HALF))
        h = (hp * cdf).astype(BF16)
        hp_ref[0] = cdf + hp * jnp.exp(-0.5 * hp * hp) * INV_SQRT_2PI
        h_ref[0] = h
        y = jnp.dot(h, w2_ref[0], preferred_element_type=F32) + b2_ref[0]
        hi = y.astype(BF16)
        y_ref[0, :, :D] = hi
        y_ref[0, :, D:] = (y - hi.astype(F32)).astype(BF16)

    @pl.when(jnp.logical_not(active))
    def _():
        y_ref[0] = jnp.zeros(y_ref.shape[1:], BF16)


def ffn_forward(counts, table_in, w1, b1, w2, b2, micro):
    tiles = CAPP // TILE
    rows = table_in.shape[1]
    row_map = lambda e, m, t, c: (m, e * tiles + t, 0)
    w_map = lambda e, m, t, c: (e, 0, 0)
    grid_spec = pltpu.PrefetchScalarGridSpec(
        num_scalar_prefetch=1,
        grid=(E, micro, tiles),
        in_specs=[
            pl.BlockSpec((1, TILE, D), row_map),
            pl.BlockSpec((1, D, F), w_map),
            pl.BlockSpec((1, 1, F), w_map),
            pl.BlockSpec((1, F, D), w_map),
            pl.BlockSpec((1, 1, D), w_map),
        ],
        out_specs=[
            pl.BlockSpec((1, TILE, F), row_map),
            pl.BlockSpec((1, TILE, F), row_map),
            pl.BlockSpec((1, TILE, 2 * D), row_map),
        ],
    )
    work = micro * rows
    return pl.pallas_call(
        functools.partial(ffn_fwd_kernel, micro),
        grid_spec=grid_spec,
        out_shape=[
            jax.ShapeDtypeStruct((micro, rows, F), F32),
            jax.ShapeDtypeStruct((micro, rows, F), BF16),
            jax.ShapeDtypeStruct((micro, rows, 2 * D), BF16),
        ],
        compiler_params=pltpu.CompilerParams(vmem_limit_bytes=48 * 1024 * 1024),
        cost_estimate=pl.CostEstimate(
            flops=4 * work * D * F // 2, bytes_accessed=work * (2 * D + 6 * F + 4 * D) // 2, transcendentals=work * F // 2
        ),
    )(counts, table_in, w1, b1, w2, b2)


def ffn_bwd_kernel(micro, counts, dy_ref, x_ref, hp_ref, h_ref, w1_ref, w2_ref, dt_ref, gu_ref, gd_ref, gb_ref, gb2_ref, gu_acc, gd_acc):
    e, m, t = pl.program_id(0), pl.program_id(1), pl.program_id(2)
    active = t * TILE_B < counts[e * micro + m]

    @pl.when((m == 0) & (t == 0))
    def _():
        gu_acc[...] = jnp.zeros(gu_acc.shape, F32)
        gd_acc[...] = jnp.zeros(gd_acc.shape, F32)
        gb_ref[...] = jnp.zeros(gb_ref.shape, F32)
        gb2_ref[...] = jnp.zeros(gb2_ref.shape, F32)

    @pl.when(active)
    def _():
        dy = dy_ref[0]
        d_hidden = lax.dot_general(dy, w2_ref[0], (((1,), (1,)), ((), ())), preferred_element_type=F32)
        d_pre = (d_hidden * hp_ref[0]).astype(BF16)
        dt = lax.dot_general(d_pre, w1_ref[0], (((1,), (1,)), ((), ())), preferred_element_type=F32)
        hi = dt.astype(BF16)
        dt_ref[0, :, :D] = hi
        dt_ref[0, :, D:] = (dt - hi.astype(F32)).astype(BF16)
        gb2_ref[0] += jnp.sum(dy.astype(F32), 0, keepdims=True)
        gu_acc[...] += lax.dot_general(x_ref[0], d_pre, (((0,), (0,)), ((), ())), preferred_element_type=F32)
        gd_acc[...] += lax.dot_general(h_ref[0], dy, (((0,), (0,)), ((), ())), preferred_element_type=F32)
        gb_ref[0] += jnp.sum(d_pre.astype(F32), 0, keepdims=True)

    @pl.when(jnp.logical_not(active))
    def _():
        dt_ref[0] = jnp.zeros(dt_ref.shape[1:], BF16)

    @pl.when((m == micro - 1) & (t == pl.num_programs(2) - 1))
    def _():
        gu_ref[0] = gu_acc[...].astype(BF16)
        gd_ref[0] = gd_acc[...].astype(BF16)


def ffn_backward(counts, d_expert, table_in, hp, h, w1, w2, micro):
    tiles = CAPP // TILE_B
    rows = table_in.shape[1]
    row_map = lambda e, m, t, c: (m, e * tiles + t, 0)
    w_map = lambda e, m, t, c: (e, 0, 0)
    grid_spec = pltpu.PrefetchScalarGridSpec(
        num_scalar_prefetch=1,
        grid=(E, micro, tiles),
        in_specs=[
            pl.BlockSpec((1, TILE_B, D), row_map),
            pl.BlockSpec((1, TILE_B, D), row_map),
            pl.BlockSpec((1, TILE_B, F), row_map),
            pl.BlockSpec((1, TILE_B, F), row_map),
            pl.BlockSpec((1, D, F), w_map),
            pl.BlockSpec((1, F, D), w_map),
        ],
        out_specs=[
            pl.BlockSpec((1, TILE_B, 2 * D), row_map),
            pl.BlockSpec((1, D, F), w_map),
            pl.BlockSpec((1, F, D), w_map),
            pl.BlockSpec((1, 1, F), w_map),
            pl.BlockSpec((1, 1, D), w_map),
        ],
        scratch_shapes=[pltpu.VMEM((D, F), F32), pltpu.VMEM((F, D), F32)],
    )
    work = micro * rows
    return pl.pallas_call(
        functools.partial(ffn_bwd_kernel, micro),
        grid_spec=grid_spec,
        out_shape=[
            jax.ShapeDtypeStruct((micro, rows, 2 * D), BF16),
            jax.ShapeDtypeStruct((E, D, F), BF16),
            jax.ShapeDtypeStruct((E, F, D), BF16),
            jax.ShapeDtypeStruct((E, 1, F), F32),
            jax.ShapeDtypeStruct((E, 1, D), F32),
        ],
        compiler_params=pltpu.CompilerParams(vmem_limit_bytes=60 * 1024 * 1024),
        cost_estimate=pl.CostEstimate(
            flops=8 * work * D * F // 2, bytes_accessed=work * (8 * D + 6 * F) // 2 + 16 * E * D * F, transcendentals=2 * work * F // 2
        ),
    )(counts, d_expert, table_in, hp, h, w1, w2)

def adamw_kernel(rate, w_ref, m_ref, g_ref, wo_ref, mo_ref):
    g = g_ref[...]
    first = 0.5 * m_ref[0] + 0.5 * g
    root = jnp.sqrt(0.5 * m_ref[1] * m_ref[1] + 0.5 * g * g)
    w = w_ref[...]
    wo_ref[...] = w - rate * (first / (root + 1e-08) + 0.1 * w)
    mo_ref[0] = first
    mo_ref[1] = root


def adamw_pass(weight, moments, grad, rate):
    n, r, c = weight.shape
    spec = pl.BlockSpec((1, r, c), lambda i: (i, 0, 0))
    mspec = pl.BlockSpec((2, 1, r, c), lambda i: (0, i, 0, 0))
    return pl.pallas_call(
        functools.partial(adamw_kernel, rate),
        grid=(n,),
        in_specs=[spec, mspec, spec],
        out_specs=[spec, mspec],
        out_shape=[jax.ShapeDtypeStruct(weight.shape, F32), jax.ShapeDtypeStruct(moments.shape, F32)],
        cost_estimate=pl.CostEstimate(flops=12 * weight.size, bytes_accessed=28 * weight.size, transcendentals=2 * weight.size),
    )(weight, moments, grad)


def layer_norm(value, gain, shift):
    center = value - jnp.mean(value, -1, keepdims=True)
    spread = jnp.mean(center * center, -1, keepdims=True)
    return center * lax.rsqrt(spread + 1e-06) * gain + shift


def gelu_exact(value):
    return jax.nn.gelu(value, approximate=False)


def split_heads(part):
    return part.reshape(-1, S, HEADS, HEAD_DIM)


def dot(a, b):
    return jnp.dot(a, b, preferred_element_type=F32)


def assign_places(route):
    chosen = jnp.concatenate([route[:, :, 0], route[:, :, 1]], 1)
    hits = (chosen[:, :, None] == jnp.arange(E, dtype=jnp.int32)).astype(jnp.int32)
    before = jnp.cumsum(hits, 1) - hits
    slot = jnp.sum(before * hits, 2)
    return chosen * CAPP + slot, jnp.sum(hits, 1)


def hi_lo(v):
    hi = v.astype(BF16)
    lo = (v - hi.astype(F32)).astype(BF16)
    return jnp.concatenate([hi, lo], -1)


def pick_rows(onehot, split):
    both = jnp.einsum("mnr,mrd->mnd", onehot, split, preferred_element_type=F32)
    return both[..., :D] + both[..., D:]


def pack_dense(qkv_w, out_w, router_w, vectors, up_bias):
    rows = qkv_w.shape[0]
    ub = up_bias.reshape(E, rows, 4).transpose(1, 0, 2).reshape(rows, E * 4)
    return jnp.concatenate([qkv_w, out_w, router_w, vectors.T, ub], 1)


def unpack_dense(packed):
    rows = packed.shape[0]
    w_qkv = packed[:, : 3 * D]
    w_out = packed[:, 3 * D : 4 * D]
    w_router = packed[:, 4 * D : 4 * D + E]
    table = packed[:, 4 * D + E : 4 * D + E + NV].T
    ub = packed[:, 4 * D + E + NV :].reshape(rows, E, 4).transpose(1, 0, 2).reshape(E, rows * 4)
    return w_qkv, w_out, w_router, table, ub


def attention_fwd(w_qkv, w_out, table, value):
    rows = value.shape[0]
    nb = rows // S
    scale = HEAD_DIM ** (-0.5)
    first = layer_norm(value, table[0], table[1]).astype(BF16)
    qkv_bias = jnp.concatenate([table[2], jnp.zeros((D,), F32), table[3]]).reshape(3, 1, HEADS, 1, HEAD_DIM)
    w3 = w_qkv.reshape(D, 3, HEADS, HEAD_DIM)
    qkv = (jnp.einsum("bsk,kthd->tbhsd", first.reshape(nb, S, D), w3, preferred_element_type=F32) + qkv_bias).astype(BF16)
    query, key_part, val_part = qkv[0], qkv[1], qkv[2]
    scores = jnp.einsum("bhqd,bhkd->bhqk", query, key_part, preferred_element_type=F32) * scale
    peak = jnp.max(scores, -1, keepdims=True)
    expo = jnp.exp(scores - peak)
    total = jnp.sum(expo, -1, keepdims=True)
    probs_att = (expo / total).astype(BF16)
    log_total = peak + jnp.log(total)
    attended = jnp.einsum("bhqk,bhkd->bqhd", probs_att, val_part, preferred_element_type=F32)
    attended = attended.reshape(rows, D).astype(BF16)
    resid = value + (dot(attended, w_out) + table[4])
    return first, qkv, log_total, attended, resid


def attention_bwd(w_qkv, w_out, table, value, first, qkv, log_total, attended, d_resid):
    rows = value.shape[0]
    nb = rows // S
    scale = HEAD_DIM ** (-0.5)
    d_branch = d_resid.astype(BF16)
    g_bias_out = jnp.sum(d_branch.astype(F32), 0)
    g_out = lax.dot_general(attended, d_branch, (((0,), (0,)), ((), ())), preferred_element_type=F32)
    d_att = jnp.einsum(
        "bsn,hdn->bhsd", d_branch.reshape(nb, S, D), w_out.reshape(HEADS, HEAD_DIM, D), preferred_element_type=F32
    ).astype(BF16)
    query, key_part, val_part = qkv[0], qkv[1], qkv[2]
    scores = jnp.einsum("bhqd,bhkd->bhqk", query, key_part, preferred_element_type=F32) * scale
    probs_f = jnp.exp(scores - log_total)
    probs_att = probs_f.astype(BF16)
    d_val = jnp.einsum("bhqk,bhqd->bhkd", probs_att, d_att, preferred_element_type=F32)
    d_prob = jnp.einsum("bhqd,bhkd->bhqk", d_att, val_part, preferred_element_type=F32)
    d_score = (probs_f * (d_prob - jnp.sum(d_prob * probs_f, -1, keepdims=True))).astype(BF16)
    d_query = jnp.einsum("bhqk,bhkd->bhqd", d_score, key_part, preferred_element_type=F32) * scale
    d_key = jnp.einsum("bhqk,bhqd->bhkd", d_score, query, preferred_element_type=F32) * scale
    d_qkv = jnp.stack([d_query, d_key, d_val]).astype(BF16)
    d_qkv_f = d_qkv.astype(F32)
    g_bias_q = jnp.sum(d_qkv_f[0], (0, 2)).reshape(D)
    g_bias_v = jnp.sum(d_qkv_f[2], (0, 2)).reshape(D)
    first_b = first.reshape(nb, S, D)
    g_qkv = jnp.einsum("bsk,tbhsd->kthd", first_b, d_qkv, preferred_element_type=F32).reshape(D, 3 * D)
    w3 = w_qkv.reshape(D, 3, HEADS, HEAD_DIM)
    d_first = jnp.einsum("tbhsd,kthd->bsk", d_qkv, w3, preferred_element_type=F32).reshape(rows, D)
    first_pull = jax.vjp(layer_norm, value, table[0], table[1])[1]
    d_input, g_gain_one, g_shift_one = first_pull(d_first)
    return (g_qkv, g_out, g_bias_out, g_bias_q, g_bias_v, g_gain_one, g_shift_one), d_input


def adamw(weight, moments, grad, rate):
    first = 0.5 * moments[0] + 0.5 * grad
    root = jnp.sqrt(0.5 * moments[1] * moments[1] + 0.5 * grad * grad)
    update = first / (root + 1e-08)
    which = lax.broadcasted_iota(jnp.int32, moments.shape, 0) == 0
    both = jnp.where(which, 0.5 * moments + 0.5 * grad, jnp.sqrt(0.5 * moments * moments + 0.5 * grad * grad))
    return (weight - rate * (update + 0.1 * weight), both)


def shards(
    tokens,
    cotangent,
    expert_index,
    qkv_weight,
    out_weight,
    router_weight,
    up_weight,
    up_bias,
    down_weight,
    vectors,
    qkv_moments,
    out_moments,
    router_moments,
    up_moments,
    up_bias_moments,
    down_moments,
    vector_moments,
):
    rows = tokens.shape[0]
    micro = rows // MB_TOK
    gs = qkv_weight.shape[0]
    group_size = D // gs
    core = lax.axis_index("core")

    dense_in = pack_dense(qkv_weight, out_weight, router_weight, vectors, up_bias)
    width = dense_in.shape[1]
    dense_in = jnp.pad(dense_in, ((0, 0), (0, DENSE_AG - width))).astype(BF16)
    w_up_all, w_down_all, dense = ring_all_gather(
        up_weight.astype(BF16), down_weight.astype(BF16), dense_in, group_size, 1
    )
    w_qkv, w_out, w_router, table_b, b_up_b = unpack_dense(dense[:, :width])
    table = table_b.astype(F32)
    b_up = b_up_b.astype(F32)

    value = tokens.astype(F32)
    d_out = cotangent.astype(F32)
    first, qkv, log_total, attended, resid = attention_fwd(w_qkv, w_out, table, value)
    second = layer_norm(resid, table[5], table[6]).astype(BF16)
    logits = dot(second, w_router)
    probs = jax.nn.softmax(logits, -1)
    picked = expert_index[:, :, None] == jnp.arange(E, dtype=jnp.int32)
    gate = jnp.sum(jnp.where(picked, probs[:, None, :], 0.0), -1)

    route = expert_index.reshape(micro, MB_TOK, 2)
    places, counts = assign_places(route)
    counts = counts.T.reshape(E * micro)
    onehot = (places[:, :, None] == jnp.arange(E * CAPP, dtype=jnp.int32)).astype(BF16)
    second_m = second.reshape(micro, MB_TOK, D)
    pair = jnp.concatenate([second_m, second_m], 1)
    table_in = jnp.einsum("mnr,mnd->mrd", onehot, pair, preferred_element_type=F32).astype(BF16)

    hidden_pre, hidden, y_all = ffn_forward(
        counts, table_in, w_up_all, b_up[:, None, :], w_down_all, table[7 : 7 + E][:, None, :], micro
    )
    picked_rows = pick_rows(onehot, y_all)
    out_zero = picked_rows[:, :MB_TOK].reshape(rows, D)
    out_one = picked_rows[:, MB_TOK:].reshape(rows, D)
    result = resid + (gate[:, 0:1] * out_zero + gate[:, 1:2] * out_one)

    d_gate = jnp.stack([jnp.sum(d_out * out_zero, -1), jnp.sum(d_out * out_one, -1)], 1)
    d_out_m = d_out.reshape(micro, MB_TOK, D)
    gate_m = gate.reshape(micro, MB_TOK, 2)
    weighted = jnp.concatenate([gate_m[:, :, 0:1] * d_out_m, gate_m[:, :, 1:2] * d_out_m], 1).astype(BF16)
    d_expert = jnp.einsum("mnr,mnd->mrd", onehot, weighted, preferred_element_type=F32).astype(BF16)

    d_table, g_up, g_down, g_b1, g_b2 = ffn_backward(counts, d_expert, table_in, hidden_pre, hidden, w_up_all, w_down_all, micro)
    g_up_bias_all = g_b1[:, 0, :]
    g_bias_down = g_b2[:, 0, :]

    onehot_sum = onehot[:, :MB_TOK] + onehot[:, MB_TOK:]
    d_picked = pick_rows(onehot_sum, d_table).reshape(rows, D)

    d_probs = jnp.sum(jnp.where(picked, d_gate[:, :, None], 0.0), 1)
    d_logit = (probs * (d_probs - jnp.sum(d_probs * probs, -1, keepdims=True))).astype(BF16)
    g_router = lax.dot_general(second, d_logit, (((0,), (0,)), ((), ())), preferred_element_type=F32)
    d_second = d_picked + lax.dot_general(d_logit, w_router, (((1,), (1,)), ((), ())), preferred_element_type=F32)
    norm_pull = jax.vjp(layer_norm, resid, table[5], table[6])[1]
    d_resid, g_gain_two, g_shift_two = norm_pull(d_second)
    d_resid = d_out + d_resid

    att_grads, d_input = attention_bwd(w_qkv, w_out, table, value, first, qkv, log_total, attended, d_resid)
    g_qkv, g_out, g_bias_out, g_bias_q, g_bias_v, g_gain_one, g_shift_one = att_grads
    input_grad = d_resid + d_input

    g_table = jnp.concatenate(
        [
            jnp.stack([g_gain_one, g_shift_one, g_bias_q, g_bias_v, g_bias_out, g_gain_two, g_shift_two]),
            g_bias_down,
        ],
        0,
    )
    dense_g = pack_dense(g_qkv, g_out, g_router, g_table, g_up_bias_all)
    width = dense_g.shape[1]
    dense_g = jnp.pad(dense_g, ((0, 0), (0, DENSE_AG - width))).astype(BF16)
    x_pair = lax.axis_size("rx") == 2
    r_up, r_down, r_dense = grad_reduce(g_up, g_down, dense_g, group_size, x_pair, 0)
    if not x_pair:
        r_up, r_down, r_dense = lax.psum((r_up, r_down, r_dense), "rx")
    r_qkv, r_out, r_router, r_table, r_ub = unpack_dense(r_dense[:, :width])

    reduced = (r_qkv, r_out, r_router, r_up, r_ub, r_down, r_table)
    rates = (
        2.0 * D ** (-0.5),
        2.0 * (D // 32) ** (-0.5),
        2.0 * (2 * D) ** (-0.5),
        2.0 * D ** (-0.5),
        0.2,
        2.0 * (F // 16) ** (-0.5),
        0.2,
    )
    params = (qkv_weight, out_weight, router_weight, up_weight, up_bias, down_weight, vectors)
    moments = (qkv_moments, out_moments, router_moments, up_moments, up_bias_moments, down_moments, vector_moments)
    news = []
    states = []
    for weight, state, grad, rate in zip(params, moments, reduced, rates):
        if weight.ndim == 3:
            new_weight, new_state = adamw_pass(weight, state, grad, rate)
        else:
            new_weight, new_state = adamw(weight, state, grad, rate)
        news.append(new_weight)
        states.append(new_state)
    return (result.astype(BF16), input_grad) + reduced + tuple(news) + tuple(states)


def solution(mesh):
    replica, group = mesh.shape["replica"], mesh.shape["group"]
    view = Mesh(np.asarray(mesh.devices).reshape(replica // 2, 2, group), ("rx", "core", "group"))
    in_specs = (
        P(TOK, None),
        P(TOK, None),
        P(TOK, None),
        P("group", None),
        P("group", None),
        P("group", None),
        P(None, "group", None),
        P(None, "group"),
        P(None, "group", None),
        P(None, "group"),
        P(None, "group", None),
        P(None, "group", None),
        P(None, "group", None),
        P(None, None, "group", None),
        P(None, None, "group"),
        P(None, None, "group", None),
        P(None, None, "group"),
    )
    out_specs = (
        P(TOK, None),
        P(TOK, None),
        P("group", None),
        P("group", None),
        P("group", None),
        P(None, "group", None),
        P(None, "group"),
        P(None, "group", None),
        P(None, "group"),
        P("group", None),
        P("group", None),
        P("group", None),
        P(None, "group", None),
        P(None, "group"),
        P(None, "group", None),
        P(None, "group"),
        P(None, "group", None),
        P(None, "group", None),
        P(None, "group", None),
        P(None, None, "group", None),
        P(None, None, "group"),
        P(None, None, "group", None),
        P(None, None, "group"),
    )
    return jax.shard_map(shards, mesh=view, in_specs=in_specs, out_specs=out_specs, check_vma=False)
```

```python
import functools

import jax
import jax.numpy as jnp
import numpy as np
from jax import lax
from jax.sharding import Mesh
from jax.sharding import PartitionSpec as P
from jax.experimental import pallas as pl
from jax.experimental.pallas import tpu as pltpu

D = 512
HEADS = 8
HEAD_DIM = 64
F = 2048
E = 4
S = 197
MB_TOK = 394
CAP = 392
NV = 11
DENSE_AG = 2560
DENSE_PAD = 2304
F32 = jnp.float32
BF16 = jnp.bfloat16
TOK = ("rx", "core", "group")


MESH_ID = pl.DeviceIdType.MESH


def ring_order(groups):
    if groups in (4, 8):
        zs = groups // 2

        def pos_of(g):
            y = g % 2
            z = g // 2
            return z + y * (2 * zs - 1 - 2 * z)

        def dev_at(p):
            p = p % groups
            yy = p // zs
            return 2 * (p + yy * (2 * zs - 1 - 2 * p)) + yy

        return pos_of, dev_at
    return (lambda g: g), (lambda p: p % groups)


def ring_rs_kernel(groups, n_in, *refs):
    ins = refs[:n_in]
    outs = refs[n_in : 2 * n_in]
    rbufs = refs[2 * n_in : 3 * n_in]
    sbufs = refs[3 * n_in : 4 * n_in]
    owns = refs[4 * n_in : 5 * n_in]
    send_sem, recv_sem, load_sem = refs[5 * n_in :]
    pos_of, dev_at = ring_order(groups)
    rx = lax.axis_index("rx")
    core = lax.axis_index("core")
    g = lax.axis_index("group")
    pos = pos_of(g)
    nbr = (dev_at(pos + 1), dev_at(pos + groups - 1))

    barrier = pltpu.get_barrier_semaphore()
    for n in nbr:
        pl.semaphore_signal(barrier, inc=1, device_id=(rx, core, n), device_id_type=MESH_ID)
    pl.semaphore_wait(barrier, 2)

    def block_dev(d, s):
        if d == 0:
            return dev_at(pos + 2 * groups - s - 1)
        return dev_at(pos + s + 1)

    def load(d, s, slot):
        b = block_dev(d, s)
        copies = []
        for i in range(n_in):
            rows = ins[i].shape[1] // groups
            half = ins[i].shape[2] // 2
            src = ins[i].at[:, pl.ds(pl.multiple_of(b * rows, rows), rows), pl.ds(d * half, half)]
            copies.append(pltpu.make_async_copy(src, owns[i].at[d, slot], load_sem.at[d, slot, i]))
        return copies

    def remote(d, s, i):
        return pltpu.make_async_remote_copy(
            src_ref=sbufs[i].at[d, s],
            dst_ref=rbufs[i].at[d, s],
            send_sem=send_sem.at[d, s, i],
            recv_sem=recv_sem.at[d, s, i],
            device_id=(rx, core, nbr[d]),
            device_id_type=MESH_ID,
        )

    for d in range(2):
        for c in load(d, 0, 0):
            c.start()
    sends = []
    for s in range(groups):
        slot = s % 2
        for d in range(2):
            for c in load(d, s, slot):
                c.wait()
            if s + 1 < groups:
                for c in load(d, s + 1, 1 - slot):
                    c.start()
            for i in range(n_in):
                if s > 0:
                    remote(d, s - 1, i).wait_recv()
                for a in range(ins[i].shape[0]):
                    mine = owns[i][d, slot, a].astype(F32)
                    if s > 0:
                        mine = mine + rbufs[i][d, s - 1, a].astype(F32)
                    if s < groups - 1:
                        sbufs[i][d, s, a] = mine.astype(sbufs[i].dtype)
                    else:
                        half = ins[i].shape[2] // 2
                        outs[i][a, :, pl.ds(d * half, half)] = mine.astype(outs[i].dtype)
                if s < groups - 1:
                    c = remote(d, s, i)
                    c.start()
                    sends.append(c)
    for c in sends:
        c.wait_send()


def ring_reduce_scatter(xs, groups, collective_id):
    n_in = len(xs)
    outs, rb, own = [], [], []
    flops = 0
    nbytes = 0
    for x in xs:
        a, total, c = x.shape
        rows = total // groups
        outs.append(jax.ShapeDtypeStruct((a, rows, c), x.dtype))
        rb.append(pltpu.VMEM((2, groups - 1, a, rows, c // 2), x.dtype))
        own.append(pltpu.VMEM((2, 2, a, rows, c // 2), x.dtype))
        flops += a * total * c
        nbytes += 3 * x.size * x.dtype.itemsize
    scratch = rb + rb + own + [
        pltpu.SemaphoreType.DMA((2, groups - 1, n_in)),
        pltpu.SemaphoreType.DMA((2, groups - 1, n_in)),
        pltpu.SemaphoreType.DMA((2, 2, n_in)),
    ]
    return pl.pallas_call(
        functools.partial(ring_rs_kernel, groups, n_in),
        out_shape=outs,
        in_specs=[pl.BlockSpec(memory_space=pl.ANY)] * n_in,
        out_specs=[pl.BlockSpec(memory_space=pltpu.VMEM)] * n_in,
        scratch_shapes=scratch,
        compiler_params=pltpu.CompilerParams(
            collective_id=collective_id, has_side_effects=True, vmem_limit_bytes=60 * 1024 * 1024
        ),
        cost_estimate=pl.CostEstimate(flops=flops, bytes_accessed=nbytes, transcendentals=0),
    )(*xs)


def ring_ag_kernel(groups, *refs):
    in_up, in_down, in_dense, out_up, out_down, out_dense = refs[:6]
    ring_send, ring_recv, part_send, part_recv, local_sem = refs[6:]
    pos_of, dev_at = ring_order(groups)
    rx = lax.axis_index("rx")
    core = lax.axis_index("core")
    g = lax.axis_index("group")
    other = 1 - core
    pos = pos_of(g)
    nbr = (dev_at(pos + 1), dev_at(pos + groups - 1))
    gs = in_up.shape[1]
    fs = in_down.shape[1]
    width = in_dense.shape[1] // 2

    barrier = pltpu.get_barrier_semaphore()
    for n in nbr:
        pl.semaphore_signal(barrier, inc=1, device_id=(rx, core, n), device_id_type=MESH_ID)
    pl.semaphore_signal(barrier, inc=1, device_id=(rx, other, g), device_id_type=MESH_ID)
    pl.semaphore_wait(barrier, 3)

    def items(owner):
        found = []
        for k in range(2):
            e = 2 * k + owner
            found.append((in_up.at[e], lambda b, e=e: out_up.at[e, pl.ds(pl.multiple_of(b * gs, gs), gs)], F // 2))
            found.append((in_down.at[e], lambda b, e=e: out_down.at[e, pl.ds(pl.multiple_of(b * fs, fs), fs)], D // 2))
        dense_in = in_dense.at[:, pl.ds(owner * width, width)]
        found.append(
            (dense_in, lambda b: out_dense.at[pl.ds(pl.multiple_of(b * gs, gs), gs), pl.ds(owner * width, width)], width // 2)
        )
        return found

    mine = items(core)
    theirs = items(other)
    n_items = len(mine)

    locals_ = [pltpu.make_async_copy(in_up.at[e], out_up.at[e, pl.ds(pl.multiple_of(g * gs, gs), gs)], local_sem.at[e]) for e in range(E)]
    locals_ += [
        pltpu.make_async_copy(in_down.at[e], out_down.at[e, pl.ds(pl.multiple_of(g * fs, fs), fs)], local_sem.at[E + e])
        for e in range(E)
    ]
    locals_.append(pltpu.make_async_copy(in_dense, out_dense.at[pl.ds(pl.multiple_of(g * gs, gs), gs)], local_sem.at[2 * E]))
    for c in locals_:
        c.start()

    def block_at(d, s):
        if d == 0:
            return dev_at(pos + 2 * groups - 1 - s)
        return dev_at(pos + 1 + s)

    def ring_copy(d, s, j, src_block):
        src_in, dst_of, half = mine[j]
        cols = pl.ds(d * half, half)
        if src_block is None:
            src = src_in.at[:, cols]
            dst = dst_of(g).at[:, cols]
        else:
            src = dst_of(src_block).at[:, cols]
            dst = src
        return pltpu.make_async_remote_copy(
            src_ref=src, dst_ref=dst, send_sem=ring_send.at[d, s, j], recv_sem=ring_recv.at[d, s, j],
            device_id=(rx, core, nbr[d]), device_id_type=MESH_ID,
        )

    def part_copy(d, s, j, table, block):
        _, dst_of, half = table[j]
        view = dst_of(block).at[:, pl.ds(d * half, half)]
        return pltpu.make_async_remote_copy(
            src_ref=view, dst_ref=view, send_sem=part_send.at[d, s, j], recv_sem=part_recv.at[d, s, j],
            device_id=(rx, other, g), device_id_type=MESH_ID,
        )

    sends = []
    for d in range(2):
        for j in range(n_items):
            c = ring_copy(d, 0, j, None)
            c.start()
            sends.append(c)
    for s in range(groups - 1):
        for d in range(2):
            b = block_at(d, s)
            for j in range(n_items):
                pltpu.make_async_remote_copy(
                    src_ref=mine[j][1](b).at[:, pl.ds(d * mine[j][2], mine[j][2])],
                    dst_ref=mine[j][1](b).at[:, pl.ds(d * mine[j][2], mine[j][2])],
                    send_sem=ring_send.at[d, s, j], recv_sem=ring_recv.at[d, s, j],
                    device_id=(rx, core, nbr[d]), device_id_type=MESH_ID,
                ).wait_recv()
                if s + 1 < groups - 1:
                    c = ring_copy(d, s + 1, j, b)
                    c.start()
                    sends.append(c)
                c = part_copy(d, s, j, mine, b)
                c.start()
                sends.append(c)
    for s in range(groups - 1):
        for d in range(2):
            b = block_at(d, s)
            for j in range(n_items):
                part_copy(d, s, j, theirs, b).wait_recv()
    for c in sends:
        c.wait_send()
    for c in locals_:
        c.wait()


def ring_all_gather(up_b, down_b, dense_b, groups, collective_id):
    n_items = 5
    gs = up_b.shape[1]
    shapes = [
        jax.ShapeDtypeStruct((E, gs * groups, F), BF16),
        jax.ShapeDtypeStruct((E, down_b.shape[1] * groups, D), BF16),
        jax.ShapeDtypeStruct((gs * groups, dense_b.shape[1]), BF16),
    ]
    nbytes = sum(int(np.prod(s.shape)) * 2 for s in shapes)
    return pl.pallas_call(
        functools.partial(ring_ag_kernel, groups),
        out_shape=shapes,
        in_specs=[pl.BlockSpec(memory_space=pl.ANY)] * 3,
        out_specs=[pl.BlockSpec(memory_space=pl.ANY)] * 3,
        scratch_shapes=[
            pltpu.SemaphoreType.DMA((2, groups - 1, n_items)),
            pltpu.SemaphoreType.DMA((2, groups - 1, n_items)),
            pltpu.SemaphoreType.DMA((2, groups - 1, n_items)),
            pltpu.SemaphoreType.DMA((2, groups - 1, n_items)),
            pltpu.SemaphoreType.DMA((2 * E + 1,)),
        ],
        compiler_params=pltpu.CompilerParams(collective_id=collective_id, has_side_effects=True),
        cost_estimate=pl.CostEstimate(flops=0, bytes_accessed=nbytes, transcendentals=0),
    )(up_b, down_b, dense_b)


def grad_items(gu, gd, gdense, owner, gs, fs, width):
    found = []
    for k in range(2):
        e = 2 * k + owner
        found.append((lambda b, e=e: gu.at[e, pl.ds(pl.multiple_of(b * gs, gs), gs)], F // 2))
        found.append((lambda b, e=e: gd.at[e, pl.ds(pl.multiple_of(b * fs, fs), fs)], D // 2))
    found.append((lambda b: gdense.at[pl.ds(pl.multiple_of(b * gs, gs), gs), pl.ds(owner * width, width)], width // 2))
    return found


def ring_rs2_kernel(groups, x_pair, *refs):
    gu, gd, gdense, out_up, out_down, out_dense = refs[:6]
    n_items = 5
    scr = refs[6:]
    rbuf, sbuf, pbuf, own, fin, xr, cr, xs = (scr[i * n_items : (i + 1) * n_items] for i in range(8))
    ring_send, ring_recv, part_send, part_recv, load_sem, x_send, x_recv, c_send, c_recv = scr[8 * n_items :]
    pos_of, dev_at = ring_order(groups)
    rx = lax.axis_index("rx")
    core = lax.axis_index("core")
    g = lax.axis_index("group")
    other = 1 - core
    pos = pos_of(g)
    nbr = (dev_at(pos + 1), dev_at(pos + groups - 1))
    gs = gu.shape[1] // groups
    fs = gd.shape[1] // groups
    width = gdense.shape[1] // 2
    mine = grad_items(gu, gd, gdense, core, gs, fs, width)
    theirs = grad_items(gu, gd, gdense, other, gs, fs, width)

    barrier = pltpu.get_barrier_semaphore()
    for n in nbr:
        pl.semaphore_signal(barrier, inc=1, device_id=(rx, core, n), device_id_type=MESH_ID)
    pl.semaphore_signal(barrier, inc=1, device_id=(rx, other, g), device_id_type=MESH_ID)
    count = 3
    if x_pair:
        pl.semaphore_signal(barrier, inc=1, device_id=(1 - rx, core, g), device_id_type=MESH_ID)
        count = 4
    pl.semaphore_wait(barrier, count)

    def block_at(d, s):
        if d == 0:
            return dev_at(pos + 2 * groups - 1 - s)
        return dev_at(pos + 1 + s)

    def cols(j, d):
        half = mine[j][1]
        return pl.ds(d * half, half)

    def load(d, s, slot, j):
        return pltpu.make_async_copy(mine[j][0](block_at(d, s)).at[:, cols(j, d)], own[j].at[d, slot], load_sem.at[d, slot, j])

    def part(d, s, j):
        return pltpu.make_async_remote_copy(
            src_ref=theirs[j][0](block_at(d, s)).at[:, cols(j, d)], dst_ref=pbuf[j].at[d, s],
            send_sem=part_send.at[d, s, j], recv_sem=part_recv.at[d, s, j],
            device_id=(rx, other, g), device_id_type=MESH_ID,
        )

    def ring(d, s, j):
        return pltpu.make_async_remote_copy(
            src_ref=sbuf[j].at[d, s], dst_ref=rbuf[j].at[d, s],
            send_sem=ring_send.at[d, s, j], recv_sem=ring_recv.at[d, s, j],
            device_id=(rx, core, nbr[d]), device_id_type=MESH_ID,
        )

    sends = []

    def ring_wave(items):
        for d in range(2):
            for j in items:
                load(d, 0, 0, j).start()
                c = part(d, 0, j)
                c.start()
                sends.append(c)
        for s in range(groups):
            slot = s % 2
            for d in range(2):
                for j in items:
                    load(d, s, slot, j).wait()
                    if s + 1 < groups:
                        load(d, s + 1, 1 - slot, j).start()
                        c = part(d, s + 1, j)
                        c.start()
                        sends.append(c)
                    part(d, s, j).wait_recv()
                    val = own[j][d, slot].astype(F32) + pbuf[j][d, s].astype(F32)
                    if s > 0:
                        ring(d, s - 1, j).wait_recv()
                        val = val + rbuf[j][d, s - 1].astype(F32)
                    if s < groups - 1:
                        sbuf[j][d, s] = val.astype(BF16)
                        c = ring(d, s, j)
                        c.start()
                        sends.append(c)
                    else:
                        fin[j][d] = val

    def x_start(items):
        copies = []
        for d in range(2):
            for j in items:
                xs[j][d] = fin[j][d].astype(BF16)
                c = pltpu.make_async_remote_copy(
                    src_ref=xs[j].at[d], dst_ref=xr[j].at[d], send_sem=x_send.at[d, j], recv_sem=x_recv.at[d, j],
                    device_id=(1 - rx, core, g), device_id_type=MESH_ID,
                )
                c.start()
                copies.append(c)
        sends.extend(copies)
        return copies

    def x_finish(items, copies):
        for c in copies:
            c.wait_recv()
        for d in range(2):
            for j in items:
                fin[j][d] = xs[j][d].astype(F32) + xr[j][d].astype(F32)

    def c_start(items):
        copies = []
        for d in range(2):
            for j in items:
                c = pltpu.make_async_remote_copy(
                    src_ref=fin[j].at[d], dst_ref=cr[j].at[d], send_sem=c_send.at[d, j], recv_sem=c_recv.at[d, j],
                    device_id=(rx, other, g), device_id_type=MESH_ID,
                )
                c.start()
                copies.append(c)
        return copies

    wave_a, wave_b = (0, 1, 2, 4), (3,)
    ring_wave(wave_a)
    if x_pair:
        xa = x_start(wave_a)
    ring_wave(wave_b)
    if x_pair:
        x_finish(wave_a, xa)
    c_copies = c_start(wave_a)
    if x_pair:
        x_finish(wave_b, x_start(wave_b))
    c_copies += c_start(wave_b)

    def out_items(owner):
        found = []
        for k in range(2):
            e = 2 * k + owner
            found.append(lambda d, e=e: out_up.at[e, :, pl.ds(d * (F // 2), F // 2)])
            found.append(lambda d, e=e: out_down.at[e, :, pl.ds(d * (D // 2), D // 2)])
        found.append(lambda d: out_dense.at[:, pl.ds(owner * width + d * (width // 2), width // 2)])
        return found

    mine_out = out_items(core)
    theirs_out = out_items(other)
    for d in range(2):
        for j in range(n_items):
            mine_out[j](d)[...] = fin[j][d]
    for c in c_copies:
        c.wait_recv()
    for d in range(2):
        for j in range(n_items):
            theirs_out[j](d)[...] = cr[j][d]
    for c in sends + c_copies:
        c.wait_send()


def grad_reduce(gu, gd, gdense, groups, x_pair, collective_id):
    gs = gu.shape[1] // groups
    fs = gd.shape[1] // groups
    width = gdense.shape[1] // 2
    item_shapes = [(gs, F // 2), (fs, D // 2), (gs, F // 2), (fs, D // 2), (gs, width // 2)]
    scratch = []
    for lead, dtype in (((2, groups - 1), BF16), ((2, groups - 1), BF16), ((2, groups), BF16), ((2, 2), BF16), ((2,), F32), ((2,), BF16), ((2,), F32), ((2,), BF16)):
        scratch += [pltpu.VMEM(lead + shp, dtype) for shp in item_shapes]
    scratch += [
        pltpu.SemaphoreType.DMA((2, groups - 1, 5)),
        pltpu.SemaphoreType.DMA((2, groups - 1, 5)),
        pltpu.SemaphoreType.DMA((2, groups, 5)),
        pltpu.SemaphoreType.DMA((2, groups, 5)),
        pltpu.SemaphoreType.DMA((2, 2, 5)),
        pltpu.SemaphoreType.DMA((2, 5)),
        pltpu.SemaphoreType.DMA((2, 5)),
        pltpu.SemaphoreType.DMA((2, 5)),
        pltpu.SemaphoreType.DMA((2, 5)),
    ]
    outs = [
        jax.ShapeDtypeStruct((E, gs, F), F32),
        jax.ShapeDtypeStruct((E, fs, D), F32),
        jax.ShapeDtypeStruct((gs, gdense.shape[1]), F32),
    ]
    nbytes = 2 * (gu.size + gd.size + gdense.size)
    return pl.pallas_call(
        functools.partial(ring_rs2_kernel, groups, x_pair),
        out_shape=outs,
        in_specs=[pl.BlockSpec(memory_space=pl.ANY)] * 3,
        out_specs=[pl.BlockSpec(memory_space=pltpu.VMEM)] * 3,
        scratch_shapes=scratch,
        compiler_params=pltpu.CompilerParams(
            collective_id=collective_id, has_side_effects=True, vmem_limit_bytes=62 * 1024 * 1024
        ),
        cost_estimate=pl.CostEstimate(flops=gu.size + gd.size + gdense.size, bytes_accessed=nbytes, transcendentals=0),
    )(gu, gd, gdense)


TILE = 256
TILE_B = 256
CAPP = 512
SQRT_HALF = float(np.sqrt(0.5))
INV_SQRT_2PI = float(1.0 / np.sqrt(2.0 * np.pi))


def ffn_fwd_kernel(micro, counts, x_ref, w1_ref, b1_ref, w2_ref, b2_ref, hp_ref, h_ref, y_ref):
    e, m, t = pl.program_id(0), pl.program_id(1), pl.program_id(2)
    active = t * TILE < counts[e * micro + m]

    @pl.when(active)
    def _():
        hp = jnp.dot(x_ref[0], w1_ref[0], preferred_element_type=F32) + b1_ref[0]
        cdf = 0.5 * (1.0 + lax.erf(hp * SQRT_HALF))
        h = (hp * cdf).astype(BF16)
        hp_ref[0] = cdf + hp * jnp.exp(-0.5 * hp * hp) * INV_SQRT_2PI
        h_ref[0] = h
        y = jnp.dot(h, w2_ref[0], preferred_element_type=F32) + b2_ref[0]
        hi = y.astype(BF16)
        y_ref[0, :, :D] = hi
        y_ref[0, :, D:] = (y - hi.astype(F32)).astype(BF16)

    @pl.when(jnp.logical_not(active))
    def _():
        y_ref[0] = jnp.zeros(y_ref.shape[1:], BF16)


def ffn_forward(counts, table_in, w1, b1, w2, b2, micro):
    tiles = CAPP // TILE
    rows = table_in.shape[1]
    row_map = lambda e, m, t, c: (m, e * tiles + t, 0)
    w_map = lambda e, m, t, c: (e, 0, 0)
    grid_spec = pltpu.PrefetchScalarGridSpec(
        num_scalar_prefetch=1,
        grid=(E, micro, tiles),
        in_specs=[
            pl.BlockSpec((1, TILE, D), row_map),
            pl.BlockSpec((1, D, F), w_map),
            pl.BlockSpec((1, 1, F), w_map),
            pl.BlockSpec((1, F, D), w_map),
            pl.BlockSpec((1, 1, D), w_map),
        ],
        out_specs=[
            pl.BlockSpec((1, TILE, F), row_map),
            pl.BlockSpec((1, TILE, F), row_map),
            pl.BlockSpec((1, TILE, 2 * D), row_map),
        ],
    )
    work = micro * rows
    return pl.pallas_call(
        functools.partial(ffn_fwd_kernel, micro),
        grid_spec=grid_spec,
        out_shape=[
            jax.ShapeDtypeStruct((micro, rows, F), F32),
            jax.ShapeDtypeStruct((micro, rows, F), BF16),
            jax.ShapeDtypeStruct((micro, rows, 2 * D), BF16),
        ],
        compiler_params=pltpu.CompilerParams(vmem_limit_bytes=48 * 1024 * 1024),
        cost_estimate=pl.CostEstimate(
            flops=4 * work * D * F // 2, bytes_accessed=work * (2 * D + 6 * F + 4 * D) // 2, transcendentals=work * F // 2
        ),
    )(counts, table_in, w1, b1, w2, b2)


def ffn_bwd_kernel(micro, counts, dy_ref, x_ref, hp_ref, h_ref, w1_ref, w2_ref, dt_ref, gu_ref, gd_ref, gb_ref, gb2_ref, gu_acc, gd_acc):
    e, m, t = pl.program_id(0), pl.program_id(1), pl.program_id(2)
    active = t * TILE_B < counts[e * micro + m]

    @pl.when((m == 0) & (t == 0))
    def _():
        gu_acc[...] = jnp.zeros(gu_acc.shape, F32)
        gd_acc[...] = jnp.zeros(gd_acc.shape, F32)
        gb_ref[...] = jnp.zeros(gb_ref.shape, F32)
        gb2_ref[...] = jnp.zeros(gb2_ref.shape, F32)

    @pl.when(active)
    def _():
        dy = dy_ref[0]
        d_hidden = lax.dot_general(dy, w2_ref[0], (((1,), (1,)), ((), ())), preferred_element_type=F32)
        d_pre = (d_hidden * hp_ref[0]).astype(BF16)
        dt = lax.dot_general(d_pre, w1_ref[0], (((1,), (1,)), ((), ())), preferred_element_type=F32)
        hi = dt.astype(BF16)
        dt_ref[0, :, :D] = hi
        dt_ref[0, :, D:] = (dt - hi.astype(F32)).astype(BF16)
        gb2_ref[0] += jnp.sum(dy.astype(F32), 0, keepdims=True)
        gu_acc[...] += lax.dot_general(x_ref[0], d_pre, (((0,), (0,)), ((), ())), preferred_element_type=F32)
        gd_acc[...] += lax.dot_general(h_ref[0], dy, (((0,), (0,)), ((), ())), preferred_element_type=F32)
        gb_ref[0] += jnp.sum(d_pre.astype(F32), 0, keepdims=True)

    @pl.when(jnp.logical_not(active))
    def _():
        dt_ref[0] = jnp.zeros(dt_ref.shape[1:], BF16)

    @pl.when((m == micro - 1) & (t == pl.num_programs(2) - 1))
    def _():
        gu_ref[0] = gu_acc[...].astype(BF16)
        gd_ref[0] = gd_acc[...].astype(BF16)


def ffn_backward(counts, d_expert, table_in, hp, h, w1, w2, micro):
    tiles = CAPP // TILE_B
    rows = table_in.shape[1]
    row_map = lambda e, m, t, c: (m, e * tiles + t, 0)
    w_map = lambda e, m, t, c: (e, 0, 0)
    grid_spec = pltpu.PrefetchScalarGridSpec(
        num_scalar_prefetch=1,
        grid=(E, micro, tiles),
        in_specs=[
            pl.BlockSpec((1, TILE_B, D), row_map),
            pl.BlockSpec((1, TILE_B, D), row_map),
            pl.BlockSpec((1, TILE_B, F), row_map),
            pl.BlockSpec((1, TILE_B, F), row_map),
            pl.BlockSpec((1, D, F), w_map),
            pl.BlockSpec((1, F, D), w_map),
        ],
        out_specs=[
            pl.BlockSpec((1, TILE_B, 2 * D), row_map),
            pl.BlockSpec((1, D, F), w_map),
            pl.BlockSpec((1, F, D), w_map),
            pl.BlockSpec((1, 1, F), w_map),
            pl.BlockSpec((1, 1, D), w_map),
        ],
        scratch_shapes=[pltpu.VMEM((D, F), F32), pltpu.VMEM((F, D), F32)],
    )
    work = micro * rows
    return pl.pallas_call(
        functools.partial(ffn_bwd_kernel, micro),
        grid_spec=grid_spec,
        out_shape=[
            jax.ShapeDtypeStruct((micro, rows, 2 * D), BF16),
            jax.ShapeDtypeStruct((E, D, F), BF16),
            jax.ShapeDtypeStruct((E, F, D), BF16),
            jax.ShapeDtypeStruct((E, 1, F), F32),
            jax.ShapeDtypeStruct((E, 1, D), F32),
        ],
        compiler_params=pltpu.CompilerParams(vmem_limit_bytes=60 * 1024 * 1024),
        cost_estimate=pl.CostEstimate(
            flops=8 * work * D * F // 2, bytes_accessed=work * (8 * D + 6 * F) // 2 + 16 * E * D * F, transcendentals=2 * work * F // 2
        ),
    )(counts, d_expert, table_in, hp, h, w1, w2)

def adamw_kernel(rate, w_ref, m_ref, g_ref, wo_ref, mo_ref):
    g = g_ref[...]
    first = 0.5 * m_ref[0] + 0.5 * g
    root = jnp.sqrt(0.5 * m_ref[1] * m_ref[1] + 0.5 * g * g)
    w = w_ref[...]
    wo_ref[...] = w - rate * (first / (root + 1e-08) + 0.1 * w)
    mo_ref[0] = first
    mo_ref[1] = root


def adamw_pass(weight, moments, grad, rate):
    n, r, c = weight.shape
    spec = pl.BlockSpec((1, r, c), lambda i: (i, 0, 0))
    mspec = pl.BlockSpec((2, 1, r, c), lambda i: (0, i, 0, 0))
    return pl.pallas_call(
        functools.partial(adamw_kernel, rate),
        grid=(n,),
        in_specs=[spec, mspec, spec],
        out_specs=[spec, mspec],
        out_shape=[jax.ShapeDtypeStruct(weight.shape, F32), jax.ShapeDtypeStruct(moments.shape, F32)],
        cost_estimate=pl.CostEstimate(flops=12 * weight.size, bytes_accessed=28 * weight.size, transcendentals=2 * weight.size),
    )(weight, moments, grad)


def layer_norm(value, gain, shift):
    center = value - jnp.mean(value, -1, keepdims=True)
    spread = jnp.mean(center * center, -1, keepdims=True)
    return center * lax.rsqrt(spread + 1e-06) * gain + shift


def gelu_exact(value):
    return jax.nn.gelu(value, approximate=False)


def split_heads(part):
    return part.reshape(-1, S, HEADS, HEAD_DIM)


def dot(a, b):
    return jnp.dot(a, b, preferred_element_type=F32)


def assign_places(route):
    chosen = jnp.concatenate([route[:, :, 0], route[:, :, 1]], 1)
    hits = (chosen[:, :, None] == jnp.arange(E, dtype=jnp.int32)).astype(jnp.int32)
    before = jnp.cumsum(hits, 1) - hits
    slot = jnp.sum(before * hits, 2)
    return chosen * CAPP + slot, jnp.sum(hits, 1)


def hi_lo(v):
    hi = v.astype(BF16)
    lo = (v - hi.astype(F32)).astype(BF16)
    return jnp.concatenate([hi, lo], -1)


def pick_rows(onehot, split):
    both = jnp.einsum("mnr,mrd->mnd", onehot, split, preferred_element_type=F32)
    return both[..., :D] + both[..., D:]


def pack_dense(qkv_w, out_w, router_w, vectors, up_bias):
    rows = qkv_w.shape[0]
    ub = up_bias.reshape(E, rows, 4).transpose(1, 0, 2).reshape(rows, E * 4)
    return jnp.concatenate([qkv_w, out_w, router_w, vectors.T, ub], 1)


def unpack_dense(packed):
    rows = packed.shape[0]
    w_qkv = packed[:, : 3 * D]
    w_out = packed[:, 3 * D : 4 * D]
    w_router = packed[:, 4 * D : 4 * D + E]
    table = packed[:, 4 * D + E : 4 * D + E + NV].T
    ub = packed[:, 4 * D + E + NV :].reshape(rows, E, 4).transpose(1, 0, 2).reshape(E, rows * 4)
    return w_qkv, w_out, w_router, table, ub


def attention_fwd(w_qkv, w_out, table, value):
    rows = value.shape[0]
    nb = rows // S
    scale = HEAD_DIM ** (-0.5)
    first = layer_norm(value, table[0], table[1]).astype(BF16)
    qkv_bias = jnp.concatenate([table[2], jnp.zeros((D,), F32), table[3]]).reshape(3, 1, HEADS, 1, HEAD_DIM)
    w3 = w_qkv.reshape(D, 3, HEADS, HEAD_DIM)
    qkv = (jnp.einsum("bsk,kthd->tbhsd", first.reshape(nb, S, D), w3, preferred_element_type=F32) + qkv_bias).astype(BF16)
    query, key_part, val_part = qkv[0], qkv[1], qkv[2]
    scores = jnp.einsum("bhqd,bhkd->bhqk", query, key_part, preferred_element_type=F32) * scale
    peak = jnp.max(scores, -1, keepdims=True)
    expo = jnp.exp(scores - peak)
    total = jnp.sum(expo, -1, keepdims=True)
    probs_att = (expo / total).astype(BF16)
    log_total = peak + jnp.log(total)
    attended = jnp.einsum("bhqk,bhkd->bqhd", probs_att, val_part, preferred_element_type=F32)
    attended = attended.reshape(rows, D).astype(BF16)
    resid = value + (dot(attended, w_out) + table[4])
    return first, qkv, log_total, attended, resid


def attention_bwd(w_qkv, w_out, table, value, first, qkv, log_total, attended, d_resid):
    rows = value.shape[0]
    nb = rows // S
    scale = HEAD_DIM ** (-0.5)
    d_branch = d_resid.astype(BF16)
    g_bias_out = jnp.sum(d_branch.astype(F32), 0)
    g_out = lax.dot_general(attended, d_branch, (((0,), (0,)), ((), ())), preferred_element_type=F32)
    d_att = jnp.einsum(
        "bsn,hdn->bhsd", d_branch.reshape(nb, S, D), w_out.reshape(HEADS, HEAD_DIM, D), preferred_element_type=F32
    ).astype(BF16)
    query, key_part, val_part = qkv[0], qkv[1], qkv[2]
    scores = jnp.einsum("bhqd,bhkd->bhqk", query, key_part, preferred_element_type=F32) * scale
    probs_f = jnp.exp(scores - log_total)
    probs_att = probs_f.astype(BF16)
    d_val = jnp.einsum("bhqk,bhqd->bhkd", probs_att, d_att, preferred_element_type=F32)
    d_prob = jnp.einsum("bhqd,bhkd->bhqk", d_att, val_part, preferred_element_type=F32)
    d_score = (probs_f * (d_prob - jnp.sum(d_prob * probs_f, -1, keepdims=True))).astype(BF16)
    d_query = jnp.einsum("bhqk,bhkd->bhqd", d_score, key_part, preferred_element_type=F32) * scale
    d_key = jnp.einsum("bhqk,bhqd->bhkd", d_score, query, preferred_element_type=F32) * scale
    d_qkv = jnp.stack([d_query, d_key, d_val]).astype(BF16)
    d_qkv_f = d_qkv.astype(F32)
    g_bias_q = jnp.sum(d_qkv_f[0], (0, 2)).reshape(D)
    g_bias_v = jnp.sum(d_qkv_f[2], (0, 2)).reshape(D)
    first_b = first.reshape(nb, S, D)
    g_qkv = jnp.einsum("bsk,tbhsd->kthd", first_b, d_qkv, preferred_element_type=F32).reshape(D, 3 * D)
    w3 = w_qkv.reshape(D, 3, HEADS, HEAD_DIM)
    d_first = jnp.einsum("tbhsd,kthd->bsk", d_qkv, w3, preferred_element_type=F32).reshape(rows, D)
    first_pull = jax.vjp(layer_norm, value, table[0], table[1])[1]
    d_input, g_gain_one, g_shift_one = first_pull(d_first)
    return (g_qkv, g_out, g_bias_out, g_bias_q, g_bias_v, g_gain_one, g_shift_one), d_input


def adamw(weight, moments, grad, rate):
    first = 0.5 * moments[0] + 0.5 * grad
    root = jnp.sqrt(0.5 * moments[1] * moments[1] + 0.5 * grad * grad)
    update = first / (root + 1e-08)
    which = lax.broadcasted_iota(jnp.int32, moments.shape, 0) == 0
    both = jnp.where(which, 0.5 * moments + 0.5 * grad, jnp.sqrt(0.5 * moments * moments + 0.5 * grad * grad))
    return (weight - rate * (update + 0.1 * weight), both)


def shards(
    tokens,
    cotangent,
    expert_index,
    qkv_weight,
    out_weight,
    router_weight,
    up_weight,
    up_bias,
    down_weight,
    vectors,
    qkv_moments,
    out_moments,
    router_moments,
    up_moments,
    up_bias_moments,
    down_moments,
    vector_moments,
):
    rows = tokens.shape[0]
    micro = rows // MB_TOK
    gs = qkv_weight.shape[0]
    group_size = D // gs
    core = lax.axis_index("core")

    dense_in = pack_dense(qkv_weight, out_weight, router_weight, vectors, up_bias)
    width = dense_in.shape[1]
    dense_in = jnp.pad(dense_in, ((0, 0), (0, DENSE_AG - width))).astype(BF16)
    w_up_all, w_down_all, dense = ring_all_gather(
        up_weight.astype(BF16), down_weight.astype(BF16), dense_in, group_size, 1
    )
    w_qkv, w_out, w_router, table_b, b_up_b = unpack_dense(dense[:, :width])
    table = table_b.astype(F32)
    b_up = b_up_b.astype(F32)

    value = tokens.astype(F32)
    d_out = cotangent.astype(F32)
    first, qkv, log_total, attended, resid = attention_fwd(w_qkv, w_out, table, value)
    second = layer_norm(resid, table[5], table[6]).astype(BF16)
    logits = dot(second, w_router)
    probs = jax.nn.softmax(logits, -1)
    picked = expert_index[:, :, None] == jnp.arange(E, dtype=jnp.int32)
    gate = jnp.sum(jnp.where(picked, probs[:, None, :], 0.0), -1)

    route = expert_index.reshape(micro, MB_TOK, 2)
    places, counts = assign_places(route)
    counts = counts.T.reshape(E * micro)
    onehot = (places[:, :, None] == jnp.arange(E * CAPP, dtype=jnp.int32)).astype(BF16)
    second_m = second.reshape(micro, MB_TOK, D)
    pair = jnp.concatenate([second_m, second_m], 1)
    table_in = jnp.einsum("mnr,mnd->mrd", onehot, pair, preferred_element_type=F32).astype(BF16)

    hidden_pre, hidden, y_all = ffn_forward(
        counts, table_in, w_up_all, b_up[:, None, :], w_down_all, table[7 : 7 + E][:, None, :], micro
    )
    picked_rows = pick_rows(onehot, y_all)
    out_zero = picked_rows[:, :MB_TOK].reshape(rows, D)
    out_one = picked_rows[:, MB_TOK:].reshape(rows, D)
    result = resid + (gate[:, 0:1] * out_zero + gate[:, 1:2] * out_one)

    d_gate = jnp.stack([jnp.sum(d_out * out_zero, -1), jnp.sum(d_out * out_one, -1)], 1)
    d_out_m = d_out.reshape(micro, MB_TOK, D)
    gate_m = gate.reshape(micro, MB_TOK, 2)
    weighted = jnp.concatenate([gate_m[:, :, 0:1] * d_out_m, gate_m[:, :, 1:2] * d_out_m], 1).astype(BF16)
    d_expert = jnp.einsum("mnr,mnd->mrd", onehot, weighted, preferred_element_type=F32).astype(BF16)

    d_table, g_up, g_down, g_b1, g_b2 = ffn_backward(counts, d_expert, table_in, hidden_pre, hidden, w_up_all, w_down_all, micro)
    g_up_bias_all = g_b1[:, 0, :]
    g_bias_down = g_b2[:, 0, :]

    onehot_sum = onehot[:, :MB_TOK] + onehot[:, MB_TOK:]
    d_picked = pick_rows(onehot_sum, d_table).reshape(rows, D)

    d_probs = jnp.sum(jnp.where(picked, d_gate[:, :, None], 0.0), 1)
    d_logit = (probs * (d_probs - jnp.sum(d_probs * probs, -1, keepdims=True))).astype(BF16)
    g_router = lax.dot_general(second, d_logit, (((0,), (0,)), ((), ())), preferred_element_type=F32)
    d_second = d_picked + lax.dot_general(d_logit, w_router, (((1,), (1,)), ((), ())), preferred_element_type=F32)
    norm_pull = jax.vjp(layer_norm, resid, table[5], table[6])[1]
    d_resid, g_gain_two, g_shift_two = norm_pull(d_second)
    d_resid = d_out + d_resid

    att_grads, d_input = attention_bwd(w_qkv, w_out, table, value, first, qkv, log_total, attended, d_resid)
    g_qkv, g_out, g_bias_out, g_bias_q, g_bias_v, g_gain_one, g_shift_one = att_grads
    input_grad = d_resid + d_input

    g_table = jnp.concatenate(
        [
            jnp.stack([g_gain_one, g_shift_one, g_bias_q, g_bias_v, g_bias_out, g_gain_two, g_shift_two]),
            g_bias_down,
        ],
        0,
    )
    dense_g = pack_dense(g_qkv, g_out, g_router, g_table, g_up_bias_all)
    width = dense_g.shape[1]
    dense_g = jnp.pad(dense_g, ((0, 0), (0, DENSE_AG - width))).astype(BF16)
    x_pair = lax.axis_size("rx") == 2
    r_up, r_down, r_dense = grad_reduce(g_up, g_down, dense_g, group_size, x_pair, 0)
    if not x_pair:
        r_up, r_down, r_dense = lax.psum((r_up, r_down, r_dense), "rx")
    r_qkv, r_out, r_router, r_table, r_ub = unpack_dense(r_dense[:, :width])

    reduced = (r_qkv, r_out, r_router, r_up, r_ub, r_down, r_table)
    rates = (
        2.0 * D ** (-0.5),
        2.0 * (D // 32) ** (-0.5),
        2.0 * (2 * D) ** (-0.5),
        2.0 * D ** (-0.5),
        0.2,
        2.0 * (F // 16) ** (-0.5),
        0.2,
    )
    params = (qkv_weight, out_weight, router_weight, up_weight, up_bias, down_weight, vectors)
    moments = (qkv_moments, out_moments, router_moments, up_moments, up_bias_moments, down_moments, vector_moments)
    news = []
    states = []
    for weight, state, grad, rate in zip(params, moments, reduced, rates):
        if weight.ndim == 3:
            new_weight, new_state = adamw_pass(weight, state, grad, rate)
        else:
            new_weight, new_state = adamw_pass(weight[None], state[:, None], grad[None], rate)
            new_weight, new_state = new_weight[0], new_state[:, 0]
        news.append(new_weight)
        states.append(new_state)
    return (result.astype(BF16), input_grad) + reduced + tuple(news) + tuple(states)


def solution(mesh):
    replica, group = mesh.shape["replica"], mesh.shape["group"]
    view = Mesh(np.asarray(mesh.devices).reshape(replica // 2, 2, group), ("rx", "core", "group"))
    in_specs = (
        P(TOK, None),
        P(TOK, None),
        P(TOK, None),
        P("group", None),
        P("group", None),
        P("group", None),
        P(None, "group", None),
        P(None, "group"),
        P(None, "group", None),
        P(None, "group"),
        P(None, "group", None),
        P(None, "group", None),
        P(None, "group", None),
        P(None, None, "group", None),
        P(None, None, "group"),
        P(None, None, "group", None),
        P(None, None, "group"),
    )
    out_specs = (
        P(TOK, None),
        P(TOK, None),
        P("group", None),
        P("group", None),
        P("group", None),
        P(None, "group", None),
        P(None, "group"),
        P(None, "group", None),
        P(None, "group"),
        P("group", None),
        P("group", None),
        P("group", None),
        P(None, "group", None),
        P(None, "group"),
        P(None, "group", None),
        P(None, "group"),
        P(None, "group", None),
        P(None, "group", None),
        P(None, "group", None),
        P(None, None, "group", None),
        P(None, None, "group"),
        P(None, None, "group", None),
        P(None, None, "group"),
    )
    return jax.shard_map(shards, mesh=view, in_specs=in_specs, out_specs=out_specs, check_vma=False)
```

```python
import functools

import jax
import jax.numpy as jnp
import numpy as np
from jax import lax
from jax.sharding import Mesh
from jax.sharding import PartitionSpec as P
from jax.experimental import pallas as pl
from jax.experimental.pallas import tpu as pltpu

D = 512
HEADS = 8
HEAD_DIM = 64
F = 2048
E = 4
S = 197
MB_TOK = 394
CAP = 392
NV = 11
DENSE_AG = 2560
DENSE_PAD = 2304
F32 = jnp.float32
BF16 = jnp.bfloat16
TOK = ("rx", "core", "group")


MESH_ID = pl.DeviceIdType.MESH


def ring_order(groups):
    if groups in (4, 8):
        zs = groups // 2

        def pos_of(g):
            y = g % 2
            z = g // 2
            return z + y * (2 * zs - 1 - 2 * z)

        def dev_at(p):
            p = p % groups
            yy = p // zs
            return 2 * (p + yy * (2 * zs - 1 - 2 * p)) + yy

        return pos_of, dev_at
    return (lambda g: g), (lambda p: p % groups)


def ring_rs_kernel(groups, n_in, *refs):
    ins = refs[:n_in]
    outs = refs[n_in : 2 * n_in]
    rbufs = refs[2 * n_in : 3 * n_in]
    sbufs = refs[3 * n_in : 4 * n_in]
    owns = refs[4 * n_in : 5 * n_in]
    send_sem, recv_sem, load_sem = refs[5 * n_in :]
    pos_of, dev_at = ring_order(groups)
    rx = lax.axis_index("rx")
    core = lax.axis_index("core")
    g = lax.axis_index("group")
    pos = pos_of(g)
    nbr = (dev_at(pos + 1), dev_at(pos + groups - 1))

    barrier = pltpu.get_barrier_semaphore()
    for n in nbr:
        pl.semaphore_signal(barrier, inc=1, device_id=(rx, core, n), device_id_type=MESH_ID)
    pl.semaphore_wait(barrier, 2)

    def block_dev(d, s):
        if d == 0:
            return dev_at(pos + 2 * groups - s - 1)
        return dev_at(pos + s + 1)

    def load(d, s, slot):
        b = block_dev(d, s)
        copies = []
        for i in range(n_in):
            rows = ins[i].shape[1] // groups
            half = ins[i].shape[2] // 2
            src = ins[i].at[:, pl.ds(pl.multiple_of(b * rows, rows), rows), pl.ds(d * half, half)]
            copies.append(pltpu.make_async_copy(src, owns[i].at[d, slot], load_sem.at[d, slot, i]))
        return copies

    def remote(d, s, i):
        return pltpu.make_async_remote_copy(
            src_ref=sbufs[i].at[d, s],
            dst_ref=rbufs[i].at[d, s],
            send_sem=send_sem.at[d, s, i],
            recv_sem=recv_sem.at[d, s, i],
            device_id=(rx, core, nbr[d]),
            device_id_type=MESH_ID,
        )

    for d in range(2):
        for c in load(d, 0, 0):
            c.start()
    sends = []
    for s in range(groups):
        slot = s % 2
        for d in range(2):
            for c in load(d, s, slot):
                c.wait()
            if s + 1 < groups:
                for c in load(d, s + 1, 1 - slot):
                    c.start()
            for i in range(n_in):
                if s > 0:
                    remote(d, s - 1, i).wait_recv()
                for a in range(ins[i].shape[0]):
                    mine = owns[i][d, slot, a].astype(F32)
                    if s > 0:
                        mine = mine + rbufs[i][d, s - 1, a].astype(F32)
                    if s < groups - 1:
                        sbufs[i][d, s, a] = mine.astype(sbufs[i].dtype)
                    else:
                        half = ins[i].shape[2] // 2
                        outs[i][a, :, pl.ds(d * half, half)] = mine.astype(outs[i].dtype)
                if s < groups - 1:
                    c = remote(d, s, i)
                    c.start()
                    sends.append(c)
    for c in sends:
        c.wait_send()


def ring_reduce_scatter(xs, groups, collective_id):
    n_in = len(xs)
    outs, rb, own = [], [], []
    flops = 0
    nbytes = 0
    for x in xs:
        a, total, c = x.shape
        rows = total // groups
        outs.append(jax.ShapeDtypeStruct((a, rows, c), x.dtype))
        rb.append(pltpu.VMEM((2, groups - 1, a, rows, c // 2), x.dtype))
        own.append(pltpu.VMEM((2, 2, a, rows, c // 2), x.dtype))
        flops += a * total * c
        nbytes += 3 * x.size * x.dtype.itemsize
    scratch = rb + rb + own + [
        pltpu.SemaphoreType.DMA((2, groups - 1, n_in)),
        pltpu.SemaphoreType.DMA((2, groups - 1, n_in)),
        pltpu.SemaphoreType.DMA((2, 2, n_in)),
    ]
    return pl.pallas_call(
        functools.partial(ring_rs_kernel, groups, n_in),
        out_shape=outs,
        in_specs=[pl.BlockSpec(memory_space=pl.ANY)] * n_in,
        out_specs=[pl.BlockSpec(memory_space=pltpu.VMEM)] * n_in,
        scratch_shapes=scratch,
        compiler_params=pltpu.CompilerParams(
            collective_id=collective_id, has_side_effects=True, vmem_limit_bytes=60 * 1024 * 1024
        ),
        cost_estimate=pl.CostEstimate(flops=flops, bytes_accessed=nbytes, transcendentals=0),
    )(*xs)


def ring_ag_kernel(groups, *refs):
    in_up, in_down, in_dense, out_up, out_down, out_dense = refs[:6]
    ring_send, ring_recv, part_send, part_recv, local_sem = refs[6:]
    pos_of, dev_at = ring_order(groups)
    rx = lax.axis_index("rx")
    core = lax.axis_index("core")
    g = lax.axis_index("group")
    other = 1 - core
    pos = pos_of(g)
    nbr = (dev_at(pos + 1), dev_at(pos + groups - 1))
    gs = in_up.shape[1]
    fs = in_down.shape[1]
    width = in_dense.shape[1] // 2

    barrier = pltpu.get_barrier_semaphore()
    for n in nbr:
        pl.semaphore_signal(barrier, inc=1, device_id=(rx, core, n), device_id_type=MESH_ID)
    pl.semaphore_signal(barrier, inc=1, device_id=(rx, other, g), device_id_type=MESH_ID)
    pl.semaphore_wait(barrier, 3)

    def items(owner):
        found = []
        for k in range(2):
            e = 2 * k + owner
            found.append((in_up.at[e], lambda b, e=e: out_up.at[e, pl.ds(pl.multiple_of(b * gs, gs), gs)], F // 2))
            found.append((in_down.at[e], lambda b, e=e: out_down.at[e, pl.ds(pl.multiple_of(b * fs, fs), fs)], D // 2))
        dense_in = in_dense.at[:, pl.ds(owner * width, width)]
        found.append(
            (dense_in, lambda b: out_dense.at[pl.ds(pl.multiple_of(b * gs, gs), gs), pl.ds(owner * width, width)], width // 2)
        )
        return found

    mine = items(core)
    theirs = items(other)
    n_items = len(mine)

    locals_ = [pltpu.make_async_copy(in_up.at[e], out_up.at[e, pl.ds(pl.multiple_of(g * gs, gs), gs)], local_sem.at[e]) for e in range(E)]
    locals_ += [
        pltpu.make_async_copy(in_down.at[e], out_down.at[e, pl.ds(pl.multiple_of(g * fs, fs), fs)], local_sem.at[E + e])
        for e in range(E)
    ]
    locals_.append(pltpu.make_async_copy(in_dense, out_dense.at[pl.ds(pl.multiple_of(g * gs, gs), gs)], local_sem.at[2 * E]))
    for c in locals_:
        c.start()

    def block_at(d, s):
        if d == 0:
            return dev_at(pos + 2 * groups - 1 - s)
        return dev_at(pos + 1 + s)

    def ring_copy(d, s, j, src_block):
        src_in, dst_of, half = mine[j]
        cols = pl.ds(d * half, half)
        if src_block is None:
            src = src_in.at[:, cols]
            dst = dst_of(g).at[:, cols]
        else:
            src = dst_of(src_block).at[:, cols]
            dst = src
        return pltpu.make_async_remote_copy(
            src_ref=src, dst_ref=dst, send_sem=ring_send.at[d, s, j], recv_sem=ring_recv.at[d, s, j],
            device_id=(rx, core, nbr[d]), device_id_type=MESH_ID,
        )

    def part_copy(d, s, j, table, block):
        _, dst_of, half = table[j]
        view = dst_of(block).at[:, pl.ds(d * half, half)]
        return pltpu.make_async_remote_copy(
            src_ref=view, dst_ref=view, send_sem=part_send.at[d, s, j], recv_sem=part_recv.at[d, s, j],
            device_id=(rx, other, g), device_id_type=MESH_ID,
        )

    sends = []
    for d in range(2):
        for j in range(n_items):
            c = ring_copy(d, 0, j, None)
            c.start()
            sends.append(c)
    for s in range(groups - 1):
        for d in range(2):
            b = block_at(d, s)
            for j in range(n_items):
                pltpu.make_async_remote_copy(
                    src_ref=mine[j][1](b).at[:, pl.ds(d * mine[j][2], mine[j][2])],
                    dst_ref=mine[j][1](b).at[:, pl.ds(d * mine[j][2], mine[j][2])],
                    send_sem=ring_send.at[d, s, j], recv_sem=ring_recv.at[d, s, j],
                    device_id=(rx, core, nbr[d]), device_id_type=MESH_ID,
                ).wait_recv()
                if s + 1 < groups - 1:
                    c = ring_copy(d, s + 1, j, b)
                    c.start()
                    sends.append(c)
                c = part_copy(d, s, j, mine, b)
                c.start()
                sends.append(c)
    for s in range(groups - 1):
        for d in range(2):
            b = block_at(d, s)
            for j in range(n_items):
                part_copy(d, s, j, theirs, b).wait_recv()
    for c in sends:
        c.wait_send()
    for c in locals_:
        c.wait()


def ring_all_gather(up_b, down_b, dense_b, groups, collective_id):
    n_items = 5
    gs = up_b.shape[1]
    shapes = [
        jax.ShapeDtypeStruct((E, gs * groups, F), BF16),
        jax.ShapeDtypeStruct((E, down_b.shape[1] * groups, D), BF16),
        jax.ShapeDtypeStruct((gs * groups, dense_b.shape[1]), BF16),
    ]
    nbytes = sum(int(np.prod(s.shape)) * 2 for s in shapes)
    return pl.pallas_call(
        functools.partial(ring_ag_kernel, groups),
        out_shape=shapes,
        in_specs=[pl.BlockSpec(memory_space=pl.ANY)] * 3,
        out_specs=[pl.BlockSpec(memory_space=pl.ANY)] * 3,
        scratch_shapes=[
            pltpu.SemaphoreType.DMA((2, groups - 1, n_items)),
            pltpu.SemaphoreType.DMA((2, groups - 1, n_items)),
            pltpu.SemaphoreType.DMA((2, groups - 1, n_items)),
            pltpu.SemaphoreType.DMA((2, groups - 1, n_items)),
            pltpu.SemaphoreType.DMA((2 * E + 1,)),
        ],
        compiler_params=pltpu.CompilerParams(collective_id=collective_id, has_side_effects=True),
        cost_estimate=pl.CostEstimate(flops=0, bytes_accessed=nbytes, transcendentals=0),
    )(up_b, down_b, dense_b)


def grad_items(gu, gd, gdense, owner, gs, fs, width):
    found = []
    for k in range(2):
        e = 2 * k + owner
        found.append((lambda b, e=e: gu.at[e, pl.ds(pl.multiple_of(b * gs, gs), gs)], F // 2))
        found.append((lambda b, e=e: gd.at[e, pl.ds(pl.multiple_of(b * fs, fs), fs)], D // 2))
    found.append((lambda b: gdense.at[pl.ds(pl.multiple_of(b * gs, gs), gs), pl.ds(owner * width, width)], width // 2))
    return found


def ring_rs2_kernel(groups, x_pair, *refs):
    gu, gd, gdense, out_up, out_down, out_dense = refs[:6]
    n_items = 5
    scr = refs[6:]
    rbuf, sbuf, pbuf, own, fin, xr, cr, xs = (scr[i * n_items : (i + 1) * n_items] for i in range(8))
    ring_send, ring_recv, part_send, part_recv, load_sem, x_send, x_recv, c_send, c_recv = scr[8 * n_items :]
    pos_of, dev_at = ring_order(groups)
    rx = lax.axis_index("rx")
    core = lax.axis_index("core")
    g = lax.axis_index("group")
    other = 1 - core
    pos = pos_of(g)
    nbr = (dev_at(pos + 1), dev_at(pos + groups - 1))
    gs = gu.shape[1] // groups
    fs = gd.shape[1] // groups
    width = gdense.shape[1] // 2
    mine = grad_items(gu, gd, gdense, core, gs, fs, width)
    theirs = grad_items(gu, gd, gdense, other, gs, fs, width)

    barrier = pltpu.get_barrier_semaphore()
    for n in nbr:
        pl.semaphore_signal(barrier, inc=1, device_id=(rx, core, n), device_id_type=MESH_ID)
    pl.semaphore_signal(barrier, inc=1, device_id=(rx, other, g), device_id_type=MESH_ID)
    count = 3
    if x_pair:
        pl.semaphore_signal(barrier, inc=1, device_id=(1 - rx, core, g), device_id_type=MESH_ID)
        count = 4
    pl.semaphore_wait(barrier, count)

    def block_at(d, s):
        if d == 0:
            return dev_at(pos + 2 * groups - 1 - s)
        return dev_at(pos + 1 + s)

    def cols(j, d):
        half = mine[j][1]
        return pl.ds(d * half, half)

    def load(d, s, slot, j):
        return pltpu.make_async_copy(mine[j][0](block_at(d, s)).at[:, cols(j, d)], own[j].at[d, slot], load_sem.at[d, slot, j])

    def part(d, s, j):
        return pltpu.make_async_remote_copy(
            src_ref=theirs[j][0](block_at(d, s)).at[:, cols(j, d)], dst_ref=pbuf[j].at[d, s],
            send_sem=part_send.at[d, s, j], recv_sem=part_recv.at[d, s, j],
            device_id=(rx, other, g), device_id_type=MESH_ID,
        )

    def ring(d, s, j):
        return pltpu.make_async_remote_copy(
            src_ref=sbuf[j].at[d, s], dst_ref=rbuf[j].at[d, s],
            send_sem=ring_send.at[d, s, j], recv_sem=ring_recv.at[d, s, j],
            device_id=(rx, core, nbr[d]), device_id_type=MESH_ID,
        )

    sends = []

    def ring_wave(items):
        for d in range(2):
            for j in items:
                load(d, 0, 0, j).start()
                c = part(d, 0, j)
                c.start()
                sends.append(c)
        for s in range(groups):
            slot = s % 2
            for d in range(2):
                for j in items:
                    load(d, s, slot, j).wait()
                    if s + 1 < groups:
                        load(d, s + 1, 1 - slot, j).start()
                        c = part(d, s + 1, j)
                        c.start()
                        sends.append(c)
                    part(d, s, j).wait_recv()
                    val = own[j][d, slot].astype(F32) + pbuf[j][d, s].astype(F32)
                    if s > 0:
                        ring(d, s - 1, j).wait_recv()
                        val = val + rbuf[j][d, s - 1].astype(F32)
                    if s < groups - 1:
                        sbuf[j][d, s] = val.astype(BF16)
                        c = ring(d, s, j)
                        c.start()
                        sends.append(c)
                    else:
                        fin[j][d] = val

    def x_start(items):
        copies = []
        for d in range(2):
            for j in items:
                xs[j][d] = fin[j][d].astype(BF16)
                c = pltpu.make_async_remote_copy(
                    src_ref=xs[j].at[d], dst_ref=xr[j].at[d], send_sem=x_send.at[d, j], recv_sem=x_recv.at[d, j],
                    device_id=(1 - rx, core, g), device_id_type=MESH_ID,
                )
                c.start()
                copies.append(c)
        sends.extend(copies)
        return copies

    def x_finish(items, copies):
        for c in copies:
            c.wait_recv()
        for d in range(2):
            for j in items:
                fin[j][d] = xs[j][d].astype(F32) + xr[j][d].astype(F32)

    def c_start(items):
        copies = []
        for d in range(2):
            for j in items:
                c = pltpu.make_async_remote_copy(
                    src_ref=fin[j].at[d], dst_ref=cr[j].at[d], send_sem=c_send.at[d, j], recv_sem=c_recv.at[d, j],
                    device_id=(rx, other, g), device_id_type=MESH_ID,
                )
                c.start()
                copies.append(c)
        return copies

    wave_a, wave_b = (0, 1, 2, 4), (3,)
    ring_wave(wave_a)
    if x_pair:
        xa = x_start(wave_a)
    ring_wave(wave_b)
    if x_pair:
        x_finish(wave_a, xa)
    c_copies = c_start(wave_a)
    if x_pair:
        x_finish(wave_b, x_start(wave_b))
    c_copies += c_start(wave_b)

    def out_items(owner):
        found = []
        for k in range(2):
            e = 2 * k + owner
            found.append(lambda d, e=e: out_up.at[e, :, pl.ds(d * (F // 2), F // 2)])
            found.append(lambda d, e=e: out_down.at[e, :, pl.ds(d * (D // 2), D // 2)])
        found.append(lambda d: out_dense.at[:, pl.ds(owner * width + d * (width // 2), width // 2)])
        return found

    mine_out = out_items(core)
    theirs_out = out_items(other)
    for d in range(2):
        for j in range(n_items):
            mine_out[j](d)[...] = fin[j][d]
    for c in c_copies:
        c.wait_recv()
    for d in range(2):
        for j in range(n_items):
            theirs_out[j](d)[...] = cr[j][d]
    for c in sends + c_copies:
        c.wait_send()


def grad_reduce(gu, gd, gdense, groups, x_pair, collective_id):
    gs = gu.shape[1] // groups
    fs = gd.shape[1] // groups
    width = gdense.shape[1] // 2
    item_shapes = [(gs, F // 2), (fs, D // 2), (gs, F // 2), (fs, D // 2), (gs, width // 2)]
    scratch = []
    for lead, dtype in (((2, groups - 1), BF16), ((2, groups - 1), BF16), ((2, groups), BF16), ((2, 2), BF16), ((2,), F32), ((2,), BF16), ((2,), F32), ((2,), BF16)):
        scratch += [pltpu.VMEM(lead + shp, dtype) for shp in item_shapes]
    scratch += [
        pltpu.SemaphoreType.DMA((2, groups - 1, 5)),
        pltpu.SemaphoreType.DMA((2, groups - 1, 5)),
        pltpu.SemaphoreType.DMA((2, groups, 5)),
        pltpu.SemaphoreType.DMA((2, groups, 5)),
        pltpu.SemaphoreType.DMA((2, 2, 5)),
        pltpu.SemaphoreType.DMA((2, 5)),
        pltpu.SemaphoreType.DMA((2, 5)),
        pltpu.SemaphoreType.DMA((2, 5)),
        pltpu.SemaphoreType.DMA((2, 5)),
    ]
    outs = [
        jax.ShapeDtypeStruct((E, gs, F), F32),
        jax.ShapeDtypeStruct((E, fs, D), F32),
        jax.ShapeDtypeStruct((gs, gdense.shape[1]), F32),
    ]
    nbytes = 2 * (gu.size + gd.size + gdense.size)
    return pl.pallas_call(
        functools.partial(ring_rs2_kernel, groups, x_pair),
        out_shape=outs,
        in_specs=[pl.BlockSpec(memory_space=pl.ANY)] * 3,
        out_specs=[pl.BlockSpec(memory_space=pltpu.VMEM)] * 3,
        scratch_shapes=scratch,
        compiler_params=pltpu.CompilerParams(
            collective_id=collective_id, has_side_effects=True, vmem_limit_bytes=62 * 1024 * 1024
        ),
        cost_estimate=pl.CostEstimate(flops=gu.size + gd.size + gdense.size, bytes_accessed=nbytes, transcendentals=0),
    )(gu, gd, gdense)


TILE = 128
TILE_B = 256
CAPP = 512
SQRT_HALF = float(np.sqrt(0.5))
INV_SQRT_2PI = float(1.0 / np.sqrt(2.0 * np.pi))


def ffn_fwd_kernel(micro, counts, x_ref, w1_ref, b1_ref, w2_ref, b2_ref, hp_ref, h_ref, y_ref):
    e, m, t = pl.program_id(0), pl.program_id(1), pl.program_id(2)
    active = t * TILE < counts[e * micro + m]

    @pl.when(active)
    def _():
        hp = jnp.dot(x_ref[0], w1_ref[0], preferred_element_type=F32) + b1_ref[0]
        cdf = 0.5 * (1.0 + lax.erf(hp * SQRT_HALF))
        h = (hp * cdf).astype(BF16)
        hp_ref[0] = cdf + hp * jnp.exp(-0.5 * hp * hp) * INV_SQRT_2PI
        h_ref[0] = h
        y = jnp.dot(h, w2_ref[0], preferred_element_type=F32) + b2_ref[0]
        hi = y.astype(BF16)
        y_ref[0, :, :D] = hi
        y_ref[0, :, D:] = (y - hi.astype(F32)).astype(BF16)

    @pl.when(jnp.logical_not(active))
    def _():
        y_ref[0] = jnp.zeros(y_ref.shape[1:], BF16)


def ffn_forward(counts, table_in, w1, b1, w2, b2, micro):
    tiles = CAPP // TILE
    rows = table_in.shape[1]
    row_map = lambda e, m, t, c: (m, e * tiles + t, 0)
    w_map = lambda e, m, t, c: (e, 0, 0)
    grid_spec = pltpu.PrefetchScalarGridSpec(
        num_scalar_prefetch=1,
        grid=(E, micro, tiles),
        in_specs=[
            pl.BlockSpec((1, TILE, D), row_map),
            pl.BlockSpec((1, D, F), w_map),
            pl.BlockSpec((1, 1, F), w_map),
            pl.BlockSpec((1, F, D), w_map),
            pl.BlockSpec((1, 1, D), w_map),
        ],
        out_specs=[
            pl.BlockSpec((1, TILE, F), row_map),
            pl.BlockSpec((1, TILE, F), row_map),
            pl.BlockSpec((1, TILE, 2 * D), row_map),
        ],
    )
    work = micro * rows
    return pl.pallas_call(
        functools.partial(ffn_fwd_kernel, micro),
        grid_spec=grid_spec,
        out_shape=[
            jax.ShapeDtypeStruct((micro, rows, F), F32),
            jax.ShapeDtypeStruct((micro, rows, F), BF16),
            jax.ShapeDtypeStruct((micro, rows, 2 * D), BF16),
        ],
        compiler_params=pltpu.CompilerParams(vmem_limit_bytes=48 * 1024 * 1024),
        cost_estimate=pl.CostEstimate(
            flops=4 * work * D * F // 2, bytes_accessed=work * (2 * D + 6 * F + 4 * D) // 2, transcendentals=work * F // 2
        ),
    )(counts, table_in, w1, b1, w2, b2)


def ffn_bwd_kernel(micro, counts, dy_ref, x_ref, hp_ref, h_ref, w1_ref, w2_ref, dt_ref, gu_ref, gd_ref, gb_ref, gb2_ref, gu_acc, gd_acc):
    e, m, t = pl.program_id(0), pl.program_id(1), pl.program_id(2)
    active = t * TILE_B < counts[e * micro + m]

    @pl.when((m == 0) & (t == 0))
    def _():
        gu_acc[...] = jnp.zeros(gu_acc.shape, F32)
        gd_acc[...] = jnp.zeros(gd_acc.shape, F32)
        gb_ref[...] = jnp.zeros(gb_ref.shape, F32)
        gb2_ref[...] = jnp.zeros(gb2_ref.shape, F32)

    @pl.when(active)
    def _():
        dy = dy_ref[0]
        d_hidden = lax.dot_general(dy, w2_ref[0], (((1,), (1,)), ((), ())), preferred_element_type=F32)
        d_pre = (d_hidden * hp_ref[0]).astype(BF16)
        dt = lax.dot_general(d_pre, w1_ref[0], (((1,), (1,)), ((), ())), preferred_element_type=F32)
        hi = dt.astype(BF16)
        dt_ref[0, :, :D] = hi
        dt_ref[0, :, D:] = (dt - hi.astype(F32)).astype(BF16)
        gb2_ref[0] += jnp.sum(dy.astype(F32), 0, keepdims=True)
        gu_acc[...] += lax.dot_general(x_ref[0], d_pre, (((0,), (0,)), ((), ())), preferred_element_type=F32)
        gd_acc[...] += lax.dot_general(h_ref[0], dy, (((0,), (0,)), ((), ())), preferred_element_type=F32)
        gb_ref[0] += jnp.sum(d_pre.astype(F32), 0, keepdims=True)

    @pl.when(jnp.logical_not(active))
    def _():
        dt_ref[0] = jnp.zeros(dt_ref.shape[1:], BF16)

    @pl.when((m == micro - 1) & (t == pl.num_programs(2) - 1))
    def _():
        gu_ref[0] = gu_acc[...].astype(BF16)
        gd_ref[0] = gd_acc[...].astype(BF16)


def ffn_backward(counts, d_expert, table_in, hp, h, w1, w2, micro):
    tiles = CAPP // TILE_B
    rows = table_in.shape[1]
    row_map = lambda e, m, t, c: (m, e * tiles + t, 0)
    w_map = lambda e, m, t, c: (e, 0, 0)
    grid_spec = pltpu.PrefetchScalarGridSpec(
        num_scalar_prefetch=1,
        grid=(E, micro, tiles),
        in_specs=[
            pl.BlockSpec((1, TILE_B, D), row_map),
            pl.BlockSpec((1, TILE_B, D), row_map),
            pl.BlockSpec((1, TILE_B, F), row_map),
            pl.BlockSpec((1, TILE_B, F), row_map),
            pl.BlockSpec((1, D, F), w_map),
            pl.BlockSpec((1, F, D), w_map),
        ],
        out_specs=[
            pl.BlockSpec((1, TILE_B, 2 * D), row_map),
            pl.BlockSpec((1, D, F), w_map),
            pl.BlockSpec((1, F, D), w_map),
            pl.BlockSpec((1, 1, F), w_map),
            pl.BlockSpec((1, 1, D), w_map),
        ],
        scratch_shapes=[pltpu.VMEM((D, F), F32), pltpu.VMEM((F, D), F32)],
    )
    work = micro * rows
    return pl.pallas_call(
        functools.partial(ffn_bwd_kernel, micro),
        grid_spec=grid_spec,
        out_shape=[
            jax.ShapeDtypeStruct((micro, rows, 2 * D), BF16),
            jax.ShapeDtypeStruct((E, D, F), BF16),
            jax.ShapeDtypeStruct((E, F, D), BF16),
            jax.ShapeDtypeStruct((E, 1, F), F32),
            jax.ShapeDtypeStruct((E, 1, D), F32),
        ],
        compiler_params=pltpu.CompilerParams(vmem_limit_bytes=60 * 1024 * 1024),
        cost_estimate=pl.CostEstimate(
            flops=8 * work * D * F // 2, bytes_accessed=work * (8 * D + 6 * F) // 2 + 16 * E * D * F, transcendentals=2 * work * F // 2
        ),
    )(counts, d_expert, table_in, hp, h, w1, w2)

def adamw_kernel(rate, w_ref, m_ref, g_ref, wo_ref, mo_ref):
    g = g_ref[...]
    first = 0.5 * m_ref[0] + 0.5 * g
    root = jnp.sqrt(0.5 * m_ref[1] * m_ref[1] + 0.5 * g * g)
    w = w_ref[...]
    wo_ref[...] = w - rate * (first / (root + 1e-08) + 0.1 * w)
    mo_ref[0] = first
    mo_ref[1] = root


def adamw_pass(weight, moments, grad, rate):
    n, r, c = weight.shape
    spec = pl.BlockSpec((1, r, c), lambda i: (i, 0, 0))
    mspec = pl.BlockSpec((2, 1, r, c), lambda i: (0, i, 0, 0))
    return pl.pallas_call(
        functools.partial(adamw_kernel, rate),
        grid=(n,),
        in_specs=[spec, mspec, spec],
        out_specs=[spec, mspec],
        out_shape=[jax.ShapeDtypeStruct(weight.shape, F32), jax.ShapeDtypeStruct(moments.shape, F32)],
        cost_estimate=pl.CostEstimate(flops=12 * weight.size, bytes_accessed=28 * weight.size, transcendentals=2 * weight.size),
    )(weight, moments, grad)


def layer_norm(value, gain, shift):
    center = value - jnp.mean(value, -1, keepdims=True)
    spread = jnp.mean(center * center, -1, keepdims=True)
    return center * lax.rsqrt(spread + 1e-06) * gain + shift


def gelu_exact(value):
    return jax.nn.gelu(value, approximate=False)


def split_heads(part):
    return part.reshape(-1, S, HEADS, HEAD_DIM)


def dot(a, b):
    return jnp.dot(a, b, preferred_element_type=F32)


def assign_places(route):
    chosen = jnp.concatenate([route[:, :, 0], route[:, :, 1]], 1)
    hits = (chosen[:, :, None] == jnp.arange(E, dtype=jnp.int32)).astype(jnp.int32)
    before = jnp.cumsum(hits, 1) - hits
    slot = jnp.sum(before * hits, 2)
    return chosen * CAPP + slot, jnp.sum(hits, 1)


def hi_lo(v):
    hi = v.astype(BF16)
    lo = (v - hi.astype(F32)).astype(BF16)
    return jnp.concatenate([hi, lo], -1)


def pick_rows(onehot, split):
    both = jnp.einsum("mnr,mrd->mnd", onehot, split, preferred_element_type=F32)
    return both[..., :D] + both[..., D:]


def pack_dense(qkv_w, out_w, router_w, vectors, up_bias):
    rows = qkv_w.shape[0]
    ub = up_bias.reshape(E, rows, 4).transpose(1, 0, 2).reshape(rows, E * 4)
    return jnp.concatenate([qkv_w, out_w, router_w, vectors.T, ub], 1)


def unpack_dense(packed):
    rows = packed.shape[0]
    w_qkv = packed[:, : 3 * D]
    w_out = packed[:, 3 * D : 4 * D]
    w_router = packed[:, 4 * D : 4 * D + E]
    table = packed[:, 4 * D + E : 4 * D + E + NV].T
    ub = packed[:, 4 * D + E + NV :].reshape(rows, E, 4).transpose(1, 0, 2).reshape(E, rows * 4)
    return w_qkv, w_out, w_router, table, ub


def attention_fwd(w_qkv, w_out, table, value):
    rows = value.shape[0]
    nb = rows // S
    scale = HEAD_DIM ** (-0.5)
    first = layer_norm(value, table[0], table[1]).astype(BF16)
    qkv_bias = jnp.concatenate([table[2], jnp.zeros((D,), F32), table[3]]).reshape(3, 1, HEADS, 1, HEAD_DIM)
    w3 = w_qkv.reshape(D, 3, HEADS, HEAD_DIM)
    qkv = (jnp.einsum("bsk,kthd->tbhsd", first.reshape(nb, S, D), w3, preferred_element_type=F32) + qkv_bias).astype(BF16)
    query, key_part, val_part = qkv[0], qkv[1], qkv[2]
    scores = jnp.einsum("bhqd,bhkd->bhqk", query, key_part, preferred_element_type=F32) * scale
    peak = jnp.max(scores, -1, keepdims=True)
    expo = jnp.exp(scores - peak)
    total = jnp.sum(expo, -1, keepdims=True)
    probs_att = (expo / total).astype(BF16)
    log_total = peak + jnp.log(total)
    attended = jnp.einsum("bhqk,bhkd->bqhd", probs_att, val_part, preferred_element_type=F32)
    attended = attended.reshape(rows, D).astype(BF16)
    resid = value + (dot(attended, w_out) + table[4])
    return first, qkv, log_total, attended, resid


def attention_bwd(w_qkv, w_out, table, value, first, qkv, log_total, attended, d_resid):
    rows = value.shape[0]
    nb = rows // S
    scale = HEAD_DIM ** (-0.5)
    d_branch = d_resid.astype(BF16)
    g_bias_out = jnp.sum(d_branch.astype(F32), 0)
    g_out = lax.dot_general(attended, d_branch, (((0,), (0,)), ((), ())), preferred_element_type=F32)
    d_att = jnp.einsum(
        "bsn,hdn->bhsd", d_branch.reshape(nb, S, D), w_out.reshape(HEADS, HEAD_DIM, D), preferred_element_type=F32
    ).astype(BF16)
    query, key_part, val_part = qkv[0], qkv[1], qkv[2]
    scores = jnp.einsum("bhqd,bhkd->bhqk", query, key_part, preferred_element_type=F32) * scale
    probs_f = jnp.exp(scores - log_total)
    probs_att = probs_f.astype(BF16)
    d_val = jnp.einsum("bhqk,bhqd->bhkd", probs_att, d_att, preferred_element_type=F32)
    d_prob = jnp.einsum("bhqd,bhkd->bhqk", d_att, val_part, preferred_element_type=F32)
    d_score = (probs_f * (d_prob - jnp.sum(d_prob * probs_f, -1, keepdims=True))).astype(BF16)
    d_query = jnp.einsum("bhqk,bhkd->bhqd", d_score, key_part, preferred_element_type=F32) * scale
    d_key = jnp.einsum("bhqk,bhqd->bhkd", d_score, query, preferred_element_type=F32) * scale
    d_qkv = jnp.stack([d_query, d_key, d_val]).astype(BF16)
    d_qkv_f = d_qkv.astype(F32)
    g_bias_q = jnp.sum(d_qkv_f[0], (0, 2)).reshape(D)
    g_bias_v = jnp.sum(d_qkv_f[2], (0, 2)).reshape(D)
    first_b = first.reshape(nb, S, D)
    g_qkv = jnp.einsum("bsk,tbhsd->kthd", first_b, d_qkv, preferred_element_type=F32).reshape(D, 3 * D)
    w3 = w_qkv.reshape(D, 3, HEADS, HEAD_DIM)
    d_first = jnp.einsum("tbhsd,kthd->bsk", d_qkv, w3, preferred_element_type=F32).reshape(rows, D)
    first_pull = jax.vjp(layer_norm, value, table[0], table[1])[1]
    d_input, g_gain_one, g_shift_one = first_pull(d_first)
    return (g_qkv, g_out, g_bias_out, g_bias_q, g_bias_v, g_gain_one, g_shift_one), d_input


def adamw(weight, moments, grad, rate):
    first = 0.5 * moments[0] + 0.5 * grad
    root = jnp.sqrt(0.5 * moments[1] * moments[1] + 0.5 * grad * grad)
    update = first / (root + 1e-08)
    which = lax.broadcasted_iota(jnp.int32, moments.shape, 0) == 0
    both = jnp.where(which, 0.5 * moments + 0.5 * grad, jnp.sqrt(0.5 * moments * moments + 0.5 * grad * grad))
    return (weight - rate * (update + 0.1 * weight), both)


def shards(
    tokens,
    cotangent,
    expert_index,
    qkv_weight,
    out_weight,
    router_weight,
    up_weight,
    up_bias,
    down_weight,
    vectors,
    qkv_moments,
    out_moments,
    router_moments,
    up_moments,
    up_bias_moments,
    down_moments,
    vector_moments,
):
    rows = tokens.shape[0]
    micro = rows // MB_TOK
    gs = qkv_weight.shape[0]
    group_size = D // gs
    core = lax.axis_index("core")

    dense_in = pack_dense(qkv_weight, out_weight, router_weight, vectors, up_bias)
    width = dense_in.shape[1]
    dense_in = jnp.pad(dense_in, ((0, 0), (0, DENSE_AG - width))).astype(BF16)
    w_up_all, w_down_all, dense = ring_all_gather(
        up_weight.astype(BF16), down_weight.astype(BF16), dense_in, group_size, 1
    )
    w_qkv, w_out, w_router, table_b, b_up_b = unpack_dense(dense[:, :width])
    table = table_b.astype(F32)
    b_up = b_up_b.astype(F32)

    value = tokens.astype(F32)
    d_out = cotangent.astype(F32)
    first, qkv, log_total, attended, resid = attention_fwd(w_qkv, w_out, table, value)
    second = layer_norm(resid, table[5], table[6]).astype(BF16)
    logits = dot(second, w_router)
    probs = jax.nn.softmax(logits, -1)
    picked = expert_index[:, :, None] == jnp.arange(E, dtype=jnp.int32)
    gate = jnp.sum(jnp.where(picked, probs[:, None, :], 0.0), -1)

    route = expert_index.reshape(micro, MB_TOK, 2)
    places, counts = assign_places(route)
    counts = counts.T.reshape(E * micro)
    onehot = (places[:, :, None] == jnp.arange(E * CAPP, dtype=jnp.int32)).astype(BF16)
    second_m = second.reshape(micro, MB_TOK, D)
    pair = jnp.concatenate([second_m, second_m], 1)
    table_in = jnp.einsum("mnr,mnd->mrd", onehot, pair, preferred_element_type=F32).astype(BF16)

    hidden_pre, hidden, y_all = ffn_forward(
        counts, table_in, w_up_all, b_up[:, None, :], w_down_all, table[7 : 7 + E][:, None, :], micro
    )
    picked_rows = pick_rows(onehot, y_all)
    out_zero = picked_rows[:, :MB_TOK].reshape(rows, D)
    out_one = picked_rows[:, MB_TOK:].reshape(rows, D)
    result = resid + (gate[:, 0:1] * out_zero + gate[:, 1:2] * out_one)

    d_gate = jnp.stack([jnp.sum(d_out * out_zero, -1), jnp.sum(d_out * out_one, -1)], 1)
    d_out_m = d_out.reshape(micro, MB_TOK, D)
    gate_m = gate.reshape(micro, MB_TOK, 2)
    weighted = jnp.concatenate([gate_m[:, :, 0:1] * d_out_m, gate_m[:, :, 1:2] * d_out_m], 1).astype(BF16)
    d_expert = jnp.einsum("mnr,mnd->mrd", onehot, weighted, preferred_element_type=F32).astype(BF16)

    d_table, g_up, g_down, g_b1, g_b2 = ffn_backward(counts, d_expert, table_in, hidden_pre, hidden, w_up_all, w_down_all, micro)
    g_up_bias_all = g_b1[:, 0, :]
    g_bias_down = g_b2[:, 0, :]

    onehot_sum = onehot[:, :MB_TOK] + onehot[:, MB_TOK:]
    d_picked = pick_rows(onehot_sum, d_table).reshape(rows, D)

    d_probs = jnp.sum(jnp.where(picked, d_gate[:, :, None], 0.0), 1)
    d_logit = (probs * (d_probs - jnp.sum(d_probs * probs, -1, keepdims=True))).astype(BF16)
    g_router = lax.dot_general(second, d_logit, (((0,), (0,)), ((), ())), preferred_element_type=F32)
    d_second = d_picked + lax.dot_general(d_logit, w_router, (((1,), (1,)), ((), ())), preferred_element_type=F32)
    norm_pull = jax.vjp(layer_norm, resid, table[5], table[6])[1]
    d_resid, g_gain_two, g_shift_two = norm_pull(d_second)
    d_resid = d_out + d_resid

    att_grads, d_input = attention_bwd(w_qkv, w_out, table, value, first, qkv, log_total, attended, d_resid)
    g_qkv, g_out, g_bias_out, g_bias_q, g_bias_v, g_gain_one, g_shift_one = att_grads
    input_grad = d_resid + d_input

    g_table = jnp.concatenate(
        [
            jnp.stack([g_gain_one, g_shift_one, g_bias_q, g_bias_v, g_bias_out, g_gain_two, g_shift_two]),
            g_bias_down,
        ],
        0,
    )
    dense_g = pack_dense(g_qkv, g_out, g_router, g_table, g_up_bias_all)
    width = dense_g.shape[1]
    dense_g = jnp.pad(dense_g, ((0, 0), (0, DENSE_AG - width))).astype(BF16)
    x_pair = lax.axis_size("rx") == 2
    r_up, r_down, r_dense = grad_reduce(g_up, g_down, dense_g, group_size, x_pair, 0)
    if not x_pair:
        r_up, r_down, r_dense = lax.psum((r_up, r_down, r_dense), "rx")
    r_qkv, r_out, r_router, r_table, r_ub = unpack_dense(r_dense[:, :width])

    reduced = (r_qkv, r_out, r_router, r_up, r_ub, r_down, r_table)
    rates = (
        2.0 * D ** (-0.5),
        2.0 * (D // 32) ** (-0.5),
        2.0 * (2 * D) ** (-0.5),
        2.0 * D ** (-0.5),
        0.2,
        2.0 * (F // 16) ** (-0.5),
        0.2,
    )
    params = (qkv_weight, out_weight, router_weight, up_weight, up_bias, down_weight, vectors)
    moments = (qkv_moments, out_moments, router_moments, up_moments, up_bias_moments, down_moments, vector_moments)
    news = []
    states = []
    for weight, state, grad, rate in zip(params, moments, reduced, rates):
        if weight.ndim == 3:
            new_weight, new_state = adamw_pass(weight, state, grad, rate)
        else:
            new_weight, new_state = adamw(weight, state, grad, rate)
        news.append(new_weight)
        states.append(new_state)
    return (result.astype(BF16), input_grad) + reduced + tuple(news) + tuple(states)


def solution(mesh):
    replica, group = mesh.shape["replica"], mesh.shape["group"]
    view = Mesh(np.asarray(mesh.devices).reshape(replica // 2, 2, group), ("rx", "core", "group"))
    in_specs = (
        P(TOK, None),
        P(TOK, None),
        P(TOK, None),
        P("group", None),
        P("group", None),
        P("group", None),
        P(None, "group", None),
        P(None, "group"),
        P(None, "group", None),
        P(None, "group"),
        P(None, "group", None),
        P(None, "group", None),
        P(None, "group", None),
        P(None, None, "group", None),
        P(None, None, "group"),
        P(None, None, "group", None),
        P(None, None, "group"),
    )
    out_specs = (
        P(TOK, None),
        P(TOK, None),
        P("group", None),
        P("group", None),
        P("group", None),
        P(None, "group", None),
        P(None, "group"),
        P(None, "group", None),
        P(None, "group"),
        P("group", None),
        P("group", None),
        P("group", None),
        P(None, "group", None),
        P(None, "group"),
        P(None, "group", None),
        P(None, "group"),
        P(None, "group", None),
        P(None, "group", None),
        P(None, "group", None),
        P(None, None, "group", None),
        P(None, None, "group"),
        P(None, None, "group", None),
        P(None, None, "group"),
    )
    return jax.shard_map(shards, mesh=view, in_specs=in_specs, out_specs=out_specs, check_vma=False)
```
